32 devices in a mesh: au: 4 (over x, core), row: 8 (over z, y).
Axes of the slice: x: 2, y: 2, z: 4, core: 2. Of those that a mesh axis runs over, the one named last changes fastest.
Arguments:
- tokens: bfloat16 [4096, 768], P(('au', 'row')), may hold values from -6 to 6
- cotangent: bfloat16 [4096, 768], P(('au', 'row')), may hold values from -6 to 6
- doc_lengths: int32 [16], replicated, may hold values from 1 to 2048, 4096 in all
- query_weight: float32 [768, 768], P(('au', 'row')), may hold values from -0.21875 to 0.21875
- query_bias: float32 [768], P(('au', 'row')), may hold values from -3 to 3
- key_weight: float32 [768, 768], P(('au', 'row')), may hold values from -0.21875 to 0.21875
- value_weight: float32 [768, 768], P(('au', 'row')), may hold values from -0.21875 to 0.21875
- value_bias: float32 [768], P(('au', 'row')), may hold values from -0.3125 to 0.3125
- mix_weight: float32 [768, 768], P(('au', 'row')), may hold values from -1.75 to 1.75
- mix_bias: float32 [768], P(('au', 'row')), may hold values from -1.5 to 1.5
- early_gain: float32 [768], P(('au', 'row')), may hold values from 0.5 to 1.5
- early_shift: float32 [768], P(('au', 'row')), may hold values from -1.5 to 1.5
- inner_weight: float32 [768, 3072], P(('au', 'row')), may hold values from -0.21875 to 0.21875
- inner_bias: float32 [3072], P(('au', 'row')), may hold values from -1.5 to 1.5
- outer_weight: float32 [3072, 768], P(('au', 'row')), may hold values from -0.109375 to 0.109375
- outer_bias: float32 [768], P(('au', 'row')), may hold values from -1.5 to 1.5
- final_gain: float32 [768], P(('au', 'row')), may hold values from 0.5 to 1.5
- final_shift: float32 [768], P(('au', 'row')), may hold values from -1.5 to 1.5
Outputs:
- output: bfloat16 [4096, 768], P(('au', 'row'))
- input_grad: bfloat16 [4096, 768], P(('au', 'row'))
- query_weight_grad: float32 [768, 768], P(('au', 'row'))
- query_bias_grad: float32 [768], P(('au', 'row'))
- key_weight_grad: float32 [768, 768], P(('au', 'row'))
- value_weight_grad: float32 [768, 768], P(('au', 'row'))
- value_bias_grad: float32 [768], P(('au', 'row'))
- mix_weight_grad: float32 [768, 768], P(('au', 'row'))
- mix_bias_grad: float32 [768], P(('au', 'row'))
- early_gain_grad: float32 [768], P(('au', 'row'))
- early_shift_grad: float32 [768], P(('au', 'row'))
- inner_weight_grad: float32 [768, 3072], P(('au', 'row'))
- inner_bias_grad: float32 [3072], P(('au', 'row'))
- outer_weight_grad: float32 [3072, 768], P(('au', 'row'))
- outer_bias_grad: float32 [768], P(('au', 'row'))
- final_gain_grad: float32 [768], P(('au', 'row'))
- final_shift_grad: float32 [768], P(('au', 'row'))
The draws below stay inside these ranges and needn't reach their ends.
Inputs may be any that keep to these rules, and one draw needn't show every extreme that they name: `doc_lengths`: the documents lie one after another and fill the sequence: the lengths add up to 4096, and the longest is exactly 2048.
All inputs are finite; a program needn't handle non-finite values.
Results may differ from the reference program's by a relative error of at most 0.017.
Values may be sent and summed in bfloat16 or wider, within the bound.
A program may use at most 192 MiB of HBM per device.

```python
import functools
import math
import jax
import jax.numpy as jnp
import numpy as np
from jax import lax

D = 768
HEADS = 12
HEAD = 64
FF = 3072
NDOC = 16
TOKENS = 4096
MAXDOC = 2048


def raised(result, rng, source, target, blocks, factor):
    def block_of(position):
        return (jnp.arange(result.shape[position]) // (result.shape[position] // blocks)).reshape((-1,) + (1,) * (result.ndim - 1 - position))

    near = jax.random.permutation(rng, blocks)[block_of(target)]
    far = (block_of(target) + blocks // 2) % blocks
    return jnp.where((block_of(source) == near) | (block_of(source) == far), factor * result, result)


def block_levels(key, extent, shards, low, largest):
    loudness = 1.0
    for dim, parts in shards:
        heights = jax.random.uniform(jax.random.fold_in(jax.random.fold_in(key, 6), dim), (parts,), jnp.float32, low / len(shards), largest / len(shards))
        loudness = loudness * jnp.repeat(jnp.exp(heights), extent[dim] // parts).reshape((-1,) + (1,) * (len(extent) - 1 - dim))
    return loudness


def profile(count, total, reach, lean):
    weights = [(1 << 20) // math.isqrt(standing ** lean) + 1 for standing in range(2, count + 1)]
    rest, holding = total - reach - (count - 1), [1] * (count - 1)
    while rest > 0:
        movable = [i for i in range(count - 1) if holding[i] < reach]
        mass, remaining = sum([weights[i] for i in movable]), rest
        for i in movable:
            addition = min(reach - holding[i], max(1, remaining * weights[i] // mass), rest)
            holding[i] = holding[i] + addition
            rest = rest - addition
    return np.array([reach] + holding)


def ragged_sizes(own_key, count, total, limit, slope):
    if count == 2:
        one = jax.random.randint(own_key, (), max(1, total - limit), min(limit, total - 1) + 1)
        return jnp.stack([one, total - one])
    sizes = jnp.asarray(profile(count, total, limit, slope), jnp.int32)
    twos = (count - 1) // 2
    giver, sink = sizes[1:1 + 2 * twos:2], sizes[2:2 + 2 * twos:2]
    room = jnp.minimum(giver - 1, limit - sink)
    shifted = jax.random.randint(jax.random.fold_in(own_key, 1), (twos,), 0, 1 << 20) % (room + 1)
    sizes = sizes.at[1:1 + 2 * twos:2].set(giver - shifted).at[2:2 + 2 * twos:2].set(sink + shifted)
    return sizes[jax.random.permutation(jax.random.fold_in(own_key, 2), count)]


def centred(key, dims, scale, bound, shards=(), kind=jnp.bfloat16):
    entries = jax.random.normal(key, dims, jnp.float32) * scale
    if len(shards) > 0:
        entries = block_levels(key, dims, shards, -0.22, 0.18) * entries
    return jnp.clip(entries, min=-bound, max=bound).astype(kind)


def noise_with(key, dims, deviation, most, shards, heavy, kind=jnp.bfloat16):
    array = deviation * jax.random.normal(key, dims, jnp.float32)
    if shards:
        array = array * block_levels(key, dims, shards, -0.22, 0.18)
    return jnp.clip(raised(array, jax.random.fold_in(key, 3), *heavy), -most, most).astype(kind)


def setup_inputs(seed: int = 0) -> dict:
    streams_of = jax.random.split(jax.random.key(seed), 19)
    return {
        "tokens": centred(streams_of[0], (TOKENS, D), 1.0, 6.0, ((0, 32),)),
        "cotangent": noise_with(streams_of[1], (TOKENS, D), 1.0, 6.0, ((0, 32),), (0, 1, 32, 2.75)),
        "doc_lengths": ragged_sizes(streams_of[2], NDOC, TOKENS, MAXDOC, 1).astype(jnp.int32),
        "query_weight": centred(streams_of[3], (D, D), D ** -0.5, 0.21875, ((0, 32),), jnp.float32),
        "query_bias": centred(streams_of[4], (D,), 0.2, 3.0, ((0, 32),), jnp.float32),
        "key_weight": centred(streams_of[5], (D, D), D ** -0.5, 0.21875, ((0, 32),), jnp.float32),
        "value_weight": centred(streams_of[6], (D, D), D ** -0.5, 0.21875, ((0, 32),), jnp.float32),
        "value_bias": centred(streams_of[7], (D,), 0.02, 0.3125, ((0, 32),), jnp.float32),
        "mix_weight": centred(streams_of[8], (D, D), (max(1, D * NDOC * 4 // TOKENS)) ** -0.5, 1.75, ((0, 32),), jnp.float32),
        "mix_bias": centred(streams_of[9], (D,), 0.1, 1.5, ((0, 32),), jnp.float32),
        "early_gain": jnp.clip(1.0 + 0.1 * jax.random.normal(streams_of[10], (D,), jnp.float32), 0.5, 1.5),
        "early_shift": centred(streams_of[11], (D,), 0.1, 1.5, ((0, 32),), jnp.float32),
        "inner_weight": centred(streams_of[12], (D, FF), D ** -0.5, 0.21875, ((0, 32),), jnp.float32),
        "inner_bias": centred(streams_of[13], (FF,), 0.1, 1.5, ((0, 32),), jnp.float32),
        "outer_weight": centred(streams_of[14], (FF, D), FF ** -0.5, 0.109375, ((0, 32),), jnp.float32),
        "outer_bias": centred(streams_of[15], (D,), 0.1, 1.5, ((0, 32),), jnp.float32),
        "final_gain": jnp.clip(1.0 + 0.1 * jax.random.normal(streams_of[16], (D,), jnp.float32), 0.5, 1.5),
        "final_shift": centred(streams_of[17], (D,), 0.1, 1.5, ((0, 32),), jnp.float32),
    }


@jax.custom_vjp
def low(v):
    return lax.optimization_barrier(v.astype(jnp.bfloat16)).astype(jnp.float32)

@jax.custom_vjp
def low_back(v):
    return v

def low_keep(v):
    return (low(v), None)

def low_pass(kept, grad):
    return (grad,)

def back_keep(v):
    return (v, None)

def back_low(kept, grad):
    return (low(grad),)
low.defvjp(low_keep, low_pass)
low_back.defvjp(back_keep, back_low)
eps_norm = 1e-06
mask_fill = -1000000000.0
highest = lax.Precision.HIGHEST

def layer_norm(hidden, gain, shift):
    mean = lax.optimization_barrier(jnp.mean(hidden, axis=-1, keepdims=True))
    centered = hidden - mean
    spread = lax.optimization_barrier(jnp.mean(centered * centered, axis=-1, keepdims=True))
    return centered * lax.rsqrt(spread + eps_norm) * gain + shift

def product(left, right):
    return jnp.dot(left, right, precision=highest)

def segment_ids(doc_lengths):
    starts = jnp.cumsum(doc_lengths) - doc_lengths
    places = jnp.arange(TOKENS, dtype=jnp.int32)
    return lax.optimization_barrier(jnp.sum((starts[None, :] <= places[:, None]).astype(jnp.int32), axis=1)) - 1

def attend(queries, keys, values, segment):
    size = math.gcd(TOKENS, 512)
    count = TOKENS // size
    query_blocks = queries.reshape(count, size, HEADS, HEAD)
    segment_blocks = segment.reshape(count, size)
    key_heads = keys.reshape(TOKENS, HEADS, HEAD)
    value_heads = values.reshape(TOKENS, HEADS, HEAD)
    scale = HEAD ** (-0.5)

    def one_block(pair):
        block_queries, block_segment = pair
        scores = jnp.einsum('qhd,khd->hqk', block_queries, key_heads, precision=highest) * scale
        same = block_segment[:, None] == segment[None, :]
        scores = low_back(jnp.where(same[None, :, :], scores, mask_fill))
        top = lax.optimization_barrier(jnp.max(scores, axis=-1, keepdims=True))
        powers = jnp.exp(scores - top)
        total = lax.optimization_barrier(jnp.sum(powers, axis=-1))
        weighted = jnp.einsum('hqk,khd->qhd', low(powers), value_heads, precision=highest)
        return weighted / jnp.transpose(total)[:, :, None]
    mixed = lax.map(jax.checkpoint(one_block), (query_blocks, segment_blocks))
    return mixed.reshape(TOKENS, HEADS * HEAD)

def forward(segment, inputs, query_weight, query_bias, key_weight, value_weight, value_bias, mix_weight, mix_bias, early_gain, early_shift, inner_weight, inner_bias, outer_weight, outer_bias, final_gain, final_shift):
    queries = low_back(low(product(inputs, low(query_weight)) + low(query_bias)))
    keys = low_back(low(product(inputs, low(key_weight))))
    values = low_back(low(product(inputs, low(value_weight)) + low(value_bias)))
    mixed = low_back(low(attend(queries, keys, values, segment)))
    attn = low_back(product(mixed, low(mix_weight)) + low(mix_bias))
    early = layer_norm(inputs + attn, low(early_gain), low(early_shift))
    inner = low_back(product(low(early), low(inner_weight)) + low(inner_bias))
    act = low(jax.nn.gelu(inner, approximate=False))
    branch = low_back(product(act, low(outer_weight)) + low(outer_bias))
    return layer_norm(early + branch, low(final_gain), low(final_shift))

def reference(tokens, cotangent, doc_lengths, query_weight, query_bias, key_weight, value_weight, value_bias, mix_weight, mix_bias, early_gain, early_shift, inner_weight, inner_bias, outer_weight, outer_bias, final_gain, final_shift):
    segment = segment_ids(doc_lengths)
    layer = functools.partial(forward, segment)
    output, pull = jax.vjp(layer, tokens.astype(jnp.float32), query_weight, query_bias, key_weight, value_weight, value_bias, mix_weight, mix_bias, early_gain, early_shift, inner_weight, inner_bias, outer_weight, outer_bias, final_gain, final_shift)
    grads = pull(cotangent.astype(jnp.float32))
    return (output.astype(jnp.bfloat16), grads[0].astype(jnp.bfloat16), grads[1], grads[2], grads[3], grads[4], grads[5], grads[6], grads[7], grads[8], grads[9], grads[10], grads[11], grads[12], grads[13], grads[14], grads[15])
```

```python
import functools

import jax
import jax.numpy as jnp
from jax import lax
from jax.experimental import pallas as pl
from jax.experimental.pallas import tpu as pltpu
from jax.sharding import PartitionSpec as P

HEAD = 64
HEADS = 12
GROUPS = 4
LOCAL = HEADS // GROUPS
LANES = 2 * HEAD
WIDE = LOCAL * LANES
PACK = 256
eps_norm = 1e-06
mask_fill = -1000000000.0
lowest_start = -1e30
low_type = jnp.bfloat16
wide = jnp.float32
MESH = pl.DeviceIdType.MESH
VMEM_LIMIT = 62 * 1024 * 1024


def layer_norm(hidden, gain, shift):
    mean = jnp.mean(hidden, axis=-1, keepdims=True)
    centered = hidden - mean
    spread = jnp.mean(centered * centered, axis=-1, keepdims=True)
    return centered * lax.rsqrt(spread + eps_norm) * gain + shift


def gelu_exact(values):
    return jax.nn.gelu(values, approximate=False)


class Place:
    def __init__(self, zs):
        self.zs = zs
        a = lax.axis_index("au")
        r = lax.axis_index("row")
        self.x, self.c = a // 2, a % 2
        self.y, q = r % 2, r // 2
        self.g, self.z = q % GROUPS, q // GROUPS

    def at(self, x=None, c=None, z=None, g=None, y=None):
        x = self.x if x is None else x
        c = self.c if c is None else c
        z = self.z if z is None else z
        g = self.g if g is None else g
        y = self.y if y is None else y
        return (x * 2 + c, (z * GROUPS + g) * 2 + y)

    def sibling(self):
        return self.at(c=1 - self.c)

    def line(self):
        return [((self.g + k) % GROUPS, (self.g + GROUPS - k) % GROUPS) for k in range(1, GROUPS)]

    def column(self):
        count = self.zs * GROUPS
        q = self.z * GROUPS + self.g
        result = []
        for k in range(1, count):
            to, source = (q + k) % count, (q + count - k) % count
            result.append(((to // GROUPS, to % GROUPS), (source // GROUPS, source % GROUPS)))
        return result

    def plane(self, everywhere=True):
        result = []
        for dx in range(2):
            for dy in range(2):
                for dz in range(self.zs if everywhere else 1):
                    if dx + dy + dz == 0:
                        continue
                    to = ((self.x + dx) % 2, (self.z + dz) % self.zs, (self.y + dy) % 2)
                    source = (
                        (self.x + dx) % 2,
                        (self.z + self.zs - dz) % self.zs,
                        (self.y + dy) % 2,
                    )
                    result.append((to, source))
        return result


class Copies:
    def __init__(self, send, recv, local):
        self.send, self.recv, self.local = send, recv, local
        self.count = 0
        self.local_count = 0
        self.started = []
        self.local_started = []

    def push(self, source, target, device):
        copy = pltpu.make_async_remote_copy(
            src_ref=source,
            dst_ref=target,
            send_sem=self.send.at[self.count],
            recv_sem=self.recv.at[self.count],
            device_id=device,
            device_id_type=MESH,
        )
        self.count += 1
        copy.start()
        self.started.append(copy)
        return copy

    def keep(self, source, target):
        copy = pltpu.make_async_copy(source, target, self.local.at[self.local_count])
        self.local_count += 1
        copy.start()
        return copy

    def finish(self):
        for copy in self.started:
            copy.wait_send()


def greet(devices, partner=None, crossing=None):
    barrier = pltpu.get_barrier_semaphore()
    for device in devices:
        pl.semaphore_signal(barrier, inc=1, device_id=device, device_id_type=MESH)
    if partner is None:
        pl.semaphore_wait(barrier, len(devices))
        return

    @pl.when(crossing)
    def _():
        pl.semaphore_signal(barrier, inc=1, device_id=partner, device_id_type=MESH)
        pl.semaphore_wait(barrier, len(devices) + 1)

    @pl.when(jnp.logical_not(crossing))
    def _():
        pl.semaphore_wait(barrier, len(devices))


def comm_call(body, name, ident, outs, copies, locals_, args, spaces=None, out_spaces=None, scratch=()):
    spaces = [pl.ANY] * len(args) if spaces is None else spaces
    out_spaces = [pl.ANY] * len(outs) if out_spaces is None else out_spaces
    return pl.pallas_call(
        body,
        name=name,
        out_shape=tuple(outs),
        in_specs=[pl.BlockSpec(memory_space=space) for space in spaces],
        out_specs=tuple(pl.BlockSpec(memory_space=space) for space in out_spaces),
        scratch_shapes=[
            pltpu.SemaphoreType.DMA((max(copies, 1),)),
            pltpu.SemaphoreType.DMA((max(copies, 1),)),
            pltpu.SemaphoreType.DMA((max(locals_, 1),)),
            *scratch,
        ],
        compiler_params=pltpu.CompilerParams(
            collective_id=ident, has_side_effects=True, vmem_limit_bytes=VMEM_LIMIT
        ),
    )(*args)


def spread_tokens(zs, tokens, slab):
    n, width = tokens.shape
    groups, rows, columns = slab.shape
    plane = 4 * zs - 1

    def body(tok, piece, tok_all, w_all, send, recv, local):
        me = Place(zs)
        copies = Copies(send, recv, local)
        greet(
            [me.at(g=to) for to, _ in me.line()]
            + [me.at(x=to[0], z=to[1], y=to[2]) for to, _ in me.plane()]
            + [me.sibling()]
        )
        first = [
            copies.push(
                piece.at[to], w_all.at[me.x, me.c, me.z, me.g, me.y], me.at(g=to)
            )
            for to, _ in me.line()
        ]
        own = copies.keep(piece.at[me.g], w_all.at[me.x, me.c, me.z, me.g, me.y])
        arrivals = [copies.push(tok, tok_all.at[me.g], me.at(g=to)) for to, _ in me.line()]
        mine = copies.keep(tok, tok_all.at[me.g])
        own.wait()
        for copy in first:
            copy.wait_recv()
        block = w_all.at[me.x, me.c, me.z, :, me.y]
        second = [
            copies.push(block, block, me.at(x=to[0], z=to[1], y=to[2])) for to, _ in me.plane()
        ]
        arrivals.append(copies.push(block, block, me.sibling()))
        for copy, (_, source) in zip(second, me.plane()):
            copy.wait_recv()
            part = w_all.at[source[0], me.c, source[1], :, source[2]]
            arrivals.append(copies.push(part, part, me.sibling()))
        for copy in arrivals:
            copy.wait_recv()
        mine.wait()
        copies.finish()

    return comm_call(
        body,
        "spread_tokens",
        0,
        [
            jax.ShapeDtypeStruct((GROUPS, n, width), low_type),
            jax.ShapeDtypeStruct((2, 2, zs, GROUPS, 2, rows, columns), low_type),
        ],
        2 * (GROUPS - 1) + 2 * plane + 1,
        2,
        (tokens, slab),
    )


def spread_keys(zs, keys, inner, outer, mix):
    groups, n, width = keys.shape
    quarters, rows, columns = inner.shape
    tall, _ = outer.shape
    plane, column = 4 * zs - 1, GROUPS * zs - 1

    def body(kv, w1s, w2s, wms, kv_all, w1, w2, wm, send, recv, local, swap_send, swap_recv):
        me = Place(zs)
        copies = Copies(send, recv, local)
        crossing = me.c != me.y
        greet(
            [me.at(x=to[0], z=to[1], y=to[2]) for to, _ in me.plane()]
            + [me.at(z=to[0], g=to[1]) for to, _ in me.column()]
            + [me.at(z=to[0], g=to[1], c=me.y, y=me.c) for to, _ in me.column()]
            + [me.sibling()],
            me.at(c=me.y, y=me.c),
            crossing,
        )

        def here(ref):
            return ref.at[me.x, me.c, me.z, me.g, me.y]

        flat = me.plane(everywhere=False)
        own = [
            copies.keep(w1s.at[me.x * 2 + me.y], here(w1)),
            copies.keep(wms, here(wm)),
            copies.keep(kv, kv_all.at[me.x, me.c, me.z, :, me.y]),
        ]
        w1_first = [
            copies.push(w1s.at[to[0] * 2 + to[2]], here(w1), me.at(x=to[0], y=to[2]))
            for to, _ in flat
        ]
        wm_first = [
            copies.push(wms, here(wm), me.at(z=to[0], g=to[1])) for to, _ in me.column()
        ]
        mine = kv_all.at[me.x, me.c, me.z, :, me.y]
        kv_first = [
            copies.push(kv, mine, me.at(x=to[0], z=to[1], y=to[2])) for to, _ in me.plane()
        ]
        arrivals = [copies.push(kv, mine, me.sibling())]
        w2_first = [
            copies.push(
                w2s, w2.at[me.z, me.g, me.y], me.at(z=to[0], g=to[1], c=me.y, y=me.c)
            )
            for to, _ in me.column()
        ]
        exchanged = pltpu.make_async_remote_copy(
            src_ref=w2s,
            dst_ref=w2.at[me.z, me.g, me.y],
            send_sem=swap_send,
            recv_sem=swap_recv,
            device_id=me.at(c=me.y, y=me.c),
            device_id_type=MESH,
        )
        stays = pltpu.make_async_copy(w2s, w2.at[me.z, me.g, me.y], swap_recv)

        @pl.when(crossing)
        def _():
            exchanged.start()

        @pl.when(jnp.logical_not(crossing))
        def _():
            stays.start()

        own[0].wait()
        for copy in w1_first:
            copy.wait_recv()
        block = w1.at[:, me.c, me.z, me.g, :]
        w1_second = [
            copies.push(block, block, me.at(z=to[0], g=to[1])) for to, _ in me.column()
        ]
        arrivals.append(copies.push(block, block, me.sibling()))
        own[1].wait()
        for copy in wm_first:
            copy.wait_recv()
        block = wm.at[me.x, me.c, :, :, me.y]
        wm_second = [copies.push(block, block, me.at(x=to[0], y=to[2])) for to, _ in flat]
        arrivals.append(copies.push(block, block, me.sibling()))
        for copy, (_, source) in zip(kv_first, me.plane()):
            copy.wait_recv()
            part = kv_all.at[source[0], me.c, source[1], :, source[2]]
            arrivals.append(copies.push(part, part, me.sibling()))

        @pl.when(crossing)
        def _():
            exchanged.wait_recv()
            exchanged.wait_send()

        @pl.when(jnp.logical_not(crossing))
        def _():
            stays.wait()

        part = w2.at[me.z, me.g, me.c]
        arrivals.append(copies.push(part, part, me.sibling()))
        for copy, (_, source) in zip(wm_second, flat):
            copy.wait_recv()
            part = wm.at[source[0], me.c, :, :, source[2]]
            arrivals.append(copies.push(part, part, me.sibling()))
        for copy, (_, source) in zip(w2_first, me.column()):
            copy.wait_recv()
            part = w2.at[source[0], source[1], me.c]
            arrivals.append(copies.push(part, part, me.sibling()))
        for copy, (_, source) in zip(w1_second, me.column()):
            copy.wait_recv()
            part = w1.at[:, me.c, source[0], source[1], :]
            arrivals.append(copies.push(part, part, me.sibling()))
        for copy in arrivals:
            copy.wait_recv()
        own[2].wait()
        copies.finish()

    return comm_call(
        body,
        "spread_keys",
        1,
        [
            jax.ShapeDtypeStruct((2, 2, zs, GROUPS, 2, n, width), low_type),
            jax.ShapeDtypeStruct((2, 2, zs, GROUPS, 2, rows, columns), low_type),
            jax.ShapeDtypeStruct((zs, GROUPS, 2, tall, columns), low_type),
            jax.ShapeDtypeStruct((2, 2, zs, GROUPS, 2) + mix.shape, low_type),
        ],
        2 * plane + 1 + 2 * (3 + column + 1 + column) + column + 3 + 8,
        3,
        (keys, inner, outer, mix),
        scratch=(pltpu.SemaphoreType.DMA, pltpu.SemaphoreType.DMA),
    )


def exchange_line(zs, ident, pieces):
    def body(source, target, send, recv, local):
        me = Place(zs)
        copies = Copies(send, recv, local)
        greet([me.at(g=to) for to, _ in me.line()])
        arrivals = [
            copies.push(source.at[to], target.at[me.g], me.at(g=to)) for to, _ in me.line()
        ]
        own = copies.keep(source.at[me.g], target.at[me.g])
        for copy in arrivals:
            copy.wait_recv()
        own.wait()
        copies.finish()

    return comm_call(
        body,
        "exchange_line",
        ident,
        [jax.ShapeDtypeStruct(pieces.shape, pieces.dtype)],
        GROUPS - 1,
        1,
        (pieces,),
    )[0]


def gather_square(zs, ident, rows):
    def body(source, target, send, recv, local):
        me = Place(zs)
        copies = Copies(send, recv, local)
        flat = me.plane(everywhere=False)
        greet([me.at(x=to[0], y=to[2]) for to, _ in flat])
        place = target.at[me.x, me.y]
        arrivals = [copies.push(source, place, me.at(x=to[0], y=to[2])) for to, _ in flat]
        own = copies.keep(source, place)
        for copy in arrivals:
            copy.wait_recv()
        own.wait()
        copies.finish()

    return comm_call(
        body,
        "gather_square",
        ident,
        [jax.ShapeDtypeStruct((2, 2) + rows.shape, rows.dtype)],
        3,
        1,
        (rows,),
    )[0]


def exchange_square(zs, ident, pieces):
    def body(source, target, send, recv, local):
        me = Place(zs)
        copies = Copies(send, recv, local)
        flat = me.plane(everywhere=False)
        greet([me.at(x=to[0], y=to[2]) for to, _ in flat])
        place = target.at[me.x, me.y]
        arrivals = [
            copies.push(source.at[to[0], to[2]], place, me.at(x=to[0], y=to[2]))
            for to, _ in flat
        ]
        own = copies.keep(source.at[me.x, me.y], place)
        for copy in arrivals:
            copy.wait_recv()
        own.wait()
        copies.finish()

    return comm_call(
        body,
        "exchange_square",
        ident,
        [jax.ShapeDtypeStruct(pieces.shape, pieces.dtype)],
        3,
        1,
        (pieces,),
    )[0]


def loop(count, step):
    def body(index, carry):
        step(index)
        return carry

    lax.fori_loop(0, count, body, 0)


def total_of(*values):
    result = values[0].astype(wide)
    for value in values[1:]:
        result = result + value.astype(wide)
    return result


def reduce_keys(zs, dkv, grad1, grad2, gradm):
    n, width = dkv.shape[-2:]
    rows, columns = grad1.shape[-2:]
    rowsm = gradm.shape[-2]
    tall = grad2.shape[-2]
    plane, column = 4 * zs - 1, GROUPS * zs - 1
    count = GROUPS * zs

    def body(
        dkv_ref, g1, g2, gm, dkv_out, out1, out2, outm,
        send, recv, local,
        swap_send, swap_recv, kst, s1, p1, f1, s2, p2, sm, pm, fm, tm,
    ):
        me = Place(zs)
        copies = Copies(send, recv, local)
        crossing = me.c != me.y
        greet(
            [me.at(x=to[0], z=to[1], y=to[2]) for to, _ in me.plane()]
            + [me.at(z=to[0], g=to[1]) for to, _ in me.column()]
            + [me.at(z=to[0], g=to[1], c=me.y, y=me.c) for to, _ in me.column()]
            + [me.sibling()],
            me.at(c=me.y, y=me.c),
            crossing,
        )

        flat = me.plane(everywhere=False)
        other = 1 - me.c
        order = [to for to, _ in me.plane()] + [(me.x, me.z, me.y)]
        w1_half = copies.push(g1.at[:, other], s1, me.sibling())
        w2_half = copies.push(g2.at[:, :, other], s2, me.sibling())
        k_half = [
            copies.push(
                dkv_ref.at[to[0], other, to[1], :, to[2]], kst.at[to[0], to[1], to[2]], me.sibling()
            )
            for to in order
        ]
        wm_half = copies.push(gm.at[:, other], sm, me.sibling())

        w1_half.wait_recv()

        def add1(index):
            x, z, g, y = index // (count * 2), index // (GROUPS * 2) % zs, index // 2 % GROUPS, index % 2
            s1[x, z, g, y] = total_of(s1[x, z, g, y], g1[x, me.c, z, g, y]).astype(low_type)

        loop(4 * count, add1)
        w1_push = [
            copies.push(s1.at[:, to[0], to[1], :], p1.at[slot], me.at(z=to[0], g=to[1]))
            for slot, (to, _) in enumerate(me.column())
        ]
        w2_half.wait_recv()

        def add2(index):
            z, g = index // GROUPS, index % GROUPS
            s2[z, g] = total_of(s2[z, g], g2[z, g, me.c]).astype(low_type)

        loop(count, add2)
        w2_push = [
            copies.push(
                s2.at[to[0], to[1]], p2.at[slot + 1], me.at(z=to[0], g=to[1], c=me.y, y=me.c)
            )
            for slot, (to, _) in enumerate(me.column())
        ]
        exchanged = pltpu.make_async_remote_copy(
            src_ref=s2.at[me.z, me.g],
            dst_ref=p2.at[0],
            send_sem=swap_send,
            recv_sem=swap_recv,
            device_id=me.at(c=me.y, y=me.c),
            device_id_type=MESH,
        )
        stays = pltpu.make_async_copy(s2.at[me.z, me.g], p2.at[0], swap_recv)

        @pl.when(crossing)
        def _():
            exchanged.start()

        @pl.when(jnp.logical_not(crossing))
        def _():
            stays.start()

        k_push = []
        for slot, to in enumerate(order):
            k_half[slot].wait_recv()

            def addk(g, to=to):
                kst[to[0], to[1], to[2], g] = total_of(
                    kst[to[0], to[1], to[2], g], dkv_ref[to[0], me.c, to[1], g, to[2]]
                ).astype(low_type)

            loop(GROUPS, addk)
            if slot < plane:
                k_push.append(
                    copies.push(
                        kst.at[to[0], to[1], to[2]],
                        dkv_out.at[slot],
                        me.at(x=to[0], z=to[1], y=to[2]),
                    )
                )
        wm_half.wait_recv()

        def addm(index):
            x, z, g, y = index // (count * 2), index // (GROUPS * 2) % zs, index // 2 % GROUPS, index % 2
            sm[x, z, g, y] = total_of(sm[x, z, g, y], gm[x, me.c, z, g, y]).astype(low_type)

        loop(4 * count, addm)
        wm_push = [
            copies.push(sm.at[to[0], :, :, to[2]], pm.at[slot], me.at(x=to[0], y=to[2]))
            for slot, (to, _) in enumerate(flat)
        ]
        keep = copies.keep(kst.at[me.x, me.z, me.y], dkv_out.at[plane])
        for copy in wm_push:
            copy.wait_recv()

        def addf(index):
            z, g = index // GROUPS, index % GROUPS
            fm[z, g] = total_of(sm[me.x, z, g, me.y], pm[0, z, g], pm[1, z, g], pm[2, z, g]).astype(
                low_type
            )

        loop(count, addf)
        wm_last = [
            copies.push(fm.at[to[0], to[1]], tm.at[slot], me.at(z=to[0], g=to[1]))
            for slot, (to, _) in enumerate(me.column())
        ]
        for copy in w1_push:
            copy.wait_recv()

        def addg(index):
            x, y = index // 2, index % 2
            f1[x, y] = total_of(
                s1[x, me.z, me.g, y], *[p1[slot, x, y] for slot in range(column)]
            ).astype(low_type)

        loop(4, addg)
        quarter = out1.at[me.x * 2 + me.y]
        w1_last = [
            copies.push(f1.at[to[0], to[2]], quarter, me.at(x=to[0], y=to[2])) for to, _ in flat
        ]
        keep1 = copies.keep(f1.at[me.x, me.y], quarter)

        @pl.when(crossing)
        def _():
            exchanged.wait_recv()
            exchanged.wait_send()

        @pl.when(jnp.logical_not(crossing))
        def _():
            stays.wait()

        for copy in w2_push:
            copy.wait_recv()
        out2[...] = total_of(*[p2[slot] for slot in range(column + 1)])
        for copy in wm_last:
            copy.wait_recv()
        outm[...] = total_of(fm[me.z, me.g], *[tm[slot] for slot in range(column)])
        for copy in w1_last + k_push:
            copy.wait_recv()
        keep.wait()
        keep1.wait()
        copies.finish()

    vmem = pltpu.VMEM
    return comm_call(
        body,
        "reduce_keys",
        8,
        [
            jax.ShapeDtypeStruct((plane + 1, GROUPS, n, width), low_type),
            jax.ShapeDtypeStruct((4, rows, columns), low_type),
            jax.ShapeDtypeStruct((tall, columns), wide),
            jax.ShapeDtypeStruct((rowsm, columns), wide),
        ],
        3 + (plane + 1) + 2 * column + plane + 3 + column + 3,
        2,
        (dkv, grad1, grad2, gradm),
        spaces=[vmem] * 4,
        out_spaces=[pl.ANY, pl.ANY, vmem, vmem],
        scratch=(
            pltpu.SemaphoreType.DMA,
            pltpu.SemaphoreType.DMA,
            vmem((2, zs, 2, GROUPS, n, width), low_type),
            vmem((2, zs, GROUPS, 2, rows, columns), low_type),
            vmem((column, 2, 2, rows, columns), low_type),
            vmem((2, 2, rows, columns), low_type),
            vmem((zs, GROUPS, tall, columns), low_type),
            vmem((column + 1, tall, columns), low_type),
            vmem((2, zs, GROUPS, 2, rowsm, columns), low_type),
            vmem((3, zs, GROUPS, rowsm, columns), low_type),
            vmem((zs, GROUPS, rowsm, columns), low_type),
            vmem((column, rowsm, columns), low_type),
        ),
    )


def reduce_tokens(zs, dx, gradq):
    rows, columns = gradq.shape[-2:]
    plane = 4 * zs - 1
    count = GROUPS * zs

    def body(dx_ref, gq, dx_out, outq, send, recv, local, sq, pq, fq):
        me = Place(zs)
        copies = Copies(send, recv, local)
        greet(
            [me.at(g=to) for to, _ in me.line()]
            + [me.at(x=to[0], z=to[1], y=to[2]) for to, _ in me.plane()]
            + [me.sibling()]
        )
        half = copies.push(gq.at[:, 1 - me.c], sq, me.sibling())
        arrivals = [
            copies.push(dx_ref.at[to], dx_out.at[me.g], me.at(g=to)) for to, _ in me.line()
        ]
        own = copies.keep(dx_ref.at[me.g], dx_out.at[me.g])
        half.wait_recv()

        def add1(index):
            x, z, g, y = index // (count * 2), index // (GROUPS * 2) % zs, index // 2 % GROUPS, index % 2
            sq[x, z, g, y] = total_of(sq[x, z, g, y], gq[x, me.c, z, g, y]).astype(low_type)

        loop(4 * count, add1)
        second = [
            copies.push(
                sq.at[to[0], to[1], :, to[2]], pq.at[slot], me.at(x=to[0], z=to[1], y=to[2])
            )
            for slot, (to, _) in enumerate(me.plane())
        ]
        for copy in second:
            copy.wait_recv()

        def add2(g):
            fq[g] = total_of(
                sq[me.x, me.z, g, me.y], *[pq[slot, g] for slot in range(plane)]
            ).astype(low_type)

        loop(GROUPS, add2)
        arrivals += [
            copies.push(fq.at[to], outq.at[me.g], me.at(g=to)) for to, _ in me.line()
        ]
        keep = copies.keep(fq.at[me.g], outq.at[me.g])
        for copy in arrivals:
            copy.wait_recv()
        own.wait()
        keep.wait()
        copies.finish()

    vmem = pltpu.VMEM
    return comm_call(
        body,
        "reduce_tokens",
        9,
        [
            jax.ShapeDtypeStruct(dx.shape, low_type),
            jax.ShapeDtypeStruct((GROUPS, rows, columns), low_type),
        ],
        1 + 2 * (GROUPS - 1) + plane,
        2,
        (dx, gradq),
        spaces=[pl.ANY, vmem],
        scratch=(
            vmem((2, zs, GROUPS, 2, rows, columns), low_type),
            vmem((plane, GROUPS, rows, columns), low_type),
            vmem((GROUPS, rows, columns), low_type),
        ),
    )


NEXT = (((1,), (1,)), ((), ()))
DOWN = (((0,), (0,)), ((), ()))


def attend_forward(queries, keys, bounds, low, high, tile, block):
    total_rows = queries.shape[0]

    def body(bounds_ref, q_ref, kv_ref, low_ref, high_ref, out_ref, keep_ref, lse_ref):
        def one(turn, unused):
            rows = pl.ds(pl.multiple_of(turn * tile, tile), tile)
            first, last = low_ref[rows, :], high_ref[rows, :]
            heads = [
                q_ref[rows, h * LANES : (h + 1) * LANES] * jnp.asarray(0.125, low_type)
                for h in range(LOCAL)
            ]

            def step(j, carry):
                begin = pl.multiple_of(j * block, block)
                place = begin + lax.broadcasted_iota(jnp.int32, (tile, block), 1)
                same = (place >= first) & (place < last)
                result = []
                for h in range(LOCAL):
                    top, total, mixed = carry[h]
                    kv = kv_ref[pl.ds(begin, block), h * LANES : (h + 1) * LANES]
                    scores = lax.dot_general(heads[h], kv, NEXT, preferred_element_type=wide)
                    scores = jnp.where(same, scores, mask_fill)
                    new_top = jnp.maximum(top, jnp.max(scores, axis=1, keepdims=True))
                    factor = jnp.exp(top - new_top)
                    powers = jnp.exp(scores - new_top)
                    total = total * factor + jnp.sum(powers, axis=1, keepdims=True)
                    mixed = mixed * factor + jnp.dot(
                        powers.astype(low_type), kv, preferred_element_type=wide
                    )
                    result.append((new_top, total, mixed))
                return tuple(result)

            start = tuple(
                (
                    jnp.full((tile, 1), lowest_start, wide),
                    jnp.zeros((tile, 1), wide),
                    jnp.zeros((tile, LANES), wide),
                )
                for _ in range(LOCAL)
            )
            done = lax.fori_loop(bounds_ref[turn, 0], bounds_ref[turn, 1], step, start)
            lane = lax.broadcasted_iota(jnp.int32, (tile, LANES), 1)
            upper = lane >= HEAD
            mixes = [mixed / total for _, total, mixed in done]
            turned = [pltpu.roll(mixed, HEAD, 1) for mixed in mixes]
            front = jnp.where(upper, mixes[1], turned[0])
            back = jnp.where(upper, 0.0, turned[2])
            both = jnp.concatenate([front, back], axis=1)
            keep_ref[rows, :] = both
            out_ref[rows, :] = both.astype(low_type)
            ends = [top + jnp.log(total) for top, total, _ in done]
            lse_ref[rows, :] = jnp.where(lane == 0, ends[0], jnp.where(lane == 1, ends[1], ends[2]))
            return unused

        lax.fori_loop(0, total_rows // tile, one, 0)

    vmem = pl.BlockSpec(memory_space=pltpu.VMEM)
    return pl.pallas_call(
        body,
        name="attend_forward",
        out_shape=(
            jax.ShapeDtypeStruct((total_rows, PACK), low_type),
            jax.ShapeDtypeStruct((total_rows, PACK), wide),
            jax.ShapeDtypeStruct((total_rows, LANES), wide),
        ),
        in_specs=[pl.BlockSpec(memory_space=pltpu.SMEM)] + [vmem] * 4,
        out_specs=(vmem,) * 3,
        compiler_params=pltpu.CompilerParams(vmem_limit_bytes=VMEM_LIMIT),
    )(bounds, queries, keys, low, high)


def attend_backward(queries, keys, grads, stats, bounds, tile, block):
    total_rows = queries.shape[0]
    tokens = keys.shape[0]

    def body(bounds_ref, q_ref, kv_ref, do_ref, stat_ref, dq_ref, dkv_ref, sums):
        h = pl.program_id(0)
        zeros = jnp.zeros((block, LANES), wide)

        def clear(j, unused):
            sums[pl.ds(pl.multiple_of(j * block, block), block), :] = zeros
            return unused

        lax.fori_loop(0, tokens // block, clear, 0)
        lane = lax.broadcasted_iota(jnp.int32, (tile, LANES), 1)
        upper = lane >= HEAD

        def one(turn, unused):
            rows = pl.ds(pl.multiple_of(turn * tile, tile), tile)
            q = q_ref[rows, :] * jnp.asarray(0.125, low_type)
            front = do_ref[rows, :LANES].astype(wide)
            back = do_ref[rows, LANES:].astype(wide)
            grad = jnp.where(h == 1, front, pltpu.roll(jnp.where(h == 0, front, back), HEAD, 1))
            grad = jnp.where(upper, grad, 0.0).astype(low_type)
            stat = stat_ref[turn, 0]
            first, last = stat[0:1, :], stat[1:2, :]
            lse, delta = stat[2:3, :], stat[3:4, :]

            def step(j, total):
                begin = pl.multiple_of(j * block, block)
                place = (begin + lax.broadcasted_iota(jnp.int32, (block, tile), 0)).astype(wide)
                same = (place >= first) & (place < last)
                kv = kv_ref[pl.ds(begin, block), :]
                scores = lax.dot_general(kv, q, NEXT, preferred_element_type=wide)
                probs = jnp.exp(jnp.where(same, scores, mask_fill) - lse)
                dots = lax.dot_general(kv, grad, NEXT, preferred_element_type=wide)
                score_grad = (probs * (dots - delta)).astype(low_type)
                sums[pl.ds(begin, block), :] += jnp.dot(
                    score_grad, q, preferred_element_type=wide
                ) + jnp.dot(probs.astype(low_type), grad, preferred_element_type=wide)
                return total + lax.dot_general(score_grad, kv, DOWN, preferred_element_type=wide)

            total = lax.fori_loop(
                bounds_ref[turn, 0], bounds_ref[turn, 1], step, jnp.zeros((tile, LANES), wide)
            )
            dq_ref[rows, :] = jnp.where(upper, 0.0, total * 0.125).astype(low_type)
            return unused

        lax.fori_loop(0, total_rows // tile, one, 0)

        def store(j, unused):
            part = pl.ds(pl.multiple_of(j * block, block), block)
            dkv_ref[part, :] = sums[part, :].astype(low_type)
            return unused

        lax.fori_loop(0, tokens // block, store, 0)

    return pl.pallas_call(
        body,
        name="attend_backward",
        grid=(LOCAL,),
        out_shape=(
            jax.ShapeDtypeStruct((total_rows, WIDE), low_type),
            jax.ShapeDtypeStruct((tokens, WIDE), low_type),
        ),
        in_specs=[
            pl.BlockSpec(memory_space=pltpu.SMEM),
            pl.BlockSpec((total_rows, LANES), lambda h: (0, h)),
            pl.BlockSpec((tokens, LANES), lambda h: (0, h)),
            pl.BlockSpec((total_rows, PACK), lambda h: (0, 0)),
            pl.BlockSpec((total_rows // tile, 1, 8, tile), lambda h: (0, h, 0, 0)),
        ],
        out_specs=(
            pl.BlockSpec((total_rows, LANES), lambda h: (0, h)),
            pl.BlockSpec((tokens, LANES), lambda h: (0, h)),
        ),
        scratch_shapes=[pltpu.VMEM((tokens, LANES), wide)],
        compiler_params=pltpu.CompilerParams(vmem_limit_bytes=VMEM_LIMIT),
    )(bounds, queries, keys, grads, stats)


def on_device(
    tokens,
    cotangent,
    doc_lengths,
    query_weight,
    query_bias,
    key_weight,
    value_weight,
    value_bias,
    mix_weight,
    mix_bias,
    early_gain,
    early_shift,
    inner_weight,
    inner_bias,
    outer_weight,
    outer_bias,
    final_gain,
    final_shift,
):
    n, depth = tokens.shape
    groups, cycle = lax.axis_size("au"), lax.axis_size("row")
    devices = groups * cycle
    zs = cycle // (2 * GROUPS)
    s = query_weight.shape[0]
    ff = inner_weight.shape[1]
    quarter = ff // 4
    e = outer_weight.shape[0]
    rows = GROUPS * n
    total_tokens = n * devices
    me = Place(zs)
    device = lax.axis_index("au") * cycle + lax.axis_index("row")
    w_me = me.x * 2 + me.y

    def by_head(weight):
        return weight.astype(low_type).reshape(-1, GROUPS, LOCAL, HEAD)

    def packed(query, key, value):
        kv = jnp.stack([key, value], axis=3).reshape(-1, GROUPS, WIDE)
        q = jnp.pad(query, ((0, 0), (0, 0), (0, 0), (0, HEAD))).reshape(-1, GROUPS, WIDE)
        return jnp.concatenate([kv, q], axis=2)

    slab = packed(by_head(query_weight), by_head(key_weight), by_head(value_weight))
    slab = jnp.transpose(slab, (1, 0, 2))
    small = jnp.concatenate(
        [
            vector.astype(low_type)
            for vector in (
                query_bias, value_bias, mix_bias, early_gain, early_shift,
                outer_bias, final_gain, final_shift, inner_bias,
            )
        ]
    )
    extra = -s % 8 or 8
    small = jnp.broadcast_to(
        jnp.pad(small, (0, 2 * WIDE - small.shape[0]))[None, None], (GROUPS, extra, 2 * WIDE)
    )
    slab = jnp.concatenate([slab, small], axis=1)
    tok_all, w_all = spread_tokens(zs, tokens, slab)
    tok_all = tok_all.reshape(rows, depth)
    w_qkv = w_all[..., :s, :].reshape(depth, 2 * WIDE)
    small = w_all[..., s, :].reshape(devices, 2 * WIDE)
    names = [small[:, i * s : (i + 1) * s].reshape(depth) for i in range(8)]
    q_bias, v_bias, m_bias, e_gain, e_shift, o_bias, f_gain, f_shift = names
    i_bias = small[:, 8 * s : 8 * s + e].reshape(4, quarter)[w_me].astype(wide)
    q_bias = q_bias.reshape(1, GROUPS, LOCAL, HEAD)
    v_bias = v_bias.reshape(1, GROUPS, LOCAL, HEAD)
    bias = packed(q_bias, jnp.zeros_like(q_bias), v_bias)[0, me.g].astype(wide)

    qkv = (jnp.dot(tok_all, w_qkv, preferred_element_type=wide) + bias).astype(low_type)
    queries = qkv[:, WIDE:]

    inner_slab = jnp.transpose(inner_weight.astype(low_type).reshape(s, 4, quarter), (1, 0, 2))
    kv_all, w1, w2, wm = spread_keys(
        zs,
        qkv[:, :WIDE].reshape(GROUPS, n, WIDE),
        inner_slab,
        outer_weight.astype(low_type),
        mix_weight.astype(low_type),
    )
    kv_all = kv_all.reshape(total_tokens, WIDE)
    w1 = w1.reshape(depth, quarter)
    w2 = w2.reshape(quarter, depth)
    wm = wm.reshape(depth, depth)

    tile, block = 128, 512
    count = doc_lengths.shape[0]
    upto = jnp.arange(count)[None, :] <= jnp.arange(count)[:, None]
    ends = jnp.sum(jnp.where(upto, doc_lengths[None, :], 0), axis=1)
    owners = ((me.x * 2 + me.c) * cycle + me.z * GROUPS * 2 + jnp.arange(GROUPS) * 2 + me.y) * n
    places = (owners[:, None] + jnp.arange(n)[None, :]).reshape(rows)
    before = ends[None, :] <= places[:, None]
    first = jnp.max(jnp.where(before, ends[None, :], 0), axis=1).astype(jnp.int32)
    last = jnp.min(jnp.where(before, total_tokens, ends[None, :]), axis=1).astype(jnp.int32)
    tiles = rows // tile
    bounds = jnp.stack(
        [
            first.reshape(tiles, tile)[:, 0] // block,
            (last.reshape(tiles, tile)[:, -1] + block - 1) // block,
        ],
        axis=1,
    )
    mixed, mixed_wide, lse = attend_forward(
        queries, kv_all, bounds, first[:, None], last[:, None], tile, block
    )
    mixed_tok = exchange_line(zs, 2, mixed.reshape(GROUPS, n, PACK))
    mixed_tok = jnp.transpose(mixed_tok[:, :, : LOCAL * HEAD], (1, 0, 2)).reshape(n, depth)

    attn = jnp.dot(mixed_tok, wm, preferred_element_type=wide) + m_bias.astype(wide)
    early, early_pull = jax.vjp(
        layer_norm, tokens.astype(wide) + attn, e_gain.astype(wide), e_shift.astype(wide)
    )
    early_all = gather_square(zs, 3, early.astype(low_type)).reshape(rows, depth)
    inner = jnp.dot(early_all, w1, preferred_element_type=wide) + i_bias
    act, gelu_pull = jax.vjp(gelu_exact, inner)
    act_low = act.astype(low_type)
    partial = jnp.dot(act_low, w2, preferred_element_type=wide).astype(low_type)
    partial = exchange_square(zs, 4, partial.reshape(2, 2, n, depth))
    branch = jnp.sum(partial.astype(wide), axis=(0, 1)) + o_bias.astype(wide)
    result, final_pull = jax.vjp(
        layer_norm, early + branch, f_gain.astype(wide), f_shift.astype(wide)
    )
    output = result.astype(low_type)
    final_grads = final_pull(cotangent.astype(wide))
    branch_grad = final_grads[0].astype(low_type)
    outer_bias_grad = jnp.sum(branch_grad.astype(wide), axis=0)
    branch_all = gather_square(zs, 5, branch_grad).reshape(rows, depth)
    act_grad = jnp.einsum("td,fd->tf", branch_all, w2, preferred_element_type=wide)
    inner_grad = gelu_pull(act_grad)[0].astype(low_type)
    partial = jnp.einsum("tf,df->td", inner_grad, w1, preferred_element_type=wide).astype(low_type)
    partial = exchange_square(zs, 6, partial.reshape(2, 2, n, depth))
    grad2 = jnp.einsum("tf,td->fd", act_low, branch_all, preferred_element_type=wide)
    grad1 = jnp.einsum("td,tf->df", early_all, inner_grad, preferred_element_type=wide)
    inner_bias_grad = jnp.sum(inner_grad.astype(wide), axis=0)
    early_grad = final_grads[0] + jnp.sum(partial.astype(wide), axis=(0, 1))
    early_grads = early_pull(early_grad)
    attn_grad = early_grads[0].astype(low_type)
    mixed_grad = jnp.einsum("td,cd->tc", attn_grad, wm, preferred_element_type=wide)
    mixed_grad = jnp.transpose(
        mixed_grad.astype(low_type).reshape(n, GROUPS, LOCAL * HEAD), (1, 0, 2)
    )
    mixed_grad = jnp.pad(mixed_grad, ((0, 0), (0, 0), (0, PACK - LOCAL * HEAD)))
    grad_all = exchange_line(zs, 7, mixed_grad).reshape(rows, PACK)
    gradm = jnp.einsum("tc,td->cd", mixed_tok, attn_grad, preferred_element_type=wide)
    mix_bias_grad = jnp.sum(attn_grad.astype(wide), axis=0)

    delta = jnp.sum(
        (grad_all.astype(wide) * mixed_wide)[:, : LOCAL * HEAD].reshape(rows, LOCAL, HEAD), axis=2
    )

    def as_stat(values):
        return jnp.transpose(values.reshape(tiles, tile, LOCAL), (0, 2, 1))

    def same_stat(values):
        return jnp.broadcast_to(
            values.astype(wide).reshape(tiles, 1, tile), (tiles, LOCAL, tile)
        )

    stats = jnp.stack(
        [same_stat(first), same_stat(last), as_stat(lse[:, :LOCAL]), as_stat(delta)], axis=2
    )
    stats = jnp.pad(stats, ((0, 0), (0, 0), (0, 4), (0, 0)))
    query_grad, dkv = attend_backward(queries, kv_all, grad_all, stats, bounds, tile, block)

    def slabs(grad, extras):
        grad = grad.astype(low_type).reshape(devices, s, -1)
        rest = -s % 8
        rest += 0 if rest >= extras.shape[0] else 8
        extras = jnp.concatenate(
            [extras.astype(low_type), jnp.zeros((rest - extras.shape[0], extras.shape[1]), low_type)]
        )
        extras = jnp.broadcast_to(extras[None], (devices,) + extras.shape)
        return jnp.concatenate([grad, extras], axis=1).reshape(2, 2, zs, GROUPS, 2, s + rest, -1)

    mix_extras = jnp.stack(
        [
            mix_bias_grad, early_grads[1], early_grads[2],
            outer_bias_grad, final_grads[1], final_grads[2],
        ]
    )
    dkv, out1, out2, outm = reduce_keys(
        zs,
        dkv.reshape(2, 2, zs, GROUPS, 2, n, WIDE),
        slabs(grad1, inner_bias_grad[None]),
        grad2.astype(low_type).reshape(zs, GROUPS, 2, e, depth),
        slabs(gradm, mix_extras),
    )
    key_grad = jnp.sum(dkv.astype(wide), axis=0).astype(low_type).reshape(rows, WIDE)
    grads = jnp.concatenate([key_grad, query_grad], axis=1)
    gradq = jnp.einsum("tc,td->cd", tok_all, grads, preferred_element_type=wide)
    bias_grad = jnp.sum(grads.astype(wide), axis=0)
    partial = jnp.einsum("td,cd->tc", grads, w_qkv, preferred_element_type=wide).astype(low_type)
    partial, outq = reduce_tokens(
        zs, partial.reshape(GROUPS, n, depth), slabs(gradq, bias_grad[None])
    )
    input_grad = early_grads[0] + jnp.sum(partial.astype(wide), axis=0)

    def own(vector, count):
        return lax.dynamic_slice_in_dim(vector, device * count, count, 0).astype(wide)

    outq = outq.astype(wide)
    kv_out = outq[:, :, :WIDE].reshape(GROUPS, -1, LOCAL, 2, HEAD)
    q_out = outq[:, :, WIDE:].reshape(GROUPS, -1, LOCAL, 2, HEAD)[:, :, :, 0]

    def unpacked(values):
        return jnp.transpose(values, (1, 0, 2, 3)).reshape(-1, depth)

    q_out, k_out, v_out = unpacked(q_out), unpacked(kv_out[:, :, :, 0]), unpacked(kv_out[:, :, :, 1])
    inner_out = jnp.transpose(out1[:, :s], (1, 0, 2)).reshape(s, ff).astype(wide)
    return (
        output,
        input_grad.astype(low_type),
        q_out[:s],
        own(q_out[s], s),
        k_out[:s],
        v_out[:s],
        own(v_out[s], s),
        outm[:s],
        own(outm[s], s),
        own(outm[s + 1], s),
        own(outm[s + 2], s),
        inner_out,
        own(out1[:, s].reshape(ff), e),
        out2,
        own(outm[s + 3], s),
        own(outm[s + 4], s),
        own(outm[s + 5], s),
    )


def solution(mesh):
    both = P(("au", "row"), None)
    flat = P(("au", "row"))
    in_specs = (
        both, both, P(), both, flat, both, both, flat, both, flat, flat, flat,
        both, flat, both, flat, flat, flat,
    )
    out_specs = (
        both, both, both, flat, both, both, flat, both, flat, flat, flat,
        both, flat, both, flat, flat, flat,
    )
    return jax.shard_map(
        on_device, mesh=mesh, in_specs=in_specs, out_specs=out_specs, check_vma=False
    )
```

```python
import functools

import jax
import jax.numpy as jnp
import numpy as np
from jax import lax
from jax.experimental import pallas as pl
from jax.experimental.pallas import tpu as pltpu
from jax.sharding import PartitionSpec as P

HEAD = 64
HEADS = 12
GROUPS = 4
LOCAL = HEADS // GROUPS
LANES = 2 * HEAD
WIDE = LOCAL * LANES
PACK = 256
eps_norm = 1e-06
mask_fill = -1000000000.0
lowest_start = -1e30
low_type = jnp.bfloat16
wide = jnp.float32
MESH = pl.DeviceIdType.MESH
VMEM_LIMIT = 62 * 1024 * 1024


def layer_norm(hidden, gain, shift):
    mean = jnp.mean(hidden, axis=-1, keepdims=True)
    centered = hidden - mean
    spread = jnp.mean(centered * centered, axis=-1, keepdims=True)
    return centered * lax.rsqrt(spread + eps_norm) * gain + shift


def gelu_exact(values):
    return jax.nn.gelu(values, approximate=False)


class Place:
    def __init__(self, zs):
        self.zs = zs
        a = lax.axis_index("au")
        r = lax.axis_index("row")
        self.x, self.c = a // 2, a % 2
        self.y, q = r % 2, r // 2
        self.g, self.z = q % GROUPS, q // GROUPS

    def at(self, x=None, c=None, z=None, g=None, y=None):
        x = self.x if x is None else x
        c = self.c if c is None else c
        z = self.z if z is None else z
        g = self.g if g is None else g
        y = self.y if y is None else y
        return (x * 2 + c, (z * GROUPS + g) * 2 + y)

    def sibling(self):
        return self.at(c=1 - self.c)

    def line(self):
        return [((self.g + k) % GROUPS, (self.g + GROUPS - k) % GROUPS) for k in range(1, GROUPS)]

    def column(self):
        count = self.zs * GROUPS
        q = self.z * GROUPS + self.g
        result = []
        for k in range(1, count):
            to, source = (q + k) % count, (q + count - k) % count
            result.append(((to // GROUPS, to % GROUPS), (source // GROUPS, source % GROUPS)))
        return result

    def plane(self, everywhere=True):
        result = []
        for dx in range(2):
            for dy in range(2):
                for dz in range(self.zs if everywhere else 1):
                    if dx + dy + dz == 0:
                        continue
                    to = ((self.x + dx) % 2, (self.z + dz) % self.zs, (self.y + dy) % 2)
                    source = (
                        (self.x + dx) % 2,
                        (self.z + self.zs - dz) % self.zs,
                        (self.y + dy) % 2,
                    )
                    result.append((to, source))
        return result


class Copies:
    def __init__(self, send, recv, local):
        self.send, self.recv, self.local = send, recv, local
        self.count = 0
        self.local_count = 0
        self.started = []
        self.local_started = []

    def push(self, source, target, device):
        copy = pltpu.make_async_remote_copy(
            src_ref=source,
            dst_ref=target,
            send_sem=self.send.at[self.count],
            recv_sem=self.recv.at[self.count],
            device_id=device,
            device_id_type=MESH,
        )
        self.count += 1
        copy.start()
        self.started.append(copy)
        return copy

    def keep(self, source, target):
        copy = pltpu.make_async_copy(source, target, self.local.at[self.local_count])
        self.local_count += 1
        copy.start()
        return copy

    def finish(self):
        for copy in self.started:
            copy.wait_send()


def greet(devices, partner=None, crossing=None):
    barrier = pltpu.get_barrier_semaphore()
    for device in devices:
        pl.semaphore_signal(barrier, inc=1, device_id=device, device_id_type=MESH)
    if partner is None:
        pl.semaphore_wait(barrier, len(devices))
        return

    @pl.when(crossing)
    def _():
        pl.semaphore_signal(barrier, inc=1, device_id=partner, device_id_type=MESH)
        pl.semaphore_wait(barrier, len(devices) + 1)

    @pl.when(jnp.logical_not(crossing))
    def _():
        pl.semaphore_wait(barrier, len(devices))


def comm_call(body, name, ident, outs, copies, locals_, args, spaces=None, out_spaces=None, scratch=()):
    spaces = [pl.ANY] * len(args) if spaces is None else spaces
    out_spaces = [pl.ANY] * len(outs) if out_spaces is None else out_spaces
    return pl.pallas_call(
        body,
        name=name,
        out_shape=tuple(outs),
        in_specs=[pl.BlockSpec(memory_space=space) for space in spaces],
        out_specs=tuple(pl.BlockSpec(memory_space=space) for space in out_spaces),
        scratch_shapes=[
            pltpu.SemaphoreType.DMA((max(copies, 1),)),
            pltpu.SemaphoreType.DMA((max(copies, 1),)),
            pltpu.SemaphoreType.DMA((max(locals_, 1),)),
            *scratch,
        ],
        compiler_params=pltpu.CompilerParams(
            collective_id=ident, has_side_effects=True, vmem_limit_bytes=VMEM_LIMIT
        ),
    )(*args)


def spread_tokens(zs, tokens, slab):
    n, width = tokens.shape
    groups, rows, columns = slab.shape
    plane = 4 * zs - 1

    def body(tok, piece, tok_all, w_all, send, recv, local):
        me = Place(zs)
        copies = Copies(send, recv, local)
        greet(
            [me.at(g=to) for to, _ in me.line()]
            + [me.at(x=to[0], z=to[1], y=to[2]) for to, _ in me.plane()]
            + [me.sibling()]
        )
        first = [
            copies.push(
                piece.at[to], w_all.at[me.x, me.c, me.z, me.g, me.y], me.at(g=to)
            )
            for to, _ in me.line()
        ]
        own = copies.keep(piece.at[me.g], w_all.at[me.x, me.c, me.z, me.g, me.y])
        arrivals = [copies.push(tok, tok_all.at[me.g], me.at(g=to)) for to, _ in me.line()]
        mine = copies.keep(tok, tok_all.at[me.g])
        own.wait()
        for copy in first:
            copy.wait_recv()
        block = w_all.at[me.x, me.c, me.z, :, me.y]
        second = [
            copies.push(block, block, me.at(x=to[0], z=to[1], y=to[2])) for to, _ in me.plane()
        ]
        arrivals.append(copies.push(block, block, me.sibling()))
        for copy, (_, source) in zip(second, me.plane()):
            copy.wait_recv()
            part = w_all.at[source[0], me.c, source[1], :, source[2]]
            arrivals.append(copies.push(part, part, me.sibling()))
        for copy in arrivals:
            copy.wait_recv()
        mine.wait()
        copies.finish()

    return comm_call(
        body,
        "spread_tokens",
        0,
        [
            jax.ShapeDtypeStruct((GROUPS, n, width), low_type),
            jax.ShapeDtypeStruct((2, 2, zs, GROUPS, 2, rows, columns), low_type),
        ],
        2 * (GROUPS - 1) + 2 * plane + 1,
        2,
        (tokens, slab),
    )


def spread_keys(zs, keys, inner, outer, mix):
    groups, n, width = keys.shape
    quarters, rows, columns = inner.shape
    tall, _ = outer.shape
    plane, column = 4 * zs - 1, GROUPS * zs - 1

    def body(kv, w1s, w2s, wms, kv_all, w1, w2, wm, send, recv, local, swap_send, swap_recv):
        me = Place(zs)
        copies = Copies(send, recv, local)
        crossing = me.c != me.y
        greet(
            [me.at(x=to[0], z=to[1], y=to[2]) for to, _ in me.plane()]
            + [me.at(z=to[0], g=to[1]) for to, _ in me.column()]
            + [me.at(z=to[0], g=to[1], c=me.y, y=me.c) for to, _ in me.column()]
            + [me.sibling()],
            me.at(c=me.y, y=me.c),
            crossing,
        )

        def here(ref):
            return ref.at[me.x, me.c, me.z, me.g, me.y]

        flat = me.plane(everywhere=False)
        own = [
            copies.keep(w1s.at[me.x * 2 + me.y], here(w1)),
            copies.keep(wms, here(wm)),
            copies.keep(kv, kv_all.at[me.x, me.c, me.z, :, me.y]),
        ]
        w1_first = [
            copies.push(w1s.at[to[0] * 2 + to[2]], here(w1), me.at(x=to[0], y=to[2]))
            for to, _ in flat
        ]
        wm_first = [
            copies.push(wms, here(wm), me.at(z=to[0], g=to[1])) for to, _ in me.column()
        ]
        mine = kv_all.at[me.x, me.c, me.z, :, me.y]
        kv_first = [
            copies.push(kv, mine, me.at(x=to[0], z=to[1], y=to[2])) for to, _ in me.plane()
        ]
        arrivals = [copies.push(kv, mine, me.sibling())]
        w2_first = [
            copies.push(
                w2s, w2.at[me.z, me.g, me.y], me.at(z=to[0], g=to[1], c=me.y, y=me.c)
            )
            for to, _ in me.column()
        ]
        exchanged = pltpu.make_async_remote_copy(
            src_ref=w2s,
            dst_ref=w2.at[me.z, me.g, me.y],
            send_sem=swap_send,
            recv_sem=swap_recv,
            device_id=me.at(c=me.y, y=me.c),
            device_id_type=MESH,
        )
        stays = pltpu.make_async_copy(w2s, w2.at[me.z, me.g, me.y], swap_recv)

        @pl.when(crossing)
        def _():
            exchanged.start()

        @pl.when(jnp.logical_not(crossing))
        def _():
            stays.start()

        own[0].wait()
        for copy in w1_first:
            copy.wait_recv()
        block = w1.at[:, me.c, me.z, me.g, :]
        w1_second = [
            copies.push(block, block, me.at(z=to[0], g=to[1])) for to, _ in me.column()
        ]
        arrivals.append(copies.push(block, block, me.sibling()))
        own[1].wait()
        for copy in wm_first:
            copy.wait_recv()
        block = wm.at[me.x, me.c, :, :, me.y]
        wm_second = [copies.push(block, block, me.at(x=to[0], y=to[2])) for to, _ in flat]
        arrivals.append(copies.push(block, block, me.sibling()))
        for copy, (_, source) in zip(kv_first, me.plane()):
            copy.wait_recv()
            part = kv_all.at[source[0], me.c, source[1], :, source[2]]
            arrivals.append(copies.push(part, part, me.sibling()))

        @pl.when(crossing)
        def _():
            exchanged.wait_recv()
            exchanged.wait_send()

        @pl.when(jnp.logical_not(crossing))
        def _():
            stays.wait()

        part = w2.at[me.z, me.g, me.c]
        arrivals.append(copies.push(part, part, me.sibling()))
        for copy, (_, source) in zip(wm_second, flat):
            copy.wait_recv()
            part = wm.at[source[0], me.c, :, :, source[2]]
            arrivals.append(copies.push(part, part, me.sibling()))
        for copy, (_, source) in zip(w2_first, me.column()):
            copy.wait_recv()
            part = w2.at[source[0], source[1], me.c]
            arrivals.append(copies.push(part, part, me.sibling()))
        for copy, (_, source) in zip(w1_second, me.column()):
            copy.wait_recv()
            part = w1.at[:, me.c, source[0], source[1], :]
            arrivals.append(copies.push(part, part, me.sibling()))
        for copy in arrivals:
            copy.wait_recv()
        own[2].wait()
        copies.finish()

    return comm_call(
        body,
        "spread_keys",
        1,
        [
            jax.ShapeDtypeStruct((2, 2, zs, GROUPS, 2, n, width), low_type),
            jax.ShapeDtypeStruct((2, 2, zs, GROUPS, 2, rows, columns), low_type),
            jax.ShapeDtypeStruct((zs, GROUPS, 2, tall, columns), low_type),
            jax.ShapeDtypeStruct((2, 2, zs, GROUPS, 2) + mix.shape, low_type),
        ],
        2 * plane + 1 + 2 * (3 + column + 1 + column) + column + 3 + 8,
        3,
        (keys, inner, outer, mix),
        scratch=(pltpu.SemaphoreType.DMA, pltpu.SemaphoreType.DMA),
    )


def exchange_line(zs, ident, pieces):
    def body(source, target, send, recv, local):
        me = Place(zs)
        copies = Copies(send, recv, local)
        greet([me.at(g=to) for to, _ in me.line()])
        arrivals = [
            copies.push(source.at[to], target.at[me.g], me.at(g=to)) for to, _ in me.line()
        ]
        own = copies.keep(source.at[me.g], target.at[me.g])
        for copy in arrivals:
            copy.wait_recv()
        own.wait()
        copies.finish()

    return comm_call(
        body,
        "exchange_line",
        ident,
        [jax.ShapeDtypeStruct(pieces.shape, pieces.dtype)],
        GROUPS - 1,
        1,
        (pieces,),
    )[0]


def gather_square(zs, ident, rows):
    def body(source, target, send, recv, local):
        me = Place(zs)
        copies = Copies(send, recv, local)
        flat = me.plane(everywhere=False)
        greet([me.at(x=to[0], y=to[2]) for to, _ in flat])
        place = target.at[me.x, me.y]
        arrivals = [copies.push(source, place, me.at(x=to[0], y=to[2])) for to, _ in flat]
        own = copies.keep(source, place)
        for copy in arrivals:
            copy.wait_recv()
        own.wait()
        copies.finish()

    return comm_call(
        body,
        "gather_square",
        ident,
        [jax.ShapeDtypeStruct((2, 2) + rows.shape, rows.dtype)],
        3,
        1,
        (rows,),
    )[0]


def exchange_square(zs, ident, pieces):
    def body(source, target, send, recv, local):
        me = Place(zs)
        copies = Copies(send, recv, local)
        flat = me.plane(everywhere=False)
        greet([me.at(x=to[0], y=to[2]) for to, _ in flat])
        place = target.at[me.x, me.y]
        arrivals = [
            copies.push(source.at[to[0], to[2]], place, me.at(x=to[0], y=to[2]))
            for to, _ in flat
        ]
        own = copies.keep(source.at[me.x, me.y], place)
        for copy in arrivals:
            copy.wait_recv()
        own.wait()
        copies.finish()

    return comm_call(
        body,
        "exchange_square",
        ident,
        [jax.ShapeDtypeStruct(pieces.shape, pieces.dtype)],
        3,
        1,
        (pieces,),
    )[0]


def loop(count, step):
    def body(index, carry):
        step(index)
        return carry

    lax.fori_loop(0, count, body, 0)


def total_of(*values):
    result = values[0].astype(wide)
    for value in values[1:]:
        result = result + value.astype(wide)
    return result


def reduce_keys(zs, dkv, grad1, grad2, gradm):
    n, width = dkv.shape[-2:]
    rows, columns = grad1.shape[-2:]
    rowsm = gradm.shape[-2]
    tall = grad2.shape[-2]
    plane, column = 4 * zs - 1, GROUPS * zs - 1
    count = GROUPS * zs

    def body(
        dkv_ref, g1, g2, gm, dkv_out, out1, out2, outm,
        send, recv, local,
        swap_send, swap_recv, kst, s1, p1, f1, s2, p2, sm, pm, fm, tm,
    ):
        me = Place(zs)
        copies = Copies(send, recv, local)
        crossing = me.c != me.y
        greet(
            [me.at(x=to[0], z=to[1], y=to[2]) for to, _ in me.plane()]
            + [me.at(z=to[0], g=to[1]) for to, _ in me.column()]
            + [me.at(z=to[0], g=to[1], c=me.y, y=me.c) for to, _ in me.column()]
            + [me.sibling()],
            me.at(c=me.y, y=me.c),
            crossing,
        )

        flat = me.plane(everywhere=False)
        other = 1 - me.c
        order = [to for to, _ in me.plane()] + [(me.x, me.z, me.y)]
        w1_half = copies.push(g1.at[:, other], s1, me.sibling())
        w2_half = copies.push(g2.at[:, :, other], s2, me.sibling())
        k_half = [
            copies.push(
                dkv_ref.at[to[0], other, to[1], :, to[2]], kst.at[to[0], to[1], to[2]], me.sibling()
            )
            for to in order
        ]
        wm_half = copies.push(gm.at[:, other], sm, me.sibling())

        w1_half.wait_recv()

        def add1(index):
            x, z, g, y = index // (count * 2), index // (GROUPS * 2) % zs, index // 2 % GROUPS, index % 2
            s1[x, z, g, y] = total_of(s1[x, z, g, y], g1[x, me.c, z, g, y]).astype(low_type)

        loop(4 * count, add1)
        w1_push = [
            copies.push(s1.at[:, to[0], to[1], :], p1.at[slot], me.at(z=to[0], g=to[1]))
            for slot, (to, _) in enumerate(me.column())
        ]
        w2_half.wait_recv()

        def add2(index):
            z, g = index // GROUPS, index % GROUPS
            s2[z, g] = total_of(s2[z, g], g2[z, g, me.c]).astype(low_type)

        loop(count, add2)
        w2_push = [
            copies.push(
                s2.at[to[0], to[1]], p2.at[slot + 1], me.at(z=to[0], g=to[1], c=me.y, y=me.c)
            )
            for slot, (to, _) in enumerate(me.column())
        ]
        exchanged = pltpu.make_async_remote_copy(
            src_ref=s2.at[me.z, me.g],
            dst_ref=p2.at[0],
            send_sem=swap_send,
            recv_sem=swap_recv,
            device_id=me.at(c=me.y, y=me.c),
            device_id_type=MESH,
        )
        stays = pltpu.make_async_copy(s2.at[me.z, me.g], p2.at[0], swap_recv)

        @pl.when(crossing)
        def _():
            exchanged.start()

        @pl.when(jnp.logical_not(crossing))
        def _():
            stays.start()

        k_push = []
        for slot, to in enumerate(order):
            k_half[slot].wait_recv()

            def addk(g, to=to):
                kst[to[0], to[1], to[2], g] = total_of(
                    kst[to[0], to[1], to[2], g], dkv_ref[to[0], me.c, to[1], g, to[2]]
                ).astype(low_type)

            loop(GROUPS, addk)
            if slot < plane:
                k_push.append(
                    copies.push(
                        kst.at[to[0], to[1], to[2]],
                        dkv_out.at[slot],
                        me.at(x=to[0], z=to[1], y=to[2]),
                    )
                )
        wm_half.wait_recv()

        def addm(index):
            x, z, g, y = index // (count * 2), index // (GROUPS * 2) % zs, index // 2 % GROUPS, index % 2
            sm[x, z, g, y] = total_of(sm[x, z, g, y], gm[x, me.c, z, g, y]).astype(low_type)

        loop(4 * count, addm)
        wm_push = [
            copies.push(sm.at[to[0], :, :, to[2]], pm.at[slot], me.at(x=to[0], y=to[2]))
            for slot, (to, _) in enumerate(flat)
        ]
        keep = copies.keep(kst.at[me.x, me.z, me.y], dkv_out.at[plane])
        for copy in wm_push:
            copy.wait_recv()

        def addf(index):
            z, g = index // GROUPS, index % GROUPS
            fm[z, g] = total_of(sm[me.x, z, g, me.y], pm[0, z, g], pm[1, z, g], pm[2, z, g]).astype(
                low_type
            )

        loop(count, addf)
        wm_last = [
            copies.push(fm.at[to[0], to[1]], tm.at[slot], me.at(z=to[0], g=to[1]))
            for slot, (to, _) in enumerate(me.column())
        ]
        for copy in w1_push:
            copy.wait_recv()

        def addg(index):
            x, y = index // 2, index % 2
            f1[x, y] = total_of(
                s1[x, me.z, me.g, y], *[p1[slot, x, y] for slot in range(column)]
            ).astype(low_type)

        loop(4, addg)
        quarter = out1.at[me.x * 2 + me.y]
        w1_last = [
            copies.push(f1.at[to[0], to[2]], quarter, me.at(x=to[0], y=to[2])) for to, _ in flat
        ]
        keep1 = copies.keep(f1.at[me.x, me.y], quarter)

        @pl.when(crossing)
        def _():
            exchanged.wait_recv()
            exchanged.wait_send()

        @pl.when(jnp.logical_not(crossing))
        def _():
            stays.wait()

        for copy in w2_push:
            copy.wait_recv()
        out2[...] = total_of(*[p2[slot] for slot in range(column + 1)])
        for copy in wm_last:
            copy.wait_recv()
        outm[...] = total_of(fm[me.z, me.g], *[tm[slot] for slot in range(column)])
        for copy in w1_last + k_push:
            copy.wait_recv()
        keep.wait()
        keep1.wait()
        copies.finish()

    vmem = pltpu.VMEM
    return comm_call(
        body,
        "reduce_keys",
        8,
        [
            jax.ShapeDtypeStruct((plane + 1, GROUPS, n, width), low_type),
            jax.ShapeDtypeStruct((4, rows, columns), low_type),
            jax.ShapeDtypeStruct((tall, columns), wide),
            jax.ShapeDtypeStruct((rowsm, columns), wide),
        ],
        3 + (plane + 1) + 2 * column + plane + 3 + column + 3,
        2,
        (dkv, grad1, grad2, gradm),
        spaces=[vmem] * 4,
        out_spaces=[pl.ANY, pl.ANY, vmem, vmem],
        scratch=(
            pltpu.SemaphoreType.DMA,
            pltpu.SemaphoreType.DMA,
            vmem((2, zs, 2, GROUPS, n, width), low_type),
            vmem((2, zs, GROUPS, 2, rows, columns), low_type),
            vmem((column, 2, 2, rows, columns), low_type),
            vmem((2, 2, rows, columns), low_type),
            vmem((zs, GROUPS, tall, columns), low_type),
            vmem((column + 1, tall, columns), low_type),
            vmem((2, zs, GROUPS, 2, rowsm, columns), low_type),
            vmem((3, zs, GROUPS, rowsm, columns), low_type),
            vmem((zs, GROUPS, rowsm, columns), low_type),
            vmem((column, rowsm, columns), low_type),
        ),
    )


def reduce_tokens(zs, dx, gradq):
    rows, columns = gradq.shape[-2:]
    plane = 4 * zs - 1
    count = GROUPS * zs

    def body(dx_ref, gq, dx_out, outq, send, recv, local, sq, pq, fq):
        me = Place(zs)
        copies = Copies(send, recv, local)
        greet(
            [me.at(g=to) for to, _ in me.line()]
            + [me.at(x=to[0], z=to[1], y=to[2]) for to, _ in me.plane()]
            + [me.sibling()]
        )
        half = copies.push(gq.at[:, 1 - me.c], sq, me.sibling())
        arrivals = [
            copies.push(dx_ref.at[to], dx_out.at[me.g], me.at(g=to)) for to, _ in me.line()
        ]
        own = copies.keep(dx_ref.at[me.g], dx_out.at[me.g])
        half.wait_recv()

        def add1(index):
            x, z, g, y = index // (count * 2), index // (GROUPS * 2) % zs, index // 2 % GROUPS, index % 2
            sq[x, z, g, y] = total_of(sq[x, z, g, y], gq[x, me.c, z, g, y]).astype(low_type)

        loop(4 * count, add1)
        second = [
            copies.push(
                sq.at[to[0], to[1], :, to[2]], pq.at[slot], me.at(x=to[0], z=to[1], y=to[2])
            )
            for slot, (to, _) in enumerate(me.plane())
        ]
        for copy in second:
            copy.wait_recv()

        def add2(g):
            fq[g] = total_of(
                sq[me.x, me.z, g, me.y], *[pq[slot, g] for slot in range(plane)]
            ).astype(low_type)

        loop(GROUPS, add2)
        arrivals += [
            copies.push(fq.at[to], outq.at[me.g], me.at(g=to)) for to, _ in me.line()
        ]
        keep = copies.keep(fq.at[me.g], outq.at[me.g])
        for copy in arrivals:
            copy.wait_recv()
        own.wait()
        keep.wait()
        copies.finish()

    vmem = pltpu.VMEM
    return comm_call(
        body,
        "reduce_tokens",
        9,
        [
            jax.ShapeDtypeStruct(dx.shape, low_type),
            jax.ShapeDtypeStruct((GROUPS, rows, columns), low_type),
        ],
        1 + 2 * (GROUPS - 1) + plane,
        2,
        (dx, gradq),
        spaces=[pl.ANY, vmem],
        scratch=(
            vmem((2, zs, GROUPS, 2, rows, columns), low_type),
            vmem((plane, GROUPS, rows, columns), low_type),
            vmem((GROUPS, rows, columns), low_type),
        ),
    )


NEXT = (((1,), (1,)), ((), ()))
DOWN = (((0,), (0,)), ((), ()))


def attend_forward(queries, keys, bounds, low, high, tile, block):
    total_rows = queries.shape[0]

    def body(bounds_ref, q_ref, kv_ref, low_ref, high_ref, out_ref, keep_ref, lse_ref):
        def one(turn, unused):
            rows = pl.ds(pl.multiple_of(turn * tile, tile), tile)
            first, last = low_ref[rows, :], high_ref[rows, :]
            heads = [
                q_ref[rows, h * LANES : (h + 1) * LANES] * jnp.asarray(0.125, low_type)
                for h in range(LOCAL)
            ]

            def step(j, carry):
                begin = pl.multiple_of(j * block, block)
                place = begin + lax.broadcasted_iota(jnp.int32, (tile, block), 1)
                same = (place >= first) & (place < last)
                result = []
                for h in range(LOCAL):
                    top, total, mixed = carry[h]
                    kv = kv_ref[pl.ds(begin, block), h * LANES : (h + 1) * LANES]
                    scores = lax.dot_general(heads[h], kv, NEXT, preferred_element_type=wide)
                    scores = jnp.where(same, scores, mask_fill)
                    new_top = jnp.maximum(top, jnp.max(scores, axis=1, keepdims=True))
                    factor = jnp.exp(top - new_top)
                    powers = jnp.exp(scores - new_top)
                    total = total * factor + jnp.sum(powers, axis=1, keepdims=True)
                    mixed = mixed * factor + jnp.dot(
                        powers.astype(low_type), kv, preferred_element_type=wide
                    )
                    result.append((new_top, total, mixed))
                return tuple(result)

            start = tuple(
                (
                    jnp.full((tile, 1), lowest_start, wide),
                    jnp.zeros((tile, 1), wide),
                    jnp.zeros((tile, LANES), wide),
                )
                for _ in range(LOCAL)
            )
            done = lax.fori_loop(bounds_ref[turn, 0], bounds_ref[turn, 1], step, start)
            lane = lax.broadcasted_iota(jnp.int32, (tile, LANES), 1)
            upper = lane >= HEAD
            mixes = [mixed / total for _, total, mixed in done]
            turned = [pltpu.roll(mixed, HEAD, 1) for mixed in mixes]
            front = jnp.where(upper, mixes[1], turned[0])
            back = jnp.where(upper, 0.0, turned[2])
            both = jnp.concatenate([front, back], axis=1)
            keep_ref[rows, :] = both
            out_ref[rows, :] = both.astype(low_type)
            ends = [top + jnp.log(total) for top, total, _ in done]
            lse_ref[rows, :] = jnp.where(lane == 0, ends[0], jnp.where(lane == 1, ends[1], ends[2]))
            return unused

        lax.fori_loop(0, total_rows // tile, one, 0)

    vmem = pl.BlockSpec(memory_space=pltpu.VMEM)
    return pl.pallas_call(
        body,
        name="attend_forward",
        out_shape=(
            jax.ShapeDtypeStruct((total_rows, PACK), low_type),
            jax.ShapeDtypeStruct((total_rows, PACK), wide),
            jax.ShapeDtypeStruct((total_rows, LANES), wide),
        ),
        in_specs=[pl.BlockSpec(memory_space=pltpu.SMEM)] + [vmem] * 4,
        out_specs=(vmem,) * 3,
        compiler_params=pltpu.CompilerParams(vmem_limit_bytes=VMEM_LIMIT),
    )(bounds, queries, keys, low, high)


def attend_backward(queries, keys, grads, stats, bounds, tile, block):
    total_rows = queries.shape[0]
    tokens = keys.shape[0]

    def body(bounds_ref, q_ref, kv_ref, do_ref, stat_ref, dq_ref, dkv_ref, sums):
        h = pl.program_id(0)
        zeros = jnp.zeros((block, LANES), wide)

        def clear(j, unused):
            sums[pl.ds(pl.multiple_of(j * block, block), block), :] = zeros
            return unused

        lax.fori_loop(0, tokens // block, clear, 0)
        lane = lax.broadcasted_iota(jnp.int32, (tile, LANES), 1)
        upper = lane >= HEAD

        def one(turn, unused):
            rows = pl.ds(pl.multiple_of(turn * tile, tile), tile)
            q = q_ref[rows, :] * jnp.asarray(0.125, low_type)
            front = do_ref[rows, :LANES].astype(wide)
            back = do_ref[rows, LANES:].astype(wide)
            grad = jnp.where(h == 1, front, pltpu.roll(jnp.where(h == 0, front, back), HEAD, 1))
            grad = jnp.where(upper, grad, 0.0).astype(low_type)
            stat = stat_ref[turn, 0]
            first, last = stat[0:1, :], stat[1:2, :]
            lse, delta = stat[2:3, :], stat[3:4, :]

            def step(j, total):
                begin = pl.multiple_of(j * block, block)
                place = (begin + lax.broadcasted_iota(jnp.int32, (block, tile), 0)).astype(wide)
                same = (place >= first) & (place < last)
                kv = kv_ref[pl.ds(begin, block), :]
                scores = lax.dot_general(kv, q, NEXT, preferred_element_type=wide)
                probs = jnp.exp(jnp.where(same, scores, mask_fill) - lse)
                dots = lax.dot_general(kv, grad, NEXT, preferred_element_type=wide)
                score_grad = (probs * (dots - delta)).astype(low_type)
                sums[pl.ds(begin, block), :] += jnp.dot(
                    score_grad, q, preferred_element_type=wide
                ) + jnp.dot(probs.astype(low_type), grad, preferred_element_type=wide)
                return total + lax.dot_general(score_grad, kv, DOWN, preferred_element_type=wide)

            total = lax.fori_loop(
                bounds_ref[turn, 0], bounds_ref[turn, 1], step, jnp.zeros((tile, LANES), wide)
            )
            dq_ref[rows, :] = jnp.where(upper, 0.0, total * 0.125).astype(low_type)
            return unused

        lax.fori_loop(0, total_rows // tile, one, 0)

        def store(j, unused):
            part = pl.ds(pl.multiple_of(j * block, block), block)
            dkv_ref[part, :] = sums[part, :].astype(low_type)
            return unused

        lax.fori_loop(0, tokens // block, store, 0)

    return pl.pallas_call(
        body,
        name="attend_backward",
        grid=(LOCAL,),
        out_shape=(
            jax.ShapeDtypeStruct((total_rows, WIDE), low_type),
            jax.ShapeDtypeStruct((tokens, WIDE), low_type),
        ),
        in_specs=[
            pl.BlockSpec(memory_space=pltpu.SMEM),
            pl.BlockSpec((total_rows, LANES), lambda h: (0, h)),
            pl.BlockSpec((tokens, LANES), lambda h: (0, h)),
            pl.BlockSpec((total_rows, PACK), lambda h: (0, 0)),
            pl.BlockSpec((total_rows // tile, 1, 8, tile), lambda h: (0, h, 0, 0)),
        ],
        out_specs=(
            pl.BlockSpec((total_rows, LANES), lambda h: (0, h)),
            pl.BlockSpec((tokens, LANES), lambda h: (0, h)),
        ),
        scratch_shapes=[pltpu.VMEM((tokens, LANES), wide)],
        compiler_params=pltpu.CompilerParams(vmem_limit_bytes=VMEM_LIMIT),
    )(bounds, queries, keys, grads, stats)


class Spot(Place):
    def __init__(self):
        super().__init__(1)
        self.half = self.g // 2
        self.a = self.x * 2 + self.c
        self.p = (self.x + self.c) % 2
        self.selfish = self.g % 2 == self.p
        self.crossing = self.c != self.y

    def square(self):
        return [(to[0], to[2]) for to, _ in self.plane()]

    def readers(self):
        result = []
        for k in range(GROUPS):
            g = (self.g + k) % GROUPS
            result.append((g, self.at(x=(self.g + self.c) % 2, g=g)))
        return result

    def owners(self):
        result = []
        for du in range(2):
            for dv in range(2):
                u, v = (self.x + du) % 2, (self.half + dv) % 2
                result.append((u * 2 + v, self.at(x=u, g=2 * v + self.p)))
        return result

    def slot(self):
        return self.x * 2 + self.half


def count_of(flag):
    return jnp.where(flag, 1, 0)


def announce(always, maybe):
    barrier = pltpu.get_barrier_semaphore()
    for device in always:
        pl.semaphore_signal(barrier, inc=1, device_id=device, device_id_type=MESH)
    for flag, device in maybe:

        @pl.when(flag)
        def _(device=device):
            pl.semaphore_signal(barrier, inc=1, device_id=device, device_id_type=MESH)

    total = len(always)
    for flag, _ in maybe:
        total = total + count_of(flag)
    return barrier, total


class Scatter:
    def __init__(self, send, recv, here):
        self.send, self.recv, self.here = send, recv, here
        self.copies = []

    def start(self, pieces, target, slot):
        for index, (source, device) in enumerate(pieces):
            copy = pltpu.make_async_remote_copy(
                src_ref=source,
                dst_ref=target,
                send_sem=self.send.at[index],
                recv_sem=self.recv.at[slot],
                device_id=device,
                device_id_type=MESH,
            )
            self.copies.append(copy)
            if index:
                copy.start()
                continue
            stay = pltpu.make_async_copy(source, target, self.recv.at[slot])

            @pl.when(self.here)
            def _(stay=stay):
                stay.start()

            @pl.when(jnp.logical_not(self.here))
            def _(copy=copy):
                copy.start()

    def arrived(self, slot, target):
        pltpu.make_async_copy(target, target, self.recv.at[slot]).wait()

    def finish(self):
        for copy in self.copies[1:]:
            copy.wait_send()

        @pl.when(jnp.logical_not(self.here))
        def _():
            self.copies[0].wait_send()


SMALL = 16


def first_tables(s, e, width):
    column = np.arange(width)
    rows = [column % s, column // s, column % e, column // e]
    return np.stack(rows + [np.zeros_like(column)] * 4).astype(np.int32)


def first_kernel(tokens, wq, wk, wv, vectors, inner, outer, mix):
    n, depth = tokens.shape
    s, e = wq.shape[0], outer.shape[0]
    quarter = inner.shape[1] // 4
    cols = 2 * WIDE + LANES
    tables = jnp.asarray(first_tables(s, e, 2 * WIDE))
    count = len(vectors)

    def body(*refs):
        tok, wq_ref, wk_ref, wv_ref, tab = refs[:5]
        vecs = refs[5 : 5 + count]
        w1f, w2f, wmf = refs[5 + count : 8 + count]
        (
            tok_out, q_out, wqkv_out, vec_out, kv_all, w1, w2, wm,
            send, recv, local, tok_send, tok_recv, swap_send, swap_recv,
            slab, toks, weights, kv_own, q_own, w1s, w2s, wms, vec, few,
        ) = refs[8 + count :]
        me = Spot()
        copies = Copies(send, recv, local)
        square = me.square()
        line = [to for to, _ in me.line()]
        sources = [device for _, device in me.owners()]
        swapped = [me.at(g=to, c=me.y, y=me.c) for to in [me.g] + line]
        barrier, expected = announce(
            [me.at(x=x, y=y) for x, y in square]
            + [me.at(g=to) for to in line]
            + swapped[1:]
            + sources[1:]
            + [me.sibling()],
            [(jnp.logical_not(me.selfish), sources[0]), (me.crossing, swapped[0])],
        )
        lane = lax.broadcasted_iota(jnp.int32, (s, LANES), 1)
        lower = lane < HEAD
        for head in range(HEADS):
            pair = slice(head // 2 * LANES, head // 2 * LANES + LANES)
            q, k, v = wq_ref[:, pair], wk_ref[:, pair], wv_ref[:, pair]
            if head % 2:
                q, k = pltpu.roll(q, HEAD, 1), pltpu.roll(k, HEAD, 1)
            else:
                v = pltpu.roll(v, HEAD, 1)
            g, h = head // LOCAL, head % LOCAL
            slab[g, :, h * LANES : (h + 1) * LANES] = jnp.where(lower, k, v).astype(low_type)
            slab[g, :, WIDE + h * LANES : WIDE + (h + 1) * LANES] = jnp.where(lower, q, 0.0).astype(
                low_type
            )
        few[...] = jnp.zeros((s, LANES), wide)
        for index in range(count):
            few[index : index + 1, : vecs[index].shape[1]] = vecs[index][...]
        small = few[...]
        for g in range(GROUPS):
            slab[g, :, 2 * WIDE :] = small.astype(low_type)
        pl.semaphore_wait(barrier, expected)

        view = weights
        place = view.at[me.a, me.g, me.y]
        slab_first = [copies.push(slab.at[to], place, me.at(g=to)) for to in line]
        slab_own = copies.keep(slab.at[me.g], place)
        tokens_go = Scatter(tok_send, tok_recv, me.selfish)
        tokens_go.start([(tok, device) for _, device in me.readers()], toks.at[me.slot()], me.slot())
        for w in range(4):
            w1s[w] = w1f[:, w * quarter : (w + 1) * quarter].astype(low_type)
        w2s[...] = w2f[...].astype(low_type)
        wms[...] = wmf[...].astype(low_type)
        place = w1.at[me.x, me.c, me.g, me.y]
        w1_first = [
            copies.push(w1s.at[x * 2 + y], place, me.at(x=x, y=y)) for x, y in square
        ]
        w1_own = copies.keep(w1s.at[me.x * 2 + me.y], place)
        wm_own = copies.keep(wms, wm.at[me.x, me.c, me.g, me.y])

        arrivals, weight_arrivals = [], []
        slab_own.wait()
        for copy in slab_first:
            copy.wait_recv()
        block = view.at[me.a, :, me.y]
        slab_second = [copies.push(block, block, me.at(x=x, y=y)) for x, y in square]
        weight_arrivals.append(copies.push(block, block, me.sibling()))
        for copy, (x, y) in zip(slab_second, square):
            copy.wait_recv()
            block = view.at[x * 2 + me.c, :, y]
            weight_arrivals.append(copies.push(block, block, me.sibling()))
        w1_own.wait()
        for copy in w1_first:
            copy.wait_recv()
        for copy in weight_arrivals:
            copy.wait_recv()

        table = tab[...]

        def spread(pieces, within, owner):
            count = pieces.shape[0] * SMALL
            item = lax.broadcasted_iota(jnp.int32, (count, 2 * WIDE), 0)
            index = lax.broadcasted_iota(jnp.int32, (LANES, 2 * WIDE), 0)
            chosen = jnp.where(index == within, 1.0, 0.0).astype(low_type)
            pieces = pieces.astype(wide).reshape(count, LANES).astype(low_type)
            found = jnp.dot(pieces, chosen, preferred_element_type=wide)
            found = jnp.where((item >> 4) == owner, found, 0.0)
            return jnp.sum(found.reshape(count // SMALL, SMALL, 2 * WIDE), axis=0)

        every = spread(
            view[:, :, :, :SMALL, 2 * WIDE :].reshape(32, SMALL, LANES), table[0:1], table[1:2]
        )
        w_me = me.x * 2 + me.y
        inner_bias = spread(
            view[w_me, :, :, :SMALL, 2 * WIDE :].reshape(8, SMALL, LANES), table[2:3], table[3:4]
        )
        rows16 = lax.broadcasted_iota(jnp.int32, (SMALL, 2 * WIDE), 0)
        vec[...] = jnp.where(rows16 == 8, inner_bias, every)
        turned = pltpu.roll(every, 2 * WIDE - me.g * LOCAL * HEAD, 1)
        lower = lax.broadcasted_iota(jnp.int32, (1, LANES), 1) < HEAD
        biases = [[], []]
        for h in range(LOCAL):
            pair = slice(h // 2 * LANES, h // 2 * LANES + LANES)
            q, v = turned[0:1, pair], turned[1:2, pair]
            if h % 2:
                q = pltpu.roll(q, HEAD, 1)
            else:
                v = pltpu.roll(v, HEAD, 1)
            biases[0].append(jnp.where(lower, 0.0, v))
            biases[1].append(jnp.where(lower, q, 0.0))
        bias = jnp.concatenate(biases[0] + biases[1], axis=1)

        slots = [(u * 2 + v) for u in range(2) for v in range(2)]
        for slot in slots:
            tokens_go.arrived(slot, toks.at[slot])
        block = w1.at[:, me.c, me.g, :]
        w1_second = [copies.push(block, block, me.at(g=to)) for to in line]
        wm_first = [
            copies.push(wms, wm.at[me.x, me.c, me.g, me.y], me.at(g=to)) for to in line
        ]
        w2_place = w2.at[me.g, me.y]
        w2_first = [
            copies.push(w2s, w2_place, device) for device in swapped[1:]
        ]
        exchanged = pltpu.make_async_remote_copy(
            src_ref=w2s,
            dst_ref=w2_place,
            send_sem=swap_send,
            recv_sem=swap_recv,
            device_id=swapped[0],
            device_id_type=MESH,
        )
        stays = pltpu.make_async_copy(w2s, w2_place, swap_recv)

        @pl.when(me.crossing)
        def _():
            exchanged.start()

        @pl.when(jnp.logical_not(me.crossing))
        def _():
            stays.start()

        matrix = weights[:, :, :, :, : 2 * WIDE].reshape(depth, 2 * WIDE)
        made = jnp.dot(
            toks[...].reshape(GROUPS * n, depth), matrix, preferred_element_type=wide
        )
        made = (made + bias).astype(low_type).reshape(GROUPS, n, 2 * WIDE)
        for slot in slots:
            kv_own[slot // 2, slot % 2] = made[slot, :, :WIDE]
            q_own[slot] = made[slot, :, WIDE:]
        mine = kv_all.at[:, me.c, :, me.p, me.y]
        kv_first = [copies.push(kv_own, mine, me.at(x=x, y=y)) for x, y in square]
        arrivals.append(copies.push(kv_own, mine, me.sibling()))
        block = w1.at[:, me.c, me.g, :]
        arrivals.append(copies.push(block, block, me.sibling()))
        kept = [
            copies.keep(kv_own, mine),
            copies.keep(toks, tok_out),
            copies.keep(q_own, q_out),
            copies.keep(weights, wqkv_out),
            copies.keep(vec, vec_out),
        ]
        wm_own.wait()
        for copy in wm_first:
            copy.wait_recv()
        block = wm.at[me.x, me.c, :, me.y]
        wm_second = [copies.push(block, block, me.at(x=x, y=y)) for x, y in square]
        arrivals.append(copies.push(block, block, me.sibling()))

        @pl.when(me.crossing)
        def _():
            exchanged.wait_recv()
            exchanged.wait_send()

        @pl.when(jnp.logical_not(me.crossing))
        def _():
            stays.wait()

        block = w2.at[me.g, me.c]
        arrivals.append(copies.push(block, block, me.sibling()))
        for copy, (x, y) in zip(kv_first, square):
            copy.wait_recv()
            block = kv_all.at[:, me.c, :, (x + me.c) % 2, y]
            arrivals.append(copies.push(block, block, me.sibling()))
        for copy, (x, y) in zip(wm_second, square):
            copy.wait_recv()
            block = wm.at[x, me.c, :, y]
            arrivals.append(copies.push(block, block, me.sibling()))
        for copy, (_, source) in zip(w2_first, me.line()):
            copy.wait_recv()
            block = w2.at[source, me.c]
            arrivals.append(copies.push(block, block, me.sibling()))
        for copy, (_, source) in zip(w1_second, me.line()):
            copy.wait_recv()
            block = w1.at[:, me.c, source, :]
            arrivals.append(copies.push(block, block, me.sibling()))
        for copy in arrivals:
            copy.wait_recv()
        for copy in kept:
            copy.wait()
        tokens_go.finish()
        copies.finish()

    vmem = pltpu.VMEM
    dma = pltpu.SemaphoreType.DMA
    total = 64
    return pl.pallas_call(
        body,
        name="first_kernel",
        out_shape=(
            jax.ShapeDtypeStruct((GROUPS, n, depth), low_type),
            jax.ShapeDtypeStruct((GROUPS, n, WIDE), low_type),
            jax.ShapeDtypeStruct((4, GROUPS, 2, s, cols), low_type),
            jax.ShapeDtypeStruct((SMALL, 2 * WIDE), wide),
            jax.ShapeDtypeStruct((2, 2, 2, 2, 2, n, WIDE), low_type),
            jax.ShapeDtypeStruct((2, 2, GROUPS, 2, s, quarter), low_type),
            jax.ShapeDtypeStruct((GROUPS, 2, e, depth), low_type),
            jax.ShapeDtypeStruct((2, 2, GROUPS, 2, s, depth), low_type),
        ),
        in_specs=[pl.BlockSpec(memory_space=vmem)] * (8 + count),
        out_specs=(pl.BlockSpec(memory_space=pl.ANY),) * 8,
        scratch_shapes=[
            dma((total,)), dma((total,)), dma((8,)), dma((4,)), dma((4,)), dma, dma,
            vmem((GROUPS, s, cols), low_type),
            vmem((GROUPS, n, depth), low_type),
            vmem((4, GROUPS, 2, s, cols), low_type),
            vmem((2, 2, n, WIDE), low_type),
            vmem((GROUPS, n, WIDE), low_type),
            vmem((4, s, quarter), low_type),
            vmem((e, depth), low_type),
            vmem((s, depth), low_type),
            vmem((SMALL, 2 * WIDE), wide),
            vmem((s, LANES), wide),
        ],
        compiler_params=pltpu.CompilerParams(
            collective_id=10, has_side_effects=True, vmem_limit_bytes=VMEM_LIMIT
        ),
    )(tokens, wq, wk, wv, tables, *vectors, inner, outer, mix)


def pass_back(ident, pieces):
    def body(source, target, send, recv):
        me = Spot()
        owners = me.owners()
        readers = [device for _, device in me.readers()]
        barrier, expected = announce(readers[1:], [(jnp.logical_not(me.selfish), readers[0])])
        pl.semaphore_wait(barrier, expected)
        move = Scatter(send, recv, me.selfish)
        move.start([(source.at[slot], device) for slot, device in owners], target.at[me.g], me.g)
        for g in range(GROUPS):
            move.arrived(g, target.at[g])
        move.finish()

    return scatter_call(body, "pass_back", ident, pieces)


def pass_on(ident, pieces):
    def body(source, target, send, recv):
        me = Spot()
        owners = [device for _, device in me.owners()]
        barrier, expected = announce(owners[1:], [(jnp.logical_not(me.selfish), owners[0])])
        pl.semaphore_wait(barrier, expected)
        move = Scatter(send, recv, me.selfish)
        slot = me.slot()
        move.start([(source.at[g], device) for g, device in me.readers()], target.at[slot], slot)
        for index in range(GROUPS):
            move.arrived(index, target.at[index])
        move.finish()

    return scatter_call(body, "pass_on", ident, pieces)


def scatter_call(body, name, ident, pieces):
    return pl.pallas_call(
        body,
        name=name,
        out_shape=jax.ShapeDtypeStruct(pieces.shape, pieces.dtype),
        in_specs=[pl.BlockSpec(memory_space=pl.ANY)],
        out_specs=pl.BlockSpec(memory_space=pl.ANY),
        scratch_shapes=[pltpu.SemaphoreType.DMA((4,)), pltpu.SemaphoreType.DMA((4,))],
        compiler_params=pltpu.CompilerParams(
            collective_id=ident, has_side_effects=True, vmem_limit_bytes=VMEM_LIMIT
        ),
    )(pieces)


def last_kernel(dkv, dq, tokens, weights, grad1, grad2, gradm):
    n = dq.shape[1]
    depth = tokens.shape[-1]
    cols = weights.shape[-1]
    rows = grad1.shape[-2]
    rowsm = gradm.shape[-2]
    tall = grad2.shape[-2]
    s = depth // 32
    cut = depth // 2

    def body(
        dkv_ref, dq_ref, tok, w_ref, g1, g2, gm, dx_out, outq, out1, out2, outm,
        send, recv, local, dx_send, dx_recv, swap_send, swap_recv,
        kst, pk, grads, dxs, gq, s1, p1, f1, s2, p2, sm, pm, fm, tm, sq, pq, fq,
    ):
        me = Spot()
        copies = Copies(send, recv, local)
        square = me.square()
        line = [to for to, _ in me.line()]
        readers = [device for _, device in me.readers()]
        swapped = [me.at(g=to, c=me.y, y=me.c) for to in [me.g] + line]
        barrier, expected = announce(
            [me.at(x=x, y=y) for x, y in square]
            + [me.at(g=to) for to in line]
            + swapped[1:]
            + readers[1:]
            + [me.sibling()],
            [(jnp.logical_not(me.selfish), readers[0]), (me.crossing, swapped[0])],
        )
        pl.semaphore_wait(barrier, expected)
        other = 1 - me.c
        order = square + [(me.x, me.y)]
        k_half = [
            copies.push(
                dkv_ref.at[:, other, :, (x + other) % 2, y], kst.at[x, y], me.sibling()
            )
            for x, y in order
        ]
        w1_half = copies.push(g1.at[:, other], s1, me.sibling())
        wm_half = copies.push(gm.at[:, other], sm, me.sibling())
        w2_half = copies.push(g2.at[:, other], s2, me.sibling())

        k_push = []
        for slot, (x, y) in enumerate(square):
            k_half[slot].wait_recv()

            def addk(index, x=x, y=y):
                u, v = index // 2, index % 2
                kst[x, y, u, v] = total_of(
                    kst[x, y, u, v], dkv_ref[u, me.c, v, (x + me.c) % 2, y]
                ).astype(low_type)

            loop(GROUPS, addk)
            k_push.append(copies.push(kst.at[x, y], pk.at[slot], me.at(x=x, y=y)))

        def at8(index):
            return index // 8, index // 2 % GROUPS, index % 2

        w1_half.wait_recv()

        def add1(index):
            x, g, y = at8(index)
            s1[x, g, y] = total_of(s1[x, g, y], g1[x, me.c, g, y]).astype(low_type)

        loop(16, add1)
        w1_push = [
            copies.push(s1.at[:, to, :], p1.at[slot], me.at(g=to)) for slot, to in enumerate(line)
        ]
        wm_half.wait_recv()

        def addm(index):
            x, g, y = at8(index)
            sm[x, g, y] = total_of(sm[x, g, y], gm[x, me.c, g, y]).astype(low_type)

        loop(16, addm)
        wm_push = [
            copies.push(sm.at[x, :, y], pm.at[slot], me.at(x=x, y=y))
            for slot, (x, y) in enumerate(square)
        ]
        w2_half.wait_recv()

        def add2(g):
            s2[g] = total_of(s2[g], g2[g, me.c]).astype(low_type)

        loop(GROUPS, add2)
        w2_push = [
            copies.push(s2.at[to], p2.at[slot + 1], swapped[slot + 1])
            for slot, to in enumerate(line)
        ]
        exchanged = pltpu.make_async_remote_copy(
            src_ref=s2.at[me.g],
            dst_ref=p2.at[0],
            send_sem=swap_send,
            recv_sem=swap_recv,
            device_id=swapped[0],
            device_id_type=MESH,
        )
        stays = pltpu.make_async_copy(s2.at[me.g], p2.at[0], swap_recv)

        @pl.when(me.crossing)
        def _():
            exchanged.start()

        @pl.when(jnp.logical_not(me.crossing))
        def _():
            stays.start()

        k_half[3].wait_recv()
        for copy in k_push:
            copy.wait_recv()

        def addg(slot):
            u, v = slot // 2, slot % 2
            grads[slot, :, :WIDE] = total_of(
                kst[me.x, me.y, u, v],
                dkv_ref[u, me.c, v, me.p, me.y],
                *[pk[index, u, v] for index in range(3)],
            ).astype(low_type)
            grads[slot, :, WIDE:] = dq_ref[slot]

        loop(GROUPS, addg)
        for slot in range(GROUPS):
            dxs[slot] = lax.dot_general(
                grads[slot], w_ref[:, : 2 * WIDE], NEXT, preferred_element_type=wide
            ).astype(low_type)
        move = Scatter(dx_send, dx_recv, me.selfish)
        move.start(
            [(dxs.at[slot], device) for slot, device in me.owners()], dx_out.at[me.g], me.g
        )
        every = grads[...].reshape(GROUPS * n, 2 * WIDE)
        bias = jnp.sum(every.astype(wide), axis=0, keepdims=True)
        bias = jnp.broadcast_to(bias, (rows - s, 2 * WIDE)).astype(low_type)
        for half in range(2):
            made = lax.dot_general(
                tok[:, :, half * cut : (half + 1) * cut].reshape(GROUPS * n, cut),
                every,
                DOWN,
                preferred_element_type=wide,
            ).astype(low_type)
            for index in range(16):
                x, c, g, y = half, index // 8, index // 2 % GROUPS, index % 2
                gq[x, c, g, y, :s] = made[index * s : (index + 1) * s]
                gq[x, c, g, y, s:] = bias
        q_half = copies.push(gq.at[:, other], sq, me.sibling())

        for copy in wm_push:
            copy.wait_recv()

        def addf(g):
            fm[g] = total_of(sm[me.x, g, me.y], pm[0, g], pm[1, g], pm[2, g]).astype(low_type)

        loop(GROUPS, addf)
        wm_last = [
            copies.push(fm.at[to], tm.at[slot], me.at(g=to)) for slot, to in enumerate(line)
        ]
        q_half.wait_recv()

        def addq(index):
            x, g, y = at8(index)
            sq[x, g, y] = total_of(sq[x, g, y], gq[x, me.c, g, y]).astype(low_type)

        loop(16, addq)
        q_push = [
            copies.push(sq.at[x, :, y], pq.at[slot], me.at(x=x, y=y))
            for slot, (x, y) in enumerate(square)
        ]
        for copy in w1_push:
            copy.wait_recv()

        def addw(index):
            x, y = index // 2, index % 2
            f1[x, y] = total_of(s1[x, me.g, y], *[p1[slot, x, y] for slot in range(3)]).astype(
                low_type
            )

        loop(4, addw)
        quarter = out1.at[me.x * 2 + me.y]
        arrivals = [copies.push(f1.at[x, y], quarter, me.at(x=x, y=y)) for x, y in square]
        kept = [copies.keep(f1.at[me.x, me.y], quarter)]
        for copy in q_push:
            copy.wait_recv()

        def addl(g):
            fq[g] = total_of(sq[me.x, g, me.y], pq[0, g], pq[1, g], pq[2, g]).astype(low_type)

        loop(GROUPS, addl)
        arrivals += [copies.push(fq.at[to], outq.at[me.g], me.at(g=to)) for to in line]
        kept.append(copies.keep(fq.at[me.g], outq.at[me.g]))

        @pl.when(me.crossing)
        def _():
            exchanged.wait_recv()
            exchanged.wait_send()

        @pl.when(jnp.logical_not(me.crossing))
        def _():
            stays.wait()

        for copy in w2_push:
            copy.wait_recv()
        out2[...] = total_of(*[p2[slot] for slot in range(4)])
        for copy in wm_last:
            copy.wait_recv()
        outm[...] = total_of(fm[me.g], *[tm[slot] for slot in range(3)])
        for copy in arrivals:
            copy.wait_recv()
        for g in range(GROUPS):
            move.arrived(g, dx_out.at[g])
        for copy in kept:
            copy.wait()
        move.finish()
        copies.finish()

    vmem = pltpu.VMEM
    dma = pltpu.SemaphoreType.DMA
    total = 48
    return pl.pallas_call(
        body,
        name="last_kernel",
        out_shape=(
            jax.ShapeDtypeStruct((GROUPS, n, depth), low_type),
            jax.ShapeDtypeStruct((GROUPS, rows, 2 * WIDE), low_type),
            jax.ShapeDtypeStruct((4, rows, depth), low_type),
            jax.ShapeDtypeStruct((tall, depth), wide),
            jax.ShapeDtypeStruct((rowsm, depth), wide),
        ),
        in_specs=[pl.BlockSpec(memory_space=vmem)] * 7,
        out_specs=[pl.BlockSpec(memory_space=space) for space in (pl.ANY, pl.ANY, pl.ANY, vmem, vmem)],
        scratch_shapes=[
            dma((total,)), dma((total,)), dma((4,)), dma((4,)), dma((4,)), dma, dma,
            vmem((2, 2, 2, 2, n, WIDE), low_type),
            vmem((3, 2, 2, n, WIDE), low_type),
            vmem((GROUPS, n, 2 * WIDE), low_type),
            vmem((GROUPS, n, depth), low_type),
            vmem((2, 2, GROUPS, 2, rows, 2 * WIDE), low_type),
            vmem((2, GROUPS, 2, rows, depth), low_type),
            vmem((3, 2, 2, rows, depth), low_type),
            vmem((2, 2, rows, depth), low_type),
            vmem((GROUPS, tall, depth), low_type),
            vmem((4, tall, depth), low_type),
            vmem((2, GROUPS, 2, rowsm, depth), low_type),
            vmem((3, GROUPS, rowsm, depth), low_type),
            vmem((GROUPS, rowsm, depth), low_type),
            vmem((3, rowsm, depth), low_type),
            vmem((2, GROUPS, 2, rows, 2 * WIDE), low_type),
            vmem((3, GROUPS, rows, 2 * WIDE), low_type),
            vmem((GROUPS, rows, 2 * WIDE), low_type),
        ],
        compiler_params=pltpu.CompilerParams(
            collective_id=11, has_side_effects=True, vmem_limit_bytes=VMEM_LIMIT
        ),
    )(dkv, dq, tokens, weights, grad1, grad2, gradm)


def final_kernel(hidden, pieces, outq, out1, out2, outm, s, e):
    n, depth = hidden.shape
    quarter = out1.shape[-1]

    def body(hid, dx, q_in, i_in, o_in, m_in, xg, qw, qb, kw, vw, vb, mw, mb, eg, es, iw, ib, ow, ob, fg, fs):
        device = lax.axis_index("au") * lax.axis_size("row") + lax.axis_index("row")
        xg[...] = total_of(hid[...], dx[0], dx[1], dx[2], dx[3]).astype(low_type)
        rows = q_in.shape[1]
        lower = lax.broadcasted_iota(jnp.int32, (rows, LANES), 1) < HEAD

        def part(head, offset):
            g, h = head // LOCAL, head % LOCAL
            return q_in[g, :, offset + h * LANES : offset + (h + 1) * LANES].astype(wide)

        biases = [[], []]
        for pair in range(HEADS // 2):
            span = slice(pair * LANES, (pair + 1) * LANES)
            kv = [part(2 * pair, 0), part(2 * pair + 1, 0)]
            q = [part(2 * pair, WIDE), part(2 * pair + 1, WIDE)]
            made_q = jnp.where(lower, q[0], pltpu.roll(q[1], HEAD, 1))
            made_k = jnp.where(lower, kv[0], pltpu.roll(kv[1], HEAD, 1))
            made_v = jnp.where(lower, pltpu.roll(kv[0], HEAD, 1), kv[1])
            qw[:, span], kw[:, span], vw[:, span] = made_q[:s], made_k[:s], made_v[:s]
            biases[0].append(made_q[s:])
            biases[1].append(made_v[s:])

        def own(eight, width, shift):
            return pltpu.roll(eight, shift, 1)[0:1, :width]

        turn = (depth - device * s) % depth
        qb[...] = own(jnp.concatenate(biases[0], axis=1), s, turn)
        vb[...] = own(jnp.concatenate(biases[1], axis=1), s, turn)
        mw[...] = m_in[:s]
        extras = pltpu.roll(m_in[s : s + 8, :], turn, 1)
        for index, ref in enumerate((mb, eg, es, ob, fg, fs)):
            ref[...] = extras[index : index + 1, :s]
        for w in range(4):
            iw[:, w * quarter : (w + 1) * quarter] = i_in[w, :s].astype(wide)
        place = lax.axis_index("row") * e
        ib[...] = own(
            i_in[lax.axis_index("au"), s : s + 8, :].astype(wide), e, (quarter - place) % quarter
        )
        ow[...] = o_in[...]

    vmem = pltpu.VMEM

    def shape(*dims):
        return jax.ShapeDtypeStruct(dims, wide)

    return pl.pallas_call(
        body,
        name="final_kernel",
        out_shape=(
            jax.ShapeDtypeStruct((n, depth), low_type),
            shape(s, depth), shape(1, s), shape(s, depth), shape(s, depth), shape(1, s),
            shape(s, depth), shape(1, s), shape(1, s), shape(1, s),
            shape(s, 4 * quarter), shape(1, e), shape(e, depth),
            shape(1, s), shape(1, s), shape(1, s),
        ),
        in_specs=[pl.BlockSpec(memory_space=vmem)] * 6,
        out_specs=(pl.BlockSpec(memory_space=vmem),) * 16,
        compiler_params=pltpu.CompilerParams(vmem_limit_bytes=VMEM_LIMIT),
    )(hidden, pieces, outq, out1, out2, outm)


def on_device_general(
    tokens,
    cotangent,
    doc_lengths,
    query_weight,
    query_bias,
    key_weight,
    value_weight,
    value_bias,
    mix_weight,
    mix_bias,
    early_gain,
    early_shift,
    inner_weight,
    inner_bias,
    outer_weight,
    outer_bias,
    final_gain,
    final_shift,
):
    n, depth = tokens.shape
    groups, cycle = lax.axis_size("au"), lax.axis_size("row")
    devices = groups * cycle
    zs = cycle // (2 * GROUPS)
    s = query_weight.shape[0]
    ff = inner_weight.shape[1]
    quarter = ff // 4
    e = outer_weight.shape[0]
    rows = GROUPS * n
    total_tokens = n * devices
    me = Place(zs)
    device = lax.axis_index("au") * cycle + lax.axis_index("row")
    w_me = me.x * 2 + me.y

    def by_head(weight):
        return weight.astype(low_type).reshape(-1, GROUPS, LOCAL, HEAD)

    def packed(query, key, value):
        kv = jnp.stack([key, value], axis=3).reshape(-1, GROUPS, WIDE)
        q = jnp.pad(query, ((0, 0), (0, 0), (0, 0), (0, HEAD))).reshape(-1, GROUPS, WIDE)
        return jnp.concatenate([kv, q], axis=2)

    slab = packed(by_head(query_weight), by_head(key_weight), by_head(value_weight))
    slab = jnp.transpose(slab, (1, 0, 2))
    small = jnp.concatenate(
        [
            vector.astype(low_type)
            for vector in (
                query_bias, value_bias, mix_bias, early_gain, early_shift,
                outer_bias, final_gain, final_shift, inner_bias,
            )
        ]
    )
    extra = -s % 8 or 8
    small = jnp.broadcast_to(
        jnp.pad(small, (0, 2 * WIDE - small.shape[0]))[None, None], (GROUPS, extra, 2 * WIDE)
    )
    slab = jnp.concatenate([slab, small], axis=1)
    tok_all, w_all = spread_tokens(zs, tokens, slab)
    tok_all = tok_all.reshape(rows, depth)
    w_qkv = w_all[..., :s, :].reshape(depth, 2 * WIDE)
    small = w_all[..., s, :].reshape(devices, 2 * WIDE)
    names = [small[:, i * s : (i + 1) * s].reshape(depth) for i in range(8)]
    q_bias, v_bias, m_bias, e_gain, e_shift, o_bias, f_gain, f_shift = names
    i_bias = small[:, 8 * s : 8 * s + e].reshape(4, quarter)[w_me].astype(wide)
    q_bias = q_bias.reshape(1, GROUPS, LOCAL, HEAD)
    v_bias = v_bias.reshape(1, GROUPS, LOCAL, HEAD)
    bias = packed(q_bias, jnp.zeros_like(q_bias), v_bias)[0, me.g].astype(wide)

    qkv = (jnp.dot(tok_all, w_qkv, preferred_element_type=wide) + bias).astype(low_type)
    queries = qkv[:, WIDE:]

    inner_slab = jnp.transpose(inner_weight.astype(low_type).reshape(s, 4, quarter), (1, 0, 2))
    kv_all, w1, w2, wm = spread_keys(
        zs,
        qkv[:, :WIDE].reshape(GROUPS, n, WIDE),
        inner_slab,
        outer_weight.astype(low_type),
        mix_weight.astype(low_type),
    )
    kv_all = kv_all.reshape(total_tokens, WIDE)
    w1 = w1.reshape(depth, quarter)
    w2 = w2.reshape(quarter, depth)
    wm = wm.reshape(depth, depth)

    tile, block = 128, 512
    count = doc_lengths.shape[0]
    upto = jnp.arange(count)[None, :] <= jnp.arange(count)[:, None]
    ends = jnp.sum(jnp.where(upto, doc_lengths[None, :], 0), axis=1)
    owners = ((me.x * 2 + me.c) * cycle + me.z * GROUPS * 2 + jnp.arange(GROUPS) * 2 + me.y) * n
    places = (owners[:, None] + jnp.arange(n)[None, :]).reshape(rows)
    before = ends[None, :] <= places[:, None]
    first = jnp.max(jnp.where(before, ends[None, :], 0), axis=1).astype(jnp.int32)
    last = jnp.min(jnp.where(before, total_tokens, ends[None, :]), axis=1).astype(jnp.int32)
    tiles = rows // tile
    bounds = jnp.stack(
        [
            first.reshape(tiles, tile)[:, 0] // block,
            (last.reshape(tiles, tile)[:, -1] + block - 1) // block,
        ],
        axis=1,
    )
    mixed, mixed_wide, lse = attend_forward(
        queries, kv_all, bounds, first[:, None], last[:, None], tile, block
    )
    mixed_tok = exchange_line(zs, 2, mixed.reshape(GROUPS, n, PACK))
    mixed_tok = jnp.transpose(mixed_tok[:, :, : LOCAL * HEAD], (1, 0, 2)).reshape(n, depth)

    attn = jnp.dot(mixed_tok, wm, preferred_element_type=wide) + m_bias.astype(wide)
    early, early_pull = jax.vjp(
        layer_norm, tokens.astype(wide) + attn, e_gain.astype(wide), e_shift.astype(wide)
    )
    early_all = gather_square(zs, 3, early.astype(low_type)).reshape(rows, depth)
    inner = jnp.dot(early_all, w1, preferred_element_type=wide) + i_bias
    act, gelu_pull = jax.vjp(gelu_exact, inner)
    act_low = act.astype(low_type)
    partial = jnp.dot(act_low, w2, preferred_element_type=wide).astype(low_type)
    partial = exchange_square(zs, 4, partial.reshape(2, 2, n, depth))
    branch = jnp.sum(partial.astype(wide), axis=(0, 1)) + o_bias.astype(wide)
    result, final_pull = jax.vjp(
        layer_norm, early + branch, f_gain.astype(wide), f_shift.astype(wide)
    )
    output = result.astype(low_type)
    final_grads = final_pull(cotangent.astype(wide))
    branch_grad = final_grads[0].astype(low_type)
    outer_bias_grad = jnp.sum(branch_grad.astype(wide), axis=0)
    branch_all = gather_square(zs, 5, branch_grad).reshape(rows, depth)
    act_grad = jnp.einsum("td,fd->tf", branch_all, w2, preferred_element_type=wide)
    inner_grad = gelu_pull(act_grad)[0].astype(low_type)
    partial = jnp.einsum("tf,df->td", inner_grad, w1, preferred_element_type=wide).astype(low_type)
    partial = exchange_square(zs, 6, partial.reshape(2, 2, n, depth))
    grad2 = jnp.einsum("tf,td->fd", act_low, branch_all, preferred_element_type=wide)
    grad1 = jnp.einsum("td,tf->df", early_all, inner_grad, preferred_element_type=wide)
    inner_bias_grad = jnp.sum(inner_grad.astype(wide), axis=0)
    early_grad = final_grads[0] + jnp.sum(partial.astype(wide), axis=(0, 1))
    early_grads = early_pull(early_grad)
    attn_grad = early_grads[0].astype(low_type)
    mixed_grad = jnp.einsum("td,cd->tc", attn_grad, wm, preferred_element_type=wide)
    mixed_grad = jnp.transpose(
        mixed_grad.astype(low_type).reshape(n, GROUPS, LOCAL * HEAD), (1, 0, 2)
    )
    mixed_grad = jnp.pad(mixed_grad, ((0, 0), (0, 0), (0, PACK - LOCAL * HEAD)))
    grad_all = exchange_line(zs, 7, mixed_grad).reshape(rows, PACK)
    gradm = jnp.einsum("tc,td->cd", mixed_tok, attn_grad, preferred_element_type=wide)
    mix_bias_grad = jnp.sum(attn_grad.astype(wide), axis=0)

    delta = jnp.sum(
        (grad_all.astype(wide) * mixed_wide)[:, : LOCAL * HEAD].reshape(rows, LOCAL, HEAD), axis=2
    )

    def as_stat(values):
        return jnp.transpose(values.reshape(tiles, tile, LOCAL), (0, 2, 1))

    def same_stat(values):
        return jnp.broadcast_to(
            values.astype(wide).reshape(tiles, 1, tile), (tiles, LOCAL, tile)
        )

    stats = jnp.stack(
        [same_stat(first), same_stat(last), as_stat(lse[:, :LOCAL]), as_stat(delta)], axis=2
    )
    stats = jnp.pad(stats, ((0, 0), (0, 0), (0, 4), (0, 0)))
    query_grad, dkv = attend_backward(queries, kv_all, grad_all, stats, bounds, tile, block)

    def slabs(grad, extras):
        grad = grad.astype(low_type).reshape(devices, s, -1)
        rest = -s % 8
        rest += 0 if rest >= extras.shape[0] else 8
        extras = jnp.concatenate(
            [extras.astype(low_type), jnp.zeros((rest - extras.shape[0], extras.shape[1]), low_type)]
        )
        extras = jnp.broadcast_to(extras[None], (devices,) + extras.shape)
        return jnp.concatenate([grad, extras], axis=1).reshape(2, 2, zs, GROUPS, 2, s + rest, -1)

    mix_extras = jnp.stack(
        [
            mix_bias_grad, early_grads[1], early_grads[2],
            outer_bias_grad, final_grads[1], final_grads[2],
        ]
    )
    dkv, out1, out2, outm = reduce_keys(
        zs,
        dkv.reshape(2, 2, zs, GROUPS, 2, n, WIDE),
        slabs(grad1, inner_bias_grad[None]),
        grad2.astype(low_type).reshape(zs, GROUPS, 2, e, depth),
        slabs(gradm, mix_extras),
    )
    key_grad = jnp.sum(dkv.astype(wide), axis=0).astype(low_type).reshape(rows, WIDE)
    grads = jnp.concatenate([key_grad, query_grad], axis=1)
    gradq = jnp.einsum("tc,td->cd", tok_all, grads, preferred_element_type=wide)
    bias_grad = jnp.sum(grads.astype(wide), axis=0)
    partial = jnp.einsum("td,cd->tc", grads, w_qkv, preferred_element_type=wide).astype(low_type)
    partial, outq = reduce_tokens(
        zs, partial.reshape(GROUPS, n, depth), slabs(gradq, bias_grad[None])
    )
    input_grad = early_grads[0] + jnp.sum(partial.astype(wide), axis=0)

    def own(vector, count):
        return lax.dynamic_slice_in_dim(vector, device * count, count, 0).astype(wide)

    outq = outq.astype(wide)
    kv_out = outq[:, :, :WIDE].reshape(GROUPS, -1, LOCAL, 2, HEAD)
    q_out = outq[:, :, WIDE:].reshape(GROUPS, -1, LOCAL, 2, HEAD)[:, :, :, 0]

    def unpacked(values):
        return jnp.transpose(values, (1, 0, 2, 3)).reshape(-1, depth)

    q_out, k_out, v_out = unpacked(q_out), unpacked(kv_out[:, :, :, 0]), unpacked(kv_out[:, :, :, 1])
    inner_out = jnp.transpose(out1[:, :s], (1, 0, 2)).reshape(s, ff).astype(wide)
    return (
        output,
        input_grad.astype(low_type),
        q_out[:s],
        own(q_out[s], s),
        k_out[:s],
        v_out[:s],
        own(v_out[s], s),
        outm[:s],
        own(outm[s], s),
        own(outm[s + 1], s),
        own(outm[s + 2], s),
        inner_out,
        own(out1[:, s].reshape(ff), e),
        out2,
        own(outm[s + 3], s),
        own(outm[s + 4], s),
        own(outm[s + 5], s),
    )


def on_device(
    tokens,
    cotangent,
    doc_lengths,
    query_weight,
    query_bias,
    key_weight,
    value_weight,
    value_bias,
    mix_weight,
    mix_bias,
    early_gain,
    early_shift,
    inner_weight,
    inner_bias,
    outer_weight,
    outer_bias,
    final_gain,
    final_shift,
):
    n, depth = tokens.shape
    cycle = lax.axis_size("row")
    devices = lax.axis_size("au") * cycle
    s = query_weight.shape[0]
    ff = inner_weight.shape[1]
    quarter = ff // 4
    e = outer_weight.shape[0]
    rows = GROUPS * n
    total_tokens = n * devices
    me = Spot()
    vectors = [
        vector.reshape(1, -1)
        for vector in (
            query_bias, value_bias, mix_bias, early_gain, early_shift,
            outer_bias, final_gain, final_shift,
        )
    ]
    vectors.append(inner_bias.reshape(1, -1))
    toks, queries, w_qkv, vec, kv_all, w1, w2, wm = first_kernel(
        tokens, query_weight, key_weight, value_weight, vectors,
        inner_weight, outer_weight, mix_weight,
    )
    queries = queries.reshape(rows, WIDE)
    kv_all = kv_all.reshape(total_tokens, WIDE)
    w_qkv = w_qkv.reshape(depth, -1)
    w1 = w1.reshape(depth, quarter)
    w2 = w2.reshape(quarter, depth)
    wm = wm.reshape(depth, depth)
    m_bias, e_gain, e_shift, o_bias, f_gain, f_shift, i_bias = [vec[i] for i in range(2, 9)]

    tile, block = 128, 512
    count = doc_lengths.shape[0]
    upto = jnp.arange(count)[None, :] <= jnp.arange(count)[:, None]
    ends = jnp.sum(jnp.where(upto, doc_lengths[None, :], 0), axis=1)
    slot = jnp.arange(GROUPS)
    owners = ((slot // 2 * 2 + me.c) * cycle + (slot % 2 * 2 + me.p) * 2 + me.y) * n
    places = (owners[:, None] + jnp.arange(n)[None, :]).reshape(rows)
    before = ends[None, :] <= places[:, None]
    first = jnp.max(jnp.where(before, ends[None, :], 0), axis=1).astype(jnp.int32)
    last = jnp.min(jnp.where(before, total_tokens, ends[None, :]), axis=1).astype(jnp.int32)
    tiles = rows // tile
    bounds = jnp.stack(
        [
            first.reshape(tiles, tile)[:, 0] // block,
            (last.reshape(tiles, tile)[:, -1] + block - 1) // block,
        ],
        axis=1,
    )
    mixed, mixed_wide, lse = attend_forward(
        queries, kv_all, bounds, first[:, None], last[:, None], tile, block
    )
    mixed_tok = pass_back(2, mixed.reshape(GROUPS, n, PACK))
    mixed_tok = jnp.transpose(mixed_tok[:, :, : LOCAL * HEAD], (1, 0, 2)).reshape(n, depth)

    attn = jnp.dot(mixed_tok, wm, preferred_element_type=wide) + m_bias
    early, early_pull = jax.vjp(layer_norm, tokens.astype(wide) + attn, e_gain, e_shift)
    early_all = gather_square(1, 3, early.astype(low_type)).reshape(rows, depth)
    inner = jnp.dot(early_all, w1, preferred_element_type=wide) + i_bias
    act, gelu_pull = jax.vjp(gelu_exact, inner)
    act_low = act.astype(low_type)
    partial = jnp.dot(act_low, w2, preferred_element_type=wide).astype(low_type)
    partial = exchange_square(1, 4, partial.reshape(2, 2, n, depth))
    branch = jnp.sum(partial.astype(wide), axis=(0, 1)) + o_bias
    result, final_pull = jax.vjp(layer_norm, early + branch, f_gain, f_shift)
    output = result.astype(low_type)
    final_grads = final_pull(cotangent.astype(wide))
    branch_grad = final_grads[0].astype(low_type)
    outer_bias_grad = jnp.sum(branch_grad.astype(wide), axis=0)
    branch_all = gather_square(1, 5, branch_grad).reshape(rows, depth)
    act_grad = jnp.einsum("td,fd->tf", branch_all, w2, preferred_element_type=wide)
    inner_grad = gelu_pull(act_grad)[0].astype(low_type)
    partial = jnp.einsum("tf,df->td", inner_grad, w1, preferred_element_type=wide).astype(low_type)
    partial = exchange_square(1, 6, partial.reshape(2, 2, n, depth))
    grad2 = jnp.einsum("tf,td->fd", act_low, branch_all, preferred_element_type=wide)
    grad1 = jnp.einsum("td,tf->df", early_all, inner_grad, preferred_element_type=wide)
    inner_bias_grad = jnp.sum(inner_grad.astype(wide), axis=0)
    early_grad = final_grads[0] + jnp.sum(partial.astype(wide), axis=(0, 1))
    early_grads = early_pull(early_grad)
    attn_grad = early_grads[0].astype(low_type)
    mixed_grad = jnp.einsum("td,cd->tc", attn_grad, wm, preferred_element_type=wide)
    mixed_grad = jnp.transpose(
        mixed_grad.astype(low_type).reshape(n, GROUPS, LOCAL * HEAD), (1, 0, 2)
    )
    mixed_grad = jnp.pad(mixed_grad, ((0, 0), (0, 0), (0, PACK - LOCAL * HEAD)))
    grad_all = pass_on(7, mixed_grad).reshape(rows, PACK)
    gradm = jnp.einsum("tc,td->cd", mixed_tok, attn_grad, preferred_element_type=wide)
    mix_bias_grad = jnp.sum(attn_grad.astype(wide), axis=0)

    delta = jnp.sum(
        (grad_all.astype(wide) * mixed_wide)[:, : LOCAL * HEAD].reshape(rows, LOCAL, HEAD), axis=2
    )

    def as_stat(values):
        return jnp.transpose(values.reshape(tiles, tile, LOCAL), (0, 2, 1))

    def same_stat(values):
        return jnp.broadcast_to(
            values.astype(wide).reshape(tiles, 1, tile), (tiles, LOCAL, tile)
        )

    stats = jnp.stack(
        [same_stat(first), same_stat(last), as_stat(lse[:, :LOCAL]), as_stat(delta)], axis=2
    )
    stats = jnp.pad(stats, ((0, 0), (0, 0), (0, 4), (0, 0)))
    query_grad, dkv = attend_backward(queries, kv_all, grad_all, stats, bounds, tile, block)

    def slabs(grad, extras):
        grad = grad.astype(low_type).reshape(devices, s, -1)
        extras = jnp.pad(extras.astype(low_type), ((0, 8 - extras.shape[0]), (0, 0)))
        extras = jnp.broadcast_to(extras[None], (devices,) + extras.shape)
        return jnp.concatenate([grad, extras], axis=1).reshape(2, 2, GROUPS, 2, s + 8, -1)

    mix_extras = jnp.stack(
        [
            mix_bias_grad, early_grads[1], early_grads[2],
            outer_bias_grad, final_grads[1], final_grads[2],
        ]
    )
    pieces, outq, out1, out2, outm = last_kernel(
        dkv.reshape(2, 2, 2, 2, 2, n, WIDE),
        query_grad.reshape(GROUPS, n, WIDE),
        toks,
        w_qkv,
        slabs(grad1, inner_bias_grad[None]),
        grad2.astype(low_type).reshape(GROUPS, 2, e, depth),
        slabs(gradm, mix_extras),
    )
    results = final_kernel(early_grads[0], pieces, outq, out1, out2, outm, s, e)
    return (output,) + tuple(
        result.reshape(-1) if result.shape[0] == 1 else result for result in results
    )


def solution(mesh):
    both = P(("au", "row"), None)
    flat = P(("au", "row"))
    in_specs = (
        both, both, P(), both, flat, both, both, flat, both, flat, flat, flat,
        both, flat, both, flat, flat, flat,
    )
    out_specs = (
        both, both, both, flat, both, both, flat, both, flat, flat, flat,
        both, flat, both, flat, flat, flat,
    )
    fast = mesh.shape["au"] == 4 and mesh.shape["row"] == 2 * GROUPS
    return jax.shard_map(
        on_device if fast else on_device_general, mesh=mesh, in_specs=in_specs, out_specs=out_specs, check_vma=False
    )
```

```python
import functools

import jax
import jax.numpy as jnp
import numpy as np
from jax import lax
from jax.experimental import pallas as pl
from jax.experimental.pallas import tpu as pltpu
from jax.sharding import PartitionSpec as P

HEAD = 64
HEADS = 12
GROUPS = 4
LOCAL = HEADS // GROUPS
LANES = 2 * HEAD
WIDE = LOCAL * LANES
PACK = 256
eps_norm = 1e-06
mask_fill = -1000000000.0
lowest_start = -1e30
low_type = jnp.bfloat16
wide = jnp.float32
MESH = pl.DeviceIdType.MESH
VMEM_LIMIT = 62 * 1024 * 1024


def layer_norm(hidden, gain, shift):
    mean = jnp.mean(hidden, axis=-1, keepdims=True)
    centered = hidden - mean
    spread = jnp.mean(centered * centered, axis=-1, keepdims=True)
    return centered * lax.rsqrt(spread + eps_norm) * gain + shift


def gelu_exact(values):
    return jax.nn.gelu(values, approximate=False)


class Place:
    def __init__(self, zs):
        self.zs = zs
        a = lax.axis_index("au")
        r = lax.axis_index("row")
        self.x, self.c = a // 2, a % 2
        self.y, q = r % 2, r // 2
        self.g, self.z = q % GROUPS, q // GROUPS

    def at(self, x=None, c=None, z=None, g=None, y=None):
        x = self.x if x is None else x
        c = self.c if c is None else c
        z = self.z if z is None else z
        g = self.g if g is None else g
        y = self.y if y is None else y
        return (x * 2 + c, (z * GROUPS + g) * 2 + y)

    def sibling(self):
        return self.at(c=1 - self.c)

    def line(self):
        return [((self.g + k) % GROUPS, (self.g + GROUPS - k) % GROUPS) for k in range(1, GROUPS)]

    def column(self):
        count = self.zs * GROUPS
        q = self.z * GROUPS + self.g
        result = []
        for k in range(1, count):
            to, source = (q + k) % count, (q + count - k) % count
            result.append(((to // GROUPS, to % GROUPS), (source // GROUPS, source % GROUPS)))
        return result

    def plane(self, everywhere=True):
        result = []
        for dx in range(2):
            for dy in range(2):
                for dz in range(self.zs if everywhere else 1):
                    if dx + dy + dz == 0:
                        continue
                    to = ((self.x + dx) % 2, (self.z + dz) % self.zs, (self.y + dy) % 2)
                    source = (
                        (self.x + dx) % 2,
                        (self.z + self.zs - dz) % self.zs,
                        (self.y + dy) % 2,
                    )
                    result.append((to, source))
        return result


class Copies:
    def __init__(self, send, recv, local):
        self.send, self.recv, self.local = send, recv, local
        self.count = 0
        self.local_count = 0
        self.started = []
        self.local_started = []

    def push(self, source, target, device):
        copy = pltpu.make_async_remote_copy(
            src_ref=source,
            dst_ref=target,
            send_sem=self.send.at[self.count],
            recv_sem=self.recv.at[self.count],
            device_id=device,
            device_id_type=MESH,
        )
        self.count += 1
        copy.start()
        self.started.append(copy)
        return copy

    def keep(self, source, target):
        copy = pltpu.make_async_copy(source, target, self.local.at[self.local_count])
        self.local_count += 1
        copy.start()
        return copy

    def finish(self):
        for copy in self.started:
            copy.wait_send()


def greet(devices, partner=None, crossing=None):
    barrier = pltpu.get_barrier_semaphore()
    for device in devices:
        pl.semaphore_signal(barrier, inc=1, device_id=device, device_id_type=MESH)
    if partner is None:
        pl.semaphore_wait(barrier, len(devices))
        return

    @pl.when(crossing)
    def _():
        pl.semaphore_signal(barrier, inc=1, device_id=partner, device_id_type=MESH)
        pl.semaphore_wait(barrier, len(devices) + 1)

    @pl.when(jnp.logical_not(crossing))
    def _():
        pl.semaphore_wait(barrier, len(devices))


def comm_call(body, name, ident, outs, copies, locals_, args, spaces=None, out_spaces=None, scratch=()):
    spaces = [pl.ANY] * len(args) if spaces is None else spaces
    out_spaces = [pl.ANY] * len(outs) if out_spaces is None else out_spaces
    return pl.pallas_call(
        body,
        name=name,
        out_shape=tuple(outs),
        in_specs=[pl.BlockSpec(memory_space=space) for space in spaces],
        out_specs=tuple(pl.BlockSpec(memory_space=space) for space in out_spaces),
        scratch_shapes=[
            pltpu.SemaphoreType.DMA((max(copies, 1),)),
            pltpu.SemaphoreType.DMA((max(copies, 1),)),
            pltpu.SemaphoreType.DMA((max(locals_, 1),)),
            *scratch,
        ],
        compiler_params=pltpu.CompilerParams(
            collective_id=ident, has_side_effects=True, vmem_limit_bytes=VMEM_LIMIT
        ),
    )(*args)


def spread_tokens(zs, tokens, slab):
    n, width = tokens.shape
    groups, rows, columns = slab.shape
    plane = 4 * zs - 1

    def body(tok, piece, tok_all, w_all, send, recv, local):
        me = Place(zs)
        copies = Copies(send, recv, local)
        greet(
            [me.at(g=to) for to, _ in me.line()]
            + [me.at(x=to[0], z=to[1], y=to[2]) for to, _ in me.plane()]
            + [me.sibling()]
        )
        first = [
            copies.push(
                piece.at[to], w_all.at[me.x, me.c, me.z, me.g, me.y], me.at(g=to)
            )
            for to, _ in me.line()
        ]
        own = copies.keep(piece.at[me.g], w_all.at[me.x, me.c, me.z, me.g, me.y])
        arrivals = [copies.push(tok, tok_all.at[me.g], me.at(g=to)) for to, _ in me.line()]
        mine = copies.keep(tok, tok_all.at[me.g])
        own.wait()
        for copy in first:
            copy.wait_recv()
        block = w_all.at[me.x, me.c, me.z, :, me.y]
        second = [
            copies.push(block, block, me.at(x=to[0], z=to[1], y=to[2])) for to, _ in me.plane()
        ]
        arrivals.append(copies.push(block, block, me.sibling()))
        for copy, (_, source) in zip(second, me.plane()):
            copy.wait_recv()
            part = w_all.at[source[0], me.c, source[1], :, source[2]]
            arrivals.append(copies.push(part, part, me.sibling()))
        for copy in arrivals:
            copy.wait_recv()
        mine.wait()
        copies.finish()

    return comm_call(
        body,
        "spread_tokens",
        0,
        [
            jax.ShapeDtypeStruct((GROUPS, n, width), low_type),
            jax.ShapeDtypeStruct((2, 2, zs, GROUPS, 2, rows, columns), low_type),
        ],
        2 * (GROUPS - 1) + 2 * plane + 1,
        2,
        (tokens, slab),
    )


def spread_keys(zs, keys, inner, outer, mix):
    groups, n, width = keys.shape
    quarters, rows, columns = inner.shape
    tall, _ = outer.shape
    plane, column = 4 * zs - 1, GROUPS * zs - 1

    def body(kv, w1s, w2s, wms, kv_all, w1, w2, wm, send, recv, local, swap_send, swap_recv):
        me = Place(zs)
        copies = Copies(send, recv, local)
        crossing = me.c != me.y
        greet(
            [me.at(x=to[0], z=to[1], y=to[2]) for to, _ in me.plane()]
            + [me.at(z=to[0], g=to[1]) for to, _ in me.column()]
            + [me.at(z=to[0], g=to[1], c=me.y, y=me.c) for to, _ in me.column()]
            + [me.sibling()],
            me.at(c=me.y, y=me.c),
            crossing,
        )

        def here(ref):
            return ref.at[me.x, me.c, me.z, me.g, me.y]

        flat = me.plane(everywhere=False)
        own = [
            copies.keep(w1s.at[me.x * 2 + me.y], here(w1)),
            copies.keep(wms, here(wm)),
            copies.keep(kv, kv_all.at[me.x, me.c, me.z, :, me.y]),
        ]
        w1_first = [
            copies.push(w1s.at[to[0] * 2 + to[2]], here(w1), me.at(x=to[0], y=to[2]))
            for to, _ in flat
        ]
        wm_first = [
            copies.push(wms, here(wm), me.at(z=to[0], g=to[1])) for to, _ in me.column()
        ]
        mine = kv_all.at[me.x, me.c, me.z, :, me.y]
        kv_first = [
            copies.push(kv, mine, me.at(x=to[0], z=to[1], y=to[2])) for to, _ in me.plane()
        ]
        arrivals = [copies.push(kv, mine, me.sibling())]
        w2_first = [
            copies.push(
                w2s, w2.at[me.z, me.g, me.y], me.at(z=to[0], g=to[1], c=me.y, y=me.c)
            )
            for to, _ in me.column()
        ]
        exchanged = pltpu.make_async_remote_copy(
            src_ref=w2s,
            dst_ref=w2.at[me.z, me.g, me.y],
            send_sem=swap_send,
            recv_sem=swap_recv,
            device_id=me.at(c=me.y, y=me.c),
            device_id_type=MESH,
        )
        stays = pltpu.make_async_copy(w2s, w2.at[me.z, me.g, me.y], swap_recv)

        @pl.when(crossing)
        def _():
            exchanged.start()

        @pl.when(jnp.logical_not(crossing))
        def _():
            stays.start()

        own[0].wait()
        for copy in w1_first:
            copy.wait_recv()
        block = w1.at[:, me.c, me.z, me.g, :]
        w1_second = [
            copies.push(block, block, me.at(z=to[0], g=to[1])) for to, _ in me.column()
        ]
        arrivals.append(copies.push(block, block, me.sibling()))
        own[1].wait()
        for copy in wm_first:
            copy.wait_recv()
        block = wm.at[me.x, me.c, :, :, me.y]
        wm_second = [copies.push(block, block, me.at(x=to[0], y=to[2])) for to, _ in flat]
        arrivals.append(copies.push(block, block, me.sibling()))
        for copy, (_, source) in zip(kv_first, me.plane()):
            copy.wait_recv()
            part = kv_all.at[source[0], me.c, source[1], :, source[2]]
            arrivals.append(copies.push(part, part, me.sibling()))

        @pl.when(crossing)
        def _():
            exchanged.wait_recv()
            exchanged.wait_send()

        @pl.when(jnp.logical_not(crossing))
        def _():
            stays.wait()

        part = w2.at[me.z, me.g, me.c]
        arrivals.append(copies.push(part, part, me.sibling()))
        for copy, (_, source) in zip(wm_second, flat):
            copy.wait_recv()
            part = wm.at[source[0], me.c, :, :, source[2]]
            arrivals.append(copies.push(part, part, me.sibling()))
        for copy, (_, source) in zip(w2_first, me.column()):
            copy.wait_recv()
            part = w2.at[source[0], source[1], me.c]
            arrivals.append(copies.push(part, part, me.sibling()))
        for copy, (_, source) in zip(w1_second, me.column()):
            copy.wait_recv()
            part = w1.at[:, me.c, source[0], source[1], :]
            arrivals.append(copies.push(part, part, me.sibling()))
        for copy in arrivals:
            copy.wait_recv()
        own[2].wait()
        copies.finish()

    return comm_call(
        body,
        "spread_keys",
        1,
        [
            jax.ShapeDtypeStruct((2, 2, zs, GROUPS, 2, n, width), low_type),
            jax.ShapeDtypeStruct((2, 2, zs, GROUPS, 2, rows, columns), low_type),
            jax.ShapeDtypeStruct((zs, GROUPS, 2, tall, columns), low_type),
            jax.ShapeDtypeStruct((2, 2, zs, GROUPS, 2) + mix.shape, low_type),
        ],
        2 * plane + 1 + 2 * (3 + column + 1 + column) + column + 3 + 8,
        3,
        (keys, inner, outer, mix),
        scratch=(pltpu.SemaphoreType.DMA, pltpu.SemaphoreType.DMA),
    )


def exchange_line(zs, ident, pieces):
    def body(source, target, send, recv, local):
        me = Place(zs)
        copies = Copies(send, recv, local)
        greet([me.at(g=to) for to, _ in me.line()])
        arrivals = [
            copies.push(source.at[to], target.at[me.g], me.at(g=to)) for to, _ in me.line()
        ]
        own = copies.keep(source.at[me.g], target.at[me.g])
        for copy in arrivals:
            copy.wait_recv()
        own.wait()
        copies.finish()

    return comm_call(
        body,
        "exchange_line",
        ident,
        [jax.ShapeDtypeStruct(pieces.shape, pieces.dtype)],
        GROUPS - 1,
        1,
        (pieces,),
    )[0]


def gather_square(zs, ident, rows):
    def body(source, target, send, recv, local):
        me = Place(zs)
        copies = Copies(send, recv, local)
        flat = me.plane(everywhere=False)
        greet([me.at(x=to[0], y=to[2]) for to, _ in flat])
        place = target.at[me.x, me.y]
        arrivals = [copies.push(source, place, me.at(x=to[0], y=to[2])) for to, _ in flat]
        own = copies.keep(source, place)
        for copy in arrivals:
            copy.wait_recv()
        own.wait()
        copies.finish()

    return comm_call(
        body,
        "gather_square",
        ident,
        [jax.ShapeDtypeStruct((2, 2) + rows.shape, rows.dtype)],
        3,
        1,
        (rows,),
    )[0]


def exchange_square(zs, ident, pieces):
    def body(source, target, send, recv, local):
        me = Place(zs)
        copies = Copies(send, recv, local)
        flat = me.plane(everywhere=False)
        greet([me.at(x=to[0], y=to[2]) for to, _ in flat])
        place = target.at[me.x, me.y]
        arrivals = [
            copies.push(source.at[to[0], to[2]], place, me.at(x=to[0], y=to[2]))
            for to, _ in flat
        ]
        own = copies.keep(source.at[me.x, me.y], place)
        for copy in arrivals:
            copy.wait_recv()
        own.wait()
        copies.finish()

    return comm_call(
        body,
        "exchange_square",
        ident,
        [jax.ShapeDtypeStruct(pieces.shape, pieces.dtype)],
        3,
        1,
        (pieces,),
    )[0]


def loop(count, step):
    def body(index, carry):
        step(index)
        return carry

    lax.fori_loop(0, count, body, 0)


def total_of(*values):
    result = values[0].astype(wide)
    for value in values[1:]:
        result = result + value.astype(wide)
    return result


def reduce_keys(zs, dkv, grad1, grad2, gradm):
    n, width = dkv.shape[-2:]
    rows, columns = grad1.shape[-2:]
    rowsm = gradm.shape[-2]
    tall = grad2.shape[-2]
    plane, column = 4 * zs - 1, GROUPS * zs - 1
    count = GROUPS * zs

    def body(
        dkv_ref, g1, g2, gm, dkv_out, out1, out2, outm,
        send, recv, local,
        swap_send, swap_recv, kst, s1, p1, f1, s2, p2, sm, pm, fm, tm,
    ):
        me = Place(zs)
        copies = Copies(send, recv, local)
        crossing = me.c != me.y
        greet(
            [me.at(x=to[0], z=to[1], y=to[2]) for to, _ in me.plane()]
            + [me.at(z=to[0], g=to[1]) for to, _ in me.column()]
            + [me.at(z=to[0], g=to[1], c=me.y, y=me.c) for to, _ in me.column()]
            + [me.sibling()],
            me.at(c=me.y, y=me.c),
            crossing,
        )

        flat = me.plane(everywhere=False)
        other = 1 - me.c
        order = [to for to, _ in me.plane()] + [(me.x, me.z, me.y)]
        w1_half = copies.push(g1.at[:, other], s1, me.sibling())
        w2_half = copies.push(g2.at[:, :, other], s2, me.sibling())
        k_half = [
            copies.push(
                dkv_ref.at[to[0], other, to[1], :, to[2]], kst.at[to[0], to[1], to[2]], me.sibling()
            )
            for to in order
        ]
        wm_half = copies.push(gm.at[:, other], sm, me.sibling())

        w1_half.wait_recv()

        def add1(index):
            x, z, g, y = index // (count * 2), index // (GROUPS * 2) % zs, index // 2 % GROUPS, index % 2
            s1[x, z, g, y] = total_of(s1[x, z, g, y], g1[x, me.c, z, g, y]).astype(low_type)

        loop(4 * count, add1)
        w1_push = [
            copies.push(s1.at[:, to[0], to[1], :], p1.at[slot], me.at(z=to[0], g=to[1]))
            for slot, (to, _) in enumerate(me.column())
        ]
        w2_half.wait_recv()

        def add2(index):
            z, g = index // GROUPS, index % GROUPS
            s2[z, g] = total_of(s2[z, g], g2[z, g, me.c]).astype(low_type)

        loop(count, add2)
        w2_push = [
            copies.push(
                s2.at[to[0], to[1]], p2.at[slot + 1], me.at(z=to[0], g=to[1], c=me.y, y=me.c)
            )
            for slot, (to, _) in enumerate(me.column())
        ]
        exchanged = pltpu.make_async_remote_copy(
            src_ref=s2.at[me.z, me.g],
            dst_ref=p2.at[0],
            send_sem=swap_send,
            recv_sem=swap_recv,
            device_id=me.at(c=me.y, y=me.c),
            device_id_type=MESH,
        )
        stays = pltpu.make_async_copy(s2.at[me.z, me.g], p2.at[0], swap_recv)

        @pl.when(crossing)
        def _():
            exchanged.start()

        @pl.when(jnp.logical_not(crossing))
        def _():
            stays.start()

        k_push = []
        for slot, to in enumerate(order):
            k_half[slot].wait_recv()

            def addk(g, to=to):
                kst[to[0], to[1], to[2], g] = total_of(
                    kst[to[0], to[1], to[2], g], dkv_ref[to[0], me.c, to[1], g, to[2]]
                ).astype(low_type)

            loop(GROUPS, addk)
            if slot < plane:
                k_push.append(
                    copies.push(
                        kst.at[to[0], to[1], to[2]],
                        dkv_out.at[slot],
                        me.at(x=to[0], z=to[1], y=to[2]),
                    )
                )
        wm_half.wait_recv()

        def addm(index):
            x, z, g, y = index // (count * 2), index // (GROUPS * 2) % zs, index // 2 % GROUPS, index % 2
            sm[x, z, g, y] = total_of(sm[x, z, g, y], gm[x, me.c, z, g, y]).astype(low_type)

        loop(4 * count, addm)
        wm_push = [
            copies.push(sm.at[to[0], :, :, to[2]], pm.at[slot], me.at(x=to[0], y=to[2]))
            for slot, (to, _) in enumerate(flat)
        ]
        keep = copies.keep(kst.at[me.x, me.z, me.y], dkv_out.at[plane])
        for copy in wm_push:
            copy.wait_recv()

        def addf(index):
            z, g = index // GROUPS, index % GROUPS
            fm[z, g] = total_of(sm[me.x, z, g, me.y], pm[0, z, g], pm[1, z, g], pm[2, z, g]).astype(
                low_type
            )

        loop(count, addf)
        wm_last = [
            copies.push(fm.at[to[0], to[1]], tm.at[slot], me.at(z=to[0], g=to[1]))
            for slot, (to, _) in enumerate(me.column())
        ]
        for copy in w1_push:
            copy.wait_recv()

        def addg(index):
            x, y = index // 2, index % 2
            f1[x, y] = total_of(
                s1[x, me.z, me.g, y], *[p1[slot, x, y] for slot in range(column)]
            ).astype(low_type)

        loop(4, addg)
        quarter = out1.at[me.x * 2 + me.y]
        w1_last = [
            copies.push(f1.at[to[0], to[2]], quarter, me.at(x=to[0], y=to[2])) for to, _ in flat
        ]
        keep1 = copies.keep(f1.at[me.x, me.y], quarter)

        @pl.when(crossing)
        def _():
            exchanged.wait_recv()
            exchanged.wait_send()

        @pl.when(jnp.logical_not(crossing))
        def _():
            stays.wait()

        for copy in w2_push:
            copy.wait_recv()
        out2[...] = total_of(*[p2[slot] for slot in range(column + 1)])
        for copy in wm_last:
            copy.wait_recv()
        outm[...] = total_of(fm[me.z, me.g], *[tm[slot] for slot in range(column)])
        for copy in w1_last + k_push:
            copy.wait_recv()
        keep.wait()
        keep1.wait()
        copies.finish()

    vmem = pltpu.VMEM
    return comm_call(
        body,
        "reduce_keys",
        8,
        [
            jax.ShapeDtypeStruct((plane + 1, GROUPS, n, width), low_type),
            jax.ShapeDtypeStruct((4, rows, columns), low_type),
            jax.ShapeDtypeStruct((tall, columns), wide),
            jax.ShapeDtypeStruct((rowsm, columns), wide),
        ],
        3 + (plane + 1) + 2 * column + plane + 3 + column + 3,
        2,
        (dkv, grad1, grad2, gradm),
        spaces=[vmem] * 4,
        out_spaces=[pl.ANY, pl.ANY, vmem, vmem],
        scratch=(
            pltpu.SemaphoreType.DMA,
            pltpu.SemaphoreType.DMA,
            vmem((2, zs, 2, GROUPS, n, width), low_type),
            vmem((2, zs, GROUPS, 2, rows, columns), low_type),
            vmem((column, 2, 2, rows, columns), low_type),
            vmem((2, 2, rows, columns), low_type),
            vmem((zs, GROUPS, tall, columns), low_type),
            vmem((column + 1, tall, columns), low_type),
            vmem((2, zs, GROUPS, 2, rowsm, columns), low_type),
            vmem((3, zs, GROUPS, rowsm, columns), low_type),
            vmem((zs, GROUPS, rowsm, columns), low_type),
            vmem((column, rowsm, columns), low_type),
        ),
    )


def reduce_tokens(zs, dx, gradq):
    rows, columns = gradq.shape[-2:]
    plane = 4 * zs - 1
    count = GROUPS * zs

    def body(dx_ref, gq, dx_out, outq, send, recv, local, sq, pq, fq):
        me = Place(zs)
        copies = Copies(send, recv, local)
        greet(
            [me.at(g=to) for to, _ in me.line()]
            + [me.at(x=to[0], z=to[1], y=to[2]) for to, _ in me.plane()]
            + [me.sibling()]
        )
        half = copies.push(gq.at[:, 1 - me.c], sq, me.sibling())
        arrivals = [
            copies.push(dx_ref.at[to], dx_out.at[me.g], me.at(g=to)) for to, _ in me.line()
        ]
        own = copies.keep(dx_ref.at[me.g], dx_out.at[me.g])
        half.wait_recv()

        def add1(index):
            x, z, g, y = index // (count * 2), index // (GROUPS * 2) % zs, index // 2 % GROUPS, index % 2
            sq[x, z, g, y] = total_of(sq[x, z, g, y], gq[x, me.c, z, g, y]).astype(low_type)

        loop(4 * count, add1)
        second = [
            copies.push(
                sq.at[to[0], to[1], :, to[2]], pq.at[slot], me.at(x=to[0], z=to[1], y=to[2])
            )
            for slot, (to, _) in enumerate(me.plane())
        ]
        for copy in second:
            copy.wait_recv()

        def add2(g):
            fq[g] = total_of(
                sq[me.x, me.z, g, me.y], *[pq[slot, g] for slot in range(plane)]
            ).astype(low_type)

        loop(GROUPS, add2)
        arrivals += [
            copies.push(fq.at[to], outq.at[me.g], me.at(g=to)) for to, _ in me.line()
        ]
        keep = copies.keep(fq.at[me.g], outq.at[me.g])
        for copy in arrivals:
            copy.wait_recv()
        own.wait()
        keep.wait()
        copies.finish()

    vmem = pltpu.VMEM
    return comm_call(
        body,
        "reduce_tokens",
        9,
        [
            jax.ShapeDtypeStruct(dx.shape, low_type),
            jax.ShapeDtypeStruct((GROUPS, rows, columns), low_type),
        ],
        1 + 2 * (GROUPS - 1) + plane,
        2,
        (dx, gradq),
        spaces=[pl.ANY, vmem],
        scratch=(
            vmem((2, zs, GROUPS, 2, rows, columns), low_type),
            vmem((plane, GROUPS, rows, columns), low_type),
            vmem((GROUPS, rows, columns), low_type),
        ),
    )


NEXT = (((1,), (1,)), ((), ()))
DOWN = (((0,), (0,)), ((), ()))


def attend_forward(queries, keys, bounds, low, high, tile, block):
    total_rows = queries.shape[0]

    def body(bounds_ref, q_ref, kv_ref, low_ref, high_ref, out_ref, keep_ref, lse_ref):
        def one(turn, unused):
            rows = pl.ds(pl.multiple_of(turn * tile, tile), tile)
            first, last = low_ref[rows, :], high_ref[rows, :]
            heads = [
                q_ref[rows, h * LANES : (h + 1) * LANES] * jnp.asarray(0.125, low_type)
                for h in range(LOCAL)
            ]

            def step(j, carry):
                begin = pl.multiple_of(j * block, block)
                place = begin + lax.broadcasted_iota(jnp.int32, (tile, block), 1)
                same = (place >= first) & (place < last)
                result = []
                for h in range(LOCAL):
                    top, total, mixed = carry[h]
                    kv = kv_ref[pl.ds(begin, block), h * LANES : (h + 1) * LANES]
                    scores = lax.dot_general(heads[h], kv, NEXT, preferred_element_type=wide)
                    scores = jnp.where(same, scores, mask_fill)
                    new_top = jnp.maximum(top, jnp.max(scores, axis=1, keepdims=True))
                    factor = jnp.exp(top - new_top)
                    powers = jnp.exp(scores - new_top)
                    total = total * factor + jnp.sum(powers, axis=1, keepdims=True)
                    mixed = mixed * factor + jnp.dot(
                        powers.astype(low_type), kv, preferred_element_type=wide
                    )
                    result.append((new_top, total, mixed))
                return tuple(result)

            start = tuple(
                (
                    jnp.full((tile, 1), lowest_start, wide),
                    jnp.zeros((tile, 1), wide),
                    jnp.zeros((tile, LANES), wide),
                )
                for _ in range(LOCAL)
            )
            done = lax.fori_loop(bounds_ref[turn, 0], bounds_ref[turn, 1], step, start)
            lane = lax.broadcasted_iota(jnp.int32, (tile, LANES), 1)
            upper = lane >= HEAD
            mixes = [mixed / total for _, total, mixed in done]
            turned = [pltpu.roll(mixed, HEAD, 1) for mixed in mixes]
            front = jnp.where(upper, mixes[1], turned[0])
            back = jnp.where(upper, 0.0, turned[2])
            both = jnp.concatenate([front, back], axis=1)
            keep_ref[rows, :] = both
            out_ref[rows, :] = both.astype(low_type)
            ends = [top + jnp.log(total) for top, total, _ in done]
            lse_ref[rows, :] = jnp.where(lane == 0, ends[0], jnp.where(lane == 1, ends[1], ends[2]))
            return unused

        lax.fori_loop(0, total_rows // tile, one, 0)

    vmem = pl.BlockSpec(memory_space=pltpu.VMEM)
    return pl.pallas_call(
        body,
        name="attend_forward",
        out_shape=(
            jax.ShapeDtypeStruct((total_rows, PACK), low_type),
            jax.ShapeDtypeStruct((total_rows, PACK), wide),
            jax.ShapeDtypeStruct((total_rows, LANES), wide),
        ),
        in_specs=[pl.BlockSpec(memory_space=pltpu.SMEM)] + [vmem] * 4,
        out_specs=(vmem,) * 3,
        compiler_params=pltpu.CompilerParams(vmem_limit_bytes=VMEM_LIMIT),
    )(bounds, queries, keys, low, high)


def attend_backward(queries, keys, grads, stats, bounds, tile, block):
    total_rows = queries.shape[0]
    tokens = keys.shape[0]

    def body(bounds_ref, q_ref, kv_ref, do_ref, stat_ref, dq_ref, dkv_ref, sums):
        h = pl.program_id(0)
        zeros = jnp.zeros((block, LANES), wide)

        def clear(j, unused):
            sums[pl.ds(pl.multiple_of(j * block, block), block), :] = zeros
            return unused

        lax.fori_loop(0, tokens // block, clear, 0)
        lane = lax.broadcasted_iota(jnp.int32, (tile, LANES), 1)
        upper = lane >= HEAD

        def one(turn, unused):
            rows = pl.ds(pl.multiple_of(turn * tile, tile), tile)
            q = q_ref[rows, :] * jnp.asarray(0.125, low_type)
            front = do_ref[rows, :LANES].astype(wide)
            back = do_ref[rows, LANES:].astype(wide)
            grad = jnp.where(h == 1, front, pltpu.roll(jnp.where(h == 0, front, back), HEAD, 1))
            grad = jnp.where(upper, grad, 0.0).astype(low_type)
            stat = stat_ref[turn, 0]
            first, last = stat[0:1, :], stat[1:2, :]
            lse, delta = stat[2:3, :], stat[3:4, :]

            def step(j, total):
                begin = pl.multiple_of(j * block, block)
                place = (begin + lax.broadcasted_iota(jnp.int32, (block, tile), 0)).astype(wide)
                same = (place >= first) & (place < last)
                kv = kv_ref[pl.ds(begin, block), :]
                scores = lax.dot_general(kv, q, NEXT, preferred_element_type=wide)
                probs = jnp.exp(jnp.where(same, scores, mask_fill) - lse)
                dots = lax.dot_general(kv, grad, NEXT, preferred_element_type=wide)
                score_grad = (probs * (dots - delta)).astype(low_type)
                sums[pl.ds(begin, block), :] += jnp.dot(
                    score_grad, q, preferred_element_type=wide
                ) + jnp.dot(probs.astype(low_type), grad, preferred_element_type=wide)
                return total + lax.dot_general(score_grad, kv, DOWN, preferred_element_type=wide)

            total = lax.fori_loop(
                bounds_ref[turn, 0], bounds_ref[turn, 1], step, jnp.zeros((tile, LANES), wide)
            )
            dq_ref[rows, :] = jnp.where(upper, 0.0, total * 0.125).astype(low_type)
            return unused

        lax.fori_loop(0, total_rows // tile, one, 0)

        def store(j, unused):
            part = pl.ds(pl.multiple_of(j * block, block), block)
            dkv_ref[part, :] = sums[part, :].astype(low_type)
            return unused

        lax.fori_loop(0, tokens // block, store, 0)

    return pl.pallas_call(
        body,
        name="attend_backward",
        grid=(LOCAL,),
        out_shape=(
            jax.ShapeDtypeStruct((total_rows, WIDE), low_type),
            jax.ShapeDtypeStruct((tokens, WIDE), low_type),
        ),
        in_specs=[
            pl.BlockSpec(memory_space=pltpu.SMEM),
            pl.BlockSpec((total_rows, LANES), lambda h: (0, h)),
            pl.BlockSpec((tokens, LANES), lambda h: (0, h)),
            pl.BlockSpec((total_rows, PACK), lambda h: (0, 0)),
            pl.BlockSpec((total_rows // tile, 1, 8, tile), lambda h: (0, h, 0, 0)),
        ],
        out_specs=(
            pl.BlockSpec((total_rows, LANES), lambda h: (0, h)),
            pl.BlockSpec((tokens, LANES), lambda h: (0, h)),
        ),
        scratch_shapes=[pltpu.VMEM((tokens, LANES), wide)],
        compiler_params=pltpu.CompilerParams(vmem_limit_bytes=VMEM_LIMIT),
    )(bounds, queries, keys, grads, stats)


class Spot(Place):
    def __init__(self):
        super().__init__(1)
        self.half = self.g // 2
        self.a = self.x * 2 + self.c
        self.p = (self.x + self.c) % 2
        self.selfish = self.g % 2 == self.p
        self.crossing = self.c != self.y

    def square(self):
        return [(to[0], to[2]) for to, _ in self.plane()]

    def readers(self):
        result = []
        for k in range(GROUPS):
            g = (self.g + k) % GROUPS
            result.append((g, self.at(x=(self.g + self.c) % 2, g=g)))
        return result

    def owners(self):
        result = []
        for dv in range(2):
            for du in range(2):
                u, v = (self.x + du) % 2, (self.half + dv) % 2
                result.append((u * 2 + v, self.at(x=u, g=2 * v + self.p)))
        return result

    def slot(self):
        return self.x * 2 + self.half


def count_of(flag):
    return jnp.where(flag, 1, 0)


def announce(always, maybe):
    barrier = pltpu.get_barrier_semaphore()
    for device in always:
        pl.semaphore_signal(barrier, inc=1, device_id=device, device_id_type=MESH)
    for flag, device in maybe:

        @pl.when(flag)
        def _(device=device):
            pl.semaphore_signal(barrier, inc=1, device_id=device, device_id_type=MESH)

    total = len(always)
    for flag, _ in maybe:
        total = total + count_of(flag)
    return barrier, total


class Scatter:
    def __init__(self, send, recv, here):
        self.send, self.recv, self.here = send, recv, here
        self.copies = []

    def start(self, pieces, target, slot):
        for source, device in pieces:
            self.send_one(source, target, slot, device)

    def send_one(self, source, target, slot, device):
        index = len(self.copies)
        copy = pltpu.make_async_remote_copy(
            src_ref=source,
            dst_ref=target,
            send_sem=self.send.at[index],
            recv_sem=self.recv.at[slot],
            device_id=device,
            device_id_type=MESH,
        )
        self.copies.append(copy)
        if index:
            copy.start()
            return
        stay = pltpu.make_async_copy(source, target, self.recv.at[slot])

        @pl.when(self.here)
        def _():
            stay.start()

        @pl.when(jnp.logical_not(self.here))
        def _():
            copy.start()

    def arrived(self, slot, target):
        pltpu.make_async_copy(target, target, self.recv.at[slot]).wait()

    def finish(self):
        for copy in self.copies[1:]:
            copy.wait_send()

        @pl.when(jnp.logical_not(self.here))
        def _():
            self.copies[0].wait_send()


SMALL = 16


def first_tables(s, e, width):
    column = np.arange(width)
    rows = [column % s, column // s, column % e, column // e]
    return np.stack(rows + [np.zeros_like(column)] * 4).astype(np.int32)


def first_kernel(tokens, wq, wk, wv, vectors, inner, outer, mix):
    n, depth = tokens.shape
    s, e = wq.shape[0], outer.shape[0]
    quarter = inner.shape[1] // 4
    cols = 2 * WIDE + LANES
    tables = jnp.asarray(first_tables(s, e, 2 * WIDE))
    count = len(vectors)

    def body(*refs):
        tok, wq_ref, wk_ref, wv_ref, tab = refs[:5]
        vecs = refs[5 : 5 + count]
        w1f, w2f, wmf = refs[5 + count : 8 + count]
        (
            tok_out, q_out, wqkv_out, vec_out, kv_all, w1, w2, wm,
            send, recv, local, tok_send, tok_recv, swap_send, swap_recv,
            slab, toks, weights, kv_own, q_own, w1s, w2s, wms, vec, few,
        ) = refs[8 + count :]
        me = Spot()
        copies = Copies(send, recv, local)
        square = me.square()
        line = [to for to, _ in me.line()]
        sources = [device for _, device in me.owners()]
        swapped = [me.at(g=to, c=me.y, y=me.c) for to in [me.g] + line]
        barrier, expected = announce(
            [me.at(x=x, y=y) for x, y in square]
            + [me.at(g=to) for to in line]
            + swapped[1:]
            + sources[1:]
            + [me.sibling()],
            [(jnp.logical_not(me.selfish), sources[0]), (me.crossing, swapped[0])],
        )
        lane = lax.broadcasted_iota(jnp.int32, (s, LANES), 1)
        lower = lane < HEAD
        for head in range(HEADS):
            pair = slice(head // 2 * LANES, head // 2 * LANES + LANES)
            q, k, v = wq_ref[:, pair], wk_ref[:, pair], wv_ref[:, pair]
            if head % 2:
                q, k = pltpu.roll(q, HEAD, 1), pltpu.roll(k, HEAD, 1)
            else:
                v = pltpu.roll(v, HEAD, 1)
            g, h = head // LOCAL, head % LOCAL
            slab[g, :, h * LANES : (h + 1) * LANES] = jnp.where(lower, k, v).astype(low_type)
            slab[g, :, WIDE + h * LANES : WIDE + (h + 1) * LANES] = jnp.where(lower, q, 0.0).astype(
                low_type
            )
        few[...] = jnp.zeros((s, LANES), wide)
        for index in range(count):
            few[index : index + 1, : vecs[index].shape[1]] = vecs[index][...]
        small = few[...]
        for g in range(GROUPS):
            slab[g, :, 2 * WIDE :] = small.astype(low_type)
        pl.semaphore_wait(barrier, expected)

        view = weights
        place = view.at[me.a, me.g, me.y]
        slab_first = [copies.push(slab.at[to], place, me.at(g=to)) for to in line]
        slab_own = copies.keep(slab.at[me.g], place)
        tokens_go = Scatter(tok_send, tok_recv, me.selfish)
        tokens_go.start([(tok, device) for _, device in me.readers()], toks.at[me.slot()], me.slot())
        for w in range(4):
            w1s[w] = w1f[:, w * quarter : (w + 1) * quarter].astype(low_type)
        w2s[...] = w2f[...].astype(low_type)
        wms[...] = wmf[...].astype(low_type)
        place = w1.at[me.x, me.c, me.g, me.y]
        w1_first = [
            copies.push(w1s.at[x * 2 + y], place, me.at(x=x, y=y)) for x, y in square
        ]
        w1_own = copies.keep(w1s.at[me.x * 2 + me.y], place)
        wm_own = copies.keep(wms, wm.at[me.x, me.c, me.g, me.y])

        arrivals, weight_arrivals = [], []
        slab_own.wait()
        for copy in slab_first:
            copy.wait_recv()
        block = view.at[me.a, :, me.y]
        slab_second = [copies.push(block, block, me.at(x=x, y=y)) for x, y in square]
        weight_arrivals.append(copies.push(block, block, me.sibling()))
        for copy, (x, y) in zip(slab_second, square):
            copy.wait_recv()
            block = view.at[x * 2 + me.c, :, y]
            weight_arrivals.append(copies.push(block, block, me.sibling()))
        w1_own.wait()
        for copy in w1_first:
            copy.wait_recv()
        for copy in weight_arrivals:
            copy.wait_recv()

        table = tab[...]

        def spread(pieces, within, owner):
            count = pieces.shape[0] * SMALL
            item = lax.broadcasted_iota(jnp.int32, (count, 2 * WIDE), 0)
            index = lax.broadcasted_iota(jnp.int32, (LANES, 2 * WIDE), 0)
            chosen = jnp.where(index == within, 1.0, 0.0).astype(low_type)
            pieces = pieces.astype(wide).reshape(count, LANES).astype(low_type)
            found = jnp.dot(pieces, chosen, preferred_element_type=wide)
            found = jnp.where((item >> 4) == owner, found, 0.0)
            return jnp.sum(found.reshape(count // SMALL, SMALL, 2 * WIDE), axis=0)

        every = spread(
            view[:, :, :, :SMALL, 2 * WIDE :].reshape(32, SMALL, LANES), table[0:1], table[1:2]
        )
        w_me = me.x * 2 + me.y
        inner_bias = spread(
            view[w_me, :, :, :SMALL, 2 * WIDE :].reshape(8, SMALL, LANES), table[2:3], table[3:4]
        )
        rows16 = lax.broadcasted_iota(jnp.int32, (SMALL, 2 * WIDE), 0)
        vec[...] = jnp.where(rows16 == 8, inner_bias, every)
        turned = pltpu.roll(every, 2 * WIDE - me.g * LOCAL * HEAD, 1)
        lower = lax.broadcasted_iota(jnp.int32, (1, LANES), 1) < HEAD
        biases = [[], []]
        for h in range(LOCAL):
            pair = slice(h // 2 * LANES, h // 2 * LANES + LANES)
            q, v = turned[0:1, pair], turned[1:2, pair]
            if h % 2:
                q = pltpu.roll(q, HEAD, 1)
            else:
                v = pltpu.roll(v, HEAD, 1)
            biases[0].append(jnp.where(lower, 0.0, v))
            biases[1].append(jnp.where(lower, q, 0.0))
        bias = jnp.concatenate(biases[0] + biases[1], axis=1)

        slots = [(u * 2 + v) for u in range(2) for v in range(2)]
        for slot in slots:
            tokens_go.arrived(slot, toks.at[slot])
        block = w1.at[:, me.c, me.g, :]
        w1_second = [copies.push(block, block, me.at(g=to)) for to in line]
        wm_first = [
            copies.push(wms, wm.at[me.x, me.c, me.g, me.y], me.at(g=to)) for to in line
        ]
        w2_place = w2.at[me.g, me.y]
        w2_first = [
            copies.push(w2s, w2_place, device) for device in swapped[1:]
        ]
        exchanged = pltpu.make_async_remote_copy(
            src_ref=w2s,
            dst_ref=w2_place,
            send_sem=swap_send,
            recv_sem=swap_recv,
            device_id=swapped[0],
            device_id_type=MESH,
        )
        stays = pltpu.make_async_copy(w2s, w2_place, swap_recv)

        @pl.when(me.crossing)
        def _():
            exchanged.start()

        @pl.when(jnp.logical_not(me.crossing))
        def _():
            stays.start()

        matrix = weights[:, :, :, :, : 2 * WIDE].reshape(depth, 2 * WIDE)
        made = jnp.dot(
            toks[...].reshape(GROUPS * n, depth), matrix, preferred_element_type=wide
        )
        made = (made + bias).astype(low_type).reshape(GROUPS, n, 2 * WIDE)
        for slot in slots:
            kv_own[slot // 2, slot % 2] = made[slot, :, :WIDE]
            q_own[slot] = made[slot, :, WIDE:]
        mine = kv_all.at[:, me.c, :, me.p, me.y]
        kv_first = [copies.push(kv_own, mine, me.at(x=x, y=y)) for x, y in square]
        arrivals.append(copies.push(kv_own, mine, me.sibling()))
        block = w1.at[:, me.c, me.g, :]
        arrivals.append(copies.push(block, block, me.sibling()))
        kept = [
            copies.keep(kv_own, mine),
            copies.keep(toks, tok_out),
            copies.keep(q_own, q_out),
            copies.keep(weights, wqkv_out),
            copies.keep(vec, vec_out),
        ]
        wm_own.wait()
        for copy in wm_first:
            copy.wait_recv()
        block = wm.at[me.x, me.c, :, me.y]
        wm_second = [copies.push(block, block, me.at(x=x, y=y)) for x, y in square]
        arrivals.append(copies.push(block, block, me.sibling()))

        @pl.when(me.crossing)
        def _():
            exchanged.wait_recv()
            exchanged.wait_send()

        @pl.when(jnp.logical_not(me.crossing))
        def _():
            stays.wait()

        block = w2.at[me.g, me.c]
        arrivals.append(copies.push(block, block, me.sibling()))
        for copy, (x, y) in zip(kv_first, square):
            copy.wait_recv()
            block = kv_all.at[:, me.c, :, (x + me.c) % 2, y]
            arrivals.append(copies.push(block, block, me.sibling()))
        for copy, (x, y) in zip(wm_second, square):
            copy.wait_recv()
            block = wm.at[x, me.c, :, y]
            arrivals.append(copies.push(block, block, me.sibling()))
        for copy, (_, source) in zip(w2_first, me.line()):
            copy.wait_recv()
            block = w2.at[source, me.c]
            arrivals.append(copies.push(block, block, me.sibling()))
        for copy, (_, source) in zip(w1_second, me.line()):
            copy.wait_recv()
            block = w1.at[:, me.c, source, :]
            arrivals.append(copies.push(block, block, me.sibling()))
        for copy in arrivals:
            copy.wait_recv()
        for copy in kept:
            copy.wait()
        tokens_go.finish()
        copies.finish()

    vmem = pltpu.VMEM
    dma = pltpu.SemaphoreType.DMA
    total = 64
    return pl.pallas_call(
        body,
        name="first_kernel",
        out_shape=(
            jax.ShapeDtypeStruct((GROUPS, n, depth), low_type),
            jax.ShapeDtypeStruct((GROUPS, n, WIDE), low_type),
            jax.ShapeDtypeStruct((4, GROUPS, 2, s, cols), low_type),
            jax.ShapeDtypeStruct((SMALL, 2 * WIDE), wide),
            jax.ShapeDtypeStruct((2, 2, 2, 2, 2, n, WIDE), low_type),
            jax.ShapeDtypeStruct((2, 2, GROUPS, 2, s, quarter), low_type),
            jax.ShapeDtypeStruct((GROUPS, 2, e, depth), low_type),
            jax.ShapeDtypeStruct((2, 2, GROUPS, 2, s, depth), low_type),
        ),
        in_specs=[pl.BlockSpec(memory_space=vmem)] * (8 + count),
        out_specs=(pl.BlockSpec(memory_space=pl.ANY),) * 8,
        scratch_shapes=[
            dma((total,)), dma((total,)), dma((8,)), dma((4,)), dma((4,)), dma, dma,
            vmem((GROUPS, s, cols), low_type),
            vmem((GROUPS, n, depth), low_type),
            vmem((4, GROUPS, 2, s, cols), low_type),
            vmem((2, 2, n, WIDE), low_type),
            vmem((GROUPS, n, WIDE), low_type),
            vmem((4, s, quarter), low_type),
            vmem((e, depth), low_type),
            vmem((s, depth), low_type),
            vmem((SMALL, 2 * WIDE), wide),
            vmem((s, LANES), wide),
        ],
        compiler_params=pltpu.CompilerParams(
            collective_id=10, has_side_effects=True, vmem_limit_bytes=VMEM_LIMIT
        ),
    )(tokens, wq, wk, wv, tables, *vectors, inner, outer, mix)


def pass_back(ident, pieces):
    def body(source, target, send, recv):
        me = Spot()
        owners = me.owners()
        readers = [device for _, device in me.readers()]
        barrier, expected = announce(readers[1:], [(jnp.logical_not(me.selfish), readers[0])])
        pl.semaphore_wait(barrier, expected)
        move = Scatter(send, recv, me.selfish)
        move.start([(source.at[slot], device) for slot, device in owners], target.at[me.g], me.g)
        for g in range(GROUPS):
            move.arrived(g, target.at[g])
        move.finish()

    return scatter_call(body, "pass_back", ident, pieces)


def pass_on(ident, pieces):
    def body(source, target, send, recv):
        me = Spot()
        owners = [device for _, device in me.owners()]
        barrier, expected = announce(owners[1:], [(jnp.logical_not(me.selfish), owners[0])])
        pl.semaphore_wait(barrier, expected)
        move = Scatter(send, recv, me.selfish)
        slot = me.slot()
        move.start([(source.at[g], device) for g, device in me.readers()], target.at[slot], slot)
        for index in range(GROUPS):
            move.arrived(index, target.at[index])
        move.finish()

    return scatter_call(body, "pass_on", ident, pieces)


def scatter_call(body, name, ident, pieces):
    return pl.pallas_call(
        body,
        name=name,
        out_shape=jax.ShapeDtypeStruct(pieces.shape, pieces.dtype),
        in_specs=[pl.BlockSpec(memory_space=pl.ANY)],
        out_specs=pl.BlockSpec(memory_space=pl.ANY),
        scratch_shapes=[pltpu.SemaphoreType.DMA((4,)), pltpu.SemaphoreType.DMA((4,))],
        compiler_params=pltpu.CompilerParams(
            collective_id=ident, has_side_effects=True, vmem_limit_bytes=VMEM_LIMIT
        ),
    )(pieces)


def last_kernel(dkv, dq, tokens, weights, sum1, gradm):
    n = dq.shape[1]
    depth = tokens.shape[-1]
    s = depth // 32
    rows = s + 8
    cut = depth // 2

    def body(
        dkv_ref, dq_ref, tok, w_ref, s1, gm, dx_out, outq, outk, out1, outm,
        send, recv, local, dx_send, dx_recv,
        kst, pk, grads, queries, dxs, gq, sq, pq, fq, gk, sk, pp, fk, p1, f1, sm, pm, fm, tm,
    ):
        me = Spot()
        copies = Copies(send, recv, local)
        square = me.square()
        line = [to for to, _ in me.line()]
        owners = me.owners()
        readers = [device for _, device in me.readers()]
        barrier, expected = announce(
            [me.at(x=x, y=y) for x, y in square]
            + [me.at(g=to) for to in line]
            + readers[1:]
            + [me.sibling()],
            [(jnp.logical_not(me.selfish), readers[0])],
        )
        pl.semaphore_wait(barrier, expected)
        other = 1 - me.c
        k_half = []
        for dv in range(2):
            v = (me.half + dv) % 2
            k_half += [
                copies.push(dkv_ref.at[u, other, v], kst.at[u, v], me.sibling()) for u in range(2)
            ]

        wm_half = copies.push(gm.at[:, other], sm, me.sibling())
        w1_push = [
            copies.push(s1.at[:, to, :], p1.at[slot], me.at(g=to)) for slot, to in enumerate(line)
        ]

        lower = lax.broadcasted_iota(jnp.int32, (n, LANES), 1) < HEAD
        for slot in range(GROUPS):
            second = pltpu.roll(dq_ref[slot, :, LANES : 2 * LANES].astype(wide), HEAD, 1)
            front = jnp.where(lower, dq_ref[slot, :, :LANES].astype(wide), second)
            queries[slot, :, :LANES] = front.astype(low_type)
            queries[slot, :, LANES:] = dq_ref[slot, :, 2 * LANES :]
            grads[slot, :, WIDE:] = dq_ref[slot]

        def weight_grad(values, target):
            width = values.shape[-1]
            bias = jnp.sum(values.astype(wide), axis=0, keepdims=True)
            bias = jnp.broadcast_to(bias, (8, width)).astype(low_type)
            for half in range(2):
                made = lax.dot_general(
                    tok[:, :, half * cut : (half + 1) * cut].reshape(GROUPS * n, cut),
                    values,
                    DOWN,
                    preferred_element_type=wide,
                ).astype(low_type)
                for index in range(16):
                    place = (half, index // 8, index // 2 % GROUPS, index % 2)
                    target[(*place, slice(None, s))] = made[index * s : (index + 1) * s]
                    target[(*place, slice(s, None))] = bias

        def keys_on(dv):
            v = (me.half + dv) % 2
            for u in range(2):
                k_half[2 * dv + u].wait_recv()
            pushed = []
            for du in range(2):
                for slot, (x, y) in enumerate(square):
                    u, p = (x + du) % 2, (x + me.c) % 2
                    kst[u, v, p, y] = kst[u, v, p, y] + dkv_ref[u, me.c, v, p, y]
                    pushed.append(
                        copies.push(
                            kst.at[u, v, p, y], pk.at[2 * dv + du, slot], me.at(x=x, y=y)
                        )
                    )
            return pushed

        k_push = keys_on(0)
        weight_grad(queries[...].reshape(GROUPS * n, PACK), gq)
        q_half = copies.push(gq.at[:, other], sq, me.sibling())
        k_push += keys_on(1)

        def at8(index):
            return index // 8, index // 2 % GROUPS, index % 2

        def pair_sum(total, mine):
            def add(index):
                x, g, y = at8(index)
                total[x, g, y] = total[x, g, y] + mine[x, me.c, g, y]

            loop(16, add)

        def square_push(total, landing):
            return [
                copies.push(total.at[x, :, y], landing.at[slot], me.at(x=x, y=y))
                for slot, (x, y) in enumerate(square)
            ]

        def square_sum(result, total, landed):
            def add(g):
                result[g] = total_of(
                    total[me.x, g, me.y], landed[0, g], landed[1, g], landed[2, g]
                ).astype(low_type)

            loop(GROUPS, add)

        q_half.wait_recv()
        pair_sum(sq, gq)
        q_push = square_push(sq, pq)
        wm_half.wait_recv()
        pair_sum(sm, gm)
        wm_push = square_push(sm, pm)

        move = Scatter(dx_send, dx_recv, me.selfish)
        for index, (slot, device) in enumerate(owners):
            for copy in k_push[3 * index : 3 * index + 3]:
                copy.wait_recv()
            u, v = slot // 2, slot % 2
            grads[slot, :, :WIDE] = total_of(
                kst[u, v, me.p, me.y],
                dkv_ref[u, me.c, v, me.p, me.y],
                *[pk[index, peer] for peer in range(3)],
            ).astype(low_type)
            dxs[slot] = lax.dot_general(
                grads[slot], w_ref[:, : 2 * WIDE], NEXT, preferred_element_type=wide
            ).astype(low_type)
            move.send_one(dxs.at[slot], dx_out.at[me.g], me.g, device)
            if index == 1:
                for copy in q_push:
                    copy.wait_recv()
                square_sum(fq, sq, pq)
                arrivals = [
                    copies.push(fq.at[to], outq.at[me.g], me.at(g=to)) for to in line
                ]
                kept = [copies.keep(fq.at[me.g], outq.at[me.g])]
                for copy in w1_push:
                    copy.wait_recv()

                def addw(index):
                    x, y = index // 2, index % 2
                    f1[x, y] = total_of(
                        s1[x, me.g, y], *[p1[peer, x, y] for peer in range(3)]
                    ).astype(low_type)

                loop(4, addw)
                quarter = out1.at[me.x * 2 + me.y]
                arrivals += [
                    copies.push(f1.at[x, y], quarter, me.at(x=x, y=y)) for x, y in square
                ]
                kept.append(copies.keep(f1.at[me.x, me.y], quarter))
        weight_grad(grads[:, :, :WIDE].reshape(GROUPS * n, WIDE), gk)
        half = copies.push(gk.at[:, other], sk, me.sibling())
        for copy in wm_push:
            copy.wait_recv()
        square_sum(fm, sm, pm)
        wm_last = [
            copies.push(fm.at[to], tm.at[peer], me.at(g=to)) for peer, to in enumerate(line)
        ]
        half.wait_recv()
        pair_sum(sk, gk)
        push = square_push(sk, pp)
        for copy in push:
            copy.wait_recv()
        square_sum(fk, sk, pp)
        arrivals += [copies.push(fk.at[to], outk.at[me.g], me.at(g=to)) for to in line]
        kept.append(copies.keep(fk.at[me.g], outk.at[me.g]))
        for copy in wm_last:
            copy.wait_recv()
        outm[...] = total_of(fm[me.g], *[tm[peer] for peer in range(3)])
        for copy in arrivals:
            copy.wait_recv()
        for g in range(GROUPS):
            move.arrived(g, dx_out.at[g])
        for copy in kept:
            copy.wait()
        move.finish()
        copies.finish()

    vmem = pltpu.VMEM
    dma = pltpu.SemaphoreType.DMA
    total = 64

    def stages(width):
        return [
            vmem((2, 2, GROUPS, 2, rows, width), low_type),
            vmem((2, GROUPS, 2, rows, width), low_type),
            vmem((3, GROUPS, rows, width), low_type),
            vmem((GROUPS, rows, width), low_type),
        ]

    return pl.pallas_call(
        body,
        name="last_kernel",
        out_shape=(
            jax.ShapeDtypeStruct((GROUPS, n, depth), low_type),
            jax.ShapeDtypeStruct((GROUPS, rows, PACK), low_type),
            jax.ShapeDtypeStruct((GROUPS, rows, WIDE), low_type),
            jax.ShapeDtypeStruct((4, rows, depth), low_type),
            jax.ShapeDtypeStruct((rows, depth), wide),
        ),
        in_specs=[pl.BlockSpec(memory_space=vmem)] * 6,
        out_specs=[pl.BlockSpec(memory_space=pl.ANY)] * 4 + [pl.BlockSpec(memory_space=vmem)],
        scratch_shapes=[
            dma((total,)), dma((total,)), dma((4,)), dma((4,)), dma((4,)),
            vmem((2, 2, 2, 2, n, WIDE), low_type),
            vmem((4, 3, n, WIDE), low_type),
            vmem((GROUPS, n, 2 * WIDE), low_type),
            vmem((GROUPS, n, PACK), low_type),
            vmem((GROUPS, n, depth), low_type),
            *stages(PACK),
            *stages(WIDE),
            vmem((3, 2, 2, rows, depth), low_type),
            vmem((2, 2, rows, depth), low_type),
            *stages(depth)[1:],
            vmem((3, rows, depth), low_type),
        ],
        compiler_params=pltpu.CompilerParams(
            collective_id=11, has_side_effects=True, vmem_limit_bytes=VMEM_LIMIT
        ),
    )(dkv, dq, tokens, weights, sum1, gradm)


def final_kernel(hidden, pieces, outq, outk, out1, out2, outm, s, e):
    n, depth = hidden.shape
    quarter = out1.shape[-1]

    def body(hid, dx, q_in, k_in, i_in, o_in, m_in, xg, qw, qb, kw, vw, vb, mw, mb, eg, es, iw, ib, ow, ob, fg, fs):
        device = lax.axis_index("au") * lax.axis_size("row") + lax.axis_index("row")
        xg[...] = total_of(hid[...], dx[0], dx[1], dx[2], dx[3]).astype(low_type)
        rows = q_in.shape[1]
        lower = lax.broadcasted_iota(jnp.int32, (rows, LANES), 1) < HEAD

        def part(head):
            g, h = head // LOCAL, head % LOCAL
            return k_in[g, :, h * LANES : (h + 1) * LANES].astype(wide)

        made_q = []
        for g in range(0, GROUPS, 2):
            a0, b0 = q_in[g, :, :LANES].astype(wide), q_in[g, :, LANES:].astype(wide)
            a1 = pltpu.roll(q_in[g + 1, :, :LANES].astype(wide), HEAD, 1)
            b1 = pltpu.roll(q_in[g + 1, :, LANES:].astype(wide), HEAD, 1)
            made_q += [a0, jnp.where(lower, b0, a1), jnp.where(lower, a1, b1)]
        biases = [[], []]
        for pair in range(HEADS // 2):
            span = slice(pair * LANES, (pair + 1) * LANES)
            kv = [part(2 * pair), part(2 * pair + 1)]
            made_k = jnp.where(lower, kv[0], pltpu.roll(kv[1], HEAD, 1))
            made_v = jnp.where(lower, pltpu.roll(kv[0], HEAD, 1), kv[1])
            qw[:, span], kw[:, span], vw[:, span] = made_q[pair][:s], made_k[:s], made_v[:s]
            biases[0].append(made_q[pair][s:])
            biases[1].append(made_v[s:])

        def own(eight, width, shift):
            return pltpu.roll(eight, shift, 1)[0:1, :width]

        turn = (depth - device * s) % depth
        qb[...] = own(jnp.concatenate(biases[0], axis=1), s, turn)
        vb[...] = own(jnp.concatenate(biases[1], axis=1), s, turn)
        mw[...] = m_in[:s]
        extras = pltpu.roll(m_in[s : s + 8, :], turn, 1)
        for index, ref in enumerate((mb, eg, es, ob, fg, fs)):
            ref[...] = extras[index : index + 1, :s]
        for w in range(4):
            iw[:, w * quarter : (w + 1) * quarter] = i_in[w, :s].astype(wide)
        place = lax.axis_index("row") * e
        ib[...] = own(
            i_in[lax.axis_index("au"), s : s + 8, :].astype(wide), e, (quarter - place) % quarter
        )
        ow[...] = o_in[...]

    vmem = pltpu.VMEM

    def shape(*dims):
        return jax.ShapeDtypeStruct(dims, wide)

    return pl.pallas_call(
        body,
        name="final_kernel",
        out_shape=(
            jax.ShapeDtypeStruct((n, depth), low_type),
            shape(s, depth), shape(1, s), shape(s, depth), shape(s, depth), shape(1, s),
            shape(s, depth), shape(1, s), shape(1, s), shape(1, s),
            shape(s, 4 * quarter), shape(1, e), shape(e, depth),
            shape(1, s), shape(1, s), shape(1, s),
        ),
        in_specs=[pl.BlockSpec(memory_space=vmem)] * 7,
        out_specs=(pl.BlockSpec(memory_space=vmem),) * 16,
        compiler_params=pltpu.CompilerParams(vmem_limit_bytes=VMEM_LIMIT),
    )(hidden, pieces, outq, outk, out1, out2, outm)


def gelu_and_slope(value):
    t = 1.0 / (1.0 + (0.3275911 * 0.7071067811865476) * jnp.abs(value))
    bell = jnp.exp(-0.5 * value * value)
    tail = 1.061405429
    for weight in (-1.453152027, 1.421413741, -0.284496736, 0.254829592):
        tail = tail * t + weight
    tail = 0.5 * tail * t * bell
    below = jnp.where(value >= 0.0, 1.0 - tail, tail)
    return value * below, below + value * bell * 0.3989422804014327


def normed(hidden):
    mean = jnp.mean(hidden, axis=-1, keepdims=True)
    centered = hidden - mean
    spread = jnp.mean(centered * centered, axis=-1, keepdims=True)
    inverse = lax.rsqrt(spread + eps_norm)
    return centered * inverse, inverse


def normed_grad(grad, norm, inverse):
    mean = jnp.mean(grad, axis=-1, keepdims=True)
    along = jnp.mean(grad * norm, axis=-1, keepdims=True)
    return inverse * (grad - mean - norm * along)


def down_sum(values):
    return jnp.sum(values, axis=0, keepdims=True)


def middle_kernel(mixed, tokens, cotangent, mix, inner, outer, vec, s, e):
    n, depth = tokens.shape
    quarter = inner.shape[1]
    rows = s + 8
    cut = depth // 2

    def body(
        mixed_ref, tok, cot, wm_in, w1_in, w2_in, vec_ref,
        out, hidden_out, do_out, gm, s1, out2,
        send, recv, local, back_send, back_recv, on_send, on_recv, swap_send, swap_recv,
        wm, w1, w2, came, mixed_tok, xs, acts, slopes, parts, sums, bgs, igs, parts2, sums2,
        pieces, extra, norm_keep, g1, g2, s2, p2,
    ):
        me = Spot()
        copies = Copies(send, recv, local)
        square = me.square()
        line = [to for to, _ in me.line()]
        owners = me.owners()
        readers = me.readers()
        swapped = [me.at(g=to, c=me.y, y=me.c) for to in [me.g] + line]
        barrier, expected = announce(
            [me.at(x=x, y=y) for x, y in square]
            + swapped[1:]
            + [device for _, device in readers[1:]]
            + [device for _, device in owners[1:]]
            + [me.sibling()],
            [
                (jnp.logical_not(me.selfish), readers[0][1]),
                (jnp.logical_not(me.selfish), owners[0][1]),
                (me.crossing, swapped[0]),
            ],
        )
        loads = [copies.keep(wm_in, wm), copies.keep(w1_in, w1), copies.keep(w2_in, w2)]
        pl.semaphore_wait(barrier, expected)

        back = Scatter(back_send, back_recv, me.selfish)
        back.start([(mixed_ref.at[slot], device) for slot, device in owners], came.at[me.g], me.g)
        lower = lax.broadcasted_iota(jnp.int32, (n, LANES), 1) < HEAD
        loads[0].wait()
        for g in range(GROUPS):
            back.arrived(g, came.at[g])
        for half in range(2):
            a0 = came[2 * half, :, :LANES]
            b0 = came[2 * half, :, LANES:].astype(wide)
            a1 = pltpu.roll(came[2 * half + 1, :, :LANES].astype(wide), HEAD, 1)
            b1 = pltpu.roll(came[2 * half + 1, :, LANES:].astype(wide), HEAD, 1)
            base = half * 3 * LANES
            mixed_tok[:, base : base + LANES] = a0
            mixed_tok[:, base + LANES : base + 2 * LANES] = jnp.where(lower, b0, a1).astype(low_type)
            mixed_tok[:, base + 2 * LANES : base + 3 * LANES] = jnp.where(lower, a1, b1).astype(
                low_type
            )

        def vector(index):
            return vec_ref[index : index + 1, :]

        attn = jnp.dot(mixed_tok[...], wm[...], preferred_element_type=wide) + vector(2)
        norm1, inverse1 = normed(tok[...].astype(wide) + attn)
        early = norm1 * vector(3) + vector(4)
        norm_keep[...] = norm1
        mine = me.x * 2 + me.y
        xs[mine] = early.astype(low_type)
        early_go = [copies.push(xs.at[mine], xs.at[mine], me.at(x=x, y=y)) for x, y in square]
        loads[1].wait()
        loads[2].wait()

        def forward(place):
            inner = jnp.dot(xs[place], w1[...], preferred_element_type=wide) + vector(8)
            act, slope = gelu_and_slope(inner)
            acts[place] = act.astype(low_type)
            slopes[place] = slope
            return jnp.dot(acts[place], w2[...], preferred_element_type=wide)

        own = forward(mine)
        branch_go = []
        for copy, (x, y) in zip(early_go, square):
            copy.wait_recv()
            place = x * 2 + y
            parts[place] = forward(place).astype(low_type)
            branch_go.append(copies.push(parts.at[place], sums.at[mine], me.at(x=x, y=y)))
        for copy in branch_go:
            copy.wait_recv()
        branch = total_of(own, *[sums[x * 2 + y] for x, y in square]) + vector(5)
        norm2, inverse2 = normed(early + branch)
        out[...] = (norm2 * vector(6) + vector(7)).astype(low_type)
        cot_wide = cot[...].astype(wide)
        final_grad = normed_grad(cot_wide * vector(6), norm2, inverse2)
        bgs[mine] = final_grad.astype(low_type)
        grad_go = [copies.push(bgs.at[mine], bgs.at[mine], me.at(x=x, y=y)) for x, y in square]
        extra[...] = jnp.zeros_like(extra)
        extra[3:4, :] = down_sum(bgs[mine].astype(wide))
        extra[4:5, :] = down_sum(cot_wide * norm2)
        extra[5:6, :] = down_sum(cot_wide)

        def backward(place):
            grad = lax.dot_general(bgs[place], w2[...], NEXT, preferred_element_type=wide)
            igs[place] = (grad * slopes[place]).astype(low_type)
            return lax.dot_general(igs[place], w1[...], NEXT, preferred_element_type=wide)

        own = backward(mine)
        token_go = []
        for copy, (x, y) in zip(grad_go, square):
            copy.wait_recv()
            place = x * 2 + y
            parts2[place] = backward(place).astype(low_type)
            token_go.append(copies.push(parts2.at[place], sums2.at[mine], me.at(x=x, y=y)))

        other = 1 - me.c
        grads = bgs[...].reshape(4 * n, depth)
        for half in range(2):
            span = slice(half * cut, (half + 1) * cut)
            made = lax.dot_general(
                acts[:, :, span].reshape(4 * n, cut), grads, DOWN, preferred_element_type=wide
            )
            g2[2 * half : 2 * half + 2] = made.astype(low_type).reshape(2, 2, e, depth)
        w2_half = copies.push(g2.at[:, other], s2, me.sibling())

        grads = igs[...].reshape(4 * n, quarter)
        bias = jnp.broadcast_to(down_sum(grads.astype(wide)), (8, quarter)).astype(low_type)
        for half in range(2):
            span = slice(half * cut, (half + 1) * cut)
            made = lax.dot_general(
                xs[:, :, span].reshape(4 * n, cut), grads, DOWN, preferred_element_type=wide
            ).astype(low_type)
            for index in range(16):
                place = (half, index // 8, index // 2 % GROUPS, index % 2)
                g1[(*place, slice(None, s))] = made[index * s : (index + 1) * s]
                g1[(*place, slice(s, None))] = bias
        w1_half = copies.push(g1.at[:, other], s1, me.sibling())
        w2_half.wait_recv()

        def add2(g):
            s2[g] = s2[g] + g2[g, me.c]

        loop(GROUPS, add2)
        w2_push = [
            copies.push(s2.at[to], p2.at[index + 1], swapped[index + 1])
            for index, to in enumerate(line)
        ]
        exchanged = pltpu.make_async_remote_copy(
            src_ref=s2.at[me.g],
            dst_ref=p2.at[0],
            send_sem=swap_send,
            recv_sem=swap_recv,
            device_id=swapped[0],
            device_id_type=MESH,
        )
        stays = pltpu.make_async_copy(s2.at[me.g], p2.at[0], swap_recv)

        @pl.when(me.crossing)
        def _():
            exchanged.start()

        @pl.when(jnp.logical_not(me.crossing))
        def _():
            stays.start()

        w1_half.wait_recv()

        def add1(index):
            x, g, y = index // 8, index // 2 % GROUPS, index % 2
            s1[x, g, y] = s1[x, g, y] + g1[x, me.c, g, y]

        loop(16, add1)
        for copy in token_go:
            copy.wait_recv()
        early_grad = total_of(final_grad, own, *[sums2[x * 2 + y] for x, y in square])
        norm1 = norm_keep[...]
        extra[1:2, :] = down_sum(early_grad * norm1)
        extra[2:3, :] = down_sum(early_grad)
        hidden = normed_grad(early_grad * vector(3), norm1, inverse1)
        hidden_out[...] = hidden
        attn_grad = hidden.astype(low_type)
        extra[0:1, :] = down_sum(attn_grad.astype(wide))
        back_grad = lax.dot_general(attn_grad, wm[...], NEXT, preferred_element_type=wide)
        for half in range(2):
            base = half * 3 * LANES
            t0 = back_grad[:, base : base + LANES]
            t1 = back_grad[:, base + LANES : base + 2 * LANES]
            t2 = back_grad[:, base + 2 * LANES : base + 3 * LANES]
            r1, r2 = pltpu.roll(t1, HEAD, 1), pltpu.roll(t2, HEAD, 1)
            pieces[2 * half, :, :LANES] = t0.astype(low_type)
            pieces[2 * half, :, LANES:] = jnp.where(lower, t1, 0.0).astype(low_type)
            pieces[2 * half + 1, :, :LANES] = jnp.where(lower, r1, r2).astype(low_type)
            pieces[2 * half + 1, :, LANES:] = jnp.where(lower, r2, 0.0).astype(low_type)
        onward = Scatter(on_send, on_recv, me.selfish)
        slot = me.slot()
        onward.start([(pieces.at[g], device) for g, device in readers], do_out.at[slot], slot)

        for half in range(2):
            span = slice(half * cut, (half + 1) * cut)
            made = lax.dot_general(
                mixed_tok[:, span], attn_grad, DOWN, preferred_element_type=wide
            ).astype(low_type)
            for index in range(16):
                place = (half, index // 8, index // 2 % GROUPS, index % 2)
                gm[(*place, slice(None, s))] = made[index * s : (index + 1) * s]
                gm[(*place, slice(s, None))] = extra[...].astype(low_type)
        @pl.when(me.crossing)
        def _():
            exchanged.wait_recv()
            exchanged.wait_send()

        @pl.when(jnp.logical_not(me.crossing))
        def _():
            stays.wait()

        for copy in w2_push:
            copy.wait_recv()
        out2[...] = total_of(*[p2[index] for index in range(4)])
        for index in range(GROUPS):
            onward.arrived(index, do_out.at[index])
        back.finish()
        onward.finish()
        copies.finish()

    vmem = pltpu.VMEM
    dma = pltpu.SemaphoreType.DMA
    tall = vmem((4, n, depth), low_type)
    space = [vmem] * 3 + [pl.ANY] * 3 + [vmem]
    return pl.pallas_call(
        body,
        name="middle_kernel",
        out_shape=(
            jax.ShapeDtypeStruct((n, depth), low_type),
            jax.ShapeDtypeStruct((n, depth), wide),
            jax.ShapeDtypeStruct((GROUPS, n, PACK), low_type),
            jax.ShapeDtypeStruct((2, 2, GROUPS, 2, rows, depth), low_type),
            jax.ShapeDtypeStruct((2, GROUPS, 2, rows, quarter), low_type),
            jax.ShapeDtypeStruct((e, depth), wide),
        ),
        in_specs=[pl.BlockSpec(memory_space=item) for item in space],
        out_specs=[
            pl.BlockSpec(memory_space=item) for item in (vmem, vmem, pl.ANY, vmem, vmem, vmem)
        ],
        scratch_shapes=[
            dma((40,)), dma((40,)), dma((8,)), dma((4,)), dma((4,)), dma((4,)), dma((4,)), dma, dma,
            vmem((depth, depth), low_type),
            vmem((depth, quarter), low_type),
            vmem((quarter, depth), low_type),
            vmem((GROUPS, n, PACK), low_type),
            vmem((n, depth), low_type),
            tall,
            vmem((4, n, quarter), low_type),
            vmem((4, n, quarter), wide),
            tall, tall, tall,
            vmem((4, n, quarter), low_type),
            tall, tall,
            vmem((GROUPS, n, PACK), low_type),
            vmem((8, depth), wide),
            vmem((n, depth), wide),
            vmem((2, 2, GROUPS, 2, rows, quarter), low_type),
            vmem((GROUPS, 2, e, depth), low_type),
            vmem((GROUPS, e, depth), low_type),
            vmem((4, e, depth), low_type),
        ],
        compiler_params=pltpu.CompilerParams(
            collective_id=12, has_side_effects=True, vmem_limit_bytes=VMEM_LIMIT
        ),
    )(mixed, tokens, cotangent, mix, inner, outer, vec)


def on_device_general(
    tokens,
    cotangent,
    doc_lengths,
    query_weight,
    query_bias,
    key_weight,
    value_weight,
    value_bias,
    mix_weight,
    mix_bias,
    early_gain,
    early_shift,
    inner_weight,
    inner_bias,
    outer_weight,
    outer_bias,
    final_gain,
    final_shift,
):
    n, depth = tokens.shape
    groups, cycle = lax.axis_size("au"), lax.axis_size("row")
    devices = groups * cycle
    zs = cycle // (2 * GROUPS)
    s = query_weight.shape[0]
    ff = inner_weight.shape[1]
    quarter = ff // 4
    e = outer_weight.shape[0]
    rows = GROUPS * n
    total_tokens = n * devices
    me = Place(zs)
    device = lax.axis_index("au") * cycle + lax.axis_index("row")
    w_me = me.x * 2 + me.y

    def by_head(weight):
        return weight.astype(low_type).reshape(-1, GROUPS, LOCAL, HEAD)

    def packed(query, key, value):
        kv = jnp.stack([key, value], axis=3).reshape(-1, GROUPS, WIDE)
        q = jnp.pad(query, ((0, 0), (0, 0), (0, 0), (0, HEAD))).reshape(-1, GROUPS, WIDE)
        return jnp.concatenate([kv, q], axis=2)

    slab = packed(by_head(query_weight), by_head(key_weight), by_head(value_weight))
    slab = jnp.transpose(slab, (1, 0, 2))
    small = jnp.concatenate(
        [
            vector.astype(low_type)
            for vector in (
                query_bias, value_bias, mix_bias, early_gain, early_shift,
                outer_bias, final_gain, final_shift, inner_bias,
            )
        ]
    )
    extra = -s % 8 or 8
    small = jnp.broadcast_to(
        jnp.pad(small, (0, 2 * WIDE - small.shape[0]))[None, None], (GROUPS, extra, 2 * WIDE)
    )
    slab = jnp.concatenate([slab, small], axis=1)
    tok_all, w_all = spread_tokens(zs, tokens, slab)
    tok_all = tok_all.reshape(rows, depth)
    w_qkv = w_all[..., :s, :].reshape(depth, 2 * WIDE)
    small = w_all[..., s, :].reshape(devices, 2 * WIDE)
    names = [small[:, i * s : (i + 1) * s].reshape(depth) for i in range(8)]
    q_bias, v_bias, m_bias, e_gain, e_shift, o_bias, f_gain, f_shift = names
    i_bias = small[:, 8 * s : 8 * s + e].reshape(4, quarter)[w_me].astype(wide)
    q_bias = q_bias.reshape(1, GROUPS, LOCAL, HEAD)
    v_bias = v_bias.reshape(1, GROUPS, LOCAL, HEAD)
    bias = packed(q_bias, jnp.zeros_like(q_bias), v_bias)[0, me.g].astype(wide)

    qkv = (jnp.dot(tok_all, w_qkv, preferred_element_type=wide) + bias).astype(low_type)
    queries = qkv[:, WIDE:]

    inner_slab = jnp.transpose(inner_weight.astype(low_type).reshape(s, 4, quarter), (1, 0, 2))
    kv_all, w1, w2, wm = spread_keys(
        zs,
        qkv[:, :WIDE].reshape(GROUPS, n, WIDE),
        inner_slab,
        outer_weight.astype(low_type),
        mix_weight.astype(low_type),
    )
    kv_all = kv_all.reshape(total_tokens, WIDE)
    w1 = w1.reshape(depth, quarter)
    w2 = w2.reshape(quarter, depth)
    wm = wm.reshape(depth, depth)

    tile, block = 128, 512
    count = doc_lengths.shape[0]
    upto = jnp.arange(count)[None, :] <= jnp.arange(count)[:, None]
    ends = jnp.sum(jnp.where(upto, doc_lengths[None, :], 0), axis=1)
    owners = ((me.x * 2 + me.c) * cycle + me.z * GROUPS * 2 + jnp.arange(GROUPS) * 2 + me.y) * n
    places = (owners[:, None] + jnp.arange(n)[None, :]).reshape(rows)
    before = ends[None, :] <= places[:, None]
    first = jnp.max(jnp.where(before, ends[None, :], 0), axis=1).astype(jnp.int32)
    last = jnp.min(jnp.where(before, total_tokens, ends[None, :]), axis=1).astype(jnp.int32)
    tiles = rows // tile
    bounds = jnp.stack(
        [
            first.reshape(tiles, tile)[:, 0] // block,
            (last.reshape(tiles, tile)[:, -1] + block - 1) // block,
        ],
        axis=1,
    )
    mixed, mixed_wide, lse = attend_forward(
        queries, kv_all, bounds, first[:, None], last[:, None], tile, block
    )
    mixed_tok = exchange_line(zs, 2, mixed.reshape(GROUPS, n, PACK))
    mixed_tok = jnp.transpose(mixed_tok[:, :, : LOCAL * HEAD], (1, 0, 2)).reshape(n, depth)

    attn = jnp.dot(mixed_tok, wm, preferred_element_type=wide) + m_bias.astype(wide)
    early, early_pull = jax.vjp(
        layer_norm, tokens.astype(wide) + attn, e_gain.astype(wide), e_shift.astype(wide)
    )
    early_all = gather_square(zs, 3, early.astype(low_type)).reshape(rows, depth)
    inner = jnp.dot(early_all, w1, preferred_element_type=wide) + i_bias
    act, gelu_pull = jax.vjp(gelu_exact, inner)
    act_low = act.astype(low_type)
    partial = jnp.dot(act_low, w2, preferred_element_type=wide).astype(low_type)
    partial = exchange_square(zs, 4, partial.reshape(2, 2, n, depth))
    branch = jnp.sum(partial.astype(wide), axis=(0, 1)) + o_bias.astype(wide)
    result, final_pull = jax.vjp(
        layer_norm, early + branch, f_gain.astype(wide), f_shift.astype(wide)
    )
    output = result.astype(low_type)
    final_grads = final_pull(cotangent.astype(wide))
    branch_grad = final_grads[0].astype(low_type)
    outer_bias_grad = jnp.sum(branch_grad.astype(wide), axis=0)
    branch_all = gather_square(zs, 5, branch_grad).reshape(rows, depth)
    act_grad = jnp.einsum("td,fd->tf", branch_all, w2, preferred_element_type=wide)
    inner_grad = gelu_pull(act_grad)[0].astype(low_type)
    partial = jnp.einsum("tf,df->td", inner_grad, w1, preferred_element_type=wide).astype(low_type)
    partial = exchange_square(zs, 6, partial.reshape(2, 2, n, depth))
    grad2 = jnp.einsum("tf,td->fd", act_low, branch_all, preferred_element_type=wide)
    grad1 = jnp.einsum("td,tf->df", early_all, inner_grad, preferred_element_type=wide)
    inner_bias_grad = jnp.sum(inner_grad.astype(wide), axis=0)
    early_grad = final_grads[0] + jnp.sum(partial.astype(wide), axis=(0, 1))
    early_grads = early_pull(early_grad)
    attn_grad = early_grads[0].astype(low_type)
    mixed_grad = jnp.einsum("td,cd->tc", attn_grad, wm, preferred_element_type=wide)
    mixed_grad = jnp.transpose(
        mixed_grad.astype(low_type).reshape(n, GROUPS, LOCAL * HEAD), (1, 0, 2)
    )
    mixed_grad = jnp.pad(mixed_grad, ((0, 0), (0, 0), (0, PACK - LOCAL * HEAD)))
    grad_all = exchange_line(zs, 7, mixed_grad).reshape(rows, PACK)
    gradm = jnp.einsum("tc,td->cd", mixed_tok, attn_grad, preferred_element_type=wide)
    mix_bias_grad = jnp.sum(attn_grad.astype(wide), axis=0)

    delta = jnp.sum(
        (grad_all.astype(wide) * mixed_wide)[:, : LOCAL * HEAD].reshape(rows, LOCAL, HEAD), axis=2
    )

    def as_stat(values):
        return jnp.transpose(values.reshape(tiles, tile, LOCAL), (0, 2, 1))

    def same_stat(values):
        return jnp.broadcast_to(
            values.astype(wide).reshape(tiles, 1, tile), (tiles, LOCAL, tile)
        )

    stats = jnp.stack(
        [same_stat(first), same_stat(last), as_stat(lse[:, :LOCAL]), as_stat(delta)], axis=2
    )
    stats = jnp.pad(stats, ((0, 0), (0, 0), (0, 4), (0, 0)))
    query_grad, dkv = attend_backward(queries, kv_all, grad_all, stats, bounds, tile, block)

    def slabs(grad, extras):
        grad = grad.astype(low_type).reshape(devices, s, -1)
        rest = -s % 8
        rest += 0 if rest >= extras.shape[0] else 8
        extras = jnp.concatenate(
            [extras.astype(low_type), jnp.zeros((rest - extras.shape[0], extras.shape[1]), low_type)]
        )
        extras = jnp.broadcast_to(extras[None], (devices,) + extras.shape)
        return jnp.concatenate([grad, extras], axis=1).reshape(2, 2, zs, GROUPS, 2, s + rest, -1)

    mix_extras = jnp.stack(
        [
            mix_bias_grad, early_grads[1], early_grads[2],
            outer_bias_grad, final_grads[1], final_grads[2],
        ]
    )
    dkv, out1, out2, outm = reduce_keys(
        zs,
        dkv.reshape(2, 2, zs, GROUPS, 2, n, WIDE),
        slabs(grad1, inner_bias_grad[None]),
        grad2.astype(low_type).reshape(zs, GROUPS, 2, e, depth),
        slabs(gradm, mix_extras),
    )
    key_grad = jnp.sum(dkv.astype(wide), axis=0).astype(low_type).reshape(rows, WIDE)
    grads = jnp.concatenate([key_grad, query_grad], axis=1)
    gradq = jnp.einsum("tc,td->cd", tok_all, grads, preferred_element_type=wide)
    bias_grad = jnp.sum(grads.astype(wide), axis=0)
    partial = jnp.einsum("td,cd->tc", grads, w_qkv, preferred_element_type=wide).astype(low_type)
    partial, outq = reduce_tokens(
        zs, partial.reshape(GROUPS, n, depth), slabs(gradq, bias_grad[None])
    )
    input_grad = early_grads[0] + jnp.sum(partial.astype(wide), axis=0)

    def own(vector, count):
        return lax.dynamic_slice_in_dim(vector, device * count, count, 0).astype(wide)

    outq = outq.astype(wide)
    kv_out = outq[:, :, :WIDE].reshape(GROUPS, -1, LOCAL, 2, HEAD)
    q_out = outq[:, :, WIDE:].reshape(GROUPS, -1, LOCAL, 2, HEAD)[:, :, :, 0]

    def unpacked(values):
        return jnp.transpose(values, (1, 0, 2, 3)).reshape(-1, depth)

    q_out, k_out, v_out = unpacked(q_out), unpacked(kv_out[:, :, :, 0]), unpacked(kv_out[:, :, :, 1])
    inner_out = jnp.transpose(out1[:, :s], (1, 0, 2)).reshape(s, ff).astype(wide)
    return (
        output,
        input_grad.astype(low_type),
        q_out[:s],
        own(q_out[s], s),
        k_out[:s],
        v_out[:s],
        own(v_out[s], s),
        outm[:s],
        own(outm[s], s),
        own(outm[s + 1], s),
        own(outm[s + 2], s),
        inner_out,
        own(out1[:, s].reshape(ff), e),
        out2,
        own(outm[s + 3], s),
        own(outm[s + 4], s),
        own(outm[s + 5], s),
    )


def on_device(
    tokens,
    cotangent,
    doc_lengths,
    query_weight,
    query_bias,
    key_weight,
    value_weight,
    value_bias,
    mix_weight,
    mix_bias,
    early_gain,
    early_shift,
    inner_weight,
    inner_bias,
    outer_weight,
    outer_bias,
    final_gain,
    final_shift,
):
    n, depth = tokens.shape
    cycle = lax.axis_size("row")
    devices = lax.axis_size("au") * cycle
    s = query_weight.shape[0]
    ff = inner_weight.shape[1]
    quarter = ff // 4
    e = outer_weight.shape[0]
    rows = GROUPS * n
    total_tokens = n * devices
    me = Spot()
    vectors = [
        vector.reshape(1, -1)
        for vector in (
            query_bias, value_bias, mix_bias, early_gain, early_shift,
            outer_bias, final_gain, final_shift,
        )
    ]
    vectors.append(inner_bias.reshape(1, -1))
    toks, queries, w_qkv, vec, kv_all, w1, w2, wm = first_kernel(
        tokens, query_weight, key_weight, value_weight, vectors,
        inner_weight, outer_weight, mix_weight,
    )
    queries = queries.reshape(rows, WIDE)
    kv_all = kv_all.reshape(total_tokens, WIDE)
    w_qkv = w_qkv.reshape(depth, -1)
    w1 = w1.reshape(depth, quarter)
    w2 = w2.reshape(quarter, depth)
    wm = wm.reshape(depth, depth)
    tile, block = 128, 1024
    count = doc_lengths.shape[0]
    upto = jnp.arange(count)[None, :] <= jnp.arange(count)[:, None]
    ends = jnp.sum(jnp.where(upto, doc_lengths[None, :], 0), axis=1)
    slot = jnp.arange(GROUPS)
    owners = ((slot // 2 * 2 + me.c) * cycle + (slot % 2 * 2 + me.p) * 2 + me.y) * n
    places = (owners[:, None] + jnp.arange(n)[None, :]).reshape(rows)
    before = ends[None, :] <= places[:, None]
    first = jnp.max(jnp.where(before, ends[None, :], 0), axis=1).astype(jnp.int32)
    last = jnp.min(jnp.where(before, total_tokens, ends[None, :]), axis=1).astype(jnp.int32)
    tiles = rows // tile
    bounds = jnp.stack(
        [
            first.reshape(tiles, tile)[:, 0] // block,
            (last.reshape(tiles, tile)[:, -1] + block - 1) // block,
        ],
        axis=1,
    )
    mixed, mixed_wide, lse = attend_forward(
        queries, kv_all, bounds, first[:, None], last[:, None], tile, block
    )
    output, hidden_grad, grad_all, gradm, sum1, out2 = middle_kernel(
        mixed.reshape(GROUPS, n, PACK), tokens, cotangent, wm, w1, w2, vec, s, e
    )
    grad_all = grad_all.reshape(rows, PACK)
    delta = jnp.sum(
        (grad_all.astype(wide) * mixed_wide)[:, : LOCAL * HEAD].reshape(rows, LOCAL, HEAD), axis=2
    )

    def as_stat(values):
        return jnp.transpose(values.reshape(tiles, tile, LOCAL), (0, 2, 1))

    def same_stat(values):
        return jnp.broadcast_to(
            values.astype(wide).reshape(tiles, 1, tile), (tiles, LOCAL, tile)
        )

    stats = jnp.stack(
        [same_stat(first), same_stat(last), as_stat(lse[:, :LOCAL]), as_stat(delta)], axis=2
    )
    stats = jnp.pad(stats, ((0, 0), (0, 0), (0, 4), (0, 0)))
    query_grad, dkv = attend_backward(queries, kv_all, grad_all, stats, bounds, tile, block)

    pieces, outq, outk, out1, outm = last_kernel(
        dkv.reshape(2, 2, 2, 2, 2, n, WIDE),
        query_grad.reshape(GROUPS, n, WIDE),
        toks,
        w_qkv,
        sum1,
        gradm,
    )
    results = final_kernel(hidden_grad, pieces, outq, outk, out1, out2, outm, s, e)
    return (output,) + tuple(
        result.reshape(-1) if result.shape[0] == 1 else result for result in results
    )


def solution(mesh):
    both = P(("au", "row"), None)
    flat = P(("au", "row"))
    in_specs = (
        both, both, P(), both, flat, both, both, flat, both, flat, flat, flat,
        both, flat, both, flat, flat, flat,
    )
    out_specs = (
        both, both, both, flat, both, both, flat, both, flat, flat, flat,
        both, flat, both, flat, flat, flat,
    )
    fast = mesh.shape["au"] == 4 and mesh.shape["row"] == 2 * GROUPS
    return jax.shard_map(
        on_device if fast else on_device_general, mesh=mesh, in_specs=in_specs, out_specs=out_specs, check_vma=False
    )
```

```python
import functools

import jax
import jax.numpy as jnp
import numpy as np
from jax import lax
from jax.experimental import pallas as pl
from jax.experimental.pallas import tpu as pltpu
from jax.sharding import PartitionSpec as P

HEAD = 64
HEADS = 12
GROUPS = 4
LOCAL = HEADS // GROUPS
LANES = 2 * HEAD
WIDE = LOCAL * LANES
PACK = 256
eps_norm = 1e-06
mask_fill = -1000000000.0
lowest_start = -1e30
low_type = jnp.bfloat16
wide = jnp.float32
MESH = pl.DeviceIdType.MESH
VMEM_LIMIT = 62 * 1024 * 1024


def layer_norm(hidden, gain, shift):
    mean = jnp.mean(hidden, axis=-1, keepdims=True)
    centered = hidden - mean
    spread = jnp.mean(centered * centered, axis=-1, keepdims=True)
    return centered * lax.rsqrt(spread + eps_norm) * gain + shift


def gelu_exact(values):
    return jax.nn.gelu(values, approximate=False)


class Place:
    def __init__(self, zs):
        self.zs = zs
        a = lax.axis_index("au")
        r = lax.axis_index("row")
        self.x, self.c = a // 2, a % 2
        self.y, q = r % 2, r // 2
        self.g, self.z = q % GROUPS, q // GROUPS

    def at(self, x=None, c=None, z=None, g=None, y=None):
        x = self.x if x is None else x
        c = self.c if c is None else c
        z = self.z if z is None else z
        g = self.g if g is None else g
        y = self.y if y is None else y
        return (x * 2 + c, (z * GROUPS + g) * 2 + y)

    def sibling(self):
        return self.at(c=1 - self.c)

    def line(self):
        return [((self.g + k) % GROUPS, (self.g + GROUPS - k) % GROUPS) for k in range(1, GROUPS)]

    def column(self):
        count = self.zs * GROUPS
        q = self.z * GROUPS + self.g
        result = []
        for k in range(1, count):
            to, source = (q + k) % count, (q + count - k) % count
            result.append(((to // GROUPS, to % GROUPS), (source // GROUPS, source % GROUPS)))
        return result

    def plane(self, everywhere=True):
        result = []
        for dx in range(2):
            for dy in range(2):
                for dz in range(self.zs if everywhere else 1):
                    if dx + dy + dz == 0:
                        continue
                    to = ((self.x + dx) % 2, (self.z + dz) % self.zs, (self.y + dy) % 2)
                    source = (
                        (self.x + dx) % 2,
                        (self.z + self.zs - dz) % self.zs,
                        (self.y + dy) % 2,
                    )
                    result.append((to, source))
        return result


class Copies:
    def __init__(self, send, recv, local):
        self.send, self.recv, self.local = send, recv, local
        self.count = 0
        self.local_count = 0
        self.started = []
        self.local_started = []

    def push(self, source, target, device):
        copy = pltpu.make_async_remote_copy(
            src_ref=source,
            dst_ref=target,
            send_sem=self.send.at[self.count],
            recv_sem=self.recv.at[self.count],
            device_id=device,
            device_id_type=MESH,
        )
        self.count += 1
        copy.start()
        self.started.append(copy)
        return copy

    def keep(self, source, target):
        copy = pltpu.make_async_copy(source, target, self.local.at[self.local_count])
        self.local_count += 1
        copy.start()
        return copy

    def finish(self):
        for copy in self.started:
            copy.wait_send()


def greet(devices, partner=None, crossing=None):
    barrier = pltpu.get_barrier_semaphore()
    for device in devices:
        pl.semaphore_signal(barrier, inc=1, device_id=device, device_id_type=MESH)
    if partner is None:
        pl.semaphore_wait(barrier, len(devices))
        return

    @pl.when(crossing)
    def _():
        pl.semaphore_signal(barrier, inc=1, device_id=partner, device_id_type=MESH)
        pl.semaphore_wait(barrier, len(devices) + 1)

    @pl.when(jnp.logical_not(crossing))
    def _():
        pl.semaphore_wait(barrier, len(devices))


def comm_call(body, name, ident, outs, copies, locals_, args, spaces=None, out_spaces=None, scratch=()):
    spaces = [pl.ANY] * len(args) if spaces is None else spaces
    out_spaces = [pl.ANY] * len(outs) if out_spaces is None else out_spaces
    return pl.pallas_call(
        body,
        name=name,
        out_shape=tuple(outs),
        in_specs=[pl.BlockSpec(memory_space=space) for space in spaces],
        out_specs=tuple(pl.BlockSpec(memory_space=space) for space in out_spaces),
        scratch_shapes=[
            pltpu.SemaphoreType.DMA((max(copies, 1),)),
            pltpu.SemaphoreType.DMA((max(copies, 1),)),
            pltpu.SemaphoreType.DMA((max(locals_, 1),)),
            *scratch,
        ],
        compiler_params=pltpu.CompilerParams(
            collective_id=ident, has_side_effects=True, vmem_limit_bytes=VMEM_LIMIT
        ),
    )(*args)


def spread_tokens(zs, tokens, slab):
    n, width = tokens.shape
    groups, rows, columns = slab.shape
    plane = 4 * zs - 1

    def body(tok, piece, tok_all, w_all, send, recv, local):
        me = Place(zs)
        copies = Copies(send, recv, local)
        greet(
            [me.at(g=to) for to, _ in me.line()]
            + [me.at(x=to[0], z=to[1], y=to[2]) for to, _ in me.plane()]
            + [me.sibling()]
        )
        first = [
            copies.push(
                piece.at[to], w_all.at[me.x, me.c, me.z, me.g, me.y], me.at(g=to)
            )
            for to, _ in me.line()
        ]
        own = copies.keep(piece.at[me.g], w_all.at[me.x, me.c, me.z, me.g, me.y])
        arrivals = [copies.push(tok, tok_all.at[me.g], me.at(g=to)) for to, _ in me.line()]
        mine = copies.keep(tok, tok_all.at[me.g])
        own.wait()
        for copy in first:
            copy.wait_recv()
        block = w_all.at[me.x, me.c, me.z, :, me.y]
        second = [
            copies.push(block, block, me.at(x=to[0], z=to[1], y=to[2])) for to, _ in me.plane()
        ]
        arrivals.append(copies.push(block, block, me.sibling()))
        for copy, (_, source) in zip(second, me.plane()):
            copy.wait_recv()
            part = w_all.at[source[0], me.c, source[1], :, source[2]]
            arrivals.append(copies.push(part, part, me.sibling()))
        for copy in arrivals:
            copy.wait_recv()
        mine.wait()
        copies.finish()

    return comm_call(
        body,
        "spread_tokens",
        0,
        [
            jax.ShapeDtypeStruct((GROUPS, n, width), low_type),
            jax.ShapeDtypeStruct((2, 2, zs, GROUPS, 2, rows, columns), low_type),
        ],
        2 * (GROUPS - 1) + 2 * plane + 1,
        2,
        (tokens, slab),
    )


def spread_keys(zs, keys, inner, outer, mix):
    groups, n, width = keys.shape
    quarters, rows, columns = inner.shape
    tall, _ = outer.shape
    plane, column = 4 * zs - 1, GROUPS * zs - 1

    def body(kv, w1s, w2s, wms, kv_all, w1, w2, wm, send, recv, local, swap_send, swap_recv):
        me = Place(zs)
        copies = Copies(send, recv, local)
        crossing = me.c != me.y
        greet(
            [me.at(x=to[0], z=to[1], y=to[2]) for to, _ in me.plane()]
            + [me.at(z=to[0], g=to[1]) for to, _ in me.column()]
            + [me.at(z=to[0], g=to[1], c=me.y, y=me.c) for to, _ in me.column()]
            + [me.sibling()],
            me.at(c=me.y, y=me.c),
            crossing,
        )

        def here(ref):
            return ref.at[me.x, me.c, me.z, me.g, me.y]

        flat = me.plane(everywhere=False)
        own = [
            copies.keep(w1s.at[me.x * 2 + me.y], here(w1)),
            copies.keep(wms, here(wm)),
            copies.keep(kv, kv_all.at[me.x, me.c, me.z, :, me.y]),
        ]
        w1_first = [
            copies.push(w1s.at[to[0] * 2 + to[2]], here(w1), me.at(x=to[0], y=to[2]))
            for to, _ in flat
        ]
        wm_first = [
            copies.push(wms, here(wm), me.at(z=to[0], g=to[1])) for to, _ in me.column()
        ]
        mine = kv_all.at[me.x, me.c, me.z, :, me.y]
        kv_first = [
            copies.push(kv, mine, me.at(x=to[0], z=to[1], y=to[2])) for to, _ in me.plane()
        ]
        arrivals = [copies.push(kv, mine, me.sibling())]
        w2_first = [
            copies.push(
                w2s, w2.at[me.z, me.g, me.y], me.at(z=to[0], g=to[1], c=me.y, y=me.c)
            )
            for to, _ in me.column()
        ]
        exchanged = pltpu.make_async_remote_copy(
            src_ref=w2s,
            dst_ref=w2.at[me.z, me.g, me.y],
            send_sem=swap_send,
            recv_sem=swap_recv,
            device_id=me.at(c=me.y, y=me.c),
            device_id_type=MESH,
        )
        stays = pltpu.make_async_copy(w2s, w2.at[me.z, me.g, me.y], swap_recv)

        @pl.when(crossing)
        def _():
            exchanged.start()

        @pl.when(jnp.logical_not(crossing))
        def _():
            stays.start()

        own[0].wait()
        for copy in w1_first:
            copy.wait_recv()
        block = w1.at[:, me.c, me.z, me.g, :]
        w1_second = [
            copies.push(block, block, me.at(z=to[0], g=to[1])) for to, _ in me.column()
        ]
        arrivals.append(copies.push(block, block, me.sibling()))
        own[1].wait()
        for copy in wm_first:
            copy.wait_recv()
        block = wm.at[me.x, me.c, :, :, me.y]
        wm_second = [copies.push(block, block, me.at(x=to[0], y=to[2])) for to, _ in flat]
        arrivals.append(copies.push(block, block, me.sibling()))
        for copy, (_, source) in zip(kv_first, me.plane()):
            copy.wait_recv()
            part = kv_all.at[source[0], me.c, source[1], :, source[2]]
            arrivals.append(copies.push(part, part, me.sibling()))

        @pl.when(crossing)
        def _():
            exchanged.wait_recv()
            exchanged.wait_send()

        @pl.when(jnp.logical_not(crossing))
        def _():
            stays.wait()

        part = w2.at[me.z, me.g, me.c]
        arrivals.append(copies.push(part, part, me.sibling()))
        for copy, (_, source) in zip(wm_second, flat):
            copy.wait_recv()
            part = wm.at[source[0], me.c, :, :, source[2]]
            arrivals.append(copies.push(part, part, me.sibling()))
        for copy, (_, source) in zip(w2_first, me.column()):
            copy.wait_recv()
            part = w2.at[source[0], source[1], me.c]
            arrivals.append(copies.push(part, part, me.sibling()))
        for copy, (_, source) in zip(w1_second, me.column()):
            copy.wait_recv()
            part = w1.at[:, me.c, source[0], source[1], :]
            arrivals.append(copies.push(part, part, me.sibling()))
        for copy in arrivals:
            copy.wait_recv()
        own[2].wait()
        copies.finish()

    return comm_call(
        body,
        "spread_keys",
        1,
        [
            jax.ShapeDtypeStruct((2, 2, zs, GROUPS, 2, n, width), low_type),
            jax.ShapeDtypeStruct((2, 2, zs, GROUPS, 2, rows, columns), low_type),
            jax.ShapeDtypeStruct((zs, GROUPS, 2, tall, columns), low_type),
            jax.ShapeDtypeStruct((2, 2, zs, GROUPS, 2) + mix.shape, low_type),
        ],
        2 * plane + 1 + 2 * (3 + column + 1 + column) + column + 3 + 8,
        3,
        (keys, inner, outer, mix),
        scratch=(pltpu.SemaphoreType.DMA, pltpu.SemaphoreType.DMA),
    )


def exchange_line(zs, ident, pieces):
    def body(source, target, send, recv, local):
        me = Place(zs)
        copies = Copies(send, recv, local)
        greet([me.at(g=to) for to, _ in me.line()])
        arrivals = [
            copies.push(source.at[to], target.at[me.g], me.at(g=to)) for to, _ in me.line()
        ]
        own = copies.keep(source.at[me.g], target.at[me.g])
        for copy in arrivals:
            copy.wait_recv()
        own.wait()
        copies.finish()

    return comm_call(
        body,
        "exchange_line",
        ident,
        [jax.ShapeDtypeStruct(pieces.shape, pieces.dtype)],
        GROUPS - 1,
        1,
        (pieces,),
    )[0]


def gather_square(zs, ident, rows):
    def body(source, target, send, recv, local):
        me = Place(zs)
        copies = Copies(send, recv, local)
        flat = me.plane(everywhere=False)
        greet([me.at(x=to[0], y=to[2]) for to, _ in flat])
        place = target.at[me.x, me.y]
        arrivals = [copies.push(source, place, me.at(x=to[0], y=to[2])) for to, _ in flat]
        own = copies.keep(source, place)
        for copy in arrivals:
            copy.wait_recv()
        own.wait()
        copies.finish()

    return comm_call(
        body,
        "gather_square",
        ident,
        [jax.ShapeDtypeStruct((2, 2) + rows.shape, rows.dtype)],
        3,
        1,
        (rows,),
    )[0]


def exchange_square(zs, ident, pieces):
    def body(source, target, send, recv, local):
        me = Place(zs)
        copies = Copies(send, recv, local)
        flat = me.plane(everywhere=False)
        greet([me.at(x=to[0], y=to[2]) for to, _ in flat])
        place = target.at[me.x, me.y]
        arrivals = [
            copies.push(source.at[to[0], to[2]], place, me.at(x=to[0], y=to[2]))
            for to, _ in flat
        ]
        own = copies.keep(source.at[me.x, me.y], place)
        for copy in arrivals:
            copy.wait_recv()
        own.wait()
        copies.finish()

    return comm_call(
        body,
        "exchange_square",
        ident,
        [jax.ShapeDtypeStruct(pieces.shape, pieces.dtype)],
        3,
        1,
        (pieces,),
    )[0]


def loop(count, step):
    def body(index, carry):
        step(index)
        return carry

    lax.fori_loop(0, count, body, 0)


def total_of(*values):
    result = values[0].astype(wide)
    for value in values[1:]:
        result = result + value.astype(wide)
    return result


def reduce_keys(zs, dkv, grad1, grad2, gradm):
    n, width = dkv.shape[-2:]
    rows, columns = grad1.shape[-2:]
    rowsm = gradm.shape[-2]
    tall = grad2.shape[-2]
    plane, column = 4 * zs - 1, GROUPS * zs - 1
    count = GROUPS * zs

    def body(
        dkv_ref, g1, g2, gm, dkv_out, out1, out2, outm,
        send, recv, local,
        swap_send, swap_recv, kst, s1, p1, f1, s2, p2, sm, pm, fm, tm,
    ):
        me = Place(zs)
        copies = Copies(send, recv, local)
        crossing = me.c != me.y
        greet(
            [me.at(x=to[0], z=to[1], y=to[2]) for to, _ in me.plane()]
            + [me.at(z=to[0], g=to[1]) for to, _ in me.column()]
            + [me.at(z=to[0], g=to[1], c=me.y, y=me.c) for to, _ in me.column()]
            + [me.sibling()],
            me.at(c=me.y, y=me.c),
            crossing,
        )

        flat = me.plane(everywhere=False)
        other = 1 - me.c
        order = [to for to, _ in me.plane()] + [(me.x, me.z, me.y)]
        w1_half = copies.push(g1.at[:, other], s1, me.sibling())
        w2_half = copies.push(g2.at[:, :, other], s2, me.sibling())
        k_half = [
            copies.push(
                dkv_ref.at[to[0], other, to[1], :, to[2]], kst.at[to[0], to[1], to[2]], me.sibling()
            )
            for to in order
        ]
        wm_half = copies.push(gm.at[:, other], sm, me.sibling())

        w1_half.wait_recv()

        def add1(index):
            x, z, g, y = index // (count * 2), index // (GROUPS * 2) % zs, index // 2 % GROUPS, index % 2
            s1[x, z, g, y] = total_of(s1[x, z, g, y], g1[x, me.c, z, g, y]).astype(low_type)

        loop(4 * count, add1)
        w1_push = [
            copies.push(s1.at[:, to[0], to[1], :], p1.at[slot], me.at(z=to[0], g=to[1]))
            for slot, (to, _) in enumerate(me.column())
        ]
        w2_half.wait_recv()

        def add2(index):
            z, g = index // GROUPS, index % GROUPS
            s2[z, g] = total_of(s2[z, g], g2[z, g, me.c]).astype(low_type)

        loop(count, add2)
        w2_push = [
            copies.push(
                s2.at[to[0], to[1]], p2.at[slot + 1], me.at(z=to[0], g=to[1], c=me.y, y=me.c)
            )
            for slot, (to, _) in enumerate(me.column())
        ]
        exchanged = pltpu.make_async_remote_copy(
            src_ref=s2.at[me.z, me.g],
            dst_ref=p2.at[0],
            send_sem=swap_send,
            recv_sem=swap_recv,
            device_id=me.at(c=me.y, y=me.c),
            device_id_type=MESH,
        )
        stays = pltpu.make_async_copy(s2.at[me.z, me.g], p2.at[0], swap_recv)

        @pl.when(crossing)
        def _():
            exchanged.start()

        @pl.when(jnp.logical_not(crossing))
        def _():
            stays.start()

        k_push = []
        for slot, to in enumerate(order):
            k_half[slot].wait_recv()

            def addk(g, to=to):
                kst[to[0], to[1], to[2], g] = total_of(
                    kst[to[0], to[1], to[2], g], dkv_ref[to[0], me.c, to[1], g, to[2]]
                ).astype(low_type)

            loop(GROUPS, addk)
            if slot < plane:
                k_push.append(
                    copies.push(
                        kst.at[to[0], to[1], to[2]],
                        dkv_out.at[slot],
                        me.at(x=to[0], z=to[1], y=to[2]),
                    )
                )
        wm_half.wait_recv()

        def addm(index):
            x, z, g, y = index // (count * 2), index // (GROUPS * 2) % zs, index // 2 % GROUPS, index % 2
            sm[x, z, g, y] = total_of(sm[x, z, g, y], gm[x, me.c, z, g, y]).astype(low_type)

        loop(4 * count, addm)
        wm_push = [
            copies.push(sm.at[to[0], :, :, to[2]], pm.at[slot], me.at(x=to[0], y=to[2]))
            for slot, (to, _) in enumerate(flat)
        ]
        keep = copies.keep(kst.at[me.x, me.z, me.y], dkv_out.at[plane])
        for copy in wm_push:
            copy.wait_recv()

        def addf(index):
            z, g = index // GROUPS, index % GROUPS
            fm[z, g] = total_of(sm[me.x, z, g, me.y], pm[0, z, g], pm[1, z, g], pm[2, z, g]).astype(
                low_type
            )

        loop(count, addf)
        wm_last = [
            copies.push(fm.at[to[0], to[1]], tm.at[slot], me.at(z=to[0], g=to[1]))
            for slot, (to, _) in enumerate(me.column())
        ]
        for copy in w1_push:
            copy.wait_recv()

        def addg(index):
            x, y = index // 2, index % 2
            f1[x, y] = total_of(
                s1[x, me.z, me.g, y], *[p1[slot, x, y] for slot in range(column)]
            ).astype(low_type)

        loop(4, addg)
        quarter = out1.at[me.x * 2 + me.y]
        w1_last = [
            copies.push(f1.at[to[0], to[2]], quarter, me.at(x=to[0], y=to[2])) for to, _ in flat
        ]
        keep1 = copies.keep(f1.at[me.x, me.y], quarter)

        @pl.when(crossing)
        def _():
            exchanged.wait_recv()
            exchanged.wait_send()

        @pl.when(jnp.logical_not(crossing))
        def _():
            stays.wait()

        for copy in w2_push:
            copy.wait_recv()
        out2[...] = total_of(*[p2[slot] for slot in range(column + 1)])
        for copy in wm_last:
            copy.wait_recv()
        outm[...] = total_of(fm[me.z, me.g], *[tm[slot] for slot in range(column)])
        for copy in w1_last + k_push:
            copy.wait_recv()
        keep.wait()
        keep1.wait()
        copies.finish()

    vmem = pltpu.VMEM
    return comm_call(
        body,
        "reduce_keys",
        8,
        [
            jax.ShapeDtypeStruct((plane + 1, GROUPS, n, width), low_type),
            jax.ShapeDtypeStruct((4, rows, columns), low_type),
            jax.ShapeDtypeStruct((tall, columns), wide),
            jax.ShapeDtypeStruct((rowsm, columns), wide),
        ],
        3 + (plane + 1) + 2 * column + plane + 3 + column + 3,
        2,
        (dkv, grad1, grad2, gradm),
        spaces=[vmem] * 4,
        out_spaces=[pl.ANY, pl.ANY, vmem, vmem],
        scratch=(
            pltpu.SemaphoreType.DMA,
            pltpu.SemaphoreType.DMA,
            vmem((2, zs, 2, GROUPS, n, width), low_type),
            vmem((2, zs, GROUPS, 2, rows, columns), low_type),
            vmem((column, 2, 2, rows, columns), low_type),
            vmem((2, 2, rows, columns), low_type),
            vmem((zs, GROUPS, tall, columns), low_type),
            vmem((column + 1, tall, columns), low_type),
            vmem((2, zs, GROUPS, 2, rowsm, columns), low_type),
            vmem((3, zs, GROUPS, rowsm, columns), low_type),
            vmem((zs, GROUPS, rowsm, columns), low_type),
            vmem((column, rowsm, columns), low_type),
        ),
    )


def reduce_tokens(zs, dx, gradq):
    rows, columns = gradq.shape[-2:]
    plane = 4 * zs - 1
    count = GROUPS * zs

    def body(dx_ref, gq, dx_out, outq, send, recv, local, sq, pq, fq):
        me = Place(zs)
        copies = Copies(send, recv, local)
        greet(
            [me.at(g=to) for to, _ in me.line()]
            + [me.at(x=to[0], z=to[1], y=to[2]) for to, _ in me.plane()]
            + [me.sibling()]
        )
        half = copies.push(gq.at[:, 1 - me.c], sq, me.sibling())
        arrivals = [
            copies.push(dx_ref.at[to], dx_out.at[me.g], me.at(g=to)) for to, _ in me.line()
        ]
        own = copies.keep(dx_ref.at[me.g], dx_out.at[me.g])
        half.wait_recv()

        def add1(index):
            x, z, g, y = index // (count * 2), index // (GROUPS * 2) % zs, index // 2 % GROUPS, index % 2
            sq[x, z, g, y] = total_of(sq[x, z, g, y], gq[x, me.c, z, g, y]).astype(low_type)

        loop(4 * count, add1)
        second = [
            copies.push(
                sq.at[to[0], to[1], :, to[2]], pq.at[slot], me.at(x=to[0], z=to[1], y=to[2])
            )
            for slot, (to, _) in enumerate(me.plane())
        ]
        for copy in second:
            copy.wait_recv()

        def add2(g):
            fq[g] = total_of(
                sq[me.x, me.z, g, me.y], *[pq[slot, g] for slot in range(plane)]
            ).astype(low_type)

        loop(GROUPS, add2)
        arrivals += [
            copies.push(fq.at[to], outq.at[me.g], me.at(g=to)) for to, _ in me.line()
        ]
        keep = copies.keep(fq.at[me.g], outq.at[me.g])
        for copy in arrivals:
            copy.wait_recv()
        own.wait()
        keep.wait()
        copies.finish()

    vmem = pltpu.VMEM
    return comm_call(
        body,
        "reduce_tokens",
        9,
        [
            jax.ShapeDtypeStruct(dx.shape, low_type),
            jax.ShapeDtypeStruct((GROUPS, rows, columns), low_type),
        ],
        1 + 2 * (GROUPS - 1) + plane,
        2,
        (dx, gradq),
        spaces=[pl.ANY, vmem],
        scratch=(
            vmem((2, zs, GROUPS, 2, rows, columns), low_type),
            vmem((plane, GROUPS, rows, columns), low_type),
            vmem((GROUPS, rows, columns), low_type),
        ),
    )


NEXT = (((1,), (1,)), ((), ()))
DOWN = (((0,), (0,)), ((), ()))


def attend_forward(queries, keys, bounds, low, high, tile, block):
    total_rows = queries.shape[0]

    def body(bounds_ref, q_ref, kv_ref, low_ref, high_ref, out_ref, keep_ref, lse_ref):
        def one(turn, unused):
            rows = pl.ds(pl.multiple_of(turn * tile, tile), tile)
            first, last = low_ref[rows, :], high_ref[rows, :]
            heads = [
                q_ref[rows, h * LANES : (h + 1) * LANES] * jnp.asarray(0.125, low_type)
                for h in range(LOCAL)
            ]

            def step(j, carry):
                begin = pl.multiple_of(j * block, block)
                place = begin + lax.broadcasted_iota(jnp.int32, (tile, block), 1)
                same = (place >= first) & (place < last)
                result = []
                for h in range(LOCAL):
                    top, total, mixed = carry[h]
                    kv = kv_ref[pl.ds(begin, block), h * LANES : (h + 1) * LANES]
                    scores = lax.dot_general(heads[h], kv, NEXT, preferred_element_type=wide)
                    scores = jnp.where(same, scores, mask_fill)
                    new_top = jnp.maximum(top, jnp.max(scores, axis=1, keepdims=True))
                    factor = jnp.exp(top - new_top)
                    powers = jnp.exp(scores - new_top)
                    total = total * factor + jnp.sum(powers, axis=1, keepdims=True)
                    mixed = mixed * factor + jnp.dot(
                        powers.astype(low_type), kv, preferred_element_type=wide
                    )
                    result.append((new_top, total, mixed))
                return tuple(result)

            start = tuple(
                (
                    jnp.full((tile, 1), lowest_start, wide),
                    jnp.zeros((tile, 1), wide),
                    jnp.zeros((tile, LANES), wide),
                )
                for _ in range(LOCAL)
            )
            done = lax.fori_loop(bounds_ref[turn, 0], bounds_ref[turn, 1], step, start)
            lane = lax.broadcasted_iota(jnp.int32, (tile, LANES), 1)
            upper = lane >= HEAD
            mixes = [mixed / total for _, total, mixed in done]
            turned = [pltpu.roll(mixed, HEAD, 1) for mixed in mixes]
            front = jnp.where(upper, mixes[1], turned[0])
            back = jnp.where(upper, 0.0, turned[2])
            both = jnp.concatenate([front, back], axis=1)
            keep_ref[rows, :] = both
            out_ref[rows, :] = both.astype(low_type)
            ends = [top + jnp.log(total) for top, total, _ in done]
            lse_ref[rows, :] = jnp.where(lane == 0, ends[0], jnp.where(lane == 1, ends[1], ends[2]))
            return unused

        lax.fori_loop(0, total_rows // tile, one, 0)

    vmem = pl.BlockSpec(memory_space=pltpu.VMEM)
    return pl.pallas_call(
        body,
        name="attend_forward",
        out_shape=(
            jax.ShapeDtypeStruct((total_rows, PACK), low_type),
            jax.ShapeDtypeStruct((total_rows, PACK), wide),
            jax.ShapeDtypeStruct((total_rows, LANES), wide),
        ),
        in_specs=[pl.BlockSpec(memory_space=pltpu.SMEM)] + [vmem] * 4,
        out_specs=(vmem,) * 3,
        compiler_params=pltpu.CompilerParams(vmem_limit_bytes=VMEM_LIMIT),
    )(bounds, queries, keys, low, high)


def attend_backward(queries, keys, grads, stats, bounds, tile, block):
    total_rows = queries.shape[0]
    tokens = keys.shape[0]

    def body(bounds_ref, q_ref, kv_ref, do_ref, stat_ref, dq_ref, dkv_ref, sums):
        h = pl.program_id(0)
        zeros = jnp.zeros((block, LANES), wide)

        def clear(j, unused):
            sums[pl.ds(pl.multiple_of(j * block, block), block), :] = zeros
            return unused

        lax.fori_loop(0, tokens // block, clear, 0)
        lane = lax.broadcasted_iota(jnp.int32, (tile, LANES), 1)
        upper = lane >= HEAD

        def one(turn, unused):
            rows = pl.ds(pl.multiple_of(turn * tile, tile), tile)
            q = q_ref[rows, :] * jnp.asarray(0.125, low_type)
            front = do_ref[rows, :LANES].astype(wide)
            back = do_ref[rows, LANES:].astype(wide)
            grad = jnp.where(h == 1, front, pltpu.roll(jnp.where(h == 0, front, back), HEAD, 1))
            grad = jnp.where(upper, grad, 0.0).astype(low_type)
            stat = stat_ref[turn, 0]
            first, last = stat[0:1, :], stat[1:2, :]
            lse, delta = stat[2:3, :], stat[3:4, :]

            def step(j, total):
                begin = pl.multiple_of(j * block, block)
                place = (begin + lax.broadcasted_iota(jnp.int32, (block, tile), 0)).astype(wide)
                same = (place >= first) & (place < last)
                kv = kv_ref[pl.ds(begin, block), :]
                scores = lax.dot_general(kv, q, NEXT, preferred_element_type=wide)
                probs = jnp.exp(jnp.where(same, scores, mask_fill) - lse)
                dots = lax.dot_general(kv, grad, NEXT, preferred_element_type=wide)
                score_grad = (probs * (dots - delta)).astype(low_type)
                sums[pl.ds(begin, block), :] += jnp.dot(
                    score_grad, q, preferred_element_type=wide
                ) + jnp.dot(probs.astype(low_type), grad, preferred_element_type=wide)
                return total + lax.dot_general(score_grad, kv, DOWN, preferred_element_type=wide)

            total = lax.fori_loop(
                bounds_ref[turn, 0], bounds_ref[turn, 1], step, jnp.zeros((tile, LANES), wide)
            )
            dq_ref[rows, :] = jnp.where(upper, 0.0, total * 0.125).astype(low_type)
            return unused

        lax.fori_loop(0, total_rows // tile, one, 0)

        def store(j, unused):
            part = pl.ds(pl.multiple_of(j * block, block), block)
            dkv_ref[part, :] = sums[part, :].astype(low_type)
            return unused

        lax.fori_loop(0, tokens // block, store, 0)

    return pl.pallas_call(
        body,
        name="attend_backward",
        grid=(LOCAL,),
        out_shape=(
            jax.ShapeDtypeStruct((total_rows, WIDE), low_type),
            jax.ShapeDtypeStruct((tokens, WIDE), low_type),
        ),
        in_specs=[
            pl.BlockSpec(memory_space=pltpu.SMEM),
            pl.BlockSpec((total_rows, LANES), lambda h: (0, h)),
            pl.BlockSpec((tokens, LANES), lambda h: (0, h)),
            pl.BlockSpec((total_rows, PACK), lambda h: (0, 0)),
            pl.BlockSpec((total_rows // tile, 1, 8, tile), lambda h: (0, h, 0, 0)),
        ],
        out_specs=(
            pl.BlockSpec((total_rows, LANES), lambda h: (0, h)),
            pl.BlockSpec((tokens, LANES), lambda h: (0, h)),
        ),
        scratch_shapes=[pltpu.VMEM((tokens, LANES), wide)],
        compiler_params=pltpu.CompilerParams(vmem_limit_bytes=VMEM_LIMIT),
    )(bounds, queries, keys, grads, stats)


class Spot(Place):
    def __init__(self):
        super().__init__(1)
        self.half = self.g // 2
        self.a = self.x * 2 + self.c
        self.p = (self.x + self.c) % 2
        self.selfish = self.g % 2 == self.p
        self.crossing = self.c != self.y

    def square(self):
        return [(to[0], to[2]) for to, _ in self.plane()]

    def readers(self):
        result = []
        for k in range(GROUPS):
            g = (self.g + k) % GROUPS
            result.append((g, self.at(x=(self.g + self.c) % 2, g=g)))
        return result

    def owners(self):
        result = []
        for dv in range(2):
            for du in range(2):
                u, v = (self.x + du) % 2, (self.half + dv) % 2
                result.append((u * 2 + v, self.at(x=u, g=2 * v + self.p)))
        return result

    def slot(self):
        return self.x * 2 + self.half


def count_of(flag):
    return jnp.where(flag, 1, 0)


def announce(always, maybe):
    barrier = pltpu.get_barrier_semaphore()
    for device in always:
        pl.semaphore_signal(barrier, inc=1, device_id=device, device_id_type=MESH)
    for flag, device in maybe:

        @pl.when(flag)
        def _(device=device):
            pl.semaphore_signal(barrier, inc=1, device_id=device, device_id_type=MESH)

    total = len(always)
    for flag, _ in maybe:
        total = total + count_of(flag)
    return barrier, total


class Scatter:
    def __init__(self, send, recv, here):
        self.send, self.recv, self.here = send, recv, here
        self.copies = []

    def start(self, pieces, target, slot):
        for source, device in pieces:
            self.send_one(source, target, slot, device)

    def send_one(self, source, target, slot, device):
        index = len(self.copies)
        copy = pltpu.make_async_remote_copy(
            src_ref=source,
            dst_ref=target,
            send_sem=self.send.at[index],
            recv_sem=self.recv.at[slot],
            device_id=device,
            device_id_type=MESH,
        )
        self.copies.append(copy)
        if index:
            copy.start()
            return
        stay = pltpu.make_async_copy(source, target, self.recv.at[slot])

        @pl.when(self.here)
        def _():
            stay.start()

        @pl.when(jnp.logical_not(self.here))
        def _():
            copy.start()

    def arrived(self, slot, target):
        pltpu.make_async_copy(target, target, self.recv.at[slot]).wait()

    def finish(self):
        for copy in self.copies[1:]:
            copy.wait_send()

        @pl.when(jnp.logical_not(self.here))
        def _():
            self.copies[0].wait_send()


SMALL = 16


def first_tables(s, e, width):
    column = np.arange(width)
    rows = [column % s, column // s, column % e, column // e]
    return np.stack(rows + [np.zeros_like(column)] * 4).astype(np.int32)


def first_kernel(tokens, wq, wk, wv, vectors, inner, mix, e):
    n, depth = tokens.shape
    s = wq.shape[0]
    quarter = inner.shape[1] // 4
    cols = 2 * WIDE + LANES
    tables = jnp.asarray(first_tables(s, e, 2 * WIDE))
    count = len(vectors)

    def body(*refs):
        tok, wq_ref, wk_ref, wv_ref, tab = refs[:5]
        vecs = refs[5 : 5 + count]
        w1f, wmf = refs[5 + count : 7 + count]
        (
            tok_out, q_out, wqkv_out, vec_out, kv_all, w1, wm,
            send, recv, local, tok_send, tok_recv,
            slab, toks, weights, kv_own, q_own, w1s, wms, vec, few,
        ) = refs[7 + count :]
        me = Spot()
        copies = Copies(send, recv, local)
        square = me.square()
        line = [to for to, _ in me.line()]
        sources = [device for _, device in me.owners()]
        barrier, expected = announce(
            [me.at(x=x, y=y) for x, y in square]
            + [me.at(g=to) for to in line]
            + sources[1:]
            + [me.sibling()],
            [(jnp.logical_not(me.selfish), sources[0])],
        )
        lane = lax.broadcasted_iota(jnp.int32, (s, LANES), 1)
        lower = lane < HEAD
        for head in range(HEADS):
            pair = slice(head // 2 * LANES, head // 2 * LANES + LANES)
            q, k, v = wq_ref[:, pair], wk_ref[:, pair], wv_ref[:, pair]
            if head % 2:
                q, k = pltpu.roll(q, HEAD, 1), pltpu.roll(k, HEAD, 1)
            else:
                v = pltpu.roll(v, HEAD, 1)
            g, h = head // LOCAL, head % LOCAL
            slab[g, :, h * LANES : (h + 1) * LANES] = jnp.where(lower, k, v).astype(low_type)
            slab[g, :, WIDE + h * LANES : WIDE + (h + 1) * LANES] = jnp.where(lower, q, 0.0).astype(
                low_type
            )
        wms[...] = wmf[...].astype(low_type)
        few[...] = jnp.zeros((s, LANES), wide)
        for index in range(count):
            few[index : index + 1, : vecs[index].shape[1]] = vecs[index][...]
        small = few[...]
        for g in range(GROUPS):
            slab[g, :, 2 * WIDE :] = small.astype(low_type)
        pl.semaphore_wait(barrier, expected)

        view = weights
        place = view.at[me.a, me.g, me.y]
        slab_first = [copies.push(slab.at[to], place, me.at(g=to)) for to in line]
        slab_own = copies.keep(slab.at[me.g], place)
        for w in range(4):
            w1s[w] = w1f[:, w * quarter : (w + 1) * quarter].astype(low_type)
        place = w1.at[me.x, me.c, me.g, me.y]
        w1_first = [
            copies.push(w1s.at[x * 2 + y], place, me.at(x=x, y=y)) for x, y in square
        ]
        w1_own = copies.keep(w1s.at[me.x * 2 + me.y], place)
        wm_own = copies.keep(wms, wm.at[me.x, me.c, me.g, me.y])

        arrivals, weight_arrivals = [], []
        slab_own.wait()
        for copy in slab_first:
            copy.wait_recv()
        wm_first = [
            copies.push(wms, wm.at[me.x, me.c, me.g, me.y], me.at(g=to)) for to in line
        ]
        tokens_go = Scatter(tok_send, tok_recv, me.selfish)
        tokens_go.start([(tok, device) for _, device in me.readers()], toks.at[me.slot()], me.slot())
        block = view.at[me.a, :, me.y]
        slab_second = [copies.push(block, block, me.at(x=x, y=y)) for x, y in square]
        weight_arrivals.append(copies.push(block, block, me.sibling()))
        for copy, (x, y) in zip(slab_second, square):
            copy.wait_recv()
            block = view.at[x * 2 + me.c, :, y]
            weight_arrivals.append(copies.push(block, block, me.sibling()))
        wm_own.wait()
        for copy in wm_first:
            copy.wait_recv()
        block = wm.at[me.x, me.c, :, me.y]
        wm_second = [copies.push(block, block, me.at(x=x, y=y)) for x, y in square]
        arrivals.append(copies.push(block, block, me.sibling()))
        w1_own.wait()
        for copy in w1_first:
            copy.wait_recv()
        for copy in weight_arrivals:
            copy.wait_recv()

        table = tab[...]

        def spread(pieces, within, owner):
            count = pieces.shape[0] * SMALL
            item = lax.broadcasted_iota(jnp.int32, (count, 2 * WIDE), 0)
            index = lax.broadcasted_iota(jnp.int32, (LANES, 2 * WIDE), 0)
            chosen = jnp.where(index == within, 1.0, 0.0).astype(low_type)
            pieces = pieces.astype(wide).reshape(count, LANES).astype(low_type)
            found = jnp.dot(pieces, chosen, preferred_element_type=wide)
            found = jnp.where((item >> 4) == owner, found, 0.0)
            return jnp.sum(found.reshape(count // SMALL, SMALL, 2 * WIDE), axis=0)

        every = spread(
            view[:, :, :, :SMALL, 2 * WIDE :].reshape(32, SMALL, LANES), table[0:1], table[1:2]
        )
        w_me = me.x * 2 + me.y
        inner_bias = spread(
            view[w_me, :, :, :SMALL, 2 * WIDE :].reshape(8, SMALL, LANES), table[2:3], table[3:4]
        )
        rows16 = lax.broadcasted_iota(jnp.int32, (SMALL, 2 * WIDE), 0)
        vec[...] = jnp.where(rows16 == 8, inner_bias, every)
        turned = pltpu.roll(every, 2 * WIDE - me.g * LOCAL * HEAD, 1)
        lower = lax.broadcasted_iota(jnp.int32, (1, LANES), 1) < HEAD
        biases = [[], []]
        for h in range(LOCAL):
            pair = slice(h // 2 * LANES, h // 2 * LANES + LANES)
            q, v = turned[0:1, pair], turned[1:2, pair]
            if h % 2:
                q = pltpu.roll(q, HEAD, 1)
            else:
                v = pltpu.roll(v, HEAD, 1)
            biases[0].append(jnp.where(lower, 0.0, v))
            biases[1].append(jnp.where(lower, q, 0.0))
        bias = jnp.concatenate(biases[0] + biases[1], axis=1)

        matrix = weights[:, :, :, :, : 2 * WIDE].reshape(depth, 2 * WIDE)
        kept, kv_first = [copies.keep(weights, wqkv_out), copies.keep(vec, vec_out)], []
        for dv in range(2):
            v = (me.half + dv) % 2
            for u in range(2):
                tokens_go.arrived(u * 2 + v, toks.at[u * 2 + v])
            if dv:
                block = w1.at[:, me.c, me.g, :]
                w1_second = [copies.push(block, block, me.at(g=to)) for to in line]
            both = jnp.concatenate([toks[v], toks[2 + v]], axis=0)
            made = jnp.dot(both, matrix, preferred_element_type=wide)
            made = (made + bias).astype(low_type)
            for u in range(2):
                kv_own[v, u] = made[u * n : (u + 1) * n, :WIDE]
                q_own[u * 2 + v] = made[u * n : (u + 1) * n, WIDE:]
            mine = kv_all.at[:, me.c, v, me.p, me.y]
            kv_first.append(
                [copies.push(kv_own.at[v], mine, me.at(x=x, y=y)) for x, y in square]
            )
            arrivals.append(copies.push(kv_own.at[v], mine, me.sibling()))
            kept.append(copies.keep(kv_own.at[v], mine))
        block = w1.at[:, me.c, me.g, :]
        arrivals.append(copies.push(block, block, me.sibling()))
        kept += [copies.keep(toks, tok_out), copies.keep(q_own, q_out)]
        for dv in range(2):
            v = (me.half + dv) % 2
            for copy, (x, y) in zip(kv_first[dv], square):
                copy.wait_recv()
                block = kv_all.at[:, me.c, v, (x + me.c) % 2, y]
                arrivals.append(copies.push(block, block, me.sibling()))
        for copy, (x, y) in zip(wm_second, square):
            copy.wait_recv()
            block = wm.at[x, me.c, :, y]
            arrivals.append(copies.push(block, block, me.sibling()))
        for copy, (_, source) in zip(w1_second, me.line()):
            copy.wait_recv()
            block = w1.at[:, me.c, source, :]
            arrivals.append(copies.push(block, block, me.sibling()))
        for copy in arrivals:
            copy.wait_recv()
        for copy in kept:
            copy.wait()
        tokens_go.finish()
        copies.finish()

    vmem = pltpu.VMEM
    dma = pltpu.SemaphoreType.DMA
    total = 64
    return pl.pallas_call(
        body,
        name="first_kernel",
        out_shape=(
            jax.ShapeDtypeStruct((GROUPS, n, depth), low_type),
            jax.ShapeDtypeStruct((GROUPS, n, WIDE), low_type),
            jax.ShapeDtypeStruct((4, GROUPS, 2, s, cols), low_type),
            jax.ShapeDtypeStruct((SMALL, 2 * WIDE), wide),
            jax.ShapeDtypeStruct((2, 2, 2, 2, 2, n, WIDE), low_type),
            jax.ShapeDtypeStruct((2, 2, GROUPS, 2, s, quarter), low_type),
            jax.ShapeDtypeStruct((2, 2, GROUPS, 2, s, depth), low_type),
        ),
        in_specs=[pl.BlockSpec(memory_space=vmem)] * (7 + count),
        out_specs=(pl.BlockSpec(memory_space=pl.ANY),) * 7,
        scratch_shapes=[
            dma((total,)), dma((total,)), dma((12,)), dma((4,)), dma((4,)),
            vmem((GROUPS, s, cols), low_type),
            vmem((GROUPS, n, depth), low_type),
            vmem((4, GROUPS, 2, s, cols), low_type),
            vmem((2, 2, n, WIDE), low_type),
            vmem((GROUPS, n, WIDE), low_type),
            vmem((4, s, quarter), low_type),
            vmem((s, depth), low_type),
            vmem((SMALL, 2 * WIDE), wide),
            vmem((s, LANES), wide),
        ],
        compiler_params=pltpu.CompilerParams(
            collective_id=10, has_side_effects=True, vmem_limit_bytes=VMEM_LIMIT
        ),
    )(tokens, wq, wk, wv, tables, *vectors, inner, mix)


def pass_back(ident, pieces):
    def body(source, target, send, recv):
        me = Spot()
        owners = me.owners()
        readers = [device for _, device in me.readers()]
        barrier, expected = announce(readers[1:], [(jnp.logical_not(me.selfish), readers[0])])
        pl.semaphore_wait(barrier, expected)
        move = Scatter(send, recv, me.selfish)
        move.start([(source.at[slot], device) for slot, device in owners], target.at[me.g], me.g)
        for g in range(GROUPS):
            move.arrived(g, target.at[g])
        move.finish()

    return scatter_call(body, "pass_back", ident, pieces)


def pass_on(ident, pieces):
    def body(source, target, send, recv):
        me = Spot()
        owners = [device for _, device in me.owners()]
        barrier, expected = announce(owners[1:], [(jnp.logical_not(me.selfish), owners[0])])
        pl.semaphore_wait(barrier, expected)
        move = Scatter(send, recv, me.selfish)
        slot = me.slot()
        move.start([(source.at[g], device) for g, device in me.readers()], target.at[slot], slot)
        for index in range(GROUPS):
            move.arrived(index, target.at[index])
        move.finish()

    return scatter_call(body, "pass_on", ident, pieces)


def scatter_call(body, name, ident, pieces):
    return pl.pallas_call(
        body,
        name=name,
        out_shape=jax.ShapeDtypeStruct(pieces.shape, pieces.dtype),
        in_specs=[pl.BlockSpec(memory_space=pl.ANY)],
        out_specs=pl.BlockSpec(memory_space=pl.ANY),
        scratch_shapes=[pltpu.SemaphoreType.DMA((4,)), pltpu.SemaphoreType.DMA((4,))],
        compiler_params=pltpu.CompilerParams(
            collective_id=ident, has_side_effects=True, vmem_limit_bytes=VMEM_LIMIT
        ),
    )(pieces)


def last_kernel(dkv, dq, tokens, weights, sum1, gradm):
    n = dq.shape[1]
    depth = tokens.shape[-1]
    s = depth // 32
    rows = s + 8
    cut = depth // 2

    def body(
        dkv_ref, dq_ref, tok, w_ref, s1, gm, dx_out, outq, outk, out1, outm,
        send, recv, local, dx_send, dx_recv,
        kst, pk, grads, queries, dxs, gq, sq, pq, fq, gk, sk, pp, fk, p1, f1, sm, pm, fm, tm,
    ):
        me = Spot()
        copies = Copies(send, recv, local)
        square = me.square()
        line = [to for to, _ in me.line()]
        owners = me.owners()
        readers = [device for _, device in me.readers()]
        barrier, expected = announce(
            [me.at(x=x, y=y) for x, y in square]
            + [me.at(g=to) for to in line]
            + readers[1:]
            + [me.sibling()],
            [(jnp.logical_not(me.selfish), readers[0])],
        )
        pl.semaphore_wait(barrier, expected)
        other = 1 - me.c
        k_half = []
        for dv in range(2):
            v = (me.half + dv) % 2
            k_half += [
                copies.push(dkv_ref.at[u, other, v], kst.at[u, v], me.sibling()) for u in range(2)
            ]

        wm_half = copies.push(gm.at[:, other], sm, me.sibling())
        w1_push = [
            copies.push(s1.at[:, to, :], p1.at[slot], me.at(g=to)) for slot, to in enumerate(line)
        ]

        lower = lax.broadcasted_iota(jnp.int32, (n, LANES), 1) < HEAD
        for slot in range(GROUPS):
            second = pltpu.roll(dq_ref[slot, :, LANES : 2 * LANES].astype(wide), HEAD, 1)
            front = jnp.where(lower, dq_ref[slot, :, :LANES].astype(wide), second)
            queries[slot, :, :LANES] = front.astype(low_type)
            queries[slot, :, LANES:] = dq_ref[slot, :, 2 * LANES :]
            grads[slot, :, WIDE:] = dq_ref[slot]

        def weight_grad(values, target):
            width = values.shape[-1]
            bias = jnp.sum(values.astype(wide), axis=0, keepdims=True)
            bias = jnp.broadcast_to(bias, (8, width)).astype(low_type)
            for half in range(2):
                made = lax.dot_general(
                    tok[:, :, half * cut : (half + 1) * cut].reshape(GROUPS * n, cut),
                    values,
                    DOWN,
                    preferred_element_type=wide,
                ).astype(low_type)
                for index in range(16):
                    place = (half, index // 8, index // 2 % GROUPS, index % 2)
                    target[(*place, slice(None, s))] = made[index * s : (index + 1) * s]
                    target[(*place, slice(s, None))] = bias

        def keys_on(dv):
            v = (me.half + dv) % 2
            for u in range(2):
                k_half[2 * dv + u].wait_recv()
            pushed = []
            for du in range(2):
                for slot, (x, y) in enumerate(square):
                    u, p = (x + du) % 2, (x + me.c) % 2
                    kst[u, v, p, y] = kst[u, v, p, y] + dkv_ref[u, me.c, v, p, y]
                    pushed.append(
                        copies.push(
                            kst.at[u, v, p, y], pk.at[2 * dv + du, slot], me.at(x=x, y=y)
                        )
                    )
            return pushed

        k_push = keys_on(0)
        weight_grad(queries[...].reshape(GROUPS * n, PACK), gq)
        q_half = copies.push(gq.at[:, other], sq, me.sibling())
        k_push += keys_on(1)

        def at8(index):
            return index // 8, index // 2 % GROUPS, index % 2

        def pair_sum(total, mine):
            def add(index):
                x, g, y = at8(index)
                total[x, g, y] = total[x, g, y] + mine[x, me.c, g, y]

            loop(16, add)

        def square_push(total, landing):
            return [
                copies.push(total.at[x, :, y], landing.at[slot], me.at(x=x, y=y))
                for slot, (x, y) in enumerate(square)
            ]

        def square_sum(result, total, landed):
            def add(g):
                result[g] = total_of(
                    total[me.x, g, me.y], landed[0, g], landed[1, g], landed[2, g]
                ).astype(low_type)

            loop(GROUPS, add)

        q_half.wait_recv()
        pair_sum(sq, gq)
        q_push = square_push(sq, pq)

        move = Scatter(dx_send, dx_recv, me.selfish)
        for index, (slot, device) in enumerate(owners):
            for copy in k_push[3 * index : 3 * index + 3]:
                copy.wait_recv()
            u, v = slot // 2, slot % 2
            grads[slot, :, :WIDE] = total_of(
                kst[u, v, me.p, me.y],
                dkv_ref[u, me.c, v, me.p, me.y],
                *[pk[index, peer] for peer in range(3)],
            ).astype(low_type)
            dxs[slot] = lax.dot_general(
                grads[slot], w_ref[:, : 2 * WIDE], NEXT, preferred_element_type=wide
            ).astype(low_type)
            move.send_one(dxs.at[slot], dx_out.at[me.g], me.g, device)
            if index == 1:
                for copy in q_push:
                    copy.wait_recv()
                square_sum(fq, sq, pq)
                arrivals = [
                    copies.push(fq.at[to], outq.at[me.g], me.at(g=to)) for to in line
                ]
                kept = [copies.keep(fq.at[me.g], outq.at[me.g])]
                for copy in w1_push:
                    copy.wait_recv()

                def addw(index):
                    x, y = index // 2, index % 2
                    f1[x, y] = total_of(
                        s1[x, me.g, y], *[p1[peer, x, y] for peer in range(3)]
                    ).astype(low_type)

                loop(4, addw)
                quarter = out1.at[me.x * 2 + me.y]
                arrivals += [
                    copies.push(f1.at[x, y], quarter, me.at(x=x, y=y)) for x, y in square
                ]
                kept.append(copies.keep(f1.at[me.x, me.y], quarter))
        wm_half.wait_recv()
        pair_sum(sm, gm)
        wm_push = square_push(sm, pm)
        weight_grad(grads[:, :, :WIDE].reshape(GROUPS * n, WIDE), gk)
        half = copies.push(gk.at[:, other], sk, me.sibling())
        half.wait_recv()
        pair_sum(sk, gk)
        push = square_push(sk, pp)
        for copy in wm_push:
            copy.wait_recv()
        square_sum(fm, sm, pm)
        wm_last = [
            copies.push(fm.at[to], tm.at[peer], me.at(g=to)) for peer, to in enumerate(line)
        ]
        for copy in push:
            copy.wait_recv()
        square_sum(fk, sk, pp)
        arrivals += [copies.push(fk.at[to], outk.at[me.g], me.at(g=to)) for to in line]
        kept.append(copies.keep(fk.at[me.g], outk.at[me.g]))
        for copy in wm_last:
            copy.wait_recv()
        outm[...] = total_of(fm[me.g], *[tm[peer] for peer in range(3)])
        for copy in arrivals:
            copy.wait_recv()
        for g in range(GROUPS):
            move.arrived(g, dx_out.at[g])
        for copy in kept:
            copy.wait()
        move.finish()
        copies.finish()

    vmem = pltpu.VMEM
    dma = pltpu.SemaphoreType.DMA
    total = 64

    def stages(width):
        return [
            vmem((2, 2, GROUPS, 2, rows, width), low_type),
            vmem((2, GROUPS, 2, rows, width), low_type),
            vmem((3, GROUPS, rows, width), low_type),
            vmem((GROUPS, rows, width), low_type),
        ]

    return pl.pallas_call(
        body,
        name="last_kernel",
        out_shape=(
            jax.ShapeDtypeStruct((GROUPS, n, depth), low_type),
            jax.ShapeDtypeStruct((GROUPS, rows, PACK), low_type),
            jax.ShapeDtypeStruct((GROUPS, rows, WIDE), low_type),
            jax.ShapeDtypeStruct((4, rows, depth), low_type),
            jax.ShapeDtypeStruct((rows, depth), wide),
        ),
        in_specs=[pl.BlockSpec(memory_space=vmem)] * 6,
        out_specs=[pl.BlockSpec(memory_space=pl.ANY)] * 4 + [pl.BlockSpec(memory_space=vmem)],
        scratch_shapes=[
            dma((total,)), dma((total,)), dma((4,)), dma((4,)), dma((4,)),
            vmem((2, 2, 2, 2, n, WIDE), low_type),
            vmem((4, 3, n, WIDE), low_type),
            vmem((GROUPS, n, 2 * WIDE), low_type),
            vmem((GROUPS, n, PACK), low_type),
            vmem((GROUPS, n, depth), low_type),
            *stages(PACK),
            *stages(WIDE),
            vmem((3, 2, 2, rows, depth), low_type),
            vmem((2, 2, rows, depth), low_type),
            *stages(depth)[1:],
            vmem((3, rows, depth), low_type),
        ],
        compiler_params=pltpu.CompilerParams(
            collective_id=11, has_side_effects=True, vmem_limit_bytes=VMEM_LIMIT
        ),
    )(dkv, dq, tokens, weights, sum1, gradm)


def final_kernel(hidden, pieces, outq, outk, out1, out2, outm, s, e):
    n, depth = hidden.shape
    quarter = out1.shape[-1]

    def body(hid, dx, q_in, k_in, i_in, o_in, m_in, xg, qw, qb, kw, vw, vb, mw, mb, eg, es, iw, ib, ow, ob, fg, fs):
        device = lax.axis_index("au") * lax.axis_size("row") + lax.axis_index("row")
        xg[...] = total_of(hid[...], dx[0], dx[1], dx[2], dx[3]).astype(low_type)
        rows = q_in.shape[1]
        lower = lax.broadcasted_iota(jnp.int32, (rows, LANES), 1) < HEAD

        def part(head):
            g, h = head // LOCAL, head % LOCAL
            return k_in[g, :, h * LANES : (h + 1) * LANES].astype(wide)

        made_q = []
        for g in range(0, GROUPS, 2):
            a0, b0 = q_in[g, :, :LANES].astype(wide), q_in[g, :, LANES:].astype(wide)
            a1 = pltpu.roll(q_in[g + 1, :, :LANES].astype(wide), HEAD, 1)
            b1 = pltpu.roll(q_in[g + 1, :, LANES:].astype(wide), HEAD, 1)
            made_q += [a0, jnp.where(lower, b0, a1), jnp.where(lower, a1, b1)]
        biases = [[], []]
        for pair in range(HEADS // 2):
            span = slice(pair * LANES, (pair + 1) * LANES)
            kv = [part(2 * pair), part(2 * pair + 1)]
            made_k = jnp.where(lower, kv[0], pltpu.roll(kv[1], HEAD, 1))
            made_v = jnp.where(lower, pltpu.roll(kv[0], HEAD, 1), kv[1])
            qw[:, span], kw[:, span], vw[:, span] = made_q[pair][:s], made_k[:s], made_v[:s]
            biases[0].append(made_q[pair][s:])
            biases[1].append(made_v[s:])

        def own(eight, width, shift):
            return pltpu.roll(eight, shift, 1)[0:1, :width]

        turn = (depth - device * s) % depth
        qb[...] = own(jnp.concatenate(biases[0], axis=1), s, turn)
        vb[...] = own(jnp.concatenate(biases[1], axis=1), s, turn)
        mw[...] = m_in[:s]
        extras = pltpu.roll(m_in[s : s + 8, :], turn, 1)
        for index, ref in enumerate((mb, eg, es, ob, fg, fs)):
            ref[...] = extras[index : index + 1, :s]
        for w in range(4):
            iw[:, w * quarter : (w + 1) * quarter] = i_in[w, :s].astype(wide)
        place = lax.axis_index("row") * e
        ib[...] = own(
            i_in[lax.axis_index("au"), s : s + 8, :].astype(wide), e, (quarter - place) % quarter
        )
        ow[...] = o_in[...]

    vmem = pltpu.VMEM

    def shape(*dims):
        return jax.ShapeDtypeStruct(dims, wide)

    return pl.pallas_call(
        body,
        name="final_kernel",
        out_shape=(
            jax.ShapeDtypeStruct((n, depth), low_type),
            shape(s, depth), shape(1, s), shape(s, depth), shape(s, depth), shape(1, s),
            shape(s, depth), shape(1, s), shape(1, s), shape(1, s),
            shape(s, 4 * quarter), shape(1, e), shape(e, depth),
            shape(1, s), shape(1, s), shape(1, s),
        ),
        in_specs=[pl.BlockSpec(memory_space=vmem)] * 7,
        out_specs=(pl.BlockSpec(memory_space=vmem),) * 16,
        compiler_params=pltpu.CompilerParams(vmem_limit_bytes=VMEM_LIMIT),
    )(hidden, pieces, outq, outk, out1, out2, outm)


def gelu_and_slope(value):
    t = 1.0 / (1.0 + (0.3275911 * 0.7071067811865476) * jnp.abs(value))
    bell = jnp.exp(-0.5 * value * value)
    tail = 1.061405429
    for weight in (-1.453152027, 1.421413741, -0.284496736, 0.254829592):
        tail = tail * t + weight
    tail = 0.5 * tail * t * bell
    below = jnp.where(value >= 0.0, 1.0 - tail, tail)
    return value * below, below + value * bell * 0.3989422804014327


def normed(hidden):
    mean = jnp.mean(hidden, axis=-1, keepdims=True)
    centered = hidden - mean
    spread = jnp.mean(centered * centered, axis=-1, keepdims=True)
    inverse = lax.rsqrt(spread + eps_norm)
    return centered * inverse, inverse


def normed_grad(grad, norm, inverse):
    mean = jnp.mean(grad, axis=-1, keepdims=True)
    along = jnp.mean(grad * norm, axis=-1, keepdims=True)
    return inverse * (grad - mean - norm * along)


def down_sum(values):
    return jnp.sum(values, axis=0, keepdims=True)


def middle_kernel(mixed, tokens, cotangent, mix, inner, outer, vec, s, e):
    n, depth = tokens.shape
    quarter = inner.shape[1]
    rows = s + 8
    cut = depth // 2
    hn = n // 2

    def body(
        mixed_ref, tok, cot, wm_in, w1_in, w2f, vec_ref,
        out, hidden_out, do_out, gm, s1, out2,
        send, recv, local, back_send, back_recv, on_send, on_recv, swap_send, swap_recv,
        swap_send2, swap_recv2, wm, w1, w2p, w2s, came, mixed_tok, xs, acts, slopes, parts, sums, bgs, igs, parts2, sums2,
        pieces, extra, attn, own1, own2, g1, g2, s2, p2,
    ):
        me = Spot()
        copies = Copies(send, recv, local)
        square = me.square()
        line = [to for to, _ in me.line()]
        owners = me.owners()
        readers = me.readers()
        swapped = [me.at(g=to, c=me.y, y=me.c) for to in [me.g] + line]
        barrier, expected = announce(
            [me.at(x=x, y=y) for x, y in square]
            + swapped[1:]
            + [device for _, device in readers[1:]]
            + [device for _, device in owners[1:]]
            + [me.sibling()],
            [
                (jnp.logical_not(me.selfish), readers[0][1]),
                (jnp.logical_not(me.selfish), owners[0][1]),
                (me.crossing, swapped[0]),
            ],
        )
        loads = [copies.keep(wm_in, wm), copies.keep(w1_in, w1)]
        w2s[...] = w2f[...].astype(low_type)
        pl.semaphore_wait(barrier, expected)

        back = Scatter(back_send, back_recv, me.selfish)
        back.start([(mixed_ref.at[slot], device) for slot, device in owners], came.at[me.g], me.g)
        lower = lax.broadcasted_iota(jnp.int32, (n, LANES), 1) < HEAD
        loads[0].wait()
        for g in range(GROUPS):
            back.arrived(g, came.at[g])
        w2_place = w2p.at[me.g, me.y]
        w2_first = [copies.push(w2s, w2_place, device) for device in swapped[1:]]
        w2_swap = pltpu.make_async_remote_copy(
            src_ref=w2s,
            dst_ref=w2_place,
            send_sem=swap_send2,
            recv_sem=swap_recv2,
            device_id=swapped[0],
            device_id_type=MESH,
        )
        w2_stays = pltpu.make_async_copy(w2s, w2_place, swap_recv2)

        @pl.when(me.crossing)
        def _():
            w2_swap.start()

        @pl.when(jnp.logical_not(me.crossing))
        def _():
            w2_stays.start()

        for half in range(2):
            a0 = came[2 * half, :, :LANES]
            b0 = came[2 * half, :, LANES:].astype(wide)
            a1 = pltpu.roll(came[2 * half + 1, :, :LANES].astype(wide), HEAD, 1)
            b1 = pltpu.roll(came[2 * half + 1, :, LANES:].astype(wide), HEAD, 1)
            base = half * 3 * LANES
            mixed_tok[:, base : base + LANES] = a0
            mixed_tok[:, base + LANES : base + 2 * LANES] = jnp.where(lower, b0, a1).astype(low_type)
            mixed_tok[:, base + 2 * LANES : base + 3 * LANES] = jnp.where(lower, a1, b1).astype(
                low_type
            )

        def vector(index):
            return vec_ref[index : index + 1, :]

        mix = jnp.dot(mixed_tok[...], wm[...], preferred_element_type=wide) + vector(2)
        norm1, inverse1 = normed(tok[...].astype(wide) + mix)
        early = norm1 * vector(3) + vector(4)
        mine = me.x * 2 + me.y
        halves = [slice(0, hn), slice(hn, n)]

        def send_rows(ref, h):
            place = ref.at[h, mine]
            return [copies.push(place, place, me.at(x=x, y=y)) for x, y in square]

        def send_back(ref, landing, h):
            return [
                copies.push(ref.at[h, x * 2 + y], landing.at[h, mine], me.at(x=x, y=y))
                for x, y in square
            ]

        def arrive(started):
            for copy in started:
                copy.wait_recv()

        def received(landing, h):
            return [landing[h, x * 2 + y] for x, y in square]

        early_go = []
        for h, half in enumerate(halves):
            xs[h, mine] = early[half].astype(low_type)
            early_go.append(send_rows(xs, h))
        loads[1].wait()

        def outer_weight():
            return w2p[...].reshape(quarter, depth)

        branch_go = []
        for h in range(2):
            arrive(early_go[h])
            inner = jnp.dot(
                xs[h].reshape(4 * hn, depth), w1[...], preferred_element_type=wide
            ) + vector(8)
            act, slope = gelu_and_slope(inner)
            act = act.astype(low_type)
            acts[h] = act.reshape(4, hn, quarter)
            slopes[h] = slope
            if h == 0:

                @pl.when(me.crossing)
                def _():
                    w2_swap.wait_recv()
                    w2_swap.wait_send()

                @pl.when(jnp.logical_not(me.crossing))
                def _():
                    w2_stays.wait()

                block = w2p.at[me.g, me.c]
                w2_last = [copies.push(block, block, me.sibling())]
                for copy, (_, source) in zip(w2_first, me.line()):
                    copy.wait_recv()
                    block = w2p.at[source, me.c]
                    w2_last.append(copies.push(block, block, me.sibling()))
                arrive(w2_last)
            made = jnp.dot(act, outer_weight(), preferred_element_type=wide).reshape(4, hn, depth)
            own1[h] = made
            parts[h] = made.astype(low_type)
            branch_go.append(send_back(parts, sums, h))

        grad_go, final_grads, norm_sums, cot_sums = [], [], [], []
        for h, half in enumerate(halves):
            arrive(branch_go[h])
            branch = total_of(own1[h, mine], *received(sums, h)) + vector(5)
            norm2, inverse2 = normed(early[half] + branch)
            out[half, :] = (norm2 * vector(6) + vector(7)).astype(low_type)
            cot_wide = cot[half, :].astype(wide)
            final_grad = normed_grad(cot_wide * vector(6), norm2, inverse2)
            bgs[h, mine] = final_grad.astype(low_type)
            grad_go.append(send_rows(bgs, h))
            final_grads.append(final_grad)
            norm_sums.append(down_sum(cot_wide * norm2))
            cot_sums.append(down_sum(cot_wide))
        extra[...] = jnp.zeros_like(extra)
        extra[3:4, :] = down_sum(bgs[0, mine].astype(wide)) + down_sum(bgs[1, mine].astype(wide))
        extra[4:5, :] = norm_sums[0] + norm_sums[1]
        extra[5:6, :] = cot_sums[0] + cot_sums[1]

        token_go = []
        for h in range(2):
            arrive(grad_go[h])
            grad = lax.dot_general(
                bgs[h].reshape(4 * hn, depth), outer_weight(), NEXT, preferred_element_type=wide
            )
            grad = (grad * slopes[h]).astype(low_type)
            igs[h] = grad.reshape(4, hn, quarter)
            made = lax.dot_general(grad, w1[...], NEXT, preferred_element_type=wide)
            made = made.reshape(4, hn, depth)
            own2[h] = made
            parts2[h] = made.astype(low_type)
            token_go.append(send_back(parts2, sums2, h))

        other = 1 - me.c
        grads = bgs[...].reshape(4 * n, depth)
        for half in range(2):
            span = slice(half * cut, (half + 1) * cut)
            made = lax.dot_general(
                acts[:, :, :, span].reshape(4 * n, cut), grads, DOWN, preferred_element_type=wide
            )
            g2[2 * half : 2 * half + 2] = made.astype(low_type).reshape(2, 2, e, depth)
        w2_half = copies.push(g2.at[:, other], s2, me.sibling())

        grads = igs[...].reshape(4 * n, quarter)
        bias = jnp.broadcast_to(down_sum(grads.astype(wide)), (8, quarter)).astype(low_type)
        for half in range(2):
            span = slice(half * cut, (half + 1) * cut)
            made = lax.dot_general(
                xs[:, :, :, span].reshape(4 * n, cut), grads, DOWN, preferred_element_type=wide
            ).astype(low_type)
            for index in range(16):
                place = (half, index // 8, index // 2 % GROUPS, index % 2)
                g1[(*place, slice(None, s))] = made[index * s : (index + 1) * s]
                g1[(*place, slice(s, None))] = bias
        w1_half = copies.push(g1.at[:, other], s1, me.sibling())
        w2_half.wait_recv()

        def add2(g):
            s2[g] = s2[g] + g2[g, me.c]

        loop(GROUPS, add2)
        w2_push = [
            copies.push(s2.at[to], p2.at[index + 1], swapped[index + 1])
            for index, to in enumerate(line)
        ]
        exchanged = pltpu.make_async_remote_copy(
            src_ref=s2.at[me.g],
            dst_ref=p2.at[0],
            send_sem=swap_send,
            recv_sem=swap_recv,
            device_id=swapped[0],
            device_id_type=MESH,
        )
        stays = pltpu.make_async_copy(s2.at[me.g], p2.at[0], swap_recv)

        @pl.when(me.crossing)
        def _():
            exchanged.start()

        @pl.when(jnp.logical_not(me.crossing))
        def _():
            stays.start()

        w1_half.wait_recv()

        def add1(index):
            x, g, y = index // 8, index // 2 % GROUPS, index % 2
            s1[x, g, y] = s1[x, g, y] + g1[x, me.c, g, y]

        loop(16, add1)
        norm_sums, grad_sums, attn_sums = [], [], []
        for h, half in enumerate(halves):
            arrive(token_go[h])
            early_grad = total_of(final_grads[h], own2[h, mine], *received(sums2, h))
            norm_sums.append(down_sum(early_grad * norm1[half]))
            grad_sums.append(down_sum(early_grad))
            hidden = normed_grad(early_grad * vector(3), norm1[half], inverse1[half])
            hidden_out[half, :] = hidden
            attn[half, :] = hidden.astype(low_type)
            attn_sums.append(down_sum(hidden.astype(low_type).astype(wide)))
        extra[0:1, :] = attn_sums[0] + attn_sums[1]
        extra[1:2, :] = norm_sums[0] + norm_sums[1]
        extra[2:3, :] = grad_sums[0] + grad_sums[1]
        attn_grad = attn[...]
        back_grad = lax.dot_general(attn_grad, wm[...], NEXT, preferred_element_type=wide)
        for half in range(2):
            base = half * 3 * LANES
            t0 = back_grad[:, base : base + LANES]
            t1 = back_grad[:, base + LANES : base + 2 * LANES]
            t2 = back_grad[:, base + 2 * LANES : base + 3 * LANES]
            r1, r2 = pltpu.roll(t1, HEAD, 1), pltpu.roll(t2, HEAD, 1)
            pieces[2 * half, :, :LANES] = t0.astype(low_type)
            pieces[2 * half, :, LANES:] = jnp.where(lower, t1, 0.0).astype(low_type)
            pieces[2 * half + 1, :, :LANES] = jnp.where(lower, r1, r2).astype(low_type)
            pieces[2 * half + 1, :, LANES:] = jnp.where(lower, r2, 0.0).astype(low_type)
        onward = Scatter(on_send, on_recv, me.selfish)
        slot = me.slot()
        onward.start([(pieces.at[g], device) for g, device in readers], do_out.at[slot], slot)

        for half in range(2):
            span = slice(half * cut, (half + 1) * cut)
            made = lax.dot_general(
                mixed_tok[:, span], attn_grad, DOWN, preferred_element_type=wide
            ).astype(low_type)
            for index in range(16):
                place = (half, index // 8, index // 2 % GROUPS, index % 2)
                gm[(*place, slice(None, s))] = made[index * s : (index + 1) * s]
                gm[(*place, slice(s, None))] = extra[...].astype(low_type)
        @pl.when(me.crossing)
        def _():
            exchanged.wait_recv()
            exchanged.wait_send()

        @pl.when(jnp.logical_not(me.crossing))
        def _():
            stays.wait()

        for copy in w2_push:
            copy.wait_recv()
        out2[...] = total_of(*[p2[index] for index in range(4)])
        for index in range(GROUPS):
            onward.arrived(index, do_out.at[index])
        back.finish()
        onward.finish()
        copies.finish()

    vmem = pltpu.VMEM
    dma = pltpu.SemaphoreType.DMA
    tall = vmem((2, 4, hn, depth), low_type)
    full = vmem((2, 4, hn, depth), wide)
    high = vmem((2, 4, hn, quarter), low_type)
    space = [vmem] * 3 + [pl.ANY] * 2 + [vmem] * 2
    return pl.pallas_call(
        body,
        name="middle_kernel",
        out_shape=(
            jax.ShapeDtypeStruct((n, depth), low_type),
            jax.ShapeDtypeStruct((n, depth), wide),
            jax.ShapeDtypeStruct((GROUPS, n, PACK), low_type),
            jax.ShapeDtypeStruct((2, 2, GROUPS, 2, rows, depth), low_type),
            jax.ShapeDtypeStruct((2, GROUPS, 2, rows, quarter), low_type),
            jax.ShapeDtypeStruct((e, depth), wide),
        ),
        in_specs=[pl.BlockSpec(memory_space=item) for item in space],
        out_specs=[
            pl.BlockSpec(memory_space=item) for item in (vmem, vmem, pl.ANY, vmem, vmem, vmem)
        ],
        scratch_shapes=[
            dma((48,)), dma((48,)), dma((8,)), dma((4,)), dma((4,)), dma((4,)), dma((4,)), dma, dma, dma, dma,
            vmem((depth, depth), low_type),
            vmem((depth, quarter), low_type),
            vmem((GROUPS, 2, e, depth), low_type),
            vmem((e, depth), low_type),
            vmem((GROUPS, n, PACK), low_type),
            vmem((n, depth), low_type),
            tall, high,
            vmem((2, 4 * hn, quarter), wide),
            tall, tall, tall, high, tall, tall,
            vmem((GROUPS, n, PACK), low_type),
            vmem((8, depth), wide),
            vmem((n, depth), low_type),
            full, full,
            vmem((2, 2, GROUPS, 2, rows, quarter), low_type),
            vmem((GROUPS, 2, e, depth), low_type),
            vmem((GROUPS, e, depth), low_type),
            vmem((4, e, depth), low_type),
        ],
        compiler_params=pltpu.CompilerParams(
            collective_id=12, has_side_effects=True, vmem_limit_bytes=VMEM_LIMIT
        ),
    )(mixed, tokens, cotangent, mix, inner, outer, vec)


def tile_base(me, slot, n):
    u, v = slot // 2, slot % 2
    return ((u * 2 + me.c) * 2 * GROUPS + (v * 2 + me.p) * 2 + me.y) * n


def ends_of(lengths_ref):
    ends = [lengths_ref[0]]
    for index in range(1, lengths_ref.shape[0]):
        ends.append(ends[-1] + lengths_ref[index])
    return ends


def document_of(place, ends):
    first, last = place * 0, place * 0 + ends[-1]
    for end in ends[:-1]:
        before = end <= place
        first = jnp.where(before, end, first)
    for end in reversed(ends[:-1]):
        last = jnp.where(end <= place, last, end)
    return first, last


def blocks_of(base, ends, n, block):
    low, _ = document_of(base, ends)
    _, high = document_of(base + n - 1, ends)
    return low // block, (high + block - 1) // block


def near_forward(lengths, queries, keys, n, block):
    total_rows = queries.shape[0]
    tokens = keys.shape[0]
    chunks = [slice(index * LANES, (index + 1) * LANES) for index in range(block // LANES)]

    def body(lengths_ref, q_ref, kv_ref, out_ref, keep_ref, lse_ref, table):
        me = Spot()
        ends = ends_of(lengths_ref)
        lane = lax.broadcasted_iota(jnp.int32, (n, LANES), 1)
        upper = lane >= HEAD
        column = lax.broadcasted_iota(jnp.int32, (n, LANES), 0)

        def one(slot, unused):
            rows = pl.ds(pl.multiple_of(slot * n, n), n)
            base = tile_base(me, slot, n)
            low, high = blocks_of(base, ends, n, block)
            first, last = document_of(column + base, ends)
            heads = [
                q_ref[rows, h * LANES : (h + 1) * LANES] * jnp.asarray(0.125, low_type)
                for h in range(LOCAL)
            ]

            def score(j, tops):
                begin = pl.multiple_of(j * block, block)
                same = []
                for chunk in chunks:
                    place = lane + (begin + chunk.start)
                    same.append((place >= first) & (place < last))
                result = []
                for h in range(LOCAL):
                    kv = kv_ref[pl.ds(begin, block), h * LANES : (h + 1) * LANES]
                    scores = lax.dot_general(heads[h], kv, NEXT, preferred_element_type=wide)
                    top = tops[h]
                    for chunk, mask in zip(chunks, same):
                        part = jnp.where(mask, scores[:, chunk], mask_fill)
                        table[h, j, :, chunk] = part
                        top = jnp.maximum(top, part)
                    result.append(top)
                return tuple(result)

            tops = lax.fori_loop(
                low, high, score, (jnp.full((n, LANES), lowest_start, wide),) * LOCAL
            )
            tops = [jnp.max(top, axis=1, keepdims=True) for top in tops]
            spread = [jnp.broadcast_to(top, (n, LANES)) for top in tops]

            def weigh(j, carry):
                begin = pl.multiple_of(j * block, block)
                result = []
                for h in range(LOCAL):
                    total, mixed = carry[h]
                    kv = kv_ref[pl.ds(begin, block), h * LANES : (h + 1) * LANES]
                    parts = []
                    for chunk in chunks:
                        part = jnp.exp(table[h, j, :, chunk] - spread[h])
                        total = total + part
                        parts.append(part.astype(low_type))
                    powers = jnp.concatenate(parts, axis=1)
                    mixed = mixed + jnp.dot(powers, kv, preferred_element_type=wide)
                    result.append((total, mixed))
                return tuple(result)

            zero = jnp.zeros((n, LANES), wide)
            done = lax.fori_loop(low, high, weigh, ((zero, zero),) * LOCAL)
            totals = [jnp.sum(total, axis=1, keepdims=True) for total, _ in done]
            mixes = [mixed / total for total, (_, mixed) in zip(totals, done)]
            turned = [pltpu.roll(mixed, HEAD, 1) for mixed in mixes]
            front = jnp.where(upper, mixes[1], turned[0])
            back = jnp.where(upper, 0.0, turned[2])
            both = jnp.concatenate([front, back], axis=1)
            keep_ref[rows, :] = both
            out_ref[rows, :] = both.astype(low_type)
            logs = [top + jnp.log(total) for top, total in zip(tops, totals)]
            logs = jnp.where(lane == 0, logs[0], jnp.where(lane == 1, logs[1], logs[2]))
            lse_ref[slot] = jnp.transpose(logs)[:8]
            return unused

        lax.fori_loop(0, GROUPS, one, 0)

    vmem = pl.BlockSpec(memory_space=pltpu.VMEM)
    return pl.pallas_call(
        body,
        name="near_forward",
        out_shape=(
            jax.ShapeDtypeStruct((total_rows, PACK), low_type),
            jax.ShapeDtypeStruct((total_rows, PACK), wide),
            jax.ShapeDtypeStruct((GROUPS, 8, n), wide),
        ),
        in_specs=[pl.BlockSpec(memory_space=pltpu.SMEM)] + [vmem] * 2,
        out_specs=(vmem,) * 3,
        scratch_shapes=[pltpu.VMEM((LOCAL, tokens // block, n, block), wide)],
        compiler_params=pltpu.CompilerParams(vmem_limit_bytes=VMEM_LIMIT),
    )(lengths, queries, keys)


def near_backward(lengths, queries, keys, grads, mixed, lse, n, block):
    total_rows = queries.shape[0]
    tokens = keys.shape[0]

    def body(lengths_ref, q_ref, kv_ref, do_ref, mixed_ref, lse_ref, dq_ref, dkv_ref, sums):
        me = Spot()
        ends = ends_of(lengths_ref)
        zeros = jnp.zeros((block, LANES), wide)
        spans = [slice(h * LANES, (h + 1) * LANES) for h in range(LOCAL)]

        def clear(j, unused):
            for span in spans:
                sums[pl.ds(pl.multiple_of(j * block, block), block), span] = zeros
            return unused

        lax.fori_loop(0, tokens // block, clear, 0)
        lane = lax.broadcasted_iota(jnp.int32, (n, LANES), 1)
        upper = lane >= HEAD
        along = lax.broadcasted_iota(jnp.int32, (1, n), 1)
        down = lax.broadcasted_iota(jnp.int32, (block, n), 0)

        def upper_halves(ref, rows):
            front = ref[rows, :LANES].astype(wide)
            back = ref[rows, LANES:].astype(wide)
            parts = (pltpu.roll(front, HEAD, 1), front, pltpu.roll(back, HEAD, 1))
            return [jnp.where(upper, part, 0.0) for part in parts]

        def one(slot, unused):
            rows = pl.ds(pl.multiple_of(slot * n, n), n)
            base = tile_base(me, slot, n)
            low, high = blocks_of(base, ends, n, block)
            first, last = document_of(along + base, ends)
            outs, inputs = upper_halves(mixed_ref, rows), upper_halves(do_ref, rows)
            logs, deltas, operands = [], [], []
            for h, span in enumerate(spans):
                q = q_ref[rows, span] * jnp.asarray(0.125, low_type)
                operands.append(jnp.concatenate([q, inputs[h].astype(low_type)], axis=0))
                deltas.append(down_sum(jnp.transpose(inputs[h] * outs[h])))
                logs.append(lse_ref[slot, h : h + 1, :])

            def step(j, totals):
                begin = pl.multiple_of(j * block, block)
                part = pl.ds(begin, block)
                place = down + begin
                same = (place >= first) & (place < last)
                kvs = [kv_ref[part, span] for span in spans]
                made = [
                    lax.dot_general(kv, both, NEXT, preferred_element_type=wide)
                    for kv, both in zip(kvs, operands)
                ]
                result = []
                for h, span in enumerate(spans):
                    probs = jnp.exp(jnp.where(same, made[h][:, :n], mask_fill) - logs[h])
                    score_grad = (probs * (made[h][:, n:] - deltas[h])).astype(low_type)
                    pairs = jnp.concatenate([score_grad, probs.astype(low_type)], axis=1)
                    sums[part, span] += jnp.dot(
                        pairs, operands[h], preferred_element_type=wide
                    )
                    result.append(
                        totals[h]
                        + lax.dot_general(score_grad, kvs[h], DOWN, preferred_element_type=wide)
                    )
                return tuple(result)

            totals = lax.fori_loop(low, high, step, (jnp.zeros((n, LANES), wide),) * LOCAL)
            for total, span in zip(totals, spans):
                dq_ref[rows, span] = jnp.where(upper, 0.0, total * 0.125).astype(low_type)
            return unused

        lax.fori_loop(0, GROUPS, one, 0)

        def store(j, unused):
            part = pl.ds(pl.multiple_of(j * block, block), block)
            for span in spans:
                dkv_ref[part, span] = sums[part, span].astype(low_type)
            return unused

        lax.fori_loop(0, tokens // block, store, 0)

    vmem = pl.BlockSpec(memory_space=pltpu.VMEM)
    return pl.pallas_call(
        body,
        name="near_backward",
        out_shape=(
            jax.ShapeDtypeStruct((total_rows, WIDE), low_type),
            jax.ShapeDtypeStruct((tokens, WIDE), low_type),
        ),
        in_specs=[pl.BlockSpec(memory_space=pltpu.SMEM)] + [vmem] * 5,
        out_specs=(vmem,) * 2,
        scratch_shapes=[pltpu.VMEM((tokens, WIDE), wide)],
        compiler_params=pltpu.CompilerParams(vmem_limit_bytes=VMEM_LIMIT),
    )(lengths, queries, keys, grads, mixed, lse)


def on_device_general(
    tokens,
    cotangent,
    doc_lengths,
    query_weight,
    query_bias,
    key_weight,
    value_weight,
    value_bias,
    mix_weight,
    mix_bias,
    early_gain,
    early_shift,
    inner_weight,
    inner_bias,
    outer_weight,
    outer_bias,
    final_gain,
    final_shift,
):
    n, depth = tokens.shape
    groups, cycle = lax.axis_size("au"), lax.axis_size("row")
    devices = groups * cycle
    zs = cycle // (2 * GROUPS)
    s = query_weight.shape[0]
    ff = inner_weight.shape[1]
    quarter = ff // 4
    e = outer_weight.shape[0]
    rows = GROUPS * n
    total_tokens = n * devices
    me = Place(zs)
    device = lax.axis_index("au") * cycle + lax.axis_index("row")
    w_me = me.x * 2 + me.y

    def by_head(weight):
        return weight.astype(low_type).reshape(-1, GROUPS, LOCAL, HEAD)

    def packed(query, key, value):
        kv = jnp.stack([key, value], axis=3).reshape(-1, GROUPS, WIDE)
        q = jnp.pad(query, ((0, 0), (0, 0), (0, 0), (0, HEAD))).reshape(-1, GROUPS, WIDE)
        return jnp.concatenate([kv, q], axis=2)

    slab = packed(by_head(query_weight), by_head(key_weight), by_head(value_weight))
    slab = jnp.transpose(slab, (1, 0, 2))
    small = jnp.concatenate(
        [
            vector.astype(low_type)
            for vector in (
                query_bias, value_bias, mix_bias, early_gain, early_shift,
                outer_bias, final_gain, final_shift, inner_bias,
            )
        ]
    )
    extra = -s % 8 or 8
    small = jnp.broadcast_to(
        jnp.pad(small, (0, 2 * WIDE - small.shape[0]))[None, None], (GROUPS, extra, 2 * WIDE)
    )
    slab = jnp.concatenate([slab, small], axis=1)
    tok_all, w_all = spread_tokens(zs, tokens, slab)
    tok_all = tok_all.reshape(rows, depth)
    w_qkv = w_all[..., :s, :].reshape(depth, 2 * WIDE)
    small = w_all[..., s, :].reshape(devices, 2 * WIDE)
    names = [small[:, i * s : (i + 1) * s].reshape(depth) for i in range(8)]
    q_bias, v_bias, m_bias, e_gain, e_shift, o_bias, f_gain, f_shift = names
    i_bias = small[:, 8 * s : 8 * s + e].reshape(4, quarter)[w_me].astype(wide)
    q_bias = q_bias.reshape(1, GROUPS, LOCAL, HEAD)
    v_bias = v_bias.reshape(1, GROUPS, LOCAL, HEAD)
    bias = packed(q_bias, jnp.zeros_like(q_bias), v_bias)[0, me.g].astype(wide)

    qkv = (jnp.dot(tok_all, w_qkv, preferred_element_type=wide) + bias).astype(low_type)
    queries = qkv[:, WIDE:]

    inner_slab = jnp.transpose(inner_weight.astype(low_type).reshape(s, 4, quarter), (1, 0, 2))
    kv_all, w1, w2, wm = spread_keys(
        zs,
        qkv[:, :WIDE].reshape(GROUPS, n, WIDE),
        inner_slab,
        outer_weight.astype(low_type),
        mix_weight.astype(low_type),
    )
    kv_all = kv_all.reshape(total_tokens, WIDE)
    w1 = w1.reshape(depth, quarter)
    w2 = w2.reshape(quarter, depth)
    wm = wm.reshape(depth, depth)

    tile, block = 128, 512
    count = doc_lengths.shape[0]
    upto = jnp.arange(count)[None, :] <= jnp.arange(count)[:, None]
    ends = jnp.sum(jnp.where(upto, doc_lengths[None, :], 0), axis=1)
    owners = ((me.x * 2 + me.c) * cycle + me.z * GROUPS * 2 + jnp.arange(GROUPS) * 2 + me.y) * n
    places = (owners[:, None] + jnp.arange(n)[None, :]).reshape(rows)
    before = ends[None, :] <= places[:, None]
    first = jnp.max(jnp.where(before, ends[None, :], 0), axis=1).astype(jnp.int32)
    last = jnp.min(jnp.where(before, total_tokens, ends[None, :]), axis=1).astype(jnp.int32)
    tiles = rows // tile
    bounds = jnp.stack(
        [
            first.reshape(tiles, tile)[:, 0] // block,
            (last.reshape(tiles, tile)[:, -1] + block - 1) // block,
        ],
        axis=1,
    )
    mixed, mixed_wide, lse = attend_forward(
        queries, kv_all, bounds, first[:, None], last[:, None], tile, block
    )
    mixed_tok = exchange_line(zs, 2, mixed.reshape(GROUPS, n, PACK))
    mixed_tok = jnp.transpose(mixed_tok[:, :, : LOCAL * HEAD], (1, 0, 2)).reshape(n, depth)

    attn = jnp.dot(mixed_tok, wm, preferred_element_type=wide) + m_bias.astype(wide)
    early, early_pull = jax.vjp(
        layer_norm, tokens.astype(wide) + attn, e_gain.astype(wide), e_shift.astype(wide)
    )
    early_all = gather_square(zs, 3, early.astype(low_type)).reshape(rows, depth)
    inner = jnp.dot(early_all, w1, preferred_element_type=wide) + i_bias
    act, gelu_pull = jax.vjp(gelu_exact, inner)
    act_low = act.astype(low_type)
    partial = jnp.dot(act_low, w2, preferred_element_type=wide).astype(low_type)
    partial = exchange_square(zs, 4, partial.reshape(2, 2, n, depth))
    branch = jnp.sum(partial.astype(wide), axis=(0, 1)) + o_bias.astype(wide)
    result, final_pull = jax.vjp(
        layer_norm, early + branch, f_gain.astype(wide), f_shift.astype(wide)
    )
    output = result.astype(low_type)
    final_grads = final_pull(cotangent.astype(wide))
    branch_grad = final_grads[0].astype(low_type)
    outer_bias_grad = jnp.sum(branch_grad.astype(wide), axis=0)
    branch_all = gather_square(zs, 5, branch_grad).reshape(rows, depth)
    act_grad = jnp.einsum("td,fd->tf", branch_all, w2, preferred_element_type=wide)
    inner_grad = gelu_pull(act_grad)[0].astype(low_type)
    partial = jnp.einsum("tf,df->td", inner_grad, w1, preferred_element_type=wide).astype(low_type)
    partial = exchange_square(zs, 6, partial.reshape(2, 2, n, depth))
    grad2 = jnp.einsum("tf,td->fd", act_low, branch_all, preferred_element_type=wide)
    grad1 = jnp.einsum("td,tf->df", early_all, inner_grad, preferred_element_type=wide)
    inner_bias_grad = jnp.sum(inner_grad.astype(wide), axis=0)
    early_grad = final_grads[0] + jnp.sum(partial.astype(wide), axis=(0, 1))
    early_grads = early_pull(early_grad)
    attn_grad = early_grads[0].astype(low_type)
    mixed_grad = jnp.einsum("td,cd->tc", attn_grad, wm, preferred_element_type=wide)
    mixed_grad = jnp.transpose(
        mixed_grad.astype(low_type).reshape(n, GROUPS, LOCAL * HEAD), (1, 0, 2)
    )
    mixed_grad = jnp.pad(mixed_grad, ((0, 0), (0, 0), (0, PACK - LOCAL * HEAD)))
    grad_all = exchange_line(zs, 7, mixed_grad).reshape(rows, PACK)
    gradm = jnp.einsum("tc,td->cd", mixed_tok, attn_grad, preferred_element_type=wide)
    mix_bias_grad = jnp.sum(attn_grad.astype(wide), axis=0)

    delta = jnp.sum(
        (grad_all.astype(wide) * mixed_wide)[:, : LOCAL * HEAD].reshape(rows, LOCAL, HEAD), axis=2
    )

    def as_stat(values):
        return jnp.transpose(values.reshape(tiles, tile, LOCAL), (0, 2, 1))

    def same_stat(values):
        return jnp.broadcast_to(
            values.astype(wide).reshape(tiles, 1, tile), (tiles, LOCAL, tile)
        )

    stats = jnp.stack(
        [same_stat(first), same_stat(last), as_stat(lse[:, :LOCAL]), as_stat(delta)], axis=2
    )
    stats = jnp.pad(stats, ((0, 0), (0, 0), (0, 4), (0, 0)))
    query_grad, dkv = attend_backward(queries, kv_all, grad_all, stats, bounds, tile, block)

    def slabs(grad, extras):
        grad = grad.astype(low_type).reshape(devices, s, -1)
        rest = -s % 8
        rest += 0 if rest >= extras.shape[0] else 8
        extras = jnp.concatenate(
            [extras.astype(low_type), jnp.zeros((rest - extras.shape[0], extras.shape[1]), low_type)]
        )
        extras = jnp.broadcast_to(extras[None], (devices,) + extras.shape)
        return jnp.concatenate([grad, extras], axis=1).reshape(2, 2, zs, GROUPS, 2, s + rest, -1)

    mix_extras = jnp.stack(
        [
            mix_bias_grad, early_grads[1], early_grads[2],
            outer_bias_grad, final_grads[1], final_grads[2],
        ]
    )
    dkv, out1, out2, outm = reduce_keys(
        zs,
        dkv.reshape(2, 2, zs, GROUPS, 2, n, WIDE),
        slabs(grad1, inner_bias_grad[None]),
        grad2.astype(low_type).reshape(zs, GROUPS, 2, e, depth),
        slabs(gradm, mix_extras),
    )
    key_grad = jnp.sum(dkv.astype(wide), axis=0).astype(low_type).reshape(rows, WIDE)
    grads = jnp.concatenate([key_grad, query_grad], axis=1)
    gradq = jnp.einsum("tc,td->cd", tok_all, grads, preferred_element_type=wide)
    bias_grad = jnp.sum(grads.astype(wide), axis=0)
    partial = jnp.einsum("td,cd->tc", grads, w_qkv, preferred_element_type=wide).astype(low_type)
    partial, outq = reduce_tokens(
        zs, partial.reshape(GROUPS, n, depth), slabs(gradq, bias_grad[None])
    )
    input_grad = early_grads[0] + jnp.sum(partial.astype(wide), axis=0)

    def own(vector, count):
        return lax.dynamic_slice_in_dim(vector, device * count, count, 0).astype(wide)

    outq = outq.astype(wide)
    kv_out = outq[:, :, :WIDE].reshape(GROUPS, -1, LOCAL, 2, HEAD)
    q_out = outq[:, :, WIDE:].reshape(GROUPS, -1, LOCAL, 2, HEAD)[:, :, :, 0]

    def unpacked(values):
        return jnp.transpose(values, (1, 0, 2, 3)).reshape(-1, depth)

    q_out, k_out, v_out = unpacked(q_out), unpacked(kv_out[:, :, :, 0]), unpacked(kv_out[:, :, :, 1])
    inner_out = jnp.transpose(out1[:, :s], (1, 0, 2)).reshape(s, ff).astype(wide)
    return (
        output,
        input_grad.astype(low_type),
        q_out[:s],
        own(q_out[s], s),
        k_out[:s],
        v_out[:s],
        own(v_out[s], s),
        outm[:s],
        own(outm[s], s),
        own(outm[s + 1], s),
        own(outm[s + 2], s),
        inner_out,
        own(out1[:, s].reshape(ff), e),
        out2,
        own(outm[s + 3], s),
        own(outm[s + 4], s),
        own(outm[s + 5], s),
    )


def on_device(
    tokens,
    cotangent,
    doc_lengths,
    query_weight,
    query_bias,
    key_weight,
    value_weight,
    value_bias,
    mix_weight,
    mix_bias,
    early_gain,
    early_shift,
    inner_weight,
    inner_bias,
    outer_weight,
    outer_bias,
    final_gain,
    final_shift,
):
    n, depth = tokens.shape
    cycle = lax.axis_size("row")
    devices = lax.axis_size("au") * cycle
    s = query_weight.shape[0]
    ff = inner_weight.shape[1]
    quarter = ff // 4
    e = outer_weight.shape[0]
    rows = GROUPS * n
    total_tokens = n * devices
    me = Spot()
    vectors = [
        vector.reshape(1, -1)
        for vector in (
            query_bias, value_bias, mix_bias, early_gain, early_shift,
            outer_bias, final_gain, final_shift,
        )
    ]
    vectors.append(inner_bias.reshape(1, -1))
    toks, queries, w_qkv, vec, kv_all, w1, wm = first_kernel(
        tokens, query_weight, key_weight, value_weight, vectors,
        inner_weight, mix_weight, e,
    )
    queries = queries.reshape(rows, WIDE)
    kv_all = kv_all.reshape(total_tokens, WIDE)
    w_qkv = w_qkv.reshape(depth, -1)
    w1 = w1.reshape(depth, quarter)
    wm = wm.reshape(depth, depth)
    mixed, mixed_wide, lse = near_forward(doc_lengths, queries, kv_all, n, 512)
    output, hidden_grad, grad_all, gradm, sum1, out2 = middle_kernel(
        mixed.reshape(GROUPS, n, PACK), tokens, cotangent, wm, w1, outer_weight, vec, s, e
    )
    grad_all = grad_all.reshape(rows, PACK)
    query_grad, dkv = near_backward(
        doc_lengths, queries, kv_all, grad_all, mixed_wide, lse, n, 512
    )
    pieces, outq, outk, out1, outm = last_kernel(
        dkv.reshape(2, 2, 2, 2, 2, n, WIDE),
        query_grad.reshape(GROUPS, n, WIDE),
        toks,
        w_qkv,
        sum1,
        gradm,
    )
    results = final_kernel(hidden_grad, pieces, outq, outk, out1, out2, outm, s, e)
    return (output,) + tuple(
        result.reshape(-1) if result.shape[0] == 1 else result for result in results
    )


def solution(mesh):
    both = P(("au", "row"), None)
    flat = P(("au", "row"))
    in_specs = (
        both, both, P(), both, flat, both, both, flat, both, flat, flat, flat,
        both, flat, both, flat, flat, flat,
    )
    out_specs = (
        both, both, both, flat, both, both, flat, both, flat, flat, flat,
        both, flat, both, flat, flat, flat,
    )
    fast = mesh.shape["au"] == 4 and mesh.shape["row"] == 2 * GROUPS
    return jax.shard_map(
        on_device if fast else on_device_general, mesh=mesh, in_specs=in_specs, out_specs=out_specs, check_vma=False
    )
```

```python
import functools

import jax
import jax.numpy as jnp
import numpy as np
from jax import lax
from jax.experimental import pallas as pl
from jax.experimental.pallas import tpu as pltpu
from jax.sharding import PartitionSpec as P

HEAD = 64
HEADS = 12
GROUPS = 4
LOCAL = HEADS // GROUPS
LANES = 2 * HEAD
WIDE = LOCAL * LANES
PACK = 256
eps_norm = 1e-06
mask_fill = -1000000000.0
lowest_start = -1e30
low_type = jnp.bfloat16
wide = jnp.float32
MESH = pl.DeviceIdType.MESH
VMEM_LIMIT = 62 * 1024 * 1024
NEAR_LIMIT = 30 * 1024 * 1024


def layer_norm(hidden, gain, shift):
    mean = jnp.mean(hidden, axis=-1, keepdims=True)
    centered = hidden - mean
    spread = jnp.mean(centered * centered, axis=-1, keepdims=True)
    return centered * lax.rsqrt(spread + eps_norm) * gain + shift


def gelu_exact(values):
    return jax.nn.gelu(values, approximate=False)


class Place:
    def __init__(self, zs):
        self.zs = zs
        a = lax.axis_index("au")
        r = lax.axis_index("row")
        self.x, self.c = a // 2, a % 2
        self.y, q = r % 2, r // 2
        self.g, self.z = q % GROUPS, q // GROUPS

    def at(self, x=None, c=None, z=None, g=None, y=None):
        x = self.x if x is None else x
        c = self.c if c is None else c
        z = self.z if z is None else z
        g = self.g if g is None else g
        y = self.y if y is None else y
        return (x * 2 + c, (z * GROUPS + g) * 2 + y)

    def sibling(self):
        return self.at(c=1 - self.c)

    def line(self):
        return [((self.g + k) % GROUPS, (self.g + GROUPS - k) % GROUPS) for k in range(1, GROUPS)]

    def column(self):
        count = self.zs * GROUPS
        q = self.z * GROUPS + self.g
        result = []
        for k in range(1, count):
            to, source = (q + k) % count, (q + count - k) % count
            result.append(((to // GROUPS, to % GROUPS), (source // GROUPS, source % GROUPS)))
        return result

    def plane(self, everywhere=True):
        result = []
        for dx in range(2):
            for dy in range(2):
                for dz in range(self.zs if everywhere else 1):
                    if dx + dy + dz == 0:
                        continue
                    to = ((self.x + dx) % 2, (self.z + dz) % self.zs, (self.y + dy) % 2)
                    source = (
                        (self.x + dx) % 2,
                        (self.z + self.zs - dz) % self.zs,
                        (self.y + dy) % 2,
                    )
                    result.append((to, source))
        return result


class Copies:
    def __init__(self, send, recv, local):
        self.send, self.recv, self.local = send, recv, local
        self.count = 0
        self.local_count = 0
        self.started = []
        self.local_started = []

    def push(self, source, target, device):
        copy = pltpu.make_async_remote_copy(
            src_ref=source,
            dst_ref=target,
            send_sem=self.send.at[self.count],
            recv_sem=self.recv.at[self.count],
            device_id=device,
            device_id_type=MESH,
        )
        self.count += 1
        copy.start()
        self.started.append(copy)
        return copy

    def keep(self, source, target):
        copy = pltpu.make_async_copy(source, target, self.local.at[self.local_count])
        self.local_count += 1
        copy.start()
        return copy

    def finish(self):
        for copy in self.started:
            copy.wait_send()


def greet(devices, partner=None, crossing=None):
    barrier = pltpu.get_barrier_semaphore()
    for device in devices:
        pl.semaphore_signal(barrier, inc=1, device_id=device, device_id_type=MESH)
    if partner is None:
        pl.semaphore_wait(barrier, len(devices))
        return

    @pl.when(crossing)
    def _():
        pl.semaphore_signal(barrier, inc=1, device_id=partner, device_id_type=MESH)
        pl.semaphore_wait(barrier, len(devices) + 1)

    @pl.when(jnp.logical_not(crossing))
    def _():
        pl.semaphore_wait(barrier, len(devices))


def comm_call(body, name, ident, outs, copies, locals_, args, spaces=None, out_spaces=None, scratch=()):
    spaces = [pl.ANY] * len(args) if spaces is None else spaces
    out_spaces = [pl.ANY] * len(outs) if out_spaces is None else out_spaces
    return pl.pallas_call(
        body,
        name=name,
        out_shape=tuple(outs),
        in_specs=[pl.BlockSpec(memory_space=space) for space in spaces],
        out_specs=tuple(pl.BlockSpec(memory_space=space) for space in out_spaces),
        scratch_shapes=[
            pltpu.SemaphoreType.DMA((max(copies, 1),)),
            pltpu.SemaphoreType.DMA((max(copies, 1),)),
            pltpu.SemaphoreType.DMA((max(locals_, 1),)),
            *scratch,
        ],
        compiler_params=pltpu.CompilerParams(
            collective_id=ident, has_side_effects=True, vmem_limit_bytes=VMEM_LIMIT
        ),
    )(*args)


def spread_tokens(zs, tokens, slab):
    n, width = tokens.shape
    groups, rows, columns = slab.shape
    plane = 4 * zs - 1

    def body(tok, piece, tok_all, w_all, send, recv, local):
        me = Place(zs)
        copies = Copies(send, recv, local)
        greet(
            [me.at(g=to) for to, _ in me.line()]
            + [me.at(x=to[0], z=to[1], y=to[2]) for to, _ in me.plane()]
            + [me.sibling()]
        )
        first = [
            copies.push(
                piece.at[to], w_all.at[me.x, me.c, me.z, me.g, me.y], me.at(g=to)
            )
            for to, _ in me.line()
        ]
        own = copies.keep(piece.at[me.g], w_all.at[me.x, me.c, me.z, me.g, me.y])
        arrivals = [copies.push(tok, tok_all.at[me.g], me.at(g=to)) for to, _ in me.line()]
        mine = copies.keep(tok, tok_all.at[me.g])
        own.wait()
        for copy in first:
            copy.wait_recv()
        block = w_all.at[me.x, me.c, me.z, :, me.y]
        second = [
            copies.push(block, block, me.at(x=to[0], z=to[1], y=to[2])) for to, _ in me.plane()
        ]
        arrivals.append(copies.push(block, block, me.sibling()))
        for copy, (_, source) in zip(second, me.plane()):
            copy.wait_recv()
            part = w_all.at[source[0], me.c, source[1], :, source[2]]
            arrivals.append(copies.push(part, part, me.sibling()))
        for copy in arrivals:
            copy.wait_recv()
        mine.wait()
        copies.finish()

    return comm_call(
        body,
        "spread_tokens",
        0,
        [
            jax.ShapeDtypeStruct((GROUPS, n, width), low_type),
            jax.ShapeDtypeStruct((2, 2, zs, GROUPS, 2, rows, columns), low_type),
        ],
        2 * (GROUPS - 1) + 2 * plane + 1,
        2,
        (tokens, slab),
    )


def spread_keys(zs, keys, inner, outer, mix):
    groups, n, width = keys.shape
    quarters, rows, columns = inner.shape
    tall, _ = outer.shape
    plane, column = 4 * zs - 1, GROUPS * zs - 1

    def body(kv, w1s, w2s, wms, kv_all, w1, w2, wm, send, recv, local, swap_send, swap_recv):
        me = Place(zs)
        copies = Copies(send, recv, local)
        crossing = me.c != me.y
        greet(
            [me.at(x=to[0], z=to[1], y=to[2]) for to, _ in me.plane()]
            + [me.at(z=to[0], g=to[1]) for to, _ in me.column()]
            + [me.at(z=to[0], g=to[1], c=me.y, y=me.c) for to, _ in me.column()]
            + [me.sibling()],
            me.at(c=me.y, y=me.c),
            crossing,
        )

        def here(ref):
            return ref.at[me.x, me.c, me.z, me.g, me.y]

        flat = me.plane(everywhere=False)
        own = [
            copies.keep(w1s.at[me.x * 2 + me.y], here(w1)),
            copies.keep(wms, here(wm)),
            copies.keep(kv, kv_all.at[me.x, me.c, me.z, :, me.y]),
        ]
        w1_first = [
            copies.push(w1s.at[to[0] * 2 + to[2]], here(w1), me.at(x=to[0], y=to[2]))
            for to, _ in flat
        ]
        wm_first = [
            copies.push(wms, here(wm), me.at(z=to[0], g=to[1])) for to, _ in me.column()
        ]
        mine = kv_all.at[me.x, me.c, me.z, :, me.y]
        kv_first = [
            copies.push(kv, mine, me.at(x=to[0], z=to[1], y=to[2])) for to, _ in me.plane()
        ]
        arrivals = [copies.push(kv, mine, me.sibling())]
        w2_first = [
            copies.push(
                w2s, w2.at[me.z, me.g, me.y], me.at(z=to[0], g=to[1], c=me.y, y=me.c)
            )
            for to, _ in me.column()
        ]
        exchanged = pltpu.make_async_remote_copy(
            src_ref=w2s,
            dst_ref=w2.at[me.z, me.g, me.y],
            send_sem=swap_send,
            recv_sem=swap_recv,
            device_id=me.at(c=me.y, y=me.c),
            device_id_type=MESH,
        )
        stays = pltpu.make_async_copy(w2s, w2.at[me.z, me.g, me.y], swap_recv)

        @pl.when(crossing)
        def _():
            exchanged.start()

        @pl.when(jnp.logical_not(crossing))
        def _():
            stays.start()

        own[0].wait()
        for copy in w1_first:
            copy.wait_recv()
        block = w1.at[:, me.c, me.z, me.g, :]
        w1_second = [
            copies.push(block, block, me.at(z=to[0], g=to[1])) for to, _ in me.column()
        ]
        arrivals.append(copies.push(block, block, me.sibling()))
        own[1].wait()
        for copy in wm_first:
            copy.wait_recv()
        block = wm.at[me.x, me.c, :, :, me.y]
        wm_second = [copies.push(block, block, me.at(x=to[0], y=to[2])) for to, _ in flat]
        arrivals.append(copies.push(block, block, me.sibling()))
        for copy, (_, source) in zip(kv_first, me.plane()):
            copy.wait_recv()
            part = kv_all.at[source[0], me.c, source[1], :, source[2]]
            arrivals.append(copies.push(part, part, me.sibling()))

        @pl.when(crossing)
        def _():
            exchanged.wait_recv()
            exchanged.wait_send()

        @pl.when(jnp.logical_not(crossing))
        def _():
            stays.wait()

        part = w2.at[me.z, me.g, me.c]
        arrivals.append(copies.push(part, part, me.sibling()))
        for copy, (_, source) in zip(wm_second, flat):
            copy.wait_recv()
            part = wm.at[source[0], me.c, :, :, source[2]]
            arrivals.append(copies.push(part, part, me.sibling()))
        for copy, (_, source) in zip(w2_first, me.column()):
            copy.wait_recv()
            part = w2.at[source[0], source[1], me.c]
            arrivals.append(copies.push(part, part, me.sibling()))
        for copy, (_, source) in zip(w1_second, me.column()):
            copy.wait_recv()
            part = w1.at[:, me.c, source[0], source[1], :]
            arrivals.append(copies.push(part, part, me.sibling()))
        for copy in arrivals:
            copy.wait_recv()
        own[2].wait()
        copies.finish()

    return comm_call(
        body,
        "spread_keys",
        1,
        [
            jax.ShapeDtypeStruct((2, 2, zs, GROUPS, 2, n, width), low_type),
            jax.ShapeDtypeStruct((2, 2, zs, GROUPS, 2, rows, columns), low_type),
            jax.ShapeDtypeStruct((zs, GROUPS, 2, tall, columns), low_type),
            jax.ShapeDtypeStruct((2, 2, zs, GROUPS, 2) + mix.shape, low_type),
        ],
        2 * plane + 1 + 2 * (3 + column + 1 + column) + column + 3 + 8,
        3,
        (keys, inner, outer, mix),
        scratch=(pltpu.SemaphoreType.DMA, pltpu.SemaphoreType.DMA),
    )


def exchange_line(zs, ident, pieces):
    def body(source, target, send, recv, local):
        me = Place(zs)
        copies = Copies(send, recv, local)
        greet([me.at(g=to) for to, _ in me.line()])
        arrivals = [
            copies.push(source.at[to], target.at[me.g], me.at(g=to)) for to, _ in me.line()
        ]
        own = copies.keep(source.at[me.g], target.at[me.g])
        for copy in arrivals:
            copy.wait_recv()
        own.wait()
        copies.finish()

    return comm_call(
        body,
        "exchange_line",
        ident,
        [jax.ShapeDtypeStruct(pieces.shape, pieces.dtype)],
        GROUPS - 1,
        1,
        (pieces,),
    )[0]


def gather_square(zs, ident, rows):
    def body(source, target, send, recv, local):
        me = Place(zs)
        copies = Copies(send, recv, local)
        flat = me.plane(everywhere=False)
        greet([me.at(x=to[0], y=to[2]) for to, _ in flat])
        place = target.at[me.x, me.y]
        arrivals = [copies.push(source, place, me.at(x=to[0], y=to[2])) for to, _ in flat]
        own = copies.keep(source, place)
        for copy in arrivals:
            copy.wait_recv()
        own.wait()
        copies.finish()

    return comm_call(
        body,
        "gather_square",
        ident,
        [jax.ShapeDtypeStruct((2, 2) + rows.shape, rows.dtype)],
        3,
        1,
        (rows,),
    )[0]


def exchange_square(zs, ident, pieces):
    def body(source, target, send, recv, local):
        me = Place(zs)
        copies = Copies(send, recv, local)
        flat = me.plane(everywhere=False)
        greet([me.at(x=to[0], y=to[2]) for to, _ in flat])
        place = target.at[me.x, me.y]
        arrivals = [
            copies.push(source.at[to[0], to[2]], place, me.at(x=to[0], y=to[2]))
            for to, _ in flat
        ]
        own = copies.keep(source.at[me.x, me.y], place)
        for copy in arrivals:
            copy.wait_recv()
        own.wait()
        copies.finish()

    return comm_call(
        body,
        "exchange_square",
        ident,
        [jax.ShapeDtypeStruct(pieces.shape, pieces.dtype)],
        3,
        1,
        (pieces,),
    )[0]


def loop(count, step):
    def body(index, carry):
        step(index)
        return carry

    lax.fori_loop(0, count, body, 0)


def total_of(*values):
    result = values[0].astype(wide)
    for value in values[1:]:
        result = result + value.astype(wide)
    return result


def reduce_keys(zs, dkv, grad1, grad2, gradm):
    n, width = dkv.shape[-2:]
    rows, columns = grad1.shape[-2:]
    rowsm = gradm.shape[-2]
    tall = grad2.shape[-2]
    plane, column = 4 * zs - 1, GROUPS * zs - 1
    count = GROUPS * zs

    def body(
        dkv_ref, g1, g2, gm, dkv_out, out1, out2, outm,
        send, recv, local,
        swap_send, swap_recv, kst, s1, p1, f1, s2, p2, sm, pm, fm, tm,
    ):
        me = Place(zs)
        copies = Copies(send, recv, local)
        crossing = me.c != me.y
        greet(
            [me.at(x=to[0], z=to[1], y=to[2]) for to, _ in me.plane()]
            + [me.at(z=to[0], g=to[1]) for to, _ in me.column()]
            + [me.at(z=to[0], g=to[1], c=me.y, y=me.c) for to, _ in me.column()]
            + [me.sibling()],
            me.at(c=me.y, y=me.c),
            crossing,
        )

        flat = me.plane(everywhere=False)
        other = 1 - me.c
        order = [to for to, _ in me.plane()] + [(me.x, me.z, me.y)]
        w1_half = copies.push(g1.at[:, other], s1, me.sibling())
        w2_half = copies.push(g2.at[:, :, other], s2, me.sibling())
        k_half = [
            copies.push(
                dkv_ref.at[to[0], other, to[1], :, to[2]], kst.at[to[0], to[1], to[2]], me.sibling()
            )
            for to in order
        ]
        wm_half = copies.push(gm.at[:, other], sm, me.sibling())

        w1_half.wait_recv()

        def add1(index):
            x, z, g, y = index // (count * 2), index // (GROUPS * 2) % zs, index // 2 % GROUPS, index % 2
            s1[x, z, g, y] = total_of(s1[x, z, g, y], g1[x, me.c, z, g, y]).astype(low_type)

        loop(4 * count, add1)
        w1_push = [
            copies.push(s1.at[:, to[0], to[1], :], p1.at[slot], me.at(z=to[0], g=to[1]))
            for slot, (to, _) in enumerate(me.column())
        ]
        w2_half.wait_recv()

        def add2(index):
            z, g = index // GROUPS, index % GROUPS
            s2[z, g] = total_of(s2[z, g], g2[z, g, me.c]).astype(low_type)

        loop(count, add2)
        w2_push = [
            copies.push(
                s2.at[to[0], to[1]], p2.at[slot + 1], me.at(z=to[0], g=to[1], c=me.y, y=me.c)
            )
            for slot, (to, _) in enumerate(me.column())
        ]
        exchanged = pltpu.make_async_remote_copy(
            src_ref=s2.at[me.z, me.g],
            dst_ref=p2.at[0],
            send_sem=swap_send,
            recv_sem=swap_recv,
            device_id=me.at(c=me.y, y=me.c),
            device_id_type=MESH,
        )
        stays = pltpu.make_async_copy(s2.at[me.z, me.g], p2.at[0], swap_recv)

        @pl.when(crossing)
        def _():
            exchanged.start()

        @pl.when(jnp.logical_not(crossing))
        def _():
            stays.start()

        k_push = []
        for slot, to in enumerate(order):
            k_half[slot].wait_recv()

            def addk(g, to=to):
                kst[to[0], to[1], to[2], g] = total_of(
                    kst[to[0], to[1], to[2], g], dkv_ref[to[0], me.c, to[1], g, to[2]]
                ).astype(low_type)

            loop(GROUPS, addk)
            if slot < plane:
                k_push.append(
                    copies.push(
                        kst.at[to[0], to[1], to[2]],
                        dkv_out.at[slot],
                        me.at(x=to[0], z=to[1], y=to[2]),
                    )
                )
        wm_half.wait_recv()

        def addm(index):
            x, z, g, y = index // (count * 2), index // (GROUPS * 2) % zs, index // 2 % GROUPS, index % 2
            sm[x, z, g, y] = total_of(sm[x, z, g, y], gm[x, me.c, z, g, y]).astype(low_type)

        loop(4 * count, addm)
        wm_push = [
            copies.push(sm.at[to[0], :, :, to[2]], pm.at[slot], me.at(x=to[0], y=to[2]))
            for slot, (to, _) in enumerate(flat)
        ]
        keep = copies.keep(kst.at[me.x, me.z, me.y], dkv_out.at[plane])
        for copy in wm_push:
            copy.wait_recv()

        def addf(index):
            z, g = index // GROUPS, index % GROUPS
            fm[z, g] = total_of(sm[me.x, z, g, me.y], pm[0, z, g], pm[1, z, g], pm[2, z, g]).astype(
                low_type
            )

        loop(count, addf)
        wm_last = [
            copies.push(fm.at[to[0], to[1]], tm.at[slot], me.at(z=to[0], g=to[1]))
            for slot, (to, _) in enumerate(me.column())
        ]
        for copy in w1_push:
            copy.wait_recv()

        def addg(index):
            x, y = index // 2, index % 2
            f1[x, y] = total_of(
                s1[x, me.z, me.g, y], *[p1[slot, x, y] for slot in range(column)]
            ).astype(low_type)

        loop(4, addg)
        quarter = out1.at[me.x * 2 + me.y]
        w1_last = [
            copies.push(f1.at[to[0], to[2]], quarter, me.at(x=to[0], y=to[2])) for to, _ in flat
        ]
        keep1 = copies.keep(f1.at[me.x, me.y], quarter)

        @pl.when(crossing)
        def _():
            exchanged.wait_recv()
            exchanged.wait_send()

        @pl.when(jnp.logical_not(crossing))
        def _():
            stays.wait()

        for copy in w2_push:
            copy.wait_recv()
        out2[...] = total_of(*[p2[slot] for slot in range(column + 1)])
        for copy in wm_last:
            copy.wait_recv()
        outm[...] = total_of(fm[me.z, me.g], *[tm[slot] for slot in range(column)])
        for copy in w1_last + k_push:
            copy.wait_recv()
        keep.wait()
        keep1.wait()
        copies.finish()

    vmem = pltpu.VMEM
    return comm_call(
        body,
        "reduce_keys",
        8,
        [
            jax.ShapeDtypeStruct((plane + 1, GROUPS, n, width), low_type),
            jax.ShapeDtypeStruct((4, rows, columns), low_type),
            jax.ShapeDtypeStruct((tall, columns), wide),
            jax.ShapeDtypeStruct((rowsm, columns), wide),
        ],
        3 + (plane + 1) + 2 * column + plane + 3 + column + 3,
        2,
        (dkv, grad1, grad2, gradm),
        spaces=[vmem] * 4,
        out_spaces=[pl.ANY, pl.ANY, vmem, vmem],
        scratch=(
            pltpu.SemaphoreType.DMA,
            pltpu.SemaphoreType.DMA,
            vmem((2, zs, 2, GROUPS, n, width), low_type),
            vmem((2, zs, GROUPS, 2, rows, columns), low_type),
            vmem((column, 2, 2, rows, columns), low_type),
            vmem((2, 2, rows, columns), low_type),
            vmem((zs, GROUPS, tall, columns), low_type),
            vmem((column + 1, tall, columns), low_type),
            vmem((2, zs, GROUPS, 2, rowsm, columns), low_type),
            vmem((3, zs, GROUPS, rowsm, columns), low_type),
            vmem((zs, GROUPS, rowsm, columns), low_type),
            vmem((column, rowsm, columns), low_type),
        ),
    )


def reduce_tokens(zs, dx, gradq):
    rows, columns = gradq.shape[-2:]
    plane = 4 * zs - 1
    count = GROUPS * zs

    def body(dx_ref, gq, dx_out, outq, send, recv, local, sq, pq, fq):
        me = Place(zs)
        copies = Copies(send, recv, local)
        greet(
            [me.at(g=to) for to, _ in me.line()]
            + [me.at(x=to[0], z=to[1], y=to[2]) for to, _ in me.plane()]
            + [me.sibling()]
        )
        half = copies.push(gq.at[:, 1 - me.c], sq, me.sibling())
        arrivals = [
            copies.push(dx_ref.at[to], dx_out.at[me.g], me.at(g=to)) for to, _ in me.line()
        ]
        own = copies.keep(dx_ref.at[me.g], dx_out.at[me.g])
        half.wait_recv()

        def add1(index):
            x, z, g, y = index // (count * 2), index // (GROUPS * 2) % zs, index // 2 % GROUPS, index % 2
            sq[x, z, g, y] = total_of(sq[x, z, g, y], gq[x, me.c, z, g, y]).astype(low_type)

        loop(4 * count, add1)
        second = [
            copies.push(
                sq.at[to[0], to[1], :, to[2]], pq.at[slot], me.at(x=to[0], z=to[1], y=to[2])
            )
            for slot, (to, _) in enumerate(me.plane())
        ]
        for copy in second:
            copy.wait_recv()

        def add2(g):
            fq[g] = total_of(
                sq[me.x, me.z, g, me.y], *[pq[slot, g] for slot in range(plane)]
            ).astype(low_type)

        loop(GROUPS, add2)
        arrivals += [
            copies.push(fq.at[to], outq.at[me.g], me.at(g=to)) for to, _ in me.line()
        ]
        keep = copies.keep(fq.at[me.g], outq.at[me.g])
        for copy in arrivals:
            copy.wait_recv()
        own.wait()
        keep.wait()
        copies.finish()

    vmem = pltpu.VMEM
    return comm_call(
        body,
        "reduce_tokens",
        9,
        [
            jax.ShapeDtypeStruct(dx.shape, low_type),
            jax.ShapeDtypeStruct((GROUPS, rows, columns), low_type),
        ],
        1 + 2 * (GROUPS - 1) + plane,
        2,
        (dx, gradq),
        spaces=[pl.ANY, vmem],
        scratch=(
            vmem((2, zs, GROUPS, 2, rows, columns), low_type),
            vmem((plane, GROUPS, rows, columns), low_type),
            vmem((GROUPS, rows, columns), low_type),
        ),
    )


NEXT = (((1,), (1,)), ((), ()))
DOWN = (((0,), (0,)), ((), ()))


def attend_forward(queries, keys, bounds, low, high, tile, block):
    total_rows = queries.shape[0]

    def body(bounds_ref, q_ref, kv_ref, low_ref, high_ref, out_ref, keep_ref, lse_ref):
        def one(turn, unused):
            rows = pl.ds(pl.multiple_of(turn * tile, tile), tile)
            first, last = low_ref[rows, :], high_ref[rows, :]
            heads = [
                q_ref[rows, h * LANES : (h + 1) * LANES] * jnp.asarray(0.125, low_type)
                for h in range(LOCAL)
            ]

            def step(j, carry):
                begin = pl.multiple_of(j * block, block)
                place = begin + lax.broadcasted_iota(jnp.int32, (tile, block), 1)
                same = (place >= first) & (place < last)
                result = []
                for h in range(LOCAL):
                    top, total, mixed = carry[h]
                    kv = kv_ref[pl.ds(begin, block), h * LANES : (h + 1) * LANES]
                    scores = lax.dot_general(heads[h], kv, NEXT, preferred_element_type=wide)
                    scores = jnp.where(same, scores, mask_fill)
                    new_top = jnp.maximum(top, jnp.max(scores, axis=1, keepdims=True))
                    factor = jnp.exp(top - new_top)
                    powers = jnp.exp(scores - new_top)
                    total = total * factor + jnp.sum(powers, axis=1, keepdims=True)
                    mixed = mixed * factor + jnp.dot(
                        powers.astype(low_type), kv, preferred_element_type=wide
                    )
                    result.append((new_top, total, mixed))
                return tuple(result)

            start = tuple(
                (
                    jnp.full((tile, 1), lowest_start, wide),
                    jnp.zeros((tile, 1), wide),
                    jnp.zeros((tile, LANES), wide),
                )
                for _ in range(LOCAL)
            )
            done = lax.fori_loop(bounds_ref[turn, 0], bounds_ref[turn, 1], step, start)
            lane = lax.broadcasted_iota(jnp.int32, (tile, LANES), 1)
            upper = lane >= HEAD
            mixes = [mixed / total for _, total, mixed in done]
            turned = [pltpu.roll(mixed, HEAD, 1) for mixed in mixes]
            front = jnp.where(upper, mixes[1], turned[0])
            back = jnp.where(upper, 0.0, turned[2])
            both = jnp.concatenate([front, back], axis=1)
            keep_ref[rows, :] = both
            out_ref[rows, :] = both.astype(low_type)
            ends = [top + jnp.log(total) for top, total, _ in done]
            lse_ref[rows, :] = jnp.where(lane == 0, ends[0], jnp.where(lane == 1, ends[1], ends[2]))
            return unused

        lax.fori_loop(0, total_rows // tile, one, 0)

    vmem = pl.BlockSpec(memory_space=pltpu.VMEM)
    return pl.pallas_call(
        body,
        name="attend_forward",
        out_shape=(
            jax.ShapeDtypeStruct((total_rows, PACK), low_type),
            jax.ShapeDtypeStruct((total_rows, PACK), wide),
            jax.ShapeDtypeStruct((total_rows, LANES), wide),
        ),
        in_specs=[pl.BlockSpec(memory_space=pltpu.SMEM)] + [vmem] * 4,
        out_specs=(vmem,) * 3,
        compiler_params=pltpu.CompilerParams(vmem_limit_bytes=VMEM_LIMIT),
    )(bounds, queries, keys, low, high)


def attend_backward(queries, keys, grads, stats, bounds, tile, block):
    total_rows = queries.shape[0]
    tokens = keys.shape[0]

    def body(bounds_ref, q_ref, kv_ref, do_ref, stat_ref, dq_ref, dkv_ref, sums):
        h = pl.program_id(0)
        zeros = jnp.zeros((block, LANES), wide)

        def clear(j, unused):
            sums[pl.ds(pl.multiple_of(j * block, block), block), :] = zeros
            return unused

        lax.fori_loop(0, tokens // block, clear, 0)
        lane = lax.broadcasted_iota(jnp.int32, (tile, LANES), 1)
        upper = lane >= HEAD

        def one(turn, unused):
            rows = pl.ds(pl.multiple_of(turn * tile, tile), tile)
            q = q_ref[rows, :] * jnp.asarray(0.125, low_type)
            front = do_ref[rows, :LANES].astype(wide)
            back = do_ref[rows, LANES:].astype(wide)
            grad = jnp.where(h == 1, front, pltpu.roll(jnp.where(h == 0, front, back), HEAD, 1))
            grad = jnp.where(upper, grad, 0.0).astype(low_type)
            stat = stat_ref[turn, 0]
            first, last = stat[0:1, :], stat[1:2, :]
            lse, delta = stat[2:3, :], stat[3:4, :]

            def step(j, total):
                begin = pl.multiple_of(j * block, block)
                place = (begin + lax.broadcasted_iota(jnp.int32, (block, tile), 0)).astype(wide)
                same = (place >= first) & (place < last)
                kv = kv_ref[pl.ds(begin, block), :]
                scores = lax.dot_general(kv, q, NEXT, preferred_element_type=wide)
                probs = jnp.exp(jnp.where(same, scores, mask_fill) - lse)
                dots = lax.dot_general(kv, grad, NEXT, preferred_element_type=wide)
                score_grad = (probs * (dots - delta)).astype(low_type)
                sums[pl.ds(begin, block), :] += jnp.dot(
                    score_grad, q, preferred_element_type=wide
                ) + jnp.dot(probs.astype(low_type), grad, preferred_element_type=wide)
                return total + lax.dot_general(score_grad, kv, DOWN, preferred_element_type=wide)

            total = lax.fori_loop(
                bounds_ref[turn, 0], bounds_ref[turn, 1], step, jnp.zeros((tile, LANES), wide)
            )
            dq_ref[rows, :] = jnp.where(upper, 0.0, total * 0.125).astype(low_type)
            return unused

        lax.fori_loop(0, total_rows // tile, one, 0)

        def store(j, unused):
            part = pl.ds(pl.multiple_of(j * block, block), block)
            dkv_ref[part, :] = sums[part, :].astype(low_type)
            return unused

        lax.fori_loop(0, tokens // block, store, 0)

    return pl.pallas_call(
        body,
        name="attend_backward",
        grid=(LOCAL,),
        out_shape=(
            jax.ShapeDtypeStruct((total_rows, WIDE), low_type),
            jax.ShapeDtypeStruct((tokens, WIDE), low_type),
        ),
        in_specs=[
            pl.BlockSpec(memory_space=pltpu.SMEM),
            pl.BlockSpec((total_rows, LANES), lambda h: (0, h)),
            pl.BlockSpec((tokens, LANES), lambda h: (0, h)),
            pl.BlockSpec((total_rows, PACK), lambda h: (0, 0)),
            pl.BlockSpec((total_rows // tile, 1, 8, tile), lambda h: (0, h, 0, 0)),
        ],
        out_specs=(
            pl.BlockSpec((total_rows, LANES), lambda h: (0, h)),
            pl.BlockSpec((tokens, LANES), lambda h: (0, h)),
        ),
        scratch_shapes=[pltpu.VMEM((tokens, LANES), wide)],
        compiler_params=pltpu.CompilerParams(vmem_limit_bytes=VMEM_LIMIT),
    )(bounds, queries, keys, grads, stats)


class Spot(Place):
    def __init__(self):
        super().__init__(1)
        self.half = self.g // 2
        self.a = self.x * 2 + self.c
        self.p = (self.x + self.c) % 2
        self.selfish = self.g % 2 == self.p
        self.crossing = self.c != self.y

    def square(self):
        return [(to[0], to[2]) for to, _ in self.plane()]

    def readers(self):
        result = []
        for k in range(GROUPS):
            g = (self.g + k) % GROUPS
            result.append((g, self.at(x=(self.g + self.c) % 2, g=g)))
        return result

    def owners(self):
        result = []
        for dv in range(2):
            for du in range(2):
                u, v = (self.x + du) % 2, (self.half + dv) % 2
                result.append((u * 2 + v, self.at(x=u, g=2 * v + self.p)))
        return result

    def slot(self):
        return self.x * 2 + self.half


def count_of(flag):
    return jnp.where(flag, 1, 0)


def announce(always, maybe):
    barrier = pltpu.get_barrier_semaphore()
    for device in always:
        pl.semaphore_signal(barrier, inc=1, device_id=device, device_id_type=MESH)
    for flag, device in maybe:

        @pl.when(flag)
        def _(device=device):
            pl.semaphore_signal(barrier, inc=1, device_id=device, device_id_type=MESH)

    total = len(always)
    for flag, _ in maybe:
        total = total + count_of(flag)
    return barrier, total


class Scatter:
    def __init__(self, send, recv, here):
        self.send, self.recv, self.here = send, recv, here
        self.copies = []

    def start(self, pieces, target, slot):
        for source, device in pieces:
            self.send_one(source, target, slot, device)

    def send_one(self, source, target, slot, device):
        index = len(self.copies)
        copy = pltpu.make_async_remote_copy(
            src_ref=source,
            dst_ref=target,
            send_sem=self.send.at[index],
            recv_sem=self.recv.at[slot],
            device_id=device,
            device_id_type=MESH,
        )
        self.copies.append(copy)
        if index:
            copy.start()
            return
        stay = pltpu.make_async_copy(source, target, self.recv.at[slot])

        @pl.when(self.here)
        def _():
            stay.start()

        @pl.when(jnp.logical_not(self.here))
        def _():
            copy.start()

    def arrived(self, slot, target):
        pltpu.make_async_copy(target, target, self.recv.at[slot]).wait()

    def finish(self):
        for copy in self.copies[1:]:
            copy.wait_send()

        @pl.when(jnp.logical_not(self.here))
        def _():
            self.copies[0].wait_send()


SMALL = 16


def first_tables(s, e, width):
    column = np.arange(width)
    rows = [column % s, column // s, column % e, column // e]
    return np.stack(rows + [np.zeros_like(column)] * 4).astype(np.int32)


def first_kernel(tokens, wq, wk, wv, vectors, inner, mix, e):
    n, depth = tokens.shape
    s = wq.shape[0]
    quarter = inner.shape[1] // 4
    cols = 2 * WIDE + LANES
    tables = jnp.asarray(first_tables(s, e, 2 * WIDE))
    count = len(vectors)

    def body(*refs):
        tok = refs[0]
        arguments = refs[1 : 7 + count]
        (
            tok_out, q_out, wqkv_out, vec_out, kv_all, w1, wm,
            send, recv, local, tok_send, tok_recv,
            slab, toks, weights, kv_own, q_own, w1s, wms, vec, few,
            loaded, *places,
        ) = refs[7 + count :]
        wq_ref, wk_ref, wv_ref, tab = places[:4]
        vecs = places[4 : 4 + count]
        w1f, wmf = places[4 + count :]
        loads = []
        for index, (argument, place) in enumerate(zip(arguments, places)):
            loads.append(pltpu.make_async_copy(argument, place, loaded.at[index]))
            loads[-1].start()
        me = Spot()
        copies = Copies(send, recv, local)
        square = me.square()
        line = [to for to, _ in me.line()]
        sources = [device for _, device in me.owners()]
        barrier, expected = announce(
            [me.at(x=x, y=y) for x, y in square]
            + [me.at(g=to) for to in line]
            + sources[1:]
            + [me.sibling()],
            [(jnp.logical_not(me.selfish), sources[0])],
        )
        for copy in loads:
            copy.wait()
        lane = lax.broadcasted_iota(jnp.int32, (s, LANES), 1)
        lower = lane < HEAD
        for head in range(HEADS):
            pair = slice(head // 2 * LANES, head // 2 * LANES + LANES)
            q, k, v = wq_ref[:, pair], wk_ref[:, pair], wv_ref[:, pair]
            if head % 2:
                q, k = pltpu.roll(q, HEAD, 1), pltpu.roll(k, HEAD, 1)
            else:
                v = pltpu.roll(v, HEAD, 1)
            g, h = head // LOCAL, head % LOCAL
            slab[g, :, h * LANES : (h + 1) * LANES] = jnp.where(lower, k, v).astype(low_type)
            slab[g, :, WIDE + h * LANES : WIDE + (h + 1) * LANES] = jnp.where(lower, q, 0.0).astype(
                low_type
            )
        wms[...] = wmf[...].astype(low_type)
        few[...] = jnp.zeros((s, LANES), wide)
        for index in range(count):
            few[index : index + 1, : vecs[index].shape[1]] = vecs[index][...]
        small = few[...]
        for g in range(GROUPS):
            slab[g, :, 2 * WIDE :] = small.astype(low_type)
        pl.semaphore_wait(barrier, expected)

        view = weights
        place = view.at[me.a, me.g, me.y]
        slab_first = [copies.push(slab.at[to], place, me.at(g=to)) for to in line]
        slab_own = copies.keep(slab.at[me.g], place)
        for w in range(4):
            w1s[w] = w1f[:, w * quarter : (w + 1) * quarter].astype(low_type)
        place = w1.at[me.x, me.c, me.g, me.y]
        w1_first = [
            copies.push(w1s.at[x * 2 + y], place, me.at(x=x, y=y)) for x, y in square
        ]
        w1_own = copies.keep(w1s.at[me.x * 2 + me.y], place)
        wm_own = copies.keep(wms, wm.at[me.x, me.c, me.g, me.y])

        arrivals, weight_arrivals = [], []
        slab_own.wait()
        for copy in slab_first:
            copy.wait_recv()
        wm_first = [
            copies.push(wms, wm.at[me.x, me.c, me.g, me.y], me.at(g=to)) for to in line
        ]
        tokens_go = Scatter(tok_send, tok_recv, me.selfish)
        tokens_go.start([(tok, device) for _, device in me.readers()], toks.at[me.slot()], me.slot())
        block = view.at[me.a, :, me.y]
        slab_second = [copies.push(block, block, me.at(x=x, y=y)) for x, y in square]
        weight_arrivals.append(copies.push(block, block, me.sibling()))
        for copy, (x, y) in zip(slab_second, square):
            copy.wait_recv()
            block = view.at[x * 2 + me.c, :, y]
            weight_arrivals.append(copies.push(block, block, me.sibling()))
        wm_own.wait()
        for copy in wm_first:
            copy.wait_recv()
        block = wm.at[me.x, me.c, :, me.y]
        wm_second = [copies.push(block, block, me.at(x=x, y=y)) for x, y in square]
        arrivals.append(copies.push(block, block, me.sibling()))
        w1_own.wait()
        for copy in w1_first:
            copy.wait_recv()
        for copy in weight_arrivals:
            copy.wait_recv()

        table = tab[...]

        def spread(pieces, within, owner):
            count = pieces.shape[0] * SMALL
            item = lax.broadcasted_iota(jnp.int32, (count, 2 * WIDE), 0)
            index = lax.broadcasted_iota(jnp.int32, (LANES, 2 * WIDE), 0)
            chosen = jnp.where(index == within, 1.0, 0.0).astype(low_type)
            pieces = pieces.astype(wide).reshape(count, LANES).astype(low_type)
            found = jnp.dot(pieces, chosen, preferred_element_type=wide)
            found = jnp.where((item >> 4) == owner, found, 0.0)
            return jnp.sum(found.reshape(count // SMALL, SMALL, 2 * WIDE), axis=0)

        every = spread(
            view[:, :, :, :SMALL, 2 * WIDE :].reshape(32, SMALL, LANES), table[0:1], table[1:2]
        )
        w_me = me.x * 2 + me.y
        inner_bias = spread(
            view[w_me, :, :, :SMALL, 2 * WIDE :].reshape(8, SMALL, LANES), table[2:3], table[3:4]
        )
        rows16 = lax.broadcasted_iota(jnp.int32, (SMALL, 2 * WIDE), 0)
        vec[...] = jnp.where(rows16 == 8, inner_bias, every)
        turned = pltpu.roll(every, 2 * WIDE - me.g * LOCAL * HEAD, 1)
        lower = lax.broadcasted_iota(jnp.int32, (1, LANES), 1) < HEAD
        biases = [[], []]
        for h in range(LOCAL):
            pair = slice(h // 2 * LANES, h // 2 * LANES + LANES)
            q, v = turned[0:1, pair], turned[1:2, pair]
            if h % 2:
                q = pltpu.roll(q, HEAD, 1)
            else:
                v = pltpu.roll(v, HEAD, 1)
            biases[0].append(jnp.where(lower, 0.0, v))
            biases[1].append(jnp.where(lower, q, 0.0))
        bias = jnp.concatenate(biases[0] + biases[1], axis=1)

        matrix = weights[:, :, :, :, : 2 * WIDE].reshape(depth, 2 * WIDE)
        kept, kv_first = [copies.keep(weights, wqkv_out), copies.keep(vec, vec_out)], []
        for dv in range(2):
            v = (me.half + dv) % 2
            for u in range(2):
                tokens_go.arrived(u * 2 + v, toks.at[u * 2 + v])
            if dv:
                block = w1.at[:, me.c, me.g, :]
                w1_second = [copies.push(block, block, me.at(g=to)) for to in line]
            both = jnp.concatenate([toks[v], toks[2 + v]], axis=0)
            made = jnp.dot(both, matrix, preferred_element_type=wide)
            made = (made + bias).astype(low_type)
            for u in range(2):
                kv_own[v, u] = made[u * n : (u + 1) * n, :WIDE]
                q_own[u * 2 + v] = made[u * n : (u + 1) * n, WIDE:]
            mine = kv_all.at[:, me.c, v, me.p, me.y]
            kv_first.append(
                [copies.push(kv_own.at[v], mine, me.at(x=x, y=y)) for x, y in square]
            )
            arrivals.append(copies.push(kv_own.at[v], mine, me.sibling()))
            kept.append(copies.keep(kv_own.at[v], mine))
        block = w1.at[:, me.c, me.g, :]
        arrivals.append(copies.push(block, block, me.sibling()))
        kept += [copies.keep(toks, tok_out), copies.keep(q_own, q_out)]
        for dv in range(2):
            v = (me.half + dv) % 2
            for copy, (x, y) in zip(kv_first[dv], square):
                copy.wait_recv()
                block = kv_all.at[:, me.c, v, (x + me.c) % 2, y]
                arrivals.append(copies.push(block, block, me.sibling()))
        for copy, (x, y) in zip(wm_second, square):
            copy.wait_recv()
            block = wm.at[x, me.c, :, y]
            arrivals.append(copies.push(block, block, me.sibling()))
        for copy, (_, source) in zip(w1_second, me.line()):
            copy.wait_recv()
            block = w1.at[:, me.c, source, :]
            arrivals.append(copies.push(block, block, me.sibling()))
        for copy in arrivals:
            copy.wait_recv()
        for copy in kept:
            copy.wait()
        tokens_go.finish()
        copies.finish()

    vmem = pltpu.VMEM
    dma = pltpu.SemaphoreType.DMA
    total = 64
    return pl.pallas_call(
        body,
        name="first_kernel",
        out_shape=(
            jax.ShapeDtypeStruct((GROUPS, n, depth), low_type),
            jax.ShapeDtypeStruct((GROUPS, n, WIDE), low_type),
            jax.ShapeDtypeStruct((4, GROUPS, 2, s, cols), low_type),
            jax.ShapeDtypeStruct((SMALL, 2 * WIDE), wide),
            jax.ShapeDtypeStruct((2, 2, 2, 2, 2, n, WIDE), low_type),
            jax.ShapeDtypeStruct((2, 2, GROUPS, 2, s, quarter), low_type),
            jax.ShapeDtypeStruct((2, 2, GROUPS, 2, s, depth), low_type),
        ),
        in_specs=[pl.BlockSpec(memory_space=pltpu.HBM)] * (7 + count),
        out_specs=(pl.BlockSpec(memory_space=pl.ANY),) * 7,
        scratch_shapes=[
            dma((total,)), dma((total,)), dma((12,)), dma((4,)), dma((4,)),
            vmem((GROUPS, s, cols), low_type),
            vmem((GROUPS, n, depth), low_type),
            vmem((4, GROUPS, 2, s, cols), low_type),
            vmem((2, 2, n, WIDE), low_type),
            vmem((GROUPS, n, WIDE), low_type),
            vmem((4, s, quarter), low_type),
            vmem((s, depth), low_type),
            vmem((SMALL, 2 * WIDE), wide),
            vmem((s, LANES), wide),
            dma((6 + count,)),
            *[vmem(item.shape, item.dtype) for item in (wq, wk, wv, tables, *vectors, inner, mix)],
        ],
        compiler_params=pltpu.CompilerParams(
            collective_id=10, has_side_effects=True, vmem_limit_bytes=NEAR_LIMIT
        ),
    )(*[pltpu.with_memory_space_constraint(item, pltpu.HBM) for item in (tokens, wq, wk, wv, tables, *vectors, inner, mix)])


def pass_back(ident, pieces):
    def body(source, target, send, recv):
        me = Spot()
        owners = me.owners()
        readers = [device for _, device in me.readers()]
        barrier, expected = announce(readers[1:], [(jnp.logical_not(me.selfish), readers[0])])
        pl.semaphore_wait(barrier, expected)
        move = Scatter(send, recv, me.selfish)
        move.start([(source.at[slot], device) for slot, device in owners], target.at[me.g], me.g)
        for g in range(GROUPS):
            move.arrived(g, target.at[g])
        move.finish()

    return scatter_call(body, "pass_back", ident, pieces)


def pass_on(ident, pieces):
    def body(source, target, send, recv):
        me = Spot()
        owners = [device for _, device in me.owners()]
        barrier, expected = announce(owners[1:], [(jnp.logical_not(me.selfish), owners[0])])
        pl.semaphore_wait(barrier, expected)
        move = Scatter(send, recv, me.selfish)
        slot = me.slot()
        move.start([(source.at[g], device) for g, device in me.readers()], target.at[slot], slot)
        for index in range(GROUPS):
            move.arrived(index, target.at[index])
        move.finish()

    return scatter_call(body, "pass_on", ident, pieces)


def scatter_call(body, name, ident, pieces):
    return pl.pallas_call(
        body,
        name=name,
        out_shape=jax.ShapeDtypeStruct(pieces.shape, pieces.dtype),
        in_specs=[pl.BlockSpec(memory_space=pl.ANY)],
        out_specs=pl.BlockSpec(memory_space=pl.ANY),
        scratch_shapes=[pltpu.SemaphoreType.DMA((4,)), pltpu.SemaphoreType.DMA((4,))],
        compiler_params=pltpu.CompilerParams(
            collective_id=ident, has_side_effects=True, vmem_limit_bytes=VMEM_LIMIT
        ),
    )(pieces)


def last_kernel(dkv, dq, tokens, weights, sum1, gradm):
    n = dq.shape[1]
    depth = tokens.shape[-1]
    s = depth // 32
    rows = s + 8
    cut = depth // 2

    def body(
        dkv_ref, dq_ref, tok, w_ref, s1, gm, dx_out, outq, outk, out1, outm,
        send, recv, local, dx_send, dx_recv,
        kst, pk, grads, queries, dxs, gq, sq, pq, fq, gk, sk, pp, fk, p1, f1, sm, pm, fm, tm,
    ):
        me = Spot()
        copies = Copies(send, recv, local)
        square = me.square()
        line = [to for to, _ in me.line()]
        owners = me.owners()
        readers = [device for _, device in me.readers()]
        barrier, expected = announce(
            [me.at(x=x, y=y) for x, y in square]
            + [me.at(g=to) for to in line]
            + readers[1:]
            + [me.sibling()],
            [(jnp.logical_not(me.selfish), readers[0])],
        )
        pl.semaphore_wait(barrier, expected)
        other = 1 - me.c
        k_half = []
        for dv in range(2):
            v = (me.half + dv) % 2
            k_half += [
                copies.push(dkv_ref.at[u, other, v], kst.at[u, v], me.sibling()) for u in range(2)
            ]

        wm_half = copies.push(gm.at[:, other], sm, me.sibling())
        w1_push = [
            copies.push(s1.at[:, to, :], p1.at[slot], me.at(g=to)) for slot, to in enumerate(line)
        ]

        lower = lax.broadcasted_iota(jnp.int32, (n, LANES), 1) < HEAD
        for slot in range(GROUPS):
            second = pltpu.roll(dq_ref[slot, :, LANES : 2 * LANES].astype(wide), HEAD, 1)
            front = jnp.where(lower, dq_ref[slot, :, :LANES].astype(wide), second)
            queries[slot, :, :LANES] = front.astype(low_type)
            queries[slot, :, LANES:] = dq_ref[slot, :, 2 * LANES :]
            grads[slot, :, WIDE:] = dq_ref[slot]

        def weight_grad(values, target):
            width = values.shape[-1]
            bias = jnp.sum(values.astype(wide), axis=0, keepdims=True)
            bias = jnp.broadcast_to(bias, (8, width)).astype(low_type)
            for half in range(2):
                made = lax.dot_general(
                    tok[:, :, half * cut : (half + 1) * cut].reshape(GROUPS * n, cut),
                    values,
                    DOWN,
                    preferred_element_type=wide,
                ).astype(low_type)
                for index in range(16):
                    place = (half, index // 8, index // 2 % GROUPS, index % 2)
                    target[(*place, slice(None, s))] = made[index * s : (index + 1) * s]
                    target[(*place, slice(s, None))] = bias

        def keys_on(dv):
            v = (me.half + dv) % 2
            for u in range(2):
                k_half[2 * dv + u].wait_recv()
            pushed = []
            for du in range(2):
                for slot, (x, y) in enumerate(square):
                    u, p = (x + du) % 2, (x + me.c) % 2
                    kst[u, v, p, y] = kst[u, v, p, y] + dkv_ref[u, me.c, v, p, y]
                    pushed.append(
                        copies.push(
                            kst.at[u, v, p, y], pk.at[2 * dv + du, slot], me.at(x=x, y=y)
                        )
                    )
            return pushed

        k_push = keys_on(0)
        weight_grad(queries[...].reshape(GROUPS * n, PACK), gq)
        q_half = copies.push(gq.at[:, other], sq, me.sibling())
        k_push += keys_on(1)

        def at8(index):
            return index // 8, index // 2 % GROUPS, index % 2

        def pair_sum(total, mine):
            def add(index):
                x, g, y = at8(index)
                total[x, g, y] = total[x, g, y] + mine[x, me.c, g, y]

            loop(16, add)

        def square_push(total, landing):
            return [
                copies.push(total.at[x, :, y], landing.at[slot], me.at(x=x, y=y))
                for slot, (x, y) in enumerate(square)
            ]

        def square_sum(result, total, landed):
            def add(g):
                result[g] = total_of(
                    total[me.x, g, me.y], landed[0, g], landed[1, g], landed[2, g]
                ).astype(low_type)

            loop(GROUPS, add)

        q_half.wait_recv()
        pair_sum(sq, gq)
        q_push = square_push(sq, pq)

        move = Scatter(dx_send, dx_recv, me.selfish)
        for index, (slot, device) in enumerate(owners):
            for copy in k_push[3 * index : 3 * index + 3]:
                copy.wait_recv()
            u, v = slot // 2, slot % 2
            grads[slot, :, :WIDE] = total_of(
                kst[u, v, me.p, me.y],
                dkv_ref[u, me.c, v, me.p, me.y],
                *[pk[index, peer] for peer in range(3)],
            ).astype(low_type)
            dxs[slot] = lax.dot_general(
                grads[slot], w_ref[:, : 2 * WIDE], NEXT, preferred_element_type=wide
            ).astype(low_type)
            move.send_one(dxs.at[slot], dx_out.at[me.g], me.g, device)
            if index == 1:
                for copy in q_push:
                    copy.wait_recv()
                square_sum(fq, sq, pq)
                arrivals = [
                    copies.push(fq.at[to], outq.at[me.g], me.at(g=to)) for to in line
                ]
                kept = [copies.keep(fq.at[me.g], outq.at[me.g])]
                for copy in w1_push:
                    copy.wait_recv()

                def addw(index):
                    x, y = index // 2, index % 2
                    f1[x, y] = total_of(
                        s1[x, me.g, y], *[p1[peer, x, y] for peer in range(3)]
                    ).astype(low_type)

                loop(4, addw)
                quarter = out1.at[me.x * 2 + me.y]
                arrivals += [
                    copies.push(f1.at[x, y], quarter, me.at(x=x, y=y)) for x, y in square
                ]
                kept.append(copies.keep(f1.at[me.x, me.y], quarter))
        wm_half.wait_recv()
        pair_sum(sm, gm)
        wm_push = square_push(sm, pm)
        weight_grad(grads[:, :, :WIDE].reshape(GROUPS * n, WIDE), gk)
        half = copies.push(gk.at[:, other], sk, me.sibling())
        half.wait_recv()
        pair_sum(sk, gk)
        push = square_push(sk, pp)
        for copy in wm_push:
            copy.wait_recv()
        square_sum(fm, sm, pm)
        wm_last = [
            copies.push(fm.at[to], tm.at[peer], me.at(g=to)) for peer, to in enumerate(line)
        ]
        for copy in push:
            copy.wait_recv()
        square_sum(fk, sk, pp)
        arrivals += [copies.push(fk.at[to], outk.at[me.g], me.at(g=to)) for to in line]
        kept.append(copies.keep(fk.at[me.g], outk.at[me.g]))
        for copy in wm_last:
            copy.wait_recv()
        outm[...] = total_of(fm[me.g], *[tm[peer] for peer in range(3)])
        for copy in arrivals:
            copy.wait_recv()
        for g in range(GROUPS):
            move.arrived(g, dx_out.at[g])
        for copy in kept:
            copy.wait()
        move.finish()
        copies.finish()

    vmem = pltpu.VMEM
    dma = pltpu.SemaphoreType.DMA
    total = 64

    def stages(width):
        return [
            vmem((2, 2, GROUPS, 2, rows, width), low_type),
            vmem((2, GROUPS, 2, rows, width), low_type),
            vmem((3, GROUPS, rows, width), low_type),
            vmem((GROUPS, rows, width), low_type),
        ]

    return pl.pallas_call(
        body,
        name="last_kernel",
        out_shape=(
            jax.ShapeDtypeStruct((GROUPS, n, depth), low_type),
            jax.ShapeDtypeStruct((GROUPS, rows, PACK), low_type),
            jax.ShapeDtypeStruct((GROUPS, rows, WIDE), low_type),
            jax.ShapeDtypeStruct((4, rows, depth), low_type),
            jax.ShapeDtypeStruct((rows, depth), wide),
        ),
        in_specs=[pl.BlockSpec(memory_space=vmem)] * 6,
        out_specs=[pl.BlockSpec(memory_space=pl.ANY)] * 4 + [pl.BlockSpec(memory_space=vmem)],
        scratch_shapes=[
            dma((total,)), dma((total,)), dma((4,)), dma((4,)), dma((4,)),
            vmem((2, 2, 2, 2, n, WIDE), low_type),
            vmem((4, 3, n, WIDE), low_type),
            vmem((GROUPS, n, 2 * WIDE), low_type),
            vmem((GROUPS, n, PACK), low_type),
            vmem((GROUPS, n, depth), low_type),
            *stages(PACK),
            *stages(WIDE),
            vmem((3, 2, 2, rows, depth), low_type),
            vmem((2, 2, rows, depth), low_type),
            *stages(depth)[1:],
            vmem((3, rows, depth), low_type),
        ],
        compiler_params=pltpu.CompilerParams(
            collective_id=11, has_side_effects=True, vmem_limit_bytes=NEAR_LIMIT
        ),
    )(dkv, dq, tokens, weights, sum1, gradm)


def final_kernel(hidden, pieces, outq, outk, out1, out2, outm, s, e):
    n, depth = hidden.shape
    quarter = out1.shape[-1]

    def body(hid, dx, q_in, k_in, i_in, o_in, m_in, xg, qw, qb, kw, vw, vb, mw, mb, eg, es, iw, ib, ow, ob, fg, fs):
        device = lax.axis_index("au") * lax.axis_size("row") + lax.axis_index("row")
        xg[...] = total_of(hid[...], dx[0], dx[1], dx[2], dx[3]).astype(low_type)
        rows = q_in.shape[1]
        lower = lax.broadcasted_iota(jnp.int32, (rows, LANES), 1) < HEAD

        def part(head):
            g, h = head // LOCAL, head % LOCAL
            return k_in[g, :, h * LANES : (h + 1) * LANES].astype(wide)

        made_q = []
        for g in range(0, GROUPS, 2):
            a0, b0 = q_in[g, :, :LANES].astype(wide), q_in[g, :, LANES:].astype(wide)
            a1 = pltpu.roll(q_in[g + 1, :, :LANES].astype(wide), HEAD, 1)
            b1 = pltpu.roll(q_in[g + 1, :, LANES:].astype(wide), HEAD, 1)
            made_q += [a0, jnp.where(lower, b0, a1), jnp.where(lower, a1, b1)]
        biases = [[], []]
        for pair in range(HEADS // 2):
            span = slice(pair * LANES, (pair + 1) * LANES)
            kv = [part(2 * pair), part(2 * pair + 1)]
            made_k = jnp.where(lower, kv[0], pltpu.roll(kv[1], HEAD, 1))
            made_v = jnp.where(lower, pltpu.roll(kv[0], HEAD, 1), kv[1])
            qw[:, span], kw[:, span], vw[:, span] = made_q[pair][:s], made_k[:s], made_v[:s]
            biases[0].append(made_q[pair][s:])
            biases[1].append(made_v[s:])

        def own(eight, width, shift):
            return pltpu.roll(eight, shift, 1)[0:1, :width]

        turn = (depth - device * s) % depth
        qb[...] = own(jnp.concatenate(biases[0], axis=1), s, turn)
        vb[...] = own(jnp.concatenate(biases[1], axis=1), s, turn)
        mw[...] = m_in[:s]
        extras = pltpu.roll(m_in[s : s + 8, :], turn, 1)
        for index, ref in enumerate((mb, eg, es, ob, fg, fs)):
            ref[...] = extras[index : index + 1, :s]
        for w in range(4):
            iw[:, w * quarter : (w + 1) * quarter] = i_in[w, :s].astype(wide)
        place = lax.axis_index("row") * e
        ib[...] = own(
            i_in[lax.axis_index("au"), s : s + 8, :].astype(wide), e, (quarter - place) % quarter
        )
        ow[...] = o_in[...]

    vmem = pltpu.VMEM

    def shape(*dims):
        return jax.ShapeDtypeStruct(dims, wide)

    return pl.pallas_call(
        body,
        name="final_kernel",
        out_shape=(
            jax.ShapeDtypeStruct((n, depth), low_type),
            shape(s, depth), shape(1, s), shape(s, depth), shape(s, depth), shape(1, s),
            shape(s, depth), shape(1, s), shape(1, s), shape(1, s),
            shape(s, 4 * quarter), shape(1, e), shape(e, depth),
            shape(1, s), shape(1, s), shape(1, s),
        ),
        in_specs=[pl.BlockSpec(memory_space=vmem)] * 7,
        out_specs=(pl.BlockSpec(memory_space=vmem),) * 16,
        compiler_params=pltpu.CompilerParams(vmem_limit_bytes=NEAR_LIMIT),
    )(hidden, pieces, outq, outk, out1, out2, outm)


def gelu_and_slope(value):
    t = 1.0 / (1.0 + (0.3275911 * 0.7071067811865476) * jnp.abs(value))
    bell = jnp.exp(-0.5 * value * value)
    tail = 1.061405429
    for weight in (-1.453152027, 1.421413741, -0.284496736, 0.254829592):
        tail = tail * t + weight
    tail = 0.5 * tail * t * bell
    below = jnp.where(value >= 0.0, 1.0 - tail, tail)
    return value * below, below + value * bell * 0.3989422804014327


def normed(hidden):
    mean = jnp.mean(hidden, axis=-1, keepdims=True)
    centered = hidden - mean
    spread = jnp.mean(centered * centered, axis=-1, keepdims=True)
    inverse = lax.rsqrt(spread + eps_norm)
    return centered * inverse, inverse


def normed_grad(grad, norm, inverse):
    mean = jnp.mean(grad, axis=-1, keepdims=True)
    along = jnp.mean(grad * norm, axis=-1, keepdims=True)
    return inverse * (grad - mean - norm * along)


def down_sum(values):
    return jnp.sum(values, axis=0, keepdims=True)


def middle_kernel(mixed, tokens, cotangent, mix, inner, outer, vec, s, e):
    n, depth = tokens.shape
    quarter = inner.shape[1]
    rows = s + 8
    cut = depth // 2
    hn = n // 2

    def body(
        mixed_ref, tok, cot, wm_in, w1_in, w2f, vec_ref,
        out, hidden_out, do_out, gm, s1, out2,
        send, recv, local, back_send, back_recv, on_send, on_recv, swap_send, swap_recv,
        swap_send2, swap_recv2, wm, w1, w2p, w2s, came, mixed_tok, xs, acts, slopes, parts, sums, bgs, igs, parts2, sums2,
        pieces, extra, attn, own1, own2, g1, g2, s2, p2,
    ):
        me = Spot()
        copies = Copies(send, recv, local)
        square = me.square()
        line = [to for to, _ in me.line()]
        owners = me.owners()
        readers = me.readers()
        swapped = [me.at(g=to, c=me.y, y=me.c) for to in [me.g] + line]
        barrier, expected = announce(
            [me.at(x=x, y=y) for x, y in square]
            + swapped[1:]
            + [device for _, device in readers[1:]]
            + [device for _, device in owners[1:]]
            + [me.sibling()],
            [
                (jnp.logical_not(me.selfish), readers[0][1]),
                (jnp.logical_not(me.selfish), owners[0][1]),
                (me.crossing, swapped[0]),
            ],
        )
        loads = [copies.keep(wm_in, wm), copies.keep(w1_in, w1)]
        w2s[...] = w2f[...].astype(low_type)
        pl.semaphore_wait(barrier, expected)

        back = Scatter(back_send, back_recv, me.selfish)
        back.start([(mixed_ref.at[slot], device) for slot, device in owners], came.at[me.g], me.g)
        lower = lax.broadcasted_iota(jnp.int32, (n, LANES), 1) < HEAD
        loads[0].wait()
        for g in range(GROUPS):
            back.arrived(g, came.at[g])
        w2_place = w2p.at[me.g, me.y]
        w2_first = [copies.push(w2s, w2_place, device) for device in swapped[1:]]
        w2_swap = pltpu.make_async_remote_copy(
            src_ref=w2s,
            dst_ref=w2_place,
            send_sem=swap_send2,
            recv_sem=swap_recv2,
            device_id=swapped[0],
            device_id_type=MESH,
        )
        w2_stays = pltpu.make_async_copy(w2s, w2_place, swap_recv2)

        @pl.when(me.crossing)
        def _():
            w2_swap.start()

        @pl.when(jnp.logical_not(me.crossing))
        def _():
            w2_stays.start()

        for half in range(2):
            a0 = came[2 * half, :, :LANES]
            b0 = came[2 * half, :, LANES:].astype(wide)
            a1 = pltpu.roll(came[2 * half + 1, :, :LANES].astype(wide), HEAD, 1)
            b1 = pltpu.roll(came[2 * half + 1, :, LANES:].astype(wide), HEAD, 1)
            base = half * 3 * LANES
            mixed_tok[:, base : base + LANES] = a0
            mixed_tok[:, base + LANES : base + 2 * LANES] = jnp.where(lower, b0, a1).astype(low_type)
            mixed_tok[:, base + 2 * LANES : base + 3 * LANES] = jnp.where(lower, a1, b1).astype(
                low_type
            )

        def vector(index):
            return vec_ref[index : index + 1, :]

        mix = jnp.dot(mixed_tok[...], wm[...], preferred_element_type=wide) + vector(2)
        norm1, inverse1 = normed(tok[...].astype(wide) + mix)
        early = norm1 * vector(3) + vector(4)
        mine = me.x * 2 + me.y
        halves = [slice(0, hn), slice(hn, n)]

        def send_rows(ref, h):
            place = ref.at[h, mine]
            return [copies.push(place, place, me.at(x=x, y=y)) for x, y in square]

        def send_back(ref, landing, h):
            return [
                copies.push(ref.at[h, x * 2 + y], landing.at[h, mine], me.at(x=x, y=y))
                for x, y in square
            ]

        def arrive(started):
            for copy in started:
                copy.wait_recv()

        def received(landing, h):
            return [landing[h, x * 2 + y] for x, y in square]

        early_go = []
        for h, half in enumerate(halves):
            xs[h, mine] = early[half].astype(low_type)
            early_go.append(send_rows(xs, h))
        loads[1].wait()

        def outer_weight():
            return w2p[...].reshape(quarter, depth)

        branch_go = []
        for h in range(2):
            arrive(early_go[h])
            inner = jnp.dot(
                xs[h].reshape(4 * hn, depth), w1[...], preferred_element_type=wide
            ) + vector(8)
            act, slope = gelu_and_slope(inner)
            act = act.astype(low_type)
            acts[h] = act.reshape(4, hn, quarter)
            slopes[h] = slope
            if h == 0:

                @pl.when(me.crossing)
                def _():
                    w2_swap.wait_recv()
                    w2_swap.wait_send()

                @pl.when(jnp.logical_not(me.crossing))
                def _():
                    w2_stays.wait()

                block = w2p.at[me.g, me.c]
                w2_last = [copies.push(block, block, me.sibling())]
                for copy, (_, source) in zip(w2_first, me.line()):
                    copy.wait_recv()
                    block = w2p.at[source, me.c]
                    w2_last.append(copies.push(block, block, me.sibling()))
                arrive(w2_last)
            made = jnp.dot(act, outer_weight(), preferred_element_type=wide).reshape(4, hn, depth)
            own1[h] = made
            parts[h] = made.astype(low_type)
            branch_go.append(send_back(parts, sums, h))

        grad_go, final_grads, norm_sums, cot_sums = [], [], [], []
        for h, half in enumerate(halves):
            arrive(branch_go[h])
            branch = total_of(own1[h, mine], *received(sums, h)) + vector(5)
            norm2, inverse2 = normed(early[half] + branch)
            out[half, :] = (norm2 * vector(6) + vector(7)).astype(low_type)
            cot_wide = cot[half, :].astype(wide)
            final_grad = normed_grad(cot_wide * vector(6), norm2, inverse2)
            bgs[h, mine] = final_grad.astype(low_type)
            grad_go.append(send_rows(bgs, h))
            final_grads.append(final_grad)
            norm_sums.append(down_sum(cot_wide * norm2))
            cot_sums.append(down_sum(cot_wide))
        extra[...] = jnp.zeros_like(extra)
        extra[3:4, :] = down_sum(bgs[0, mine].astype(wide)) + down_sum(bgs[1, mine].astype(wide))
        extra[4:5, :] = norm_sums[0] + norm_sums[1]
        extra[5:6, :] = cot_sums[0] + cot_sums[1]

        token_go = []
        for h in range(2):
            arrive(grad_go[h])
            grad = lax.dot_general(
                bgs[h].reshape(4 * hn, depth), outer_weight(), NEXT, preferred_element_type=wide
            )
            grad = (grad * slopes[h]).astype(low_type)
            igs[h] = grad.reshape(4, hn, quarter)
            made = lax.dot_general(grad, w1[...], NEXT, preferred_element_type=wide)
            made = made.reshape(4, hn, depth)
            own2[h] = made
            parts2[h] = made.astype(low_type)
            token_go.append(send_back(parts2, sums2, h))

        other = 1 - me.c
        grads = bgs[...].reshape(4 * n, depth)
        for half in range(2):
            span = slice(half * cut, (half + 1) * cut)
            made = lax.dot_general(
                acts[:, :, :, span].reshape(4 * n, cut), grads, DOWN, preferred_element_type=wide
            )
            g2[2 * half : 2 * half + 2] = made.astype(low_type).reshape(2, 2, e, depth)
        w2_half = copies.push(g2.at[:, other], s2, me.sibling())

        grads = igs[...].reshape(4 * n, quarter)
        bias = jnp.broadcast_to(down_sum(grads.astype(wide)), (8, quarter)).astype(low_type)
        for half in range(2):
            span = slice(half * cut, (half + 1) * cut)
            made = lax.dot_general(
                xs[:, :, :, span].reshape(4 * n, cut), grads, DOWN, preferred_element_type=wide
            ).astype(low_type)
            for index in range(16):
                place = (half, index // 8, index // 2 % GROUPS, index % 2)
                g1[(*place, slice(None, s))] = made[index * s : (index + 1) * s]
                g1[(*place, slice(s, None))] = bias
        w1_half = copies.push(g1.at[:, other], s1, me.sibling())
        w2_half.wait_recv()

        def add2(g):
            s2[g] = s2[g] + g2[g, me.c]

        loop(GROUPS, add2)
        w2_push = [
            copies.push(s2.at[to], p2.at[index + 1], swapped[index + 1])
            for index, to in enumerate(line)
        ]
        exchanged = pltpu.make_async_remote_copy(
            src_ref=s2.at[me.g],
            dst_ref=p2.at[0],
            send_sem=swap_send,
            recv_sem=swap_recv,
            device_id=swapped[0],
            device_id_type=MESH,
        )
        stays = pltpu.make_async_copy(s2.at[me.g], p2.at[0], swap_recv)

        @pl.when(me.crossing)
        def _():
            exchanged.start()

        @pl.when(jnp.logical_not(me.crossing))
        def _():
            stays.start()

        w1_half.wait_recv()

        def add1(index):
            x, g, y = index // 8, index // 2 % GROUPS, index % 2
            s1[x, g, y] = s1[x, g, y] + g1[x, me.c, g, y]

        loop(16, add1)
        norm_sums, grad_sums, attn_sums = [], [], []
        for h, half in enumerate(halves):
            arrive(token_go[h])
            early_grad = total_of(final_grads[h], own2[h, mine], *received(sums2, h))
            norm_sums.append(down_sum(early_grad * norm1[half]))
            grad_sums.append(down_sum(early_grad))
            hidden = normed_grad(early_grad * vector(3), norm1[half], inverse1[half])
            hidden_out[half, :] = hidden
            attn[half, :] = hidden.astype(low_type)
            attn_sums.append(down_sum(hidden.astype(low_type).astype(wide)))
        extra[0:1, :] = attn_sums[0] + attn_sums[1]
        extra[1:2, :] = norm_sums[0] + norm_sums[1]
        extra[2:3, :] = grad_sums[0] + grad_sums[1]
        attn_grad = attn[...]
        back_grad = lax.dot_general(attn_grad, wm[...], NEXT, preferred_element_type=wide)
        for half in range(2):
            base = half * 3 * LANES
            t0 = back_grad[:, base : base + LANES]
            t1 = back_grad[:, base + LANES : base + 2 * LANES]
            t2 = back_grad[:, base + 2 * LANES : base + 3 * LANES]
            r1, r2 = pltpu.roll(t1, HEAD, 1), pltpu.roll(t2, HEAD, 1)
            pieces[2 * half, :, :LANES] = t0.astype(low_type)
            pieces[2 * half, :, LANES:] = jnp.where(lower, t1, 0.0).astype(low_type)
            pieces[2 * half + 1, :, :LANES] = jnp.where(lower, r1, r2).astype(low_type)
            pieces[2 * half + 1, :, LANES:] = jnp.where(lower, r2, 0.0).astype(low_type)
        onward = Scatter(on_send, on_recv, me.selfish)
        slot = me.slot()
        onward.start([(pieces.at[g], device) for g, device in readers], do_out.at[slot], slot)

        for half in range(2):
            span = slice(half * cut, (half + 1) * cut)
            made = lax.dot_general(
                mixed_tok[:, span], attn_grad, DOWN, preferred_element_type=wide
            ).astype(low_type)
            for index in range(16):
                place = (half, index // 8, index // 2 % GROUPS, index % 2)
                gm[(*place, slice(None, s))] = made[index * s : (index + 1) * s]
                gm[(*place, slice(s, None))] = extra[...].astype(low_type)
        @pl.when(me.crossing)
        def _():
            exchanged.wait_recv()
            exchanged.wait_send()

        @pl.when(jnp.logical_not(me.crossing))
        def _():
            stays.wait()

        for copy in w2_push:
            copy.wait_recv()
        out2[...] = total_of(*[p2[index] for index in range(4)])
        for index in range(GROUPS):
            onward.arrived(index, do_out.at[index])
        back.finish()
        onward.finish()
        copies.finish()

    vmem = pltpu.VMEM
    dma = pltpu.SemaphoreType.DMA
    tall = vmem((2, 4, hn, depth), low_type)
    full = vmem((2, 4, hn, depth), wide)
    high = vmem((2, 4, hn, quarter), low_type)
    space = [vmem] * 3 + [pl.ANY] * 2 + [vmem] * 2
    return pl.pallas_call(
        body,
        name="middle_kernel",
        out_shape=(
            jax.ShapeDtypeStruct((n, depth), low_type),
            jax.ShapeDtypeStruct((n, depth), wide),
            jax.ShapeDtypeStruct((GROUPS, n, PACK), low_type),
            jax.ShapeDtypeStruct((2, 2, GROUPS, 2, rows, depth), low_type),
            jax.ShapeDtypeStruct((2, GROUPS, 2, rows, quarter), low_type),
            jax.ShapeDtypeStruct((e, depth), wide),
        ),
        in_specs=[pl.BlockSpec(memory_space=item) for item in space],
        out_specs=[
            pl.BlockSpec(memory_space=item) for item in (vmem, vmem, pl.ANY, vmem, vmem, vmem)
        ],
        scratch_shapes=[
            dma((48,)), dma((48,)), dma((8,)), dma((4,)), dma((4,)), dma((4,)), dma((4,)), dma, dma, dma, dma,
            vmem((depth, depth), low_type),
            vmem((depth, quarter), low_type),
            vmem((GROUPS, 2, e, depth), low_type),
            vmem((e, depth), low_type),
            vmem((GROUPS, n, PACK), low_type),
            vmem((n, depth), low_type),
            tall, high,
            vmem((2, 4 * hn, quarter), wide),
            tall, tall, tall, high, tall, tall,
            vmem((GROUPS, n, PACK), low_type),
            vmem((8, depth), wide),
            vmem((n, depth), low_type),
            full, full,
            vmem((2, 2, GROUPS, 2, rows, quarter), low_type),
            vmem((GROUPS, 2, e, depth), low_type),
            vmem((GROUPS, e, depth), low_type),
            vmem((4, e, depth), low_type),
        ],
        compiler_params=pltpu.CompilerParams(
            collective_id=12, has_side_effects=True, vmem_limit_bytes=NEAR_LIMIT
        ),
    )(mixed, tokens, cotangent, mix, inner, outer, vec)


def tile_base(me, slot, n):
    u, v = slot // 2, slot % 2
    return ((u * 2 + me.c) * 2 * GROUPS + (v * 2 + me.p) * 2 + me.y) * n


def ends_of(lengths_ref):
    ends = [lengths_ref[0]]
    for index in range(1, lengths_ref.shape[0]):
        ends.append(ends[-1] + lengths_ref[index])
    return ends


def document_of(place, ends):
    first, last = place * 0, place * 0 + ends[-1]
    for end in ends[:-1]:
        before = end <= place
        first = jnp.where(before, end, first)
    for end in reversed(ends[:-1]):
        last = jnp.where(end <= place, last, end)
    return first, last


def blocks_of(base, ends, n, block):
    low, _ = document_of(base, ends)
    _, high = document_of(base + n - 1, ends)
    return low // block, (high + block - 1) // block


def near_forward(lengths, queries, keys, n, block):
    total_rows = queries.shape[0]
    tokens = keys.shape[0]
    chunks = [slice(index * LANES, (index + 1) * LANES) for index in range(block // LANES)]

    def body(lengths_ref, q_ref, kv_ref, out_ref, keep_ref, lse_ref, table):
        me = Spot()
        ends = ends_of(lengths_ref)
        lane = lax.broadcasted_iota(jnp.int32, (n, LANES), 1)
        upper = lane >= HEAD
        column = lax.broadcasted_iota(jnp.int32, (n, LANES), 0)

        def one(slot, unused):
            rows = pl.ds(pl.multiple_of(slot * n, n), n)
            base = tile_base(me, slot, n)
            low, high = blocks_of(base, ends, n, block)
            first, last = document_of(column + base, ends)
            heads = [
                q_ref[rows, h * LANES : (h + 1) * LANES] * jnp.asarray(0.125, low_type)
                for h in range(LOCAL)
            ]

            def score(j, tops):
                begin = pl.multiple_of(j * block, block)
                same = []
                for chunk in chunks:
                    place = lane + (begin + chunk.start)
                    same.append((place >= first) & (place < last))
                result = []
                for h in range(LOCAL):
                    kv = kv_ref[pl.ds(begin, block), h * LANES : (h + 1) * LANES]
                    scores = lax.dot_general(heads[h], kv, NEXT, preferred_element_type=wide)
                    top = tops[h]
                    for chunk, mask in zip(chunks, same):
                        part = jnp.where(mask, scores[:, chunk], mask_fill)
                        table[h, j, :, chunk] = part
                        top = jnp.maximum(top, part)
                    result.append(top)
                return tuple(result)

            tops = lax.fori_loop(
                low, high, score, (jnp.full((n, LANES), lowest_start, wide),) * LOCAL
            )
            tops = [jnp.max(top, axis=1, keepdims=True) for top in tops]
            spread = [jnp.broadcast_to(top, (n, LANES)) for top in tops]

            def weigh(j, carry):
                begin = pl.multiple_of(j * block, block)
                result = []
                for h in range(LOCAL):
                    total, mixed = carry[h]
                    kv = kv_ref[pl.ds(begin, block), h * LANES : (h + 1) * LANES]
                    parts = []
                    for chunk in chunks:
                        part = jnp.exp(table[h, j, :, chunk] - spread[h])
                        total = total + part
                        parts.append(part.astype(low_type))
                    powers = jnp.concatenate(parts, axis=1)
                    mixed = mixed + jnp.dot(powers, kv, preferred_element_type=wide)
                    result.append((total, mixed))
                return tuple(result)

            zero = jnp.zeros((n, LANES), wide)
            done = lax.fori_loop(low, high, weigh, ((zero, zero),) * LOCAL)
            totals = [jnp.sum(total, axis=1, keepdims=True) for total, _ in done]
            mixes = [mixed / total for total, (_, mixed) in zip(totals, done)]
            turned = [pltpu.roll(mixed, HEAD, 1) for mixed in mixes]
            front = jnp.where(upper, mixes[1], turned[0])
            back = jnp.where(upper, 0.0, turned[2])
            both = jnp.concatenate([front, back], axis=1)
            keep_ref[rows, :] = both
            out_ref[rows, :] = both.astype(low_type)
            logs = [top + jnp.log(total) for top, total in zip(tops, totals)]
            logs = jnp.where(lane == 0, logs[0], jnp.where(lane == 1, logs[1], logs[2]))
            lse_ref[slot] = jnp.transpose(logs)[:8]
            return unused

        lax.fori_loop(0, GROUPS, one, 0)

    vmem = pl.BlockSpec(memory_space=pltpu.VMEM)
    return pl.pallas_call(
        body,
        name="near_forward",
        out_shape=(
            jax.ShapeDtypeStruct((total_rows, PACK), low_type),
            jax.ShapeDtypeStruct((total_rows, PACK), wide),
            jax.ShapeDtypeStruct((GROUPS, 8, n), wide),
        ),
        in_specs=[pl.BlockSpec(memory_space=pltpu.SMEM)] + [vmem] * 2,
        out_specs=(vmem,) * 3,
        scratch_shapes=[pltpu.VMEM((LOCAL, tokens // block, n, block), wide)],
        compiler_params=pltpu.CompilerParams(vmem_limit_bytes=NEAR_LIMIT),
    )(lengths, queries, keys)


def near_backward(lengths, queries, keys, grads, mixed, lse, n, block):
    total_rows = queries.shape[0]
    tokens = keys.shape[0]

    def body(lengths_ref, q_ref, kv_ref, do_ref, mixed_ref, lse_ref, dq_ref, dkv_ref, sums):
        me = Spot()
        ends = ends_of(lengths_ref)
        zeros = jnp.zeros((block, LANES), wide)
        spans = [slice(h * LANES, (h + 1) * LANES) for h in range(LOCAL)]

        def clear(j, unused):
            for span in spans:
                sums[pl.ds(pl.multiple_of(j * block, block), block), span] = zeros
            return unused

        lax.fori_loop(0, tokens // block, clear, 0)
        lane = lax.broadcasted_iota(jnp.int32, (n, LANES), 1)
        upper = lane >= HEAD
        along = lax.broadcasted_iota(jnp.int32, (1, n), 1)
        down = lax.broadcasted_iota(jnp.int32, (block, n), 0)

        def upper_halves(ref, rows):
            front = ref[rows, :LANES].astype(wide)
            back = ref[rows, LANES:].astype(wide)
            parts = (pltpu.roll(front, HEAD, 1), front, pltpu.roll(back, HEAD, 1))
            return [jnp.where(upper, part, 0.0) for part in parts]

        def one(slot, unused):
            rows = pl.ds(pl.multiple_of(slot * n, n), n)
            base = tile_base(me, slot, n)
            low, high = blocks_of(base, ends, n, block)
            first, last = document_of(along + base, ends)
            outs, inputs = upper_halves(mixed_ref, rows), upper_halves(do_ref, rows)
            logs, deltas, operands = [], [], []
            for h, span in enumerate(spans):
                q = q_ref[rows, span] * jnp.asarray(0.125, low_type)
                operands.append(jnp.concatenate([q, inputs[h].astype(low_type)], axis=0))
                deltas.append(down_sum(jnp.transpose(inputs[h] * outs[h])))
                logs.append(lse_ref[slot, h : h + 1, :])

            def step(j, totals):
                begin = pl.multiple_of(j * block, block)
                part = pl.ds(begin, block)
                place = down + begin
                same = (place >= first) & (place < last)
                kvs = [kv_ref[part, span] for span in spans]
                made = [
                    lax.dot_general(kv, both, NEXT, preferred_element_type=wide)
                    for kv, both in zip(kvs, operands)
                ]
                result = []
                for h, span in enumerate(spans):
                    probs = jnp.exp(jnp.where(same, made[h][:, :n], mask_fill) - logs[h])
                    score_grad = (probs * (made[h][:, n:] - deltas[h])).astype(low_type)
                    pairs = jnp.concatenate([score_grad, probs.astype(low_type)], axis=1)
                    sums[part, span] += jnp.dot(
                        pairs, operands[h], preferred_element_type=wide
                    )
                    result.append(
                        totals[h]
                        + lax.dot_general(score_grad, kvs[h], DOWN, preferred_element_type=wide)
                    )
                return tuple(result)

            totals = lax.fori_loop(low, high, step, (jnp.zeros((n, LANES), wide),) * LOCAL)
            for total, span in zip(totals, spans):
                dq_ref[rows, span] = jnp.where(upper, 0.0, total * 0.125).astype(low_type)
            return unused

        lax.fori_loop(0, GROUPS, one, 0)

        def store(j, unused):
            part = pl.ds(pl.multiple_of(j * block, block), block)
            for span in spans:
                dkv_ref[part, span] = sums[part, span].astype(low_type)
            return unused

        lax.fori_loop(0, tokens // block, store, 0)

    vmem = pl.BlockSpec(memory_space=pltpu.VMEM)
    return pl.pallas_call(
        body,
        name="near_backward",
        out_shape=(
            jax.ShapeDtypeStruct((total_rows, WIDE), low_type),
            jax.ShapeDtypeStruct((tokens, WIDE), low_type),
        ),
        in_specs=[pl.BlockSpec(memory_space=pltpu.SMEM)] + [vmem] * 5,
        out_specs=(vmem,) * 2,
        scratch_shapes=[pltpu.VMEM((tokens, WIDE), wide)],
        compiler_params=pltpu.CompilerParams(vmem_limit_bytes=NEAR_LIMIT),
    )(lengths, queries, keys, grads, mixed, lse)


def on_device_general(
    tokens,
    cotangent,
    doc_lengths,
    query_weight,
    query_bias,
    key_weight,
    value_weight,
    value_bias,
    mix_weight,
    mix_bias,
    early_gain,
    early_shift,
    inner_weight,
    inner_bias,
    outer_weight,
    outer_bias,
    final_gain,
    final_shift,
):
    n, depth = tokens.shape
    groups, cycle = lax.axis_size("au"), lax.axis_size("row")
    devices = groups * cycle
    zs = cycle // (2 * GROUPS)
    s = query_weight.shape[0]
    ff = inner_weight.shape[1]
    quarter = ff // 4
    e = outer_weight.shape[0]
    rows = GROUPS * n
    total_tokens = n * devices
    me = Place(zs)
    device = lax.axis_index("au") * cycle + lax.axis_index("row")
    w_me = me.x * 2 + me.y

    def by_head(weight):
        return weight.astype(low_type).reshape(-1, GROUPS, LOCAL, HEAD)

    def packed(query, key, value):
        kv = jnp.stack([key, value], axis=3).reshape(-1, GROUPS, WIDE)
        q = jnp.pad(query, ((0, 0), (0, 0), (0, 0), (0, HEAD))).reshape(-1, GROUPS, WIDE)
        return jnp.concatenate([kv, q], axis=2)

    slab = packed(by_head(query_weight), by_head(key_weight), by_head(value_weight))
    slab = jnp.transpose(slab, (1, 0, 2))
    small = jnp.concatenate(
        [
            vector.astype(low_type)
            for vector in (
                query_bias, value_bias, mix_bias, early_gain, early_shift,
                outer_bias, final_gain, final_shift, inner_bias,
            )
        ]
    )
    extra = -s % 8 or 8
    small = jnp.broadcast_to(
        jnp.pad(small, (0, 2 * WIDE - small.shape[0]))[None, None], (GROUPS, extra, 2 * WIDE)
    )
    slab = jnp.concatenate([slab, small], axis=1)
    tok_all, w_all = spread_tokens(zs, tokens, slab)
    tok_all = tok_all.reshape(rows, depth)
    w_qkv = w_all[..., :s, :].reshape(depth, 2 * WIDE)
    small = w_all[..., s, :].reshape(devices, 2 * WIDE)
    names = [small[:, i * s : (i + 1) * s].reshape(depth) for i in range(8)]
    q_bias, v_bias, m_bias, e_gain, e_shift, o_bias, f_gain, f_shift = names
    i_bias = small[:, 8 * s : 8 * s + e].reshape(4, quarter)[w_me].astype(wide)
    q_bias = q_bias.reshape(1, GROUPS, LOCAL, HEAD)
    v_bias = v_bias.reshape(1, GROUPS, LOCAL, HEAD)
    bias = packed(q_bias, jnp.zeros_like(q_bias), v_bias)[0, me.g].astype(wide)

    qkv = (jnp.dot(tok_all, w_qkv, preferred_element_type=wide) + bias).astype(low_type)
    queries = qkv[:, WIDE:]

    inner_slab = jnp.transpose(inner_weight.astype(low_type).reshape(s, 4, quarter), (1, 0, 2))
    kv_all, w1, w2, wm = spread_keys(
        zs,
        qkv[:, :WIDE].reshape(GROUPS, n, WIDE),
        inner_slab,
        outer_weight.astype(low_type),
        mix_weight.astype(low_type),
    )
    kv_all = kv_all.reshape(total_tokens, WIDE)
    w1 = w1.reshape(depth, quarter)
    w2 = w2.reshape(quarter, depth)
    wm = wm.reshape(depth, depth)

    tile, block = 128, 512
    count = doc_lengths.shape[0]
    upto = jnp.arange(count)[None, :] <= jnp.arange(count)[:, None]
    ends = jnp.sum(jnp.where(upto, doc_lengths[None, :], 0), axis=1)
    owners = ((me.x * 2 + me.c) * cycle + me.z * GROUPS * 2 + jnp.arange(GROUPS) * 2 + me.y) * n
    places = (owners[:, None] + jnp.arange(n)[None, :]).reshape(rows)
    before = ends[None, :] <= places[:, None]
    first = jnp.max(jnp.where(before, ends[None, :], 0), axis=1).astype(jnp.int32)
    last = jnp.min(jnp.where(before, total_tokens, ends[None, :]), axis=1).astype(jnp.int32)
    tiles = rows // tile
    bounds = jnp.stack(
        [
            first.reshape(tiles, tile)[:, 0] // block,
            (last.reshape(tiles, tile)[:, -1] + block - 1) // block,
        ],
        axis=1,
    )
    mixed, mixed_wide, lse = attend_forward(
        queries, kv_all, bounds, first[:, None], last[:, None], tile, block
    )
    mixed_tok = exchange_line(zs, 2, mixed.reshape(GROUPS, n, PACK))
    mixed_tok = jnp.transpose(mixed_tok[:, :, : LOCAL * HEAD], (1, 0, 2)).reshape(n, depth)

    attn = jnp.dot(mixed_tok, wm, preferred_element_type=wide) + m_bias.astype(wide)
    early, early_pull = jax.vjp(
        layer_norm, tokens.astype(wide) + attn, e_gain.astype(wide), e_shift.astype(wide)
    )
    early_all = gather_square(zs, 3, early.astype(low_type)).reshape(rows, depth)
    inner = jnp.dot(early_all, w1, preferred_element_type=wide) + i_bias
    act, gelu_pull = jax.vjp(gelu_exact, inner)
    act_low = act.astype(low_type)
    partial = jnp.dot(act_low, w2, preferred_element_type=wide).astype(low_type)
    partial = exchange_square(zs, 4, partial.reshape(2, 2, n, depth))
    branch = jnp.sum(partial.astype(wide), axis=(0, 1)) + o_bias.astype(wide)
    result, final_pull = jax.vjp(
        layer_norm, early + branch, f_gain.astype(wide), f_shift.astype(wide)
    )
    output = result.astype(low_type)
    final_grads = final_pull(cotangent.astype(wide))
    branch_grad = final_grads[0].astype(low_type)
    outer_bias_grad = jnp.sum(branch_grad.astype(wide), axis=0)
    branch_all = gather_square(zs, 5, branch_grad).reshape(rows, depth)
    act_grad = jnp.einsum("td,fd->tf", branch_all, w2, preferred_element_type=wide)
    inner_grad = gelu_pull(act_grad)[0].astype(low_type)
    partial = jnp.einsum("tf,df->td", inner_grad, w1, preferred_element_type=wide).astype(low_type)
    partial = exchange_square(zs, 6, partial.reshape(2, 2, n, depth))
    grad2 = jnp.einsum("tf,td->fd", act_low, branch_all, preferred_element_type=wide)
    grad1 = jnp.einsum("td,tf->df", early_all, inner_grad, preferred_element_type=wide)
    inner_bias_grad = jnp.sum(inner_grad.astype(wide), axis=0)
    early_grad = final_grads[0] + jnp.sum(partial.astype(wide), axis=(0, 1))
    early_grads = early_pull(early_grad)
    attn_grad = early_grads[0].astype(low_type)
    mixed_grad = jnp.einsum("td,cd->tc", attn_grad, wm, preferred_element_type=wide)
    mixed_grad = jnp.transpose(
        mixed_grad.astype(low_type).reshape(n, GROUPS, LOCAL * HEAD), (1, 0, 2)
    )
    mixed_grad = jnp.pad(mixed_grad, ((0, 0), (0, 0), (0, PACK - LOCAL * HEAD)))
    grad_all = exchange_line(zs, 7, mixed_grad).reshape(rows, PACK)
    gradm = jnp.einsum("tc,td->cd", mixed_tok, attn_grad, preferred_element_type=wide)
    mix_bias_grad = jnp.sum(attn_grad.astype(wide), axis=0)

    delta = jnp.sum(
        (grad_all.astype(wide) * mixed_wide)[:, : LOCAL * HEAD].reshape(rows, LOCAL, HEAD), axis=2
    )

    def as_stat(values):
        return jnp.transpose(values.reshape(tiles, tile, LOCAL), (0, 2, 1))

    def same_stat(values):
        return jnp.broadcast_to(
            values.astype(wide).reshape(tiles, 1, tile), (tiles, LOCAL, tile)
        )

    stats = jnp.stack(
        [same_stat(first), same_stat(last), as_stat(lse[:, :LOCAL]), as_stat(delta)], axis=2
    )
    stats = jnp.pad(stats, ((0, 0), (0, 0), (0, 4), (0, 0)))
    query_grad, dkv = attend_backward(queries, kv_all, grad_all, stats, bounds, tile, block)

    def slabs(grad, extras):
        grad = grad.astype(low_type).reshape(devices, s, -1)
        rest = -s % 8
        rest += 0 if rest >= extras.shape[0] else 8
        extras = jnp.concatenate(
            [extras.astype(low_type), jnp.zeros((rest - extras.shape[0], extras.shape[1]), low_type)]
        )
        extras = jnp.broadcast_to(extras[None], (devices,) + extras.shape)
        return jnp.concatenate([grad, extras], axis=1).reshape(2, 2, zs, GROUPS, 2, s + rest, -1)

    mix_extras = jnp.stack(
        [
            mix_bias_grad, early_grads[1], early_grads[2],
            outer_bias_grad, final_grads[1], final_grads[2],
        ]
    )
    dkv, out1, out2, outm = reduce_keys(
        zs,
        dkv.reshape(2, 2, zs, GROUPS, 2, n, WIDE),
        slabs(grad1, inner_bias_grad[None]),
        grad2.astype(low_type).reshape(zs, GROUPS, 2, e, depth),
        slabs(gradm, mix_extras),
    )
    key_grad = jnp.sum(dkv.astype(wide), axis=0).astype(low_type).reshape(rows, WIDE)
    grads = jnp.concatenate([key_grad, query_grad], axis=1)
    gradq = jnp.einsum("tc,td->cd", tok_all, grads, preferred_element_type=wide)
    bias_grad = jnp.sum(grads.astype(wide), axis=0)
    partial = jnp.einsum("td,cd->tc", grads, w_qkv, preferred_element_type=wide).astype(low_type)
    partial, outq = reduce_tokens(
        zs, partial.reshape(GROUPS, n, depth), slabs(gradq, bias_grad[None])
    )
    input_grad = early_grads[0] + jnp.sum(partial.astype(wide), axis=0)

    def own(vector, count):
        return lax.dynamic_slice_in_dim(vector, device * count, count, 0).astype(wide)

    outq = outq.astype(wide)
    kv_out = outq[:, :, :WIDE].reshape(GROUPS, -1, LOCAL, 2, HEAD)
    q_out = outq[:, :, WIDE:].reshape(GROUPS, -1, LOCAL, 2, HEAD)[:, :, :, 0]

    def unpacked(values):
        return jnp.transpose(values, (1, 0, 2, 3)).reshape(-1, depth)

    q_out, k_out, v_out = unpacked(q_out), unpacked(kv_out[:, :, :, 0]), unpacked(kv_out[:, :, :, 1])
    inner_out = jnp.transpose(out1[:, :s], (1, 0, 2)).reshape(s, ff).astype(wide)
    return (
        output,
        input_grad.astype(low_type),
        q_out[:s],
        own(q_out[s], s),
        k_out[:s],
        v_out[:s],
        own(v_out[s], s),
        outm[:s],
        own(outm[s], s),
        own(outm[s + 1], s),
        own(outm[s + 2], s),
        inner_out,
        own(out1[:, s].reshape(ff), e),
        out2,
        own(outm[s + 3], s),
        own(outm[s + 4], s),
        own(outm[s + 5], s),
    )


def on_device(
    tokens,
    cotangent,
    doc_lengths,
    query_weight,
    query_bias,
    key_weight,
    value_weight,
    value_bias,
    mix_weight,
    mix_bias,
    early_gain,
    early_shift,
    inner_weight,
    inner_bias,
    outer_weight,
    outer_bias,
    final_gain,
    final_shift,
):
    n, depth = tokens.shape
    cycle = lax.axis_size("row")
    devices = lax.axis_size("au") * cycle
    s = query_weight.shape[0]
    ff = inner_weight.shape[1]
    quarter = ff // 4
    e = outer_weight.shape[0]
    rows = GROUPS * n
    total_tokens = n * devices
    me = Spot()
    vectors = [
        vector.reshape(1, -1)
        for vector in (
            query_bias, value_bias, mix_bias, early_gain, early_shift,
            outer_bias, final_gain, final_shift,
        )
    ]
    vectors.append(inner_bias.reshape(1, -1))
    toks, queries, w_qkv, vec, kv_all, w1, wm = first_kernel(
        tokens, query_weight, key_weight, value_weight, vectors,
        inner_weight, mix_weight, e,
    )
    queries = queries.reshape(rows, WIDE)
    kv_all = kv_all.reshape(total_tokens, WIDE)
    w_qkv = w_qkv.reshape(depth, -1)
    w1 = w1.reshape(depth, quarter)
    wm = wm.reshape(depth, depth)
    mixed, mixed_wide, lse = near_forward(doc_lengths, queries, kv_all, n, 512)
    output, hidden_grad, grad_all, gradm, sum1, out2 = middle_kernel(
        mixed.reshape(GROUPS, n, PACK), tokens, cotangent, wm, w1, outer_weight, vec, s, e
    )
    grad_all = grad_all.reshape(rows, PACK)
    query_grad, dkv = near_backward(
        doc_lengths, queries, kv_all, grad_all, mixed_wide, lse, n, 512
    )
    pieces, outq, outk, out1, outm = last_kernel(
        dkv.reshape(2, 2, 2, 2, 2, n, WIDE),
        query_grad.reshape(GROUPS, n, WIDE),
        toks,
        w_qkv,
        sum1,
        gradm,
    )
    results = final_kernel(hidden_grad, pieces, outq, outk, out1, out2, outm, s, e)
    return (output,) + tuple(
        result.reshape(-1) if result.shape[0] == 1 else result for result in results
    )


def solution(mesh):
    both = P(("au", "row"), None)
    flat = P(("au", "row"))
    in_specs = (
        both, both, P(), both, flat, both, both, flat, both, flat, flat, flat,
        both, flat, both, flat, flat, flat,
    )
    out_specs = (
        both, both, both, flat, both, both, flat, both, flat, flat, flat,
        both, flat, both, flat, flat, flat,
    )
    fast = mesh.shape["au"] == 4 and mesh.shape["row"] == 2 * GROUPS
    return jax.shard_map(
        on_device if fast else on_device_general, mesh=mesh, in_specs=in_specs, out_specs=out_specs, check_vma=False
    )
```

```python
import functools

import jax
import jax.numpy as jnp
import numpy as np
from jax import lax
from jax.experimental import pallas as pl
from jax.experimental.pallas import tpu as pltpu
from jax.sharding import PartitionSpec as P

HEAD = 64
HEADS = 12
GROUPS = 4
LOCAL = HEADS // GROUPS
LANES = 2 * HEAD
WIDE = LOCAL * LANES
PACK = 256
eps_norm = 1e-06
mask_fill = -1000000000.0
lowest_start = -1e30
low_type = jnp.bfloat16
wide = jnp.float32
MESH = pl.DeviceIdType.MESH
VMEM_LIMIT = 62 * 1024 * 1024
NEAR_LIMIT = 30 * 1024 * 1024
TURN_LIMIT = 48 * 1024 * 1024


def layer_norm(hidden, gain, shift):
    mean = jnp.mean(hidden, axis=-1, keepdims=True)
    centered = hidden - mean
    spread = jnp.mean(centered * centered, axis=-1, keepdims=True)
    return centered * lax.rsqrt(spread + eps_norm) * gain + shift


def gelu_exact(values):
    return jax.nn.gelu(values, approximate=False)


class Place:
    def __init__(self, zs):
        self.zs = zs
        a = lax.axis_index("au")
        r = lax.axis_index("row")
        self.x, self.c = a // 2, a % 2
        self.y, q = r % 2, r // 2
        self.g, self.z = q % GROUPS, q // GROUPS

    def at(self, x=None, c=None, z=None, g=None, y=None):
        x = self.x if x is None else x
        c = self.c if c is None else c
        z = self.z if z is None else z
        g = self.g if g is None else g
        y = self.y if y is None else y
        return (x * 2 + c, (z * GROUPS + g) * 2 + y)

    def sibling(self):
        return self.at(c=1 - self.c)

    def line(self):
        return [((self.g + k) % GROUPS, (self.g + GROUPS - k) % GROUPS) for k in range(1, GROUPS)]

    def column(self):
        count = self.zs * GROUPS
        q = self.z * GROUPS + self.g
        result = []
        for k in range(1, count):
            to, source = (q + k) % count, (q + count - k) % count
            result.append(((to // GROUPS, to % GROUPS), (source // GROUPS, source % GROUPS)))
        return result

    def plane(self, everywhere=True):
        result = []
        for dx in range(2):
            for dy in range(2):
                for dz in range(self.zs if everywhere else 1):
                    if dx + dy + dz == 0:
                        continue
                    to = ((self.x + dx) % 2, (self.z + dz) % self.zs, (self.y + dy) % 2)
                    source = (
                        (self.x + dx) % 2,
                        (self.z + self.zs - dz) % self.zs,
                        (self.y + dy) % 2,
                    )
                    result.append((to, source))
        return result


class Copies:
    def __init__(self, send, recv, local):
        self.send, self.recv, self.local = send, recv, local
        self.count = 0
        self.local_count = 0
        self.started = []
        self.local_started = []

    def push(self, source, target, device):
        copy = pltpu.make_async_remote_copy(
            src_ref=source,
            dst_ref=target,
            send_sem=self.send.at[self.count],
            recv_sem=self.recv.at[self.count],
            device_id=device,
            device_id_type=MESH,
        )
        self.count += 1
        copy.start()
        self.started.append(copy)
        return copy

    def keep(self, source, target):
        copy = pltpu.make_async_copy(source, target, self.local.at[self.local_count])
        self.local_count += 1
        copy.start()
        return copy

    def finish(self):
        for copy in self.started:
            copy.wait_send()


def greet(devices, partner=None, crossing=None):
    barrier = pltpu.get_barrier_semaphore()
    for device in devices:
        pl.semaphore_signal(barrier, inc=1, device_id=device, device_id_type=MESH)
    if partner is None:
        pl.semaphore_wait(barrier, len(devices))
        return

    @pl.when(crossing)
    def _():
        pl.semaphore_signal(barrier, inc=1, device_id=partner, device_id_type=MESH)
        pl.semaphore_wait(barrier, len(devices) + 1)

    @pl.when(jnp.logical_not(crossing))
    def _():
        pl.semaphore_wait(barrier, len(devices))


def comm_call(body, name, ident, outs, copies, locals_, args, spaces=None, out_spaces=None, scratch=()):
    spaces = [pl.ANY] * len(args) if spaces is None else spaces
    out_spaces = [pl.ANY] * len(outs) if out_spaces is None else out_spaces
    return pl.pallas_call(
        body,
        name=name,
        out_shape=tuple(outs),
        in_specs=[pl.BlockSpec(memory_space=space) for space in spaces],
        out_specs=tuple(pl.BlockSpec(memory_space=space) for space in out_spaces),
        scratch_shapes=[
            pltpu.SemaphoreType.DMA((max(copies, 1),)),
            pltpu.SemaphoreType.DMA((max(copies, 1),)),
            pltpu.SemaphoreType.DMA((max(locals_, 1),)),
            *scratch,
        ],
        compiler_params=pltpu.CompilerParams(
            collective_id=ident, has_side_effects=True, vmem_limit_bytes=VMEM_LIMIT
        ),
    )(*args)


def spread_tokens(zs, tokens, slab):
    n, width = tokens.shape
    groups, rows, columns = slab.shape
    plane = 4 * zs - 1

    def body(tok, piece, tok_all, w_all, send, recv, local):
        me = Place(zs)
        copies = Copies(send, recv, local)
        greet(
            [me.at(g=to) for to, _ in me.line()]
            + [me.at(x=to[0], z=to[1], y=to[2]) for to, _ in me.plane()]
            + [me.sibling()]
        )
        first = [
            copies.push(
                piece.at[to], w_all.at[me.x, me.c, me.z, me.g, me.y], me.at(g=to)
            )
            for to, _ in me.line()
        ]
        own = copies.keep(piece.at[me.g], w_all.at[me.x, me.c, me.z, me.g, me.y])
        arrivals = [copies.push(tok, tok_all.at[me.g], me.at(g=to)) for to, _ in me.line()]
        mine = copies.keep(tok, tok_all.at[me.g])
        own.wait()
        for copy in first:
            copy.wait_recv()
        block = w_all.at[me.x, me.c, me.z, :, me.y]
        second = [
            copies.push(block, block, me.at(x=to[0], z=to[1], y=to[2])) for to, _ in me.plane()
        ]
        arrivals.append(copies.push(block, block, me.sibling()))
        for copy, (_, source) in zip(second, me.plane()):
            copy.wait_recv()
            part = w_all.at[source[0], me.c, source[1], :, source[2]]
            arrivals.append(copies.push(part, part, me.sibling()))
        for copy in arrivals:
            copy.wait_recv()
        mine.wait()
        copies.finish()

    return comm_call(
        body,
        "spread_tokens",
        0,
        [
            jax.ShapeDtypeStruct((GROUPS, n, width), low_type),
            jax.ShapeDtypeStruct((2, 2, zs, GROUPS, 2, rows, columns), low_type),
        ],
        2 * (GROUPS - 1) + 2 * plane + 1,
        2,
        (tokens, slab),
    )


def spread_keys(zs, keys, inner, outer, mix):
    groups, n, width = keys.shape
    quarters, rows, columns = inner.shape
    tall, _ = outer.shape
    plane, column = 4 * zs - 1, GROUPS * zs - 1

    def body(kv, w1s, w2s, wms, kv_all, w1, w2, wm, send, recv, local, swap_send, swap_recv):
        me = Place(zs)
        copies = Copies(send, recv, local)
        crossing = me.c != me.y
        greet(
            [me.at(x=to[0], z=to[1], y=to[2]) for to, _ in me.plane()]
            + [me.at(z=to[0], g=to[1]) for to, _ in me.column()]
            + [me.at(z=to[0], g=to[1], c=me.y, y=me.c) for to, _ in me.column()]
            + [me.sibling()],
            me.at(c=me.y, y=me.c),
            crossing,
        )

        def here(ref):
            return ref.at[me.x, me.c, me.z, me.g, me.y]

        flat = me.plane(everywhere=False)
        own = [
            copies.keep(w1s.at[me.x * 2 + me.y], here(w1)),
            copies.keep(wms, here(wm)),
            copies.keep(kv, kv_all.at[me.x, me.c, me.z, :, me.y]),
        ]
        w1_first = [
            copies.push(w1s.at[to[0] * 2 + to[2]], here(w1), me.at(x=to[0], y=to[2]))
            for to, _ in flat
        ]
        wm_first = [
            copies.push(wms, here(wm), me.at(z=to[0], g=to[1])) for to, _ in me.column()
        ]
        mine = kv_all.at[me.x, me.c, me.z, :, me.y]
        kv_first = [
            copies.push(kv, mine, me.at(x=to[0], z=to[1], y=to[2])) for to, _ in me.plane()
        ]
        arrivals = [copies.push(kv, mine, me.sibling())]
        w2_first = [
            copies.push(
                w2s, w2.at[me.z, me.g, me.y], me.at(z=to[0], g=to[1], c=me.y, y=me.c)
            )
            for to, _ in me.column()
        ]
        exchanged = pltpu.make_async_remote_copy(
            src_ref=w2s,
            dst_ref=w2.at[me.z, me.g, me.y],
            send_sem=swap_send,
            recv_sem=swap_recv,
            device_id=me.at(c=me.y, y=me.c),
            device_id_type=MESH,
        )
        stays = pltpu.make_async_copy(w2s, w2.at[me.z, me.g, me.y], swap_recv)

        @pl.when(crossing)
        def _():
            exchanged.start()

        @pl.when(jnp.logical_not(crossing))
        def _():
            stays.start()

        own[0].wait()
        for copy in w1_first:
            copy.wait_recv()
        block = w1.at[:, me.c, me.z, me.g, :]
        w1_second = [
            copies.push(block, block, me.at(z=to[0], g=to[1])) for to, _ in me.column()
        ]
        arrivals.append(copies.push(block, block, me.sibling()))
        own[1].wait()
        for copy in wm_first:
            copy.wait_recv()
        block = wm.at[me.x, me.c, :, :, me.y]
        wm_second = [copies.push(block, block, me.at(x=to[0], y=to[2])) for to, _ in flat]
        arrivals.append(copies.push(block, block, me.sibling()))
        for copy, (_, source) in zip(kv_first, me.plane()):
            copy.wait_recv()
            part = kv_all.at[source[0], me.c, source[1], :, source[2]]
            arrivals.append(copies.push(part, part, me.sibling()))

        @pl.when(crossing)
        def _():
            exchanged.wait_recv()
            exchanged.wait_send()

        @pl.when(jnp.logical_not(crossing))
        def _():
            stays.wait()

        part = w2.at[me.z, me.g, me.c]
        arrivals.append(copies.push(part, part, me.sibling()))
        for copy, (_, source) in zip(wm_second, flat):
            copy.wait_recv()
            part = wm.at[source[0], me.c, :, :, source[2]]
            arrivals.append(copies.push(part, part, me.sibling()))
        for copy, (_, source) in zip(w2_first, me.column()):
            copy.wait_recv()
            part = w2.at[source[0], source[1], me.c]
            arrivals.append(copies.push(part, part, me.sibling()))
        for copy, (_, source) in zip(w1_second, me.column()):
            copy.wait_recv()
            part = w1.at[:, me.c, source[0], source[1], :]
            arrivals.append(copies.push(part, part, me.sibling()))
        for copy in arrivals:
            copy.wait_recv()
        own[2].wait()
        copies.finish()

    return comm_call(
        body,
        "spread_keys",
        1,
        [
            jax.ShapeDtypeStruct((2, 2, zs, GROUPS, 2, n, width), low_type),
            jax.ShapeDtypeStruct((2, 2, zs, GROUPS, 2, rows, columns), low_type),
            jax.ShapeDtypeStruct((zs, GROUPS, 2, tall, columns), low_type),
            jax.ShapeDtypeStruct((2, 2, zs, GROUPS, 2) + mix.shape, low_type),
        ],
        2 * plane + 1 + 2 * (3 + column + 1 + column) + column + 3 + 8,
        3,
        (keys, inner, outer, mix),
        scratch=(pltpu.SemaphoreType.DMA, pltpu.SemaphoreType.DMA),
    )


def exchange_line(zs, ident, pieces):
    def body(source, target, send, recv, local):
        me = Place(zs)
        copies = Copies(send, recv, local)
        greet([me.at(g=to) for to, _ in me.line()])
        arrivals = [
            copies.push(source.at[to], target.at[me.g], me.at(g=to)) for to, _ in me.line()
        ]
        own = copies.keep(source.at[me.g], target.at[me.g])
        for copy in arrivals:
            copy.wait_recv()
        own.wait()
        copies.finish()

    return comm_call(
        body,
        "exchange_line",
        ident,
        [jax.ShapeDtypeStruct(pieces.shape, pieces.dtype)],
        GROUPS - 1,
        1,
        (pieces,),
    )[0]


def gather_square(zs, ident, rows):
    def body(source, target, send, recv, local):
        me = Place(zs)
        copies = Copies(send, recv, local)
        flat = me.plane(everywhere=False)
        greet([me.at(x=to[0], y=to[2]) for to, _ in flat])
        place = target.at[me.x, me.y]
        arrivals = [copies.push(source, place, me.at(x=to[0], y=to[2])) for to, _ in flat]
        own = copies.keep(source, place)
        for copy in arrivals:
            copy.wait_recv()
        own.wait()
        copies.finish()

    return comm_call(
        body,
        "gather_square",
        ident,
        [jax.ShapeDtypeStruct((2, 2) + rows.shape, rows.dtype)],
        3,
        1,
        (rows,),
    )[0]


def exchange_square(zs, ident, pieces):
    def body(source, target, send, recv, local):
        me = Place(zs)
        copies = Copies(send, recv, local)
        flat = me.plane(everywhere=False)
        greet([me.at(x=to[0], y=to[2]) for to, _ in flat])
        place = target.at[me.x, me.y]
        arrivals = [
            copies.push(source.at[to[0], to[2]], place, me.at(x=to[0], y=to[2]))
            for to, _ in flat
        ]
        own = copies.keep(source.at[me.x, me.y], place)
        for copy in arrivals:
            copy.wait_recv()
        own.wait()
        copies.finish()

    return comm_call(
        body,
        "exchange_square",
        ident,
        [jax.ShapeDtypeStruct(pieces.shape, pieces.dtype)],
        3,
        1,
        (pieces,),
    )[0]


def loop(count, step):
    def body(index, carry):
        step(index)
        return carry

    lax.fori_loop(0, count, body, 0)


def total_of(*values):
    result = values[0].astype(wide)
    for value in values[1:]:
        result = result + value.astype(wide)
    return result


def reduce_keys(zs, dkv, grad1, grad2, gradm):
    n, width = dkv.shape[-2:]
    rows, columns = grad1.shape[-2:]
    rowsm = gradm.shape[-2]
    tall = grad2.shape[-2]
    plane, column = 4 * zs - 1, GROUPS * zs - 1
    count = GROUPS * zs

    def body(
        dkv_ref, g1, g2, gm, dkv_out, out1, out2, outm,
        send, recv, local,
        swap_send, swap_recv, kst, s1, p1, f1, s2, p2, sm, pm, fm, tm,
    ):
        me = Place(zs)
        copies = Copies(send, recv, local)
        crossing = me.c != me.y
        greet(
            [me.at(x=to[0], z=to[1], y=to[2]) for to, _ in me.plane()]
            + [me.at(z=to[0], g=to[1]) for to, _ in me.column()]
            + [me.at(z=to[0], g=to[1], c=me.y, y=me.c) for to, _ in me.column()]
            + [me.sibling()],
            me.at(c=me.y, y=me.c),
            crossing,
        )

        flat = me.plane(everywhere=False)
        other = 1 - me.c
        order = [to for to, _ in me.plane()] + [(me.x, me.z, me.y)]
        w1_half = copies.push(g1.at[:, other], s1, me.sibling())
        w2_half = copies.push(g2.at[:, :, other], s2, me.sibling())
        k_half = [
            copies.push(
                dkv_ref.at[to[0], other, to[1], :, to[2]], kst.at[to[0], to[1], to[2]], me.sibling()
            )
            for to in order
        ]
        wm_half = copies.push(gm.at[:, other], sm, me.sibling())

        w1_half.wait_recv()

        def add1(index):
            x, z, g, y = index // (count * 2), index // (GROUPS * 2) % zs, index // 2 % GROUPS, index % 2
            s1[x, z, g, y] = total_of(s1[x, z, g, y], g1[x, me.c, z, g, y]).astype(low_type)

        loop(4 * count, add1)
        w1_push = [
            copies.push(s1.at[:, to[0], to[1], :], p1.at[slot], me.at(z=to[0], g=to[1]))
            for slot, (to, _) in enumerate(me.column())
        ]
        w2_half.wait_recv()

        def add2(index):
            z, g = index // GROUPS, index % GROUPS
            s2[z, g] = total_of(s2[z, g], g2[z, g, me.c]).astype(low_type)

        loop(count, add2)
        w2_push = [
            copies.push(
                s2.at[to[0], to[1]], p2.at[slot + 1], me.at(z=to[0], g=to[1], c=me.y, y=me.c)
            )
            for slot, (to, _) in enumerate(me.column())
        ]
        exchanged = pltpu.make_async_remote_copy(
            src_ref=s2.at[me.z, me.g],
            dst_ref=p2.at[0],
            send_sem=swap_send,
            recv_sem=swap_recv,
            device_id=me.at(c=me.y, y=me.c),
            device_id_type=MESH,
        )
        stays = pltpu.make_async_copy(s2.at[me.z, me.g], p2.at[0], swap_recv)

        @pl.when(crossing)
        def _():
            exchanged.start()

        @pl.when(jnp.logical_not(crossing))
        def _():
            stays.start()

        k_push = []
        for slot, to in enumerate(order):
            k_half[slot].wait_recv()

            def addk(g, to=to):
                kst[to[0], to[1], to[2], g] = total_of(
                    kst[to[0], to[1], to[2], g], dkv_ref[to[0], me.c, to[1], g, to[2]]
                ).astype(low_type)

            loop(GROUPS, addk)
            if slot < plane:
                k_push.append(
                    copies.push(
                        kst.at[to[0], to[1], to[2]],
                        dkv_out.at[slot],
                        me.at(x=to[0], z=to[1], y=to[2]),
                    )
                )
        wm_half.wait_recv()

        def addm(index):
            x, z, g, y = index // (count * 2), index // (GROUPS * 2) % zs, index // 2 % GROUPS, index % 2
            sm[x, z, g, y] = total_of(sm[x, z, g, y], gm[x, me.c, z, g, y]).astype(low_type)

        loop(4 * count, addm)
        wm_push = [
            copies.push(sm.at[to[0], :, :, to[2]], pm.at[slot], me.at(x=to[0], y=to[2]))
            for slot, (to, _) in enumerate(flat)
        ]
        keep = copies.keep(kst.at[me.x, me.z, me.y], dkv_out.at[plane])
        for copy in wm_push:
            copy.wait_recv()

        def addf(index):
            z, g = index // GROUPS, index % GROUPS
            fm[z, g] = total_of(sm[me.x, z, g, me.y], pm[0, z, g], pm[1, z, g], pm[2, z, g]).astype(
                low_type
            )

        loop(count, addf)
        wm_last = [
            copies.push(fm.at[to[0], to[1]], tm.at[slot], me.at(z=to[0], g=to[1]))
            for slot, (to, _) in enumerate(me.column())
        ]
        for copy in w1_push:
            copy.wait_recv()

        def addg(index):
            x, y = index // 2, index % 2
            f1[x, y] = total_of(
                s1[x, me.z, me.g, y], *[p1[slot, x, y] for slot in range(column)]
            ).astype(low_type)

        loop(4, addg)
        quarter = out1.at[me.x * 2 + me.y]
        w1_last = [
            copies.push(f1.at[to[0], to[2]], quarter, me.at(x=to[0], y=to[2])) for to, _ in flat
        ]
        keep1 = copies.keep(f1.at[me.x, me.y], quarter)

        @pl.when(crossing)
        def _():
            exchanged.wait_recv()
            exchanged.wait_send()

        @pl.when(jnp.logical_not(crossing))
        def _():
            stays.wait()

        for copy in w2_push:
            copy.wait_recv()
        out2[...] = total_of(*[p2[slot] for slot in range(column + 1)])
        for copy in wm_last:
            copy.wait_recv()
        outm[...] = total_of(fm[me.z, me.g], *[tm[slot] for slot in range(column)])
        for copy in w1_last + k_push:
            copy.wait_recv()
        keep.wait()
        keep1.wait()
        copies.finish()

    vmem = pltpu.VMEM
    return comm_call(
        body,
        "reduce_keys",
        8,
        [
            jax.ShapeDtypeStruct((plane + 1, GROUPS, n, width), low_type),
            jax.ShapeDtypeStruct((4, rows, columns), low_type),
            jax.ShapeDtypeStruct((tall, columns), wide),
            jax.ShapeDtypeStruct((rowsm, columns), wide),
        ],
        3 + (plane + 1) + 2 * column + plane + 3 + column + 3,
        2,
        (dkv, grad1, grad2, gradm),
        spaces=[vmem] * 4,
        out_spaces=[pl.ANY, pl.ANY, vmem, vmem],
        scratch=(
            pltpu.SemaphoreType.DMA,
            pltpu.SemaphoreType.DMA,
            vmem((2, zs, 2, GROUPS, n, width), low_type),
            vmem((2, zs, GROUPS, 2, rows, columns), low_type),
            vmem((column, 2, 2, rows, columns), low_type),
            vmem((2, 2, rows, columns), low_type),
            vmem((zs, GROUPS, tall, columns), low_type),
            vmem((column + 1, tall, columns), low_type),
            vmem((2, zs, GROUPS, 2, rowsm, columns), low_type),
            vmem((3, zs, GROUPS, rowsm, columns), low_type),
            vmem((zs, GROUPS, rowsm, columns), low_type),
            vmem((column, rowsm, columns), low_type),
        ),
    )


def reduce_tokens(zs, dx, gradq):
    rows, columns = gradq.shape[-2:]
    plane = 4 * zs - 1
    count = GROUPS * zs

    def body(dx_ref, gq, dx_out, outq, send, recv, local, sq, pq, fq):
        me = Place(zs)
        copies = Copies(send, recv, local)
        greet(
            [me.at(g=to) for to, _ in me.line()]
            + [me.at(x=to[0], z=to[1], y=to[2]) for to, _ in me.plane()]
            + [me.sibling()]
        )
        half = copies.push(gq.at[:, 1 - me.c], sq, me.sibling())
        arrivals = [
            copies.push(dx_ref.at[to], dx_out.at[me.g], me.at(g=to)) for to, _ in me.line()
        ]
        own = copies.keep(dx_ref.at[me.g], dx_out.at[me.g])
        half.wait_recv()

        def add1(index):
            x, z, g, y = index // (count * 2), index // (GROUPS * 2) % zs, index // 2 % GROUPS, index % 2
            sq[x, z, g, y] = total_of(sq[x, z, g, y], gq[x, me.c, z, g, y]).astype(low_type)

        loop(4 * count, add1)
        second = [
            copies.push(
                sq.at[to[0], to[1], :, to[2]], pq.at[slot], me.at(x=to[0], z=to[1], y=to[2])
            )
            for slot, (to, _) in enumerate(me.plane())
        ]
        for copy in second:
            copy.wait_recv()

        def add2(g):
            fq[g] = total_of(
                sq[me.x, me.z, g, me.y], *[pq[slot, g] for slot in range(plane)]
            ).astype(low_type)

        loop(GROUPS, add2)
        arrivals += [
            copies.push(fq.at[to], outq.at[me.g], me.at(g=to)) for to, _ in me.line()
        ]
        keep = copies.keep(fq.at[me.g], outq.at[me.g])
        for copy in arrivals:
            copy.wait_recv()
        own.wait()
        keep.wait()
        copies.finish()

    vmem = pltpu.VMEM
    return comm_call(
        body,
        "reduce_tokens",
        9,
        [
            jax.ShapeDtypeStruct(dx.shape, low_type),
            jax.ShapeDtypeStruct((GROUPS, rows, columns), low_type),
        ],
        1 + 2 * (GROUPS - 1) + plane,
        2,
        (dx, gradq),
        spaces=[pl.ANY, vmem],
        scratch=(
            vmem((2, zs, GROUPS, 2, rows, columns), low_type),
            vmem((plane, GROUPS, rows, columns), low_type),
            vmem((GROUPS, rows, columns), low_type),
        ),
    )


NEXT = (((1,), (1,)), ((), ()))
DOWN = (((0,), (0,)), ((), ()))


def attend_forward(queries, keys, bounds, low, high, tile, block):
    total_rows = queries.shape[0]

    def body(bounds_ref, q_ref, kv_ref, low_ref, high_ref, out_ref, keep_ref, lse_ref):
        def one(turn, unused):
            rows = pl.ds(pl.multiple_of(turn * tile, tile), tile)
            first, last = low_ref[rows, :], high_ref[rows, :]
            heads = [
                q_ref[rows, h * LANES : (h + 1) * LANES] * jnp.asarray(0.125, low_type)
                for h in range(LOCAL)
            ]

            def step(j, carry):
                begin = pl.multiple_of(j * block, block)
                place = begin + lax.broadcasted_iota(jnp.int32, (tile, block), 1)
                same = (place >= first) & (place < last)
                result = []
                for h in range(LOCAL):
                    top, total, mixed = carry[h]
                    kv = kv_ref[pl.ds(begin, block), h * LANES : (h + 1) * LANES]
                    scores = lax.dot_general(heads[h], kv, NEXT, preferred_element_type=wide)
                    scores = jnp.where(same, scores, mask_fill)
                    new_top = jnp.maximum(top, jnp.max(scores, axis=1, keepdims=True))
                    factor = jnp.exp(top - new_top)
                    powers = jnp.exp(scores - new_top)
                    total = total * factor + jnp.sum(powers, axis=1, keepdims=True)
                    mixed = mixed * factor + jnp.dot(
                        powers.astype(low_type), kv, preferred_element_type=wide
                    )
                    result.append((new_top, total, mixed))
                return tuple(result)

            start = tuple(
                (
                    jnp.full((tile, 1), lowest_start, wide),
                    jnp.zeros((tile, 1), wide),
                    jnp.zeros((tile, LANES), wide),
                )
                for _ in range(LOCAL)
            )
            done = lax.fori_loop(bounds_ref[turn, 0], bounds_ref[turn, 1], step, start)
            lane = lax.broadcasted_iota(jnp.int32, (tile, LANES), 1)
            upper = lane >= HEAD
            mixes = [mixed / total for _, total, mixed in done]
            turned = [pltpu.roll(mixed, HEAD, 1) for mixed in mixes]
            front = jnp.where(upper, mixes[1], turned[0])
            back = jnp.where(upper, 0.0, turned[2])
            both = jnp.concatenate([front, back], axis=1)
            keep_ref[rows, :] = both
            out_ref[rows, :] = both.astype(low_type)
            ends = [top + jnp.log(total) for top, total, _ in done]
            lse_ref[rows, :] = jnp.where(lane == 0, ends[0], jnp.where(lane == 1, ends[1], ends[2]))
            return unused

        lax.fori_loop(0, total_rows // tile, one, 0)

    vmem = pl.BlockSpec(memory_space=pltpu.VMEM)
    return pl.pallas_call(
        body,
        name="attend_forward",
        out_shape=(
            jax.ShapeDtypeStruct((total_rows, PACK), low_type),
            jax.ShapeDtypeStruct((total_rows, PACK), wide),
            jax.ShapeDtypeStruct((total_rows, LANES), wide),
        ),
        in_specs=[pl.BlockSpec(memory_space=pltpu.SMEM)] + [vmem] * 4,
        out_specs=(vmem,) * 3,
        compiler_params=pltpu.CompilerParams(vmem_limit_bytes=VMEM_LIMIT),
    )(bounds, queries, keys, low, high)


def attend_backward(queries, keys, grads, stats, bounds, tile, block):
    total_rows = queries.shape[0]
    tokens = keys.shape[0]

    def body(bounds_ref, q_ref, kv_ref, do_ref, stat_ref, dq_ref, dkv_ref, sums):
        h = pl.program_id(0)
        zeros = jnp.zeros((block, LANES), wide)

        def clear(j, unused):
            sums[pl.ds(pl.multiple_of(j * block, block), block), :] = zeros
            return unused

        lax.fori_loop(0, tokens // block, clear, 0)
        lane = lax.broadcasted_iota(jnp.int32, (tile, LANES), 1)
        upper = lane >= HEAD

        def one(turn, unused):
            rows = pl.ds(pl.multiple_of(turn * tile, tile), tile)
            q = q_ref[rows, :] * jnp.asarray(0.125, low_type)
            front = do_ref[rows, :LANES].astype(wide)
            back = do_ref[rows, LANES:].astype(wide)
            grad = jnp.where(h == 1, front, pltpu.roll(jnp.where(h == 0, front, back), HEAD, 1))
            grad = jnp.where(upper, grad, 0.0).astype(low_type)
            stat = stat_ref[turn, 0]
            first, last = stat[0:1, :], stat[1:2, :]
            lse, delta = stat[2:3, :], stat[3:4, :]

            def step(j, total):
                begin = pl.multiple_of(j * block, block)
                place = (begin + lax.broadcasted_iota(jnp.int32, (block, tile), 0)).astype(wide)
                same = (place >= first) & (place < last)
                kv = kv_ref[pl.ds(begin, block), :]
                scores = lax.dot_general(kv, q, NEXT, preferred_element_type=wide)
                probs = jnp.exp(jnp.where(same, scores, mask_fill) - lse)
                dots = lax.dot_general(kv, grad, NEXT, preferred_element_type=wide)
                score_grad = (probs * (dots - delta)).astype(low_type)
                sums[pl.ds(begin, block), :] += jnp.dot(
                    score_grad, q, preferred_element_type=wide
                ) + jnp.dot(probs.astype(low_type), grad, preferred_element_type=wide)
                return total + lax.dot_general(score_grad, kv, DOWN, preferred_element_type=wide)

            total = lax.fori_loop(
                bounds_ref[turn, 0], bounds_ref[turn, 1], step, jnp.zeros((tile, LANES), wide)
            )
            dq_ref[rows, :] = jnp.where(upper, 0.0, total * 0.125).astype(low_type)
            return unused

        lax.fori_loop(0, total_rows // tile, one, 0)

        def store(j, unused):
            part = pl.ds(pl.multiple_of(j * block, block), block)
            dkv_ref[part, :] = sums[part, :].astype(low_type)
            return unused

        lax.fori_loop(0, tokens // block, store, 0)

    return pl.pallas_call(
        body,
        name="attend_backward",
        grid=(LOCAL,),
        out_shape=(
            jax.ShapeDtypeStruct((total_rows, WIDE), low_type),
            jax.ShapeDtypeStruct((tokens, WIDE), low_type),
        ),
        in_specs=[
            pl.BlockSpec(memory_space=pltpu.SMEM),
            pl.BlockSpec((total_rows, LANES), lambda h: (0, h)),
            pl.BlockSpec((tokens, LANES), lambda h: (0, h)),
            pl.BlockSpec((total_rows, PACK), lambda h: (0, 0)),
            pl.BlockSpec((total_rows // tile, 1, 8, tile), lambda h: (0, h, 0, 0)),
        ],
        out_specs=(
            pl.BlockSpec((total_rows, LANES), lambda h: (0, h)),
            pl.BlockSpec((tokens, LANES), lambda h: (0, h)),
        ),
        scratch_shapes=[pltpu.VMEM((tokens, LANES), wide)],
        compiler_params=pltpu.CompilerParams(vmem_limit_bytes=VMEM_LIMIT),
    )(bounds, queries, keys, grads, stats)


class Spot(Place):
    def __init__(self):
        super().__init__(1)
        self.half = self.g // 2
        self.a = self.x * 2 + self.c
        self.p = (self.x + self.c) % 2
        self.selfish = self.g % 2 == self.p
        self.crossing = self.c != self.y

    def square(self):
        return [(to[0], to[2]) for to, _ in self.plane()]

    def readers(self):
        result = []
        for k in range(GROUPS):
            g = (self.g + k) % GROUPS
            result.append((g, self.at(x=(self.g + self.c) % 2, g=g)))
        return result

    def owners(self):
        result = []
        for dv in range(2):
            for du in range(2):
                u, v = (self.x + du) % 2, (self.half + dv) % 2
                result.append((u * 2 + v, self.at(x=u, g=2 * v + self.p)))
        return result

    def slot(self):
        return self.x * 2 + self.half


def count_of(flag):
    return jnp.where(flag, 1, 0)


def announce(always, maybe):
    barrier = pltpu.get_barrier_semaphore()
    for device in always:
        pl.semaphore_signal(barrier, inc=1, device_id=device, device_id_type=MESH)
    for flag, device in maybe:

        @pl.when(flag)
        def _(device=device):
            pl.semaphore_signal(barrier, inc=1, device_id=device, device_id_type=MESH)

    total = len(always)
    for flag, _ in maybe:
        total = total + count_of(flag)
    return barrier, total


class Scatter:
    def __init__(self, send, recv, here):
        self.send, self.recv, self.here = send, recv, here
        self.copies = []

    def start(self, pieces, target, slot):
        for source, device in pieces:
            self.send_one(source, target, slot, device)

    def send_one(self, source, target, slot, device):
        index = len(self.copies)
        copy = pltpu.make_async_remote_copy(
            src_ref=source,
            dst_ref=target,
            send_sem=self.send.at[index],
            recv_sem=self.recv.at[slot],
            device_id=device,
            device_id_type=MESH,
        )
        self.copies.append(copy)
        if index:
            copy.start()
            return
        stay = pltpu.make_async_copy(source, target, self.recv.at[slot])

        @pl.when(self.here)
        def _():
            stay.start()

        @pl.when(jnp.logical_not(self.here))
        def _():
            copy.start()

    def arrived(self, slot, target):
        pltpu.make_async_copy(target, target, self.recv.at[slot]).wait()

    def finish(self):
        for copy in self.copies[1:]:
            copy.wait_send()

        @pl.when(jnp.logical_not(self.here))
        def _():
            self.copies[0].wait_send()


SMALL = 16


def first_tables(s, e, width):
    column = np.arange(width)
    rows = [column % s, column // s, column % e, column // e]
    return np.stack(rows + [np.zeros_like(column)] * 4).astype(np.int32)


def first_kernel(tokens, wq, wk, wv, vectors, inner, mix, e):
    n, depth = tokens.shape
    s = wq.shape[0]
    quarter = inner.shape[1] // 4
    cols = 2 * WIDE + LANES
    tables = jnp.asarray(first_tables(s, e, 2 * WIDE))
    count = len(vectors)

    def body(*refs):
        tok = refs[0]
        arguments = refs[1 : 7 + count]
        (
            tok_out, q_out, wqkv_out, vec_out, kv_all, w1, wm,
            send, recv, local, tok_send, tok_recv,
            slab, toks, weights, kv_own, q_own, w1s, wms, vec, few,
            loaded, *places,
        ) = refs[7 + count :]
        wq_ref, wk_ref, wv_ref, tab = places[:4]
        vecs = places[4 : 4 + count]
        w1f, wmf = places[4 + count :]
        loads = []
        for index, (argument, place) in enumerate(zip(arguments, places)):
            loads.append(pltpu.make_async_copy(argument, place, loaded.at[index]))
            loads[-1].start()
        me = Spot()
        copies = Copies(send, recv, local)
        square = me.square()
        line = [to for to, _ in me.line()]
        sources = [device for _, device in me.owners()]
        barrier, expected = announce(
            [me.at(x=x, y=y) for x, y in square]
            + [me.at(g=to) for to in line]
            + sources[1:]
            + [me.sibling()],
            [(jnp.logical_not(me.selfish), sources[0])],
        )
        for copy in loads:
            copy.wait()
        lane = lax.broadcasted_iota(jnp.int32, (s, LANES), 1)
        lower = lane < HEAD
        for head in range(HEADS):
            pair = slice(head // 2 * LANES, head // 2 * LANES + LANES)
            q, k, v = wq_ref[:, pair], wk_ref[:, pair], wv_ref[:, pair]
            if head % 2:
                q, k = pltpu.roll(q, HEAD, 1), pltpu.roll(k, HEAD, 1)
            else:
                v = pltpu.roll(v, HEAD, 1)
            g, h = head // LOCAL, head % LOCAL
            slab[g, :, h * LANES : (h + 1) * LANES] = jnp.where(lower, k, v).astype(low_type)
            slab[g, :, WIDE + h * LANES : WIDE + (h + 1) * LANES] = jnp.where(lower, q, 0.0).astype(
                low_type
            )
        wms[...] = wmf[...].astype(low_type)
        few[...] = jnp.zeros((s, LANES), wide)
        for index in range(count):
            few[index : index + 1, : vecs[index].shape[1]] = vecs[index][...]
        small = few[...]
        for g in range(GROUPS):
            slab[g, :, 2 * WIDE :] = small.astype(low_type)
        pl.semaphore_wait(barrier, expected)

        view = weights
        place = view.at[me.a, me.g, me.y]
        slab_first = [copies.push(slab.at[to], place, me.at(g=to)) for to in line]
        slab_own = copies.keep(slab.at[me.g], place)
        for w in range(4):
            w1s[w] = w1f[:, w * quarter : (w + 1) * quarter].astype(low_type)
        place = w1.at[me.x, me.c, me.g, me.y]
        w1_first = [
            copies.push(w1s.at[x * 2 + y], place, me.at(x=x, y=y)) for x, y in square
        ]
        w1_own = copies.keep(w1s.at[me.x * 2 + me.y], place)
        wm_own = copies.keep(wms, wm.at[me.x, me.c, me.g, me.y])

        arrivals, weight_arrivals = [], []
        slab_own.wait()
        for copy in slab_first:
            copy.wait_recv()
        wm_first = [
            copies.push(wms, wm.at[me.x, me.c, me.g, me.y], me.at(g=to)) for to in line
        ]
        tokens_go = Scatter(tok_send, tok_recv, me.selfish)
        tokens_go.start([(tok, device) for _, device in me.readers()], toks.at[me.slot()], me.slot())
        block = view.at[me.a, :, me.y]
        slab_second = [copies.push(block, block, me.at(x=x, y=y)) for x, y in square]
        weight_arrivals.append(copies.push(block, block, me.sibling()))
        for copy, (x, y) in zip(slab_second, square):
            copy.wait_recv()
            block = view.at[x * 2 + me.c, :, y]
            weight_arrivals.append(copies.push(block, block, me.sibling()))
        wm_own.wait()
        for copy in wm_first:
            copy.wait_recv()
        block = wm.at[me.x, me.c, :, me.y]
        wm_second = [copies.push(block, block, me.at(x=x, y=y)) for x, y in square]
        arrivals.append(copies.push(block, block, me.sibling()))
        w1_own.wait()
        for copy in w1_first:
            copy.wait_recv()
        for copy in weight_arrivals:
            copy.wait_recv()

        table = tab[...]

        def spread(pieces, within, owner):
            count = pieces.shape[0] * SMALL
            item = lax.broadcasted_iota(jnp.int32, (count, 2 * WIDE), 0)
            index = lax.broadcasted_iota(jnp.int32, (LANES, 2 * WIDE), 0)
            chosen = jnp.where(index == within, 1.0, 0.0).astype(low_type)
            pieces = pieces.astype(wide).reshape(count, LANES).astype(low_type)
            found = jnp.dot(pieces, chosen, preferred_element_type=wide)
            found = jnp.where((item >> 4) == owner, found, 0.0)
            return jnp.sum(found.reshape(count // SMALL, SMALL, 2 * WIDE), axis=0)

        every = spread(
            view[:, :, :, :SMALL, 2 * WIDE :].reshape(32, SMALL, LANES), table[0:1], table[1:2]
        )
        w_me = me.x * 2 + me.y
        inner_bias = spread(
            view[w_me, :, :, :SMALL, 2 * WIDE :].reshape(8, SMALL, LANES), table[2:3], table[3:4]
        )
        rows16 = lax.broadcasted_iota(jnp.int32, (SMALL, 2 * WIDE), 0)
        vec[...] = jnp.where(rows16 == 8, inner_bias, every)
        turned = pltpu.roll(every, 2 * WIDE - me.g * LOCAL * HEAD, 1)
        lower = lax.broadcasted_iota(jnp.int32, (1, LANES), 1) < HEAD
        biases = [[], []]
        for h in range(LOCAL):
            pair = slice(h // 2 * LANES, h // 2 * LANES + LANES)
            q, v = turned[0:1, pair], turned[1:2, pair]
            if h % 2:
                q = pltpu.roll(q, HEAD, 1)
            else:
                v = pltpu.roll(v, HEAD, 1)
            biases[0].append(jnp.where(lower, 0.0, v))
            biases[1].append(jnp.where(lower, q, 0.0))
        bias = jnp.concatenate(biases[0] + biases[1], axis=1)

        matrix = weights[:, :, :, :, : 2 * WIDE].reshape(depth, 2 * WIDE)
        kept, kv_first = [copies.keep(weights, wqkv_out), copies.keep(vec, vec_out)], []
        for dv in range(2):
            v = (me.half + dv) % 2
            for u in range(2):
                tokens_go.arrived(u * 2 + v, toks.at[u * 2 + v])
            if dv:
                block = w1.at[:, me.c, me.g, :]
                w1_second = [copies.push(block, block, me.at(g=to)) for to in line]
            both = jnp.concatenate([toks[v], toks[2 + v]], axis=0)
            made = jnp.dot(both, matrix, preferred_element_type=wide)
            made = (made + bias).astype(low_type)
            for u in range(2):
                kv_own[v, u] = made[u * n : (u + 1) * n, :WIDE]
                q_own[u * 2 + v] = made[u * n : (u + 1) * n, WIDE:]
            mine = kv_all.at[:, me.c, v, me.p, me.y]
            kv_first.append(
                [copies.push(kv_own.at[v], mine, me.at(x=x, y=y)) for x, y in square]
            )
            arrivals.append(copies.push(kv_own.at[v], mine, me.sibling()))
            kept.append(copies.keep(kv_own.at[v], mine))
        block = w1.at[:, me.c, me.g, :]
        arrivals.append(copies.push(block, block, me.sibling()))
        kept += [copies.keep(toks, tok_out), copies.keep(q_own, q_out)]
        for dv in range(2):
            v = (me.half + dv) % 2
            for copy, (x, y) in zip(kv_first[dv], square):
                copy.wait_recv()
                block = kv_all.at[:, me.c, v, (x + me.c) % 2, y]
                arrivals.append(copies.push(block, block, me.sibling()))
        for copy, (x, y) in zip(wm_second, square):
            copy.wait_recv()
            block = wm.at[x, me.c, :, y]
            arrivals.append(copies.push(block, block, me.sibling()))
        for copy, (_, source) in zip(w1_second, me.line()):
            copy.wait_recv()
            block = w1.at[:, me.c, source, :]
            arrivals.append(copies.push(block, block, me.sibling()))
        for copy in arrivals:
            copy.wait_recv()
        for copy in kept:
            copy.wait()
        tokens_go.finish()
        copies.finish()

    vmem = pltpu.VMEM
    dma = pltpu.SemaphoreType.DMA
    total = 64
    return pl.pallas_call(
        body,
        name="first_kernel",
        out_shape=(
            jax.ShapeDtypeStruct((GROUPS, n, depth), low_type),
            jax.ShapeDtypeStruct((GROUPS, n, WIDE), low_type),
            jax.ShapeDtypeStruct((4, GROUPS, 2, s, cols), low_type),
            jax.ShapeDtypeStruct((SMALL, 2 * WIDE), wide),
            jax.ShapeDtypeStruct((2, 2, 2, 2, 2, n, WIDE), low_type),
            jax.ShapeDtypeStruct((2, 2, GROUPS, 2, s, quarter), low_type),
            jax.ShapeDtypeStruct((2, 2, GROUPS, 2, s, depth), low_type),
        ),
        in_specs=[pl.BlockSpec(memory_space=pltpu.HBM)] * (7 + count),
        out_specs=(pl.BlockSpec(memory_space=pl.ANY),) * 7,
        scratch_shapes=[
            dma((total,)), dma((total,)), dma((12,)), dma((4,)), dma((4,)),
            vmem((GROUPS, s, cols), low_type),
            vmem((GROUPS, n, depth), low_type),
            vmem((4, GROUPS, 2, s, cols), low_type),
            vmem((2, 2, n, WIDE), low_type),
            vmem((GROUPS, n, WIDE), low_type),
            vmem((4, s, quarter), low_type),
            vmem((s, depth), low_type),
            vmem((SMALL, 2 * WIDE), wide),
            vmem((s, LANES), wide),
            dma((6 + count,)),
            *[vmem(item.shape, item.dtype) for item in (wq, wk, wv, tables, *vectors, inner, mix)],
        ],
        compiler_params=pltpu.CompilerParams(
            collective_id=10, has_side_effects=True, vmem_limit_bytes=NEAR_LIMIT
        ),
    )(*[pltpu.with_memory_space_constraint(item, pltpu.HBM) for item in (tokens, wq, wk, wv, tables, *vectors, inner, mix)])


def pass_back(ident, pieces):
    def body(source, target, send, recv):
        me = Spot()
        owners = me.owners()
        readers = [device for _, device in me.readers()]
        barrier, expected = announce(readers[1:], [(jnp.logical_not(me.selfish), readers[0])])
        pl.semaphore_wait(barrier, expected)
        move = Scatter(send, recv, me.selfish)
        move.start([(source.at[slot], device) for slot, device in owners], target.at[me.g], me.g)
        for g in range(GROUPS):
            move.arrived(g, target.at[g])
        move.finish()

    return scatter_call(body, "pass_back", ident, pieces)


def pass_on(ident, pieces):
    def body(source, target, send, recv):
        me = Spot()
        owners = [device for _, device in me.owners()]
        barrier, expected = announce(owners[1:], [(jnp.logical_not(me.selfish), owners[0])])
        pl.semaphore_wait(barrier, expected)
        move = Scatter(send, recv, me.selfish)
        slot = me.slot()
        move.start([(source.at[g], device) for g, device in me.readers()], target.at[slot], slot)
        for index in range(GROUPS):
            move.arrived(index, target.at[index])
        move.finish()

    return scatter_call(body, "pass_on", ident, pieces)


def scatter_call(body, name, ident, pieces):
    return pl.pallas_call(
        body,
        name=name,
        out_shape=jax.ShapeDtypeStruct(pieces.shape, pieces.dtype),
        in_specs=[pl.BlockSpec(memory_space=pl.ANY)],
        out_specs=pl.BlockSpec(memory_space=pl.ANY),
        scratch_shapes=[pltpu.SemaphoreType.DMA((4,)), pltpu.SemaphoreType.DMA((4,))],
        compiler_params=pltpu.CompilerParams(
            collective_id=ident, has_side_effects=True, vmem_limit_bytes=VMEM_LIMIT
        ),
    )(pieces)


def final_kernel(hidden, pieces, outqk, out1, out2, outm, s, e):
    n, depth = hidden.shape
    quarter = out1.shape[-1]

    def body(hid, dx, qk_in, i_in, o_in, m_in, xg, qw, qb, kw, vw, vb, mw, mb, eg, es, iw, ib, ow, ob, fg, fs):
        device = lax.axis_index("au") * lax.axis_size("row") + lax.axis_index("row")
        xg[...] = total_of(hid[...], dx[0], dx[1], dx[2], dx[3]).astype(low_type)
        rows = qk_in.shape[1]
        q_in, k_in = qk_in.at[:, :, WIDE:], qk_in.at[:, :, :WIDE]
        lower = lax.broadcasted_iota(jnp.int32, (rows, LANES), 1) < HEAD

        def part(head):
            g, h = head // LOCAL, head % LOCAL
            return k_in[g, :, h * LANES : (h + 1) * LANES].astype(wide)

        made_q = []
        for g in range(0, GROUPS, 2):
            a0, b0 = q_in[g, :, :LANES].astype(wide), q_in[g, :, LANES:].astype(wide)
            a1 = pltpu.roll(q_in[g + 1, :, :LANES].astype(wide), HEAD, 1)
            b1 = pltpu.roll(q_in[g + 1, :, LANES:].astype(wide), HEAD, 1)
            made_q += [a0, jnp.where(lower, b0, a1), jnp.where(lower, a1, b1)]
        biases = [[], []]
        for pair in range(HEADS // 2):
            span = slice(pair * LANES, (pair + 1) * LANES)
            kv = [part(2 * pair), part(2 * pair + 1)]
            made_k = jnp.where(lower, kv[0], pltpu.roll(kv[1], HEAD, 1))
            made_v = jnp.where(lower, pltpu.roll(kv[0], HEAD, 1), kv[1])
            qw[:, span], kw[:, span], vw[:, span] = made_q[pair][:s], made_k[:s], made_v[:s]
            biases[0].append(made_q[pair][s:])
            biases[1].append(made_v[s:])

        def own(eight, width, shift):
            return pltpu.roll(eight, shift, 1)[0:1, :width]

        turn = (depth - device * s) % depth
        qb[...] = own(jnp.concatenate(biases[0], axis=1), s, turn)
        vb[...] = own(jnp.concatenate(biases[1], axis=1), s, turn)
        mw[...] = m_in[:s]
        extras = pltpu.roll(m_in[s : s + 8, :], turn, 1)
        for index, ref in enumerate((mb, eg, es, ob, fg, fs)):
            ref[...] = extras[index : index + 1, :s]
        for w in range(4):
            iw[:, w * quarter : (w + 1) * quarter] = i_in[w, :s].astype(wide)
        place = lax.axis_index("row") * e
        ib[...] = own(
            i_in[lax.axis_index("au"), s : s + 8, :].astype(wide), e, (quarter - place) % quarter
        )
        ow[...] = o_in[...]

    vmem = pltpu.VMEM

    def shape(*dims):
        return jax.ShapeDtypeStruct(dims, wide)

    return pl.pallas_call(
        body,
        name="final_kernel",
        out_shape=(
            jax.ShapeDtypeStruct((n, depth), low_type),
            shape(s, depth), shape(1, s), shape(s, depth), shape(s, depth), shape(1, s),
            shape(s, depth), shape(1, s), shape(1, s), shape(1, s),
            shape(s, 4 * quarter), shape(1, e), shape(e, depth),
            shape(1, s), shape(1, s), shape(1, s),
        ),
        in_specs=[pl.BlockSpec(memory_space=vmem)] * 6,
        out_specs=(pl.BlockSpec(memory_space=vmem),) * 16,
        compiler_params=pltpu.CompilerParams(vmem_limit_bytes=NEAR_LIMIT),
    )(hidden, pieces, outqk, out1, out2, outm)


def gelu_and_slope(value):
    t = 1.0 / (1.0 + (0.3275911 * 0.7071067811865476) * jnp.abs(value))
    bell = jnp.exp(-0.5 * value * value)
    tail = 1.061405429
    for weight in (-1.453152027, 1.421413741, -0.284496736, 0.254829592):
        tail = tail * t + weight
    tail = 0.5 * tail * t * bell
    below = jnp.where(value >= 0.0, 1.0 - tail, tail)
    return value * below, below + value * bell * 0.3989422804014327


def normed(hidden):
    mean = jnp.mean(hidden, axis=-1, keepdims=True)
    centered = hidden - mean
    spread = jnp.mean(centered * centered, axis=-1, keepdims=True)
    inverse = lax.rsqrt(spread + eps_norm)
    return centered * inverse, inverse


def normed_grad(grad, norm, inverse):
    mean = jnp.mean(grad, axis=-1, keepdims=True)
    along = jnp.mean(grad * norm, axis=-1, keepdims=True)
    return inverse * (grad - mean - norm * along)


def down_sum(values):
    return jnp.sum(values, axis=0, keepdims=True)


def middle_kernel(mixed, tokens, cotangent, mix, inner, outer, vec, s, e):
    n, depth = tokens.shape
    quarter = inner.shape[1]
    rows = s + 8
    cut = depth // 2
    hn = n // 2

    def body(
        mixed_ref, tok, cot, wm_in, w1_in, w2f, vec_ref,
        out, hidden_out, do_out, sm, s1, s2,
        send, recv, local, back_send, back_recv, on_send, on_recv,
        swap_send2, swap_recv2, wm, w1, w2p, w2s, came, mixed_tok, xs, acts, slopes, parts, sums, bgs, igs, parts2, sums2,
        pieces, extra, attn, own1, own2, g1, g2, gm,
    ):
        me = Spot()
        copies = Copies(send, recv, local)
        square = me.square()
        line = [to for to, _ in me.line()]
        owners = me.owners()
        readers = me.readers()
        swapped = [me.at(g=to, c=me.y, y=me.c) for to in [me.g] + line]
        barrier, expected = announce(
            [me.at(x=x, y=y) for x, y in square]
            + swapped[1:]
            + [device for _, device in readers[1:]]
            + [device for _, device in owners[1:]]
            + [me.sibling()],
            [
                (jnp.logical_not(me.selfish), readers[0][1]),
                (jnp.logical_not(me.selfish), owners[0][1]),
                (me.crossing, swapped[0]),
            ],
        )
        loads = [copies.keep(wm_in, wm), copies.keep(w1_in, w1)]
        w2s[...] = w2f[...].astype(low_type)
        pl.semaphore_wait(barrier, expected)

        back = Scatter(back_send, back_recv, me.selfish)
        back.start([(mixed_ref.at[slot], device) for slot, device in owners], came.at[me.g], me.g)
        lower = lax.broadcasted_iota(jnp.int32, (n, LANES), 1) < HEAD
        loads[0].wait()
        for g in range(GROUPS):
            back.arrived(g, came.at[g])
        w2_place = w2p.at[me.g, me.y]
        w2_first = [copies.push(w2s, w2_place, device) for device in swapped[1:]]
        w2_swap = pltpu.make_async_remote_copy(
            src_ref=w2s,
            dst_ref=w2_place,
            send_sem=swap_send2,
            recv_sem=swap_recv2,
            device_id=swapped[0],
            device_id_type=MESH,
        )
        w2_stays = pltpu.make_async_copy(w2s, w2_place, swap_recv2)

        @pl.when(me.crossing)
        def _():
            w2_swap.start()

        @pl.when(jnp.logical_not(me.crossing))
        def _():
            w2_stays.start()

        for half in range(2):
            a0 = came[2 * half, :, :LANES]
            b0 = came[2 * half, :, LANES:].astype(wide)
            a1 = pltpu.roll(came[2 * half + 1, :, :LANES].astype(wide), HEAD, 1)
            b1 = pltpu.roll(came[2 * half + 1, :, LANES:].astype(wide), HEAD, 1)
            base = half * 3 * LANES
            mixed_tok[:, base : base + LANES] = a0
            mixed_tok[:, base + LANES : base + 2 * LANES] = jnp.where(lower, b0, a1).astype(low_type)
            mixed_tok[:, base + 2 * LANES : base + 3 * LANES] = jnp.where(lower, a1, b1).astype(
                low_type
            )

        def vector(index):
            return vec_ref[index : index + 1, :]

        mix = jnp.dot(mixed_tok[...], wm[...], preferred_element_type=wide) + vector(2)
        norm1, inverse1 = normed(tok[...].astype(wide) + mix)
        early = norm1 * vector(3) + vector(4)
        mine = me.x * 2 + me.y
        halves = [slice(0, hn), slice(hn, n)]

        def send_rows(ref, h):
            place = ref.at[h, mine]
            return [copies.push(place, place, me.at(x=x, y=y)) for x, y in square]

        def send_back(ref, landing, h):
            return [
                copies.push(ref.at[h, x * 2 + y], landing.at[h, mine], me.at(x=x, y=y))
                for x, y in square
            ]

        def arrive(started):
            for copy in started:
                copy.wait_recv()

        def received(landing, h):
            return [landing[h, x * 2 + y] for x, y in square]

        early_go = []
        for h, half in enumerate(halves):
            xs[h, mine] = early[half].astype(low_type)
            early_go.append(send_rows(xs, h))
        loads[1].wait()

        def outer_weight():
            return w2p[...].reshape(quarter, depth)

        branch_go = []
        for h in range(2):
            arrive(early_go[h])
            inner = jnp.dot(
                xs[h].reshape(4 * hn, depth), w1[...], preferred_element_type=wide
            ) + vector(8)
            act, slope = gelu_and_slope(inner)
            act = act.astype(low_type)
            acts[h] = act.reshape(4, hn, quarter)
            slopes[h] = slope
            if h == 0:

                @pl.when(me.crossing)
                def _():
                    w2_swap.wait_recv()
                    w2_swap.wait_send()

                @pl.when(jnp.logical_not(me.crossing))
                def _():
                    w2_stays.wait()

                block = w2p.at[me.g, me.c]
                w2_last = [copies.push(block, block, me.sibling())]
                for copy, (_, source) in zip(w2_first, me.line()):
                    copy.wait_recv()
                    block = w2p.at[source, me.c]
                    w2_last.append(copies.push(block, block, me.sibling()))
                arrive(w2_last)
            made = jnp.dot(act, outer_weight(), preferred_element_type=wide).reshape(4, hn, depth)
            own1[h] = made
            parts[h] = made.astype(low_type)
            branch_go.append(send_back(parts, sums, h))

        grad_go, final_grads, norm_sums, cot_sums = [], [], [], []
        for h, half in enumerate(halves):
            arrive(branch_go[h])
            branch = total_of(own1[h, mine], *received(sums, h)) + vector(5)
            norm2, inverse2 = normed(early[half] + branch)
            out[half, :] = (norm2 * vector(6) + vector(7)).astype(low_type)
            cot_wide = cot[half, :].astype(wide)
            final_grad = normed_grad(cot_wide * vector(6), norm2, inverse2)
            bgs[h, mine] = final_grad.astype(low_type)
            grad_go.append(send_rows(bgs, h))
            final_grads.append(final_grad)
            norm_sums.append(down_sum(cot_wide * norm2))
            cot_sums.append(down_sum(cot_wide))
        extra[...] = jnp.zeros_like(extra)
        extra[3:4, :] = down_sum(bgs[0, mine].astype(wide)) + down_sum(bgs[1, mine].astype(wide))
        extra[4:5, :] = norm_sums[0] + norm_sums[1]
        extra[5:6, :] = cot_sums[0] + cot_sums[1]

        token_go = []
        for h in range(2):
            arrive(grad_go[h])
            grad = lax.dot_general(
                bgs[h].reshape(4 * hn, depth), outer_weight(), NEXT, preferred_element_type=wide
            )
            grad = (grad * slopes[h]).astype(low_type)
            igs[h] = grad.reshape(4, hn, quarter)
            made = lax.dot_general(grad, w1[...], NEXT, preferred_element_type=wide)
            made = made.reshape(4, hn, depth)
            own2[h] = made
            parts2[h] = made.astype(low_type)
            token_go.append(send_back(parts2, sums2, h))

        other = 1 - me.c
        grads = bgs[...].reshape(4 * n, depth)
        for half in range(2):
            span = slice(half * cut, (half + 1) * cut)
            made = lax.dot_general(
                acts[:, :, :, span].reshape(4 * n, cut), grads, DOWN, preferred_element_type=wide
            )
            g2[2 * half : 2 * half + 2] = made.astype(low_type).reshape(2, 2, e, depth)
        w2_half = copies.push(g2.at[:, other], s2, me.sibling())

        grads = igs[...].reshape(4 * n, quarter)
        bias = jnp.broadcast_to(down_sum(grads.astype(wide)), (8, quarter)).astype(low_type)
        for half in range(2):
            span = slice(half * cut, (half + 1) * cut)
            made = lax.dot_general(
                xs[:, :, :, span].reshape(4 * n, cut), grads, DOWN, preferred_element_type=wide
            ).astype(low_type)
            for index in range(16):
                place = (half, index // 8, index // 2 % GROUPS, index % 2)
                g1[(*place, slice(None, s))] = made[index * s : (index + 1) * s]
                g1[(*place, slice(s, None))] = bias
        w1_half = copies.push(g1.at[:, other], s1, me.sibling())
        w2_half.wait_recv()

        def add2(g):
            s2[g] = s2[g] + g2[g, me.c]

        loop(GROUPS, add2)
        w1_half.wait_recv()

        def add1(index):
            x, g, y = index // 8, index // 2 % GROUPS, index % 2
            s1[x, g, y] = s1[x, g, y] + g1[x, me.c, g, y]

        loop(16, add1)
        norm_sums, grad_sums, attn_sums = [], [], []
        for h, half in enumerate(halves):
            arrive(token_go[h])
            early_grad = total_of(final_grads[h], own2[h, mine], *received(sums2, h))
            norm_sums.append(down_sum(early_grad * norm1[half]))
            grad_sums.append(down_sum(early_grad))
            hidden = normed_grad(early_grad * vector(3), norm1[half], inverse1[half])
            hidden_out[half, :] = hidden
            attn[half, :] = hidden.astype(low_type)
            attn_sums.append(down_sum(hidden.astype(low_type).astype(wide)))
        extra[0:1, :] = attn_sums[0] + attn_sums[1]
        extra[1:2, :] = norm_sums[0] + norm_sums[1]
        extra[2:3, :] = grad_sums[0] + grad_sums[1]
        attn_grad = attn[...]
        back_grad = lax.dot_general(attn_grad, wm[...], NEXT, preferred_element_type=wide)
        for half in range(2):
            base = half * 3 * LANES
            t0 = back_grad[:, base : base + LANES]
            t1 = back_grad[:, base + LANES : base + 2 * LANES]
            t2 = back_grad[:, base + 2 * LANES : base + 3 * LANES]
            r1, r2 = pltpu.roll(t1, HEAD, 1), pltpu.roll(t2, HEAD, 1)
            pieces[2 * half, :, :LANES] = t0.astype(low_type)
            pieces[2 * half, :, LANES:] = jnp.where(lower, t1, 0.0).astype(low_type)
            pieces[2 * half + 1, :, :LANES] = jnp.where(lower, r1, r2).astype(low_type)
            pieces[2 * half + 1, :, LANES:] = jnp.where(lower, r2, 0.0).astype(low_type)
        onward = Scatter(on_send, on_recv, me.selfish)
        slot = me.slot()
        onward.start([(pieces.at[g], device) for g, device in readers], do_out.at[slot], slot)

        for half in range(2):
            span = slice(half * cut, (half + 1) * cut)
            made = lax.dot_general(
                mixed_tok[:, span], attn_grad, DOWN, preferred_element_type=wide
            ).astype(low_type)
            for index in range(16):
                place = (half, index // 8, index // 2 % GROUPS, index % 2)
                gm[(*place, slice(None, s))] = made[index * s : (index + 1) * s]
                gm[(*place, slice(s, None))] = extra[...].astype(low_type)
        wm_half = copies.push(gm.at[:, other], sm, me.sibling())
        wm_half.wait_recv()

        def addm(index):
            x, g, y = index // 8, index // 2 % GROUPS, index % 2
            sm[x, g, y] = sm[x, g, y] + gm[x, me.c, g, y]

        loop(16, addm)
        for index in range(GROUPS):
            onward.arrived(index, do_out.at[index])
        back.finish()
        onward.finish()
        copies.finish()

    vmem = pltpu.VMEM
    dma = pltpu.SemaphoreType.DMA
    tall = vmem((2, 4, hn, depth), low_type)
    full = vmem((2, 4, hn, depth), wide)
    high = vmem((2, 4, hn, quarter), low_type)
    space = [vmem] * 3 + [pl.ANY] * 2 + [vmem] * 2
    return pl.pallas_call(
        body,
        name="middle_kernel",
        out_shape=(
            jax.ShapeDtypeStruct((n, depth), low_type),
            jax.ShapeDtypeStruct((n, depth), wide),
            jax.ShapeDtypeStruct((GROUPS, n, PACK), low_type),
            jax.ShapeDtypeStruct((2, GROUPS, 2, rows, depth), low_type),
            jax.ShapeDtypeStruct((2, GROUPS, 2, rows, quarter), low_type),
            jax.ShapeDtypeStruct((GROUPS, e, depth), low_type),
        ),
        in_specs=[pl.BlockSpec(memory_space=item) for item in space],
        out_specs=[
            pl.BlockSpec(memory_space=item) for item in (vmem, vmem, pl.ANY, vmem, vmem, vmem)
        ],
        scratch_shapes=[
            dma((48,)), dma((48,)), dma((8,)), dma((4,)), dma((4,)), dma((4,)), dma((4,)), dma, dma,
            vmem((depth, depth), low_type),
            vmem((depth, quarter), low_type),
            vmem((GROUPS, 2, e, depth), low_type),
            vmem((e, depth), low_type),
            vmem((GROUPS, n, PACK), low_type),
            vmem((n, depth), low_type),
            tall, high,
            vmem((2, 4 * hn, quarter), wide),
            tall, tall, tall, high, tall, tall,
            vmem((GROUPS, n, PACK), low_type),
            vmem((8, depth), wide),
            vmem((n, depth), low_type),
            full, full,
            vmem((2, 2, GROUPS, 2, rows, quarter), low_type),
            vmem((GROUPS, 2, e, depth), low_type),
            vmem((2, 2, GROUPS, 2, rows, depth), low_type),
        ],
        compiler_params=pltpu.CompilerParams(
            collective_id=12, has_side_effects=True, vmem_limit_bytes=NEAR_LIMIT
        ),
    )(mixed, tokens, cotangent, mix, inner, outer, vec)


def tile_base(me, slot, n):
    u, v = slot // 2, slot % 2
    return ((u * 2 + me.c) * 2 * GROUPS + (v * 2 + me.p) * 2 + me.y) * n


def ends_of(lengths_ref):
    ends = [lengths_ref[0]]
    for index in range(1, lengths_ref.shape[0]):
        ends.append(ends[-1] + lengths_ref[index])
    return ends


def document_of(place, ends):
    first, last = place * 0, place * 0 + ends[-1]
    for end in ends[:-1]:
        before = end <= place
        first = jnp.where(before, end, first)
    for end in reversed(ends[:-1]):
        last = jnp.where(end <= place, last, end)
    return first, last


def blocks_of(base, ends, n, block):
    low, _ = document_of(base, ends)
    _, high = document_of(base + n - 1, ends)
    return low // block, (high + block - 1) // block


def near_forward(lengths, queries, keys, n, block):
    total_rows = queries.shape[0]
    tokens = keys.shape[0]
    chunks = [slice(index * LANES, (index + 1) * LANES) for index in range(block // LANES)]

    def body(lengths_ref, q_ref, kv_ref, out_ref, keep_ref, lse_ref, table):
        me = Spot()
        ends = ends_of(lengths_ref)
        lane = lax.broadcasted_iota(jnp.int32, (n, LANES), 1)
        upper = lane >= HEAD
        column = lax.broadcasted_iota(jnp.int32, (n, LANES), 0)

        def one(slot, unused):
            rows = pl.ds(pl.multiple_of(slot * n, n), n)
            base = tile_base(me, slot, n)
            low, high = blocks_of(base, ends, n, block)
            first, last = document_of(column + base, ends)
            heads = [
                q_ref[rows, h * LANES : (h + 1) * LANES] * jnp.asarray(0.125, low_type)
                for h in range(LOCAL)
            ]

            def score(j, tops):
                begin = pl.multiple_of(j * block, block)
                same = []
                for chunk in chunks:
                    place = lane + (begin + chunk.start)
                    same.append((place >= first) & (place < last))
                result = []
                for h in range(LOCAL):
                    kv = kv_ref[pl.ds(begin, block), h * LANES : (h + 1) * LANES]
                    scores = lax.dot_general(heads[h], kv, NEXT, preferred_element_type=wide)
                    top = tops[h]
                    for chunk, mask in zip(chunks, same):
                        part = jnp.where(mask, scores[:, chunk], mask_fill)
                        table[h, j, :, chunk] = part
                        top = jnp.maximum(top, part)
                    result.append(top)
                return tuple(result)

            tops = lax.fori_loop(
                low, high, score, (jnp.full((n, LANES), lowest_start, wide),) * LOCAL
            )
            tops = [jnp.max(top, axis=1, keepdims=True) for top in tops]
            spread = [jnp.broadcast_to(top, (n, LANES)) for top in tops]

            def weigh(j, carry):
                begin = pl.multiple_of(j * block, block)
                result = []
                for h in range(LOCAL):
                    total, mixed = carry[h]
                    kv = kv_ref[pl.ds(begin, block), h * LANES : (h + 1) * LANES]
                    parts = []
                    for chunk in chunks:
                        part = jnp.exp(table[h, j, :, chunk] - spread[h])
                        total = total + part
                        parts.append(part.astype(low_type))
                    powers = jnp.concatenate(parts, axis=1)
                    mixed = mixed + jnp.dot(powers, kv, preferred_element_type=wide)
                    result.append((total, mixed))
                return tuple(result)

            zero = jnp.zeros((n, LANES), wide)
            done = lax.fori_loop(low, high, weigh, ((zero, zero),) * LOCAL)
            totals = [jnp.sum(total, axis=1, keepdims=True) for total, _ in done]
            mixes = [mixed / total for total, (_, mixed) in zip(totals, done)]
            turned = [pltpu.roll(mixed, HEAD, 1) for mixed in mixes]
            front = jnp.where(upper, mixes[1], turned[0])
            back = jnp.where(upper, 0.0, turned[2])
            both = jnp.concatenate([front, back], axis=1)
            keep_ref[rows, :] = both
            out_ref[rows, :] = both.astype(low_type)
            logs = [top + jnp.log(total) for top, total in zip(tops, totals)]
            logs = jnp.where(lane == 0, logs[0], jnp.where(lane == 1, logs[1], logs[2]))
            lse_ref[slot] = jnp.transpose(logs)[:8]
            return unused

        lax.fori_loop(0, GROUPS, one, 0)

    vmem = pl.BlockSpec(memory_space=pltpu.VMEM)
    return pl.pallas_call(
        body,
        name="near_forward",
        out_shape=(
            jax.ShapeDtypeStruct((total_rows, PACK), low_type),
            jax.ShapeDtypeStruct((total_rows, PACK), wide),
            jax.ShapeDtypeStruct((GROUPS, 8, n), wide),
        ),
        in_specs=[pl.BlockSpec(memory_space=pltpu.SMEM)] + [vmem] * 2,
        out_specs=(vmem,) * 3,
        scratch_shapes=[pltpu.VMEM((LOCAL, tokens // block, n, block), wide)],
        compiler_params=pltpu.CompilerParams(vmem_limit_bytes=NEAR_LIMIT),
    )(lengths, queries, keys)


def turn_kernel(lengths, queries, keys, grads_in, mixed, lse, tokens, weights, sum1, sum2, summ):
    n = tokens.shape[1]
    depth = tokens.shape[-1]
    s = depth // 32
    rows = s + 8
    cut = depth // 2
    tall = sum2.shape[1]
    block = GROUPS * n
    width = WIDE + PACK
    spans = [slice(h * LANES, (h + 1) * LANES) for h in range(LOCAL)]

    def body(
        lengths_ref, q_ref, kv_ref, do_ref, mixed_ref, lse_ref, tok, w_ref, s1, s2, sm,
        dx_out, outqk, out1, out2, outm,
        send, recv, local, dx_send, dx_recv, swap_send, swap_recv, ks, kr, ps, pr,
        both, kbuf, kin, pk, dqs, grads, narrow, dxs, gk, sk, pp, fk, p1, f1, pm, fm, tm, p2,
    ):
        me = Spot()
        copies = Copies(send, recv, local)
        square = me.square()
        line = [to for to, _ in me.line()]
        readers = [device for _, device in me.readers()]
        swapped = [me.at(g=to, c=me.y, y=me.c) for to in [me.g] + line]
        barrier, expected = announce(
            [me.at(x=x, y=y) for x, y in square]
            + [me.at(g=to) for to in line]
            + readers[1:]
            + swapped[1:]
            + [me.sibling()],
            [(jnp.logical_not(me.selfish), readers[0]), (me.crossing, swapped[0])],
        )
        ends = ends_of(lengths_ref)
        lane = lax.broadcasted_iota(jnp.int32, (n, LANES), 1)
        upper = lane >= HEAD
        along = lax.broadcasted_iota(jnp.int32, (1, n), 1)
        down = lax.broadcasted_iota(jnp.int32, (block, n), 0)

        def upper_halves(ref, part):
            front = ref[part, :LANES].astype(wide)
            back = ref[part, LANES:].astype(wide)
            parts = (pltpu.roll(front, HEAD, 1), front, pltpu.roll(back, HEAD, 1))
            return [jnp.where(upper, item, 0.0) for item in parts]

        firsts, lasts, logs, deltas = [], [], [], []
        for slot in range(GROUPS):
            part = slice(slot * n, (slot + 1) * n)
            first, last = document_of(along + tile_base(me, slot, n), ends)
            firsts.append(first)
            lasts.append(last)
            outs, inputs = upper_halves(mixed_ref, part), upper_halves(do_ref, part)
            for h, span in enumerate(spans):
                base = slot * 2 * n
                both[h, base : base + n] = q_ref[part, span] * jnp.asarray(0.125, low_type)
                both[h, base + n : base + 2 * n] = inputs[h].astype(low_type)
            deltas.append([down_sum(jnp.transpose(i * o)) for i, o in zip(inputs, outs)])
            logs.append([lse_ref[slot, h : h + 1, :] for h in range(LOCAL)])
        dqs[...] = jnp.zeros_like(dqs)
        pl.semaphore_wait(barrier, expected)

        wm_push = [
            copies.push(sm.at[x, :, y], pm.at[peer], me.at(x=x, y=y))
            for peer, (x, y) in enumerate(square)
        ]
        w1_push = [
            copies.push(s1.at[:, to, :], p1.at[slot], me.at(g=to)) for slot, to in enumerate(line)
        ]
        w2_push = [
            copies.push(s2.at[to], p2.at[index + 1], swapped[index + 1])
            for index, to in enumerate(line)
        ]
        exchanged = pltpu.make_async_remote_copy(
            src_ref=s2.at[me.g],
            dst_ref=p2.at[0],
            send_sem=swap_send,
            recv_sem=swap_recv,
            device_id=swapped[0],
            device_id_type=MESH,
        )
        stays = pltpu.make_async_copy(s2.at[me.g], p2.at[0], swap_recv)

        @pl.when(me.crossing)
        def _():
            exchanged.start()

        @pl.when(jnp.logical_not(me.crossing))
        def _():
            stays.start()

        other = 1 - me.c

        def attend(u, c, v, target):
            begin = pl.multiple_of(((u * 2 + c) * 2 + v) * block, block)
            place = down + begin
            same = [(place >= first) & (place < last) for first, last in zip(firsts, lasts)]
            for h, span in enumerate(spans):
                kv = kv_ref[pl.ds(begin, block), span]
                made = lax.dot_general(kv, both[h], NEXT, preferred_element_type=wide)
                pairs = []
                for slot in range(GROUPS):
                    base = slot * 2 * n
                    scores = jnp.where(same[slot], made[:, base : base + n], mask_fill)
                    probs = jnp.exp(scores - logs[slot][h])
                    dots = made[:, base + n : base + 2 * n]
                    score_grad = (probs * (dots - deltas[slot][h])).astype(low_type)
                    pairs += [score_grad, probs.astype(low_type)]
                    dqs[slot, :, span] += lax.dot_general(
                        score_grad, kv, DOWN, preferred_element_type=wide
                    )
                made = jnp.dot(
                    jnp.concatenate(pairs, axis=1), both[h], preferred_element_type=wide
                )
                target[:, :, :, span] = made.astype(low_type).reshape(2, 2, n, LANES)

        def to_sibling(turn):
            return pltpu.make_async_remote_copy(
                src_ref=kbuf.at[0, turn],
                dst_ref=kin.at[turn],
                send_sem=ks.at[turn],
                recv_sem=kr.at[turn],
                device_id=me.sibling(),
                device_id_type=MESH,
            )

        def to_peer(turn, peer):
            x, y = square[peer]
            return pltpu.make_async_remote_copy(
                src_ref=kbuf.at[1, turn, (x + me.c) % 2, y],
                dst_ref=pk.at[turn, peer],
                send_sem=ps.at[turn * 3 + peer],
                recv_sem=pr.at[turn * 3 + peer],
                device_id=me.at(x=x, y=y),
                device_id_type=MESH,
            )

        def key_turn(turn):
            u, v = turn % 2, (me.half + turn // 2) % 2

            def of_core(index):
                attend(u, jnp.where(index == 0, other, me.c), v, kbuf.at[index, turn])

                @pl.when(index == 0)
                def _():
                    to_sibling(turn).start()

            loop(2, of_core)
            to_sibling(turn).wait_recv()
            for p in range(2):
                for y in range(2):
                    kbuf[1, turn, p, y] = kbuf[1, turn, p, y] + kin[turn, p, y]
            for peer in range(3):
                to_peer(turn, peer).start()

        loop(4, key_turn)

        def square_push(total, landing):
            return [
                copies.push(total.at[x, :, y], landing.at[slot], me.at(x=x, y=y))
                for slot, (x, y) in enumerate(square)
            ]

        def square_sum(result, total, landed):
            def add(g):
                result[g] = total_of(
                    total[me.x, g, me.y], landed[0, g], landed[1, g], landed[2, g]
                ).astype(low_type)

            loop(GROUPS, add)

        moves = []
        for turn in range(4):
            u, dv = turn % 2, turn // 2
            v = (me.half + dv) % 2
            slot = u * 2 + v
            wides = [dqs[slot, :, span] * 0.125 for span in spans]
            for h, span in enumerate(spans):
                grads[slot, :, WIDE + span.start : WIDE + span.stop] = jnp.where(
                    upper, 0.0, wides[h]
                ).astype(low_type)
            narrow[slot, :, WIDE : WIDE + LANES] = jnp.where(
                upper, pltpu.roll(wides[1], HEAD, 1), wides[0]
            ).astype(low_type)
            narrow[slot, :, WIDE + LANES :] = jnp.where(upper, 0.0, wides[2]).astype(low_type)
            for peer in range(3):
                to_peer(turn, peer).wait_recv()
            here = total_of(
                kbuf[1, turn, me.p, me.y], *[pk[turn, peer] for peer in range(3)]
            ).astype(low_type)
            grads[slot, :, :WIDE] = here
            narrow[slot, :, :WIDE] = here
            dxs[slot] = lax.dot_general(
                grads[slot], w_ref[:, : 2 * WIDE], NEXT, preferred_element_type=wide
            ).astype(low_type)
            copy = pltpu.make_async_remote_copy(
                src_ref=dxs.at[slot],
                dst_ref=dx_out.at[me.g],
                send_sem=dx_send.at[turn],
                recv_sem=dx_recv.at[me.g],
                device_id=me.at(x=u, g=2 * v + me.p),
                device_id_type=MESH,
            )
            if dv:
                copy.start()
                moves.append((copy, None))
                continue
            stay = pltpu.make_async_copy(dxs.at[slot], dx_out.at[me.g], dx_recv.at[me.g])
            at_home = me.selfish & (me.x == u)
            away = jnp.logical_not(at_home)
            moves.append((copy, away))

            @pl.when(at_home)
            def _(stay=stay):
                stay.start()

            @pl.when(away)
            def _(copy=copy):
                copy.start()

        values = narrow[...].reshape(GROUPS * n, width)
        bias = jnp.broadcast_to(down_sum(values.astype(wide)), (8, width)).astype(low_type)
        for half in range(2):
            made = lax.dot_general(
                tok[:, :, half * cut : (half + 1) * cut].reshape(GROUPS * n, cut),
                values,
                DOWN,
                preferred_element_type=wide,
            ).astype(low_type)
            for index in range(16):
                place = (half, index // 8, index // 2 % GROUPS, index % 2)
                gk[(*place, slice(None, s))] = made[index * s : (index + 1) * s]
                gk[(*place, slice(s, None))] = bias
        g_half = copies.push(gk.at[:, other], sk, me.sibling())

        for copy in wm_push:
            copy.wait_recv()
        square_sum(fm, sm, pm)
        wm_last = [
            copies.push(fm.at[to], tm.at[peer], me.at(g=to)) for peer, to in enumerate(line)
        ]
        for copy in w1_push:
            copy.wait_recv()

        def addw(index):
            x, y = index // 2, index % 2
            f1[x, y] = total_of(s1[x, me.g, y], *[p1[peer, x, y] for peer in range(3)]).astype(
                low_type
            )

        loop(4, addw)
        quarter = out1.at[me.x * 2 + me.y]
        g_half.wait_recv()

        def pair_sum(index):
            x, g, y = index // 8, index // 2 % GROUPS, index % 2
            sk[x, g, y] = sk[x, g, y] + gk[x, me.c, g, y]

        loop(16, pair_sum)
        push = square_push(sk, pp)
        arrivals = [copies.push(f1.at[x, y], quarter, me.at(x=x, y=y)) for x, y in square]
        kept = [copies.keep(f1.at[me.x, me.y], quarter)]

        @pl.when(me.crossing)
        def _():
            exchanged.wait_recv()
            exchanged.wait_send()

        @pl.when(jnp.logical_not(me.crossing))
        def _():
            stays.wait()

        for copy in w2_push:
            copy.wait_recv()
        out2[...] = total_of(*[p2[index] for index in range(4)])
        for copy in push:
            copy.wait_recv()
        square_sum(fk, sk, pp)
        arrivals += [copies.push(fk.at[to], outqk.at[me.g], me.at(g=to)) for to in line]
        kept.append(copies.keep(fk.at[me.g], outqk.at[me.g]))
        for copy in wm_last:
            copy.wait_recv()
        outm[...] = total_of(fm[me.g], *[tm[peer] for peer in range(3)])
        for copy in arrivals:
            copy.wait_recv()
        for g in range(GROUPS):
            pltpu.make_async_copy(dx_out.at[g], dx_out.at[g], dx_recv.at[g]).wait()
        for copy in kept:
            copy.wait()
        for copy, away in moves:
            if away is None:
                copy.wait_send()
                continue

            @pl.when(away)
            def _(copy=copy):
                copy.wait_send()

        for turn in range(4):
            to_sibling(turn).wait_send()
            for peer in range(3):
                to_peer(turn, peer).wait_send()
        copies.finish()

    vmem = pltpu.VMEM
    dma = pltpu.SemaphoreType.DMA
    total = 40
    return pl.pallas_call(
        body,
        name="turn_kernel",
        out_shape=(
            jax.ShapeDtypeStruct((GROUPS, n, depth), low_type),
            jax.ShapeDtypeStruct((GROUPS, rows, width), low_type),
            jax.ShapeDtypeStruct((4, rows, depth), low_type),
            jax.ShapeDtypeStruct((tall, depth), wide),
            jax.ShapeDtypeStruct((rows, depth), wide),
        ),
        in_specs=[pl.BlockSpec(memory_space=pltpu.SMEM)] + [pl.BlockSpec(memory_space=vmem)] * 10,
        out_specs=[pl.BlockSpec(memory_space=pl.ANY)] * 3 + [pl.BlockSpec(memory_space=vmem)] * 2,
        scratch_shapes=[
            dma((total,)), dma((total,)), dma((4,)), dma((4,)), dma((4,)), dma, dma,
            dma((4,)), dma((4,)), dma((12,)), dma((12,)),
            vmem((LOCAL, 2 * block, LANES), low_type),
            vmem((2, 4, 2, 2, n, WIDE), low_type),
            vmem((4, 2, 2, n, WIDE), low_type),
            vmem((4, 3, n, WIDE), low_type),
            vmem((GROUPS, n, WIDE), wide),
            vmem((GROUPS, n, 2 * WIDE), low_type),
            vmem((GROUPS, n, width), low_type),
            vmem((GROUPS, n, depth), low_type),
            vmem((2, 2, GROUPS, 2, rows, width), low_type),
            vmem((2, GROUPS, 2, rows, width), low_type),
            vmem((3, GROUPS, rows, width), low_type),
            vmem((GROUPS, rows, width), low_type),
            vmem((3, 2, 2, rows, depth), low_type),
            vmem((2, 2, rows, depth), low_type),
            vmem((3, GROUPS, rows, depth), low_type),
            vmem((GROUPS, rows, depth), low_type),
            vmem((3, rows, depth), low_type),
            vmem((4, tall, depth), low_type),
        ],
        compiler_params=pltpu.CompilerParams(
            collective_id=11, has_side_effects=True, vmem_limit_bytes=TURN_LIMIT
        ),
    )(lengths, queries, keys, grads_in, mixed, lse, tokens, weights, sum1, sum2, summ)


def on_device_general(
    tokens,
    cotangent,
    doc_lengths,
    query_weight,
    query_bias,
    key_weight,
    value_weight,
    value_bias,
    mix_weight,
    mix_bias,
    early_gain,
    early_shift,
    inner_weight,
    inner_bias,
    outer_weight,
    outer_bias,
    final_gain,
    final_shift,
):
    n, depth = tokens.shape
    groups, cycle = lax.axis_size("au"), lax.axis_size("row")
    devices = groups * cycle
    zs = cycle // (2 * GROUPS)
    s = query_weight.shape[0]
    ff = inner_weight.shape[1]
    quarter = ff // 4
    e = outer_weight.shape[0]
    rows = GROUPS * n
    total_tokens = n * devices
    me = Place(zs)
    device = lax.axis_index("au") * cycle + lax.axis_index("row")
    w_me = me.x * 2 + me.y

    def by_head(weight):
        return weight.astype(low_type).reshape(-1, GROUPS, LOCAL, HEAD)

    def packed(query, key, value):
        kv = jnp.stack([key, value], axis=3).reshape(-1, GROUPS, WIDE)
        q = jnp.pad(query, ((0, 0), (0, 0), (0, 0), (0, HEAD))).reshape(-1, GROUPS, WIDE)
        return jnp.concatenate([kv, q], axis=2)

    slab = packed(by_head(query_weight), by_head(key_weight), by_head(value_weight))
    slab = jnp.transpose(slab, (1, 0, 2))
    small = jnp.concatenate(
        [
            vector.astype(low_type)
            for vector in (
                query_bias, value_bias, mix_bias, early_gain, early_shift,
                outer_bias, final_gain, final_shift, inner_bias,
            )
        ]
    )
    extra = -s % 8 or 8
    small = jnp.broadcast_to(
        jnp.pad(small, (0, 2 * WIDE - small.shape[0]))[None, None], (GROUPS, extra, 2 * WIDE)
    )
    slab = jnp.concatenate([slab, small], axis=1)
    tok_all, w_all = spread_tokens(zs, tokens, slab)
    tok_all = tok_all.reshape(rows, depth)
    w_qkv = w_all[..., :s, :].reshape(depth, 2 * WIDE)
    small = w_all[..., s, :].reshape(devices, 2 * WIDE)
    names = [small[:, i * s : (i + 1) * s].reshape(depth) for i in range(8)]
    q_bias, v_bias, m_bias, e_gain, e_shift, o_bias, f_gain, f_shift = names
    i_bias = small[:, 8 * s : 8 * s + e].reshape(4, quarter)[w_me].astype(wide)
    q_bias = q_bias.reshape(1, GROUPS, LOCAL, HEAD)
    v_bias = v_bias.reshape(1, GROUPS, LOCAL, HEAD)
    bias = packed(q_bias, jnp.zeros_like(q_bias), v_bias)[0, me.g].astype(wide)

    qkv = (jnp.dot(tok_all, w_qkv, preferred_element_type=wide) + bias).astype(low_type)
    queries = qkv[:, WIDE:]

    inner_slab = jnp.transpose(inner_weight.astype(low_type).reshape(s, 4, quarter), (1, 0, 2))
    kv_all, w1, w2, wm = spread_keys(
        zs,
        qkv[:, :WIDE].reshape(GROUPS, n, WIDE),
        inner_slab,
        outer_weight.astype(low_type),
        mix_weight.astype(low_type),
    )
    kv_all = kv_all.reshape(total_tokens, WIDE)
    w1 = w1.reshape(depth, quarter)
    w2 = w2.reshape(quarter, depth)
    wm = wm.reshape(depth, depth)

    tile, block = 128, 512
    count = doc_lengths.shape[0]
    upto = jnp.arange(count)[None, :] <= jnp.arange(count)[:, None]
    ends = jnp.sum(jnp.where(upto, doc_lengths[None, :], 0), axis=1)
    owners = ((me.x * 2 + me.c) * cycle + me.z * GROUPS * 2 + jnp.arange(GROUPS) * 2 + me.y) * n
    places = (owners[:, None] + jnp.arange(n)[None, :]).reshape(rows)
    before = ends[None, :] <= places[:, None]
    first = jnp.max(jnp.where(before, ends[None, :], 0), axis=1).astype(jnp.int32)
    last = jnp.min(jnp.where(before, total_tokens, ends[None, :]), axis=1).astype(jnp.int32)
    tiles = rows // tile
    bounds = jnp.stack(
        [
            first.reshape(tiles, tile)[:, 0] // block,
            (last.reshape(tiles, tile)[:, -1] + block - 1) // block,
        ],
        axis=1,
    )
    mixed, mixed_wide, lse = attend_forward(
        queries, kv_all, bounds, first[:, None], last[:, None], tile, block
    )
    mixed_tok = exchange_line(zs, 2, mixed.reshape(GROUPS, n, PACK))
    mixed_tok = jnp.transpose(mixed_tok[:, :, : LOCAL * HEAD], (1, 0, 2)).reshape(n, depth)

    attn = jnp.dot(mixed_tok, wm, preferred_element_type=wide) + m_bias.astype(wide)
    early, early_pull = jax.vjp(
        layer_norm, tokens.astype(wide) + attn, e_gain.astype(wide), e_shift.astype(wide)
    )
    early_all = gather_square(zs, 3, early.astype(low_type)).reshape(rows, depth)
    inner = jnp.dot(early_all, w1, preferred_element_type=wide) + i_bias
    act, gelu_pull = jax.vjp(gelu_exact, inner)
    act_low = act.astype(low_type)
    partial = jnp.dot(act_low, w2, preferred_element_type=wide).astype(low_type)
    partial = exchange_square(zs, 4, partial.reshape(2, 2, n, depth))
    branch = jnp.sum(partial.astype(wide), axis=(0, 1)) + o_bias.astype(wide)
    result, final_pull = jax.vjp(
        layer_norm, early + branch, f_gain.astype(wide), f_shift.astype(wide)
    )
    output = result.astype(low_type)
    final_grads = final_pull(cotangent.astype(wide))
    branch_grad = final_grads[0].astype(low_type)
    outer_bias_grad = jnp.sum(branch_grad.astype(wide), axis=0)
    branch_all = gather_square(zs, 5, branch_grad).reshape(rows, depth)
    act_grad = jnp.einsum("td,fd->tf", branch_all, w2, preferred_element_type=wide)
    inner_grad = gelu_pull(act_grad)[0].astype(low_type)
    partial = jnp.einsum("tf,df->td", inner_grad, w1, preferred_element_type=wide).astype(low_type)
    partial = exchange_square(zs, 6, partial.reshape(2, 2, n, depth))
    grad2 = jnp.einsum("tf,td->fd", act_low, branch_all, preferred_element_type=wide)
    grad1 = jnp.einsum("td,tf->df", early_all, inner_grad, preferred_element_type=wide)
    inner_bias_grad = jnp.sum(inner_grad.astype(wide), axis=0)
    early_grad = final_grads[0] + jnp.sum(partial.astype(wide), axis=(0, 1))
    early_grads = early_pull(early_grad)
    attn_grad = early_grads[0].astype(low_type)
    mixed_grad = jnp.einsum("td,cd->tc", attn_grad, wm, preferred_element_type=wide)
    mixed_grad = jnp.transpose(
        mixed_grad.astype(low_type).reshape(n, GROUPS, LOCAL * HEAD), (1, 0, 2)
    )
    mixed_grad = jnp.pad(mixed_grad, ((0, 0), (0, 0), (0, PACK - LOCAL * HEAD)))
    grad_all = exchange_line(zs, 7, mixed_grad).reshape(rows, PACK)
    gradm = jnp.einsum("tc,td->cd", mixed_tok, attn_grad, preferred_element_type=wide)
    mix_bias_grad = jnp.sum(attn_grad.astype(wide), axis=0)

    delta = jnp.sum(
        (grad_all.astype(wide) * mixed_wide)[:, : LOCAL * HEAD].reshape(rows, LOCAL, HEAD), axis=2
    )

    def as_stat(values):
        return jnp.transpose(values.reshape(tiles, tile, LOCAL), (0, 2, 1))

    def same_stat(values):
        return jnp.broadcast_to(
            values.astype(wide).reshape(tiles, 1, tile), (tiles, LOCAL, tile)
        )

    stats = jnp.stack(
        [same_stat(first), same_stat(last), as_stat(lse[:, :LOCAL]), as_stat(delta)], axis=2
    )
    stats = jnp.pad(stats, ((0, 0), (0, 0), (0, 4), (0, 0)))
    query_grad, dkv = attend_backward(queries, kv_all, grad_all, stats, bounds, tile, block)

    def slabs(grad, extras):
        grad = grad.astype(low_type).reshape(devices, s, -1)
        rest = -s % 8
        rest += 0 if rest >= extras.shape[0] else 8
        extras = jnp.concatenate(
            [extras.astype(low_type), jnp.zeros((rest - extras.shape[0], extras.shape[1]), low_type)]
        )
        extras = jnp.broadcast_to(extras[None], (devices,) + extras.shape)
        return jnp.concatenate([grad, extras], axis=1).reshape(2, 2, zs, GROUPS, 2, s + rest, -1)

    mix_extras = jnp.stack(
        [
            mix_bias_grad, early_grads[1], early_grads[2],
            outer_bias_grad, final_grads[1], final_grads[2],
        ]
    )
    dkv, out1, out2, outm = reduce_keys(
        zs,
        dkv.reshape(2, 2, zs, GROUPS, 2, n, WIDE),
        slabs(grad1, inner_bias_grad[None]),
        grad2.astype(low_type).reshape(zs, GROUPS, 2, e, depth),
        slabs(gradm, mix_extras),
    )
    key_grad = jnp.sum(dkv.astype(wide), axis=0).astype(low_type).reshape(rows, WIDE)
    grads = jnp.concatenate([key_grad, query_grad], axis=1)
    gradq = jnp.einsum("tc,td->cd", tok_all, grads, preferred_element_type=wide)
    bias_grad = jnp.sum(grads.astype(wide), axis=0)
    partial = jnp.einsum("td,cd->tc", grads, w_qkv, preferred_element_type=wide).astype(low_type)
    partial, outq = reduce_tokens(
        zs, partial.reshape(GROUPS, n, depth), slabs(gradq, bias_grad[None])
    )
    input_grad = early_grads[0] + jnp.sum(partial.astype(wide), axis=0)

    def own(vector, count):
        return lax.dynamic_slice_in_dim(vector, device * count, count, 0).astype(wide)

    outq = outq.astype(wide)
    kv_out = outq[:, :, :WIDE].reshape(GROUPS, -1, LOCAL, 2, HEAD)
    q_out = outq[:, :, WIDE:].reshape(GROUPS, -1, LOCAL, 2, HEAD)[:, :, :, 0]

    def unpacked(values):
        return jnp.transpose(values, (1, 0, 2, 3)).reshape(-1, depth)

    q_out, k_out, v_out = unpacked(q_out), unpacked(kv_out[:, :, :, 0]), unpacked(kv_out[:, :, :, 1])
    inner_out = jnp.transpose(out1[:, :s], (1, 0, 2)).reshape(s, ff).astype(wide)
    return (
        output,
        input_grad.astype(low_type),
        q_out[:s],
        own(q_out[s], s),
        k_out[:s],
        v_out[:s],
        own(v_out[s], s),
        outm[:s],
        own(outm[s], s),
        own(outm[s + 1], s),
        own(outm[s + 2], s),
        inner_out,
        own(out1[:, s].reshape(ff), e),
        out2,
        own(outm[s + 3], s),
        own(outm[s + 4], s),
        own(outm[s + 5], s),
    )


def on_device(
    tokens,
    cotangent,
    doc_lengths,
    query_weight,
    query_bias,
    key_weight,
    value_weight,
    value_bias,
    mix_weight,
    mix_bias,
    early_gain,
    early_shift,
    inner_weight,
    inner_bias,
    outer_weight,
    outer_bias,
    final_gain,
    final_shift,
):
    n, depth = tokens.shape
    cycle = lax.axis_size("row")
    devices = lax.axis_size("au") * cycle
    s = query_weight.shape[0]
    ff = inner_weight.shape[1]
    quarter = ff // 4
    e = outer_weight.shape[0]
    rows = GROUPS * n
    total_tokens = n * devices
    me = Spot()
    vectors = [
        vector.reshape(1, -1)
        for vector in (
            query_bias, value_bias, mix_bias, early_gain, early_shift,
            outer_bias, final_gain, final_shift,
        )
    ]
    vectors.append(inner_bias.reshape(1, -1))
    toks, queries, w_qkv, vec, kv_all, w1, wm = first_kernel(
        tokens, query_weight, key_weight, value_weight, vectors,
        inner_weight, mix_weight, e,
    )
    queries = queries.reshape(rows, WIDE)
    kv_all = kv_all.reshape(total_tokens, WIDE)
    w_qkv = w_qkv.reshape(depth, -1)
    w1 = w1.reshape(depth, quarter)
    wm = wm.reshape(depth, depth)
    mixed, mixed_wide, lse = near_forward(doc_lengths, queries, kv_all, n, 512)
    output, hidden_grad, grad_all, summ, sum1, sum2 = middle_kernel(
        mixed.reshape(GROUPS, n, PACK), tokens, cotangent, wm, w1, outer_weight, vec, s, e
    )
    grad_all = grad_all.reshape(rows, PACK)
    pieces, outqk, out1, out2, outm = turn_kernel(
        doc_lengths, queries, kv_all, grad_all, mixed_wide, lse, toks, w_qkv, sum1, sum2, summ
    )
    results = final_kernel(hidden_grad, pieces, outqk, out1, out2, outm, s, e)
    return (output,) + tuple(
        result.reshape(-1) if result.shape[0] == 1 else result for result in results
    )


def solution(mesh):
    both = P(("au", "row"), None)
    flat = P(("au", "row"))
    in_specs = (
        both, both, P(), both, flat, both, both, flat, both, flat, flat, flat,
        both, flat, both, flat, flat, flat,
    )
    out_specs = (
        both, both, both, flat, both, both, flat, both, flat, flat, flat,
        both, flat, both, flat, flat, flat,
    )
    fast = mesh.shape["au"] == 4 and mesh.shape["row"] == 2 * GROUPS
    return jax.shard_map(
        on_device if fast else on_device_general, mesh=mesh, in_specs=in_specs, out_specs=out_specs, check_vma=False
    )
```

```python
import functools

import jax
import jax.numpy as jnp
import numpy as np
from jax import lax
from jax.experimental import pallas as pl
from jax.experimental.pallas import tpu as pltpu
from jax.sharding import PartitionSpec as P

HEAD = 64
HEADS = 12
GROUPS = 4
LOCAL = HEADS // GROUPS
LANES = 2 * HEAD
WIDE = LOCAL * LANES
PACK = 256
eps_norm = 1e-06
mask_fill = -1000000000.0
lowest_start = -1e30
low_type = jnp.bfloat16
wide = jnp.float32
MESH = pl.DeviceIdType.MESH
VMEM_LIMIT = 62 * 1024 * 1024
NEAR_LIMIT = 30 * 1024 * 1024
TURN_LIMIT = 48 * 1024 * 1024


def layer_norm(hidden, gain, shift):
    mean = jnp.mean(hidden, axis=-1, keepdims=True)
    centered = hidden - mean
    spread = jnp.mean(centered * centered, axis=-1, keepdims=True)
    return centered * lax.rsqrt(spread + eps_norm) * gain + shift


def gelu_exact(values):
    return jax.nn.gelu(values, approximate=False)


class Place:
    def __init__(self, zs):
        self.zs = zs
        a = lax.axis_index("au")
        r = lax.axis_index("row")
        self.x, self.c = a // 2, a % 2
        self.y, q = r % 2, r // 2
        self.g, self.z = q % GROUPS, q // GROUPS

    def at(self, x=None, c=None, z=None, g=None, y=None):
        x = self.x if x is None else x
        c = self.c if c is None else c
        z = self.z if z is None else z
        g = self.g if g is None else g
        y = self.y if y is None else y
        return (x * 2 + c, (z * GROUPS + g) * 2 + y)

    def sibling(self):
        return self.at(c=1 - self.c)

    def line(self):
        return [((self.g + k) % GROUPS, (self.g + GROUPS - k) % GROUPS) for k in range(1, GROUPS)]

    def column(self):
        count = self.zs * GROUPS
        q = self.z * GROUPS + self.g
        result = []
        for k in range(1, count):
            to, source = (q + k) % count, (q + count - k) % count
            result.append(((to // GROUPS, to % GROUPS), (source // GROUPS, source % GROUPS)))
        return result

    def plane(self, everywhere=True):
        result = []
        for dx in range(2):
            for dy in range(2):
                for dz in range(self.zs if everywhere else 1):
                    if dx + dy + dz == 0:
                        continue
                    to = ((self.x + dx) % 2, (self.z + dz) % self.zs, (self.y + dy) % 2)
                    source = (
                        (self.x + dx) % 2,
                        (self.z + self.zs - dz) % self.zs,
                        (self.y + dy) % 2,
                    )
                    result.append((to, source))
        return result


class Copies:
    def __init__(self, send, recv, local):
        self.send, self.recv, self.local = send, recv, local
        self.count = 0
        self.local_count = 0
        self.started = []
        self.local_started = []

    def push(self, source, target, device):
        copy = pltpu.make_async_remote_copy(
            src_ref=source,
            dst_ref=target,
            send_sem=self.send.at[self.count],
            recv_sem=self.recv.at[self.count],
            device_id=device,
            device_id_type=MESH,
        )
        self.count += 1
        copy.start()
        self.started.append(copy)
        return copy

    def keep(self, source, target):
        copy = pltpu.make_async_copy(source, target, self.local.at[self.local_count])
        self.local_count += 1
        copy.start()
        return copy

    def finish(self):
        for copy in self.started:
            copy.wait_send()


def greet(devices, partner=None, crossing=None):
    barrier = pltpu.get_barrier_semaphore()
    for device in devices:
        pl.semaphore_signal(barrier, inc=1, device_id=device, device_id_type=MESH)
    if partner is None:
        pl.semaphore_wait(barrier, len(devices))
        return

    @pl.when(crossing)
    def _():
        pl.semaphore_signal(barrier, inc=1, device_id=partner, device_id_type=MESH)
        pl.semaphore_wait(barrier, len(devices) + 1)

    @pl.when(jnp.logical_not(crossing))
    def _():
        pl.semaphore_wait(barrier, len(devices))


def comm_call(body, name, ident, outs, copies, locals_, args, spaces=None, out_spaces=None, scratch=()):
    spaces = [pl.ANY] * len(args) if spaces is None else spaces
    out_spaces = [pl.ANY] * len(outs) if out_spaces is None else out_spaces
    return pl.pallas_call(
        body,
        name=name,
        out_shape=tuple(outs),
        in_specs=[pl.BlockSpec(memory_space=space) for space in spaces],
        out_specs=tuple(pl.BlockSpec(memory_space=space) for space in out_spaces),
        scratch_shapes=[
            pltpu.SemaphoreType.DMA((max(copies, 1),)),
            pltpu.SemaphoreType.DMA((max(copies, 1),)),
            pltpu.SemaphoreType.DMA((max(locals_, 1),)),
            *scratch,
        ],
        compiler_params=pltpu.CompilerParams(
            collective_id=ident, has_side_effects=True, vmem_limit_bytes=VMEM_LIMIT
        ),
    )(*args)


def spread_tokens(zs, tokens, slab):
    n, width = tokens.shape
    groups, rows, columns = slab.shape
    plane = 4 * zs - 1

    def body(tok, piece, tok_all, w_all, send, recv, local):
        me = Place(zs)
        copies = Copies(send, recv, local)
        greet(
            [me.at(g=to) for to, _ in me.line()]
            + [me.at(x=to[0], z=to[1], y=to[2]) for to, _ in me.plane()]
            + [me.sibling()]
        )
        first = [
            copies.push(
                piece.at[to], w_all.at[me.x, me.c, me.z, me.g, me.y], me.at(g=to)
            )
            for to, _ in me.line()
        ]
        own = copies.keep(piece.at[me.g], w_all.at[me.x, me.c, me.z, me.g, me.y])
        arrivals = [copies.push(tok, tok_all.at[me.g], me.at(g=to)) for to, _ in me.line()]
        mine = copies.keep(tok, tok_all.at[me.g])
        own.wait()
        for copy in first:
            copy.wait_recv()
        block = w_all.at[me.x, me.c, me.z, :, me.y]
        second = [
            copies.push(block, block, me.at(x=to[0], z=to[1], y=to[2])) for to, _ in me.plane()
        ]
        arrivals.append(copies.push(block, block, me.sibling()))
        for copy, (_, source) in zip(second, me.plane()):
            copy.wait_recv()
            part = w_all.at[source[0], me.c, source[1], :, source[2]]
            arrivals.append(copies.push(part, part, me.sibling()))
        for copy in arrivals:
            copy.wait_recv()
        mine.wait()
        copies.finish()

    return comm_call(
        body,
        "spread_tokens",
        0,
        [
            jax.ShapeDtypeStruct((GROUPS, n, width), low_type),
            jax.ShapeDtypeStruct((2, 2, zs, GROUPS, 2, rows, columns), low_type),
        ],
        2 * (GROUPS - 1) + 2 * plane + 1,
        2,
        (tokens, slab),
    )


def spread_keys(zs, keys, inner, outer, mix):
    groups, n, width = keys.shape
    quarters, rows, columns = inner.shape
    tall, _ = outer.shape
    plane, column = 4 * zs - 1, GROUPS * zs - 1

    def body(kv, w1s, w2s, wms, kv_all, w1, w2, wm, send, recv, local, swap_send, swap_recv):
        me = Place(zs)
        copies = Copies(send, recv, local)
        crossing = me.c != me.y
        greet(
            [me.at(x=to[0], z=to[1], y=to[2]) for to, _ in me.plane()]
            + [me.at(z=to[0], g=to[1]) for to, _ in me.column()]
            + [me.at(z=to[0], g=to[1], c=me.y, y=me.c) for to, _ in me.column()]
            + [me.sibling()],
            me.at(c=me.y, y=me.c),
            crossing,
        )

        def here(ref):
            return ref.at[me.x, me.c, me.z, me.g, me.y]

        flat = me.plane(everywhere=False)
        own = [
            copies.keep(w1s.at[me.x * 2 + me.y], here(w1)),
            copies.keep(wms, here(wm)),
            copies.keep(kv, kv_all.at[me.x, me.c, me.z, :, me.y]),
        ]
        w1_first = [
            copies.push(w1s.at[to[0] * 2 + to[2]], here(w1), me.at(x=to[0], y=to[2]))
            for to, _ in flat
        ]
        wm_first = [
            copies.push(wms, here(wm), me.at(z=to[0], g=to[1])) for to, _ in me.column()
        ]
        mine = kv_all.at[me.x, me.c, me.z, :, me.y]
        kv_first = [
            copies.push(kv, mine, me.at(x=to[0], z=to[1], y=to[2])) for to, _ in me.plane()
        ]
        arrivals = [copies.push(kv, mine, me.sibling())]
        w2_first = [
            copies.push(
                w2s, w2.at[me.z, me.g, me.y], me.at(z=to[0], g=to[1], c=me.y, y=me.c)
            )
            for to, _ in me.column()
        ]
        exchanged = pltpu.make_async_remote_copy(
            src_ref=w2s,
            dst_ref=w2.at[me.z, me.g, me.y],
            send_sem=swap_send,
            recv_sem=swap_recv,
            device_id=me.at(c=me.y, y=me.c),
            device_id_type=MESH,
        )
        stays = pltpu.make_async_copy(w2s, w2.at[me.z, me.g, me.y], swap_recv)

        @pl.when(crossing)
        def _():
            exchanged.start()

        @pl.when(jnp.logical_not(crossing))
        def _():
            stays.start()

        own[0].wait()
        for copy in w1_first:
            copy.wait_recv()
        block = w1.at[:, me.c, me.z, me.g, :]
        w1_second = [
            copies.push(block, block, me.at(z=to[0], g=to[1])) for to, _ in me.column()
        ]
        arrivals.append(copies.push(block, block, me.sibling()))
        own[1].wait()
        for copy in wm_first:
            copy.wait_recv()
        block = wm.at[me.x, me.c, :, :, me.y]
        wm_second = [copies.push(block, block, me.at(x=to[0], y=to[2])) for to, _ in flat]
        arrivals.append(copies.push(block, block, me.sibling()))
        for copy, (_, source) in zip(kv_first, me.plane()):
            copy.wait_recv()
            part = kv_all.at[source[0], me.c, source[1], :, source[2]]
            arrivals.append(copies.push(part, part, me.sibling()))

        @pl.when(crossing)
        def _():
            exchanged.wait_recv()
            exchanged.wait_send()

        @pl.when(jnp.logical_not(crossing))
        def _():
            stays.wait()

        part = w2.at[me.z, me.g, me.c]
        arrivals.append(copies.push(part, part, me.sibling()))
        for copy, (_, source) in zip(wm_second, flat):
            copy.wait_recv()
            part = wm.at[source[0], me.c, :, :, source[2]]
            arrivals.append(copies.push(part, part, me.sibling()))
        for copy, (_, source) in zip(w2_first, me.column()):
            copy.wait_recv()
            part = w2.at[source[0], source[1], me.c]
            arrivals.append(copies.push(part, part, me.sibling()))
        for copy, (_, source) in zip(w1_second, me.column()):
            copy.wait_recv()
            part = w1.at[:, me.c, source[0], source[1], :]
            arrivals.append(copies.push(part, part, me.sibling()))
        for copy in arrivals:
            copy.wait_recv()
        own[2].wait()
        copies.finish()

    return comm_call(
        body,
        "spread_keys",
        1,
        [
            jax.ShapeDtypeStruct((2, 2, zs, GROUPS, 2, n, width), low_type),
            jax.ShapeDtypeStruct((2, 2, zs, GROUPS, 2, rows, columns), low_type),
            jax.ShapeDtypeStruct((zs, GROUPS, 2, tall, columns), low_type),
            jax.ShapeDtypeStruct((2, 2, zs, GROUPS, 2) + mix.shape, low_type),
        ],
        2 * plane + 1 + 2 * (3 + column + 1 + column) + column + 3 + 8,
        3,
        (keys, inner, outer, mix),
        scratch=(pltpu.SemaphoreType.DMA, pltpu.SemaphoreType.DMA),
    )


def exchange_line(zs, ident, pieces):
    def body(source, target, send, recv, local):
        me = Place(zs)
        copies = Copies(send, recv, local)
        greet([me.at(g=to) for to, _ in me.line()])
        arrivals = [
            copies.push(source.at[to], target.at[me.g], me.at(g=to)) for to, _ in me.line()
        ]
        own = copies.keep(source.at[me.g], target.at[me.g])
        for copy in arrivals:
            copy.wait_recv()
        own.wait()
        copies.finish()

    return comm_call(
        body,
        "exchange_line",
        ident,
        [jax.ShapeDtypeStruct(pieces.shape, pieces.dtype)],
        GROUPS - 1,
        1,
        (pieces,),
    )[0]


def gather_square(zs, ident, rows):
    def body(source, target, send, recv, local):
        me = Place(zs)
        copies = Copies(send, recv, local)
        flat = me.plane(everywhere=False)
        greet([me.at(x=to[0], y=to[2]) for to, _ in flat])
        place = target.at[me.x, me.y]
        arrivals = [copies.push(source, place, me.at(x=to[0], y=to[2])) for to, _ in flat]
        own = copies.keep(source, place)
        for copy in arrivals:
            copy.wait_recv()
        own.wait()
        copies.finish()

    return comm_call(
        body,
        "gather_square",
        ident,
        [jax.ShapeDtypeStruct((2, 2) + rows.shape, rows.dtype)],
        3,
        1,
        (rows,),
    )[0]


def exchange_square(zs, ident, pieces):
    def body(source, target, send, recv, local):
        me = Place(zs)
        copies = Copies(send, recv, local)
        flat = me.plane(everywhere=False)
        greet([me.at(x=to[0], y=to[2]) for to, _ in flat])
        place = target.at[me.x, me.y]
        arrivals = [
            copies.push(source.at[to[0], to[2]], place, me.at(x=to[0], y=to[2]))
            for to, _ in flat
        ]
        own = copies.keep(source.at[me.x, me.y], place)
        for copy in arrivals:
            copy.wait_recv()
        own.wait()
        copies.finish()

    return comm_call(
        body,
        "exchange_square",
        ident,
        [jax.ShapeDtypeStruct(pieces.shape, pieces.dtype)],
        3,
        1,
        (pieces,),
    )[0]


def loop(count, step):
    def body(index, carry):
        step(index)
        return carry

    lax.fori_loop(0, count, body, 0)


def total_of(*values):
    result = values[0].astype(wide)
    for value in values[1:]:
        result = result + value.astype(wide)
    return result


def reduce_keys(zs, dkv, grad1, grad2, gradm):
    n, width = dkv.shape[-2:]
    rows, columns = grad1.shape[-2:]
    rowsm = gradm.shape[-2]
    tall = grad2.shape[-2]
    plane, column = 4 * zs - 1, GROUPS * zs - 1
    count = GROUPS * zs

    def body(
        dkv_ref, g1, g2, gm, dkv_out, out1, out2, outm,
        send, recv, local,
        swap_send, swap_recv, kst, s1, p1, f1, s2, p2, sm, pm, fm, tm,
    ):
        me = Place(zs)
        copies = Copies(send, recv, local)
        crossing = me.c != me.y
        greet(
            [me.at(x=to[0], z=to[1], y=to[2]) for to, _ in me.plane()]
            + [me.at(z=to[0], g=to[1]) for to, _ in me.column()]
            + [me.at(z=to[0], g=to[1], c=me.y, y=me.c) for to, _ in me.column()]
            + [me.sibling()],
            me.at(c=me.y, y=me.c),
            crossing,
        )

        flat = me.plane(everywhere=False)
        other = 1 - me.c
        order = [to for to, _ in me.plane()] + [(me.x, me.z, me.y)]
        w1_half = copies.push(g1.at[:, other], s1, me.sibling())
        w2_half = copies.push(g2.at[:, :, other], s2, me.sibling())
        k_half = [
            copies.push(
                dkv_ref.at[to[0], other, to[1], :, to[2]], kst.at[to[0], to[1], to[2]], me.sibling()
            )
            for to in order
        ]
        wm_half = copies.push(gm.at[:, other], sm, me.sibling())

        w1_half.wait_recv()

        def add1(index):
            x, z, g, y = index // (count * 2), index // (GROUPS * 2) % zs, index // 2 % GROUPS, index % 2
            s1[x, z, g, y] = total_of(s1[x, z, g, y], g1[x, me.c, z, g, y]).astype(low_type)

        loop(4 * count, add1)
        w1_push = [
            copies.push(s1.at[:, to[0], to[1], :], p1.at[slot], me.at(z=to[0], g=to[1]))
            for slot, (to, _) in enumerate(me.column())
        ]
        w2_half.wait_recv()

        def add2(index):
            z, g = index // GROUPS, index % GROUPS
            s2[z, g] = total_of(s2[z, g], g2[z, g, me.c]).astype(low_type)

        loop(count, add2)
        w2_push = [
            copies.push(
                s2.at[to[0], to[1]], p2.at[slot + 1], me.at(z=to[0], g=to[1], c=me.y, y=me.c)
            )
            for slot, (to, _) in enumerate(me.column())
        ]
        exchanged = pltpu.make_async_remote_copy(
            src_ref=s2.at[me.z, me.g],
            dst_ref=p2.at[0],
            send_sem=swap_send,
            recv_sem=swap_recv,
            device_id=me.at(c=me.y, y=me.c),
            device_id_type=MESH,
        )
        stays = pltpu.make_async_copy(s2.at[me.z, me.g], p2.at[0], swap_recv)

        @pl.when(crossing)
        def _():
            exchanged.start()

        @pl.when(jnp.logical_not(crossing))
        def _():
            stays.start()

        k_push = []
        for slot, to in enumerate(order):
            k_half[slot].wait_recv()

            def addk(g, to=to):
                kst[to[0], to[1], to[2], g] = total_of(
                    kst[to[0], to[1], to[2], g], dkv_ref[to[0], me.c, to[1], g, to[2]]
                ).astype(low_type)

            loop(GROUPS, addk)
            if slot < plane:
                k_push.append(
                    copies.push(
                        kst.at[to[0], to[1], to[2]],
                        dkv_out.at[slot],
                        me.at(x=to[0], z=to[1], y=to[2]),
                    )
                )
        wm_half.wait_recv()

        def addm(index):
            x, z, g, y = index // (count * 2), index // (GROUPS * 2) % zs, index // 2 % GROUPS, index % 2
            sm[x, z, g, y] = total_of(sm[x, z, g, y], gm[x, me.c, z, g, y]).astype(low_type)

        loop(4 * count, addm)
        wm_push = [
            copies.push(sm.at[to[0], :, :, to[2]], pm.at[slot], me.at(x=to[0], y=to[2]))
            for slot, (to, _) in enumerate(flat)
        ]
        keep = copies.keep(kst.at[me.x, me.z, me.y], dkv_out.at[plane])
        for copy in wm_push:
            copy.wait_recv()

        def addf(index):
            z, g = index // GROUPS, index % GROUPS
            fm[z, g] = total_of(sm[me.x, z, g, me.y], pm[0, z, g], pm[1, z, g], pm[2, z, g]).astype(
                low_type
            )

        loop(count, addf)
        wm_last = [
            copies.push(fm.at[to[0], to[1]], tm.at[slot], me.at(z=to[0], g=to[1]))
            for slot, (to, _) in enumerate(me.column())
        ]
        for copy in w1_push:
            copy.wait_recv()

        def addg(index):
            x, y = index // 2, index % 2
            f1[x, y] = total_of(
                s1[x, me.z, me.g, y], *[p1[slot, x, y] for slot in range(column)]
            ).astype(low_type)

        loop(4, addg)
        quarter = out1.at[me.x * 2 + me.y]
        w1_last = [
            copies.push(f1.at[to[0], to[2]], quarter, me.at(x=to[0], y=to[2])) for to, _ in flat
        ]
        keep1 = copies.keep(f1.at[me.x, me.y], quarter)

        @pl.when(crossing)
        def _():
            exchanged.wait_recv()
            exchanged.wait_send()

        @pl.when(jnp.logical_not(crossing))
        def _():
            stays.wait()

        for copy in w2_push:
            copy.wait_recv()
        out2[...] = total_of(*[p2[slot] for slot in range(column + 1)])
        for copy in wm_last:
            copy.wait_recv()
        outm[...] = total_of(fm[me.z, me.g], *[tm[slot] for slot in range(column)])
        for copy in w1_last + k_push:
            copy.wait_recv()
        keep.wait()
        keep1.wait()
        copies.finish()

    vmem = pltpu.VMEM
    return comm_call(
        body,
        "reduce_keys",
        8,
        [
            jax.ShapeDtypeStruct((plane + 1, GROUPS, n, width), low_type),
            jax.ShapeDtypeStruct((4, rows, columns), low_type),
            jax.ShapeDtypeStruct((tall, columns), wide),
            jax.ShapeDtypeStruct((rowsm, columns), wide),
        ],
        3 + (plane + 1) + 2 * column + plane + 3 + column + 3,
        2,
        (dkv, grad1, grad2, gradm),
        spaces=[vmem] * 4,
        out_spaces=[pl.ANY, pl.ANY, vmem, vmem],
        scratch=(
            pltpu.SemaphoreType.DMA,
            pltpu.SemaphoreType.DMA,
            vmem((2, zs, 2, GROUPS, n, width), low_type),
            vmem((2, zs, GROUPS, 2, rows, columns), low_type),
            vmem((column, 2, 2, rows, columns), low_type),
            vmem((2, 2, rows, columns), low_type),
            vmem((zs, GROUPS, tall, columns), low_type),
            vmem((column + 1, tall, columns), low_type),
            vmem((2, zs, GROUPS, 2, rowsm, columns), low_type),
            vmem((3, zs, GROUPS, rowsm, columns), low_type),
            vmem((zs, GROUPS, rowsm, columns), low_type),
            vmem((column, rowsm, columns), low_type),
        ),
    )


def reduce_tokens(zs, dx, gradq):
    rows, columns = gradq.shape[-2:]
    plane = 4 * zs - 1
    count = GROUPS * zs

    def body(dx_ref, gq, dx_out, outq, send, recv, local, sq, pq, fq):
        me = Place(zs)
        copies = Copies(send, recv, local)
        greet(
            [me.at(g=to) for to, _ in me.line()]
            + [me.at(x=to[0], z=to[1], y=to[2]) for to, _ in me.plane()]
            + [me.sibling()]
        )
        half = copies.push(gq.at[:, 1 - me.c], sq, me.sibling())
        arrivals = [
            copies.push(dx_ref.at[to], dx_out.at[me.g], me.at(g=to)) for to, _ in me.line()
        ]
        own = copies.keep(dx_ref.at[me.g], dx_out.at[me.g])
        half.wait_recv()

        def add1(index):
            x, z, g, y = index // (count * 2), index // (GROUPS * 2) % zs, index // 2 % GROUPS, index % 2
            sq[x, z, g, y] = total_of(sq[x, z, g, y], gq[x, me.c, z, g, y]).astype(low_type)

        loop(4 * count, add1)
        second = [
            copies.push(
                sq.at[to[0], to[1], :, to[2]], pq.at[slot], me.at(x=to[0], z=to[1], y=to[2])
            )
            for slot, (to, _) in enumerate(me.plane())
        ]
        for copy in second:
            copy.wait_recv()

        def add2(g):
            fq[g] = total_of(
                sq[me.x, me.z, g, me.y], *[pq[slot, g] for slot in range(plane)]
            ).astype(low_type)

        loop(GROUPS, add2)
        arrivals += [
            copies.push(fq.at[to], outq.at[me.g], me.at(g=to)) for to, _ in me.line()
        ]
        keep = copies.keep(fq.at[me.g], outq.at[me.g])
        for copy in arrivals:
            copy.wait_recv()
        own.wait()
        keep.wait()
        copies.finish()

    vmem = pltpu.VMEM
    return comm_call(
        body,
        "reduce_tokens",
        9,
        [
            jax.ShapeDtypeStruct(dx.shape, low_type),
            jax.ShapeDtypeStruct((GROUPS, rows, columns), low_type),
        ],
        1 + 2 * (GROUPS - 1) + plane,
        2,
        (dx, gradq),
        spaces=[pl.ANY, vmem],
        scratch=(
            vmem((2, zs, GROUPS, 2, rows, columns), low_type),
            vmem((plane, GROUPS, rows, columns), low_type),
            vmem((GROUPS, rows, columns), low_type),
        ),
    )


NEXT = (((1,), (1,)), ((), ()))
DOWN = (((0,), (0,)), ((), ()))


def attend_forward(queries, keys, bounds, low, high, tile, block):
    total_rows = queries.shape[0]

    def body(bounds_ref, q_ref, kv_ref, low_ref, high_ref, out_ref, keep_ref, lse_ref):
        def one(turn, unused):
            rows = pl.ds(pl.multiple_of(turn * tile, tile), tile)
            first, last = low_ref[rows, :], high_ref[rows, :]
            heads = [
                q_ref[rows, h * LANES : (h + 1) * LANES] * jnp.asarray(0.125, low_type)
                for h in range(LOCAL)
            ]

            def step(j, carry):
                begin = pl.multiple_of(j * block, block)
                place = begin + lax.broadcasted_iota(jnp.int32, (tile, block), 1)
                same = (place >= first) & (place < last)
                result = []
                for h in range(LOCAL):
                    top, total, mixed = carry[h]
                    kv = kv_ref[pl.ds(begin, block), h * LANES : (h + 1) * LANES]
                    scores = lax.dot_general(heads[h], kv, NEXT, preferred_element_type=wide)
                    scores = jnp.where(same, scores, mask_fill)
                    new_top = jnp.maximum(top, jnp.max(scores, axis=1, keepdims=True))
                    factor = jnp.exp(top - new_top)
                    powers = jnp.exp(scores - new_top)
                    total = total * factor + jnp.sum(powers, axis=1, keepdims=True)
                    mixed = mixed * factor + jnp.dot(
                        powers.astype(low_type), kv, preferred_element_type=wide
                    )
                    result.append((new_top, total, mixed))
                return tuple(result)

            start = tuple(
                (
                    jnp.full((tile, 1), lowest_start, wide),
                    jnp.zeros((tile, 1), wide),
                    jnp.zeros((tile, LANES), wide),
                )
                for _ in range(LOCAL)
            )
            done = lax.fori_loop(bounds_ref[turn, 0], bounds_ref[turn, 1], step, start)
            lane = lax.broadcasted_iota(jnp.int32, (tile, LANES), 1)
            upper = lane >= HEAD
            mixes = [mixed / total for _, total, mixed in done]
            turned = [pltpu.roll(mixed, HEAD, 1) for mixed in mixes]
            front = jnp.where(upper, mixes[1], turned[0])
            back = jnp.where(upper, 0.0, turned[2])
            both = jnp.concatenate([front, back], axis=1)
            keep_ref[rows, :] = both
            out_ref[rows, :] = both.astype(low_type)
            ends = [top + jnp.log(total) for top, total, _ in done]
            lse_ref[rows, :] = jnp.where(lane == 0, ends[0], jnp.where(lane == 1, ends[1], ends[2]))
            return unused

        lax.fori_loop(0, total_rows // tile, one, 0)

    vmem = pl.BlockSpec(memory_space=pltpu.VMEM)
    return pl.pallas_call(
        body,
        name="attend_forward",
        out_shape=(
            jax.ShapeDtypeStruct((total_rows, PACK), low_type),
            jax.ShapeDtypeStruct((total_rows, PACK), wide),
            jax.ShapeDtypeStruct((total_rows, LANES), wide),
        ),
        in_specs=[pl.BlockSpec(memory_space=pltpu.SMEM)] + [vmem] * 4,
        out_specs=(vmem,) * 3,
        compiler_params=pltpu.CompilerParams(vmem_limit_bytes=VMEM_LIMIT),
    )(bounds, queries, keys, low, high)


def attend_backward(queries, keys, grads, stats, bounds, tile, block):
    total_rows = queries.shape[0]
    tokens = keys.shape[0]

    def body(bounds_ref, q_ref, kv_ref, do_ref, stat_ref, dq_ref, dkv_ref, sums):
        h = pl.program_id(0)
        zeros = jnp.zeros((block, LANES), wide)

        def clear(j, unused):
            sums[pl.ds(pl.multiple_of(j * block, block), block), :] = zeros
            return unused

        lax.fori_loop(0, tokens // block, clear, 0)
        lane = lax.broadcasted_iota(jnp.int32, (tile, LANES), 1)
        upper = lane >= HEAD

        def one(turn, unused):
            rows = pl.ds(pl.multiple_of(turn * tile, tile), tile)
            q = q_ref[rows, :] * jnp.asarray(0.125, low_type)
            front = do_ref[rows, :LANES].astype(wide)
            back = do_ref[rows, LANES:].astype(wide)
            grad = jnp.where(h == 1, front, pltpu.roll(jnp.where(h == 0, front, back), HEAD, 1))
            grad = jnp.where(upper, grad, 0.0).astype(low_type)
            stat = stat_ref[turn, 0]
            first, last = stat[0:1, :], stat[1:2, :]
            lse, delta = stat[2:3, :], stat[3:4, :]

            def step(j, total):
                begin = pl.multiple_of(j * block, block)
                place = (begin + lax.broadcasted_iota(jnp.int32, (block, tile), 0)).astype(wide)
                same = (place >= first) & (place < last)
                kv = kv_ref[pl.ds(begin, block), :]
                scores = lax.dot_general(kv, q, NEXT, preferred_element_type=wide)
                probs = jnp.exp(jnp.where(same, scores, mask_fill) - lse)
                dots = lax.dot_general(kv, grad, NEXT, preferred_element_type=wide)
                score_grad = (probs * (dots - delta)).astype(low_type)
                sums[pl.ds(begin, block), :] += jnp.dot(
                    score_grad, q, preferred_element_type=wide
                ) + jnp.dot(probs.astype(low_type), grad, preferred_element_type=wide)
                return total + lax.dot_general(score_grad, kv, DOWN, preferred_element_type=wide)

            total = lax.fori_loop(
                bounds_ref[turn, 0], bounds_ref[turn, 1], step, jnp.zeros((tile, LANES), wide)
            )
            dq_ref[rows, :] = jnp.where(upper, 0.0, total * 0.125).astype(low_type)
            return unused

        lax.fori_loop(0, total_rows // tile, one, 0)

        def store(j, unused):
            part = pl.ds(pl.multiple_of(j * block, block), block)
            dkv_ref[part, :] = sums[part, :].astype(low_type)
            return unused

        lax.fori_loop(0, tokens // block, store, 0)

    return pl.pallas_call(
        body,
        name="attend_backward",
        grid=(LOCAL,),
        out_shape=(
            jax.ShapeDtypeStruct((total_rows, WIDE), low_type),
            jax.ShapeDtypeStruct((tokens, WIDE), low_type),
        ),
        in_specs=[
            pl.BlockSpec(memory_space=pltpu.SMEM),
            pl.BlockSpec((total_rows, LANES), lambda h: (0, h)),
            pl.BlockSpec((tokens, LANES), lambda h: (0, h)),
            pl.BlockSpec((total_rows, PACK), lambda h: (0, 0)),
            pl.BlockSpec((total_rows // tile, 1, 8, tile), lambda h: (0, h, 0, 0)),
        ],
        out_specs=(
            pl.BlockSpec((total_rows, LANES), lambda h: (0, h)),
            pl.BlockSpec((tokens, LANES), lambda h: (0, h)),
        ),
        scratch_shapes=[pltpu.VMEM((tokens, LANES), wide)],
        compiler_params=pltpu.CompilerParams(vmem_limit_bytes=VMEM_LIMIT),
    )(bounds, queries, keys, grads, stats)


class Spot(Place):
    def __init__(self):
        super().__init__(1)
        self.half = self.g // 2
        self.a = self.x * 2 + self.c
        self.p = (self.x + self.c) % 2
        self.selfish = self.g % 2 == self.p
        self.crossing = self.c != self.y

    def square(self):
        return [(to[0], to[2]) for to, _ in self.plane()]

    def readers(self):
        result = []
        for k in range(GROUPS):
            g = (self.g + k) % GROUPS
            result.append((g, self.at(x=(self.g + self.c) % 2, g=g)))
        return result

    def owners(self):
        result = []
        for dv in range(2):
            for du in range(2):
                u, v = (self.x + du) % 2, (self.half + dv) % 2
                result.append((u * 2 + v, self.at(x=u, g=2 * v + self.p)))
        return result

    def slot(self):
        return self.x * 2 + self.half


def count_of(flag):
    return jnp.where(flag, 1, 0)


def announce(always, maybe):
    barrier = pltpu.get_barrier_semaphore()
    for device in always:
        pl.semaphore_signal(barrier, inc=1, device_id=device, device_id_type=MESH)
    for flag, device in maybe:

        @pl.when(flag)
        def _(device=device):
            pl.semaphore_signal(barrier, inc=1, device_id=device, device_id_type=MESH)

    total = len(always)
    for flag, _ in maybe:
        total = total + count_of(flag)
    return barrier, total


class Scatter:
    def __init__(self, send, recv, here):
        self.send, self.recv, self.here = send, recv, here
        self.copies = []

    def start(self, pieces, target, slot):
        for source, device in pieces:
            self.send_one(source, target, slot, device)

    def send_one(self, source, target, slot, device):
        index = len(self.copies)
        copy = pltpu.make_async_remote_copy(
            src_ref=source,
            dst_ref=target,
            send_sem=self.send.at[index],
            recv_sem=self.recv.at[slot],
            device_id=device,
            device_id_type=MESH,
        )
        self.copies.append(copy)
        if index:
            copy.start()
            return
        stay = pltpu.make_async_copy(source, target, self.recv.at[slot])

        @pl.when(self.here)
        def _():
            stay.start()

        @pl.when(jnp.logical_not(self.here))
        def _():
            copy.start()

    def arrived(self, slot, target):
        pltpu.make_async_copy(target, target, self.recv.at[slot]).wait()

    def finish(self):
        for copy in self.copies[1:]:
            copy.wait_send()

        @pl.when(jnp.logical_not(self.here))
        def _():
            self.copies[0].wait_send()


SMALL = 16


def first_tables(s, e, width):
    column = np.arange(width)
    rows = [column % s, column // s, column % e, column // e]
    return np.stack(rows + [np.zeros_like(column)] * 4).astype(np.int32)


def first_kernel(lengths, tokens, wq, wk, wv, vectors, inner, mix, e):
    n, depth = tokens.shape
    s = wq.shape[0]
    quarter = inner.shape[1] // 4
    cols = 2 * WIDE + LANES
    tables = jnp.asarray(first_tables(s, e, 2 * WIDE))
    count = len(vectors)

    def body(*refs):
        lengths_in, tok = refs[:2]
        arguments = refs[2 : 8 + count]
        (
            tok_out, q_out, wqkv_out, vec_out, kv_out, w1, wm, mixed_out, mixed_wide, lse_out,
            send, recv, local, tok_send, tok_recv,
            slab, toks, weights, kv_own, q_own, w1s, wms, vec, few, kv_all, scaled, sums,
            loaded, lengths_ref, lengths_sem, *places,
        ) = refs[8 + count :]
        wq_ref, wk_ref, wv_ref, tab = places[:4]
        vecs = places[4 : 4 + count]
        w1f, wmf = places[4 + count :]
        loads = [pltpu.make_async_copy(lengths_in, lengths_ref, lengths_sem)]
        loads[0].start()
        for index, (argument, place) in enumerate(zip(arguments, places)):
            loads.append(pltpu.make_async_copy(argument, place, loaded.at[index]))
            loads[-1].start()
        me = Spot()
        copies = Copies(send, recv, local)
        square = me.square()
        line = [to for to, _ in me.line()]
        sources = [device for _, device in me.owners()]
        barrier, expected = announce(
            [me.at(x=x, y=y) for x, y in square]
            + [me.at(g=to) for to in line]
            + sources[1:]
            + [me.sibling()],
            [(jnp.logical_not(me.selfish), sources[0])],
        )
        for copy in loads:
            copy.wait()
        lane = lax.broadcasted_iota(jnp.int32, (s, LANES), 1)
        lower = lane < HEAD
        for head in range(HEADS):
            pair = slice(head // 2 * LANES, head // 2 * LANES + LANES)
            q, k, v = wq_ref[:, pair], wk_ref[:, pair], wv_ref[:, pair]
            if head % 2:
                q, k = pltpu.roll(q, HEAD, 1), pltpu.roll(k, HEAD, 1)
            else:
                v = pltpu.roll(v, HEAD, 1)
            g, h = head // LOCAL, head % LOCAL
            slab[g, :, h * LANES : (h + 1) * LANES] = jnp.where(lower, k, v).astype(low_type)
            slab[g, :, WIDE + h * LANES : WIDE + (h + 1) * LANES] = jnp.where(lower, q, 0.0).astype(
                low_type
            )
        wms[...] = wmf[...].astype(low_type)
        few[...] = jnp.zeros((s, LANES), wide)
        for index in range(count):
            few[index : index + 1, : vecs[index].shape[1]] = vecs[index][...]
        small = few[...]
        for g in range(GROUPS):
            slab[g, :, 2 * WIDE :] = small.astype(low_type)
        pl.semaphore_wait(barrier, expected)

        view = weights
        place = view.at[me.a, me.g, me.y]
        slab_first = [copies.push(slab.at[to], place, me.at(g=to)) for to in line]
        slab_own = copies.keep(slab.at[me.g], place)
        for w in range(4):
            w1s[w] = w1f[:, w * quarter : (w + 1) * quarter].astype(low_type)
        place = w1.at[me.x, me.c, me.g, me.y]
        w1_first = [
            copies.push(w1s.at[x * 2 + y], place, me.at(x=x, y=y)) for x, y in square
        ]
        w1_own = copies.keep(w1s.at[me.x * 2 + me.y], place)
        wm_own = copies.keep(wms, wm.at[me.x, me.c, me.g, me.y])

        arrivals, weight_arrivals = [], []
        slab_own.wait()
        for copy in slab_first:
            copy.wait_recv()
        wm_first = [
            copies.push(wms, wm.at[me.x, me.c, me.g, me.y], me.at(g=to)) for to in line
        ]
        tokens_go = Scatter(tok_send, tok_recv, me.selfish)
        tokens_go.start([(tok, device) for _, device in me.readers()], toks.at[me.slot()], me.slot())
        block = view.at[me.a, :, me.y]
        slab_second = [copies.push(block, block, me.at(x=x, y=y)) for x, y in square]
        weight_arrivals.append(copies.push(block, block, me.sibling()))
        for copy, (x, y) in zip(slab_second, square):
            copy.wait_recv()
            block = view.at[x * 2 + me.c, :, y]
            weight_arrivals.append(copies.push(block, block, me.sibling()))
        wm_own.wait()
        for copy in wm_first:
            copy.wait_recv()
        block = wm.at[me.x, me.c, :, me.y]
        wm_second = [copies.push(block, block, me.at(x=x, y=y)) for x, y in square]
        arrivals.append(copies.push(block, block, me.sibling()))
        w1_own.wait()
        for copy in w1_first:
            copy.wait_recv()
        for copy in weight_arrivals:
            copy.wait_recv()

        table = tab[...]

        def spread(pieces, within, owner):
            count = pieces.shape[0] * SMALL
            item = lax.broadcasted_iota(jnp.int32, (count, 2 * WIDE), 0)
            index = lax.broadcasted_iota(jnp.int32, (LANES, 2 * WIDE), 0)
            chosen = jnp.where(index == within, 1.0, 0.0).astype(low_type)
            pieces = pieces.astype(wide).reshape(count, LANES).astype(low_type)
            found = jnp.dot(pieces, chosen, preferred_element_type=wide)
            found = jnp.where((item >> 4) == owner, found, 0.0)
            return jnp.sum(found.reshape(count // SMALL, SMALL, 2 * WIDE), axis=0)

        every = spread(
            view[:, :, :, :SMALL, 2 * WIDE :].reshape(32, SMALL, LANES), table[0:1], table[1:2]
        )
        w_me = me.x * 2 + me.y
        inner_bias = spread(
            view[w_me, :, :, :SMALL, 2 * WIDE :].reshape(8, SMALL, LANES), table[2:3], table[3:4]
        )
        rows16 = lax.broadcasted_iota(jnp.int32, (SMALL, 2 * WIDE), 0)
        vec[...] = jnp.where(rows16 == 8, inner_bias, every)
        turned = pltpu.roll(every, 2 * WIDE - me.g * LOCAL * HEAD, 1)
        lower = lax.broadcasted_iota(jnp.int32, (1, LANES), 1) < HEAD
        biases = [[], []]
        for h in range(LOCAL):
            pair = slice(h // 2 * LANES, h // 2 * LANES + LANES)
            q, v = turned[0:1, pair], turned[1:2, pair]
            if h % 2:
                q = pltpu.roll(q, HEAD, 1)
            else:
                v = pltpu.roll(v, HEAD, 1)
            biases[0].append(jnp.where(lower, 0.0, v))
            biases[1].append(jnp.where(lower, q, 0.0))
        bias = jnp.concatenate(biases[0] + biases[1], axis=1)

        matrix = weights[:, :, :, :, : 2 * WIDE].reshape(depth, 2 * WIDE)
        kept, kv_first = [copies.keep(weights, wqkv_out), copies.keep(vec, vec_out)], []
        kv_sibling, kv_kept = [], []
        for dv in range(2):
            v = (me.half + dv) % 2
            for u in range(2):
                tokens_go.arrived(u * 2 + v, toks.at[u * 2 + v])
            if dv:
                block = w1.at[:, me.c, me.g, :]
                w1_second = [copies.push(block, block, me.at(g=to)) for to in line]
            both = jnp.concatenate([toks[v], toks[2 + v]], axis=0)
            made = jnp.dot(both, matrix, preferred_element_type=wide)
            made = (made + bias).astype(low_type)
            for u in range(2):
                kv_own[v, u] = made[u * n : (u + 1) * n, :WIDE]
                q_own[u * 2 + v] = made[u * n : (u + 1) * n, WIDE:]
            mine = kv_all.at[:, me.c, v, me.p, me.y]
            kv_first.append(
                [copies.push(kv_own.at[v], mine, me.at(x=x, y=y)) for x, y in square]
            )
            kv_sibling.append(copies.push(kv_own.at[v], mine, me.sibling()))
            kv_kept.append(copies.keep(kv_own.at[v], mine))
        block = w1.at[:, me.c, me.g, :]
        arrivals.append(copies.push(block, block, me.sibling()))
        kept += [copies.keep(toks, tok_out), copies.keep(q_own, q_out)]
        for copy, (x, y) in zip(wm_second, square):
            copy.wait_recv()
            block = wm.at[x, me.c, :, y]
            arrivals.append(copies.push(block, block, me.sibling()))

        ends = ends_of(lengths_ref)
        rows = GROUPS * n
        spans = [slice(h * LANES, (h + 1) * LANES) for h in range(LOCAL)]
        along = lax.broadcasted_iota(jnp.int32, (1, n), 1)
        ranges = [document_of(along + tile_base(me, slot, n), ends) for slot in range(GROUPS)]
        first = jnp.concatenate([low for low, _ in ranges], axis=1)
        last = jnp.concatenate([high for _, high in ranges], axis=1)
        down = lax.broadcasted_iota(jnp.int32, (rows, rows), 0)
        for slot in range(GROUPS):
            for h, span in enumerate(spans):
                scaled[h, slot * n : (slot + 1) * n] = q_own[slot, :, span] * jnp.asarray(
                    0.125, low_type
                )
        sums[...] = jnp.zeros_like(sums)

        def attend(u, c, v, carry):
            begin = ((u * 2 + c) * 2 + v) * rows
            place = down + begin
            same = (place >= first) & (place < last)
            result = []
            for h, span in enumerate(spans):
                top, total = carry[h]
                kv = kv_all[u, c, v, :, :, :, span].reshape(rows, LANES)
                scores = lax.dot_general(kv, scaled[h], NEXT, preferred_element_type=wide)
                scores = jnp.where(same, scores, mask_fill)
                new_top = jnp.maximum(top, jnp.max(scores, axis=0, keepdims=True))
                factor = jnp.exp(top - new_top)
                powers = jnp.exp(scores - new_top)
                total = total * factor + jnp.sum(powers, axis=0, keepdims=True)
                sums[h] = sums[h] * factor + lax.dot_general(
                    kv, powers.astype(low_type), DOWN, preferred_element_type=wide
                )
                result.append((new_top, total))
            return tuple(result)

        state = tuple(
            (jnp.full((1, rows), lowest_start, wide), jnp.zeros((1, rows), wide))
            for _ in range(LOCAL)
        )
        for dv in range(2):
            v = (me.half + dv) % 2
            forwards = [kv_sibling[dv]]
            for copy, (x, y) in zip(kv_first[dv], square):
                copy.wait_recv()
                block = kv_all.at[:, me.c, v, (x + me.c) % 2, y]
                forwards.append(copies.push(block, block, me.sibling()))
            kv_kept[dv].wait()
            state = lax.fori_loop(
                0, 2, lambda u, carry, v=v: attend(u, me.c, v, carry), state
            )
            for copy in forwards:
                copy.wait_recv()
            state = lax.fori_loop(
                0, 2, lambda u, carry, v=v: attend(u, 1 - me.c, v, carry), state
            )
        kept.append(copies.keep(kv_all, kv_out))
        for copy, (_, source) in zip(w1_second, me.line()):
            copy.wait_recv()
            block = w1.at[:, me.c, source, :]
            arrivals.append(copies.push(block, block, me.sibling()))
        lane = lax.broadcasted_iota(jnp.int32, (n, LANES), 1)
        upper = lane >= HEAD
        for slot in range(GROUPS):
            part = slice(slot * n, (slot + 1) * n)
            mixes = []
            for h in range(LOCAL):
                top, total = state[h]
                mixes.append(jnp.transpose(sums[h, :, part] / total[:, part]))
                lse_out[slot, h : h + 1, :] = top[:, part] + jnp.log(total[:, part])
            turned = [pltpu.roll(mixes[h], HEAD, 1) for h in (0, 2)]
            both = jnp.concatenate(
                [jnp.where(upper, mixes[1], turned[0]), jnp.where(upper, 0.0, turned[1])], axis=1
            )
            mixed_wide[part, :] = both
            mixed_out[slot] = both.astype(low_type)
        for copy in arrivals:
            copy.wait_recv()
        for copy in kept:
            copy.wait()
        tokens_go.finish()
        copies.finish()

    vmem = pltpu.VMEM
    dma = pltpu.SemaphoreType.DMA
    total = 64
    return pl.pallas_call(
        body,
        name="first_kernel",
        out_shape=(
            jax.ShapeDtypeStruct((GROUPS, n, depth), low_type),
            jax.ShapeDtypeStruct((GROUPS, n, WIDE), low_type),
            pltpu.HBM((4, GROUPS, 2, s, cols), low_type),
            jax.ShapeDtypeStruct((SMALL, 2 * WIDE), wide),
            pltpu.HBM((2, 2, 2, 2, 2, n, WIDE), low_type),
            jax.ShapeDtypeStruct((2, 2, GROUPS, 2, s, quarter), low_type),
            jax.ShapeDtypeStruct((2, 2, GROUPS, 2, s, depth), low_type),
            jax.ShapeDtypeStruct((GROUPS, n, PACK), low_type),
            jax.ShapeDtypeStruct((GROUPS * n, PACK), wide),
            jax.ShapeDtypeStruct((GROUPS, 8, n), wide),
        ),
        in_specs=[pl.BlockSpec(memory_space=pltpu.HBM)] * (8 + count),
        out_specs=(pl.BlockSpec(memory_space=pl.ANY),) * 7
        + (pl.BlockSpec(memory_space=vmem),) * 3,
        scratch_shapes=[
            dma((total,)), dma((total,)), dma((12,)), dma((4,)), dma((4,)),
            vmem((GROUPS, s, cols), low_type),
            vmem((GROUPS, n, depth), low_type),
            vmem((4, GROUPS, 2, s, cols), low_type),
            vmem((2, 2, n, WIDE), low_type),
            vmem((GROUPS, n, WIDE), low_type),
            vmem((4, s, quarter), low_type),
            vmem((s, depth), low_type),
            vmem((SMALL, 2 * WIDE), wide),
            vmem((s, LANES), wide),
            vmem((2, 2, 2, 2, 2, n, WIDE), low_type),
            vmem((LOCAL, GROUPS * n, LANES), low_type),
            vmem((LOCAL, LANES, GROUPS * n), wide),
            dma((6 + count,)),
            pltpu.SMEM(lengths.shape, jnp.int32),
            dma,
            *[vmem(item.shape, item.dtype) for item in (wq, wk, wv, tables, *vectors, inner, mix)],
        ],
        compiler_params=pltpu.CompilerParams(
            collective_id=10, has_side_effects=True, vmem_limit_bytes=NEAR_LIMIT
        ),
    )(*[pltpu.with_memory_space_constraint(item, pltpu.HBM) for item in (lengths, tokens, wq, wk, wv, tables, *vectors, inner, mix)])


def pass_back(ident, pieces):
    def body(source, target, send, recv):
        me = Spot()
        owners = me.owners()
        readers = [device for _, device in me.readers()]
        barrier, expected = announce(readers[1:], [(jnp.logical_not(me.selfish), readers[0])])
        pl.semaphore_wait(barrier, expected)
        move = Scatter(send, recv, me.selfish)
        move.start([(source.at[slot], device) for slot, device in owners], target.at[me.g], me.g)
        for g in range(GROUPS):
            move.arrived(g, target.at[g])
        move.finish()

    return scatter_call(body, "pass_back", ident, pieces)


def pass_on(ident, pieces):
    def body(source, target, send, recv):
        me = Spot()
        owners = [device for _, device in me.owners()]
        barrier, expected = announce(owners[1:], [(jnp.logical_not(me.selfish), owners[0])])
        pl.semaphore_wait(barrier, expected)
        move = Scatter(send, recv, me.selfish)
        slot = me.slot()
        move.start([(source.at[g], device) for g, device in me.readers()], target.at[slot], slot)
        for index in range(GROUPS):
            move.arrived(index, target.at[index])
        move.finish()

    return scatter_call(body, "pass_on", ident, pieces)


def scatter_call(body, name, ident, pieces):
    return pl.pallas_call(
        body,
        name=name,
        out_shape=jax.ShapeDtypeStruct(pieces.shape, pieces.dtype),
        in_specs=[pl.BlockSpec(memory_space=pl.ANY)],
        out_specs=pl.BlockSpec(memory_space=pl.ANY),
        scratch_shapes=[pltpu.SemaphoreType.DMA((4,)), pltpu.SemaphoreType.DMA((4,))],
        compiler_params=pltpu.CompilerParams(
            collective_id=ident, has_side_effects=True, vmem_limit_bytes=VMEM_LIMIT
        ),
    )(pieces)


def final_kernel(hidden, pieces, outqk, out1, out2, outm, s, e):
    n, depth = hidden.shape
    quarter = out1.shape[-1]

    def body(hid, dx, qk_in, i_in, o_in, m_in, xg, qw, qb, kw, vw, vb, mw, mb, eg, es, iw, ib, ow, ob, fg, fs):
        device = lax.axis_index("au") * lax.axis_size("row") + lax.axis_index("row")
        xg[...] = total_of(hid[...], dx[0], dx[1], dx[2], dx[3]).astype(low_type)
        rows = qk_in.shape[1]
        q_in, k_in = qk_in.at[:, :, WIDE:], qk_in.at[:, :, :WIDE]
        lower = lax.broadcasted_iota(jnp.int32, (rows, LANES), 1) < HEAD

        def part(head):
            g, h = head // LOCAL, head % LOCAL
            return k_in[g, :, h * LANES : (h + 1) * LANES].astype(wide)

        made_q = []
        for g in range(0, GROUPS, 2):
            a0, b0 = q_in[g, :, :LANES].astype(wide), q_in[g, :, LANES:].astype(wide)
            a1 = pltpu.roll(q_in[g + 1, :, :LANES].astype(wide), HEAD, 1)
            b1 = pltpu.roll(q_in[g + 1, :, LANES:].astype(wide), HEAD, 1)
            made_q += [a0, jnp.where(lower, b0, a1), jnp.where(lower, a1, b1)]
        biases = [[], []]
        for pair in range(HEADS // 2):
            span = slice(pair * LANES, (pair + 1) * LANES)
            kv = [part(2 * pair), part(2 * pair + 1)]
            made_k = jnp.where(lower, kv[0], pltpu.roll(kv[1], HEAD, 1))
            made_v = jnp.where(lower, pltpu.roll(kv[0], HEAD, 1), kv[1])
            qw[:, span], kw[:, span], vw[:, span] = made_q[pair][:s], made_k[:s], made_v[:s]
            biases[0].append(made_q[pair][s:])
            biases[1].append(made_v[s:])

        def own(eight, width, shift):
            return pltpu.roll(eight, shift, 1)[0:1, :width]

        turn = (depth - device * s) % depth
        qb[...] = own(jnp.concatenate(biases[0], axis=1), s, turn)
        vb[...] = own(jnp.concatenate(biases[1], axis=1), s, turn)
        mw[...] = m_in[:s]
        extras = pltpu.roll(m_in[s : s + 8, :], turn, 1)
        for index, ref in enumerate((mb, eg, es, ob, fg, fs)):
            ref[...] = extras[index : index + 1, :s]
        for w in range(4):
            iw[:, w * quarter : (w + 1) * quarter] = i_in[w, :s].astype(wide)
        place = lax.axis_index("row") * e
        ib[...] = own(
            i_in[lax.axis_index("au"), s : s + 8, :].astype(wide), e, (quarter - place) % quarter
        )
        ow[...] = o_in[...]

    vmem = pltpu.VMEM

    def shape(*dims):
        return jax.ShapeDtypeStruct(dims, wide)

    return pl.pallas_call(
        body,
        name="final_kernel",
        out_shape=(
            jax.ShapeDtypeStruct((n, depth), low_type),
            shape(s, depth), shape(1, s), shape(s, depth), shape(s, depth), shape(1, s),
            shape(s, depth), shape(1, s), shape(1, s), shape(1, s),
            shape(s, 4 * quarter), shape(1, e), shape(e, depth),
            shape(1, s), shape(1, s), shape(1, s),
        ),
        in_specs=[pl.BlockSpec(memory_space=vmem)] * 6,
        out_specs=(pl.BlockSpec(memory_space=vmem),) * 16,
        compiler_params=pltpu.CompilerParams(vmem_limit_bytes=NEAR_LIMIT),
    )(hidden, pieces, outqk, out1, out2, outm)


def gelu_and_slope(value):
    t = 1.0 / (1.0 + (0.3275911 * 0.7071067811865476) * jnp.abs(value))
    bell = jnp.exp(-0.5 * value * value)
    tail = 1.061405429
    for weight in (-1.453152027, 1.421413741, -0.284496736, 0.254829592):
        tail = tail * t + weight
    tail = 0.5 * tail * t * bell
    below = jnp.where(value >= 0.0, 1.0 - tail, tail)
    return value * below, below + value * bell * 0.3989422804014327


def normed(hidden):
    mean = jnp.mean(hidden, axis=-1, keepdims=True)
    centered = hidden - mean
    spread = jnp.mean(centered * centered, axis=-1, keepdims=True)
    inverse = lax.rsqrt(spread + eps_norm)
    return centered * inverse, inverse


def normed_grad(grad, norm, inverse):
    mean = jnp.mean(grad, axis=-1, keepdims=True)
    along = jnp.mean(grad * norm, axis=-1, keepdims=True)
    return inverse * (grad - mean - norm * along)


def down_sum(values):
    return jnp.sum(values, axis=0, keepdims=True)


def middle_kernel(mixed, tokens, cotangent, mix, inner, outer, vec, s, e):
    n, depth = tokens.shape
    quarter = inner.shape[1]
    rows = s + 8
    cut = depth // 2
    hn = n // 2

    def body(
        mixed_ref, tok_in, cot_in, wm_in, w1_in, w2f_in, vec_in,
        out, hidden_out, do_out, sm, s1, s2,
        send, recv, local, back_send, back_recv, on_send, on_recv,
        swap_send2, swap_recv2, tok, cot, w2f, vec_ref, wm, w1, w2p, w2s, came, mixed_tok, xs, acts, slopes, parts, sums, bgs, igs, parts2, sums2,
        pieces, extra, attn, own1, own2, g1, g2, gm,
    ):
        me = Spot()
        copies = Copies(send, recv, local)
        square = me.square()
        line = [to for to, _ in me.line()]
        owners = me.owners()
        readers = me.readers()
        swapped = [me.at(g=to, c=me.y, y=me.c) for to in [me.g] + line]
        barrier, expected = announce(
            [me.at(x=x, y=y) for x, y in square]
            + swapped[1:]
            + [device for _, device in readers[1:]]
            + [device for _, device in owners[1:]]
            + [me.sibling()],
            [
                (jnp.logical_not(me.selfish), readers[0][1]),
                (jnp.logical_not(me.selfish), owners[0][1]),
                (me.crossing, swapped[0]),
            ],
        )
        loads = [copies.keep(wm_in, wm), copies.keep(w1_in, w1)]
        small_loads = [
            copies.keep(source, target)
            for source, target in ((tok_in, tok), (vec_in, vec_ref), (w2f_in, w2f), (cot_in, cot))
        ]
        pl.semaphore_wait(barrier, expected)

        back = Scatter(back_send, back_recv, me.selfish)
        back.start([(mixed_ref.at[slot], device) for slot, device in owners], came.at[me.g], me.g)
        lower = lax.broadcasted_iota(jnp.int32, (n, LANES), 1) < HEAD
        loads[0].wait()
        for copy in small_loads:
            copy.wait()
        w2s[...] = w2f[...].astype(low_type)
        for g in range(GROUPS):
            back.arrived(g, came.at[g])
        w2_place = w2p.at[me.g, me.y]
        w2_first = [copies.push(w2s, w2_place, device) for device in swapped[1:]]
        w2_swap = pltpu.make_async_remote_copy(
            src_ref=w2s,
            dst_ref=w2_place,
            send_sem=swap_send2,
            recv_sem=swap_recv2,
            device_id=swapped[0],
            device_id_type=MESH,
        )
        w2_stays = pltpu.make_async_copy(w2s, w2_place, swap_recv2)

        @pl.when(me.crossing)
        def _():
            w2_swap.start()

        @pl.when(jnp.logical_not(me.crossing))
        def _():
            w2_stays.start()

        for half in range(2):
            a0 = came[2 * half, :, :LANES]
            b0 = came[2 * half, :, LANES:].astype(wide)
            a1 = pltpu.roll(came[2 * half + 1, :, :LANES].astype(wide), HEAD, 1)
            b1 = pltpu.roll(came[2 * half + 1, :, LANES:].astype(wide), HEAD, 1)
            base = half * 3 * LANES
            mixed_tok[:, base : base + LANES] = a0
            mixed_tok[:, base + LANES : base + 2 * LANES] = jnp.where(lower, b0, a1).astype(low_type)
            mixed_tok[:, base + 2 * LANES : base + 3 * LANES] = jnp.where(lower, a1, b1).astype(
                low_type
            )

        def vector(index):
            return vec_ref[index : index + 1, :]

        mix = jnp.dot(mixed_tok[...], wm[...], preferred_element_type=wide) + vector(2)
        norm1, inverse1 = normed(tok[...].astype(wide) + mix)
        early = norm1 * vector(3) + vector(4)
        mine = me.x * 2 + me.y
        halves = [slice(0, hn), slice(hn, n)]

        def send_rows(ref, h):
            place = ref.at[h, mine]
            return [copies.push(place, place, me.at(x=x, y=y)) for x, y in square]

        def send_back(ref, landing, h):
            return [
                copies.push(ref.at[h, x * 2 + y], landing.at[h, mine], me.at(x=x, y=y))
                for x, y in square
            ]

        def arrive(started):
            for copy in started:
                copy.wait_recv()

        def received(landing, h):
            return [landing[h, x * 2 + y] for x, y in square]

        early_go = []
        for h, half in enumerate(halves):
            xs[h, mine] = early[half].astype(low_type)
            early_go.append(send_rows(xs, h))
        loads[1].wait()

        def outer_weight():
            return w2p[...].reshape(quarter, depth)

        branch_go = []
        for h in range(2):
            arrive(early_go[h])
            inner = jnp.dot(
                xs[h].reshape(4 * hn, depth), w1[...], preferred_element_type=wide
            ) + vector(8)
            act, slope = gelu_and_slope(inner)
            act = act.astype(low_type)
            acts[h] = act.reshape(4, hn, quarter)
            slopes[h] = slope
            if h == 0:

                @pl.when(me.crossing)
                def _():
                    w2_swap.wait_recv()
                    w2_swap.wait_send()

                @pl.when(jnp.logical_not(me.crossing))
                def _():
                    w2_stays.wait()

                block = w2p.at[me.g, me.c]
                w2_last = [copies.push(block, block, me.sibling())]
                for copy, (_, source) in zip(w2_first, me.line()):
                    copy.wait_recv()
                    block = w2p.at[source, me.c]
                    w2_last.append(copies.push(block, block, me.sibling()))
                arrive(w2_last)
            made = jnp.dot(act, outer_weight(), preferred_element_type=wide).reshape(4, hn, depth)
            own1[h] = made
            parts[h] = made.astype(low_type)
            branch_go.append(send_back(parts, sums, h))

        grad_go, final_grads, norm_sums, cot_sums = [], [], [], []
        for h, half in enumerate(halves):
            arrive(branch_go[h])
            branch = total_of(own1[h, mine], *received(sums, h)) + vector(5)
            norm2, inverse2 = normed(early[half] + branch)
            out[half, :] = (norm2 * vector(6) + vector(7)).astype(low_type)
            cot_wide = cot[half, :].astype(wide)
            final_grad = normed_grad(cot_wide * vector(6), norm2, inverse2)
            bgs[h, mine] = final_grad.astype(low_type)
            grad_go.append(send_rows(bgs, h))
            final_grads.append(final_grad)
            norm_sums.append(down_sum(cot_wide * norm2))
            cot_sums.append(down_sum(cot_wide))
        extra[...] = jnp.zeros_like(extra)
        extra[3:4, :] = down_sum(bgs[0, mine].astype(wide)) + down_sum(bgs[1, mine].astype(wide))
        extra[4:5, :] = norm_sums[0] + norm_sums[1]
        extra[5:6, :] = cot_sums[0] + cot_sums[1]

        token_go = []
        for h in range(2):
            arrive(grad_go[h])
            grad = lax.dot_general(
                bgs[h].reshape(4 * hn, depth), outer_weight(), NEXT, preferred_element_type=wide
            )
            grad = (grad * slopes[h]).astype(low_type)
            igs[h] = grad.reshape(4, hn, quarter)
            made = lax.dot_general(grad, w1[...], NEXT, preferred_element_type=wide)
            made = made.reshape(4, hn, depth)
            own2[h] = made
            parts2[h] = made.astype(low_type)
            token_go.append(send_back(parts2, sums2, h))

        other = 1 - me.c
        grads = bgs[...].reshape(4 * n, depth)
        for half in range(2):
            span = slice(half * cut, (half + 1) * cut)
            made = lax.dot_general(
                acts[:, :, :, span].reshape(4 * n, cut), grads, DOWN, preferred_element_type=wide
            )
            g2[2 * half : 2 * half + 2] = made.astype(low_type).reshape(2, 2, e, depth)
        w2_half = copies.push(g2.at[:, other], s2, me.sibling())

        grads = igs[...].reshape(4 * n, quarter)
        bias = jnp.broadcast_to(down_sum(grads.astype(wide)), (8, quarter)).astype(low_type)
        for half in range(2):
            span = slice(half * cut, (half + 1) * cut)
            made = lax.dot_general(
                xs[:, :, :, span].reshape(4 * n, cut), grads, DOWN, preferred_element_type=wide
            ).astype(low_type)
            for index in range(16):
                place = (half, index // 8, index // 2 % GROUPS, index % 2)
                g1[(*place, slice(None, s))] = made[index * s : (index + 1) * s]
                g1[(*place, slice(s, None))] = bias
        w1_half = copies.push(g1.at[:, other], s1, me.sibling())
        w2_half.wait_recv()

        def add2(g):
            s2[g] = s2[g] + g2[g, me.c]

        loop(GROUPS, add2)
        w1_half.wait_recv()

        def add1(index):
            x, g, y = index // 8, index // 2 % GROUPS, index % 2
            s1[x, g, y] = s1[x, g, y] + g1[x, me.c, g, y]

        loop(16, add1)
        norm_sums, grad_sums, attn_sums = [], [], []
        for h, half in enumerate(halves):
            arrive(token_go[h])
            early_grad = total_of(final_grads[h], own2[h, mine], *received(sums2, h))
            norm_sums.append(down_sum(early_grad * norm1[half]))
            grad_sums.append(down_sum(early_grad))
            hidden = normed_grad(early_grad * vector(3), norm1[half], inverse1[half])
            hidden_out[half, :] = hidden
            attn[half, :] = hidden.astype(low_type)
            attn_sums.append(down_sum(hidden.astype(low_type).astype(wide)))
        extra[0:1, :] = attn_sums[0] + attn_sums[1]
        extra[1:2, :] = norm_sums[0] + norm_sums[1]
        extra[2:3, :] = grad_sums[0] + grad_sums[1]
        attn_grad = attn[...]
        back_grad = lax.dot_general(attn_grad, wm[...], NEXT, preferred_element_type=wide)
        for half in range(2):
            base = half * 3 * LANES
            t0 = back_grad[:, base : base + LANES]
            t1 = back_grad[:, base + LANES : base + 2 * LANES]
            t2 = back_grad[:, base + 2 * LANES : base + 3 * LANES]
            r1, r2 = pltpu.roll(t1, HEAD, 1), pltpu.roll(t2, HEAD, 1)
            pieces[2 * half, :, :LANES] = t0.astype(low_type)
            pieces[2 * half, :, LANES:] = jnp.where(lower, t1, 0.0).astype(low_type)
            pieces[2 * half + 1, :, :LANES] = jnp.where(lower, r1, r2).astype(low_type)
            pieces[2 * half + 1, :, LANES:] = jnp.where(lower, r2, 0.0).astype(low_type)
        onward = Scatter(on_send, on_recv, me.selfish)
        slot = me.slot()
        onward.start([(pieces.at[g], device) for g, device in readers], do_out.at[slot], slot)

        for half in range(2):
            span = slice(half * cut, (half + 1) * cut)
            made = lax.dot_general(
                mixed_tok[:, span], attn_grad, DOWN, preferred_element_type=wide
            ).astype(low_type)
            for index in range(16):
                place = (half, index // 8, index // 2 % GROUPS, index % 2)
                gm[(*place, slice(None, s))] = made[index * s : (index + 1) * s]
                gm[(*place, slice(s, None))] = extra[...].astype(low_type)
        wm_half = copies.push(gm.at[:, other], sm, me.sibling())
        wm_half.wait_recv()

        def addm(index):
            x, g, y = index // 8, index // 2 % GROUPS, index % 2
            sm[x, g, y] = sm[x, g, y] + gm[x, me.c, g, y]

        loop(16, addm)
        for index in range(GROUPS):
            onward.arrived(index, do_out.at[index])
        back.finish()
        onward.finish()
        copies.finish()

    vmem = pltpu.VMEM
    dma = pltpu.SemaphoreType.DMA
    tall = vmem((2, 4, hn, depth), low_type)
    full = vmem((2, 4, hn, depth), wide)
    high = vmem((2, 4, hn, quarter), low_type)
    tokens, cotangent, outer = [
        pltpu.with_memory_space_constraint(item, pltpu.HBM) for item in (tokens, cotangent, outer)
    ]
    return pl.pallas_call(
        body,
        name="middle_kernel",
        out_shape=(
            jax.ShapeDtypeStruct((n, depth), low_type),
            jax.ShapeDtypeStruct((n, depth), wide),
            jax.ShapeDtypeStruct((GROUPS, n, PACK), low_type),
            jax.ShapeDtypeStruct((2, GROUPS, 2, rows, depth), low_type),
            jax.ShapeDtypeStruct((2, GROUPS, 2, rows, quarter), low_type),
            jax.ShapeDtypeStruct((GROUPS, e, depth), low_type),
        ),
        in_specs=[
            pl.BlockSpec(memory_space=item)
            for item in (pl.ANY, pltpu.HBM, pltpu.HBM, pl.ANY, pl.ANY, pltpu.HBM, pl.ANY)
        ],
        out_specs=[
            pl.BlockSpec(memory_space=item) for item in (vmem, vmem, pl.ANY, vmem, vmem, vmem)
        ],
        scratch_shapes=[
            dma((48,)), dma((48,)), dma((8,)), dma((4,)), dma((4,)), dma((4,)), dma((4,)), dma, dma,
            vmem((n, depth), low_type),
            vmem((n, depth), low_type),
            vmem((e, depth), wide),
            vmem(vec.shape, wide),
            vmem((depth, depth), low_type),
            vmem((depth, quarter), low_type),
            vmem((GROUPS, 2, e, depth), low_type),
            vmem((e, depth), low_type),
            vmem((GROUPS, n, PACK), low_type),
            vmem((n, depth), low_type),
            tall, high,
            vmem((2, 4 * hn, quarter), wide),
            tall, tall, tall, high, tall, tall,
            vmem((GROUPS, n, PACK), low_type),
            vmem((8, depth), wide),
            vmem((n, depth), low_type),
            full, full,
            vmem((2, 2, GROUPS, 2, rows, quarter), low_type),
            vmem((GROUPS, 2, e, depth), low_type),
            vmem((2, 2, GROUPS, 2, rows, depth), low_type),
        ],
        compiler_params=pltpu.CompilerParams(
            collective_id=12, has_side_effects=True, vmem_limit_bytes=NEAR_LIMIT
        ),
    )(mixed, tokens, cotangent, mix, inner, outer, vec)


def tile_base(me, slot, n):
    u, v = slot // 2, slot % 2
    return ((u * 2 + me.c) * 2 * GROUPS + (v * 2 + me.p) * 2 + me.y) * n


def ends_of(lengths_ref):
    ends = [lengths_ref[0]]
    for index in range(1, lengths_ref.shape[0]):
        ends.append(ends[-1] + lengths_ref[index])
    return ends


def document_of(place, ends):
    first, last = place * 0, place * 0 + ends[-1]
    for end in ends[:-1]:
        before = end <= place
        first = jnp.where(before, end, first)
    for end in reversed(ends[:-1]):
        last = jnp.where(end <= place, last, end)
    return first, last


def turn_kernel(lengths, queries, keys, grads_in, mixed, lse, tokens, weights, sum1, sum2, summ):
    n = tokens.shape[1]
    depth = tokens.shape[-1]
    s = depth // 32
    rows = s + 8
    cut = depth // 2
    tall = sum2.shape[1]
    block = GROUPS * n
    width = WIDE + PACK
    spans = [slice(h * LANES, (h + 1) * LANES) for h in range(LOCAL)]

    def body(
        lengths_ref, q_ref, kv_ref, do_ref, mixed_ref, lse_ref, tok, w_ref, s1, s2, sm,
        dx_out, outqk, out1, out2, outm,
        send, recv, local, dx_send, dx_recv, swap_send, swap_recv, ks, kr, ps, pr,
        both, kbuf, kin, pk, dqs, grads, narrow, dxs, gk, sk, pp, fk, p1, f1, pm, fm, tm, p2,
    ):
        me = Spot()
        copies = Copies(send, recv, local)
        square = me.square()
        line = [to for to, _ in me.line()]
        readers = [device for _, device in me.readers()]
        swapped = [me.at(g=to, c=me.y, y=me.c) for to in [me.g] + line]
        barrier, expected = announce(
            [me.at(x=x, y=y) for x, y in square]
            + [me.at(g=to) for to in line]
            + readers[1:]
            + swapped[1:]
            + [me.sibling()],
            [(jnp.logical_not(me.selfish), readers[0]), (me.crossing, swapped[0])],
        )
        ends = ends_of(lengths_ref)
        lane = lax.broadcasted_iota(jnp.int32, (n, LANES), 1)
        upper = lane >= HEAD
        along = lax.broadcasted_iota(jnp.int32, (1, n), 1)
        down = lax.broadcasted_iota(jnp.int32, (block, n), 0)

        def upper_halves(ref, part):
            front = ref[part, :LANES].astype(wide)
            back = ref[part, LANES:].astype(wide)
            parts = (pltpu.roll(front, HEAD, 1), front, pltpu.roll(back, HEAD, 1))
            return [jnp.where(upper, item, 0.0) for item in parts]

        firsts, lasts, logs, deltas = [], [], [], []
        for slot in range(GROUPS):
            part = slice(slot * n, (slot + 1) * n)
            first, last = document_of(along + tile_base(me, slot, n), ends)
            firsts.append(first)
            lasts.append(last)
            outs, inputs = upper_halves(mixed_ref, part), upper_halves(do_ref, part)
            for h, span in enumerate(spans):
                base = slot * 2 * n
                both[h, base : base + n] = q_ref[part, span] * jnp.asarray(0.125, low_type)
                both[h, base + n : base + 2 * n] = inputs[h].astype(low_type)
            deltas.append([down_sum(jnp.transpose(i * o)) for i, o in zip(inputs, outs)])
            logs.append([lse_ref[slot, h : h + 1, :] for h in range(LOCAL)])
        dqs[...] = jnp.zeros_like(dqs)
        pl.semaphore_wait(barrier, expected)

        wm_push = [
            copies.push(sm.at[x, :, y], pm.at[peer], me.at(x=x, y=y))
            for peer, (x, y) in enumerate(square)
        ]
        w1_push = [
            copies.push(s1.at[:, to, :], p1.at[slot], me.at(g=to)) for slot, to in enumerate(line)
        ]
        w2_push = [
            copies.push(s2.at[to], p2.at[index + 1], swapped[index + 1])
            for index, to in enumerate(line)
        ]
        exchanged = pltpu.make_async_remote_copy(
            src_ref=s2.at[me.g],
            dst_ref=p2.at[0],
            send_sem=swap_send,
            recv_sem=swap_recv,
            device_id=swapped[0],
            device_id_type=MESH,
        )
        stays = pltpu.make_async_copy(s2.at[me.g], p2.at[0], swap_recv)

        @pl.when(me.crossing)
        def _():
            exchanged.start()

        @pl.when(jnp.logical_not(me.crossing))
        def _():
            stays.start()

        other = 1 - me.c

        def attend(u, c, v, target):
            begin = pl.multiple_of(((u * 2 + c) * 2 + v) * block, block)
            place = down + begin
            same = [(place >= first) & (place < last) for first, last in zip(firsts, lasts)]
            for h, span in enumerate(spans):
                kv = kv_ref[pl.ds(begin, block), span]
                made = lax.dot_general(kv, both[h], NEXT, preferred_element_type=wide)
                pairs = []
                for slot in range(GROUPS):
                    base = slot * 2 * n
                    scores = jnp.where(same[slot], made[:, base : base + n], mask_fill)
                    probs = jnp.exp(scores - logs[slot][h])
                    dots = made[:, base + n : base + 2 * n]
                    score_grad = (probs * (dots - deltas[slot][h])).astype(low_type)
                    pairs += [score_grad, probs.astype(low_type)]
                    dqs[slot, :, span] += lax.dot_general(
                        score_grad, kv, DOWN, preferred_element_type=wide
                    )
                made = jnp.dot(
                    jnp.concatenate(pairs, axis=1), both[h], preferred_element_type=wide
                )
                target[:, :, :, span] = made.astype(low_type).reshape(2, 2, n, LANES)

        def to_sibling(turn):
            return pltpu.make_async_remote_copy(
                src_ref=kbuf.at[0, turn],
                dst_ref=kin.at[turn],
                send_sem=ks.at[turn],
                recv_sem=kr.at[turn],
                device_id=me.sibling(),
                device_id_type=MESH,
            )

        def to_peer(turn, peer):
            x, y = square[peer]
            return pltpu.make_async_remote_copy(
                src_ref=kbuf.at[1, turn, (x + me.c) % 2, y],
                dst_ref=pk.at[turn, peer],
                send_sem=ps.at[turn * 3 + peer],
                recv_sem=pr.at[turn * 3 + peer],
                device_id=me.at(x=x, y=y),
                device_id_type=MESH,
            )

        def key_turn(turn):
            u, v = turn % 2, (me.half + turn // 2) % 2

            def of_core(index):
                attend(u, jnp.where(index == 0, other, me.c), v, kbuf.at[index, turn])

                @pl.when(index == 0)
                def _():
                    to_sibling(turn).start()

            loop(2, of_core)
            to_sibling(turn).wait_recv()
            for p in range(2):
                for y in range(2):
                    kbuf[1, turn, p, y] = kbuf[1, turn, p, y] + kin[turn, p, y]
            for peer in range(3):
                to_peer(turn, peer).start()

        loop(4, key_turn)

        def square_push(total, landing):
            return [
                copies.push(total.at[x, :, y], landing.at[slot], me.at(x=x, y=y))
                for slot, (x, y) in enumerate(square)
            ]

        def square_sum(result, total, landed):
            def add(g):
                result[g] = total_of(
                    total[me.x, g, me.y], landed[0, g], landed[1, g], landed[2, g]
                ).astype(low_type)

            loop(GROUPS, add)

        moves = []
        for turn in range(4):
            u, dv = turn % 2, turn // 2
            v = (me.half + dv) % 2
            slot = u * 2 + v
            wides = [dqs[slot, :, span] * 0.125 for span in spans]
            for h, span in enumerate(spans):
                grads[slot, :, WIDE + span.start : WIDE + span.stop] = jnp.where(
                    upper, 0.0, wides[h]
                ).astype(low_type)
            narrow[slot, :, WIDE : WIDE + LANES] = jnp.where(
                upper, pltpu.roll(wides[1], HEAD, 1), wides[0]
            ).astype(low_type)
            narrow[slot, :, WIDE + LANES :] = jnp.where(upper, 0.0, wides[2]).astype(low_type)
            for peer in range(3):
                to_peer(turn, peer).wait_recv()
            here = total_of(
                kbuf[1, turn, me.p, me.y], *[pk[turn, peer] for peer in range(3)]
            ).astype(low_type)
            grads[slot, :, :WIDE] = here
            narrow[slot, :, :WIDE] = here
            dxs[slot] = lax.dot_general(
                grads[slot], w_ref[:, : 2 * WIDE], NEXT, preferred_element_type=wide
            ).astype(low_type)
            copy = pltpu.make_async_remote_copy(
                src_ref=dxs.at[slot],
                dst_ref=dx_out.at[me.g],
                send_sem=dx_send.at[turn],
                recv_sem=dx_recv.at[me.g],
                device_id=me.at(x=u, g=2 * v + me.p),
                device_id_type=MESH,
            )
            if dv:
                copy.start()
                moves.append((copy, None))
                continue
            stay = pltpu.make_async_copy(dxs.at[slot], dx_out.at[me.g], dx_recv.at[me.g])
            at_home = me.selfish & (me.x == u)
            away = jnp.logical_not(at_home)
            moves.append((copy, away))

            @pl.when(at_home)
            def _(stay=stay):
                stay.start()

            @pl.when(away)
            def _(copy=copy):
                copy.start()

        values = narrow[...].reshape(GROUPS * n, width)
        bias = jnp.broadcast_to(down_sum(values.astype(wide)), (8, width)).astype(low_type)
        for half in range(2):
            made = lax.dot_general(
                tok[:, :, half * cut : (half + 1) * cut].reshape(GROUPS * n, cut),
                values,
                DOWN,
                preferred_element_type=wide,
            ).astype(low_type)
            for index in range(16):
                place = (half, index // 8, index // 2 % GROUPS, index % 2)
                gk[(*place, slice(None, s))] = made[index * s : (index + 1) * s]
                gk[(*place, slice(s, None))] = bias
        g_half = copies.push(gk.at[:, other], sk, me.sibling())

        for copy in wm_push:
            copy.wait_recv()
        square_sum(fm, sm, pm)
        wm_last = [
            copies.push(fm.at[to], tm.at[peer], me.at(g=to)) for peer, to in enumerate(line)
        ]
        for copy in w1_push:
            copy.wait_recv()

        def addw(index):
            x, y = index // 2, index % 2
            f1[x, y] = total_of(s1[x, me.g, y], *[p1[peer, x, y] for peer in range(3)]).astype(
                low_type
            )

        loop(4, addw)
        quarter = out1.at[me.x * 2 + me.y]
        g_half.wait_recv()

        def pair_sum(index):
            x, g, y = index // 8, index // 2 % GROUPS, index % 2
            sk[x, g, y] = sk[x, g, y] + gk[x, me.c, g, y]

        loop(16, pair_sum)
        push = square_push(sk, pp)
        arrivals = [copies.push(f1.at[x, y], quarter, me.at(x=x, y=y)) for x, y in square]
        kept = [copies.keep(f1.at[me.x, me.y], quarter)]

        @pl.when(me.crossing)
        def _():
            exchanged.wait_recv()
            exchanged.wait_send()

        @pl.when(jnp.logical_not(me.crossing))
        def _():
            stays.wait()

        for copy in w2_push:
            copy.wait_recv()
        out2[...] = total_of(*[p2[index] for index in range(4)])
        for copy in push:
            copy.wait_recv()
        square_sum(fk, sk, pp)
        arrivals += [copies.push(fk.at[to], outqk.at[me.g], me.at(g=to)) for to in line]
        kept.append(copies.keep(fk.at[me.g], outqk.at[me.g]))
        for copy in wm_last:
            copy.wait_recv()
        outm[...] = total_of(fm[me.g], *[tm[peer] for peer in range(3)])
        for copy in arrivals:
            copy.wait_recv()
        for g in range(GROUPS):
            pltpu.make_async_copy(dx_out.at[g], dx_out.at[g], dx_recv.at[g]).wait()
        for copy in kept:
            copy.wait()
        for copy, away in moves:
            if away is None:
                copy.wait_send()
                continue

            @pl.when(away)
            def _(copy=copy):
                copy.wait_send()

        for turn in range(4):
            to_sibling(turn).wait_send()
            for peer in range(3):
                to_peer(turn, peer).wait_send()
        copies.finish()

    vmem = pltpu.VMEM
    dma = pltpu.SemaphoreType.DMA
    total = 40
    return pl.pallas_call(
        body,
        name="turn_kernel",
        out_shape=(
            jax.ShapeDtypeStruct((GROUPS, n, depth), low_type),
            jax.ShapeDtypeStruct((GROUPS, rows, width), low_type),
            jax.ShapeDtypeStruct((4, rows, depth), low_type),
            jax.ShapeDtypeStruct((tall, depth), wide),
            jax.ShapeDtypeStruct((rows, depth), wide),
        ),
        in_specs=[pl.BlockSpec(memory_space=pltpu.SMEM)] + [pl.BlockSpec(memory_space=vmem)] * 10,
        out_specs=[pl.BlockSpec(memory_space=pl.ANY)] * 3 + [pl.BlockSpec(memory_space=vmem)] * 2,
        scratch_shapes=[
            dma((total,)), dma((total,)), dma((4,)), dma((4,)), dma((4,)), dma, dma,
            dma((4,)), dma((4,)), dma((12,)), dma((12,)),
            vmem((LOCAL, 2 * block, LANES), low_type),
            vmem((2, 4, 2, 2, n, WIDE), low_type),
            vmem((4, 2, 2, n, WIDE), low_type),
            vmem((4, 3, n, WIDE), low_type),
            vmem((GROUPS, n, WIDE), wide),
            vmem((GROUPS, n, 2 * WIDE), low_type),
            vmem((GROUPS, n, width), low_type),
            vmem((GROUPS, n, depth), low_type),
            vmem((2, 2, GROUPS, 2, rows, width), low_type),
            vmem((2, GROUPS, 2, rows, width), low_type),
            vmem((3, GROUPS, rows, width), low_type),
            vmem((GROUPS, rows, width), low_type),
            vmem((3, 2, 2, rows, depth), low_type),
            vmem((2, 2, rows, depth), low_type),
            vmem((3, GROUPS, rows, depth), low_type),
            vmem((GROUPS, rows, depth), low_type),
            vmem((3, rows, depth), low_type),
            vmem((4, tall, depth), low_type),
        ],
        compiler_params=pltpu.CompilerParams(
            collective_id=11, has_side_effects=True, vmem_limit_bytes=TURN_LIMIT
        ),
    )(lengths, queries, keys, grads_in, mixed, lse, tokens, weights, sum1, sum2, summ)


def on_device_general(
    tokens,
    cotangent,
    doc_lengths,
    query_weight,
    query_bias,
    key_weight,
    value_weight,
    value_bias,
    mix_weight,
    mix_bias,
    early_gain,
    early_shift,
    inner_weight,
    inner_bias,
    outer_weight,
    outer_bias,
    final_gain,
    final_shift,
):
    n, depth = tokens.shape
    groups, cycle = lax.axis_size("au"), lax.axis_size("row")
    devices = groups * cycle
    zs = cycle // (2 * GROUPS)
    s = query_weight.shape[0]
    ff = inner_weight.shape[1]
    quarter = ff // 4
    e = outer_weight.shape[0]
    rows = GROUPS * n
    total_tokens = n * devices
    me = Place(zs)
    device = lax.axis_index("au") * cycle + lax.axis_index("row")
    w_me = me.x * 2 + me.y

    def by_head(weight):
        return weight.astype(low_type).reshape(-1, GROUPS, LOCAL, HEAD)

    def packed(query, key, value):
        kv = jnp.stack([key, value], axis=3).reshape(-1, GROUPS, WIDE)
        q = jnp.pad(query, ((0, 0), (0, 0), (0, 0), (0, HEAD))).reshape(-1, GROUPS, WIDE)
        return jnp.concatenate([kv, q], axis=2)

    slab = packed(by_head(query_weight), by_head(key_weight), by_head(value_weight))
    slab = jnp.transpose(slab, (1, 0, 2))
    small = jnp.concatenate(
        [
            vector.astype(low_type)
            for vector in (
                query_bias, value_bias, mix_bias, early_gain, early_shift,
                outer_bias, final_gain, final_shift, inner_bias,
            )
        ]
    )
    extra = -s % 8 or 8
    small = jnp.broadcast_to(
        jnp.pad(small, (0, 2 * WIDE - small.shape[0]))[None, None], (GROUPS, extra, 2 * WIDE)
    )
    slab = jnp.concatenate([slab, small], axis=1)
    tok_all, w_all = spread_tokens(zs, tokens, slab)
    tok_all = tok_all.reshape(rows, depth)
    w_qkv = w_all[..., :s, :].reshape(depth, 2 * WIDE)
    small = w_all[..., s, :].reshape(devices, 2 * WIDE)
    names = [small[:, i * s : (i + 1) * s].reshape(depth) for i in range(8)]
    q_bias, v_bias, m_bias, e_gain, e_shift, o_bias, f_gain, f_shift = names
    i_bias = small[:, 8 * s : 8 * s + e].reshape(4, quarter)[w_me].astype(wide)
    q_bias = q_bias.reshape(1, GROUPS, LOCAL, HEAD)
    v_bias = v_bias.reshape(1, GROUPS, LOCAL, HEAD)
    bias = packed(q_bias, jnp.zeros_like(q_bias), v_bias)[0, me.g].astype(wide)

    qkv = (jnp.dot(tok_all, w_qkv, preferred_element_type=wide) + bias).astype(low_type)
    queries = qkv[:, WIDE:]

    inner_slab = jnp.transpose(inner_weight.astype(low_type).reshape(s, 4, quarter), (1, 0, 2))
    kv_all, w1, w2, wm = spread_keys(
        zs,
        qkv[:, :WIDE].reshape(GROUPS, n, WIDE),
        inner_slab,
        outer_weight.astype(low_type),
        mix_weight.astype(low_type),
    )
    kv_all = kv_all.reshape(total_tokens, WIDE)
    w1 = w1.reshape(depth, quarter)
    w2 = w2.reshape(quarter, depth)
    wm = wm.reshape(depth, depth)

    tile, block = 128, 512
    count = doc_lengths.shape[0]
    upto = jnp.arange(count)[None, :] <= jnp.arange(count)[:, None]
    ends = jnp.sum(jnp.where(upto, doc_lengths[None, :], 0), axis=1)
    owners = ((me.x * 2 + me.c) * cycle + me.z * GROUPS * 2 + jnp.arange(GROUPS) * 2 + me.y) * n
    places = (owners[:, None] + jnp.arange(n)[None, :]).reshape(rows)
    before = ends[None, :] <= places[:, None]
    first = jnp.max(jnp.where(before, ends[None, :], 0), axis=1).astype(jnp.int32)
    last = jnp.min(jnp.where(before, total_tokens, ends[None, :]), axis=1).astype(jnp.int32)
    tiles = rows // tile
    bounds = jnp.stack(
        [
            first.reshape(tiles, tile)[:, 0] // block,
            (last.reshape(tiles, tile)[:, -1] + block - 1) // block,
        ],
        axis=1,
    )
    mixed, mixed_wide, lse = attend_forward(
        queries, kv_all, bounds, first[:, None], last[:, None], tile, block
    )
    mixed_tok = exchange_line(zs, 2, mixed.reshape(GROUPS, n, PACK))
    mixed_tok = jnp.transpose(mixed_tok[:, :, : LOCAL * HEAD], (1, 0, 2)).reshape(n, depth)

    attn = jnp.dot(mixed_tok, wm, preferred_element_type=wide) + m_bias.astype(wide)
    early, early_pull = jax.vjp(
        layer_norm, tokens.astype(wide) + attn, e_gain.astype(wide), e_shift.astype(wide)
    )
    early_all = gather_square(zs, 3, early.astype(low_type)).reshape(rows, depth)
    inner = jnp.dot(early_all, w1, preferred_element_type=wide) + i_bias
    act, gelu_pull = jax.vjp(gelu_exact, inner)
    act_low = act.astype(low_type)
    partial = jnp.dot(act_low, w2, preferred_element_type=wide).astype(low_type)
    partial = exchange_square(zs, 4, partial.reshape(2, 2, n, depth))
    branch = jnp.sum(partial.astype(wide), axis=(0, 1)) + o_bias.astype(wide)
    result, final_pull = jax.vjp(
        layer_norm, early + branch, f_gain.astype(wide), f_shift.astype(wide)
    )
    output = result.astype(low_type)
    final_grads = final_pull(cotangent.astype(wide))
    branch_grad = final_grads[0].astype(low_type)
    outer_bias_grad = jnp.sum(branch_grad.astype(wide), axis=0)
    branch_all = gather_square(zs, 5, branch_grad).reshape(rows, depth)
    act_grad = jnp.einsum("td,fd->tf", branch_all, w2, preferred_element_type=wide)
    inner_grad = gelu_pull(act_grad)[0].astype(low_type)
    partial = jnp.einsum("tf,df->td", inner_grad, w1, preferred_element_type=wide).astype(low_type)
    partial = exchange_square(zs, 6, partial.reshape(2, 2, n, depth))
    grad2 = jnp.einsum("tf,td->fd", act_low, branch_all, preferred_element_type=wide)
    grad1 = jnp.einsum("td,tf->df", early_all, inner_grad, preferred_element_type=wide)
    inner_bias_grad = jnp.sum(inner_grad.astype(wide), axis=0)
    early_grad = final_grads[0] + jnp.sum(partial.astype(wide), axis=(0, 1))
    early_grads = early_pull(early_grad)
    attn_grad = early_grads[0].astype(low_type)
    mixed_grad = jnp.einsum("td,cd->tc", attn_grad, wm, preferred_element_type=wide)
    mixed_grad = jnp.transpose(
        mixed_grad.astype(low_type).reshape(n, GROUPS, LOCAL * HEAD), (1, 0, 2)
    )
    mixed_grad = jnp.pad(mixed_grad, ((0, 0), (0, 0), (0, PACK - LOCAL * HEAD)))
    grad_all = exchange_line(zs, 7, mixed_grad).reshape(rows, PACK)
    gradm = jnp.einsum("tc,td->cd", mixed_tok, attn_grad, preferred_element_type=wide)
    mix_bias_grad = jnp.sum(attn_grad.astype(wide), axis=0)

    delta = jnp.sum(
        (grad_all.astype(wide) * mixed_wide)[:, : LOCAL * HEAD].reshape(rows, LOCAL, HEAD), axis=2
    )

    def as_stat(values):
        return jnp.transpose(values.reshape(tiles, tile, LOCAL), (0, 2, 1))

    def same_stat(values):
        return jnp.broadcast_to(
            values.astype(wide).reshape(tiles, 1, tile), (tiles, LOCAL, tile)
        )

    stats = jnp.stack(
        [same_stat(first), same_stat(last), as_stat(lse[:, :LOCAL]), as_stat(delta)], axis=2
    )
    stats = jnp.pad(stats, ((0, 0), (0, 0), (0, 4), (0, 0)))
    query_grad, dkv = attend_backward(queries, kv_all, grad_all, stats, bounds, tile, block)

    def slabs(grad, extras):
        grad = grad.astype(low_type).reshape(devices, s, -1)
        rest = -s % 8
        rest += 0 if rest >= extras.shape[0] else 8
        extras = jnp.concatenate(
            [extras.astype(low_type), jnp.zeros((rest - extras.shape[0], extras.shape[1]), low_type)]
        )
        extras = jnp.broadcast_to(extras[None], (devices,) + extras.shape)
        return jnp.concatenate([grad, extras], axis=1).reshape(2, 2, zs, GROUPS, 2, s + rest, -1)

    mix_extras = jnp.stack(
        [
            mix_bias_grad, early_grads[1], early_grads[2],
            outer_bias_grad, final_grads[1], final_grads[2],
        ]
    )
    dkv, out1, out2, outm = reduce_keys(
        zs,
        dkv.reshape(2, 2, zs, GROUPS, 2, n, WIDE),
        slabs(grad1, inner_bias_grad[None]),
        grad2.astype(low_type).reshape(zs, GROUPS, 2, e, depth),
        slabs(gradm, mix_extras),
    )
    key_grad = jnp.sum(dkv.astype(wide), axis=0).astype(low_type).reshape(rows, WIDE)
    grads = jnp.concatenate([key_grad, query_grad], axis=1)
    gradq = jnp.einsum("tc,td->cd", tok_all, grads, preferred_element_type=wide)
    bias_grad = jnp.sum(grads.astype(wide), axis=0)
    partial = jnp.einsum("td,cd->tc", grads, w_qkv, preferred_element_type=wide).astype(low_type)
    partial, outq = reduce_tokens(
        zs, partial.reshape(GROUPS, n, depth), slabs(gradq, bias_grad[None])
    )
    input_grad = early_grads[0] + jnp.sum(partial.astype(wide), axis=0)

    def own(vector, count):
        return lax.dynamic_slice_in_dim(vector, device * count, count, 0).astype(wide)

    outq = outq.astype(wide)
    kv_out = outq[:, :, :WIDE].reshape(GROUPS, -1, LOCAL, 2, HEAD)
    q_out = outq[:, :, WIDE:].reshape(GROUPS, -1, LOCAL, 2, HEAD)[:, :, :, 0]

    def unpacked(values):
        return jnp.transpose(values, (1, 0, 2, 3)).reshape(-1, depth)

    q_out, k_out, v_out = unpacked(q_out), unpacked(kv_out[:, :, :, 0]), unpacked(kv_out[:, :, :, 1])
    inner_out = jnp.transpose(out1[:, :s], (1, 0, 2)).reshape(s, ff).astype(wide)
    return (
        output,
        input_grad.astype(low_type),
        q_out[:s],
        own(q_out[s], s),
        k_out[:s],
        v_out[:s],
        own(v_out[s], s),
        outm[:s],
        own(outm[s], s),
        own(outm[s + 1], s),
        own(outm[s + 2], s),
        inner_out,
        own(out1[:, s].reshape(ff), e),
        out2,
        own(outm[s + 3], s),
        own(outm[s + 4], s),
        own(outm[s + 5], s),
    )


def on_device(
    tokens,
    cotangent,
    doc_lengths,
    query_weight,
    query_bias,
    key_weight,
    value_weight,
    value_bias,
    mix_weight,
    mix_bias,
    early_gain,
    early_shift,
    inner_weight,
    inner_bias,
    outer_weight,
    outer_bias,
    final_gain,
    final_shift,
):
    n, depth = tokens.shape
    cycle = lax.axis_size("row")
    devices = lax.axis_size("au") * cycle
    s = query_weight.shape[0]
    ff = inner_weight.shape[1]
    quarter = ff // 4
    e = outer_weight.shape[0]
    rows = GROUPS * n
    total_tokens = n * devices
    me = Spot()
    vectors = [
        vector.reshape(1, -1)
        for vector in (
            query_bias, value_bias, mix_bias, early_gain, early_shift,
            outer_bias, final_gain, final_shift,
        )
    ]
    vectors.append(inner_bias.reshape(1, -1))
    toks, queries, w_qkv, vec, kv_all, w1, wm, mixed, mixed_wide, lse = first_kernel(
        doc_lengths, tokens, query_weight, key_weight, value_weight, vectors,
        inner_weight, mix_weight, e,
    )
    queries = queries.reshape(rows, WIDE)
    kv_all = kv_all.reshape(total_tokens, WIDE)
    w_qkv = w_qkv.reshape(depth, -1)
    w1 = w1.reshape(depth, quarter)
    wm = wm.reshape(depth, depth)
    output, hidden_grad, grad_all, summ, sum1, sum2 = middle_kernel(
        mixed.reshape(GROUPS, n, PACK), tokens, cotangent, wm, w1, outer_weight, vec, s, e
    )
    grad_all = grad_all.reshape(rows, PACK)
    pieces, outqk, out1, out2, outm = turn_kernel(
        doc_lengths, queries, kv_all, grad_all, mixed_wide, lse, toks, w_qkv, sum1, sum2, summ
    )
    results = final_kernel(hidden_grad, pieces, outqk, out1, out2, outm, s, e)
    return (output,) + tuple(
        result.reshape(-1) if result.shape[0] == 1 else result for result in results
    )


def solution(mesh):
    both = P(("au", "row"), None)
    flat = P(("au", "row"))
    in_specs = (
        both, both, P(), both, flat, both, both, flat, both, flat, flat, flat,
        both, flat, both, flat, flat, flat,
    )
    out_specs = (
        both, both, both, flat, both, both, flat, both, flat, flat, flat,
        both, flat, both, flat, flat, flat,
    )
    fast = mesh.shape["au"] == 4 and mesh.shape["row"] == 2 * GROUPS
    return jax.shard_map(
        on_device if fast else on_device_general, mesh=mesh, in_specs=in_specs, out_specs=out_specs, check_vma=False
    )
```

```python
import functools

import jax
import jax.numpy as jnp
import numpy as np
from jax import lax
from jax.experimental import pallas as pl
from jax.experimental.pallas import tpu as pltpu
from jax.sharding import PartitionSpec as P

HEAD = 64
HEADS = 12
GROUPS = 4
LOCAL = HEADS // GROUPS
LANES = 2 * HEAD
WIDE = LOCAL * LANES
PACK = 256
eps_norm = 1e-06
mask_fill = -1000000000.0
lowest_start = -1e30
low_type = jnp.bfloat16
wide = jnp.float32
MESH = pl.DeviceIdType.MESH
VMEM_LIMIT = 62 * 1024 * 1024
NEAR_LIMIT = 30 * 1024 * 1024
TURN_LIMIT = 48 * 1024 * 1024


def layer_norm(hidden, gain, shift):
    mean = jnp.mean(hidden, axis=-1, keepdims=True)
    centered = hidden - mean
    spread = jnp.mean(centered * centered, axis=-1, keepdims=True)
    return centered * lax.rsqrt(spread + eps_norm) * gain + shift


def gelu_exact(values):
    return jax.nn.gelu(values, approximate=False)


class Place:
    def __init__(self, zs):
        self.zs = zs
        a = lax.axis_index("au")
        r = lax.axis_index("row")
        self.x, self.c = a // 2, a % 2
        self.y, q = r % 2, r // 2
        self.g, self.z = q % GROUPS, q // GROUPS

    def at(self, x=None, c=None, z=None, g=None, y=None):
        x = self.x if x is None else x
        c = self.c if c is None else c
        z = self.z if z is None else z
        g = self.g if g is None else g
        y = self.y if y is None else y
        return (x * 2 + c, (z * GROUPS + g) * 2 + y)

    def sibling(self):
        return self.at(c=1 - self.c)

    def line(self):
        return [((self.g + k) % GROUPS, (self.g + GROUPS - k) % GROUPS) for k in range(1, GROUPS)]

    def column(self):
        count = self.zs * GROUPS
        q = self.z * GROUPS + self.g
        result = []
        for k in range(1, count):
            to, source = (q + k) % count, (q + count - k) % count
            result.append(((to // GROUPS, to % GROUPS), (source // GROUPS, source % GROUPS)))
        return result

    def plane(self, everywhere=True):
        result = []
        for dx in range(2):
            for dy in range(2):
                for dz in range(self.zs if everywhere else 1):
                    if dx + dy + dz == 0:
                        continue
                    to = ((self.x + dx) % 2, (self.z + dz) % self.zs, (self.y + dy) % 2)
                    source = (
                        (self.x + dx) % 2,
                        (self.z + self.zs - dz) % self.zs,
                        (self.y + dy) % 2,
                    )
                    result.append((to, source))
        return result


class Copies:
    def __init__(self, send, recv, local):
        self.send, self.recv, self.local = send, recv, local
        self.count = 0
        self.local_count = 0
        self.started = []
        self.local_started = []

    def push(self, source, target, device):
        copy = pltpu.make_async_remote_copy(
            src_ref=source,
            dst_ref=target,
            send_sem=self.send.at[self.count],
            recv_sem=self.recv.at[self.count],
            device_id=device,
            device_id_type=MESH,
        )
        self.count += 1
        copy.start()
        self.started.append(copy)
        return copy

    def keep(self, source, target):
        copy = pltpu.make_async_copy(source, target, self.local.at[self.local_count])
        self.local_count += 1
        copy.start()
        return copy

    def finish(self):
        for copy in self.started:
            copy.wait_send()


def greet(devices, partner=None, crossing=None):
    barrier = pltpu.get_barrier_semaphore()
    for device in devices:
        pl.semaphore_signal(barrier, inc=1, device_id=device, device_id_type=MESH)
    if partner is None:
        pl.semaphore_wait(barrier, len(devices))
        return

    @pl.when(crossing)
    def _():
        pl.semaphore_signal(barrier, inc=1, device_id=partner, device_id_type=MESH)
        pl.semaphore_wait(barrier, len(devices) + 1)

    @pl.when(jnp.logical_not(crossing))
    def _():
        pl.semaphore_wait(barrier, len(devices))


def comm_call(body, name, ident, outs, copies, locals_, args, spaces=None, out_spaces=None, scratch=()):
    spaces = [pl.ANY] * len(args) if spaces is None else spaces
    out_spaces = [pl.ANY] * len(outs) if out_spaces is None else out_spaces
    return pl.pallas_call(
        body,
        name=name,
        out_shape=tuple(outs),
        in_specs=[pl.BlockSpec(memory_space=space) for space in spaces],
        out_specs=tuple(pl.BlockSpec(memory_space=space) for space in out_spaces),
        scratch_shapes=[
            pltpu.SemaphoreType.DMA((max(copies, 1),)),
            pltpu.SemaphoreType.DMA((max(copies, 1),)),
            pltpu.SemaphoreType.DMA((max(locals_, 1),)),
            *scratch,
        ],
        compiler_params=pltpu.CompilerParams(
            collective_id=ident, has_side_effects=True, vmem_limit_bytes=VMEM_LIMIT
        ),
    )(*args)


def spread_tokens(zs, tokens, slab):
    n, width = tokens.shape
    groups, rows, columns = slab.shape
    plane = 4 * zs - 1

    def body(tok, piece, tok_all, w_all, send, recv, local):
        me = Place(zs)
        copies = Copies(send, recv, local)
        greet(
            [me.at(g=to) for to, _ in me.line()]
            + [me.at(x=to[0], z=to[1], y=to[2]) for to, _ in me.plane()]
            + [me.sibling()]
        )
        first = [
            copies.push(
                piece.at[to], w_all.at[me.x, me.c, me.z, me.g, me.y], me.at(g=to)
            )
            for to, _ in me.line()
        ]
        own = copies.keep(piece.at[me.g], w_all.at[me.x, me.c, me.z, me.g, me.y])
        arrivals = [copies.push(tok, tok_all.at[me.g], me.at(g=to)) for to, _ in me.line()]
        mine = copies.keep(tok, tok_all.at[me.g])
        own.wait()
        for copy in first:
            copy.wait_recv()
        block = w_all.at[me.x, me.c, me.z, :, me.y]
        second = [
            copies.push(block, block, me.at(x=to[0], z=to[1], y=to[2])) for to, _ in me.plane()
        ]
        arrivals.append(copies.push(block, block, me.sibling()))
        for copy, (_, source) in zip(second, me.plane()):
            copy.wait_recv()
            part = w_all.at[source[0], me.c, source[1], :, source[2]]
            arrivals.append(copies.push(part, part, me.sibling()))
        for copy in arrivals:
            copy.wait_recv()
        mine.wait()
        copies.finish()

    return comm_call(
        body,
        "spread_tokens",
        0,
        [
            jax.ShapeDtypeStruct((GROUPS, n, width), low_type),
            jax.ShapeDtypeStruct((2, 2, zs, GROUPS, 2, rows, columns), low_type),
        ],
        2 * (GROUPS - 1) + 2 * plane + 1,
        2,
        (tokens, slab),
    )


def spread_keys(zs, keys, inner, outer, mix):
    groups, n, width = keys.shape
    quarters, rows, columns = inner.shape
    tall, _ = outer.shape
    plane, column = 4 * zs - 1, GROUPS * zs - 1

    def body(kv, w1s, w2s, wms, kv_all, w1, w2, wm, send, recv, local, swap_send, swap_recv):
        me = Place(zs)
        copies = Copies(send, recv, local)
        crossing = me.c != me.y
        greet(
            [me.at(x=to[0], z=to[1], y=to[2]) for to, _ in me.plane()]
            + [me.at(z=to[0], g=to[1]) for to, _ in me.column()]
            + [me.at(z=to[0], g=to[1], c=me.y, y=me.c) for to, _ in me.column()]
            + [me.sibling()],
            me.at(c=me.y, y=me.c),
            crossing,
        )

        def here(ref):
            return ref.at[me.x, me.c, me.z, me.g, me.y]

        flat = me.plane(everywhere=False)
        own = [
            copies.keep(w1s.at[me.x * 2 + me.y], here(w1)),
            copies.keep(wms, here(wm)),
            copies.keep(kv, kv_all.at[me.x, me.c, me.z, :, me.y]),
        ]
        w1_first = [
            copies.push(w1s.at[to[0] * 2 + to[2]], here(w1), me.at(x=to[0], y=to[2]))
            for to, _ in flat
        ]
        wm_first = [
            copies.push(wms, here(wm), me.at(z=to[0], g=to[1])) for to, _ in me.column()
        ]
        mine = kv_all.at[me.x, me.c, me.z, :, me.y]
        kv_first = [
            copies.push(kv, mine, me.at(x=to[0], z=to[1], y=to[2])) for to, _ in me.plane()
        ]
        arrivals = [copies.push(kv, mine, me.sibling())]
        w2_first = [
            copies.push(
                w2s, w2.at[me.z, me.g, me.y], me.at(z=to[0], g=to[1], c=me.y, y=me.c)
            )
            for to, _ in me.column()
        ]
        exchanged = pltpu.make_async_remote_copy(
            src_ref=w2s,
            dst_ref=w2.at[me.z, me.g, me.y],
            send_sem=swap_send,
            recv_sem=swap_recv,
            device_id=me.at(c=me.y, y=me.c),
            device_id_type=MESH,
        )
        stays = pltpu.make_async_copy(w2s, w2.at[me.z, me.g, me.y], swap_recv)

        @pl.when(crossing)
        def _():
            exchanged.start()

        @pl.when(jnp.logical_not(crossing))
        def _():
            stays.start()

        own[0].wait()
        for copy in w1_first:
            copy.wait_recv()
        block = w1.at[:, me.c, me.z, me.g, :]
        w1_second = [
            copies.push(block, block, me.at(z=to[0], g=to[1])) for to, _ in me.column()
        ]
        arrivals.append(copies.push(block, block, me.sibling()))
        own[1].wait()
        for copy in wm_first:
            copy.wait_recv()
        block = wm.at[me.x, me.c, :, :, me.y]
        wm_second = [copies.push(block, block, me.at(x=to[0], y=to[2])) for to, _ in flat]
        arrivals.append(copies.push(block, block, me.sibling()))
        for copy, (_, source) in zip(kv_first, me.plane()):
            copy.wait_recv()
            part = kv_all.at[source[0], me.c, source[1], :, source[2]]
            arrivals.append(copies.push(part, part, me.sibling()))

        @pl.when(crossing)
        def _():
            exchanged.wait_recv()
            exchanged.wait_send()

        @pl.when(jnp.logical_not(crossing))
        def _():
            stays.wait()

        part = w2.at[me.z, me.g, me.c]
        arrivals.append(copies.push(part, part, me.sibling()))
        for copy, (_, source) in zip(wm_second, flat):
            copy.wait_recv()
            part = wm.at[source[0], me.c, :, :, source[2]]
            arrivals.append(copies.push(part, part, me.sibling()))
        for copy, (_, source) in zip(w2_first, me.column()):
            copy.wait_recv()
            part = w2.at[source[0], source[1], me.c]
            arrivals.append(copies.push(part, part, me.sibling()))
        for copy, (_, source) in zip(w1_second, me.column()):
            copy.wait_recv()
            part = w1.at[:, me.c, source[0], source[1], :]
            arrivals.append(copies.push(part, part, me.sibling()))
        for copy in arrivals:
            copy.wait_recv()
        own[2].wait()
        copies.finish()

    return comm_call(
        body,
        "spread_keys",
        1,
        [
            jax.ShapeDtypeStruct((2, 2, zs, GROUPS, 2, n, width), low_type),
            jax.ShapeDtypeStruct((2, 2, zs, GROUPS, 2, rows, columns), low_type),
            jax.ShapeDtypeStruct((zs, GROUPS, 2, tall, columns), low_type),
            jax.ShapeDtypeStruct((2, 2, zs, GROUPS, 2) + mix.shape, low_type),
        ],
        2 * plane + 1 + 2 * (3 + column + 1 + column) + column + 3 + 8,
        3,
        (keys, inner, outer, mix),
        scratch=(pltpu.SemaphoreType.DMA, pltpu.SemaphoreType.DMA),
    )


def exchange_line(zs, ident, pieces):
    def body(source, target, send, recv, local):
        me = Place(zs)
        copies = Copies(send, recv, local)
        greet([me.at(g=to) for to, _ in me.line()])
        arrivals = [
            copies.push(source.at[to], target.at[me.g], me.at(g=to)) for to, _ in me.line()
        ]
        own = copies.keep(source.at[me.g], target.at[me.g])
        for copy in arrivals:
            copy.wait_recv()
        own.wait()
        copies.finish()

    return comm_call(
        body,
        "exchange_line",
        ident,
        [jax.ShapeDtypeStruct(pieces.shape, pieces.dtype)],
        GROUPS - 1,
        1,
        (pieces,),
    )[0]


def gather_square(zs, ident, rows):
    def body(source, target, send, recv, local):
        me = Place(zs)
        copies = Copies(send, recv, local)
        flat = me.plane(everywhere=False)
        greet([me.at(x=to[0], y=to[2]) for to, _ in flat])
        place = target.at[me.x, me.y]
        arrivals = [copies.push(source, place, me.at(x=to[0], y=to[2])) for to, _ in flat]
        own = copies.keep(source, place)
        for copy in arrivals:
            copy.wait_recv()
        own.wait()
        copies.finish()

    return comm_call(
        body,
        "gather_square",
        ident,
        [jax.ShapeDtypeStruct((2, 2) + rows.shape, rows.dtype)],
        3,
        1,
        (rows,),
    )[0]


def exchange_square(zs, ident, pieces):
    def body(source, target, send, recv, local):
        me = Place(zs)
        copies = Copies(send, recv, local)
        flat = me.plane(everywhere=False)
        greet([me.at(x=to[0], y=to[2]) for to, _ in flat])
        place = target.at[me.x, me.y]
        arrivals = [
            copies.push(source.at[to[0], to[2]], place, me.at(x=to[0], y=to[2]))
            for to, _ in flat
        ]
        own = copies.keep(source.at[me.x, me.y], place)
        for copy in arrivals:
            copy.wait_recv()
        own.wait()
        copies.finish()

    return comm_call(
        body,
        "exchange_square",
        ident,
        [jax.ShapeDtypeStruct(pieces.shape, pieces.dtype)],
        3,
        1,
        (pieces,),
    )[0]


def loop(count, step):
    def body(index, carry):
        step(index)
        return carry

    lax.fori_loop(0, count, body, 0)


def total_of(*values):
    result = values[0].astype(wide)
    for value in values[1:]:
        result = result + value.astype(wide)
    return result


def reduce_keys(zs, dkv, grad1, grad2, gradm):
    n, width = dkv.shape[-2:]
    rows, columns = grad1.shape[-2:]
    rowsm = gradm.shape[-2]
    tall = grad2.shape[-2]
    plane, column = 4 * zs - 1, GROUPS * zs - 1
    count = GROUPS * zs

    def body(
        dkv_ref, g1, g2, gm, dkv_out, out1, out2, outm,
        send, recv, local,
        swap_send, swap_recv, kst, s1, p1, f1, s2, p2, sm, pm, fm, tm,
    ):
        me = Place(zs)
        copies = Copies(send, recv, local)
        crossing = me.c != me.y
        greet(
            [me.at(x=to[0], z=to[1], y=to[2]) for to, _ in me.plane()]
            + [me.at(z=to[0], g=to[1]) for to, _ in me.column()]
            + [me.at(z=to[0], g=to[1], c=me.y, y=me.c) for to, _ in me.column()]
            + [me.sibling()],
            me.at(c=me.y, y=me.c),
            crossing,
        )

        flat = me.plane(everywhere=False)
        other = 1 - me.c
        order = [to for to, _ in me.plane()] + [(me.x, me.z, me.y)]
        w1_half = copies.push(g1.at[:, other], s1, me.sibling())
        w2_half = copies.push(g2.at[:, :, other], s2, me.sibling())
        k_half = [
            copies.push(
                dkv_ref.at[to[0], other, to[1], :, to[2]], kst.at[to[0], to[1], to[2]], me.sibling()
            )
            for to in order
        ]
        wm_half = copies.push(gm.at[:, other], sm, me.sibling())

        w1_half.wait_recv()

        def add1(index):
            x, z, g, y = index // (count * 2), index // (GROUPS * 2) % zs, index // 2 % GROUPS, index % 2
            s1[x, z, g, y] = total_of(s1[x, z, g, y], g1[x, me.c, z, g, y]).astype(low_type)

        loop(4 * count, add1)
        w1_push = [
            copies.push(s1.at[:, to[0], to[1], :], p1.at[slot], me.at(z=to[0], g=to[1]))
            for slot, (to, _) in enumerate(me.column())
        ]
        w2_half.wait_recv()

        def add2(index):
            z, g = index // GROUPS, index % GROUPS
            s2[z, g] = total_of(s2[z, g], g2[z, g, me.c]).astype(low_type)

        loop(count, add2)
        w2_push = [
            copies.push(
                s2.at[to[0], to[1]], p2.at[slot + 1], me.at(z=to[0], g=to[1], c=me.y, y=me.c)
            )
            for slot, (to, _) in enumerate(me.column())
        ]
        exchanged = pltpu.make_async_remote_copy(
            src_ref=s2.at[me.z, me.g],
            dst_ref=p2.at[0],
            send_sem=swap_send,
            recv_sem=swap_recv,
            device_id=me.at(c=me.y, y=me.c),
            device_id_type=MESH,
        )
        stays = pltpu.make_async_copy(s2.at[me.z, me.g], p2.at[0], swap_recv)

        @pl.when(crossing)
        def _():
            exchanged.start()

        @pl.when(jnp.logical_not(crossing))
        def _():
            stays.start()

        k_push = []
        for slot, to in enumerate(order):
            k_half[slot].wait_recv()

            def addk(g, to=to):
                kst[to[0], to[1], to[2], g] = total_of(
                    kst[to[0], to[1], to[2], g], dkv_ref[to[0], me.c, to[1], g, to[2]]
                ).astype(low_type)

            loop(GROUPS, addk)
            if slot < plane:
                k_push.append(
                    copies.push(
                        kst.at[to[0], to[1], to[2]],
                        dkv_out.at[slot],
                        me.at(x=to[0], z=to[1], y=to[2]),
                    )
                )
        wm_half.wait_recv()

        def addm(index):
            x, z, g, y = index // (count * 2), index // (GROUPS * 2) % zs, index // 2 % GROUPS, index % 2
            sm[x, z, g, y] = total_of(sm[x, z, g, y], gm[x, me.c, z, g, y]).astype(low_type)

        loop(4 * count, addm)
        wm_push = [
            copies.push(sm.at[to[0], :, :, to[2]], pm.at[slot], me.at(x=to[0], y=to[2]))
            for slot, (to, _) in enumerate(flat)
        ]
        keep = copies.keep(kst.at[me.x, me.z, me.y], dkv_out.at[plane])
        for copy in wm_push:
            copy.wait_recv()

        def addf(index):
            z, g = index // GROUPS, index % GROUPS
            fm[z, g] = total_of(sm[me.x, z, g, me.y], pm[0, z, g], pm[1, z, g], pm[2, z, g]).astype(
                low_type
            )

        loop(count, addf)
        wm_last = [
            copies.push(fm.at[to[0], to[1]], tm.at[slot], me.at(z=to[0], g=to[1]))
            for slot, (to, _) in enumerate(me.column())
        ]
        for copy in w1_push:
            copy.wait_recv()

        def addg(index):
            x, y = index // 2, index % 2
            f1[x, y] = total_of(
                s1[x, me.z, me.g, y], *[p1[slot, x, y] for slot in range(column)]
            ).astype(low_type)

        loop(4, addg)
        quarter = out1.at[me.x * 2 + me.y]
        w1_last = [
            copies.push(f1.at[to[0], to[2]], quarter, me.at(x=to[0], y=to[2])) for to, _ in flat
        ]
        keep1 = copies.keep(f1.at[me.x, me.y], quarter)

        @pl.when(crossing)
        def _():
            exchanged.wait_recv()
            exchanged.wait_send()

        @pl.when(jnp.logical_not(crossing))
        def _():
            stays.wait()

        for copy in w2_push:
            copy.wait_recv()
        out2[...] = total_of(*[p2[slot] for slot in range(column + 1)])
        for copy in wm_last:
            copy.wait_recv()
        outm[...] = total_of(fm[me.z, me.g], *[tm[slot] for slot in range(column)])
        for copy in w1_last + k_push:
            copy.wait_recv()
        keep.wait()
        keep1.wait()
        copies.finish()

    vmem = pltpu.VMEM
    return comm_call(
        body,
        "reduce_keys",
        8,
        [
            jax.ShapeDtypeStruct((plane + 1, GROUPS, n, width), low_type),
            jax.ShapeDtypeStruct((4, rows, columns), low_type),
            jax.ShapeDtypeStruct((tall, columns), wide),
            jax.ShapeDtypeStruct((rowsm, columns), wide),
        ],
        3 + (plane + 1) + 2 * column + plane + 3 + column + 3,
        2,
        (dkv, grad1, grad2, gradm),
        spaces=[vmem] * 4,
        out_spaces=[pl.ANY, pl.ANY, vmem, vmem],
        scratch=(
            pltpu.SemaphoreType.DMA,
            pltpu.SemaphoreType.DMA,
            vmem((2, zs, 2, GROUPS, n, width), low_type),
            vmem((2, zs, GROUPS, 2, rows, columns), low_type),
            vmem((column, 2, 2, rows, columns), low_type),
            vmem((2, 2, rows, columns), low_type),
            vmem((zs, GROUPS, tall, columns), low_type),
            vmem((column + 1, tall, columns), low_type),
            vmem((2, zs, GROUPS, 2, rowsm, columns), low_type),
            vmem((3, zs, GROUPS, rowsm, columns), low_type),
            vmem((zs, GROUPS, rowsm, columns), low_type),
            vmem((column, rowsm, columns), low_type),
        ),
    )


def reduce_tokens(zs, dx, gradq):
    rows, columns = gradq.shape[-2:]
    plane = 4 * zs - 1
    count = GROUPS * zs

    def body(dx_ref, gq, dx_out, outq, send, recv, local, sq, pq, fq):
        me = Place(zs)
        copies = Copies(send, recv, local)
        greet(
            [me.at(g=to) for to, _ in me.line()]
            + [me.at(x=to[0], z=to[1], y=to[2]) for to, _ in me.plane()]
            + [me.sibling()]
        )
        half = copies.push(gq.at[:, 1 - me.c], sq, me.sibling())
        arrivals = [
            copies.push(dx_ref.at[to], dx_out.at[me.g], me.at(g=to)) for to, _ in me.line()
        ]
        own = copies.keep(dx_ref.at[me.g], dx_out.at[me.g])
        half.wait_recv()

        def add1(index):
            x, z, g, y = index // (count * 2), index // (GROUPS * 2) % zs, index // 2 % GROUPS, index % 2
            sq[x, z, g, y] = total_of(sq[x, z, g, y], gq[x, me.c, z, g, y]).astype(low_type)

        loop(4 * count, add1)
        second = [
            copies.push(
                sq.at[to[0], to[1], :, to[2]], pq.at[slot], me.at(x=to[0], z=to[1], y=to[2])
            )
            for slot, (to, _) in enumerate(me.plane())
        ]
        for copy in second:
            copy.wait_recv()

        def add2(g):
            fq[g] = total_of(
                sq[me.x, me.z, g, me.y], *[pq[slot, g] for slot in range(plane)]
            ).astype(low_type)

        loop(GROUPS, add2)
        arrivals += [
            copies.push(fq.at[to], outq.at[me.g], me.at(g=to)) for to, _ in me.line()
        ]
        keep = copies.keep(fq.at[me.g], outq.at[me.g])
        for copy in arrivals:
            copy.wait_recv()
        own.wait()
        keep.wait()
        copies.finish()

    vmem = pltpu.VMEM
    return comm_call(
        body,
        "reduce_tokens",
        9,
        [
            jax.ShapeDtypeStruct(dx.shape, low_type),
            jax.ShapeDtypeStruct((GROUPS, rows, columns), low_type),
        ],
        1 + 2 * (GROUPS - 1) + plane,
        2,
        (dx, gradq),
        spaces=[pl.ANY, vmem],
        scratch=(
            vmem((2, zs, GROUPS, 2, rows, columns), low_type),
            vmem((plane, GROUPS, rows, columns), low_type),
            vmem((GROUPS, rows, columns), low_type),
        ),
    )


NEXT = (((1,), (1,)), ((), ()))
DOWN = (((0,), (0,)), ((), ()))


def attend_forward(queries, keys, bounds, low, high, tile, block):
    total_rows = queries.shape[0]

    def body(bounds_ref, q_ref, kv_ref, low_ref, high_ref, out_ref, keep_ref, lse_ref):
        def one(turn, unused):
            rows = pl.ds(pl.multiple_of(turn * tile, tile), tile)
            first, last = low_ref[rows, :], high_ref[rows, :]
            heads = [
                q_ref[rows, h * LANES : (h + 1) * LANES] * jnp.asarray(0.125, low_type)
                for h in range(LOCAL)
            ]

            def step(j, carry):
                begin = pl.multiple_of(j * block, block)
                place = begin + lax.broadcasted_iota(jnp.int32, (tile, block), 1)
                same = (place >= first) & (place < last)
                result = []
                for h in range(LOCAL):
                    top, total, mixed = carry[h]
                    kv = kv_ref[pl.ds(begin, block), h * LANES : (h + 1) * LANES]
                    scores = lax.dot_general(heads[h], kv, NEXT, preferred_element_type=wide)
                    scores = jnp.where(same, scores, mask_fill)
                    new_top = jnp.maximum(top, jnp.max(scores, axis=1, keepdims=True))
                    factor = jnp.exp(top - new_top)
                    powers = jnp.exp(scores - new_top)
                    total = total * factor + jnp.sum(powers, axis=1, keepdims=True)
                    mixed = mixed * factor + jnp.dot(
                        powers.astype(low_type), kv, preferred_element_type=wide
                    )
                    result.append((new_top, total, mixed))
                return tuple(result)

            start = tuple(
                (
                    jnp.full((tile, 1), lowest_start, wide),
                    jnp.zeros((tile, 1), wide),
                    jnp.zeros((tile, LANES), wide),
                )
                for _ in range(LOCAL)
            )
            done = lax.fori_loop(bounds_ref[turn, 0], bounds_ref[turn, 1], step, start)
            lane = lax.broadcasted_iota(jnp.int32, (tile, LANES), 1)
            upper = lane >= HEAD
            mixes = [mixed / total for _, total, mixed in done]
            turned = [pltpu.roll(mixed, HEAD, 1) for mixed in mixes]
            front = jnp.where(upper, mixes[1], turned[0])
            back = jnp.where(upper, 0.0, turned[2])
            both = jnp.concatenate([front, back], axis=1)
            keep_ref[rows, :] = both
            out_ref[rows, :] = both.astype(low_type)
            ends = [top + jnp.log(total) for top, total, _ in done]
            lse_ref[rows, :] = jnp.where(lane == 0, ends[0], jnp.where(lane == 1, ends[1], ends[2]))
            return unused

        lax.fori_loop(0, total_rows // tile, one, 0)

    vmem = pl.BlockSpec(memory_space=pltpu.VMEM)
    return pl.pallas_call(
        body,
        name="attend_forward",
        out_shape=(
            jax.ShapeDtypeStruct((total_rows, PACK), low_type),
            jax.ShapeDtypeStruct((total_rows, PACK), wide),
            jax.ShapeDtypeStruct((total_rows, LANES), wide),
        ),
        in_specs=[pl.BlockSpec(memory_space=pltpu.SMEM)] + [vmem] * 4,
        out_specs=(vmem,) * 3,
        compiler_params=pltpu.CompilerParams(vmem_limit_bytes=VMEM_LIMIT),
    )(bounds, queries, keys, low, high)


def attend_backward(queries, keys, grads, stats, bounds, tile, block):
    total_rows = queries.shape[0]
    tokens = keys.shape[0]

    def body(bounds_ref, q_ref, kv_ref, do_ref, stat_ref, dq_ref, dkv_ref, sums):
        h = pl.program_id(0)
        zeros = jnp.zeros((block, LANES), wide)

        def clear(j, unused):
            sums[pl.ds(pl.multiple_of(j * block, block), block), :] = zeros
            return unused

        lax.fori_loop(0, tokens // block, clear, 0)
        lane = lax.broadcasted_iota(jnp.int32, (tile, LANES), 1)
        upper = lane >= HEAD

        def one(turn, unused):
            rows = pl.ds(pl.multiple_of(turn * tile, tile), tile)
            q = q_ref[rows, :] * jnp.asarray(0.125, low_type)
            front = do_ref[rows, :LANES].astype(wide)
            back = do_ref[rows, LANES:].astype(wide)
            grad = jnp.where(h == 1, front, pltpu.roll(jnp.where(h == 0, front, back), HEAD, 1))
            grad = jnp.where(upper, grad, 0.0).astype(low_type)
            stat = stat_ref[turn, 0]
            first, last = stat[0:1, :], stat[1:2, :]
            lse, delta = stat[2:3, :], stat[3:4, :]

            def step(j, total):
                begin = pl.multiple_of(j * block, block)
                place = (begin + lax.broadcasted_iota(jnp.int32, (block, tile), 0)).astype(wide)
                same = (place >= first) & (place < last)
                kv = kv_ref[pl.ds(begin, block), :]
                scores = lax.dot_general(kv, q, NEXT, preferred_element_type=wide)
                probs = jnp.exp(jnp.where(same, scores, mask_fill) - lse)
                dots = lax.dot_general(kv, grad, NEXT, preferred_element_type=wide)
                score_grad = (probs * (dots - delta)).astype(low_type)
                sums[pl.ds(begin, block), :] += jnp.dot(
                    score_grad, q, preferred_element_type=wide
                ) + jnp.dot(probs.astype(low_type), grad, preferred_element_type=wide)
                return total + lax.dot_general(score_grad, kv, DOWN, preferred_element_type=wide)

            total = lax.fori_loop(
                bounds_ref[turn, 0], bounds_ref[turn, 1], step, jnp.zeros((tile, LANES), wide)
            )
            dq_ref[rows, :] = jnp.where(upper, 0.0, total * 0.125).astype(low_type)
            return unused

        lax.fori_loop(0, total_rows // tile, one, 0)

        def store(j, unused):
            part = pl.ds(pl.multiple_of(j * block, block), block)
            dkv_ref[part, :] = sums[part, :].astype(low_type)
            return unused

        lax.fori_loop(0, tokens // block, store, 0)

    return pl.pallas_call(
        body,
        name="attend_backward",
        grid=(LOCAL,),
        out_shape=(
            jax.ShapeDtypeStruct((total_rows, WIDE), low_type),
            jax.ShapeDtypeStruct((tokens, WIDE), low_type),
        ),
        in_specs=[
            pl.BlockSpec(memory_space=pltpu.SMEM),
            pl.BlockSpec((total_rows, LANES), lambda h: (0, h)),
            pl.BlockSpec((tokens, LANES), lambda h: (0, h)),
            pl.BlockSpec((total_rows, PACK), lambda h: (0, 0)),
            pl.BlockSpec((total_rows // tile, 1, 8, tile), lambda h: (0, h, 0, 0)),
        ],
        out_specs=(
            pl.BlockSpec((total_rows, LANES), lambda h: (0, h)),
            pl.BlockSpec((tokens, LANES), lambda h: (0, h)),
        ),
        scratch_shapes=[pltpu.VMEM((tokens, LANES), wide)],
        compiler_params=pltpu.CompilerParams(vmem_limit_bytes=VMEM_LIMIT),
    )(bounds, queries, keys, grads, stats)


class Spot(Place):
    def __init__(self):
        super().__init__(1)
        self.half = self.g // 2
        self.a = self.x * 2 + self.c
        self.p = (self.x + self.c) % 2
        self.selfish = self.g % 2 == self.p
        self.crossing = self.c != self.y

    def square(self):
        return [(to[0], to[2]) for to, _ in self.plane()]

    def readers(self):
        result = []
        for k in range(GROUPS):
            g = (self.g + k) % GROUPS
            result.append((g, self.at(x=(self.g + self.c) % 2, g=g)))
        return result

    def owners(self):
        result = []
        for dv in range(2):
            for du in range(2):
                u, v = (self.x + du) % 2, (self.half + dv) % 2
                result.append((u * 2 + v, self.at(x=u, g=2 * v + self.p)))
        return result

    def slot(self):
        return self.x * 2 + self.half


def count_of(flag):
    return jnp.where(flag, 1, 0)


def announce(always, maybe):
    barrier = pltpu.get_barrier_semaphore()
    for device in always:
        pl.semaphore_signal(barrier, inc=1, device_id=device, device_id_type=MESH)
    for flag, device in maybe:

        @pl.when(flag)
        def _(device=device):
            pl.semaphore_signal(barrier, inc=1, device_id=device, device_id_type=MESH)

    total = len(always)
    for flag, _ in maybe:
        total = total + count_of(flag)
    return barrier, total


class Scatter:
    def __init__(self, send, recv, here):
        self.send, self.recv, self.here = send, recv, here
        self.copies = []

    def start(self, pieces, target, slot):
        for source, device in pieces:
            self.send_one(source, target, slot, device)

    def send_one(self, source, target, slot, device):
        index = len(self.copies)
        copy = pltpu.make_async_remote_copy(
            src_ref=source,
            dst_ref=target,
            send_sem=self.send.at[index],
            recv_sem=self.recv.at[slot],
            device_id=device,
            device_id_type=MESH,
        )
        self.copies.append(copy)
        if index:
            copy.start()
            return
        stay = pltpu.make_async_copy(source, target, self.recv.at[slot])

        @pl.when(self.here)
        def _():
            stay.start()

        @pl.when(jnp.logical_not(self.here))
        def _():
            copy.start()

    def arrived(self, slot, target):
        pltpu.make_async_copy(target, target, self.recv.at[slot]).wait()

    def finish(self):
        for copy in self.copies[1:]:
            copy.wait_send()

        @pl.when(jnp.logical_not(self.here))
        def _():
            self.copies[0].wait_send()


SMALL = 16


def first_tables(s, e, width):
    column = np.arange(width)
    rows = [column % s, column // s, column % e, column // e]
    return np.stack(rows + [np.zeros_like(column)] * 4).astype(np.int32)


def first_kernel(lengths, tokens, wq, wk, wv, vectors, inner, mix, e):
    n, depth = tokens.shape
    s = wq.shape[0]
    quarter = inner.shape[1] // 4
    cols = 2 * WIDE + LANES
    tables = jnp.asarray(first_tables(s, e, 2 * WIDE))
    count = len(vectors)

    def body(*refs):
        lengths_in, tok = refs[:2]
        arguments = refs[2 : 8 + count]
        (
            tok_out, q_out, wqkv_out, vec_out, kv_out, w1, wm, mixed_out, mixed_wide, lse_out,
            send, recv, local, tok_send, tok_recv,
            slab, toks, weights, kv_own, q_own, w1s, wms, vec, few, kv_all, scaled, sums,
            loaded, lengths_ref, lengths_sem, *places,
        ) = refs[8 + count :]
        wq_ref, wk_ref, wv_ref, tab = places[:4]
        vecs = places[4 : 4 + count]
        w1f, wmf = places[4 + count :]
        loads = [pltpu.make_async_copy(lengths_in, lengths_ref, lengths_sem)]
        loads[0].start()
        for index, (argument, place) in enumerate(zip(arguments, places)):
            loads.append(pltpu.make_async_copy(argument, place, loaded.at[index]))
            loads[-1].start()
        me = Spot()
        copies = Copies(send, recv, local)
        square = me.square()
        line = [to for to, _ in me.line()]
        sources = [device for _, device in me.owners()]
        barrier, expected = announce(
            [me.at(x=x, y=y) for x, y in square]
            + [me.at(g=to) for to in line]
            + sources[1:]
            + [me.sibling()],
            [(jnp.logical_not(me.selfish), sources[0])],
        )
        for copy in loads:
            copy.wait()
        lane = lax.broadcasted_iota(jnp.int32, (s, LANES), 1)
        lower = lane < HEAD
        for head in range(HEADS):
            pair = slice(head // 2 * LANES, head // 2 * LANES + LANES)
            q, k, v = wq_ref[:, pair], wk_ref[:, pair], wv_ref[:, pair]
            if head % 2:
                q, k = pltpu.roll(q, HEAD, 1), pltpu.roll(k, HEAD, 1)
            else:
                v = pltpu.roll(v, HEAD, 1)
            g, h = head // LOCAL, head % LOCAL
            slab[g, :, h * LANES : (h + 1) * LANES] = jnp.where(lower, k, v).astype(low_type)
            slab[g, :, WIDE + h * LANES : WIDE + (h + 1) * LANES] = jnp.where(lower, q, 0.0).astype(
                low_type
            )
        wms[...] = wmf[...].astype(low_type)
        few[...] = jnp.zeros((s, LANES), wide)
        for index in range(count):
            few[index : index + 1, : vecs[index].shape[1]] = vecs[index][...]
        small = few[...]
        for g in range(GROUPS):
            slab[g, :, 2 * WIDE :] = small.astype(low_type)
        pl.semaphore_wait(barrier, expected)

        view = weights
        place = view.at[me.a, me.g, me.y]
        slab_first = [copies.push(slab.at[to], place, me.at(g=to)) for to in line]
        slab_own = copies.keep(slab.at[me.g], place)
        for w in range(4):
            w1s[w] = w1f[:, w * quarter : (w + 1) * quarter].astype(low_type)
        place = w1.at[me.x, me.c, me.g, me.y]
        w1_first = [
            copies.push(w1s.at[x * 2 + y], place, me.at(x=x, y=y)) for x, y in square
        ]
        w1_own = copies.keep(w1s.at[me.x * 2 + me.y], place)
        wm_own = copies.keep(wms, wm.at[me.x, me.c, me.g, me.y])

        arrivals, weight_arrivals = [], []
        slab_own.wait()
        for copy in slab_first:
            copy.wait_recv()
        tokens_go = Scatter(tok_send, tok_recv, me.selfish)
        tokens_go.start([(tok, device) for _, device in me.readers()], toks.at[me.slot()], me.slot())
        block = view.at[me.a, :, me.y]
        slab_second = [copies.push(block, block, me.at(x=x, y=y)) for x, y in square]
        weight_arrivals.append(copies.push(block, block, me.sibling()))
        for copy, (x, y) in zip(slab_second, square):
            copy.wait_recv()
            block = view.at[x * 2 + me.c, :, y]
            weight_arrivals.append(copies.push(block, block, me.sibling()))
        w1_own.wait()
        for copy in w1_first:
            copy.wait_recv()
        for copy in weight_arrivals:
            copy.wait_recv()

        table = tab[...]

        def spread(pieces, within, owner):
            count = pieces.shape[0] * SMALL
            item = lax.broadcasted_iota(jnp.int32, (count, 2 * WIDE), 0)
            index = lax.broadcasted_iota(jnp.int32, (LANES, 2 * WIDE), 0)
            chosen = jnp.where(index == within, 1.0, 0.0).astype(low_type)
            pieces = pieces.astype(wide).reshape(count, LANES).astype(low_type)
            found = jnp.dot(pieces, chosen, preferred_element_type=wide)
            found = jnp.where((item >> 4) == owner, found, 0.0)
            return jnp.sum(found.reshape(count // SMALL, SMALL, 2 * WIDE), axis=0)

        every = spread(
            view[:, :, :, :SMALL, 2 * WIDE :].reshape(32, SMALL, LANES), table[0:1], table[1:2]
        )
        w_me = me.x * 2 + me.y
        inner_bias = spread(
            view[w_me, :, :, :SMALL, 2 * WIDE :].reshape(8, SMALL, LANES), table[2:3], table[3:4]
        )
        rows16 = lax.broadcasted_iota(jnp.int32, (SMALL, 2 * WIDE), 0)
        vec[...] = jnp.where(rows16 == 8, inner_bias, every)
        turned = pltpu.roll(every, 2 * WIDE - me.g * LOCAL * HEAD, 1)
        lower = lax.broadcasted_iota(jnp.int32, (1, LANES), 1) < HEAD
        biases = [[], []]
        for h in range(LOCAL):
            pair = slice(h // 2 * LANES, h // 2 * LANES + LANES)
            q, v = turned[0:1, pair], turned[1:2, pair]
            if h % 2:
                q = pltpu.roll(q, HEAD, 1)
            else:
                v = pltpu.roll(v, HEAD, 1)
            biases[0].append(jnp.where(lower, 0.0, v))
            biases[1].append(jnp.where(lower, q, 0.0))
        bias = jnp.concatenate(biases[0] + biases[1], axis=1)

        matrix = weights[:, :, :, :, : 2 * WIDE].reshape(depth, 2 * WIDE)
        kept, kv_first = [copies.keep(weights, wqkv_out), copies.keep(vec, vec_out)], []
        kv_sibling, kv_kept = [], []
        for dv in range(2):
            v = (me.half + dv) % 2
            for u in range(2):
                tokens_go.arrived(u * 2 + v, toks.at[u * 2 + v])
            if dv:
                block = w1.at[:, me.c, me.g, :]
                wm_first = [
                    copies.push(wms, wm.at[me.x, me.c, me.g, me.y], me.at(g=to)) for to in line
                ]
                w1_second = [copies.push(block, block, me.at(g=to)) for to in line]
            both = jnp.concatenate([toks[v], toks[2 + v]], axis=0)
            made = jnp.dot(both, matrix, preferred_element_type=wide)
            made = (made + bias).astype(low_type)
            for u in range(2):
                kv_own[v, u] = made[u * n : (u + 1) * n, :WIDE]
                q_own[u * 2 + v] = made[u * n : (u + 1) * n, WIDE:]
            mine = kv_all.at[:, me.c, v, me.p, me.y]
            kv_first.append(
                [copies.push(kv_own.at[v], mine, me.at(x=x, y=y)) for x, y in square]
            )
            kv_sibling.append(copies.push(kv_own.at[v], mine, me.sibling()))
            kv_kept.append(copies.keep(kv_own.at[v], mine))
        block = w1.at[:, me.c, me.g, :]
        arrivals.append(copies.push(block, block, me.sibling()))
        kept += [copies.keep(toks, tok_out), copies.keep(q_own, q_out)]

        ends = ends_of(lengths_ref)
        rows = GROUPS * n
        spans = [slice(h * LANES, (h + 1) * LANES) for h in range(LOCAL)]
        along = lax.broadcasted_iota(jnp.int32, (1, n), 1)
        ranges = [document_of(along + tile_base(me, slot, n), ends) for slot in range(GROUPS)]
        first = jnp.concatenate([low for low, _ in ranges], axis=1)
        last = jnp.concatenate([high for _, high in ranges], axis=1)
        down = lax.broadcasted_iota(jnp.int32, (rows, rows), 0)
        for slot in range(GROUPS):
            for h, span in enumerate(spans):
                scaled[h, slot * n : (slot + 1) * n] = q_own[slot, :, span] * jnp.asarray(
                    0.125, low_type
                )
        sums[...] = jnp.zeros_like(sums)

        def attend(u, c, v, carry):
            begin = ((u * 2 + c) * 2 + v) * rows
            place = down + begin
            same = (place >= first) & (place < last)
            result = []
            for h, span in enumerate(spans):
                top, total = carry[h]
                kv = kv_all[u, c, v, :, :, :, span].reshape(rows, LANES)
                scores = lax.dot_general(kv, scaled[h], NEXT, preferred_element_type=wide)
                scores = jnp.where(same, scores, mask_fill)
                new_top = jnp.maximum(top, jnp.max(scores, axis=0, keepdims=True))
                factor = jnp.exp(top - new_top)
                powers = jnp.exp(scores - new_top)
                total = total * factor + jnp.sum(powers, axis=0, keepdims=True)
                sums[h] = sums[h] * factor + lax.dot_general(
                    kv, powers.astype(low_type), DOWN, preferred_element_type=wide
                )
                result.append((new_top, total))
            return tuple(result)

        state = tuple(
            (jnp.full((1, rows), lowest_start, wide), jnp.zeros((1, rows), wide))
            for _ in range(LOCAL)
        )
        for dv in range(2):
            v = (me.half + dv) % 2
            forwards = [kv_sibling[dv]]
            for copy, (x, y) in zip(kv_first[dv], square):
                copy.wait_recv()
                block = kv_all.at[:, me.c, v, (x + me.c) % 2, y]
                forwards.append(copies.push(block, block, me.sibling()))
            kv_kept[dv].wait()
            if dv:
                wm_own.wait()
                for copy in wm_first:
                    copy.wait_recv()
                block = wm.at[me.x, me.c, :, me.y]
                wm_second = [copies.push(block, block, me.at(x=x, y=y)) for x, y in square]
                arrivals.append(copies.push(block, block, me.sibling()))
            state = lax.fori_loop(
                0, 2, lambda u, carry, v=v: attend(u, me.c, v, carry), state
            )
            for copy in forwards:
                copy.wait_recv()
            state = lax.fori_loop(
                0, 2, lambda u, carry, v=v: attend(u, 1 - me.c, v, carry), state
            )
        kept.append(copies.keep(kv_all, kv_out))
        for copy, (x, y) in zip(wm_second, square):
            copy.wait_recv()
            block = wm.at[x, me.c, :, y]
            arrivals.append(copies.push(block, block, me.sibling()))
        for copy, (_, source) in zip(w1_second, me.line()):
            copy.wait_recv()
            block = w1.at[:, me.c, source, :]
            arrivals.append(copies.push(block, block, me.sibling()))
        lane = lax.broadcasted_iota(jnp.int32, (n, LANES), 1)
        upper = lane >= HEAD
        for slot in range(GROUPS):
            part = slice(slot * n, (slot + 1) * n)
            mixes = []
            for h in range(LOCAL):
                top, total = state[h]
                mixes.append(jnp.transpose(sums[h, :, part] / total[:, part]))
                lse_out[slot, h : h + 1, :] = top[:, part] + jnp.log(total[:, part])
            turned = [pltpu.roll(mixes[h], HEAD, 1) for h in (0, 2)]
            both = jnp.concatenate(
                [jnp.where(upper, mixes[1], turned[0]), jnp.where(upper, 0.0, turned[1])], axis=1
            )
            mixed_wide[part, :] = both
            mixed_out[slot] = both.astype(low_type)
        for copy in arrivals:
            copy.wait_recv()
        for copy in kept:
            copy.wait()
        tokens_go.finish()
        copies.finish()

    vmem = pltpu.VMEM
    dma = pltpu.SemaphoreType.DMA
    total = 64
    return pl.pallas_call(
        body,
        name="first_kernel",
        out_shape=(
            jax.ShapeDtypeStruct((GROUPS, n, depth), low_type),
            jax.ShapeDtypeStruct((GROUPS, n, WIDE), low_type),
            pltpu.HBM((4, GROUPS, 2, s, cols), low_type),
            jax.ShapeDtypeStruct((SMALL, 2 * WIDE), wide),
            pltpu.HBM((2, 2, 2, 2, 2, n, WIDE), low_type),
            jax.ShapeDtypeStruct((2, 2, GROUPS, 2, s, quarter), low_type),
            jax.ShapeDtypeStruct((2, 2, GROUPS, 2, s, depth), low_type),
            jax.ShapeDtypeStruct((GROUPS, n, PACK), low_type),
            jax.ShapeDtypeStruct((GROUPS * n, PACK), wide),
            jax.ShapeDtypeStruct((GROUPS, 8, n), wide),
        ),
        in_specs=[pl.BlockSpec(memory_space=pltpu.HBM)] * (8 + count),
        out_specs=(pl.BlockSpec(memory_space=pl.ANY),) * 7
        + (pl.BlockSpec(memory_space=vmem),) * 3,
        scratch_shapes=[
            dma((total,)), dma((total,)), dma((12,)), dma((4,)), dma((4,)),
            vmem((GROUPS, s, cols), low_type),
            vmem((GROUPS, n, depth), low_type),
            vmem((4, GROUPS, 2, s, cols), low_type),
            vmem((2, 2, n, WIDE), low_type),
            vmem((GROUPS, n, WIDE), low_type),
            vmem((4, s, quarter), low_type),
            vmem((s, depth), low_type),
            vmem((SMALL, 2 * WIDE), wide),
            vmem((s, LANES), wide),
            vmem((2, 2, 2, 2, 2, n, WIDE), low_type),
            vmem((LOCAL, GROUPS * n, LANES), low_type),
            vmem((LOCAL, LANES, GROUPS * n), wide),
            dma((6 + count,)),
            pltpu.SMEM(lengths.shape, jnp.int32),
            dma,
            *[vmem(item.shape, item.dtype) for item in (wq, wk, wv, tables, *vectors, inner, mix)],
        ],
        compiler_params=pltpu.CompilerParams(
            collective_id=10, has_side_effects=True, vmem_limit_bytes=NEAR_LIMIT
        ),
    )(*[pltpu.with_memory_space_constraint(item, pltpu.HBM) for item in (lengths, tokens, wq, wk, wv, tables, *vectors, inner, mix)])


def pass_back(ident, pieces):
    def body(source, target, send, recv):
        me = Spot()
        owners = me.owners()
        readers = [device for _, device in me.readers()]
        barrier, expected = announce(readers[1:], [(jnp.logical_not(me.selfish), readers[0])])
        pl.semaphore_wait(barrier, expected)
        move = Scatter(send, recv, me.selfish)
        move.start([(source.at[slot], device) for slot, device in owners], target.at[me.g], me.g)
        for g in range(GROUPS):
            move.arrived(g, target.at[g])
        move.finish()

    return scatter_call(body, "pass_back", ident, pieces)


def pass_on(ident, pieces):
    def body(source, target, send, recv):
        me = Spot()
        owners = [device for _, device in me.owners()]
        barrier, expected = announce(owners[1:], [(jnp.logical_not(me.selfish), owners[0])])
        pl.semaphore_wait(barrier, expected)
        move = Scatter(send, recv, me.selfish)
        slot = me.slot()
        move.start([(source.at[g], device) for g, device in me.readers()], target.at[slot], slot)
        for index in range(GROUPS):
            move.arrived(index, target.at[index])
        move.finish()

    return scatter_call(body, "pass_on", ident, pieces)


def scatter_call(body, name, ident, pieces):
    return pl.pallas_call(
        body,
        name=name,
        out_shape=jax.ShapeDtypeStruct(pieces.shape, pieces.dtype),
        in_specs=[pl.BlockSpec(memory_space=pl.ANY)],
        out_specs=pl.BlockSpec(memory_space=pl.ANY),
        scratch_shapes=[pltpu.SemaphoreType.DMA((4,)), pltpu.SemaphoreType.DMA((4,))],
        compiler_params=pltpu.CompilerParams(
            collective_id=ident, has_side_effects=True, vmem_limit_bytes=VMEM_LIMIT
        ),
    )(pieces)


def final_kernel(output, hidden, pieces, outqk, out1, out2, outm, s, e):
    n, depth = hidden.shape
    quarter = out1.shape[-1]

    def body(y_in, hid, dx, qk_in, i_in, o_in, m_in, yo, xg, qw, qb, kw, vw, vb, mw, mb, eg, es, iw, ib, ow, ob, fg, fs):
        device = lax.axis_index("au") * lax.axis_size("row") + lax.axis_index("row")
        yo[...] = y_in[...]
        xg[...] = total_of(hid[...], dx[0], dx[1], dx[2], dx[3]).astype(low_type)
        rows = qk_in.shape[1]
        q_in, k_in = qk_in.at[:, :, WIDE:], qk_in.at[:, :, :WIDE]
        lower = lax.broadcasted_iota(jnp.int32, (rows, LANES), 1) < HEAD

        def part(head):
            g, h = head // LOCAL, head % LOCAL
            return k_in[g, :, h * LANES : (h + 1) * LANES].astype(wide)

        made_q = []
        for g in range(0, GROUPS, 2):
            a0, b0 = q_in[g, :, :LANES].astype(wide), q_in[g, :, LANES:].astype(wide)
            a1 = pltpu.roll(q_in[g + 1, :, :LANES].astype(wide), HEAD, 1)
            b1 = pltpu.roll(q_in[g + 1, :, LANES:].astype(wide), HEAD, 1)
            made_q += [a0, jnp.where(lower, b0, a1), jnp.where(lower, a1, b1)]
        biases = [[], []]
        for pair in range(HEADS // 2):
            span = slice(pair * LANES, (pair + 1) * LANES)
            kv = [part(2 * pair), part(2 * pair + 1)]
            made_k = jnp.where(lower, kv[0], pltpu.roll(kv[1], HEAD, 1))
            made_v = jnp.where(lower, pltpu.roll(kv[0], HEAD, 1), kv[1])
            qw[:, span], kw[:, span], vw[:, span] = made_q[pair][:s], made_k[:s], made_v[:s]
            biases[0].append(made_q[pair][s:])
            biases[1].append(made_v[s:])

        def own(eight, width, shift):
            return pltpu.roll(eight, shift, 1)[0:1, :width]

        turn = (depth - device * s) % depth
        qb[...] = own(jnp.concatenate(biases[0], axis=1), s, turn)
        vb[...] = own(jnp.concatenate(biases[1], axis=1), s, turn)
        mw[...] = m_in[:s]
        extras = pltpu.roll(m_in[s : s + 8, :], turn, 1)
        for index, ref in enumerate((mb, eg, es, ob, fg, fs)):
            ref[...] = extras[index : index + 1, :s]
        for w in range(4):
            iw[:, w * quarter : (w + 1) * quarter] = i_in[w, :s].astype(wide)
        place = lax.axis_index("row") * e
        ib[...] = own(
            i_in[lax.axis_index("au"), s : s + 8, :].astype(wide), e, (quarter - place) % quarter
        )
        ow[...] = o_in[...]

    vmem = pltpu.VMEM

    def shape(*dims):
        return jax.ShapeDtypeStruct(dims, wide)

    return pl.pallas_call(
        body,
        name="final_kernel",
        out_shape=(
            jax.ShapeDtypeStruct((n, depth), low_type),
            jax.ShapeDtypeStruct((n, depth), low_type),
            shape(s, depth), shape(1, s), shape(s, depth), shape(s, depth), shape(1, s),
            shape(s, depth), shape(1, s), shape(1, s), shape(1, s),
            shape(s, 4 * quarter), shape(1, e), shape(e, depth),
            shape(1, s), shape(1, s), shape(1, s),
        ),
        in_specs=[pl.BlockSpec(memory_space=vmem)] * 7,
        out_specs=(pl.BlockSpec(memory_space=vmem),) * 17,
        compiler_params=pltpu.CompilerParams(vmem_limit_bytes=NEAR_LIMIT),
    )(output, hidden, pieces, outqk, out1, out2, outm)


def gelu_and_slope(value):
    t = 1.0 / (1.0 + (0.3275911 * 0.7071067811865476) * jnp.abs(value))
    bell = jnp.exp(-0.5 * value * value)
    tail = 1.061405429
    for weight in (-1.453152027, 1.421413741, -0.284496736, 0.254829592):
        tail = tail * t + weight
    tail = 0.5 * tail * t * bell
    below = jnp.where(value >= 0.0, 1.0 - tail, tail)
    return value * below, below + value * bell * 0.3989422804014327


def normed(hidden):
    mean = jnp.mean(hidden, axis=-1, keepdims=True)
    centered = hidden - mean
    spread = jnp.mean(centered * centered, axis=-1, keepdims=True)
    inverse = lax.rsqrt(spread + eps_norm)
    return centered * inverse, inverse


def normed_grad(grad, norm, inverse):
    mean = jnp.mean(grad, axis=-1, keepdims=True)
    along = jnp.mean(grad * norm, axis=-1, keepdims=True)
    return inverse * (grad - mean - norm * along)


def down_sum(values):
    return jnp.sum(values, axis=0, keepdims=True)


def middle_kernel(mixed, tokens, cotangent, mix, inner, outer, vec, s, e):
    n, depth = tokens.shape
    quarter = inner.shape[1]
    rows = s + 8
    cut = depth // 2
    hn = n // 2

    def body(
        mixed_ref, tok_in, cot_in, wm_in, w1_in, w2f_in, vec_in,
        out, hidden_out, do_out, sm, s1, s2,
        send, recv, local, back_send, back_recv, on_send, on_recv,
        swap_send2, swap_recv2, tok, cot, w2f, vec_ref, wm, w1, w2p, w2s, came, mixed_tok, xs, acts, slopes, parts, sums, bgs, igs, parts2, sums2,
        pieces, extra, attn, own1, own2, g1, g2, gm,
    ):
        me = Spot()
        copies = Copies(send, recv, local)
        square = me.square()
        line = [to for to, _ in me.line()]
        owners = me.owners()
        readers = me.readers()
        swapped = [me.at(g=to, c=me.y, y=me.c) for to in [me.g] + line]
        barrier, expected = announce(
            [me.at(x=x, y=y) for x, y in square]
            + swapped[1:]
            + [device for _, device in readers[1:]]
            + [device for _, device in owners[1:]]
            + [me.sibling()],
            [
                (jnp.logical_not(me.selfish), readers[0][1]),
                (jnp.logical_not(me.selfish), owners[0][1]),
                (me.crossing, swapped[0]),
            ],
        )
        loads = [copies.keep(wm_in, wm), copies.keep(w1_in, w1)]
        small_loads = [
            copies.keep(source, target)
            for source, target in ((tok_in, tok), (vec_in, vec_ref), (w2f_in, w2f), (cot_in, cot))
        ]
        pl.semaphore_wait(barrier, expected)

        back = Scatter(back_send, back_recv, me.selfish)
        back.start([(mixed_ref.at[slot], device) for slot, device in owners], came.at[me.g], me.g)
        lower = lax.broadcasted_iota(jnp.int32, (n, LANES), 1) < HEAD
        loads[0].wait()
        for copy in small_loads:
            copy.wait()
        w2s[...] = w2f[...].astype(low_type)
        for g in range(GROUPS):
            back.arrived(g, came.at[g])
        w2_place = w2p.at[me.g, me.y]
        w2_first = [copies.push(w2s, w2_place, device) for device in swapped[1:]]
        w2_swap = pltpu.make_async_remote_copy(
            src_ref=w2s,
            dst_ref=w2_place,
            send_sem=swap_send2,
            recv_sem=swap_recv2,
            device_id=swapped[0],
            device_id_type=MESH,
        )
        w2_stays = pltpu.make_async_copy(w2s, w2_place, swap_recv2)

        @pl.when(me.crossing)
        def _():
            w2_swap.start()

        @pl.when(jnp.logical_not(me.crossing))
        def _():
            w2_stays.start()

        for half in range(2):
            a0 = came[2 * half, :, :LANES]
            b0 = came[2 * half, :, LANES:].astype(wide)
            a1 = pltpu.roll(came[2 * half + 1, :, :LANES].astype(wide), HEAD, 1)
            b1 = pltpu.roll(came[2 * half + 1, :, LANES:].astype(wide), HEAD, 1)
            base = half * 3 * LANES
            mixed_tok[:, base : base + LANES] = a0
            mixed_tok[:, base + LANES : base + 2 * LANES] = jnp.where(lower, b0, a1).astype(low_type)
            mixed_tok[:, base + 2 * LANES : base + 3 * LANES] = jnp.where(lower, a1, b1).astype(
                low_type
            )

        def vector(index):
            return vec_ref[index : index + 1, :]

        mix = jnp.dot(mixed_tok[...], wm[...], preferred_element_type=wide) + vector(2)
        norm1, inverse1 = normed(tok[...].astype(wide) + mix)
        early = norm1 * vector(3) + vector(4)
        mine = me.x * 2 + me.y
        halves = [slice(0, hn), slice(hn, n)]

        def send_rows(ref, h):
            place = ref.at[h, mine]
            return [copies.push(place, place, me.at(x=x, y=y)) for x, y in square]

        def send_back(ref, landing, h):
            return [
                copies.push(ref.at[h, x * 2 + y], landing.at[h, mine], me.at(x=x, y=y))
                for x, y in square
            ]

        def arrive(started):
            for copy in started:
                copy.wait_recv()

        def received(landing, h):
            return [landing[h, x * 2 + y] for x, y in square]

        early_go = []
        for h, half in enumerate(halves):
            xs[h, mine] = early[half].astype(low_type)
            early_go.append(send_rows(xs, h))
        loads[1].wait()

        def outer_weight():
            return w2p[...].reshape(quarter, depth)

        branch_go = []
        for h in range(2):
            arrive(early_go[h])
            inner = jnp.dot(
                xs[h].reshape(4 * hn, depth), w1[...], preferred_element_type=wide
            ) + vector(8)
            act, slope = gelu_and_slope(inner)
            act = act.astype(low_type)
            acts[h] = act.reshape(4, hn, quarter)
            slopes[h] = slope
            if h == 0:

                @pl.when(me.crossing)
                def _():
                    w2_swap.wait_recv()
                    w2_swap.wait_send()

                @pl.when(jnp.logical_not(me.crossing))
                def _():
                    w2_stays.wait()

                block = w2p.at[me.g, me.c]
                w2_last = [copies.push(block, block, me.sibling())]
                for copy, (_, source) in zip(w2_first, me.line()):
                    copy.wait_recv()
                    block = w2p.at[source, me.c]
                    w2_last.append(copies.push(block, block, me.sibling()))
                arrive(w2_last)
            made = jnp.dot(act, outer_weight(), preferred_element_type=wide).reshape(4, hn, depth)
            own1[h] = made
            parts[h] = made.astype(low_type)
            branch_go.append(send_back(parts, sums, h))

        grad_go, final_grads, norm_sums, cot_sums = [], [], [], []
        for h, half in enumerate(halves):
            arrive(branch_go[h])
            branch = total_of(own1[h, mine], *received(sums, h)) + vector(5)
            norm2, inverse2 = normed(early[half] + branch)
            out[half, :] = (norm2 * vector(6) + vector(7)).astype(low_type)
            cot_wide = cot[half, :].astype(wide)
            final_grad = normed_grad(cot_wide * vector(6), norm2, inverse2)
            bgs[h, mine] = final_grad.astype(low_type)
            grad_go.append(send_rows(bgs, h))
            final_grads.append(final_grad)
            norm_sums.append(down_sum(cot_wide * norm2))
            cot_sums.append(down_sum(cot_wide))
        extra[...] = jnp.zeros_like(extra)
        extra[3:4, :] = down_sum(bgs[0, mine].astype(wide)) + down_sum(bgs[1, mine].astype(wide))
        extra[4:5, :] = norm_sums[0] + norm_sums[1]
        extra[5:6, :] = cot_sums[0] + cot_sums[1]

        token_go = []
        for h in range(2):
            arrive(grad_go[h])
            grad = lax.dot_general(
                bgs[h].reshape(4 * hn, depth), outer_weight(), NEXT, preferred_element_type=wide
            )
            grad = (grad * slopes[h]).astype(low_type)
            igs[h] = grad.reshape(4, hn, quarter)
            made = lax.dot_general(grad, w1[...], NEXT, preferred_element_type=wide)
            made = made.reshape(4, hn, depth)
            own2[h] = made
            parts2[h] = made.astype(low_type)
            token_go.append(send_back(parts2, sums2, h))

        other = 1 - me.c
        grads = bgs[...].reshape(4 * n, depth)
        for half in range(2):
            span = slice(half * cut, (half + 1) * cut)
            made = lax.dot_general(
                acts[:, :, :, span].reshape(4 * n, cut), grads, DOWN, preferred_element_type=wide
            )
            g2[2 * half : 2 * half + 2] = made.astype(low_type).reshape(2, 2, e, depth)
        w2_half = copies.push(g2.at[:, other], s2, me.sibling())

        grads = igs[...].reshape(4 * n, quarter)
        bias = jnp.broadcast_to(down_sum(grads.astype(wide)), (8, quarter)).astype(low_type)
        for half in range(2):
            span = slice(half * cut, (half + 1) * cut)
            made = lax.dot_general(
                xs[:, :, :, span].reshape(4 * n, cut), grads, DOWN, preferred_element_type=wide
            ).astype(low_type)
            for index in range(16):
                place = (half, index // 8, index // 2 % GROUPS, index % 2)
                g1[(*place, slice(None, s))] = made[index * s : (index + 1) * s]
                g1[(*place, slice(s, None))] = bias
        w1_half = copies.push(g1.at[:, other], s1, me.sibling())
        w2_half.wait_recv()

        def add2(g):
            s2[g] = s2[g] + g2[g, me.c]

        loop(GROUPS, add2)
        w1_half.wait_recv()

        def add1(index):
            x, g, y = index // 8, index // 2 % GROUPS, index % 2
            s1[x, g, y] = s1[x, g, y] + g1[x, me.c, g, y]

        loop(16, add1)
        norm_sums, grad_sums, attn_sums = [], [], []
        for h, half in enumerate(halves):
            arrive(token_go[h])
            early_grad = total_of(final_grads[h], own2[h, mine], *received(sums2, h))
            norm_sums.append(down_sum(early_grad * norm1[half]))
            grad_sums.append(down_sum(early_grad))
            hidden = normed_grad(early_grad * vector(3), norm1[half], inverse1[half])
            hidden_out[half, :] = hidden
            attn[half, :] = hidden.astype(low_type)
            attn_sums.append(down_sum(hidden.astype(low_type).astype(wide)))
        extra[0:1, :] = attn_sums[0] + attn_sums[1]
        extra[1:2, :] = norm_sums[0] + norm_sums[1]
        extra[2:3, :] = grad_sums[0] + grad_sums[1]
        attn_grad = attn[...]
        back_grad = lax.dot_general(attn_grad, wm[...], NEXT, preferred_element_type=wide)
        for half in range(2):
            base = half * 3 * LANES
            t0 = back_grad[:, base : base + LANES]
            t1 = back_grad[:, base + LANES : base + 2 * LANES]
            t2 = back_grad[:, base + 2 * LANES : base + 3 * LANES]
            r1, r2 = pltpu.roll(t1, HEAD, 1), pltpu.roll(t2, HEAD, 1)
            pieces[2 * half, :, :LANES] = t0.astype(low_type)
            pieces[2 * half, :, LANES:] = jnp.where(lower, t1, 0.0).astype(low_type)
            pieces[2 * half + 1, :, :LANES] = jnp.where(lower, r1, r2).astype(low_type)
            pieces[2 * half + 1, :, LANES:] = jnp.where(lower, r2, 0.0).astype(low_type)
        onward = Scatter(on_send, on_recv, me.selfish)
        slot = me.slot()
        onward.start([(pieces.at[g], device) for g, device in readers], do_out.at[slot], slot)

        for half in range(2):
            span = slice(half * cut, (half + 1) * cut)
            made = lax.dot_general(
                mixed_tok[:, span], attn_grad, DOWN, preferred_element_type=wide
            ).astype(low_type)
            for index in range(16):
                place = (half, index // 8, index // 2 % GROUPS, index % 2)
                gm[(*place, slice(None, s))] = made[index * s : (index + 1) * s]
                gm[(*place, slice(s, None))] = extra[...].astype(low_type)
        wm_half = copies.push(gm.at[:, other], sm, me.sibling())
        wm_half.wait_recv()

        def addm(index):
            x, g, y = index // 8, index // 2 % GROUPS, index % 2
            sm[x, g, y] = sm[x, g, y] + gm[x, me.c, g, y]

        loop(16, addm)
        for index in range(GROUPS):
            onward.arrived(index, do_out.at[index])
        back.finish()
        onward.finish()
        copies.finish()

    vmem = pltpu.VMEM
    dma = pltpu.SemaphoreType.DMA
    tall = vmem((2, 4, hn, depth), low_type)
    full = vmem((2, 4, hn, depth), wide)
    high = vmem((2, 4, hn, quarter), low_type)
    tokens, cotangent, outer = [
        pltpu.with_memory_space_constraint(item, pltpu.HBM) for item in (tokens, cotangent, outer)
    ]
    return pl.pallas_call(
        body,
        name="middle_kernel",
        out_shape=(
            jax.ShapeDtypeStruct((n, depth), low_type),
            jax.ShapeDtypeStruct((n, depth), wide),
            jax.ShapeDtypeStruct((GROUPS, n, PACK), low_type),
            jax.ShapeDtypeStruct((2, GROUPS, 2, rows, depth), low_type),
            jax.ShapeDtypeStruct((2, GROUPS, 2, rows, quarter), low_type),
            jax.ShapeDtypeStruct((GROUPS, e, depth), low_type),
        ),
        in_specs=[
            pl.BlockSpec(memory_space=item)
            for item in (pl.ANY, pltpu.HBM, pltpu.HBM, pl.ANY, pl.ANY, pltpu.HBM, pl.ANY)
        ],
        out_specs=[
            pl.BlockSpec(memory_space=item) for item in (vmem, vmem, pl.ANY, vmem, vmem, vmem)
        ],
        scratch_shapes=[
            dma((48,)), dma((48,)), dma((8,)), dma((4,)), dma((4,)), dma((4,)), dma((4,)), dma, dma,
            vmem((n, depth), low_type),
            vmem((n, depth), low_type),
            vmem((e, depth), wide),
            vmem(vec.shape, wide),
            vmem((depth, depth), low_type),
            vmem((depth, quarter), low_type),
            vmem((GROUPS, 2, e, depth), low_type),
            vmem((e, depth), low_type),
            vmem((GROUPS, n, PACK), low_type),
            vmem((n, depth), low_type),
            tall, high,
            vmem((2, 4 * hn, quarter), wide),
            tall, tall, tall, high, tall, tall,
            vmem((GROUPS, n, PACK), low_type),
            vmem((8, depth), wide),
            vmem((n, depth), low_type),
            full, full,
            vmem((2, 2, GROUPS, 2, rows, quarter), low_type),
            vmem((GROUPS, 2, e, depth), low_type),
            vmem((2, 2, GROUPS, 2, rows, depth), low_type),
        ],
        compiler_params=pltpu.CompilerParams(
            collective_id=12, has_side_effects=True, vmem_limit_bytes=NEAR_LIMIT
        ),
    )(mixed, tokens, cotangent, mix, inner, outer, vec)


def tile_base(me, slot, n):
    u, v = slot // 2, slot % 2
    return ((u * 2 + me.c) * 2 * GROUPS + (v * 2 + me.p) * 2 + me.y) * n


def ends_of(lengths_ref):
    ends = [lengths_ref[0]]
    for index in range(1, lengths_ref.shape[0]):
        ends.append(ends[-1] + lengths_ref[index])
    return ends


def document_of(place, ends):
    first, last = place * 0, place * 0 + ends[-1]
    for end in ends[:-1]:
        before = end <= place
        first = jnp.where(before, end, first)
    for end in reversed(ends[:-1]):
        last = jnp.where(end <= place, last, end)
    return first, last


def turn_kernel(lengths, queries, keys, grads_in, mixed, lse, tokens, weights, sum1, sum2, summ):
    n = tokens.shape[1]
    depth = tokens.shape[-1]
    s = depth // 32
    rows = s + 8
    cut = depth // 2
    tall = sum2.shape[1]
    block = GROUPS * n
    width = WIDE + PACK
    spans = [slice(h * LANES, (h + 1) * LANES) for h in range(LOCAL)]

    def body(
        lengths_ref, q_ref, kv_ref, do_ref, mixed_ref, lse_ref, tok, w_ref, s1, s2, sm,
        dx_out, outqk, out1, out2, outm,
        send, recv, local, dx_send, dx_recv, swap_send, swap_recv, ks, kr, ps, pr,
        both, kbuf, kin, pk, dqs, grads, narrow, dxs, gk, sk, pp, fk, p1, f1, pm, fm, tm, p2, early,
    ):
        me = Spot()
        copies = Copies(send, recv, local)
        square = me.square()
        line = [to for to, _ in me.line()]
        readers = [device for _, device in me.readers()]
        swapped = [me.at(g=to, c=me.y, y=me.c) for to in [me.g] + line]
        barrier, expected = announce(
            [me.at(x=x, y=y) for x, y in square]
            + [me.at(g=to) for to in line]
            + readers[1:]
            + swapped[1:]
            + [me.sibling()],
            [(jnp.logical_not(me.selfish), readers[0]), (me.crossing, swapped[0])],
        )
        ends = ends_of(lengths_ref)
        lane = lax.broadcasted_iota(jnp.int32, (n, LANES), 1)
        upper = lane >= HEAD
        along = lax.broadcasted_iota(jnp.int32, (1, n), 1)
        down = lax.broadcasted_iota(jnp.int32, (block, n), 0)

        def upper_halves(ref, part):
            front = ref[part, :LANES].astype(wide)
            back = ref[part, LANES:].astype(wide)
            parts = (pltpu.roll(front, HEAD, 1), front, pltpu.roll(back, HEAD, 1))
            return [jnp.where(upper, item, 0.0) for item in parts]

        firsts, lasts, logs, deltas = [], [], [], []
        for slot in range(GROUPS):
            part = slice(slot * n, (slot + 1) * n)
            first, last = document_of(along + tile_base(me, slot, n), ends)
            firsts.append(first)
            lasts.append(last)
            outs, inputs = upper_halves(mixed_ref, part), upper_halves(do_ref, part)
            for h, span in enumerate(spans):
                base = slot * 2 * n
                both[h, base : base + n] = q_ref[part, span] * jnp.asarray(0.125, low_type)
                both[h, base + n : base + 2 * n] = inputs[h].astype(low_type)
            deltas.append([down_sum(jnp.transpose(i * o)) for i, o in zip(inputs, outs)])
            logs.append([lse_ref[slot, h : h + 1, :] for h in range(LOCAL)])
        dqs[...] = jnp.zeros_like(dqs)
        pl.semaphore_wait(barrier, expected)

        wm_push = [
            copies.push(sm.at[x, :, y], pm.at[peer], me.at(x=x, y=y))
            for peer, (x, y) in enumerate(square)
        ]
        w1_push = [
            copies.push(s1.at[:, to, :], p1.at[slot], me.at(g=to)) for slot, to in enumerate(line)
        ]
        w2_push = [
            copies.push(s2.at[to], p2.at[index + 1], swapped[index + 1])
            for index, to in enumerate(line)
        ]
        exchanged = pltpu.make_async_remote_copy(
            src_ref=s2.at[me.g],
            dst_ref=p2.at[0],
            send_sem=swap_send,
            recv_sem=swap_recv,
            device_id=swapped[0],
            device_id_type=MESH,
        )
        stays = pltpu.make_async_copy(s2.at[me.g], p2.at[0], swap_recv)

        @pl.when(me.crossing)
        def _():
            exchanged.start()

        @pl.when(jnp.logical_not(me.crossing))
        def _():
            stays.start()

        other = 1 - me.c

        def attend(u, c, v, target):
            begin = pl.multiple_of(((u * 2 + c) * 2 + v) * block, block)
            place = down + begin
            same = [(place >= first) & (place < last) for first, last in zip(firsts, lasts)]
            for h, span in enumerate(spans):
                kv = kv_ref[pl.ds(begin, block), span]
                made = lax.dot_general(kv, both[h], NEXT, preferred_element_type=wide)
                pairs = []
                for slot in range(GROUPS):
                    base = slot * 2 * n
                    scores = jnp.where(same[slot], made[:, base : base + n], mask_fill)
                    probs = jnp.exp(scores - logs[slot][h])
                    dots = made[:, base + n : base + 2 * n]
                    score_grad = (probs * (dots - deltas[slot][h])).astype(low_type)
                    pairs += [score_grad, probs.astype(low_type)]
                    dqs[slot, :, span] += lax.dot_general(
                        score_grad, kv, DOWN, preferred_element_type=wide
                    )
                made = jnp.dot(
                    jnp.concatenate(pairs, axis=1), both[h], preferred_element_type=wide
                )
                target[:, :, :, span] = made.astype(low_type).reshape(2, 2, n, LANES)

        def to_sibling(turn):
            return pltpu.make_async_remote_copy(
                src_ref=kbuf.at[0, turn],
                dst_ref=kin.at[turn],
                send_sem=ks.at[turn],
                recv_sem=kr.at[turn],
                device_id=me.sibling(),
                device_id_type=MESH,
            )

        def to_peer(turn, peer):
            x, y = square[peer]
            return pltpu.make_async_remote_copy(
                src_ref=kbuf.at[1, turn, (x + me.c) % 2, y],
                dst_ref=pk.at[turn, peer],
                send_sem=ps.at[turn * 3 + peer],
                recv_sem=pr.at[turn * 3 + peer],
                device_id=me.at(x=x, y=y),
                device_id_type=MESH,
            )

        def key_turn(turn):
            u, v = turn % 2, (me.half + turn // 2) % 2

            def of_core(index):
                attend(u, jnp.where(index == 0, other, me.c), v, kbuf.at[index, turn])

                @pl.when(index == 0)
                def _():
                    to_sibling(turn).start()

            loop(2, of_core)
            to_sibling(turn).wait_recv()
            for p in range(2):
                for y in range(2):
                    kbuf[1, turn, p, y] = kbuf[1, turn, p, y] + kin[turn, p, y]
            for peer in range(3):
                to_peer(turn, peer).start()

        loop(4, key_turn)

        def square_push(total, landing):
            return [
                copies.push(total.at[x, :, y], landing.at[slot], me.at(x=x, y=y))
                for slot, (x, y) in enumerate(square)
            ]

        def square_sum(result, total, landed):
            def add(g):
                result[g] = total_of(
                    total[me.x, g, me.y], landed[0, g], landed[1, g], landed[2, g]
                ).astype(low_type)

            loop(GROUPS, add)

        def weight_grad(slots, half):
            span = slice(half * cut, (half + 1) * cut)
            return lax.dot_general(
                jnp.concatenate([tok[slot, :, span] for slot in slots], axis=0),
                jnp.concatenate([narrow[slot] for slot in slots], axis=0),
                DOWN,
                preferred_element_type=wide,
            )

        moves = []
        slots = [turn % 2 * 2 + (me.half + turn // 2) % 2 for turn in range(4)]
        for turn in range(4):
            if turn == 3:
                for half in range(2):
                    early[half] = weight_grad(slots[:3], half)
            u, dv = turn % 2, turn // 2
            v = (me.half + dv) % 2
            slot = u * 2 + v
            wides = [dqs[slot, :, span] * 0.125 for span in spans]
            for h, span in enumerate(spans):
                grads[slot, :, WIDE + span.start : WIDE + span.stop] = jnp.where(
                    upper, 0.0, wides[h]
                ).astype(low_type)
            narrow[slot, :, WIDE : WIDE + LANES] = jnp.where(
                upper, pltpu.roll(wides[1], HEAD, 1), wides[0]
            ).astype(low_type)
            narrow[slot, :, WIDE + LANES :] = jnp.where(upper, 0.0, wides[2]).astype(low_type)
            for peer in range(3):
                to_peer(turn, peer).wait_recv()
            here = total_of(
                kbuf[1, turn, me.p, me.y], *[pk[turn, peer] for peer in range(3)]
            ).astype(low_type)
            grads[slot, :, :WIDE] = here
            narrow[slot, :, :WIDE] = here
            dxs[slot] = lax.dot_general(
                grads[slot], w_ref[:, : 2 * WIDE], NEXT, preferred_element_type=wide
            ).astype(low_type)
            copy = pltpu.make_async_remote_copy(
                src_ref=dxs.at[slot],
                dst_ref=dx_out.at[me.g],
                send_sem=dx_send.at[turn],
                recv_sem=dx_recv.at[me.g],
                device_id=me.at(x=u, g=2 * v + me.p),
                device_id_type=MESH,
            )
            if dv:
                copy.start()
                moves.append((copy, None))
                continue
            stay = pltpu.make_async_copy(dxs.at[slot], dx_out.at[me.g], dx_recv.at[me.g])
            at_home = me.selfish & (me.x == u)
            away = jnp.logical_not(at_home)
            moves.append((copy, away))

            @pl.when(at_home)
            def _(stay=stay):
                stay.start()

            @pl.when(away)
            def _(copy=copy):
                copy.start()

        bias = down_sum(total_of(*[down_sum(narrow[slot].astype(wide)) for slot in range(GROUPS)]))
        bias = jnp.broadcast_to(bias, (8, width)).astype(low_type)
        for half in range(2):
            made = (early[half] + weight_grad(slots[3:], half)).astype(low_type)
            for index in range(16):
                place = (half, index // 8, index // 2 % GROUPS, index % 2)
                gk[(*place, slice(None, s))] = made[index * s : (index + 1) * s]
                gk[(*place, slice(s, None))] = bias
        g_half = copies.push(gk.at[:, other], sk, me.sibling())

        for copy in wm_push:
            copy.wait_recv()
        square_sum(fm, sm, pm)
        wm_last = [
            copies.push(fm.at[to], tm.at[peer], me.at(g=to)) for peer, to in enumerate(line)
        ]
        for copy in w1_push:
            copy.wait_recv()

        def addw(index):
            x, y = index // 2, index % 2
            f1[x, y] = total_of(s1[x, me.g, y], *[p1[peer, x, y] for peer in range(3)]).astype(
                low_type
            )

        loop(4, addw)
        quarter = out1.at[me.x * 2 + me.y]
        g_half.wait_recv()

        def pair_sum(index):
            x, g, y = index // 8, index // 2 % GROUPS, index % 2
            sk[x, g, y] = sk[x, g, y] + gk[x, me.c, g, y]

        loop(16, pair_sum)
        push = square_push(sk, pp)
        arrivals = [copies.push(f1.at[x, y], quarter, me.at(x=x, y=y)) for x, y in square]
        kept = [copies.keep(f1.at[me.x, me.y], quarter)]

        @pl.when(me.crossing)
        def _():
            exchanged.wait_recv()
            exchanged.wait_send()

        @pl.when(jnp.logical_not(me.crossing))
        def _():
            stays.wait()

        for copy in w2_push:
            copy.wait_recv()
        out2[...] = total_of(*[p2[index] for index in range(4)])
        for copy in push:
            copy.wait_recv()
        square_sum(fk, sk, pp)
        arrivals += [copies.push(fk.at[to], outqk.at[me.g], me.at(g=to)) for to in line]
        kept.append(copies.keep(fk.at[me.g], outqk.at[me.g]))
        for copy in wm_last:
            copy.wait_recv()
        outm[...] = total_of(fm[me.g], *[tm[peer] for peer in range(3)])
        for copy in arrivals:
            copy.wait_recv()
        for g in range(GROUPS):
            pltpu.make_async_copy(dx_out.at[g], dx_out.at[g], dx_recv.at[g]).wait()
        for copy in kept:
            copy.wait()
        for copy, away in moves:
            if away is None:
                copy.wait_send()
                continue

            @pl.when(away)
            def _(copy=copy):
                copy.wait_send()

        for turn in range(4):
            to_sibling(turn).wait_send()
            for peer in range(3):
                to_peer(turn, peer).wait_send()
        copies.finish()

    vmem = pltpu.VMEM
    dma = pltpu.SemaphoreType.DMA
    total = 40
    return pl.pallas_call(
        body,
        name="turn_kernel",
        out_shape=(
            jax.ShapeDtypeStruct((GROUPS, n, depth), low_type),
            jax.ShapeDtypeStruct((GROUPS, rows, width), low_type),
            jax.ShapeDtypeStruct((4, rows, depth), low_type),
            jax.ShapeDtypeStruct((tall, depth), wide),
            jax.ShapeDtypeStruct((rows, depth), wide),
        ),
        in_specs=[pl.BlockSpec(memory_space=pltpu.SMEM)] + [pl.BlockSpec(memory_space=vmem)] * 10,
        out_specs=[pl.BlockSpec(memory_space=pl.ANY)] * 3 + [pl.BlockSpec(memory_space=vmem)] * 2,
        scratch_shapes=[
            dma((total,)), dma((total,)), dma((4,)), dma((4,)), dma((4,)), dma, dma,
            dma((4,)), dma((4,)), dma((12,)), dma((12,)),
            vmem((LOCAL, 2 * block, LANES), low_type),
            vmem((2, 4, 2, 2, n, WIDE), low_type),
            vmem((4, 2, 2, n, WIDE), low_type),
            vmem((4, 3, n, WIDE), low_type),
            vmem((GROUPS, n, WIDE), wide),
            vmem((GROUPS, n, 2 * WIDE), low_type),
            vmem((GROUPS, n, width), low_type),
            vmem((GROUPS, n, depth), low_type),
            vmem((2, 2, GROUPS, 2, rows, width), low_type),
            vmem((2, GROUPS, 2, rows, width), low_type),
            vmem((3, GROUPS, rows, width), low_type),
            vmem((GROUPS, rows, width), low_type),
            vmem((3, 2, 2, rows, depth), low_type),
            vmem((2, 2, rows, depth), low_type),
            vmem((3, GROUPS, rows, depth), low_type),
            vmem((GROUPS, rows, depth), low_type),
            vmem((3, rows, depth), low_type),
            vmem((4, tall, depth), low_type),
            vmem((2, cut, width), wide),
        ],
        compiler_params=pltpu.CompilerParams(
            collective_id=11, has_side_effects=True, vmem_limit_bytes=TURN_LIMIT
        ),
    )(lengths, queries, keys, grads_in, mixed, lse, tokens, weights, sum1, sum2, summ)


def on_device_general(
    tokens,
    cotangent,
    doc_lengths,
    query_weight,
    query_bias,
    key_weight,
    value_weight,
    value_bias,
    mix_weight,
    mix_bias,
    early_gain,
    early_shift,
    inner_weight,
    inner_bias,
    outer_weight,
    outer_bias,
    final_gain,
    final_shift,
):
    n, depth = tokens.shape
    groups, cycle = lax.axis_size("au"), lax.axis_size("row")
    devices = groups * cycle
    zs = cycle // (2 * GROUPS)
    s = query_weight.shape[0]
    ff = inner_weight.shape[1]
    quarter = ff // 4
    e = outer_weight.shape[0]
    rows = GROUPS * n
    total_tokens = n * devices
    me = Place(zs)
    device = lax.axis_index("au") * cycle + lax.axis_index("row")
    w_me = me.x * 2 + me.y

    def by_head(weight):
        return weight.astype(low_type).reshape(-1, GROUPS, LOCAL, HEAD)

    def packed(query, key, value):
        kv = jnp.stack([key, value], axis=3).reshape(-1, GROUPS, WIDE)
        q = jnp.pad(query, ((0, 0), (0, 0), (0, 0), (0, HEAD))).reshape(-1, GROUPS, WIDE)
        return jnp.concatenate([kv, q], axis=2)

    slab = packed(by_head(query_weight), by_head(key_weight), by_head(value_weight))
    slab = jnp.transpose(slab, (1, 0, 2))
    small = jnp.concatenate(
        [
            vector.astype(low_type)
            for vector in (
                query_bias, value_bias, mix_bias, early_gain, early_shift,
                outer_bias, final_gain, final_shift, inner_bias,
            )
        ]
    )
    extra = -s % 8 or 8
    small = jnp.broadcast_to(
        jnp.pad(small, (0, 2 * WIDE - small.shape[0]))[None, None], (GROUPS, extra, 2 * WIDE)
    )
    slab = jnp.concatenate([slab, small], axis=1)
    tok_all, w_all = spread_tokens(zs, tokens, slab)
    tok_all = tok_all.reshape(rows, depth)
    w_qkv = w_all[..., :s, :].reshape(depth, 2 * WIDE)
    small = w_all[..., s, :].reshape(devices, 2 * WIDE)
    names = [small[:, i * s : (i + 1) * s].reshape(depth) for i in range(8)]
    q_bias, v_bias, m_bias, e_gain, e_shift, o_bias, f_gain, f_shift = names
    i_bias = small[:, 8 * s : 8 * s + e].reshape(4, quarter)[w_me].astype(wide)
    q_bias = q_bias.reshape(1, GROUPS, LOCAL, HEAD)
    v_bias = v_bias.reshape(1, GROUPS, LOCAL, HEAD)
    bias = packed(q_bias, jnp.zeros_like(q_bias), v_bias)[0, me.g].astype(wide)

    qkv = (jnp.dot(tok_all, w_qkv, preferred_element_type=wide) + bias).astype(low_type)
    queries = qkv[:, WIDE:]

    inner_slab = jnp.transpose(inner_weight.astype(low_type).reshape(s, 4, quarter), (1, 0, 2))
    kv_all, w1, w2, wm = spread_keys(
        zs,
        qkv[:, :WIDE].reshape(GROUPS, n, WIDE),
        inner_slab,
        outer_weight.astype(low_type),
        mix_weight.astype(low_type),
    )
    kv_all = kv_all.reshape(total_tokens, WIDE)
    w1 = w1.reshape(depth, quarter)
    w2 = w2.reshape(quarter, depth)
    wm = wm.reshape(depth, depth)

    tile, block = 128, 512
    count = doc_lengths.shape[0]
    upto = jnp.arange(count)[None, :] <= jnp.arange(count)[:, None]
    ends = jnp.sum(jnp.where(upto, doc_lengths[None, :], 0), axis=1)
    owners = ((me.x * 2 + me.c) * cycle + me.z * GROUPS * 2 + jnp.arange(GROUPS) * 2 + me.y) * n
    places = (owners[:, None] + jnp.arange(n)[None, :]).reshape(rows)
    before = ends[None, :] <= places[:, None]
    first = jnp.max(jnp.where(before, ends[None, :], 0), axis=1).astype(jnp.int32)
    last = jnp.min(jnp.where(before, total_tokens, ends[None, :]), axis=1).astype(jnp.int32)
    tiles = rows // tile
    bounds = jnp.stack(
        [
            first.reshape(tiles, tile)[:, 0] // block,
            (last.reshape(tiles, tile)[:, -1] + block - 1) // block,
        ],
        axis=1,
    )
    mixed, mixed_wide, lse = attend_forward(
        queries, kv_all, bounds, first[:, None], last[:, None], tile, block
    )
    mixed_tok = exchange_line(zs, 2, mixed.reshape(GROUPS, n, PACK))
    mixed_tok = jnp.transpose(mixed_tok[:, :, : LOCAL * HEAD], (1, 0, 2)).reshape(n, depth)

    attn = jnp.dot(mixed_tok, wm, preferred_element_type=wide) + m_bias.astype(wide)
    early, early_pull = jax.vjp(
        layer_norm, tokens.astype(wide) + attn, e_gain.astype(wide), e_shift.astype(wide)
    )
    early_all = gather_square(zs, 3, early.astype(low_type)).reshape(rows, depth)
    inner = jnp.dot(early_all, w1, preferred_element_type=wide) + i_bias
    act, gelu_pull = jax.vjp(gelu_exact, inner)
    act_low = act.astype(low_type)
    partial = jnp.dot(act_low, w2, preferred_element_type=wide).astype(low_type)
    partial = exchange_square(zs, 4, partial.reshape(2, 2, n, depth))
    branch = jnp.sum(partial.astype(wide), axis=(0, 1)) + o_bias.astype(wide)
    result, final_pull = jax.vjp(
        layer_norm, early + branch, f_gain.astype(wide), f_shift.astype(wide)
    )
    output = result.astype(low_type)
    final_grads = final_pull(cotangent.astype(wide))
    branch_grad = final_grads[0].astype(low_type)
    outer_bias_grad = jnp.sum(branch_grad.astype(wide), axis=0)
    branch_all = gather_square(zs, 5, branch_grad).reshape(rows, depth)
    act_grad = jnp.einsum("td,fd->tf", branch_all, w2, preferred_element_type=wide)
    inner_grad = gelu_pull(act_grad)[0].astype(low_type)
    partial = jnp.einsum("tf,df->td", inner_grad, w1, preferred_element_type=wide).astype(low_type)
    partial = exchange_square(zs, 6, partial.reshape(2, 2, n, depth))
    grad2 = jnp.einsum("tf,td->fd", act_low, branch_all, preferred_element_type=wide)
    grad1 = jnp.einsum("td,tf->df", early_all, inner_grad, preferred_element_type=wide)
    inner_bias_grad = jnp.sum(inner_grad.astype(wide), axis=0)
    early_grad = final_grads[0] + jnp.sum(partial.astype(wide), axis=(0, 1))
    early_grads = early_pull(early_grad)
    attn_grad = early_grads[0].astype(low_type)
    mixed_grad = jnp.einsum("td,cd->tc", attn_grad, wm, preferred_element_type=wide)
    mixed_grad = jnp.transpose(
        mixed_grad.astype(low_type).reshape(n, GROUPS, LOCAL * HEAD), (1, 0, 2)
    )
    mixed_grad = jnp.pad(mixed_grad, ((0, 0), (0, 0), (0, PACK - LOCAL * HEAD)))
    grad_all = exchange_line(zs, 7, mixed_grad).reshape(rows, PACK)
    gradm = jnp.einsum("tc,td->cd", mixed_tok, attn_grad, preferred_element_type=wide)
    mix_bias_grad = jnp.sum(attn_grad.astype(wide), axis=0)

    delta = jnp.sum(
        (grad_all.astype(wide) * mixed_wide)[:, : LOCAL * HEAD].reshape(rows, LOCAL, HEAD), axis=2
    )

    def as_stat(values):
        return jnp.transpose(values.reshape(tiles, tile, LOCAL), (0, 2, 1))

    def same_stat(values):
        return jnp.broadcast_to(
            values.astype(wide).reshape(tiles, 1, tile), (tiles, LOCAL, tile)
        )

    stats = jnp.stack(
        [same_stat(first), same_stat(last), as_stat(lse[:, :LOCAL]), as_stat(delta)], axis=2
    )
    stats = jnp.pad(stats, ((0, 0), (0, 0), (0, 4), (0, 0)))
    query_grad, dkv = attend_backward(queries, kv_all, grad_all, stats, bounds, tile, block)

    def slabs(grad, extras):
        grad = grad.astype(low_type).reshape(devices, s, -1)
        rest = -s % 8
        rest += 0 if rest >= extras.shape[0] else 8
        extras = jnp.concatenate(
            [extras.astype(low_type), jnp.zeros((rest - extras.shape[0], extras.shape[1]), low_type)]
        )
        extras = jnp.broadcast_to(extras[None], (devices,) + extras.shape)
        return jnp.concatenate([grad, extras], axis=1).reshape(2, 2, zs, GROUPS, 2, s + rest, -1)

    mix_extras = jnp.stack(
        [
            mix_bias_grad, early_grads[1], early_grads[2],
            outer_bias_grad, final_grads[1], final_grads[2],
        ]
    )
    dkv, out1, out2, outm = reduce_keys(
        zs,
        dkv.reshape(2, 2, zs, GROUPS, 2, n, WIDE),
        slabs(grad1, inner_bias_grad[None]),
        grad2.astype(low_type).reshape(zs, GROUPS, 2, e, depth),
        slabs(gradm, mix_extras),
    )
    key_grad = jnp.sum(dkv.astype(wide), axis=0).astype(low_type).reshape(rows, WIDE)
    grads = jnp.concatenate([key_grad, query_grad], axis=1)
    gradq = jnp.einsum("tc,td->cd", tok_all, grads, preferred_element_type=wide)
    bias_grad = jnp.sum(grads.astype(wide), axis=0)
    partial = jnp.einsum("td,cd->tc", grads, w_qkv, preferred_element_type=wide).astype(low_type)
    partial, outq = reduce_tokens(
        zs, partial.reshape(GROUPS, n, depth), slabs(gradq, bias_grad[None])
    )
    input_grad = early_grads[0] + jnp.sum(partial.astype(wide), axis=0)

    def own(vector, count):
        return lax.dynamic_slice_in_dim(vector, device * count, count, 0).astype(wide)

    outq = outq.astype(wide)
    kv_out = outq[:, :, :WIDE].reshape(GROUPS, -1, LOCAL, 2, HEAD)
    q_out = outq[:, :, WIDE:].reshape(GROUPS, -1, LOCAL, 2, HEAD)[:, :, :, 0]

    def unpacked(values):
        return jnp.transpose(values, (1, 0, 2, 3)).reshape(-1, depth)

    q_out, k_out, v_out = unpacked(q_out), unpacked(kv_out[:, :, :, 0]), unpacked(kv_out[:, :, :, 1])
    inner_out = jnp.transpose(out1[:, :s], (1, 0, 2)).reshape(s, ff).astype(wide)
    return (
        output,
        input_grad.astype(low_type),
        q_out[:s],
        own(q_out[s], s),
        k_out[:s],
        v_out[:s],
        own(v_out[s], s),
        outm[:s],
        own(outm[s], s),
        own(outm[s + 1], s),
        own(outm[s + 2], s),
        inner_out,
        own(out1[:, s].reshape(ff), e),
        out2,
        own(outm[s + 3], s),
        own(outm[s + 4], s),
        own(outm[s + 5], s),
    )


def on_device(
    tokens,
    cotangent,
    doc_lengths,
    query_weight,
    query_bias,
    key_weight,
    value_weight,
    value_bias,
    mix_weight,
    mix_bias,
    early_gain,
    early_shift,
    inner_weight,
    inner_bias,
    outer_weight,
    outer_bias,
    final_gain,
    final_shift,
):
    n, depth = tokens.shape
    cycle = lax.axis_size("row")
    devices = lax.axis_size("au") * cycle
    s = query_weight.shape[0]
    ff = inner_weight.shape[1]
    quarter = ff // 4
    e = outer_weight.shape[0]
    rows = GROUPS * n
    total_tokens = n * devices
    me = Spot()
    vectors = [
        vector.reshape(1, -1)
        for vector in (
            query_bias, value_bias, mix_bias, early_gain, early_shift,
            outer_bias, final_gain, final_shift,
        )
    ]
    vectors.append(inner_bias.reshape(1, -1))
    toks, queries, w_qkv, vec, kv_all, w1, wm, mixed, mixed_wide, lse = first_kernel(
        doc_lengths, tokens, query_weight, key_weight, value_weight, vectors,
        inner_weight, mix_weight, e,
    )
    queries = queries.reshape(rows, WIDE)
    kv_all = kv_all.reshape(total_tokens, WIDE)
    w_qkv = w_qkv.reshape(depth, -1)
    w1 = w1.reshape(depth, quarter)
    wm = wm.reshape(depth, depth)
    output, hidden_grad, grad_all, summ, sum1, sum2 = middle_kernel(
        mixed.reshape(GROUPS, n, PACK), tokens, cotangent, wm, w1, outer_weight, vec, s, e
    )
    grad_all = grad_all.reshape(rows, PACK)
    pieces, outqk, out1, out2, outm = turn_kernel(
        doc_lengths, queries, kv_all, grad_all, mixed_wide, lse, toks, w_qkv, sum1, sum2, summ
    )
    results = final_kernel(output, hidden_grad, pieces, outqk, out1, out2, outm, s, e)
    return tuple(
        result.reshape(-1) if result.shape[0] == 1 else result for result in results
    )


def solution(mesh):
    both = P(("au", "row"), None)
    flat = P(("au", "row"))
    in_specs = (
        both, both, P(), both, flat, both, both, flat, both, flat, flat, flat,
        both, flat, both, flat, flat, flat,
    )
    out_specs = (
        both, both, both, flat, both, both, flat, both, flat, flat, flat,
        both, flat, both, flat, flat, flat,
    )
    fast = mesh.shape["au"] == 4 and mesh.shape["row"] == 2 * GROUPS
    return jax.shard_map(
        on_device if fast else on_device_general, mesh=mesh, in_specs=in_specs, out_specs=out_specs, check_vma=False
    )
```

```python
import functools

import jax
import jax.numpy as jnp
import numpy as np
from jax import lax
from jax.experimental import pallas as pl
from jax.experimental.pallas import tpu as pltpu
from jax.sharding import PartitionSpec as P

HEAD = 64
HEADS = 12
GROUPS = 4
LOCAL = HEADS // GROUPS
LANES = 2 * HEAD
WIDE = LOCAL * LANES
PACK = 256
eps_norm = 1e-06
mask_fill = -1000000000.0
lowest_start = -1e30
low_type = jnp.bfloat16
wide = jnp.float32
MESH = pl.DeviceIdType.MESH
VMEM_LIMIT = 62 * 1024 * 1024
NEAR_LIMIT = 30 * 1024 * 1024
TURN_LIMIT = 48 * 1024 * 1024


def layer_norm(hidden, gain, shift):
    mean = jnp.mean(hidden, axis=-1, keepdims=True)
    centered = hidden - mean
    spread = jnp.mean(centered * centered, axis=-1, keepdims=True)
    return centered * lax.rsqrt(spread + eps_norm) * gain + shift


def gelu_exact(values):
    return jax.nn.gelu(values, approximate=False)


class Place:
    def __init__(self, zs):
        self.zs = zs
        a = lax.axis_index("au")
        r = lax.axis_index("row")
        self.x, self.c = a // 2, a % 2
        self.y, q = r % 2, r // 2
        self.g, self.z = q % GROUPS, q // GROUPS

    def at(self, x=None, c=None, z=None, g=None, y=None):
        x = self.x if x is None else x
        c = self.c if c is None else c
        z = self.z if z is None else z
        g = self.g if g is None else g
        y = self.y if y is None else y
        return (x * 2 + c, (z * GROUPS + g) * 2 + y)

    def sibling(self):
        return self.at(c=1 - self.c)

    def line(self):
        return [((self.g + k) % GROUPS, (self.g + GROUPS - k) % GROUPS) for k in range(1, GROUPS)]

    def column(self):
        count = self.zs * GROUPS
        q = self.z * GROUPS + self.g
        result = []
        for k in range(1, count):
            to, source = (q + k) % count, (q + count - k) % count
            result.append(((to // GROUPS, to % GROUPS), (source // GROUPS, source % GROUPS)))
        return result

    def plane(self, everywhere=True):
        result = []
        for dx in range(2):
            for dy in range(2):
                for dz in range(self.zs if everywhere else 1):
                    if dx + dy + dz == 0:
                        continue
                    to = ((self.x + dx) % 2, (self.z + dz) % self.zs, (self.y + dy) % 2)
                    source = (
                        (self.x + dx) % 2,
                        (self.z + self.zs - dz) % self.zs,
                        (self.y + dy) % 2,
                    )
                    result.append((to, source))
        return result


class Copies:
    def __init__(self, send, recv, local):
        self.send, self.recv, self.local = send, recv, local
        self.count = 0
        self.local_count = 0
        self.started = []
        self.local_started = []

    def push(self, source, target, device):
        copy = pltpu.make_async_remote_copy(
            src_ref=source,
            dst_ref=target,
            send_sem=self.send.at[self.count],
            recv_sem=self.recv.at[self.count],
            device_id=device,
            device_id_type=MESH,
        )
        self.count += 1
        copy.start()
        self.started.append(copy)
        return copy

    def keep(self, source, target):
        copy = pltpu.make_async_copy(source, target, self.local.at[self.local_count])
        self.local_count += 1
        copy.start()
        return copy

    def finish(self):
        for copy in self.started:
            copy.wait_send()


def greet(devices, partner=None, crossing=None):
    barrier = pltpu.get_barrier_semaphore()
    for device in devices:
        pl.semaphore_signal(barrier, inc=1, device_id=device, device_id_type=MESH)
    if partner is None:
        pl.semaphore_wait(barrier, len(devices))
        return

    @pl.when(crossing)
    def _():
        pl.semaphore_signal(barrier, inc=1, device_id=partner, device_id_type=MESH)
        pl.semaphore_wait(barrier, len(devices) + 1)

    @pl.when(jnp.logical_not(crossing))
    def _():
        pl.semaphore_wait(barrier, len(devices))


def comm_call(body, name, ident, outs, copies, locals_, args, spaces=None, out_spaces=None, scratch=()):
    spaces = [pl.ANY] * len(args) if spaces is None else spaces
    out_spaces = [pl.ANY] * len(outs) if out_spaces is None else out_spaces
    return pl.pallas_call(
        body,
        name=name,
        out_shape=tuple(outs),
        in_specs=[pl.BlockSpec(memory_space=space) for space in spaces],
        out_specs=tuple(pl.BlockSpec(memory_space=space) for space in out_spaces),
        scratch_shapes=[
            pltpu.SemaphoreType.DMA((max(copies, 1),)),
            pltpu.SemaphoreType.DMA((max(copies, 1),)),
            pltpu.SemaphoreType.DMA((max(locals_, 1),)),
            *scratch,
        ],
        compiler_params=pltpu.CompilerParams(
            collective_id=ident, has_side_effects=True, vmem_limit_bytes=VMEM_LIMIT
        ),
    )(*args)


def spread_tokens(zs, tokens, slab):
    n, width = tokens.shape
    groups, rows, columns = slab.shape
    plane = 4 * zs - 1

    def body(tok, piece, tok_all, w_all, send, recv, local):
        me = Place(zs)
        copies = Copies(send, recv, local)
        greet(
            [me.at(g=to) for to, _ in me.line()]
            + [me.at(x=to[0], z=to[1], y=to[2]) for to, _ in me.plane()]
            + [me.sibling()]
        )
        first = [
            copies.push(
                piece.at[to], w_all.at[me.x, me.c, me.z, me.g, me.y], me.at(g=to)
            )
            for to, _ in me.line()
        ]
        own = copies.keep(piece.at[me.g], w_all.at[me.x, me.c, me.z, me.g, me.y])
        arrivals = [copies.push(tok, tok_all.at[me.g], me.at(g=to)) for to, _ in me.line()]
        mine = copies.keep(tok, tok_all.at[me.g])
        own.wait()
        for copy in first:
            copy.wait_recv()
        block = w_all.at[me.x, me.c, me.z, :, me.y]
        second = [
            copies.push(block, block, me.at(x=to[0], z=to[1], y=to[2])) for to, _ in me.plane()
        ]
        arrivals.append(copies.push(block, block, me.sibling()))
        for copy, (_, source) in zip(second, me.plane()):
            copy.wait_recv()
            part = w_all.at[source[0], me.c, source[1], :, source[2]]
            arrivals.append(copies.push(part, part, me.sibling()))
        for copy in arrivals:
            copy.wait_recv()
        mine.wait()
        copies.finish()

    return comm_call(
        body,
        "spread_tokens",
        0,
        [
            jax.ShapeDtypeStruct((GROUPS, n, width), low_type),
            jax.ShapeDtypeStruct((2, 2, zs, GROUPS, 2, rows, columns), low_type),
        ],
        2 * (GROUPS - 1) + 2 * plane + 1,
        2,
        (tokens, slab),
    )


def spread_keys(zs, keys, inner, outer, mix):
    groups, n, width = keys.shape
    quarters, rows, columns = inner.shape
    tall, _ = outer.shape
    plane, column = 4 * zs - 1, GROUPS * zs - 1

    def body(kv, w1s, w2s, wms, kv_all, w1, w2, wm, send, recv, local, swap_send, swap_recv):
        me = Place(zs)
        copies = Copies(send, recv, local)
        crossing = me.c != me.y
        greet(
            [me.at(x=to[0], z=to[1], y=to[2]) for to, _ in me.plane()]
            + [me.at(z=to[0], g=to[1]) for to, _ in me.column()]
            + [me.at(z=to[0], g=to[1], c=me.y, y=me.c) for to, _ in me.column()]
            + [me.sibling()],
            me.at(c=me.y, y=me.c),
            crossing,
        )

        def here(ref):
            return ref.at[me.x, me.c, me.z, me.g, me.y]

        flat = me.plane(everywhere=False)
        own = [
            copies.keep(w1s.at[me.x * 2 + me.y], here(w1)),
            copies.keep(wms, here(wm)),
            copies.keep(kv, kv_all.at[me.x, me.c, me.z, :, me.y]),
        ]
        w1_first = [
            copies.push(w1s.at[to[0] * 2 + to[2]], here(w1), me.at(x=to[0], y=to[2]))
            for to, _ in flat
        ]
        wm_first = [
            copies.push(wms, here(wm), me.at(z=to[0], g=to[1])) for to, _ in me.column()
        ]
        mine = kv_all.at[me.x, me.c, me.z, :, me.y]
        kv_first = [
            copies.push(kv, mine, me.at(x=to[0], z=to[1], y=to[2])) for to, _ in me.plane()
        ]
        arrivals = [copies.push(kv, mine, me.sibling())]
        w2_first = [
            copies.push(
                w2s, w2.at[me.z, me.g, me.y], me.at(z=to[0], g=to[1], c=me.y, y=me.c)
            )
            for to, _ in me.column()
        ]
        exchanged = pltpu.make_async_remote_copy(
            src_ref=w2s,
            dst_ref=w2.at[me.z, me.g, me.y],
            send_sem=swap_send,
            recv_sem=swap_recv,
            device_id=me.at(c=me.y, y=me.c),
            device_id_type=MESH,
        )
        stays = pltpu.make_async_copy(w2s, w2.at[me.z, me.g, me.y], swap_recv)

        @pl.when(crossing)
        def _():
            exchanged.start()

        @pl.when(jnp.logical_not(crossing))
        def _():
            stays.start()

        own[0].wait()
        for copy in w1_first:
            copy.wait_recv()
        block = w1.at[:, me.c, me.z, me.g, :]
        w1_second = [
            copies.push(block, block, me.at(z=to[0], g=to[1])) for to, _ in me.column()
        ]
        arrivals.append(copies.push(block, block, me.sibling()))
        own[1].wait()
        for copy in wm_first:
            copy.wait_recv()
        block = wm.at[me.x, me.c, :, :, me.y]
        wm_second = [copies.push(block, block, me.at(x=to[0], y=to[2])) for to, _ in flat]
        arrivals.append(copies.push(block, block, me.sibling()))
        for copy, (_, source) in zip(kv_first, me.plane()):
            copy.wait_recv()
            part = kv_all.at[source[0], me.c, source[1], :, source[2]]
            arrivals.append(copies.push(part, part, me.sibling()))

        @pl.when(crossing)
        def _():
            exchanged.wait_recv()
            exchanged.wait_send()

        @pl.when(jnp.logical_not(crossing))
        def _():
            stays.wait()

        part = w2.at[me.z, me.g, me.c]
        arrivals.append(copies.push(part, part, me.sibling()))
        for copy, (_, source) in zip(wm_second, flat):
            copy.wait_recv()
            part = wm.at[source[0], me.c, :, :, source[2]]
            arrivals.append(copies.push(part, part, me.sibling()))
        for copy, (_, source) in zip(w2_first, me.column()):
            copy.wait_recv()
            part = w2.at[source[0], source[1], me.c]
            arrivals.append(copies.push(part, part, me.sibling()))
        for copy, (_, source) in zip(w1_second, me.column()):
            copy.wait_recv()
            part = w1.at[:, me.c, source[0], source[1], :]
            arrivals.append(copies.push(part, part, me.sibling()))
        for copy in arrivals:
            copy.wait_recv()
        own[2].wait()
        copies.finish()

    return comm_call(
        body,
        "spread_keys",
        1,
        [
            jax.ShapeDtypeStruct((2, 2, zs, GROUPS, 2, n, width), low_type),
            jax.ShapeDtypeStruct((2, 2, zs, GROUPS, 2, rows, columns), low_type),
            jax.ShapeDtypeStruct((zs, GROUPS, 2, tall, columns), low_type),
            jax.ShapeDtypeStruct((2, 2, zs, GROUPS, 2) + mix.shape, low_type),
        ],
        2 * plane + 1 + 2 * (3 + column + 1 + column) + column + 3 + 8,
        3,
        (keys, inner, outer, mix),
        scratch=(pltpu.SemaphoreType.DMA, pltpu.SemaphoreType.DMA),
    )


def exchange_line(zs, ident, pieces):
    def body(source, target, send, recv, local):
        me = Place(zs)
        copies = Copies(send, recv, local)
        greet([me.at(g=to) for to, _ in me.line()])
        arrivals = [
            copies.push(source.at[to], target.at[me.g], me.at(g=to)) for to, _ in me.line()
        ]
        own = copies.keep(source.at[me.g], target.at[me.g])
        for copy in arrivals:
            copy.wait_recv()
        own.wait()
        copies.finish()

    return comm_call(
        body,
        "exchange_line",
        ident,
        [jax.ShapeDtypeStruct(pieces.shape, pieces.dtype)],
        GROUPS - 1,
        1,
        (pieces,),
    )[0]


def gather_square(zs, ident, rows):
    def body(source, target, send, recv, local):
        me = Place(zs)
        copies = Copies(send, recv, local)
        flat = me.plane(everywhere=False)
        greet([me.at(x=to[0], y=to[2]) for to, _ in flat])
        place = target.at[me.x, me.y]
        arrivals = [copies.push(source, place, me.at(x=to[0], y=to[2])) for to, _ in flat]
        own = copies.keep(source, place)
        for copy in arrivals:
            copy.wait_recv()
        own.wait()
        copies.finish()

    return comm_call(
        body,
        "gather_square",
        ident,
        [jax.ShapeDtypeStruct((2, 2) + rows.shape, rows.dtype)],
        3,
        1,
        (rows,),
    )[0]


def exchange_square(zs, ident, pieces):
    def body(source, target, send, recv, local):
        me = Place(zs)
        copies = Copies(send, recv, local)
        flat = me.plane(everywhere=False)
        greet([me.at(x=to[0], y=to[2]) for to, _ in flat])
        place = target.at[me.x, me.y]
        arrivals = [
            copies.push(source.at[to[0], to[2]], place, me.at(x=to[0], y=to[2]))
            for to, _ in flat
        ]
        own = copies.keep(source.at[me.x, me.y], place)
        for copy in arrivals:
            copy.wait_recv()
        own.wait()
        copies.finish()

    return comm_call(
        body,
        "exchange_square",
        ident,
        [jax.ShapeDtypeStruct(pieces.shape, pieces.dtype)],
        3,
        1,
        (pieces,),
    )[0]


def loop(count, step):
    def body(index, carry):
        step(index)
        return carry

    lax.fori_loop(0, count, body, 0)


def total_of(*values):
    result = values[0].astype(wide)
    for value in values[1:]:
        result = result + value.astype(wide)
    return result


def reduce_keys(zs, dkv, grad1, grad2, gradm):
    n, width = dkv.shape[-2:]
    rows, columns = grad1.shape[-2:]
    rowsm = gradm.shape[-2]
    tall = grad2.shape[-2]
    plane, column = 4 * zs - 1, GROUPS * zs - 1
    count = GROUPS * zs

    def body(
        dkv_ref, g1, g2, gm, dkv_out, out1, out2, outm,
        send, recv, local,
        swap_send, swap_recv, kst, s1, p1, f1, s2, p2, sm, pm, fm, tm,
    ):
        me = Place(zs)
        copies = Copies(send, recv, local)
        crossing = me.c != me.y
        greet(
            [me.at(x=to[0], z=to[1], y=to[2]) for to, _ in me.plane()]
            + [me.at(z=to[0], g=to[1]) for to, _ in me.column()]
            + [me.at(z=to[0], g=to[1], c=me.y, y=me.c) for to, _ in me.column()]
            + [me.sibling()],
            me.at(c=me.y, y=me.c),
            crossing,
        )

        flat = me.plane(everywhere=False)
        other = 1 - me.c
        order = [to for to, _ in me.plane()] + [(me.x, me.z, me.y)]
        w1_half = copies.push(g1.at[:, other], s1, me.sibling())
        w2_half = copies.push(g2.at[:, :, other], s2, me.sibling())
        k_half = [
            copies.push(
                dkv_ref.at[to[0], other, to[1], :, to[2]], kst.at[to[0], to[1], to[2]], me.sibling()
            )
            for to in order
        ]
        wm_half = copies.push(gm.at[:, other], sm, me.sibling())

        w1_half.wait_recv()

        def add1(index):
            x, z, g, y = index // (count * 2), index // (GROUPS * 2) % zs, index // 2 % GROUPS, index % 2
            s1[x, z, g, y] = total_of(s1[x, z, g, y], g1[x, me.c, z, g, y]).astype(low_type)

        loop(4 * count, add1)
        w1_push = [
            copies.push(s1.at[:, to[0], to[1], :], p1.at[slot], me.at(z=to[0], g=to[1]))
            for slot, (to, _) in enumerate(me.column())
        ]
        w2_half.wait_recv()

        def add2(index):
            z, g = index // GROUPS, index % GROUPS
            s2[z, g] = total_of(s2[z, g], g2[z, g, me.c]).astype(low_type)

        loop(count, add2)
        w2_push = [
            copies.push(
                s2.at[to[0], to[1]], p2.at[slot + 1], me.at(z=to[0], g=to[1], c=me.y, y=me.c)
            )
            for slot, (to, _) in enumerate(me.column())
        ]
        exchanged = pltpu.make_async_remote_copy(
            src_ref=s2.at[me.z, me.g],
            dst_ref=p2.at[0],
            send_sem=swap_send,
            recv_sem=swap_recv,
            device_id=me.at(c=me.y, y=me.c),
            device_id_type=MESH,
        )
        stays = pltpu.make_async_copy(s2.at[me.z, me.g], p2.at[0], swap_recv)

        @pl.when(crossing)
        def _():
            exchanged.start()

        @pl.when(jnp.logical_not(crossing))
        def _():
            stays.start()

        k_push = []
        for slot, to in enumerate(order):
            k_half[slot].wait_recv()

            def addk(g, to=to):
                kst[to[0], to[1], to[2], g] = total_of(
                    kst[to[0], to[1], to[2], g], dkv_ref[to[0], me.c, to[1], g, to[2]]
                ).astype(low_type)

            loop(GROUPS, addk)
            if slot < plane:
                k_push.append(
                    copies.push(
                        kst.at[to[0], to[1], to[2]],
                        dkv_out.at[slot],
                        me.at(x=to[0], z=to[1], y=to[2]),
                    )
                )
        wm_half.wait_recv()

        def addm(index):
            x, z, g, y = index // (count * 2), index // (GROUPS * 2) % zs, index // 2 % GROUPS, index % 2
            sm[x, z, g, y] = total_of(sm[x, z, g, y], gm[x, me.c, z, g, y]).astype(low_type)

        loop(4 * count, addm)
        wm_push = [
            copies.push(sm.at[to[0], :, :, to[2]], pm.at[slot], me.at(x=to[0], y=to[2]))
            for slot, (to, _) in enumerate(flat)
        ]
        keep = copies.keep(kst.at[me.x, me.z, me.y], dkv_out.at[plane])
        for copy in wm_push:
            copy.wait_recv()

        def addf(index):
            z, g = index // GROUPS, index % GROUPS
            fm[z, g] = total_of(sm[me.x, z, g, me.y], pm[0, z, g], pm[1, z, g], pm[2, z, g]).astype(
                low_type
            )

        loop(count, addf)
        wm_last = [
            copies.push(fm.at[to[0], to[1]], tm.at[slot], me.at(z=to[0], g=to[1]))
            for slot, (to, _) in enumerate(me.column())
        ]
        for copy in w1_push:
            copy.wait_recv()

        def addg(index):
            x, y = index // 2, index % 2
            f1[x, y] = total_of(
                s1[x, me.z, me.g, y], *[p1[slot, x, y] for slot in range(column)]
            ).astype(low_type)

        loop(4, addg)
        quarter = out1.at[me.x * 2 + me.y]
        w1_last = [
            copies.push(f1.at[to[0], to[2]], quarter, me.at(x=to[0], y=to[2])) for to, _ in flat
        ]
        keep1 = copies.keep(f1.at[me.x, me.y], quarter)

        @pl.when(crossing)
        def _():
            exchanged.wait_recv()
            exchanged.wait_send()

        @pl.when(jnp.logical_not(crossing))
        def _():
            stays.wait()

        for copy in w2_push:
            copy.wait_recv()
        out2[...] = total_of(*[p2[slot] for slot in range(column + 1)])
        for copy in wm_last:
            copy.wait_recv()
        outm[...] = total_of(fm[me.z, me.g], *[tm[slot] for slot in range(column)])
        for copy in w1_last + k_push:
            copy.wait_recv()
        keep.wait()
        keep1.wait()
        copies.finish()

    vmem = pltpu.VMEM
    return comm_call(
        body,
        "reduce_keys",
        8,
        [
            jax.ShapeDtypeStruct((plane + 1, GROUPS, n, width), low_type),
            jax.ShapeDtypeStruct((4, rows, columns), low_type),
            jax.ShapeDtypeStruct((tall, columns), wide),
            jax.ShapeDtypeStruct((rowsm, columns), wide),
        ],
        3 + (plane + 1) + 2 * column + plane + 3 + column + 3,
        2,
        (dkv, grad1, grad2, gradm),
        spaces=[vmem] * 4,
        out_spaces=[pl.ANY, pl.ANY, vmem, vmem],
        scratch=(
            pltpu.SemaphoreType.DMA,
            pltpu.SemaphoreType.DMA,
            vmem((2, zs, 2, GROUPS, n, width), low_type),
            vmem((2, zs, GROUPS, 2, rows, columns), low_type),
            vmem((column, 2, 2, rows, columns), low_type),
            vmem((2, 2, rows, columns), low_type),
            vmem((zs, GROUPS, tall, columns), low_type),
            vmem((column + 1, tall, columns), low_type),
            vmem((2, zs, GROUPS, 2, rowsm, columns), low_type),
            vmem((3, zs, GROUPS, rowsm, columns), low_type),
            vmem((zs, GROUPS, rowsm, columns), low_type),
            vmem((column, rowsm, columns), low_type),
        ),
    )


def reduce_tokens(zs, dx, gradq):
    rows, columns = gradq.shape[-2:]
    plane = 4 * zs - 1
    count = GROUPS * zs

    def body(dx_ref, gq, dx_out, outq, send, recv, local, sq, pq, fq):
        me = Place(zs)
        copies = Copies(send, recv, local)
        greet(
            [me.at(g=to) for to, _ in me.line()]
            + [me.at(x=to[0], z=to[1], y=to[2]) for to, _ in me.plane()]
            + [me.sibling()]
        )
        half = copies.push(gq.at[:, 1 - me.c], sq, me.sibling())
        arrivals = [
            copies.push(dx_ref.at[to], dx_out.at[me.g], me.at(g=to)) for to, _ in me.line()
        ]
        own = copies.keep(dx_ref.at[me.g], dx_out.at[me.g])
        half.wait_recv()

        def add1(index):
            x, z, g, y = index // (count * 2), index // (GROUPS * 2) % zs, index // 2 % GROUPS, index % 2
            sq[x, z, g, y] = total_of(sq[x, z, g, y], gq[x, me.c, z, g, y]).astype(low_type)

        loop(4 * count, add1)
        second = [
            copies.push(
                sq.at[to[0], to[1], :, to[2]], pq.at[slot], me.at(x=to[0], z=to[1], y=to[2])
            )
            for slot, (to, _) in enumerate(me.plane())
        ]
        for copy in second:
            copy.wait_recv()

        def add2(g):
            fq[g] = total_of(
                sq[me.x, me.z, g, me.y], *[pq[slot, g] for slot in range(plane)]
            ).astype(low_type)

        loop(GROUPS, add2)
        arrivals += [
            copies.push(fq.at[to], outq.at[me.g], me.at(g=to)) for to, _ in me.line()
        ]
        keep = copies.keep(fq.at[me.g], outq.at[me.g])
        for copy in arrivals:
            copy.wait_recv()
        own.wait()
        keep.wait()
        copies.finish()

    vmem = pltpu.VMEM
    return comm_call(
        body,
        "reduce_tokens",
        9,
        [
            jax.ShapeDtypeStruct(dx.shape, low_type),
            jax.ShapeDtypeStruct((GROUPS, rows, columns), low_type),
        ],
        1 + 2 * (GROUPS - 1) + plane,
        2,
        (dx, gradq),
        spaces=[pl.ANY, vmem],
        scratch=(
            vmem((2, zs, GROUPS, 2, rows, columns), low_type),
            vmem((plane, GROUPS, rows, columns), low_type),
            vmem((GROUPS, rows, columns), low_type),
        ),
    )


NEXT = (((1,), (1,)), ((), ()))
DOWN = (((0,), (0,)), ((), ()))


def attend_forward(queries, keys, bounds, low, high, tile, block):
    total_rows = queries.shape[0]

    def body(bounds_ref, q_ref, kv_ref, low_ref, high_ref, out_ref, keep_ref, lse_ref):
        def one(turn, unused):
            rows = pl.ds(pl.multiple_of(turn * tile, tile), tile)
            first, last = low_ref[rows, :], high_ref[rows, :]
            heads = [
                q_ref[rows, h * LANES : (h + 1) * LANES] * jnp.asarray(0.125, low_type)
                for h in range(LOCAL)
            ]

            def step(j, carry):
                begin = pl.multiple_of(j * block, block)
                place = begin + lax.broadcasted_iota(jnp.int32, (tile, block), 1)
                same = (place >= first) & (place < last)
                result = []
                for h in range(LOCAL):
                    top, total, mixed = carry[h]
                    kv = kv_ref[pl.ds(begin, block), h * LANES : (h + 1) * LANES]
                    scores = lax.dot_general(heads[h], kv, NEXT, preferred_element_type=wide)
                    scores = jnp.where(same, scores, mask_fill)
                    new_top = jnp.maximum(top, jnp.max(scores, axis=1, keepdims=True))
                    factor = jnp.exp(top - new_top)
                    powers = jnp.exp(scores - new_top)
                    total = total * factor + jnp.sum(powers, axis=1, keepdims=True)
                    mixed = mixed * factor + jnp.dot(
                        powers.astype(low_type), kv, preferred_element_type=wide
                    )
                    result.append((new_top, total, mixed))
                return tuple(result)

            start = tuple(
                (
                    jnp.full((tile, 1), lowest_start, wide),
                    jnp.zeros((tile, 1), wide),
                    jnp.zeros((tile, LANES), wide),
                )
                for _ in range(LOCAL)
            )
            done = lax.fori_loop(bounds_ref[turn, 0], bounds_ref[turn, 1], step, start)
            lane = lax.broadcasted_iota(jnp.int32, (tile, LANES), 1)
            upper = lane >= HEAD
            mixes = [mixed / total for _, total, mixed in done]
            turned = [pltpu.roll(mixed, HEAD, 1) for mixed in mixes]
            front = jnp.where(upper, mixes[1], turned[0])
            back = jnp.where(upper, 0.0, turned[2])
            both = jnp.concatenate([front, back], axis=1)
            keep_ref[rows, :] = both
            out_ref[rows, :] = both.astype(low_type)
            ends = [top + jnp.log(total) for top, total, _ in done]
            lse_ref[rows, :] = jnp.where(lane == 0, ends[0], jnp.where(lane == 1, ends[1], ends[2]))
            return unused

        lax.fori_loop(0, total_rows // tile, one, 0)

    vmem = pl.BlockSpec(memory_space=pltpu.VMEM)
    return pl.pallas_call(
        body,
        name="attend_forward",
        out_shape=(
            jax.ShapeDtypeStruct((total_rows, PACK), low_type),
            jax.ShapeDtypeStruct((total_rows, PACK), wide),
            jax.ShapeDtypeStruct((total_rows, LANES), wide),
        ),
        in_specs=[pl.BlockSpec(memory_space=pltpu.SMEM)] + [vmem] * 4,
        out_specs=(vmem,) * 3,
        compiler_params=pltpu.CompilerParams(vmem_limit_bytes=VMEM_LIMIT),
    )(bounds, queries, keys, low, high)


def attend_backward(queries, keys, grads, stats, bounds, tile, block):
    total_rows = queries.shape[0]
    tokens = keys.shape[0]

    def body(bounds_ref, q_ref, kv_ref, do_ref, stat_ref, dq_ref, dkv_ref, sums):
        h = pl.program_id(0)
        zeros = jnp.zeros((block, LANES), wide)

        def clear(j, unused):
            sums[pl.ds(pl.multiple_of(j * block, block), block), :] = zeros
            return unused

        lax.fori_loop(0, tokens // block, clear, 0)
        lane = lax.broadcasted_iota(jnp.int32, (tile, LANES), 1)
        upper = lane >= HEAD

        def one(turn, unused):
            rows = pl.ds(pl.multiple_of(turn * tile, tile), tile)
            q = q_ref[rows, :] * jnp.asarray(0.125, low_type)
            front = do_ref[rows, :LANES].astype(wide)
            back = do_ref[rows, LANES:].astype(wide)
            grad = jnp.where(h == 1, front, pltpu.roll(jnp.where(h == 0, front, back), HEAD, 1))
            grad = jnp.where(upper, grad, 0.0).astype(low_type)
            stat = stat_ref[turn, 0]
            first, last = stat[0:1, :], stat[1:2, :]
            lse, delta = stat[2:3, :], stat[3:4, :]

            def step(j, total):
                begin = pl.multiple_of(j * block, block)
                place = (begin + lax.broadcasted_iota(jnp.int32, (block, tile), 0)).astype(wide)
                same = (place >= first) & (place < last)
                kv = kv_ref[pl.ds(begin, block), :]
                scores = lax.dot_general(kv, q, NEXT, preferred_element_type=wide)
                probs = jnp.exp(jnp.where(same, scores, mask_fill) - lse)
                dots = lax.dot_general(kv, grad, NEXT, preferred_element_type=wide)
                score_grad = (probs * (dots - delta)).astype(low_type)
                sums[pl.ds(begin, block), :] += jnp.dot(
                    score_grad, q, preferred_element_type=wide
                ) + jnp.dot(probs.astype(low_type), grad, preferred_element_type=wide)
                return total + lax.dot_general(score_grad, kv, DOWN, preferred_element_type=wide)

            total = lax.fori_loop(
                bounds_ref[turn, 0], bounds_ref[turn, 1], step, jnp.zeros((tile, LANES), wide)
            )
            dq_ref[rows, :] = jnp.where(upper, 0.0, total * 0.125).astype(low_type)
            return unused

        lax.fori_loop(0, total_rows // tile, one, 0)

        def store(j, unused):
            part = pl.ds(pl.multiple_of(j * block, block), block)
            dkv_ref[part, :] = sums[part, :].astype(low_type)
            return unused

        lax.fori_loop(0, tokens // block, store, 0)

    return pl.pallas_call(
        body,
        name="attend_backward",
        grid=(LOCAL,),
        out_shape=(
            jax.ShapeDtypeStruct((total_rows, WIDE), low_type),
            jax.ShapeDtypeStruct((tokens, WIDE), low_type),
        ),
        in_specs=[
            pl.BlockSpec(memory_space=pltpu.SMEM),
            pl.BlockSpec((total_rows, LANES), lambda h: (0, h)),
            pl.BlockSpec((tokens, LANES), lambda h: (0, h)),
            pl.BlockSpec((total_rows, PACK), lambda h: (0, 0)),
            pl.BlockSpec((total_rows // tile, 1, 8, tile), lambda h: (0, h, 0, 0)),
        ],
        out_specs=(
            pl.BlockSpec((total_rows, LANES), lambda h: (0, h)),
            pl.BlockSpec((tokens, LANES), lambda h: (0, h)),
        ),
        scratch_shapes=[pltpu.VMEM((tokens, LANES), wide)],
        compiler_params=pltpu.CompilerParams(vmem_limit_bytes=VMEM_LIMIT),
    )(bounds, queries, keys, grads, stats)


class Spot(Place):
    def __init__(self):
        super().__init__(1)
        self.half = self.g // 2
        self.a = self.x * 2 + self.c
        self.p = (self.x + self.c) % 2
        self.selfish = self.g % 2 == self.p
        self.crossing = self.c != self.y

    def square(self):
        return [(to[0], to[2]) for to, _ in self.plane()]

    def readers(self):
        result = []
        for k in range(GROUPS):
            g = (self.g + k) % GROUPS
            result.append((g, self.at(x=(self.g + self.c) % 2, g=g)))
        return result

    def owners(self):
        result = []
        for dv in range(2):
            for du in range(2):
                u, v = (self.x + du) % 2, (self.half + dv) % 2
                result.append((u * 2 + v, self.at(x=u, g=2 * v + self.p)))
        return result

    def slot(self):
        return self.x * 2 + self.half


def count_of(flag):
    return jnp.where(flag, 1, 0)


def announce(always, maybe):
    barrier = pltpu.get_barrier_semaphore()
    for device in always:
        pl.semaphore_signal(barrier, inc=1, device_id=device, device_id_type=MESH)
    for flag, device in maybe:

        @pl.when(flag)
        def _(device=device):
            pl.semaphore_signal(barrier, inc=1, device_id=device, device_id_type=MESH)

    total = len(always)
    for flag, _ in maybe:
        total = total + count_of(flag)
    return barrier, total


class Scatter:
    def __init__(self, send, recv, here):
        self.send, self.recv, self.here = send, recv, here
        self.copies = []

    def start(self, pieces, target, slot):
        for source, device in pieces:
            self.send_one(source, target, slot, device)

    def send_one(self, source, target, slot, device):
        index = len(self.copies)
        copy = pltpu.make_async_remote_copy(
            src_ref=source,
            dst_ref=target,
            send_sem=self.send.at[index],
            recv_sem=self.recv.at[slot],
            device_id=device,
            device_id_type=MESH,
        )
        self.copies.append(copy)
        if index:
            copy.start()
            return
        stay = pltpu.make_async_copy(source, target, self.recv.at[slot])

        @pl.when(self.here)
        def _():
            stay.start()

        @pl.when(jnp.logical_not(self.here))
        def _():
            copy.start()

    def arrived(self, slot, target):
        pltpu.make_async_copy(target, target, self.recv.at[slot]).wait()

    def finish(self):
        for copy in self.copies[1:]:
            copy.wait_send()

        @pl.when(jnp.logical_not(self.here))
        def _():
            self.copies[0].wait_send()


SMALL = 16


def first_tables(s, e, width):
    column = np.arange(width)
    rows = [column % s, column // s, column % e, column // e]
    return np.stack(rows + [np.zeros_like(column)] * 4).astype(np.int32)


def first_kernel(lengths, tokens, wq, wk, wv, vectors, inner, mix, e):
    n, depth = tokens.shape
    s = wq.shape[0]
    quarter = inner.shape[1] // 4
    width = WIDE + PACK
    cols = width + LANES
    tables = jnp.asarray(first_tables(s, e, 2 * WIDE))
    count = len(vectors)

    def body(*refs):
        lengths_in, tok = refs[:2]
        arguments = refs[2 : 8 + count]
        (
            tok_out, q_out, wqkv_out, vec_out, kv_out, w1, wm, mixed_out, mixed_wide, lse_out,
            send, recv, local, tok_send, tok_recv,
            slab, toks, weights, kv_own, q_own, w1s, wms, vec, few, kv_all, scaled, sums,
            loaded, lengths_ref, lengths_sem, *places,
        ) = refs[8 + count :]
        wq_ref, wk_ref, wv_ref, tab = places[:4]
        vecs = places[4 : 4 + count]
        w1f, wmf = places[4 + count :]
        loads = [pltpu.make_async_copy(lengths_in, lengths_ref, lengths_sem)]
        loads[0].start()
        for index, (argument, place) in enumerate(zip(arguments, places)):
            loads.append(pltpu.make_async_copy(argument, place, loaded.at[index]))
            loads[-1].start()
        me = Spot()
        copies = Copies(send, recv, local)
        square = me.square()
        line = [to for to, _ in me.line()]
        sources = [device for _, device in me.owners()]
        barrier, expected = announce(
            [me.at(x=x, y=y) for x, y in square]
            + [me.at(g=to) for to in line]
            + sources[1:]
            + [me.sibling()],
            [(jnp.logical_not(me.selfish), sources[0])],
        )
        for copy in loads:
            copy.wait()
        lane = lax.broadcasted_iota(jnp.int32, (s, LANES), 1)
        lower = lane < HEAD
        for head in range(HEADS):
            pair = slice(head // 2 * LANES, head // 2 * LANES + LANES)
            k, v = wk_ref[:, pair], wv_ref[:, pair]
            if head % 2:
                k = pltpu.roll(k, HEAD, 1)
            else:
                v = pltpu.roll(v, HEAD, 1)
            g, h = head // LOCAL, head % LOCAL
            slab[g, :, h * LANES : (h + 1) * LANES] = jnp.where(lower, k, v).astype(low_type)
        for half in range(2):
            b0, b1, b2 = [
                wq_ref[:, (3 * half + index) * LANES : (3 * half + index + 1) * LANES]
                for index in range(3)
            ]
            r1, r2 = pltpu.roll(b1, HEAD, 1), pltpu.roll(b2, HEAD, 1)
            tiles = [(b0, b1), (jnp.where(lower, r1, r2), r2)]
            for odd, (front, back) in enumerate(tiles):
                slab[2 * half + odd, :, WIDE : WIDE + LANES] = front.astype(low_type)
                slab[2 * half + odd, :, WIDE + LANES : width] = jnp.where(lower, back, 0.0).astype(
                    low_type
                )
        wms[...] = wmf[...].astype(low_type)
        few[...] = jnp.zeros((s, LANES), wide)
        for index in range(count):
            few[index : index + 1, : vecs[index].shape[1]] = vecs[index][...]
        small = few[...]
        for g in range(GROUPS):
            slab[g, :, width:] = small.astype(low_type)
        pl.semaphore_wait(barrier, expected)

        view = weights
        place = view.at[me.a, me.g, me.y]
        slab_first = [copies.push(slab.at[to], place, me.at(g=to)) for to in line]
        slab_own = copies.keep(slab.at[me.g], place)
        for w in range(4):
            w1s[w] = w1f[:, w * quarter : (w + 1) * quarter].astype(low_type)
        place = w1.at[me.x, me.c, me.g, me.y]
        w1_first = [
            copies.push(w1s.at[x * 2 + y], place, me.at(x=x, y=y)) for x, y in square
        ]
        w1_own = copies.keep(w1s.at[me.x * 2 + me.y], place)
        wm_own = copies.keep(wms, wm.at[me.x, me.c, me.g, me.y])

        arrivals, weight_arrivals = [], []
        slab_own.wait()
        for copy in slab_first:
            copy.wait_recv()
        tokens_go = Scatter(tok_send, tok_recv, me.selfish)
        tokens_go.start([(tok, device) for _, device in me.readers()], toks.at[me.slot()], me.slot())
        block = view.at[me.a, :, me.y]
        slab_second = [copies.push(block, block, me.at(x=x, y=y)) for x, y in square]
        weight_arrivals.append(copies.push(block, block, me.sibling()))
        for copy, (x, y) in zip(slab_second, square):
            copy.wait_recv()
            block = view.at[x * 2 + me.c, :, y]
            weight_arrivals.append(copies.push(block, block, me.sibling()))
        w1_own.wait()
        for copy in w1_first:
            copy.wait_recv()
        for copy in weight_arrivals:
            copy.wait_recv()

        table = tab[...]

        def spread(pieces, within, owner):
            count = pieces.shape[0] * SMALL
            item = lax.broadcasted_iota(jnp.int32, (count, 2 * WIDE), 0)
            index = lax.broadcasted_iota(jnp.int32, (LANES, 2 * WIDE), 0)
            chosen = jnp.where(index == within, 1.0, 0.0).astype(low_type)
            pieces = pieces.astype(wide).reshape(count, LANES).astype(low_type)
            found = jnp.dot(pieces, chosen, preferred_element_type=wide)
            found = jnp.where((item >> 4) == owner, found, 0.0)
            return jnp.sum(found.reshape(count // SMALL, SMALL, 2 * WIDE), axis=0)

        every = spread(
            view[:, :, :, :SMALL, width:].reshape(32, SMALL, LANES), table[0:1], table[1:2]
        )
        w_me = me.x * 2 + me.y
        inner_bias = spread(
            view[w_me, :, :, :SMALL, width:].reshape(8, SMALL, LANES), table[2:3], table[3:4]
        )
        rows16 = lax.broadcasted_iota(jnp.int32, (SMALL, 2 * WIDE), 0)
        vec[...] = jnp.where(rows16 == 8, inner_bias, every)
        turned = pltpu.roll(every, 2 * WIDE - me.g * LOCAL * HEAD, 1)
        lower = lax.broadcasted_iota(jnp.int32, (1, LANES), 1) < HEAD
        biases = []
        for h in range(LOCAL):
            v = turned[1:2, h // 2 * LANES : h // 2 * LANES + LANES]
            v = v if h % 2 else pltpu.roll(v, HEAD, 1)
            biases.append(jnp.where(lower, 0.0, v))
        biases.append(turned[0:1, :LANES])
        biases.append(jnp.where(lower, turned[0:1, LANES : 2 * LANES], 0.0))
        bias = jnp.concatenate(biases, axis=1)
        lower_rows = lax.broadcasted_iota(jnp.int32, (n, LANES), 1) < HEAD

        matrix = weights[:, :, :, :, :width].reshape(depth, width)
        kept, kv_first = [copies.keep(weights, wqkv_out), copies.keep(vec, vec_out)], []
        kv_sibling, kv_kept = [], []
        for dv in range(2):
            v = (me.half + dv) % 2
            for u in range(2):
                tokens_go.arrived(u * 2 + v, toks.at[u * 2 + v])
            if dv:
                block = w1.at[:, me.c, me.g, :]
                wm_first = [
                    copies.push(wms, wm.at[me.x, me.c, me.g, me.y], me.at(g=to)) for to in line
                ]
                w1_second = [copies.push(block, block, me.at(g=to)) for to in line]
            both = jnp.concatenate([toks[v], toks[2 + v]], axis=0)
            made = jnp.dot(both, matrix, preferred_element_type=wide)
            made = made + bias
            for u in range(2):
                mine = made[u * n : (u + 1) * n]
                kv_own[v, u] = mine[:, :WIDE].astype(low_type)
                front, back = mine[:, WIDE : WIDE + LANES], mine[:, WIDE + LANES :]
                for h, part in enumerate((front, pltpu.roll(front, HEAD, 1), back)):
                    q_own[u * 2 + v, :, h * LANES : (h + 1) * LANES] = jnp.where(
                        lower_rows, part, 0.0
                    ).astype(low_type)
            mine = kv_all.at[:, me.c, v, me.p, me.y]
            kv_first.append(
                [copies.push(kv_own.at[v], mine, me.at(x=x, y=y)) for x, y in square]
            )
            kv_sibling.append(copies.push(kv_own.at[v], mine, me.sibling()))
            kv_kept.append(copies.keep(kv_own.at[v], mine))
        block = w1.at[:, me.c, me.g, :]
        arrivals.append(copies.push(block, block, me.sibling()))
        kept += [copies.keep(toks, tok_out), copies.keep(q_own, q_out)]

        ends = ends_of(lengths_ref)
        rows = GROUPS * n
        spans = [slice(h * LANES, (h + 1) * LANES) for h in range(LOCAL)]
        along = lax.broadcasted_iota(jnp.int32, (1, n), 1)
        ranges = [document_of(along + tile_base(me, slot, n), ends) for slot in range(GROUPS)]
        first = jnp.concatenate([low for low, _ in ranges], axis=1)
        last = jnp.concatenate([high for _, high in ranges], axis=1)
        down = lax.broadcasted_iota(jnp.int32, (rows, rows), 0)
        for slot in range(GROUPS):
            for h, span in enumerate(spans):
                scaled[h, slot * n : (slot + 1) * n] = q_own[slot, :, span] * jnp.asarray(
                    0.125, low_type
                )
        sums[...] = jnp.zeros_like(sums)

        def attend(u, c, v, carry):
            begin = ((u * 2 + c) * 2 + v) * rows
            place = down + begin
            same = (place >= first) & (place < last)
            result = []
            for h, span in enumerate(spans):
                top, total = carry[h]
                kv = kv_all[u, c, v, :, :, :, span].reshape(rows, LANES)
                scores = lax.dot_general(kv, scaled[h], NEXT, preferred_element_type=wide)
                scores = jnp.where(same, scores, mask_fill)
                new_top = jnp.maximum(top, jnp.max(scores, axis=0, keepdims=True))
                factor = jnp.exp(top - new_top)
                powers = jnp.exp(scores - new_top)
                total = total * factor + jnp.sum(powers, axis=0, keepdims=True)
                sums[h] = sums[h] * factor + lax.dot_general(
                    kv, powers.astype(low_type), DOWN, preferred_element_type=wide
                )
                result.append((new_top, total))
            return tuple(result)

        state = tuple(
            (jnp.full((1, rows), lowest_start, wide), jnp.zeros((1, rows), wide))
            for _ in range(LOCAL)
        )
        for dv in range(2):
            v = (me.half + dv) % 2
            forwards = [kv_sibling[dv]]
            for copy, (x, y) in zip(kv_first[dv], square):
                copy.wait_recv()
                block = kv_all.at[:, me.c, v, (x + me.c) % 2, y]
                forwards.append(copies.push(block, block, me.sibling()))
            kv_kept[dv].wait()
            if dv:
                wm_own.wait()
                for copy in wm_first:
                    copy.wait_recv()
                block = wm.at[me.x, me.c, :, me.y]
                wm_second = [copies.push(block, block, me.at(x=x, y=y)) for x, y in square]
                arrivals.append(copies.push(block, block, me.sibling()))
            state = lax.fori_loop(
                0, 2, lambda u, carry, v=v: attend(u, me.c, v, carry), state
            )
            for copy in forwards:
                copy.wait_recv()
            state = lax.fori_loop(
                0, 2, lambda u, carry, v=v: attend(u, 1 - me.c, v, carry), state
            )
        kept.append(copies.keep(kv_all, kv_out))
        for copy, (x, y) in zip(wm_second, square):
            copy.wait_recv()
            block = wm.at[x, me.c, :, y]
            arrivals.append(copies.push(block, block, me.sibling()))
        for copy, (_, source) in zip(w1_second, me.line()):
            copy.wait_recv()
            block = w1.at[:, me.c, source, :]
            arrivals.append(copies.push(block, block, me.sibling()))
        lane = lax.broadcasted_iota(jnp.int32, (n, LANES), 1)
        upper = lane >= HEAD
        for slot in range(GROUPS):
            part = slice(slot * n, (slot + 1) * n)
            mixes = []
            for h in range(LOCAL):
                top, total = state[h]
                mixes.append(jnp.transpose(sums[h, :, part] / total[:, part]))
                lse_out[slot, h : h + 1, :] = top[:, part] + jnp.log(total[:, part])
            turned = [pltpu.roll(mixes[h], HEAD, 1) for h in (0, 2)]
            both = jnp.concatenate(
                [jnp.where(upper, mixes[1], turned[0]), jnp.where(upper, 0.0, turned[1])], axis=1
            )
            mixed_wide[part, :] = both
            mixed_out[slot] = both.astype(low_type)
        for copy in arrivals:
            copy.wait_recv()
        for copy in kept:
            copy.wait()
        tokens_go.finish()
        copies.finish()

    vmem = pltpu.VMEM
    dma = pltpu.SemaphoreType.DMA
    total = 64
    return pl.pallas_call(
        body,
        name="first_kernel",
        out_shape=(
            jax.ShapeDtypeStruct((GROUPS, n, depth), low_type),
            jax.ShapeDtypeStruct((GROUPS, n, WIDE), low_type),
            pltpu.HBM((4, GROUPS, 2, s, cols), low_type),
            jax.ShapeDtypeStruct((SMALL, 2 * WIDE), wide),
            pltpu.HBM((2, 2, 2, 2, 2, n, WIDE), low_type),
            jax.ShapeDtypeStruct((2, 2, GROUPS, 2, s, quarter), low_type),
            jax.ShapeDtypeStruct((2, 2, GROUPS, 2, s, depth), low_type),
            jax.ShapeDtypeStruct((GROUPS, n, PACK), low_type),
            jax.ShapeDtypeStruct((GROUPS * n, PACK), wide),
            jax.ShapeDtypeStruct((GROUPS, 8, n), wide),
        ),
        in_specs=[pl.BlockSpec(memory_space=pltpu.HBM)] * (8 + count),
        out_specs=(pl.BlockSpec(memory_space=pl.ANY),) * 7
        + (pl.BlockSpec(memory_space=vmem),) * 3,
        scratch_shapes=[
            dma((total,)), dma((total,)), dma((12,)), dma((4,)), dma((4,)),
            vmem((GROUPS, s, cols), low_type),
            vmem((GROUPS, n, depth), low_type),
            vmem((4, GROUPS, 2, s, cols), low_type),
            vmem((2, 2, n, WIDE), low_type),
            vmem((GROUPS, n, WIDE), low_type),
            vmem((4, s, quarter), low_type),
            vmem((s, depth), low_type),
            vmem((SMALL, 2 * WIDE), wide),
            vmem((s, LANES), wide),
            vmem((2, 2, 2, 2, 2, n, WIDE), low_type),
            vmem((LOCAL, GROUPS * n, LANES), low_type),
            vmem((LOCAL, LANES, GROUPS * n), wide),
            dma((6 + count,)),
            pltpu.SMEM(lengths.shape, jnp.int32),
            dma,
            *[vmem(item.shape, item.dtype) for item in (wq, wk, wv, tables, *vectors, inner, mix)],
        ],
        compiler_params=pltpu.CompilerParams(
            collective_id=10, has_side_effects=True, vmem_limit_bytes=NEAR_LIMIT
        ),
    )(*[pltpu.with_memory_space_constraint(item, pltpu.HBM) for item in (lengths, tokens, wq, wk, wv, tables, *vectors, inner, mix)])


def pass_back(ident, pieces):
    def body(source, target, send, recv):
        me = Spot()
        owners = me.owners()
        readers = [device for _, device in me.readers()]
        barrier, expected = announce(readers[1:], [(jnp.logical_not(me.selfish), readers[0])])
        pl.semaphore_wait(barrier, expected)
        move = Scatter(send, recv, me.selfish)
        move.start([(source.at[slot], device) for slot, device in owners], target.at[me.g], me.g)
        for g in range(GROUPS):
            move.arrived(g, target.at[g])
        move.finish()

    return scatter_call(body, "pass_back", ident, pieces)


def pass_on(ident, pieces):
    def body(source, target, send, recv):
        me = Spot()
        owners = [device for _, device in me.owners()]
        barrier, expected = announce(owners[1:], [(jnp.logical_not(me.selfish), owners[0])])
        pl.semaphore_wait(barrier, expected)
        move = Scatter(send, recv, me.selfish)
        slot = me.slot()
        move.start([(source.at[g], device) for g, device in me.readers()], target.at[slot], slot)
        for index in range(GROUPS):
            move.arrived(index, target.at[index])
        move.finish()

    return scatter_call(body, "pass_on", ident, pieces)


def scatter_call(body, name, ident, pieces):
    return pl.pallas_call(
        body,
        name=name,
        out_shape=jax.ShapeDtypeStruct(pieces.shape, pieces.dtype),
        in_specs=[pl.BlockSpec(memory_space=pl.ANY)],
        out_specs=pl.BlockSpec(memory_space=pl.ANY),
        scratch_shapes=[pltpu.SemaphoreType.DMA((4,)), pltpu.SemaphoreType.DMA((4,))],
        compiler_params=pltpu.CompilerParams(
            collective_id=ident, has_side_effects=True, vmem_limit_bytes=VMEM_LIMIT
        ),
    )(pieces)


def final_kernel(output, hidden, pieces, outqk, out1, out2, outm, s, e):
    n, depth = hidden.shape
    quarter = out1.shape[-1]

    def body(y_in, hid, dx, qk_in, i_in, o_in, m_in, yo, xg, qw, qb, kw, vw, vb, mw, mb, eg, es, iw, ib, ow, ob, fg, fs):
        device = lax.axis_index("au") * lax.axis_size("row") + lax.axis_index("row")
        yo[...] = y_in[...]
        xg[...] = total_of(hid[...], dx[0], dx[1], dx[2], dx[3]).astype(low_type)
        rows = qk_in.shape[1]
        q_in, k_in = qk_in.at[:, :, WIDE:], qk_in.at[:, :, :WIDE]
        lower = lax.broadcasted_iota(jnp.int32, (rows, LANES), 1) < HEAD

        def part(head):
            g, h = head // LOCAL, head % LOCAL
            return k_in[g, :, h * LANES : (h + 1) * LANES].astype(wide)

        made_q = []
        for g in range(0, GROUPS, 2):
            a0, b0 = q_in[g, :, :LANES].astype(wide), q_in[g, :, LANES:].astype(wide)
            a1 = pltpu.roll(q_in[g + 1, :, :LANES].astype(wide), HEAD, 1)
            b1 = pltpu.roll(q_in[g + 1, :, LANES:].astype(wide), HEAD, 1)
            made_q += [a0, jnp.where(lower, b0, a1), jnp.where(lower, a1, b1)]
        biases = [[], []]
        for pair in range(HEADS // 2):
            span = slice(pair * LANES, (pair + 1) * LANES)
            kv = [part(2 * pair), part(2 * pair + 1)]
            made_k = jnp.where(lower, kv[0], pltpu.roll(kv[1], HEAD, 1))
            made_v = jnp.where(lower, pltpu.roll(kv[0], HEAD, 1), kv[1])
            qw[:, span], kw[:, span], vw[:, span] = made_q[pair][:s], made_k[:s], made_v[:s]
            biases[0].append(made_q[pair][s:])
            biases[1].append(made_v[s:])

        def own(eight, width, shift):
            return pltpu.roll(eight, shift, 1)[0:1, :width]

        turn = (depth - device * s) % depth
        qb[...] = own(jnp.concatenate(biases[0], axis=1), s, turn)
        vb[...] = own(jnp.concatenate(biases[1], axis=1), s, turn)
        mw[...] = m_in[:s]
        extras = pltpu.roll(m_in[s : s + 8, :], turn, 1)
        for index, ref in enumerate((mb, eg, es, ob, fg, fs)):
            ref[...] = extras[index : index + 1, :s]
        for w in range(4):
            iw[:, w * quarter : (w + 1) * quarter] = i_in[w, :s].astype(wide)
        place = lax.axis_index("row") * e
        ib[...] = own(
            i_in[lax.axis_index("au"), s : s + 8, :].astype(wide), e, (quarter - place) % quarter
        )
        ow[...] = o_in[...]

    vmem = pltpu.VMEM

    def shape(*dims):
        return jax.ShapeDtypeStruct(dims, wide)

    return pl.pallas_call(
        body,
        name="final_kernel",
        out_shape=(
            jax.ShapeDtypeStruct((n, depth), low_type),
            jax.ShapeDtypeStruct((n, depth), low_type),
            shape(s, depth), shape(1, s), shape(s, depth), shape(s, depth), shape(1, s),
            shape(s, depth), shape(1, s), shape(1, s), shape(1, s),
            shape(s, 4 * quarter), shape(1, e), shape(e, depth),
            shape(1, s), shape(1, s), shape(1, s),
        ),
        in_specs=[pl.BlockSpec(memory_space=vmem)] * 7,
        out_specs=(pl.BlockSpec(memory_space=vmem),) * 17,
        compiler_params=pltpu.CompilerParams(vmem_limit_bytes=NEAR_LIMIT),
    )(output, hidden, pieces, outqk, out1, out2, outm)


def gelu_and_slope(value):
    t = 1.0 / (1.0 + (0.3275911 * 0.7071067811865476) * jnp.abs(value))
    bell = jnp.exp(-0.5 * value * value)
    tail = 1.061405429
    for weight in (-1.453152027, 1.421413741, -0.284496736, 0.254829592):
        tail = tail * t + weight
    tail = 0.5 * tail * t * bell
    below = jnp.where(value >= 0.0, 1.0 - tail, tail)
    return value * below, below + value * bell * 0.3989422804014327


def normed(hidden):
    mean = jnp.mean(hidden, axis=-1, keepdims=True)
    centered = hidden - mean
    spread = jnp.mean(centered * centered, axis=-1, keepdims=True)
    inverse = lax.rsqrt(spread + eps_norm)
    return centered * inverse, inverse


def normed_grad(grad, norm, inverse):
    mean = jnp.mean(grad, axis=-1, keepdims=True)
    along = jnp.mean(grad * norm, axis=-1, keepdims=True)
    return inverse * (grad - mean - norm * along)


def down_sum(values):
    return jnp.sum(values, axis=0, keepdims=True)


def middle_kernel(mixed, tokens, cotangent, mix, inner, outer, vec, s, e):
    n, depth = tokens.shape
    quarter = inner.shape[1]
    rows = s + 8
    cut = depth // 2
    hn = n // 2

    def body(
        mixed_ref, tok_in, cot_in, wm_in, w1_in, w2f_in, vec_in,
        out, hidden_out, do_out, sm, s1, s2,
        send, recv, local, back_send, back_recv, on_send, on_recv,
        swap_send2, swap_recv2, tok, cot, w2f, vec_ref, wm, w1, w2p, w2s, came, mixed_tok, xs, acts, slopes, parts, sums, bgs, igs, parts2, sums2,
        pieces, extra, attn, own1, own2, g1, g2, gm,
    ):
        me = Spot()
        copies = Copies(send, recv, local)
        square = me.square()
        line = [to for to, _ in me.line()]
        owners = me.owners()
        readers = me.readers()
        swapped = [me.at(g=to, c=me.y, y=me.c) for to in [me.g] + line]
        barrier, expected = announce(
            [me.at(x=x, y=y) for x, y in square]
            + swapped[1:]
            + [device for _, device in readers[1:]]
            + [device for _, device in owners[1:]]
            + [me.sibling()],
            [
                (jnp.logical_not(me.selfish), readers[0][1]),
                (jnp.logical_not(me.selfish), owners[0][1]),
                (me.crossing, swapped[0]),
            ],
        )
        loads = [copies.keep(wm_in, wm), copies.keep(w1_in, w1)]
        small_loads = [
            copies.keep(source, target)
            for source, target in ((tok_in, tok), (vec_in, vec_ref), (w2f_in, w2f), (cot_in, cot))
        ]
        pl.semaphore_wait(barrier, expected)

        back = Scatter(back_send, back_recv, me.selfish)
        back.start([(mixed_ref.at[slot], device) for slot, device in owners], came.at[me.g], me.g)
        lower = lax.broadcasted_iota(jnp.int32, (n, LANES), 1) < HEAD
        loads[0].wait()
        for copy in small_loads:
            copy.wait()
        w2s[...] = w2f[...].astype(low_type)
        for g in range(GROUPS):
            back.arrived(g, came.at[g])
        w2_place = w2p.at[me.g, me.y]
        w2_first = [copies.push(w2s, w2_place, device) for device in swapped[1:]]
        w2_swap = pltpu.make_async_remote_copy(
            src_ref=w2s,
            dst_ref=w2_place,
            send_sem=swap_send2,
            recv_sem=swap_recv2,
            device_id=swapped[0],
            device_id_type=MESH,
        )
        w2_stays = pltpu.make_async_copy(w2s, w2_place, swap_recv2)

        @pl.when(me.crossing)
        def _():
            w2_swap.start()

        @pl.when(jnp.logical_not(me.crossing))
        def _():
            w2_stays.start()

        for half in range(2):
            a0 = came[2 * half, :, :LANES]
            b0 = came[2 * half, :, LANES:].astype(wide)
            a1 = pltpu.roll(came[2 * half + 1, :, :LANES].astype(wide), HEAD, 1)
            b1 = pltpu.roll(came[2 * half + 1, :, LANES:].astype(wide), HEAD, 1)
            base = half * 3 * LANES
            mixed_tok[:, base : base + LANES] = a0
            mixed_tok[:, base + LANES : base + 2 * LANES] = jnp.where(lower, b0, a1).astype(low_type)
            mixed_tok[:, base + 2 * LANES : base + 3 * LANES] = jnp.where(lower, a1, b1).astype(
                low_type
            )

        def vector(index):
            return vec_ref[index : index + 1, :]

        mix = jnp.dot(mixed_tok[...], wm[...], preferred_element_type=wide) + vector(2)
        norm1, inverse1 = normed(tok[...].astype(wide) + mix)
        early = norm1 * vector(3) + vector(4)
        mine = me.x * 2 + me.y
        halves = [slice(0, hn), slice(hn, n)]

        def send_rows(ref, h):
            place = ref.at[h, mine]
            return [copies.push(place, place, me.at(x=x, y=y)) for x, y in square]

        def send_back(ref, landing, h):
            return [
                copies.push(ref.at[h, x * 2 + y], landing.at[h, mine], me.at(x=x, y=y))
                for x, y in square
            ]

        def arrive(started):
            for copy in started:
                copy.wait_recv()

        def received(landing, h):
            return [landing[h, x * 2 + y] for x, y in square]

        early_go = []
        for h, half in enumerate(halves):
            xs[h, mine] = early[half].astype(low_type)
            early_go.append(send_rows(xs, h))
            if h == 0:
                for copy in early_go[0]:
                    copy.wait_send()
                copies.started = [
                    item for item in copies.started if all(item is not copy for copy in early_go[0])
                ]
        loads[1].wait()

        def outer_weight():
            return w2p[...].reshape(quarter, depth)

        branch_go = []
        for h in range(2):
            arrive(early_go[h])
            inner = jnp.dot(
                xs[h].reshape(4 * hn, depth), w1[...], preferred_element_type=wide
            ) + vector(8)
            act, slope = gelu_and_slope(inner)
            act = act.astype(low_type)
            acts[h] = act.reshape(4, hn, quarter)
            slopes[h] = slope
            if h == 0:

                @pl.when(me.crossing)
                def _():
                    w2_swap.wait_recv()
                    w2_swap.wait_send()

                @pl.when(jnp.logical_not(me.crossing))
                def _():
                    w2_stays.wait()

                block = w2p.at[me.g, me.c]
                w2_last = [copies.push(block, block, me.sibling())]
                for copy, (_, source) in zip(w2_first, me.line()):
                    copy.wait_recv()
                    block = w2p.at[source, me.c]
                    w2_last.append(copies.push(block, block, me.sibling()))
                arrive(w2_last)
            made = jnp.dot(act, outer_weight(), preferred_element_type=wide).reshape(4, hn, depth)
            own1[h] = made
            parts[h] = made.astype(low_type)
            branch_go.append(send_back(parts, sums, h))

        grad_go, final_grads, norm_sums, cot_sums = [], [], [], []
        for h, half in enumerate(halves):
            arrive(branch_go[h])
            branch = total_of(own1[h, mine], *received(sums, h)) + vector(5)
            norm2, inverse2 = normed(early[half] + branch)
            out[half, :] = (norm2 * vector(6) + vector(7)).astype(low_type)
            cot_wide = cot[half, :].astype(wide)
            final_grad = normed_grad(cot_wide * vector(6), norm2, inverse2)
            bgs[h, mine] = final_grad.astype(low_type)
            grad_go.append(send_rows(bgs, h))
            final_grads.append(final_grad)
            norm_sums.append(down_sum(cot_wide * norm2))
            cot_sums.append(down_sum(cot_wide))
        extra[...] = jnp.zeros_like(extra)
        extra[3:4, :] = down_sum(bgs[0, mine].astype(wide)) + down_sum(bgs[1, mine].astype(wide))
        extra[4:5, :] = norm_sums[0] + norm_sums[1]
        extra[5:6, :] = cot_sums[0] + cot_sums[1]

        token_go = []
        for h in range(2):
            arrive(grad_go[h])
            grad = lax.dot_general(
                bgs[h].reshape(4 * hn, depth), outer_weight(), NEXT, preferred_element_type=wide
            )
            grad = (grad * slopes[h]).astype(low_type)
            igs[h] = grad.reshape(4, hn, quarter)
            made = lax.dot_general(grad, w1[...], NEXT, preferred_element_type=wide)
            made = made.reshape(4, hn, depth)
            own2[h] = made
            parts2[h] = made.astype(low_type)
            token_go.append(send_back(parts2, sums2, h))

        other = 1 - me.c
        grads = bgs[...].reshape(4 * n, depth)
        for half in range(2):
            span = slice(half * cut, (half + 1) * cut)
            made = lax.dot_general(
                acts[:, :, :, span].reshape(4 * n, cut), grads, DOWN, preferred_element_type=wide
            )
            g2[2 * half : 2 * half + 2] = made.astype(low_type).reshape(2, 2, e, depth)
        w2_half = copies.push(g2.at[:, other], s2, me.sibling())

        grads = igs[...].reshape(4 * n, quarter)
        bias = jnp.broadcast_to(down_sum(grads.astype(wide)), (8, quarter)).astype(low_type)
        for half in range(2):
            span = slice(half * cut, (half + 1) * cut)
            made = lax.dot_general(
                xs[:, :, :, span].reshape(4 * n, cut), grads, DOWN, preferred_element_type=wide
            ).astype(low_type)
            for index in range(16):
                place = (half, index // 8, index // 2 % GROUPS, index % 2)
                g1[(*place, slice(None, s))] = made[index * s : (index + 1) * s]
                g1[(*place, slice(s, None))] = bias
        w1_half = copies.push(g1.at[:, other], s1, me.sibling())
        w2_half.wait_recv()

        def add2(g):
            s2[g] = s2[g] + g2[g, me.c]

        loop(GROUPS, add2)
        w1_half.wait_recv()

        def add1(index):
            x, g, y = index // 8, index // 2 % GROUPS, index % 2
            s1[x, g, y] = s1[x, g, y] + g1[x, me.c, g, y]

        loop(16, add1)
        norm_sums, grad_sums, attn_sums = [], [], []
        for h, half in enumerate(halves):
            arrive(token_go[h])
            early_grad = total_of(final_grads[h], own2[h, mine], *received(sums2, h))
            norm_sums.append(down_sum(early_grad * norm1[half]))
            grad_sums.append(down_sum(early_grad))
            hidden = normed_grad(early_grad * vector(3), norm1[half], inverse1[half])
            hidden_out[half, :] = hidden
            attn[half, :] = hidden.astype(low_type)
            attn_sums.append(down_sum(hidden.astype(low_type).astype(wide)))
        extra[0:1, :] = attn_sums[0] + attn_sums[1]
        extra[1:2, :] = norm_sums[0] + norm_sums[1]
        extra[2:3, :] = grad_sums[0] + grad_sums[1]
        attn_grad = attn[...]
        back_grad = lax.dot_general(attn_grad, wm[...], NEXT, preferred_element_type=wide)
        for half in range(2):
            base = half * 3 * LANES
            t0 = back_grad[:, base : base + LANES]
            t1 = back_grad[:, base + LANES : base + 2 * LANES]
            t2 = back_grad[:, base + 2 * LANES : base + 3 * LANES]
            r1, r2 = pltpu.roll(t1, HEAD, 1), pltpu.roll(t2, HEAD, 1)
            pieces[2 * half, :, :LANES] = t0.astype(low_type)
            pieces[2 * half, :, LANES:] = jnp.where(lower, t1, 0.0).astype(low_type)
            pieces[2 * half + 1, :, :LANES] = jnp.where(lower, r1, r2).astype(low_type)
            pieces[2 * half + 1, :, LANES:] = jnp.where(lower, r2, 0.0).astype(low_type)
        onward = Scatter(on_send, on_recv, me.selfish)
        slot = me.slot()
        onward.start([(pieces.at[g], device) for g, device in readers], do_out.at[slot], slot)

        for half in range(2):
            span = slice(half * cut, (half + 1) * cut)
            made = lax.dot_general(
                mixed_tok[:, span], attn_grad, DOWN, preferred_element_type=wide
            ).astype(low_type)
            for index in range(16):
                place = (half, index // 8, index // 2 % GROUPS, index % 2)
                gm[(*place, slice(None, s))] = made[index * s : (index + 1) * s]
                gm[(*place, slice(s, None))] = extra[...].astype(low_type)
        wm_half = copies.push(gm.at[:, other], sm, me.sibling())
        wm_half.wait_recv()

        def addm(index):
            x, g, y = index // 8, index // 2 % GROUPS, index % 2
            sm[x, g, y] = sm[x, g, y] + gm[x, me.c, g, y]

        loop(16, addm)
        for index in range(GROUPS):
            onward.arrived(index, do_out.at[index])
        back.finish()
        onward.finish()
        copies.finish()

    vmem = pltpu.VMEM
    dma = pltpu.SemaphoreType.DMA
    tall = vmem((2, 4, hn, depth), low_type)
    full = vmem((2, 4, hn, depth), wide)
    high = vmem((2, 4, hn, quarter), low_type)
    tokens, cotangent, outer = [
        pltpu.with_memory_space_constraint(item, pltpu.HBM) for item in (tokens, cotangent, outer)
    ]
    return pl.pallas_call(
        body,
        name="middle_kernel",
        out_shape=(
            jax.ShapeDtypeStruct((n, depth), low_type),
            jax.ShapeDtypeStruct((n, depth), wide),
            jax.ShapeDtypeStruct((GROUPS, n, PACK), low_type),
            jax.ShapeDtypeStruct((2, GROUPS, 2, rows, depth), low_type),
            jax.ShapeDtypeStruct((2, GROUPS, 2, rows, quarter), low_type),
            jax.ShapeDtypeStruct((GROUPS, e, depth), low_type),
        ),
        in_specs=[
            pl.BlockSpec(memory_space=item)
            for item in (pl.ANY, pltpu.HBM, pltpu.HBM, pl.ANY, pl.ANY, pltpu.HBM, pl.ANY)
        ],
        out_specs=[
            pl.BlockSpec(memory_space=item) for item in (vmem, vmem, pl.ANY, vmem, vmem, vmem)
        ],
        scratch_shapes=[
            dma((48,)), dma((48,)), dma((8,)), dma((4,)), dma((4,)), dma((4,)), dma((4,)), dma, dma,
            vmem((n, depth), low_type),
            vmem((n, depth), low_type),
            vmem((e, depth), wide),
            vmem(vec.shape, wide),
            vmem((depth, depth), low_type),
            vmem((depth, quarter), low_type),
            vmem((GROUPS, 2, e, depth), low_type),
            vmem((e, depth), low_type),
            vmem((GROUPS, n, PACK), low_type),
            vmem((n, depth), low_type),
            tall, high,
            vmem((2, 4 * hn, quarter), wide),
            tall, tall, tall, high, tall, tall,
            vmem((GROUPS, n, PACK), low_type),
            vmem((8, depth), wide),
            vmem((n, depth), low_type),
            full, full,
            vmem((2, 2, GROUPS, 2, rows, quarter), low_type),
            vmem((GROUPS, 2, e, depth), low_type),
            vmem((2, 2, GROUPS, 2, rows, depth), low_type),
        ],
        compiler_params=pltpu.CompilerParams(
            collective_id=12, has_side_effects=True, vmem_limit_bytes=NEAR_LIMIT
        ),
    )(mixed, tokens, cotangent, mix, inner, outer, vec)


def tile_base(me, slot, n):
    u, v = slot // 2, slot % 2
    return ((u * 2 + me.c) * 2 * GROUPS + (v * 2 + me.p) * 2 + me.y) * n


def ends_of(lengths_ref):
    ends = [lengths_ref[0]]
    for index in range(1, lengths_ref.shape[0]):
        ends.append(ends[-1] + lengths_ref[index])
    return ends


def document_of(place, ends):
    first, last = place * 0, place * 0 + ends[-1]
    for end in ends[:-1]:
        before = end <= place
        first = jnp.where(before, end, first)
    for end in reversed(ends[:-1]):
        last = jnp.where(end <= place, last, end)
    return first, last


def turn_kernel(lengths, queries, keys, grads_in, mixed, lse, tokens, weights, sum1, sum2, summ):
    n = tokens.shape[1]
    depth = tokens.shape[-1]
    s = depth // 32
    rows = s + 8
    cut = depth // 2
    tall = sum2.shape[1]
    block = GROUPS * n
    width = WIDE + PACK
    spans = [slice(h * LANES, (h + 1) * LANES) for h in range(LOCAL)]

    def body(
        lengths_ref, q_ref, kv_ref, do_ref, mixed_ref, lse_ref, tok, w_ref, s1, s2, sm,
        dx_out, outqk, out1, out2, outm,
        send, recv, local, dx_send, dx_recv, swap_send, swap_recv, ks, kr, ps, pr,
        both, kbuf, kin, pk, dqs, narrow, dxs, gk, sk, pp, fk, p1, f1, pm, fm, tm, p2, early,
    ):
        me = Spot()
        copies = Copies(send, recv, local)
        square = me.square()
        line = [to for to, _ in me.line()]
        readers = [device for _, device in me.readers()]
        swapped = [me.at(g=to, c=me.y, y=me.c) for to in [me.g] + line]
        barrier, expected = announce(
            [me.at(x=x, y=y) for x, y in square]
            + [me.at(g=to) for to in line]
            + readers[1:]
            + swapped[1:]
            + [me.sibling()],
            [(jnp.logical_not(me.selfish), readers[0]), (me.crossing, swapped[0])],
        )
        ends = ends_of(lengths_ref)
        lane = lax.broadcasted_iota(jnp.int32, (n, LANES), 1)
        upper = lane >= HEAD
        along = lax.broadcasted_iota(jnp.int32, (1, n), 1)
        down = lax.broadcasted_iota(jnp.int32, (block, n), 0)

        def upper_halves(ref, part):
            front = ref[part, :LANES].astype(wide)
            back = ref[part, LANES:].astype(wide)
            parts = (pltpu.roll(front, HEAD, 1), front, pltpu.roll(back, HEAD, 1))
            return [jnp.where(upper, item, 0.0) for item in parts]

        firsts, lasts, logs, deltas = [], [], [], []
        for slot in range(GROUPS):
            part = slice(slot * n, (slot + 1) * n)
            first, last = document_of(along + tile_base(me, slot, n), ends)
            firsts.append(first)
            lasts.append(last)
            outs, inputs = upper_halves(mixed_ref, part), upper_halves(do_ref, part)
            for h, span in enumerate(spans):
                base = slot * 2 * n
                both[h, base : base + n] = q_ref[part, span] * jnp.asarray(0.125, low_type)
                both[h, base + n : base + 2 * n] = inputs[h].astype(low_type)
            deltas.append([down_sum(jnp.transpose(i * o)) for i, o in zip(inputs, outs)])
            logs.append([lse_ref[slot, h : h + 1, :] for h in range(LOCAL)])
        dqs[...] = jnp.zeros_like(dqs)
        pl.semaphore_wait(barrier, expected)

        wm_push = [
            copies.push(sm.at[x, :, y], pm.at[peer], me.at(x=x, y=y))
            for peer, (x, y) in enumerate(square)
        ]
        w1_push = [
            copies.push(s1.at[:, to, :], p1.at[slot], me.at(g=to)) for slot, to in enumerate(line)
        ]
        w2_push = [
            copies.push(s2.at[to], p2.at[index + 1], swapped[index + 1])
            for index, to in enumerate(line)
        ]
        exchanged = pltpu.make_async_remote_copy(
            src_ref=s2.at[me.g],
            dst_ref=p2.at[0],
            send_sem=swap_send,
            recv_sem=swap_recv,
            device_id=swapped[0],
            device_id_type=MESH,
        )
        stays = pltpu.make_async_copy(s2.at[me.g], p2.at[0], swap_recv)

        @pl.when(me.crossing)
        def _():
            exchanged.start()

        @pl.when(jnp.logical_not(me.crossing))
        def _():
            stays.start()

        other = 1 - me.c

        def attend(u, c, v, target):
            begin = pl.multiple_of(((u * 2 + c) * 2 + v) * block, block)
            place = down + begin
            same = [(place >= first) & (place < last) for first, last in zip(firsts, lasts)]
            for h, span in enumerate(spans):
                kv = kv_ref[pl.ds(begin, block), span]
                made = lax.dot_general(kv, both[h], NEXT, preferred_element_type=wide)
                pairs = []
                for slot in range(GROUPS):
                    base = slot * 2 * n
                    scores = jnp.where(same[slot], made[:, base : base + n], mask_fill)
                    probs = jnp.exp(scores - logs[slot][h])
                    dots = made[:, base + n : base + 2 * n]
                    score_grad = (probs * (dots - deltas[slot][h])).astype(low_type)
                    pairs += [score_grad, probs.astype(low_type)]
                    dqs[slot, :, span] += lax.dot_general(
                        score_grad, kv, DOWN, preferred_element_type=wide
                    )
                made = jnp.dot(
                    jnp.concatenate(pairs, axis=1), both[h], preferred_element_type=wide
                )
                target[:, :, :, span] = made.astype(low_type).reshape(2, 2, n, LANES)

        def to_sibling(turn):
            return pltpu.make_async_remote_copy(
                src_ref=kbuf.at[0, turn],
                dst_ref=kin.at[turn],
                send_sem=ks.at[turn],
                recv_sem=kr.at[turn],
                device_id=me.sibling(),
                device_id_type=MESH,
            )

        def to_peer(turn, peer):
            x, y = square[peer]
            return pltpu.make_async_remote_copy(
                src_ref=kbuf.at[1, turn, (x + me.c) % 2, y],
                dst_ref=pk.at[turn, peer],
                send_sem=ps.at[turn * 3 + peer],
                recv_sem=pr.at[turn * 3 + peer],
                device_id=me.at(x=x, y=y),
                device_id_type=MESH,
            )

        def key_turn(turn):
            u, v = turn % 2, (me.half + turn // 2) % 2

            def of_core(index):
                attend(u, jnp.where(index == 0, other, me.c), v, kbuf.at[index, turn])

                @pl.when(index == 0)
                def _():
                    to_sibling(turn).start()

            loop(2, of_core)
            to_sibling(turn).wait_recv()
            for p in range(2):
                for y in range(2):
                    kbuf[1, turn, p, y] = kbuf[1, turn, p, y] + kin[turn, p, y]
            for peer in range(3):
                to_peer(turn, peer).start()

        loop(4, key_turn)

        def square_push(total, landing):
            return [
                copies.push(total.at[x, :, y], landing.at[slot], me.at(x=x, y=y))
                for slot, (x, y) in enumerate(square)
            ]

        def square_sum(result, total, landed):
            def add(g):
                result[g] = total_of(
                    total[me.x, g, me.y], landed[0, g], landed[1, g], landed[2, g]
                ).astype(low_type)

            loop(GROUPS, add)

        def weight_grad(slots, half):
            span = slice(half * cut, (half + 1) * cut)
            return lax.dot_general(
                jnp.concatenate([tok[slot, :, span] for slot in slots], axis=0),
                jnp.concatenate([narrow[slot] for slot in slots], axis=0),
                DOWN,
                preferred_element_type=wide,
            )

        moves = []
        slots = [turn % 2 * 2 + (me.half + turn // 2) % 2 for turn in range(4)]
        for turn in range(4):
            if turn == 3:
                for half in range(2):
                    early[half] = weight_grad(slots[:3], half)
            u, dv = turn % 2, turn // 2
            v = (me.half + dv) % 2
            slot = u * 2 + v
            wides = [dqs[slot, :, span] * 0.125 for span in spans]
            narrow[slot, :, WIDE : WIDE + LANES] = jnp.where(
                upper, pltpu.roll(wides[1], HEAD, 1), wides[0]
            ).astype(low_type)
            narrow[slot, :, WIDE + LANES :] = jnp.where(upper, 0.0, wides[2]).astype(low_type)
            for peer in range(3):
                to_peer(turn, peer).wait_recv()
            here = total_of(
                kbuf[1, turn, me.p, me.y], *[pk[turn, peer] for peer in range(3)]
            ).astype(low_type)
            narrow[slot, :, :WIDE] = here
            dxs[slot] = lax.dot_general(
                narrow[slot], w_ref[:, :width], NEXT, preferred_element_type=wide
            ).astype(low_type)
            copy = pltpu.make_async_remote_copy(
                src_ref=dxs.at[slot],
                dst_ref=dx_out.at[me.g],
                send_sem=dx_send.at[turn],
                recv_sem=dx_recv.at[me.g],
                device_id=me.at(x=u, g=2 * v + me.p),
                device_id_type=MESH,
            )
            if dv:
                copy.start()
                moves.append((copy, None))
                continue
            stay = pltpu.make_async_copy(dxs.at[slot], dx_out.at[me.g], dx_recv.at[me.g])
            at_home = me.selfish & (me.x == u)
            away = jnp.logical_not(at_home)
            moves.append((copy, away))

            @pl.when(at_home)
            def _(stay=stay):
                stay.start()

            @pl.when(away)
            def _(copy=copy):
                copy.start()

        bias = down_sum(total_of(*[down_sum(narrow[slot].astype(wide)) for slot in range(GROUPS)]))
        bias = jnp.broadcast_to(bias, (8, width)).astype(low_type)
        for half in range(2):
            made = (early[half] + weight_grad(slots[3:], half)).astype(low_type)
            for index in range(16):
                place = (half, index // 8, index // 2 % GROUPS, index % 2)
                gk[(*place, slice(None, s))] = made[index * s : (index + 1) * s]
                gk[(*place, slice(s, None))] = bias
        g_half = copies.push(gk.at[:, other], sk, me.sibling())

        for copy in wm_push:
            copy.wait_recv()
        square_sum(fm, sm, pm)
        wm_last = [
            copies.push(fm.at[to], tm.at[peer], me.at(g=to)) for peer, to in enumerate(line)
        ]
        for copy in w1_push:
            copy.wait_recv()

        def addw(index):
            x, y = index // 2, index % 2
            f1[x, y] = total_of(s1[x, me.g, y], *[p1[peer, x, y] for peer in range(3)]).astype(
                low_type
            )

        loop(4, addw)
        quarter = out1.at[me.x * 2 + me.y]
        g_half.wait_recv()

        def pair_sum(index):
            x, g, y = index // 8, index // 2 % GROUPS, index % 2
            sk[x, g, y] = sk[x, g, y] + gk[x, me.c, g, y]

        loop(16, pair_sum)
        push = square_push(sk, pp)
        arrivals = [copies.push(f1.at[x, y], quarter, me.at(x=x, y=y)) for x, y in square]
        kept = [copies.keep(f1.at[me.x, me.y], quarter)]

        @pl.when(me.crossing)
        def _():
            exchanged.wait_recv()
            exchanged.wait_send()

        @pl.when(jnp.logical_not(me.crossing))
        def _():
            stays.wait()

        for copy in w2_push:
            copy.wait_recv()
        out2[...] = total_of(*[p2[index] for index in range(4)])
        for copy in push:
            copy.wait_recv()
        square_sum(fk, sk, pp)
        arrivals += [copies.push(fk.at[to], outqk.at[me.g], me.at(g=to)) for to in line]
        kept.append(copies.keep(fk.at[me.g], outqk.at[me.g]))
        for copy in wm_last:
            copy.wait_recv()
        outm[...] = total_of(fm[me.g], *[tm[peer] for peer in range(3)])
        for copy in arrivals:
            copy.wait_recv()
        for g in range(GROUPS):
            pltpu.make_async_copy(dx_out.at[g], dx_out.at[g], dx_recv.at[g]).wait()
        for copy in kept:
            copy.wait()
        for copy, away in moves:
            if away is None:
                copy.wait_send()
                continue

            @pl.when(away)
            def _(copy=copy):
                copy.wait_send()

        for turn in range(4):
            to_sibling(turn).wait_send()
            for peer in range(3):
                to_peer(turn, peer).wait_send()
        copies.finish()

    vmem = pltpu.VMEM
    dma = pltpu.SemaphoreType.DMA
    total = 40
    return pl.pallas_call(
        body,
        name="turn_kernel",
        out_shape=(
            jax.ShapeDtypeStruct((GROUPS, n, depth), low_type),
            jax.ShapeDtypeStruct((GROUPS, rows, width), low_type),
            jax.ShapeDtypeStruct((4, rows, depth), low_type),
            jax.ShapeDtypeStruct((tall, depth), wide),
            jax.ShapeDtypeStruct((rows, depth), wide),
        ),
        in_specs=[pl.BlockSpec(memory_space=pltpu.SMEM)] + [pl.BlockSpec(memory_space=vmem)] * 10,
        out_specs=[pl.BlockSpec(memory_space=pl.ANY)] * 3 + [pl.BlockSpec(memory_space=vmem)] * 2,
        scratch_shapes=[
            dma((total,)), dma((total,)), dma((4,)), dma((4,)), dma((4,)), dma, dma,
            dma((4,)), dma((4,)), dma((12,)), dma((12,)),
            vmem((LOCAL, 2 * block, LANES), low_type),
            vmem((2, 4, 2, 2, n, WIDE), low_type),
            vmem((4, 2, 2, n, WIDE), low_type),
            vmem((4, 3, n, WIDE), low_type),
            vmem((GROUPS, n, WIDE), wide),
            vmem((GROUPS, n, width), low_type),
            vmem((GROUPS, n, depth), low_type),
            vmem((2, 2, GROUPS, 2, rows, width), low_type),
            vmem((2, GROUPS, 2, rows, width), low_type),
            vmem((3, GROUPS, rows, width), low_type),
            vmem((GROUPS, rows, width), low_type),
            vmem((3, 2, 2, rows, depth), low_type),
            vmem((2, 2, rows, depth), low_type),
            vmem((3, GROUPS, rows, depth), low_type),
            vmem((GROUPS, rows, depth), low_type),
            vmem((3, rows, depth), low_type),
            vmem((4, tall, depth), low_type),
            vmem((2, cut, width), wide),
        ],
        compiler_params=pltpu.CompilerParams(
            collective_id=11, has_side_effects=True, vmem_limit_bytes=TURN_LIMIT
        ),
    )(lengths, queries, keys, grads_in, mixed, lse, tokens, weights, sum1, sum2, summ)


def on_device_general(
    tokens,
    cotangent,
    doc_lengths,
    query_weight,
    query_bias,
    key_weight,
    value_weight,
    value_bias,
    mix_weight,
    mix_bias,
    early_gain,
    early_shift,
    inner_weight,
    inner_bias,
    outer_weight,
    outer_bias,
    final_gain,
    final_shift,
):
    n, depth = tokens.shape
    groups, cycle = lax.axis_size("au"), lax.axis_size("row")
    devices = groups * cycle
    zs = cycle // (2 * GROUPS)
    s = query_weight.shape[0]
    ff = inner_weight.shape[1]
    quarter = ff // 4
    e = outer_weight.shape[0]
    rows = GROUPS * n
    total_tokens = n * devices
    me = Place(zs)
    device = lax.axis_index("au") * cycle + lax.axis_index("row")
    w_me = me.x * 2 + me.y

    def by_head(weight):
        return weight.astype(low_type).reshape(-1, GROUPS, LOCAL, HEAD)

    def packed(query, key, value):
        kv = jnp.stack([key, value], axis=3).reshape(-1, GROUPS, WIDE)
        q = jnp.pad(query, ((0, 0), (0, 0), (0, 0), (0, HEAD))).reshape(-1, GROUPS, WIDE)
        return jnp.concatenate([kv, q], axis=2)

    slab = packed(by_head(query_weight), by_head(key_weight), by_head(value_weight))
    slab = jnp.transpose(slab, (1, 0, 2))
    small = jnp.concatenate(
        [
            vector.astype(low_type)
            for vector in (
                query_bias, value_bias, mix_bias, early_gain, early_shift,
                outer_bias, final_gain, final_shift, inner_bias,
            )
        ]
    )
    extra = -s % 8 or 8
    small = jnp.broadcast_to(
        jnp.pad(small, (0, 2 * WIDE - small.shape[0]))[None, None], (GROUPS, extra, 2 * WIDE)
    )
    slab = jnp.concatenate([slab, small], axis=1)
    tok_all, w_all = spread_tokens(zs, tokens, slab)
    tok_all = tok_all.reshape(rows, depth)
    w_qkv = w_all[..., :s, :].reshape(depth, 2 * WIDE)
    small = w_all[..., s, :].reshape(devices, 2 * WIDE)
    names = [small[:, i * s : (i + 1) * s].reshape(depth) for i in range(8)]
    q_bias, v_bias, m_bias, e_gain, e_shift, o_bias, f_gain, f_shift = names
    i_bias = small[:, 8 * s : 8 * s + e].reshape(4, quarter)[w_me].astype(wide)
    q_bias = q_bias.reshape(1, GROUPS, LOCAL, HEAD)
    v_bias = v_bias.reshape(1, GROUPS, LOCAL, HEAD)
    bias = packed(q_bias, jnp.zeros_like(q_bias), v_bias)[0, me.g].astype(wide)

    qkv = (jnp.dot(tok_all, w_qkv, preferred_element_type=wide) + bias).astype(low_type)
    queries = qkv[:, WIDE:]

    inner_slab = jnp.transpose(inner_weight.astype(low_type).reshape(s, 4, quarter), (1, 0, 2))
    kv_all, w1, w2, wm = spread_keys(
        zs,
        qkv[:, :WIDE].reshape(GROUPS, n, WIDE),
        inner_slab,
        outer_weight.astype(low_type),
        mix_weight.astype(low_type),
    )
    kv_all = kv_all.reshape(total_tokens, WIDE)
    w1 = w1.reshape(depth, quarter)
    w2 = w2.reshape(quarter, depth)
    wm = wm.reshape(depth, depth)

    tile, block = 128, 512
    count = doc_lengths.shape[0]
    upto = jnp.arange(count)[None, :] <= jnp.arange(count)[:, None]
    ends = jnp.sum(jnp.where(upto, doc_lengths[None, :], 0), axis=1)
    owners = ((me.x * 2 + me.c) * cycle + me.z * GROUPS * 2 + jnp.arange(GROUPS) * 2 + me.y) * n
    places = (owners[:, None] + jnp.arange(n)[None, :]).reshape(rows)
    before = ends[None, :] <= places[:, None]
    first = jnp.max(jnp.where(before, ends[None, :], 0), axis=1).astype(jnp.int32)
    last = jnp.min(jnp.where(before, total_tokens, ends[None, :]), axis=1).astype(jnp.int32)
    tiles = rows // tile
    bounds = jnp.stack(
        [
            first.reshape(tiles, tile)[:, 0] // block,
            (last.reshape(tiles, tile)[:, -1] + block - 1) // block,
        ],
        axis=1,
    )
    mixed, mixed_wide, lse = attend_forward(
        queries, kv_all, bounds, first[:, None], last[:, None], tile, block
    )
    mixed_tok = exchange_line(zs, 2, mixed.reshape(GROUPS, n, PACK))
    mixed_tok = jnp.transpose(mixed_tok[:, :, : LOCAL * HEAD], (1, 0, 2)).reshape(n, depth)

    attn = jnp.dot(mixed_tok, wm, preferred_element_type=wide) + m_bias.astype(wide)
    early, early_pull = jax.vjp(
        layer_norm, tokens.astype(wide) + attn, e_gain.astype(wide), e_shift.astype(wide)
    )
    early_all = gather_square(zs, 3, early.astype(low_type)).reshape(rows, depth)
    inner = jnp.dot(early_all, w1, preferred_element_type=wide) + i_bias
    act, gelu_pull = jax.vjp(gelu_exact, inner)
    act_low = act.astype(low_type)
    partial = jnp.dot(act_low, w2, preferred_element_type=wide).astype(low_type)
    partial = exchange_square(zs, 4, partial.reshape(2, 2, n, depth))
    branch = jnp.sum(partial.astype(wide), axis=(0, 1)) + o_bias.astype(wide)
    result, final_pull = jax.vjp(
        layer_norm, early + branch, f_gain.astype(wide), f_shift.astype(wide)
    )
    output = result.astype(low_type)
    final_grads = final_pull(cotangent.astype(wide))
    branch_grad = final_grads[0].astype(low_type)
    outer_bias_grad = jnp.sum(branch_grad.astype(wide), axis=0)
    branch_all = gather_square(zs, 5, branch_grad).reshape(rows, depth)
    act_grad = jnp.einsum("td,fd->tf", branch_all, w2, preferred_element_type=wide)
    inner_grad = gelu_pull(act_grad)[0].astype(low_type)
    partial = jnp.einsum("tf,df->td", inner_grad, w1, preferred_element_type=wide).astype(low_type)
    partial = exchange_square(zs, 6, partial.reshape(2, 2, n, depth))
    grad2 = jnp.einsum("tf,td->fd", act_low, branch_all, preferred_element_type=wide)
    grad1 = jnp.einsum("td,tf->df", early_all, inner_grad, preferred_element_type=wide)
    inner_bias_grad = jnp.sum(inner_grad.astype(wide), axis=0)
    early_grad = final_grads[0] + jnp.sum(partial.astype(wide), axis=(0, 1))
    early_grads = early_pull(early_grad)
    attn_grad = early_grads[0].astype(low_type)
    mixed_grad = jnp.einsum("td,cd->tc", attn_grad, wm, preferred_element_type=wide)
    mixed_grad = jnp.transpose(
        mixed_grad.astype(low_type).reshape(n, GROUPS, LOCAL * HEAD), (1, 0, 2)
    )
    mixed_grad = jnp.pad(mixed_grad, ((0, 0), (0, 0), (0, PACK - LOCAL * HEAD)))
    grad_all = exchange_line(zs, 7, mixed_grad).reshape(rows, PACK)
    gradm = jnp.einsum("tc,td->cd", mixed_tok, attn_grad, preferred_element_type=wide)
    mix_bias_grad = jnp.sum(attn_grad.astype(wide), axis=0)

    delta = jnp.sum(
        (grad_all.astype(wide) * mixed_wide)[:, : LOCAL * HEAD].reshape(rows, LOCAL, HEAD), axis=2
    )

    def as_stat(values):
        return jnp.transpose(values.reshape(tiles, tile, LOCAL), (0, 2, 1))

    def same_stat(values):
        return jnp.broadcast_to(
            values.astype(wide).reshape(tiles, 1, tile), (tiles, LOCAL, tile)
        )

    stats = jnp.stack(
        [same_stat(first), same_stat(last), as_stat(lse[:, :LOCAL]), as_stat(delta)], axis=2
    )
    stats = jnp.pad(stats, ((0, 0), (0, 0), (0, 4), (0, 0)))
    query_grad, dkv = attend_backward(queries, kv_all, grad_all, stats, bounds, tile, block)

    def slabs(grad, extras):
        grad = grad.astype(low_type).reshape(devices, s, -1)
        rest = -s % 8
        rest += 0 if rest >= extras.shape[0] else 8
        extras = jnp.concatenate(
            [extras.astype(low_type), jnp.zeros((rest - extras.shape[0], extras.shape[1]), low_type)]
        )
        extras = jnp.broadcast_to(extras[None], (devices,) + extras.shape)
        return jnp.concatenate([grad, extras], axis=1).reshape(2, 2, zs, GROUPS, 2, s + rest, -1)

    mix_extras = jnp.stack(
        [
            mix_bias_grad, early_grads[1], early_grads[2],
            outer_bias_grad, final_grads[1], final_grads[2],
        ]
    )
    dkv, out1, out2, outm = reduce_keys(
        zs,
        dkv.reshape(2, 2, zs, GROUPS, 2, n, WIDE),
        slabs(grad1, inner_bias_grad[None]),
        grad2.astype(low_type).reshape(zs, GROUPS, 2, e, depth),
        slabs(gradm, mix_extras),
    )
    key_grad = jnp.sum(dkv.astype(wide), axis=0).astype(low_type).reshape(rows, WIDE)
    grads = jnp.concatenate([key_grad, query_grad], axis=1)
    gradq = jnp.einsum("tc,td->cd", tok_all, grads, preferred_element_type=wide)
    bias_grad = jnp.sum(grads.astype(wide), axis=0)
    partial = jnp.einsum("td,cd->tc", grads, w_qkv, preferred_element_type=wide).astype(low_type)
    partial, outq = reduce_tokens(
        zs, partial.reshape(GROUPS, n, depth), slabs(gradq, bias_grad[None])
    )
    input_grad = early_grads[0] + jnp.sum(partial.astype(wide), axis=0)

    def own(vector, count):
        return lax.dynamic_slice_in_dim(vector, device * count, count, 0).astype(wide)

    outq = outq.astype(wide)
    kv_out = outq[:, :, :WIDE].reshape(GROUPS, -1, LOCAL, 2, HEAD)
    q_out = outq[:, :, WIDE:].reshape(GROUPS, -1, LOCAL, 2, HEAD)[:, :, :, 0]

    def unpacked(values):
        return jnp.transpose(values, (1, 0, 2, 3)).reshape(-1, depth)

    q_out, k_out, v_out = unpacked(q_out), unpacked(kv_out[:, :, :, 0]), unpacked(kv_out[:, :, :, 1])
    inner_out = jnp.transpose(out1[:, :s], (1, 0, 2)).reshape(s, ff).astype(wide)
    return (
        output,
        input_grad.astype(low_type),
        q_out[:s],
        own(q_out[s], s),
        k_out[:s],
        v_out[:s],
        own(v_out[s], s),
        outm[:s],
        own(outm[s], s),
        own(outm[s + 1], s),
        own(outm[s + 2], s),
        inner_out,
        own(out1[:, s].reshape(ff), e),
        out2,
        own(outm[s + 3], s),
        own(outm[s + 4], s),
        own(outm[s + 5], s),
    )


def on_device(
    tokens,
    cotangent,
    doc_lengths,
    query_weight,
    query_bias,
    key_weight,
    value_weight,
    value_bias,
    mix_weight,
    mix_bias,
    early_gain,
    early_shift,
    inner_weight,
    inner_bias,
    outer_weight,
    outer_bias,
    final_gain,
    final_shift,
):
    n, depth = tokens.shape
    cycle = lax.axis_size("row")
    devices = lax.axis_size("au") * cycle
    s = query_weight.shape[0]
    ff = inner_weight.shape[1]
    quarter = ff // 4
    e = outer_weight.shape[0]
    rows = GROUPS * n
    total_tokens = n * devices
    me = Spot()
    vectors = [
        vector.reshape(1, -1)
        for vector in (
            query_bias, value_bias, mix_bias, early_gain, early_shift,
            outer_bias, final_gain, final_shift,
        )
    ]
    vectors.append(inner_bias.reshape(1, -1))
    toks, queries, w_qkv, vec, kv_all, w1, wm, mixed, mixed_wide, lse = first_kernel(
        doc_lengths, tokens, query_weight, key_weight, value_weight, vectors,
        inner_weight, mix_weight, e,
    )
    queries = queries.reshape(rows, WIDE)
    kv_all = kv_all.reshape(total_tokens, WIDE)
    w_qkv = w_qkv.reshape(depth, -1)
    w1 = w1.reshape(depth, quarter)
    wm = wm.reshape(depth, depth)
    output, hidden_grad, grad_all, summ, sum1, sum2 = middle_kernel(
        mixed.reshape(GROUPS, n, PACK), tokens, cotangent, wm, w1, outer_weight, vec, s, e
    )
    grad_all = grad_all.reshape(rows, PACK)
    pieces, outqk, out1, out2, outm = turn_kernel(
        doc_lengths, queries, kv_all, grad_all, mixed_wide, lse, toks, w_qkv, sum1, sum2, summ
    )
    results = final_kernel(output, hidden_grad, pieces, outqk, out1, out2, outm, s, e)
    return tuple(
        result.reshape(-1) if result.shape[0] == 1 else result for result in results
    )


def solution(mesh):
    both = P(("au", "row"), None)
    flat = P(("au", "row"))
    in_specs = (
        both, both, P(), both, flat, both, both, flat, both, flat, flat, flat,
        both, flat, both, flat, flat, flat,
    )
    out_specs = (
        both, both, both, flat, both, both, flat, both, flat, flat, flat,
        both, flat, both, flat, flat, flat,
    )
    fast = mesh.shape["au"] == 4 and mesh.shape["row"] == 2 * GROUPS
    return jax.shard_map(
        on_device if fast else on_device_general, mesh=mesh, in_specs=in_specs, out_specs=out_specs, check_vma=False
    )
```

```python
import functools

import jax
import jax.numpy as jnp
import numpy as np
from jax import lax
from jax.experimental import pallas as pl
from jax.experimental.pallas import tpu as pltpu
from jax.sharding import PartitionSpec as P

HEAD = 64
HEADS = 12
GROUPS = 4
LOCAL = HEADS // GROUPS
LANES = 2 * HEAD
WIDE = LOCAL * LANES
PACK = 256
eps_norm = 1e-06
mask_fill = -1000000000.0
lowest_start = -1e30
low_type = jnp.bfloat16
wide = jnp.float32
MESH = pl.DeviceIdType.MESH
VMEM_LIMIT = 62 * 1024 * 1024
NEAR_LIMIT = 30 * 1024 * 1024
TURN_LIMIT = 48 * 1024 * 1024


def layer_norm(hidden, gain, shift):
    mean = jnp.mean(hidden, axis=-1, keepdims=True)
    centered = hidden - mean
    spread = jnp.mean(centered * centered, axis=-1, keepdims=True)
    return centered * lax.rsqrt(spread + eps_norm) * gain + shift


def gelu_exact(values):
    return jax.nn.gelu(values, approximate=False)


class Place:
    def __init__(self, zs):
        self.zs = zs
        a = lax.axis_index("au")
        r = lax.axis_index("row")
        self.x, self.c = a // 2, a % 2
        self.y, q = r % 2, r // 2
        self.g, self.z = q % GROUPS, q // GROUPS

    def at(self, x=None, c=None, z=None, g=None, y=None):
        x = self.x if x is None else x
        c = self.c if c is None else c
        z = self.z if z is None else z
        g = self.g if g is None else g
        y = self.y if y is None else y
        return (x * 2 + c, (z * GROUPS + g) * 2 + y)

    def sibling(self):
        return self.at(c=1 - self.c)

    def line(self):
        return [((self.g + k) % GROUPS, (self.g + GROUPS - k) % GROUPS) for k in range(1, GROUPS)]

    def column(self):
        count = self.zs * GROUPS
        q = self.z * GROUPS + self.g
        result = []
        for k in range(1, count):
            to, source = (q + k) % count, (q + count - k) % count
            result.append(((to // GROUPS, to % GROUPS), (source // GROUPS, source % GROUPS)))
        return result

    def plane(self, everywhere=True):
        result = []
        for dx in range(2):
            for dy in range(2):
                for dz in range(self.zs if everywhere else 1):
                    if dx + dy + dz == 0:
                        continue
                    to = ((self.x + dx) % 2, (self.z + dz) % self.zs, (self.y + dy) % 2)
                    source = (
                        (self.x + dx) % 2,
                        (self.z + self.zs - dz) % self.zs,
                        (self.y + dy) % 2,
                    )
                    result.append((to, source))
        return result


class Copies:
    def __init__(self, send, recv, local):
        self.send, self.recv, self.local = send, recv, local
        self.count = 0
        self.local_count = 0
        self.started = []
        self.local_started = []

    def push(self, source, target, device):
        copy = pltpu.make_async_remote_copy(
            src_ref=source,
            dst_ref=target,
            send_sem=self.send.at[self.count],
            recv_sem=self.recv.at[self.count],
            device_id=device,
            device_id_type=MESH,
        )
        self.count += 1
        copy.start()
        self.started.append(copy)
        return copy

    def keep(self, source, target):
        copy = pltpu.make_async_copy(source, target, self.local.at[self.local_count])
        self.local_count += 1
        copy.start()
        return copy

    def finish(self):
        for copy in self.started:
            copy.wait_send()


def greet(devices, partner=None, crossing=None):
    barrier = pltpu.get_barrier_semaphore()
    for device in devices:
        pl.semaphore_signal(barrier, inc=1, device_id=device, device_id_type=MESH)
    if partner is None:
        pl.semaphore_wait(barrier, len(devices))
        return

    @pl.when(crossing)
    def _():
        pl.semaphore_signal(barrier, inc=1, device_id=partner, device_id_type=MESH)
        pl.semaphore_wait(barrier, len(devices) + 1)

    @pl.when(jnp.logical_not(crossing))
    def _():
        pl.semaphore_wait(barrier, len(devices))


def comm_call(body, name, ident, outs, copies, locals_, args, spaces=None, out_spaces=None, scratch=()):
    spaces = [pl.ANY] * len(args) if spaces is None else spaces
    out_spaces = [pl.ANY] * len(outs) if out_spaces is None else out_spaces
    return pl.pallas_call(
        body,
        name=name,
        out_shape=tuple(outs),
        in_specs=[pl.BlockSpec(memory_space=space) for space in spaces],
        out_specs=tuple(pl.BlockSpec(memory_space=space) for space in out_spaces),
        scratch_shapes=[
            pltpu.SemaphoreType.DMA((max(copies, 1),)),
            pltpu.SemaphoreType.DMA((max(copies, 1),)),
            pltpu.SemaphoreType.DMA((max(locals_, 1),)),
            *scratch,
        ],
        compiler_params=pltpu.CompilerParams(
            collective_id=ident, has_side_effects=True, vmem_limit_bytes=VMEM_LIMIT
        ),
    )(*args)


def spread_tokens(zs, tokens, slab):
    n, width = tokens.shape
    groups, rows, columns = slab.shape
    plane = 4 * zs - 1

    def body(tok, piece, tok_all, w_all, send, recv, local):
        me = Place(zs)
        copies = Copies(send, recv, local)
        greet(
            [me.at(g=to) for to, _ in me.line()]
            + [me.at(x=to[0], z=to[1], y=to[2]) for to, _ in me.plane()]
            + [me.sibling()]
        )
        first = [
            copies.push(
                piece.at[to], w_all.at[me.x, me.c, me.z, me.g, me.y], me.at(g=to)
            )
            for to, _ in me.line()
        ]
        own = copies.keep(piece.at[me.g], w_all.at[me.x, me.c, me.z, me.g, me.y])
        arrivals = [copies.push(tok, tok_all.at[me.g], me.at(g=to)) for to, _ in me.line()]
        mine = copies.keep(tok, tok_all.at[me.g])
        own.wait()
        for copy in first:
            copy.wait_recv()
        block = w_all.at[me.x, me.c, me.z, :, me.y]
        second = [
            copies.push(block, block, me.at(x=to[0], z=to[1], y=to[2])) for to, _ in me.plane()
        ]
        arrivals.append(copies.push(block, block, me.sibling()))
        for copy, (_, source) in zip(second, me.plane()):
            copy.wait_recv()
            part = w_all.at[source[0], me.c, source[1], :, source[2]]
            arrivals.append(copies.push(part, part, me.sibling()))
        for copy in arrivals:
            copy.wait_recv()
        mine.wait()
        copies.finish()

    return comm_call(
        body,
        "spread_tokens",
        0,
        [
            jax.ShapeDtypeStruct((GROUPS, n, width), low_type),
            jax.ShapeDtypeStruct((2, 2, zs, GROUPS, 2, rows, columns), low_type),
        ],
        2 * (GROUPS - 1) + 2 * plane + 1,
        2,
        (tokens, slab),
    )


def spread_keys(zs, keys, inner, outer, mix):
    groups, n, width = keys.shape
    quarters, rows, columns = inner.shape
    tall, _ = outer.shape
    plane, column = 4 * zs - 1, GROUPS * zs - 1

    def body(kv, w1s, w2s, wms, kv_all, w1, w2, wm, send, recv, local, swap_send, swap_recv):
        me = Place(zs)
        copies = Copies(send, recv, local)
        crossing = me.c != me.y
        greet(
            [me.at(x=to[0], z=to[1], y=to[2]) for to, _ in me.plane()]
            + [me.at(z=to[0], g=to[1]) for to, _ in me.column()]
            + [me.at(z=to[0], g=to[1], c=me.y, y=me.c) for to, _ in me.column()]
            + [me.sibling()],
            me.at(c=me.y, y=me.c),
            crossing,
        )

        def here(ref):
            return ref.at[me.x, me.c, me.z, me.g, me.y]

        flat = me.plane(everywhere=False)
        own = [
            copies.keep(w1s.at[me.x * 2 + me.y], here(w1)),
            copies.keep(wms, here(wm)),
            copies.keep(kv, kv_all.at[me.x, me.c, me.z, :, me.y]),
        ]
        w1_first = [
            copies.push(w1s.at[to[0] * 2 + to[2]], here(w1), me.at(x=to[0], y=to[2]))
            for to, _ in flat
        ]
        wm_first = [
            copies.push(wms, here(wm), me.at(z=to[0], g=to[1])) for to, _ in me.column()
        ]
        mine = kv_all.at[me.x, me.c, me.z, :, me.y]
        kv_first = [
            copies.push(kv, mine, me.at(x=to[0], z=to[1], y=to[2])) for to, _ in me.plane()
        ]
        arrivals = [copies.push(kv, mine, me.sibling())]
        w2_first = [
            copies.push(
                w2s, w2.at[me.z, me.g, me.y], me.at(z=to[0], g=to[1], c=me.y, y=me.c)
            )
            for to, _ in me.column()
        ]
        exchanged = pltpu.make_async_remote_copy(
            src_ref=w2s,
            dst_ref=w2.at[me.z, me.g, me.y],
            send_sem=swap_send,
            recv_sem=swap_recv,
            device_id=me.at(c=me.y, y=me.c),
            device_id_type=MESH,
        )
        stays = pltpu.make_async_copy(w2s, w2.at[me.z, me.g, me.y], swap_recv)

        @pl.when(crossing)
        def _():
            exchanged.start()

        @pl.when(jnp.logical_not(crossing))
        def _():
            stays.start()

        own[0].wait()
        for copy in w1_first:
            copy.wait_recv()
        block = w1.at[:, me.c, me.z, me.g, :]
        w1_second = [
            copies.push(block, block, me.at(z=to[0], g=to[1])) for to, _ in me.column()
        ]
        arrivals.append(copies.push(block, block, me.sibling()))
        own[1].wait()
        for copy in wm_first:
            copy.wait_recv()
        block = wm.at[me.x, me.c, :, :, me.y]
        wm_second = [copies.push(block, block, me.at(x=to[0], y=to[2])) for to, _ in flat]
        arrivals.append(copies.push(block, block, me.sibling()))
        for copy, (_, source) in zip(kv_first, me.plane()):
            copy.wait_recv()
            part = kv_all.at[source[0], me.c, source[1], :, source[2]]
            arrivals.append(copies.push(part, part, me.sibling()))

        @pl.when(crossing)
        def _():
            exchanged.wait_recv()
            exchanged.wait_send()

        @pl.when(jnp.logical_not(crossing))
        def _():
            stays.wait()

        part = w2.at[me.z, me.g, me.c]
        arrivals.append(copies.push(part, part, me.sibling()))
        for copy, (_, source) in zip(wm_second, flat):
            copy.wait_recv()
            part = wm.at[source[0], me.c, :, :, source[2]]
            arrivals.append(copies.push(part, part, me.sibling()))
        for copy, (_, source) in zip(w2_first, me.column()):
            copy.wait_recv()
            part = w2.at[source[0], source[1], me.c]
            arrivals.append(copies.push(part, part, me.sibling()))
        for copy, (_, source) in zip(w1_second, me.column()):
            copy.wait_recv()
            part = w1.at[:, me.c, source[0], source[1], :]
            arrivals.append(copies.push(part, part, me.sibling()))
        for copy in arrivals:
            copy.wait_recv()
        own[2].wait()
        copies.finish()

    return comm_call(
        body,
        "spread_keys",
        1,
        [
            jax.ShapeDtypeStruct((2, 2, zs, GROUPS, 2, n, width), low_type),
            jax.ShapeDtypeStruct((2, 2, zs, GROUPS, 2, rows, columns), low_type),
            jax.ShapeDtypeStruct((zs, GROUPS, 2, tall, columns), low_type),
            jax.ShapeDtypeStruct((2, 2, zs, GROUPS, 2) + mix.shape, low_type),
        ],
        2 * plane + 1 + 2 * (3 + column + 1 + column) + column + 3 + 8,
        3,
        (keys, inner, outer, mix),
        scratch=(pltpu.SemaphoreType.DMA, pltpu.SemaphoreType.DMA),
    )


def exchange_line(zs, ident, pieces):
    def body(source, target, send, recv, local):
        me = Place(zs)
        copies = Copies(send, recv, local)
        greet([me.at(g=to) for to, _ in me.line()])
        arrivals = [
            copies.push(source.at[to], target.at[me.g], me.at(g=to)) for to, _ in me.line()
        ]
        own = copies.keep(source.at[me.g], target.at[me.g])
        for copy in arrivals:
            copy.wait_recv()
        own.wait()
        copies.finish()

    return comm_call(
        body,
        "exchange_line",
        ident,
        [jax.ShapeDtypeStruct(pieces.shape, pieces.dtype)],
        GROUPS - 1,
        1,
        (pieces,),
    )[0]


def gather_square(zs, ident, rows):
    def body(source, target, send, recv, local):
        me = Place(zs)
        copies = Copies(send, recv, local)
        flat = me.plane(everywhere=False)
        greet([me.at(x=to[0], y=to[2]) for to, _ in flat])
        place = target.at[me.x, me.y]
        arrivals = [copies.push(source, place, me.at(x=to[0], y=to[2])) for to, _ in flat]
        own = copies.keep(source, place)
        for copy in arrivals:
            copy.wait_recv()
        own.wait()
        copies.finish()

    return comm_call(
        body,
        "gather_square",
        ident,
        [jax.ShapeDtypeStruct((2, 2) + rows.shape, rows.dtype)],
        3,
        1,
        (rows,),
    )[0]


def exchange_square(zs, ident, pieces):
    def body(source, target, send, recv, local):
        me = Place(zs)
        copies = Copies(send, recv, local)
        flat = me.plane(everywhere=False)
        greet([me.at(x=to[0], y=to[2]) for to, _ in flat])
        place = target.at[me.x, me.y]
        arrivals = [
            copies.push(source.at[to[0], to[2]], place, me.at(x=to[0], y=to[2]))
            for to, _ in flat
        ]
        own = copies.keep(source.at[me.x, me.y], place)
        for copy in arrivals:
            copy.wait_recv()
        own.wait()
        copies.finish()

    return comm_call(
        body,
        "exchange_square",
        ident,
        [jax.ShapeDtypeStruct(pieces.shape, pieces.dtype)],
        3,
        1,
        (pieces,),
    )[0]


def loop(count, step):
    def body(index, carry):
        step(index)
        return carry

    lax.fori_loop(0, count, body, 0)


def total_of(*values):
    result = values[0].astype(wide)
    for value in values[1:]:
        result = result + value.astype(wide)
    return result


def reduce_keys(zs, dkv, grad1, grad2, gradm):
    n, width = dkv.shape[-2:]
    rows, columns = grad1.shape[-2:]
    rowsm = gradm.shape[-2]
    tall = grad2.shape[-2]
    plane, column = 4 * zs - 1, GROUPS * zs - 1
    count = GROUPS * zs

    def body(
        dkv_ref, g1, g2, gm, dkv_out, out1, out2, outm,
        send, recv, local,
        swap_send, swap_recv, kst, s1, p1, f1, s2, p2, sm, pm, fm, tm,
    ):
        me = Place(zs)
        copies = Copies(send, recv, local)
        crossing = me.c != me.y
        greet(
            [me.at(x=to[0], z=to[1], y=to[2]) for to, _ in me.plane()]
            + [me.at(z=to[0], g=to[1]) for to, _ in me.column()]
            + [me.at(z=to[0], g=to[1], c=me.y, y=me.c) for to, _ in me.column()]
            + [me.sibling()],
            me.at(c=me.y, y=me.c),
            crossing,
        )

        flat = me.plane(everywhere=False)
        other = 1 - me.c
        order = [to for to, _ in me.plane()] + [(me.x, me.z, me.y)]
        w1_half = copies.push(g1.at[:, other], s1, me.sibling())
        w2_half = copies.push(g2.at[:, :, other], s2, me.sibling())
        k_half = [
            copies.push(
                dkv_ref.at[to[0], other, to[1], :, to[2]], kst.at[to[0], to[1], to[2]], me.sibling()
            )
            for to in order
        ]
        wm_half = copies.push(gm.at[:, other], sm, me.sibling())

        w1_half.wait_recv()

        def add1(index):
            x, z, g, y = index // (count * 2), index // (GROUPS * 2) % zs, index // 2 % GROUPS, index % 2
            s1[x, z, g, y] = total_of(s1[x, z, g, y], g1[x, me.c, z, g, y]).astype(low_type)

        loop(4 * count, add1)
        w1_push = [
            copies.push(s1.at[:, to[0], to[1], :], p1.at[slot], me.at(z=to[0], g=to[1]))
            for slot, (to, _) in enumerate(me.column())
        ]
        w2_half.wait_recv()

        def add2(index):
            z, g = index // GROUPS, index % GROUPS
            s2[z, g] = total_of(s2[z, g], g2[z, g, me.c]).astype(low_type)

        loop(count, add2)
        w2_push = [
            copies.push(
                s2.at[to[0], to[1]], p2.at[slot + 1], me.at(z=to[0], g=to[1], c=me.y, y=me.c)
            )
            for slot, (to, _) in enumerate(me.column())
        ]
        exchanged = pltpu.make_async_remote_copy(
            src_ref=s2.at[me.z, me.g],
            dst_ref=p2.at[0],
            send_sem=swap_send,
            recv_sem=swap_recv,
            device_id=me.at(c=me.y, y=me.c),
            device_id_type=MESH,
        )
        stays = pltpu.make_async_copy(s2.at[me.z, me.g], p2.at[0], swap_recv)

        @pl.when(crossing)
        def _():
            exchanged.start()

        @pl.when(jnp.logical_not(crossing))
        def _():
            stays.start()

        k_push = []
        for slot, to in enumerate(order):
            k_half[slot].wait_recv()

            def addk(g, to=to):
                kst[to[0], to[1], to[2], g] = total_of(
                    kst[to[0], to[1], to[2], g], dkv_ref[to[0], me.c, to[1], g, to[2]]
                ).astype(low_type)

            loop(GROUPS, addk)
            if slot < plane:
                k_push.append(
                    copies.push(
                        kst.at[to[0], to[1], to[2]],
                        dkv_out.at[slot],
                        me.at(x=to[0], z=to[1], y=to[2]),
                    )
                )
        wm_half.wait_recv()

        def addm(index):
            x, z, g, y = index // (count * 2), index // (GROUPS * 2) % zs, index // 2 % GROUPS, index % 2
            sm[x, z, g, y] = total_of(sm[x, z, g, y], gm[x, me.c, z, g, y]).astype(low_type)

        loop(4 * count, addm)
        wm_push = [
            copies.push(sm.at[to[0], :, :, to[2]], pm.at[slot], me.at(x=to[0], y=to[2]))
            for slot, (to, _) in enumerate(flat)
        ]
        keep = copies.keep(kst.at[me.x, me.z, me.y], dkv_out.at[plane])
        for copy in wm_push:
            copy.wait_recv()

        def addf(index):
            z, g = index // GROUPS, index % GROUPS
            fm[z, g] = total_of(sm[me.x, z, g, me.y], pm[0, z, g], pm[1, z, g], pm[2, z, g]).astype(
                low_type
            )

        loop(count, addf)
        wm_last = [
            copies.push(fm.at[to[0], to[1]], tm.at[slot], me.at(z=to[0], g=to[1]))
            for slot, (to, _) in enumerate(me.column())
        ]
        for copy in w1_push:
            copy.wait_recv()

        def addg(index):
            x, y = index // 2, index % 2
            f1[x, y] = total_of(
                s1[x, me.z, me.g, y], *[p1[slot, x, y] for slot in range(column)]
            ).astype(low_type)

        loop(4, addg)
        quarter = out1.at[me.x * 2 + me.y]
        w1_last = [
            copies.push(f1.at[to[0], to[2]], quarter, me.at(x=to[0], y=to[2])) for to, _ in flat
        ]
        keep1 = copies.keep(f1.at[me.x, me.y], quarter)

        @pl.when(crossing)
        def _():
            exchanged.wait_recv()
            exchanged.wait_send()

        @pl.when(jnp.logical_not(crossing))
        def _():
            stays.wait()

        for copy in w2_push:
            copy.wait_recv()
        out2[...] = total_of(*[p2[slot] for slot in range(column + 1)])
        for copy in wm_last:
            copy.wait_recv()
        outm[...] = total_of(fm[me.z, me.g], *[tm[slot] for slot in range(column)])
        for copy in w1_last + k_push:
            copy.wait_recv()
        keep.wait()
        keep1.wait()
        copies.finish()

    vmem = pltpu.VMEM
    return comm_call(
        body,
        "reduce_keys",
        8,
        [
            jax.ShapeDtypeStruct((plane + 1, GROUPS, n, width), low_type),
            jax.ShapeDtypeStruct((4, rows, columns), low_type),
            jax.ShapeDtypeStruct((tall, columns), wide),
            jax.ShapeDtypeStruct((rowsm, columns), wide),
        ],
        3 + (plane + 1) + 2 * column + plane + 3 + column + 3,
        2,
        (dkv, grad1, grad2, gradm),
        spaces=[vmem] * 4,
        out_spaces=[pl.ANY, pl.ANY, vmem, vmem],
        scratch=(
            pltpu.SemaphoreType.DMA,
            pltpu.SemaphoreType.DMA,
            vmem((2, zs, 2, GROUPS, n, width), low_type),
            vmem((2, zs, GROUPS, 2, rows, columns), low_type),
            vmem((column, 2, 2, rows, columns), low_type),
            vmem((2, 2, rows, columns), low_type),
            vmem((zs, GROUPS, tall, columns), low_type),
            vmem((column + 1, tall, columns), low_type),
            vmem((2, zs, GROUPS, 2, rowsm, columns), low_type),
            vmem((3, zs, GROUPS, rowsm, columns), low_type),
            vmem((zs, GROUPS, rowsm, columns), low_type),
            vmem((column, rowsm, columns), low_type),
        ),
    )


def reduce_tokens(zs, dx, gradq):
    rows, columns = gradq.shape[-2:]
    plane = 4 * zs - 1
    count = GROUPS * zs

    def body(dx_ref, gq, dx_out, outq, send, recv, local, sq, pq, fq):
        me = Place(zs)
        copies = Copies(send, recv, local)
        greet(
            [me.at(g=to) for to, _ in me.line()]
            + [me.at(x=to[0], z=to[1], y=to[2]) for to, _ in me.plane()]
            + [me.sibling()]
        )
        half = copies.push(gq.at[:, 1 - me.c], sq, me.sibling())
        arrivals = [
            copies.push(dx_ref.at[to], dx_out.at[me.g], me.at(g=to)) for to, _ in me.line()
        ]
        own = copies.keep(dx_ref.at[me.g], dx_out.at[me.g])
        half.wait_recv()

        def add1(index):
            x, z, g, y = index // (count * 2), index // (GROUPS * 2) % zs, index // 2 % GROUPS, index % 2
            sq[x, z, g, y] = total_of(sq[x, z, g, y], gq[x, me.c, z, g, y]).astype(low_type)

        loop(4 * count, add1)
        second = [
            copies.push(
                sq.at[to[0], to[1], :, to[2]], pq.at[slot], me.at(x=to[0], z=to[1], y=to[2])
            )
            for slot, (to, _) in enumerate(me.plane())
        ]
        for copy in second:
            copy.wait_recv()

        def add2(g):
            fq[g] = total_of(
                sq[me.x, me.z, g, me.y], *[pq[slot, g] for slot in range(plane)]
            ).astype(low_type)

        loop(GROUPS, add2)
        arrivals += [
            copies.push(fq.at[to], outq.at[me.g], me.at(g=to)) for to, _ in me.line()
        ]
        keep = copies.keep(fq.at[me.g], outq.at[me.g])
        for copy in arrivals:
            copy.wait_recv()
        own.wait()
        keep.wait()
        copies.finish()

    vmem = pltpu.VMEM
    return comm_call(
        body,
        "reduce_tokens",
        9,
        [
            jax.ShapeDtypeStruct(dx.shape, low_type),
            jax.ShapeDtypeStruct((GROUPS, rows, columns), low_type),
        ],
        1 + 2 * (GROUPS - 1) + plane,
        2,
        (dx, gradq),
        spaces=[pl.ANY, vmem],
        scratch=(
            vmem((2, zs, GROUPS, 2, rows, columns), low_type),
            vmem((plane, GROUPS, rows, columns), low_type),
            vmem((GROUPS, rows, columns), low_type),
        ),
    )


NEXT = (((1,), (1,)), ((), ()))
DOWN = (((0,), (0,)), ((), ()))


def attend_forward(queries, keys, bounds, low, high, tile, block):
    total_rows = queries.shape[0]

    def body(bounds_ref, q_ref, kv_ref, low_ref, high_ref, out_ref, keep_ref, lse_ref):
        def one(turn, unused):
            rows = pl.ds(pl.multiple_of(turn * tile, tile), tile)
            first, last = low_ref[rows, :], high_ref[rows, :]
            heads = [
                q_ref[rows, h * LANES : (h + 1) * LANES] * jnp.asarray(0.125, low_type)
                for h in range(LOCAL)
            ]

            def step(j, carry):
                begin = pl.multiple_of(j * block, block)
                place = begin + lax.broadcasted_iota(jnp.int32, (tile, block), 1)
                same = (place >= first) & (place < last)
                result = []
                for h in range(LOCAL):
                    top, total, mixed = carry[h]
                    kv = kv_ref[pl.ds(begin, block), h * LANES : (h + 1) * LANES]
                    scores = lax.dot_general(heads[h], kv, NEXT, preferred_element_type=wide)
                    scores = jnp.where(same, scores, mask_fill)
                    new_top = jnp.maximum(top, jnp.max(scores, axis=1, keepdims=True))
                    factor = jnp.exp(top - new_top)
                    powers = jnp.exp(scores - new_top)
                    total = total * factor + jnp.sum(powers, axis=1, keepdims=True)
                    mixed = mixed * factor + jnp.dot(
                        powers.astype(low_type), kv, preferred_element_type=wide
                    )
                    result.append((new_top, total, mixed))
                return tuple(result)

            start = tuple(
                (
                    jnp.full((tile, 1), lowest_start, wide),
                    jnp.zeros((tile, 1), wide),
                    jnp.zeros((tile, LANES), wide),
                )
                for _ in range(LOCAL)
            )
            done = lax.fori_loop(bounds_ref[turn, 0], bounds_ref[turn, 1], step, start)
            lane = lax.broadcasted_iota(jnp.int32, (tile, LANES), 1)
            upper = lane >= HEAD
            mixes = [mixed / total for _, total, mixed in done]
            turned = [pltpu.roll(mixed, HEAD, 1) for mixed in mixes]
            front = jnp.where(upper, mixes[1], turned[0])
            back = jnp.where(upper, 0.0, turned[2])
            both = jnp.concatenate([front, back], axis=1)
            keep_ref[rows, :] = both
            out_ref[rows, :] = both.astype(low_type)
            ends = [top + jnp.log(total) for top, total, _ in done]
            lse_ref[rows, :] = jnp.where(lane == 0, ends[0], jnp.where(lane == 1, ends[1], ends[2]))
            return unused

        lax.fori_loop(0, total_rows // tile, one, 0)

    vmem = pl.BlockSpec(memory_space=pltpu.VMEM)
    return pl.pallas_call(
        body,
        name="attend_forward",
        out_shape=(
            jax.ShapeDtypeStruct((total_rows, PACK), low_type),
            jax.ShapeDtypeStruct((total_rows, PACK), wide),
            jax.ShapeDtypeStruct((total_rows, LANES), wide),
        ),
        in_specs=[pl.BlockSpec(memory_space=pltpu.SMEM)] + [vmem] * 4,
        out_specs=(vmem,) * 3,
        compiler_params=pltpu.CompilerParams(vmem_limit_bytes=VMEM_LIMIT),
    )(bounds, queries, keys, low, high)


def attend_backward(queries, keys, grads, stats, bounds, tile, block):
    total_rows = queries.shape[0]
    tokens = keys.shape[0]

    def body(bounds_ref, q_ref, kv_ref, do_ref, stat_ref, dq_ref, dkv_ref, sums):
        h = pl.program_id(0)
        zeros = jnp.zeros((block, LANES), wide)

        def clear(j, unused):
            sums[pl.ds(pl.multiple_of(j * block, block), block), :] = zeros
            return unused

        lax.fori_loop(0, tokens // block, clear, 0)
        lane = lax.broadcasted_iota(jnp.int32, (tile, LANES), 1)
        upper = lane >= HEAD

        def one(turn, unused):
            rows = pl.ds(pl.multiple_of(turn * tile, tile), tile)
            q = q_ref[rows, :] * jnp.asarray(0.125, low_type)
            front = do_ref[rows, :LANES].astype(wide)
            back = do_ref[rows, LANES:].astype(wide)
            grad = jnp.where(h == 1, front, pltpu.roll(jnp.where(h == 0, front, back), HEAD, 1))
            grad = jnp.where(upper, grad, 0.0).astype(low_type)
            stat = stat_ref[turn, 0]
            first, last = stat[0:1, :], stat[1:2, :]
            lse, delta = stat[2:3, :], stat[3:4, :]

            def step(j, total):
                begin = pl.multiple_of(j * block, block)
                place = (begin + lax.broadcasted_iota(jnp.int32, (block, tile), 0)).astype(wide)
                same = (place >= first) & (place < last)
                kv = kv_ref[pl.ds(begin, block), :]
                scores = lax.dot_general(kv, q, NEXT, preferred_element_type=wide)
                probs = jnp.exp(jnp.where(same, scores, mask_fill) - lse)
                dots = lax.dot_general(kv, grad, NEXT, preferred_element_type=wide)
                score_grad = (probs * (dots - delta)).astype(low_type)
                sums[pl.ds(begin, block), :] += jnp.dot(
                    score_grad, q, preferred_element_type=wide
                ) + jnp.dot(probs.astype(low_type), grad, preferred_element_type=wide)
                return total + lax.dot_general(score_grad, kv, DOWN, preferred_element_type=wide)

            total = lax.fori_loop(
                bounds_ref[turn, 0], bounds_ref[turn, 1], step, jnp.zeros((tile, LANES), wide)
            )
            dq_ref[rows, :] = jnp.where(upper, 0.0, total * 0.125).astype(low_type)
            return unused

        lax.fori_loop(0, total_rows // tile, one, 0)

        def store(j, unused):
            part = pl.ds(pl.multiple_of(j * block, block), block)
            dkv_ref[part, :] = sums[part, :].astype(low_type)
            return unused

        lax.fori_loop(0, tokens // block, store, 0)

    return pl.pallas_call(
        body,
        name="attend_backward",
        grid=(LOCAL,),
        out_shape=(
            jax.ShapeDtypeStruct((total_rows, WIDE), low_type),
            jax.ShapeDtypeStruct((tokens, WIDE), low_type),
        ),
        in_specs=[
            pl.BlockSpec(memory_space=pltpu.SMEM),
            pl.BlockSpec((total_rows, LANES), lambda h: (0, h)),
            pl.BlockSpec((tokens, LANES), lambda h: (0, h)),
            pl.BlockSpec((total_rows, PACK), lambda h: (0, 0)),
            pl.BlockSpec((total_rows // tile, 1, 8, tile), lambda h: (0, h, 0, 0)),
        ],
        out_specs=(
            pl.BlockSpec((total_rows, LANES), lambda h: (0, h)),
            pl.BlockSpec((tokens, LANES), lambda h: (0, h)),
        ),
        scratch_shapes=[pltpu.VMEM((tokens, LANES), wide)],
        compiler_params=pltpu.CompilerParams(vmem_limit_bytes=VMEM_LIMIT),
    )(bounds, queries, keys, grads, stats)


class Spot(Place):
    def __init__(self):
        super().__init__(1)
        self.half = self.g // 2
        self.a = self.x * 2 + self.c
        self.p = (self.x + self.c) % 2
        self.selfish = self.g % 2 == self.p
        self.crossing = self.c != self.y

    def square(self):
        return [(to[0], to[2]) for to, _ in reversed(self.plane())]

    def readers(self):
        result = []
        for k in range(GROUPS):
            g = (self.g + k) % GROUPS
            result.append((g, self.at(x=(self.g + self.c) % 2, g=g)))
        return result

    def owners(self):
        result = []
        for dv in range(2):
            for du in range(2):
                u, v = (self.x + du) % 2, (self.half + dv) % 2
                result.append((u * 2 + v, self.at(x=u, g=2 * v + self.p)))
        return result

    def slot(self):
        return self.x * 2 + self.half


def count_of(flag):
    return jnp.where(flag, 1, 0)


def announce(always, maybe):
    barrier = pltpu.get_barrier_semaphore()
    for device in always:
        pl.semaphore_signal(barrier, inc=1, device_id=device, device_id_type=MESH)
    for flag, device in maybe:

        @pl.when(flag)
        def _(device=device):
            pl.semaphore_signal(barrier, inc=1, device_id=device, device_id_type=MESH)

    total = len(always)
    for flag, _ in maybe:
        total = total + count_of(flag)
    return barrier, total


class Scatter:
    def __init__(self, send, recv, here):
        self.send, self.recv, self.here = send, recv, here
        self.copies = []

    def start(self, pieces, target, slot):
        for source, device in pieces:
            self.send_one(source, target, slot, device)

    def send_one(self, source, target, slot, device):
        index = len(self.copies)
        copy = pltpu.make_async_remote_copy(
            src_ref=source,
            dst_ref=target,
            send_sem=self.send.at[index],
            recv_sem=self.recv.at[slot],
            device_id=device,
            device_id_type=MESH,
        )
        self.copies.append(copy)
        if index:
            copy.start()
            return
        stay = pltpu.make_async_copy(source, target, self.recv.at[slot])

        @pl.when(self.here)
        def _():
            stay.start()

        @pl.when(jnp.logical_not(self.here))
        def _():
            copy.start()

    def arrived(self, slot, target):
        pltpu.make_async_copy(target, target, self.recv.at[slot]).wait()

    def finish(self):
        for copy in self.copies[1:]:
            copy.wait_send()

        @pl.when(jnp.logical_not(self.here))
        def _():
            self.copies[0].wait_send()


SMALL = 16


def first_tables(s, e, width):
    column = np.arange(width)
    rows = [column % s, column // s, column % e, column // e]
    return np.stack(rows + [np.zeros_like(column)] * 4).astype(np.int32)


def first_kernel(lengths, tokens, wq, wk, wv, vectors, inner, mix, e):
    n, depth = tokens.shape
    s = wq.shape[0]
    quarter = inner.shape[1] // 4
    width = WIDE + PACK
    cols = width + LANES
    tables = jnp.asarray(first_tables(s, e, 2 * WIDE))
    count = len(vectors)

    def body(*refs):
        lengths_in, tok = refs[:2]
        arguments = refs[2 : 8 + count]
        (
            tok_out, q_out, wqkv_out, vec_out, kv_out, w1, wm, mixed_out, mixed_wide, lse_out,
            send, recv, local, tok_send, tok_recv,
            slab, toks, weights, kv_own, q_own, w1s, wms, vec, few, kv_all, scaled, sums,
            loaded, lengths_ref, lengths_sem, *places,
        ) = refs[8 + count :]
        wq_ref, wk_ref, wv_ref, tab = places[:4]
        vecs = places[4 : 4 + count]
        w1f, wmf = places[4 + count :]
        loads = [pltpu.make_async_copy(lengths_in, lengths_ref, lengths_sem)]
        loads[0].start()
        for index, (argument, place) in enumerate(zip(arguments, places)):
            loads.append(pltpu.make_async_copy(argument, place, loaded.at[index]))
            loads[-1].start()
        me = Spot()
        copies = Copies(send, recv, local)
        square = me.square()
        line = [to for to, _ in me.line()]
        sources = [device for _, device in me.owners()]
        barrier, expected = announce(
            [me.at(x=x, y=y) for x, y in square]
            + [me.at(g=to) for to in line]
            + sources[1:]
            + [me.sibling()],
            [(jnp.logical_not(me.selfish), sources[0])],
        )
        for copy in loads:
            copy.wait()
        lane = lax.broadcasted_iota(jnp.int32, (s, LANES), 1)
        lower = lane < HEAD
        for head in range(HEADS):
            pair = slice(head // 2 * LANES, head // 2 * LANES + LANES)
            k, v = wk_ref[:, pair], wv_ref[:, pair]
            if head % 2:
                k = pltpu.roll(k, HEAD, 1)
            else:
                v = pltpu.roll(v, HEAD, 1)
            g, h = head // LOCAL, head % LOCAL
            slab[g, :, h * LANES : (h + 1) * LANES] = jnp.where(lower, k, v).astype(low_type)
        for half in range(2):
            b0, b1, b2 = [
                wq_ref[:, (3 * half + index) * LANES : (3 * half + index + 1) * LANES]
                for index in range(3)
            ]
            r1, r2 = pltpu.roll(b1, HEAD, 1), pltpu.roll(b2, HEAD, 1)
            tiles = [(b0, b1), (jnp.where(lower, r1, r2), r2)]
            for odd, (front, back) in enumerate(tiles):
                slab[2 * half + odd, :, WIDE : WIDE + LANES] = front.astype(low_type)
                slab[2 * half + odd, :, WIDE + LANES : width] = jnp.where(lower, back, 0.0).astype(
                    low_type
                )
        wms[...] = wmf[...].astype(low_type)
        few[...] = jnp.zeros((s, LANES), wide)
        for index in range(count):
            few[index : index + 1, : vecs[index].shape[1]] = vecs[index][...]
        small = few[...]
        for g in range(GROUPS):
            slab[g, :, width:] = small.astype(low_type)
        pl.semaphore_wait(barrier, expected)

        view = weights
        place = view.at[me.a, me.g, me.y]
        slab_first = [copies.push(slab.at[to], place, me.at(g=to)) for to in line]
        slab_own = copies.keep(slab.at[me.g], place)
        for w in range(4):
            w1s[w] = w1f[:, w * quarter : (w + 1) * quarter].astype(low_type)
        place = w1.at[me.x, me.c, me.g, me.y]
        w1_first = [
            copies.push(w1s.at[x * 2 + y], place, me.at(x=x, y=y)) for x, y in square
        ]
        w1_own = copies.keep(w1s.at[me.x * 2 + me.y], place)
        wm_own = copies.keep(wms, wm.at[me.x, me.c, me.g, me.y])

        arrivals, weight_arrivals = [], []
        slab_own.wait()
        for copy in slab_first:
            copy.wait_recv()
        tokens_go = Scatter(tok_send, tok_recv, me.selfish)
        tokens_go.start([(tok, device) for _, device in me.readers()], toks.at[me.slot()], me.slot())
        block = view.at[me.a, :, me.y]
        slab_second = [copies.push(block, block, me.at(x=x, y=y)) for x, y in square]
        weight_arrivals.append(copies.push(block, block, me.sibling()))
        for copy, (x, y) in zip(slab_second, square):
            copy.wait_recv()
            block = view.at[x * 2 + me.c, :, y]
            weight_arrivals.append(copies.push(block, block, me.sibling()))
        w1_own.wait()
        for copy in w1_first:
            copy.wait_recv()
        for copy in weight_arrivals:
            copy.wait_recv()

        table = tab[...]

        def spread(pieces, within, owner):
            count = pieces.shape[0] * SMALL
            item = lax.broadcasted_iota(jnp.int32, (count, 2 * WIDE), 0)
            index = lax.broadcasted_iota(jnp.int32, (LANES, 2 * WIDE), 0)
            chosen = jnp.where(index == within, 1.0, 0.0).astype(low_type)
            pieces = pieces.astype(wide).reshape(count, LANES).astype(low_type)
            found = jnp.dot(pieces, chosen, preferred_element_type=wide)
            found = jnp.where((item >> 4) == owner, found, 0.0)
            return jnp.sum(found.reshape(count // SMALL, SMALL, 2 * WIDE), axis=0)

        every = spread(
            view[:, :, :, :SMALL, width:].reshape(32, SMALL, LANES), table[0:1], table[1:2]
        )
        w_me = me.x * 2 + me.y
        inner_bias = spread(
            view[w_me, :, :, :SMALL, width:].reshape(8, SMALL, LANES), table[2:3], table[3:4]
        )
        rows16 = lax.broadcasted_iota(jnp.int32, (SMALL, 2 * WIDE), 0)
        vec[...] = jnp.where(rows16 == 8, inner_bias, every)
        turned = pltpu.roll(every, 2 * WIDE - me.g * LOCAL * HEAD, 1)
        lower = lax.broadcasted_iota(jnp.int32, (1, LANES), 1) < HEAD
        biases = []
        for h in range(LOCAL):
            v = turned[1:2, h // 2 * LANES : h // 2 * LANES + LANES]
            v = v if h % 2 else pltpu.roll(v, HEAD, 1)
            biases.append(jnp.where(lower, 0.0, v))
        biases.append(turned[0:1, :LANES])
        biases.append(jnp.where(lower, turned[0:1, LANES : 2 * LANES], 0.0))
        bias = jnp.concatenate(biases, axis=1)
        lower_rows = lax.broadcasted_iota(jnp.int32, (n, LANES), 1) < HEAD

        matrix = weights[:, :, :, :, :width].reshape(depth, width)
        kept, kv_first = [copies.keep(weights, wqkv_out), copies.keep(vec, vec_out)], []
        kv_sibling, kv_kept = [], []
        for dv in range(2):
            v = (me.half + dv) % 2
            for u in range(2):
                tokens_go.arrived(u * 2 + v, toks.at[u * 2 + v])
            if dv:
                block = w1.at[:, me.c, me.g, :]
                wm_first = [
                    copies.push(wms, wm.at[me.x, me.c, me.g, me.y], me.at(g=to)) for to in line
                ]
                w1_second = [copies.push(block, block, me.at(g=to)) for to in line]
            both = jnp.concatenate([toks[v], toks[2 + v]], axis=0)
            made = jnp.dot(both, matrix, preferred_element_type=wide)
            made = made + bias
            for u in range(2):
                mine = made[u * n : (u + 1) * n]
                kv_own[v, u] = mine[:, :WIDE].astype(low_type)
                front, back = mine[:, WIDE : WIDE + LANES], mine[:, WIDE + LANES :]
                for h, part in enumerate((front, pltpu.roll(front, HEAD, 1), back)):
                    q_own[u * 2 + v, :, h * LANES : (h + 1) * LANES] = jnp.where(
                        lower_rows, part, 0.0
                    ).astype(low_type)
            mine = kv_all.at[:, me.c, v, me.p, me.y]
            kv_first.append(
                [copies.push(kv_own.at[v], mine, me.at(x=x, y=y)) for x, y in square]
            )
            kv_sibling.append(copies.push(kv_own.at[v], mine, me.sibling()))
            kv_kept.append(copies.keep(kv_own.at[v], mine))
        block = w1.at[:, me.c, me.g, :]
        arrivals.append(copies.push(block, block, me.sibling()))
        kept += [copies.keep(toks, tok_out), copies.keep(q_own, q_out)]

        ends = ends_of(lengths_ref)
        rows = GROUPS * n
        spans = [slice(h * LANES, (h + 1) * LANES) for h in range(LOCAL)]
        along = lax.broadcasted_iota(jnp.int32, (1, n), 1)
        ranges = [document_of(along + tile_base(me, slot, n), ends) for slot in range(GROUPS)]
        first = jnp.concatenate([low for low, _ in ranges], axis=1)
        last = jnp.concatenate([high for _, high in ranges], axis=1)
        down = lax.broadcasted_iota(jnp.int32, (rows, rows), 0)
        for slot in range(GROUPS):
            for h, span in enumerate(spans):
                scaled[h, slot * n : (slot + 1) * n] = q_own[slot, :, span] * jnp.asarray(
                    0.125, low_type
                )
        sums[...] = jnp.zeros_like(sums)

        def attend(u, c, v, carry):
            begin = ((u * 2 + c) * 2 + v) * rows
            place = down + begin
            same = (place >= first) & (place < last)
            result = []
            for h, span in enumerate(spans):
                top, total = carry[h]
                kv = kv_all[u, c, v, :, :, :, span].reshape(rows, LANES)
                scores = lax.dot_general(kv, scaled[h], NEXT, preferred_element_type=wide)
                scores = jnp.where(same, scores, mask_fill)
                new_top = jnp.maximum(top, jnp.max(scores, axis=0, keepdims=True))
                factor = jnp.exp(top - new_top)
                powers = jnp.exp(scores - new_top)
                total = total * factor + jnp.sum(powers, axis=0, keepdims=True)
                sums[h] = sums[h] * factor + lax.dot_general(
                    kv, powers.astype(low_type), DOWN, preferred_element_type=wide
                )
                result.append((new_top, total))
            return tuple(result)

        state = tuple(
            (jnp.full((1, rows), lowest_start, wide), jnp.zeros((1, rows), wide))
            for _ in range(LOCAL)
        )
        for dv in range(2):
            v = (me.half + dv) % 2
            forwards = [kv_sibling[dv]]
            for copy, (x, y) in zip(kv_first[dv], square):
                copy.wait_recv()
                block = kv_all.at[:, me.c, v, (x + me.c) % 2, y]
                forwards.append(copies.push(block, block, me.sibling()))
            kv_kept[dv].wait()
            if dv:
                wm_own.wait()
                for copy in wm_first:
                    copy.wait_recv()
                block = wm.at[me.x, me.c, :, me.y]
                wm_second = [copies.push(block, block, me.at(x=x, y=y)) for x, y in square]
                arrivals.append(copies.push(block, block, me.sibling()))
            state = lax.fori_loop(
                0, 2, lambda u, carry, v=v: attend(u, me.c, v, carry), state
            )
            for copy in forwards:
                copy.wait_recv()
            state = lax.fori_loop(
                0, 2, lambda u, carry, v=v: attend(u, 1 - me.c, v, carry), state
            )
        kept.append(copies.keep(kv_all, kv_out))
        for copy, (x, y) in zip(wm_second, square):
            copy.wait_recv()
            block = wm.at[x, me.c, :, y]
            arrivals.append(copies.push(block, block, me.sibling()))
        for copy, (_, source) in zip(w1_second, me.line()):
            copy.wait_recv()
            block = w1.at[:, me.c, source, :]
            arrivals.append(copies.push(block, block, me.sibling()))
        lane = lax.broadcasted_iota(jnp.int32, (n, LANES), 1)
        upper = lane >= HEAD
        for slot in range(GROUPS):
            part = slice(slot * n, (slot + 1) * n)
            mixes = []
            for h in range(LOCAL):
                top, total = state[h]
                mixes.append(jnp.transpose(sums[h, :, part] / total[:, part]))
                lse_out[slot, h : h + 1, :] = top[:, part] + jnp.log(total[:, part])
            turned = [pltpu.roll(mixes[h], HEAD, 1) for h in (0, 2)]
            both = jnp.concatenate(
                [jnp.where(upper, mixes[1], turned[0]), jnp.where(upper, 0.0, turned[1])], axis=1
            )
            mixed_wide[part, :] = both
            mixed_out[slot] = both.astype(low_type)
        for copy in arrivals:
            copy.wait_recv()
        for copy in kept:
            copy.wait()
        tokens_go.finish()
        copies.finish()

    vmem = pltpu.VMEM
    dma = pltpu.SemaphoreType.DMA
    total = 64
    return pl.pallas_call(
        body,
        name="first_kernel",
        out_shape=(
            jax.ShapeDtypeStruct((GROUPS, n, depth), low_type),
            jax.ShapeDtypeStruct((GROUPS, n, WIDE), low_type),
            pltpu.HBM((4, GROUPS, 2, s, cols), low_type),
            jax.ShapeDtypeStruct((SMALL, 2 * WIDE), wide),
            pltpu.HBM((2, 2, 2, 2, 2, n, WIDE), low_type),
            jax.ShapeDtypeStruct((2, 2, GROUPS, 2, s, quarter), low_type),
            jax.ShapeDtypeStruct((2, 2, GROUPS, 2, s, depth), low_type),
            jax.ShapeDtypeStruct((GROUPS, n, PACK), low_type),
            jax.ShapeDtypeStruct((GROUPS * n, PACK), wide),
            jax.ShapeDtypeStruct((GROUPS, 8, n), wide),
        ),
        in_specs=[pl.BlockSpec(memory_space=pltpu.HBM)] * (8 + count),
        out_specs=(pl.BlockSpec(memory_space=pl.ANY),) * 7
        + (pl.BlockSpec(memory_space=vmem),) * 3,
        scratch_shapes=[
            dma((total,)), dma((total,)), dma((12,)), dma((4,)), dma((4,)),
            vmem((GROUPS, s, cols), low_type),
            vmem((GROUPS, n, depth), low_type),
            vmem((4, GROUPS, 2, s, cols), low_type),
            vmem((2, 2, n, WIDE), low_type),
            vmem((GROUPS, n, WIDE), low_type),
            vmem((4, s, quarter), low_type),
            vmem((s, depth), low_type),
            vmem((SMALL, 2 * WIDE), wide),
            vmem((s, LANES), wide),
            vmem((2, 2, 2, 2, 2, n, WIDE), low_type),
            vmem((LOCAL, GROUPS * n, LANES), low_type),
            vmem((LOCAL, LANES, GROUPS * n), wide),
            dma((6 + count,)),
            pltpu.SMEM(lengths.shape, jnp.int32),
            dma,
            *[vmem(item.shape, item.dtype) for item in (wq, wk, wv, tables, *vectors, inner, mix)],
        ],
        compiler_params=pltpu.CompilerParams(
            collective_id=10, has_side_effects=True, vmem_limit_bytes=NEAR_LIMIT
        ),
    )(*[pltpu.with_memory_space_constraint(item, pltpu.HBM) for item in (lengths, tokens, wq, wk, wv, tables, *vectors, inner, mix)])


def pass_back(ident, pieces):
    def body(source, target, send, recv):
        me = Spot()
        owners = me.owners()
        readers = [device for _, device in me.readers()]
        barrier, expected = announce(readers[1:], [(jnp.logical_not(me.selfish), readers[0])])
        pl.semaphore_wait(barrier, expected)
        move = Scatter(send, recv, me.selfish)
        move.start([(source.at[slot], device) for slot, device in owners], target.at[me.g], me.g)
        for g in range(GROUPS):
            move.arrived(g, target.at[g])
        move.finish()

    return scatter_call(body, "pass_back", ident, pieces)


def pass_on(ident, pieces):
    def body(source, target, send, recv):
        me = Spot()
        owners = [device for _, device in me.owners()]
        barrier, expected = announce(owners[1:], [(jnp.logical_not(me.selfish), owners[0])])
        pl.semaphore_wait(barrier, expected)
        move = Scatter(send, recv, me.selfish)
        slot = me.slot()
        move.start([(source.at[g], device) for g, device in me.readers()], target.at[slot], slot)
        for index in range(GROUPS):
            move.arrived(index, target.at[index])
        move.finish()

    return scatter_call(body, "pass_on", ident, pieces)


def scatter_call(body, name, ident, pieces):
    return pl.pallas_call(
        body,
        name=name,
        out_shape=jax.ShapeDtypeStruct(pieces.shape, pieces.dtype),
        in_specs=[pl.BlockSpec(memory_space=pl.ANY)],
        out_specs=pl.BlockSpec(memory_space=pl.ANY),
        scratch_shapes=[pltpu.SemaphoreType.DMA((4,)), pltpu.SemaphoreType.DMA((4,))],
        compiler_params=pltpu.CompilerParams(
            collective_id=ident, has_side_effects=True, vmem_limit_bytes=VMEM_LIMIT
        ),
    )(pieces)


def final_kernel(output, hidden, pieces, outqk, out1, out2, outm, s, e):
    n, depth = hidden.shape
    quarter = out1.shape[-1]

    def body(y_in, hid, dx, qk_in, i_in, o_in, m_in, yo, xg, qw, qb, kw, vw, vb, mw, mb, eg, es, iw, ib, ow, ob, fg, fs):
        device = lax.axis_index("au") * lax.axis_size("row") + lax.axis_index("row")
        yo[...] = y_in[...]
        xg[...] = total_of(hid[...], dx[0], dx[1], dx[2], dx[3]).astype(low_type)
        rows = qk_in.shape[1]
        q_in, k_in = qk_in.at[:, :, WIDE:], qk_in.at[:, :, :WIDE]
        lower = lax.broadcasted_iota(jnp.int32, (rows, LANES), 1) < HEAD

        def part(head):
            g, h = head // LOCAL, head % LOCAL
            return k_in[g, :, h * LANES : (h + 1) * LANES].astype(wide)

        made_q = []
        for g in range(0, GROUPS, 2):
            a0, b0 = q_in[g, :, :LANES].astype(wide), q_in[g, :, LANES:].astype(wide)
            a1 = pltpu.roll(q_in[g + 1, :, :LANES].astype(wide), HEAD, 1)
            b1 = pltpu.roll(q_in[g + 1, :, LANES:].astype(wide), HEAD, 1)
            made_q += [a0, jnp.where(lower, b0, a1), jnp.where(lower, a1, b1)]
        biases = [[], []]
        for pair in range(HEADS // 2):
            span = slice(pair * LANES, (pair + 1) * LANES)
            kv = [part(2 * pair), part(2 * pair + 1)]
            made_k = jnp.where(lower, kv[0], pltpu.roll(kv[1], HEAD, 1))
            made_v = jnp.where(lower, pltpu.roll(kv[0], HEAD, 1), kv[1])
            qw[:, span], kw[:, span], vw[:, span] = made_q[pair][:s], made_k[:s], made_v[:s]
            biases[0].append(made_q[pair][s:])
            biases[1].append(made_v[s:])

        def own(eight, width, shift):
            return pltpu.roll(eight, shift, 1)[0:1, :width]

        turn = (depth - device * s) % depth
        qb[...] = own(jnp.concatenate(biases[0], axis=1), s, turn)
        vb[...] = own(jnp.concatenate(biases[1], axis=1), s, turn)
        mw[...] = m_in[:s]
        extras = pltpu.roll(m_in[s : s + 8, :], turn, 1)
        for index, ref in enumerate((mb, eg, es, ob, fg, fs)):
            ref[...] = extras[index : index + 1, :s]
        for w in range(4):
            iw[:, w * quarter : (w + 1) * quarter] = i_in[w, :s].astype(wide)
        place = lax.axis_index("row") * e
        ib[...] = own(
            i_in[lax.axis_index("au"), s : s + 8, :].astype(wide), e, (quarter - place) % quarter
        )
        ow[...] = o_in[...]

    vmem = pltpu.VMEM

    def shape(*dims):
        return jax.ShapeDtypeStruct(dims, wide)

    return pl.pallas_call(
        body,
        name="final_kernel",
        out_shape=(
            jax.ShapeDtypeStruct((n, depth), low_type),
            jax.ShapeDtypeStruct((n, depth), low_type),
            shape(s, depth), shape(1, s), shape(s, depth), shape(s, depth), shape(1, s),
            shape(s, depth), shape(1, s), shape(1, s), shape(1, s),
            shape(s, 4 * quarter), shape(1, e), shape(e, depth),
            shape(1, s), shape(1, s), shape(1, s),
        ),
        in_specs=[pl.BlockSpec(memory_space=vmem)] * 7,
        out_specs=(pl.BlockSpec(memory_space=vmem),) * 17,
        compiler_params=pltpu.CompilerParams(vmem_limit_bytes=NEAR_LIMIT),
    )(output, hidden, pieces, outqk, out1, out2, outm)


def gelu_and_slope(value):
    t = 1.0 / (1.0 + (0.3275911 * 0.7071067811865476) * jnp.abs(value))
    bell = jnp.exp(-0.5 * value * value)
    tail = 1.061405429
    for weight in (-1.453152027, 1.421413741, -0.284496736, 0.254829592):
        tail = tail * t + weight
    tail = 0.5 * tail * t * bell
    below = jnp.where(value >= 0.0, 1.0 - tail, tail)
    return value * below, below + value * bell * 0.3989422804014327


def normed(hidden):
    mean = jnp.mean(hidden, axis=-1, keepdims=True)
    centered = hidden - mean
    spread = jnp.mean(centered * centered, axis=-1, keepdims=True)
    inverse = lax.rsqrt(spread + eps_norm)
    return centered * inverse, inverse


def normed_grad(grad, norm, inverse):
    mean = jnp.mean(grad, axis=-1, keepdims=True)
    along = jnp.mean(grad * norm, axis=-1, keepdims=True)
    return inverse * (grad - mean - norm * along)


def down_sum(values):
    return jnp.sum(values, axis=0, keepdims=True)


def middle_kernel(mixed, tokens, cotangent, mix, inner, outer, vec, s, e):
    n, depth = tokens.shape
    quarter = inner.shape[1]
    rows = s + 8
    cut = depth // 2
    hn = n // 2

    def body(
        mixed_ref, tok_in, cot_in, wm_in, w1_in, w2f_in, vec_in,
        out, hidden_out, do_out, sm, s1, s2,
        send, recv, local, back_send, back_recv, on_send, on_recv,
        swap_send2, swap_recv2, tok, cot, w2f, vec_ref, wm, w1, w2p, w2s, came, mixed_tok, xs, acts, slopes, parts, sums, bgs, igs, parts2, sums2,
        pieces, extra, attn, own1, own2, g1, g2, gm,
    ):
        me = Spot()
        copies = Copies(send, recv, local)
        square = me.square()
        line = [to for to, _ in me.line()]
        owners = me.owners()
        readers = me.readers()
        swapped = [me.at(g=to, c=me.y, y=me.c) for to in [me.g] + line]
        barrier, expected = announce(
            [me.at(x=x, y=y) for x, y in square]
            + swapped[1:]
            + [device for _, device in readers[1:]]
            + [device for _, device in owners[1:]]
            + [me.sibling()],
            [
                (jnp.logical_not(me.selfish), readers[0][1]),
                (jnp.logical_not(me.selfish), owners[0][1]),
                (me.crossing, swapped[0]),
            ],
        )
        loads = [copies.keep(wm_in, wm), copies.keep(w1_in, w1)]
        small_loads = [
            copies.keep(source, target)
            for source, target in ((tok_in, tok), (vec_in, vec_ref), (w2f_in, w2f), (cot_in, cot))
        ]
        pl.semaphore_wait(barrier, expected)

        back = Scatter(back_send, back_recv, me.selfish)
        back.start([(mixed_ref.at[slot], device) for slot, device in owners], came.at[me.g], me.g)
        lower = lax.broadcasted_iota(jnp.int32, (n, LANES), 1) < HEAD
        loads[0].wait()
        for copy in small_loads:
            copy.wait()
        w2s[...] = w2f[...].astype(low_type)
        for g in range(GROUPS):
            back.arrived(g, came.at[g])
        w2_place = w2p.at[me.g, me.y]
        w2_first = [copies.push(w2s, w2_place, device) for device in swapped[1:]]
        w2_swap = pltpu.make_async_remote_copy(
            src_ref=w2s,
            dst_ref=w2_place,
            send_sem=swap_send2,
            recv_sem=swap_recv2,
            device_id=swapped[0],
            device_id_type=MESH,
        )
        w2_stays = pltpu.make_async_copy(w2s, w2_place, swap_recv2)

        @pl.when(me.crossing)
        def _():
            w2_swap.start()

        @pl.when(jnp.logical_not(me.crossing))
        def _():
            w2_stays.start()

        for half in range(2):
            a0 = came[2 * half, :, :LANES]
            b0 = came[2 * half, :, LANES:].astype(wide)
            a1 = pltpu.roll(came[2 * half + 1, :, :LANES].astype(wide), HEAD, 1)
            b1 = pltpu.roll(came[2 * half + 1, :, LANES:].astype(wide), HEAD, 1)
            base = half * 3 * LANES
            mixed_tok[:, base : base + LANES] = a0
            mixed_tok[:, base + LANES : base + 2 * LANES] = jnp.where(lower, b0, a1).astype(low_type)
            mixed_tok[:, base + 2 * LANES : base + 3 * LANES] = jnp.where(lower, a1, b1).astype(
                low_type
            )

        def vector(index):
            return vec_ref[index : index + 1, :]

        mix = jnp.dot(mixed_tok[...], wm[...], preferred_element_type=wide) + vector(2)
        norm1, inverse1 = normed(tok[...].astype(wide) + mix)
        early = norm1 * vector(3) + vector(4)
        mine = me.x * 2 + me.y
        halves = [slice(0, hn), slice(hn, n)]

        def send_rows(ref, h):
            place = ref.at[h, mine]
            return [copies.push(place, place, me.at(x=x, y=y)) for x, y in square]

        def send_back(ref, landing, h):
            return [
                copies.push(ref.at[h, x * 2 + y], landing.at[h, mine], me.at(x=x, y=y))
                for x, y in square
            ]

        def arrive(started):
            for copy in started:
                copy.wait_recv()

        def received(landing, h):
            return [landing[h, x * 2 + y] for x, y in square]

        early_go = []
        for h, half in enumerate(halves):
            xs[h, mine] = early[half].astype(low_type)
            early_go.append(send_rows(xs, h))
            if h == 0:
                for copy in early_go[0]:
                    copy.wait_send()
                copies.started = [
                    item for item in copies.started if all(item is not copy for copy in early_go[0])
                ]
        loads[1].wait()

        def outer_weight():
            return w2p[...].reshape(quarter, depth)

        branch_go = []
        for h in range(2):
            arrive(early_go[h])
            inner = jnp.dot(
                xs[h].reshape(4 * hn, depth), w1[...], preferred_element_type=wide
            ) + vector(8)
            act, slope = gelu_and_slope(inner)
            act = act.astype(low_type)
            acts[h] = act.reshape(4, hn, quarter)
            slopes[h] = slope
            if h == 0:

                @pl.when(me.crossing)
                def _():
                    w2_swap.wait_recv()
                    w2_swap.wait_send()

                @pl.when(jnp.logical_not(me.crossing))
                def _():
                    w2_stays.wait()

                block = w2p.at[me.g, me.c]
                w2_last = [copies.push(block, block, me.sibling())]
                for copy, (_, source) in zip(w2_first, me.line()):
                    copy.wait_recv()
                    block = w2p.at[source, me.c]
                    w2_last.append(copies.push(block, block, me.sibling()))
                arrive(w2_last)
            made = jnp.dot(act, outer_weight(), preferred_element_type=wide).reshape(4, hn, depth)
            own1[h] = made
            parts[h] = made.astype(low_type)
            branch_go.append(send_back(parts, sums, h))

        grad_go, final_grads, norm_sums, cot_sums = [], [], [], []
        for h, half in enumerate(halves):
            arrive(branch_go[h])
            branch = total_of(own1[h, mine], *received(sums, h)) + vector(5)
            norm2, inverse2 = normed(early[half] + branch)
            out[half, :] = (norm2 * vector(6) + vector(7)).astype(low_type)
            cot_wide = cot[half, :].astype(wide)
            final_grad = normed_grad(cot_wide * vector(6), norm2, inverse2)
            bgs[h, mine] = final_grad.astype(low_type)
            grad_go.append(send_rows(bgs, h))
            final_grads.append(final_grad)
            norm_sums.append(down_sum(cot_wide * norm2))
            cot_sums.append(down_sum(cot_wide))
        extra[...] = jnp.zeros_like(extra)
        extra[3:4, :] = down_sum(bgs[0, mine].astype(wide)) + down_sum(bgs[1, mine].astype(wide))
        extra[4:5, :] = norm_sums[0] + norm_sums[1]
        extra[5:6, :] = cot_sums[0] + cot_sums[1]

        token_go = []
        for h in range(2):
            arrive(grad_go[h])
            grad = lax.dot_general(
                bgs[h].reshape(4 * hn, depth), outer_weight(), NEXT, preferred_element_type=wide
            )
            grad = (grad * slopes[h]).astype(low_type)
            igs[h] = grad.reshape(4, hn, quarter)
            made = lax.dot_general(grad, w1[...], NEXT, preferred_element_type=wide)
            made = made.reshape(4, hn, depth)
            own2[h] = made
            parts2[h] = made.astype(low_type)
            token_go.append(send_back(parts2, sums2, h))

        other = 1 - me.c
        grads = bgs[...].reshape(4 * n, depth)
        for half in range(2):
            span = slice(half * cut, (half + 1) * cut)
            made = lax.dot_general(
                acts[:, :, :, span].reshape(4 * n, cut), grads, DOWN, preferred_element_type=wide
            )
            g2[2 * half : 2 * half + 2] = made.astype(low_type).reshape(2, 2, e, depth)
        w2_half = copies.push(g2.at[:, other], s2, me.sibling())

        grads = igs[...].reshape(4 * n, quarter)
        bias = jnp.broadcast_to(down_sum(grads.astype(wide)), (8, quarter)).astype(low_type)
        for half in range(2):
            span = slice(half * cut, (half + 1) * cut)
            made = lax.dot_general(
                xs[:, :, :, span].reshape(4 * n, cut), grads, DOWN, preferred_element_type=wide
            ).astype(low_type)
            for index in range(16):
                place = (half, index // 8, index // 2 % GROUPS, index % 2)
                g1[(*place, slice(None, s))] = made[index * s : (index + 1) * s]
                g1[(*place, slice(s, None))] = bias
        w1_half = copies.push(g1.at[:, other], s1, me.sibling())
        w2_half.wait_recv()

        def add2(g):
            s2[g] = s2[g] + g2[g, me.c]

        loop(GROUPS, add2)
        w1_half.wait_recv()

        def add1(index):
            x, g, y = index // 8, index // 2 % GROUPS, index % 2
            s1[x, g, y] = s1[x, g, y] + g1[x, me.c, g, y]

        loop(16, add1)
        norm_sums, grad_sums, attn_sums = [], [], []
        for h, half in enumerate(halves):
            arrive(token_go[h])
            early_grad = total_of(final_grads[h], own2[h, mine], *received(sums2, h))
            norm_sums.append(down_sum(early_grad * norm1[half]))
            grad_sums.append(down_sum(early_grad))
            hidden = normed_grad(early_grad * vector(3), norm1[half], inverse1[half])
            hidden_out[half, :] = hidden
            attn[half, :] = hidden.astype(low_type)
            attn_sums.append(down_sum(hidden.astype(low_type).astype(wide)))
        extra[0:1, :] = attn_sums[0] + attn_sums[1]
        extra[1:2, :] = norm_sums[0] + norm_sums[1]
        extra[2:3, :] = grad_sums[0] + grad_sums[1]
        attn_grad = attn[...]
        back_grad = lax.dot_general(attn_grad, wm[...], NEXT, preferred_element_type=wide)
        for half in range(2):
            base = half * 3 * LANES
            t0 = back_grad[:, base : base + LANES]
            t1 = back_grad[:, base + LANES : base + 2 * LANES]
            t2 = back_grad[:, base + 2 * LANES : base + 3 * LANES]
            r1, r2 = pltpu.roll(t1, HEAD, 1), pltpu.roll(t2, HEAD, 1)
            pieces[2 * half, :, :LANES] = t0.astype(low_type)
            pieces[2 * half, :, LANES:] = jnp.where(lower, t1, 0.0).astype(low_type)
            pieces[2 * half + 1, :, :LANES] = jnp.where(lower, r1, r2).astype(low_type)
            pieces[2 * half + 1, :, LANES:] = jnp.where(lower, r2, 0.0).astype(low_type)
        onward = Scatter(on_send, on_recv, me.selfish)
        slot = me.slot()
        onward.start([(pieces.at[g], device) for g, device in readers], do_out.at[slot], slot)

        for half in range(2):
            span = slice(half * cut, (half + 1) * cut)
            made = lax.dot_general(
                mixed_tok[:, span], attn_grad, DOWN, preferred_element_type=wide
            ).astype(low_type)
            for index in range(16):
                place = (half, index // 8, index // 2 % GROUPS, index % 2)
                gm[(*place, slice(None, s))] = made[index * s : (index + 1) * s]
                gm[(*place, slice(s, None))] = extra[...].astype(low_type)
        wm_half = copies.push(gm.at[:, other], sm, me.sibling())
        wm_half.wait_recv()

        def addm(index):
            x, g, y = index // 8, index // 2 % GROUPS, index % 2
            sm[x, g, y] = sm[x, g, y] + gm[x, me.c, g, y]

        loop(16, addm)
        for index in range(GROUPS):
            onward.arrived(index, do_out.at[index])
        back.finish()
        onward.finish()
        copies.finish()

    vmem = pltpu.VMEM
    dma = pltpu.SemaphoreType.DMA
    tall = vmem((2, 4, hn, depth), low_type)
    full = vmem((2, 4, hn, depth), wide)
    high = vmem((2, 4, hn, quarter), low_type)
    tokens, cotangent, outer = [
        pltpu.with_memory_space_constraint(item, pltpu.HBM) for item in (tokens, cotangent, outer)
    ]
    return pl.pallas_call(
        body,
        name="middle_kernel",
        out_shape=(
            jax.ShapeDtypeStruct((n, depth), low_type),
            jax.ShapeDtypeStruct((n, depth), wide),
            jax.ShapeDtypeStruct((GROUPS, n, PACK), low_type),
            jax.ShapeDtypeStruct((2, GROUPS, 2, rows, depth), low_type),
            jax.ShapeDtypeStruct((2, GROUPS, 2, rows, quarter), low_type),
            jax.ShapeDtypeStruct((GROUPS, e, depth), low_type),
        ),
        in_specs=[
            pl.BlockSpec(memory_space=item)
            for item in (pl.ANY, pltpu.HBM, pltpu.HBM, pl.ANY, pl.ANY, pltpu.HBM, pl.ANY)
        ],
        out_specs=[
            pl.BlockSpec(memory_space=item) for item in (vmem, vmem, pl.ANY, vmem, vmem, vmem)
        ],
        scratch_shapes=[
            dma((48,)), dma((48,)), dma((8,)), dma((4,)), dma((4,)), dma((4,)), dma((4,)), dma, dma,
            vmem((n, depth), low_type),
            vmem((n, depth), low_type),
            vmem((e, depth), wide),
            vmem(vec.shape, wide),
            vmem((depth, depth), low_type),
            vmem((depth, quarter), low_type),
            vmem((GROUPS, 2, e, depth), low_type),
            vmem((e, depth), low_type),
            vmem((GROUPS, n, PACK), low_type),
            vmem((n, depth), low_type),
            tall, high,
            vmem((2, 4 * hn, quarter), wide),
            tall, tall, tall, high, tall, tall,
            vmem((GROUPS, n, PACK), low_type),
            vmem((8, depth), wide),
            vmem((n, depth), low_type),
            full, full,
            vmem((2, 2, GROUPS, 2, rows, quarter), low_type),
            vmem((GROUPS, 2, e, depth), low_type),
            vmem((2, 2, GROUPS, 2, rows, depth), low_type),
        ],
        compiler_params=pltpu.CompilerParams(
            collective_id=12, has_side_effects=True, vmem_limit_bytes=NEAR_LIMIT
        ),
    )(mixed, tokens, cotangent, mix, inner, outer, vec)


def tile_base(me, slot, n):
    u, v = slot // 2, slot % 2
    return ((u * 2 + me.c) * 2 * GROUPS + (v * 2 + me.p) * 2 + me.y) * n


def ends_of(lengths_ref):
    ends = [lengths_ref[0]]
    for index in range(1, lengths_ref.shape[0]):
        ends.append(ends[-1] + lengths_ref[index])
    return ends


def document_of(place, ends):
    first, last = place * 0, place * 0 + ends[-1]
    for end in ends[:-1]:
        before = end <= place
        first = jnp.where(before, end, first)
    for end in reversed(ends[:-1]):
        last = jnp.where(end <= place, last, end)
    return first, last


def turn_kernel(lengths, queries, keys, grads_in, mixed, lse, tokens, weights, sum1, sum2, summ):
    n = tokens.shape[1]
    depth = tokens.shape[-1]
    s = depth // 32
    rows = s + 8
    cut = depth // 2
    tall = sum2.shape[1]
    block = GROUPS * n
    width = WIDE + PACK
    spans = [slice(h * LANES, (h + 1) * LANES) for h in range(LOCAL)]

    def body(
        lengths_ref, q_ref, kv_ref, do_ref, mixed_ref, lse_ref, tok, w_ref, s1, s2, sm,
        dx_out, outqk, out1, out2, outm,
        send, recv, local, dx_send, dx_recv, swap_send, swap_recv, ks, kr, ps, pr,
        both, kbuf, kin, pk, dqs, narrow, dxs, gk, sk, pp, fk, p1, f1, pm, fm, tm, p2, early,
    ):
        me = Spot()
        copies = Copies(send, recv, local)
        square = me.square()
        line = [to for to, _ in me.line()]
        readers = [device for _, device in me.readers()]
        swapped = [me.at(g=to, c=me.y, y=me.c) for to in [me.g] + line]
        barrier, expected = announce(
            [me.at(x=x, y=y) for x, y in square]
            + [me.at(g=to) for to in line]
            + readers[1:]
            + swapped[1:]
            + [me.sibling()],
            [(jnp.logical_not(me.selfish), readers[0]), (me.crossing, swapped[0])],
        )
        ends = ends_of(lengths_ref)
        lane = lax.broadcasted_iota(jnp.int32, (n, LANES), 1)
        upper = lane >= HEAD
        along = lax.broadcasted_iota(jnp.int32, (1, n), 1)
        down = lax.broadcasted_iota(jnp.int32, (block, n), 0)

        def upper_halves(ref, part):
            front = ref[part, :LANES].astype(wide)
            back = ref[part, LANES:].astype(wide)
            parts = (pltpu.roll(front, HEAD, 1), front, pltpu.roll(back, HEAD, 1))
            return [jnp.where(upper, item, 0.0) for item in parts]

        firsts, lasts, logs, deltas = [], [], [], []
        for slot in range(GROUPS):
            part = slice(slot * n, (slot + 1) * n)
            first, last = document_of(along + tile_base(me, slot, n), ends)
            firsts.append(first)
            lasts.append(last)
            outs, inputs = upper_halves(mixed_ref, part), upper_halves(do_ref, part)
            for h, span in enumerate(spans):
                base = slot * 2 * n
                both[h, base : base + n] = q_ref[part, span] * jnp.asarray(0.125, low_type)
                both[h, base + n : base + 2 * n] = inputs[h].astype(low_type)
            deltas.append([down_sum(jnp.transpose(i * o)) for i, o in zip(inputs, outs)])
            logs.append([lse_ref[slot, h : h + 1, :] for h in range(LOCAL)])
        dqs[...] = jnp.zeros_like(dqs)
        pl.semaphore_wait(barrier, expected)

        wm_push = [
            copies.push(sm.at[x, :, y], pm.at[peer], me.at(x=x, y=y))
            for peer, (x, y) in enumerate(square)
        ]
        w1_push = [
            copies.push(s1.at[:, to, :], p1.at[slot], me.at(g=to)) for slot, to in enumerate(line)
        ]
        w2_push = [
            copies.push(s2.at[to], p2.at[index + 1], swapped[index + 1])
            for index, to in enumerate(line)
        ]
        exchanged = pltpu.make_async_remote_copy(
            src_ref=s2.at[me.g],
            dst_ref=p2.at[0],
            send_sem=swap_send,
            recv_sem=swap_recv,
            device_id=swapped[0],
            device_id_type=MESH,
        )
        stays = pltpu.make_async_copy(s2.at[me.g], p2.at[0], swap_recv)

        @pl.when(me.crossing)
        def _():
            exchanged.start()

        @pl.when(jnp.logical_not(me.crossing))
        def _():
            stays.start()

        other = 1 - me.c

        def attend(u, c, v, target):
            begin = pl.multiple_of(((u * 2 + c) * 2 + v) * block, block)
            place = down + begin
            same = [(place >= first) & (place < last) for first, last in zip(firsts, lasts)]
            for h, span in enumerate(spans):
                kv = kv_ref[pl.ds(begin, block), span]
                made = lax.dot_general(kv, both[h], NEXT, preferred_element_type=wide)
                pairs = []
                for slot in range(GROUPS):
                    base = slot * 2 * n
                    scores = jnp.where(same[slot], made[:, base : base + n], mask_fill)
                    probs = jnp.exp(scores - logs[slot][h])
                    dots = made[:, base + n : base + 2 * n]
                    score_grad = (probs * (dots - deltas[slot][h])).astype(low_type)
                    pairs += [score_grad, probs.astype(low_type)]
                    dqs[slot, :, span] += lax.dot_general(
                        score_grad, kv, DOWN, preferred_element_type=wide
                    )
                made = jnp.dot(
                    jnp.concatenate(pairs, axis=1), both[h], preferred_element_type=wide
                )
                target[:, :, :, span] = made.astype(low_type).reshape(2, 2, n, LANES)

        def to_sibling(turn):
            return pltpu.make_async_remote_copy(
                src_ref=kbuf.at[0, turn],
                dst_ref=kin.at[turn],
                send_sem=ks.at[turn],
                recv_sem=kr.at[turn],
                device_id=me.sibling(),
                device_id_type=MESH,
            )

        def to_peer(turn, peer):
            x, y = square[peer]
            return pltpu.make_async_remote_copy(
                src_ref=kbuf.at[1, turn, (x + me.c) % 2, y],
                dst_ref=pk.at[turn, peer],
                send_sem=ps.at[turn * 3 + peer],
                recv_sem=pr.at[turn * 3 + peer],
                device_id=me.at(x=x, y=y),
                device_id_type=MESH,
            )

        def key_turn(turn):
            u, v = turn % 2, (me.half + turn // 2) % 2

            def of_core(index):
                attend(u, jnp.where(index == 0, other, me.c), v, kbuf.at[index, turn])

                @pl.when(index == 0)
                def _():
                    to_sibling(turn).start()

            loop(2, of_core)
            to_sibling(turn).wait_recv()
            for p in range(2):
                for y in range(2):
                    kbuf[1, turn, p, y] = kbuf[1, turn, p, y] + kin[turn, p, y]
            for peer in range(3):
                to_peer(turn, peer).start()

        loop(4, key_turn)

        def square_push(total, landing):
            return [
                copies.push(total.at[x, :, y], landing.at[slot], me.at(x=x, y=y))
                for slot, (x, y) in enumerate(square)
            ]

        def square_sum(result, total, landed):
            def add(g):
                result[g] = total_of(
                    total[me.x, g, me.y], landed[0, g], landed[1, g], landed[2, g]
                ).astype(low_type)

            loop(GROUPS, add)

        def weight_grad(slots, half):
            span = slice(half * cut, (half + 1) * cut)
            return lax.dot_general(
                jnp.concatenate([tok[slot, :, span] for slot in slots], axis=0),
                jnp.concatenate([narrow[slot] for slot in slots], axis=0),
                DOWN,
                preferred_element_type=wide,
            )

        moves = []
        slots = [turn % 2 * 2 + (me.half + turn // 2) % 2 for turn in range(4)]
        for turn in range(4):
            if turn == 3:
                for half in range(2):
                    early[half] = weight_grad(slots[:3], half)
            u, dv = turn % 2, turn // 2
            v = (me.half + dv) % 2
            slot = u * 2 + v
            wides = [dqs[slot, :, span] * 0.125 for span in spans]
            narrow[slot, :, WIDE : WIDE + LANES] = jnp.where(
                upper, pltpu.roll(wides[1], HEAD, 1), wides[0]
            ).astype(low_type)
            narrow[slot, :, WIDE + LANES :] = jnp.where(upper, 0.0, wides[2]).astype(low_type)
            for peer in range(3):
                to_peer(turn, peer).wait_recv()
            here = total_of(
                kbuf[1, turn, me.p, me.y], *[pk[turn, peer] for peer in range(3)]
            ).astype(low_type)
            narrow[slot, :, :WIDE] = here
            dxs[slot] = lax.dot_general(
                narrow[slot], w_ref[:, :width], NEXT, preferred_element_type=wide
            ).astype(low_type)
            copy = pltpu.make_async_remote_copy(
                src_ref=dxs.at[slot],
                dst_ref=dx_out.at[me.g],
                send_sem=dx_send.at[turn],
                recv_sem=dx_recv.at[me.g],
                device_id=me.at(x=u, g=2 * v + me.p),
                device_id_type=MESH,
            )
            if dv:
                copy.start()
                moves.append((copy, None))
                continue
            stay = pltpu.make_async_copy(dxs.at[slot], dx_out.at[me.g], dx_recv.at[me.g])
            at_home = me.selfish & (me.x == u)
            away = jnp.logical_not(at_home)
            moves.append((copy, away))

            @pl.when(at_home)
            def _(stay=stay):
                stay.start()

            @pl.when(away)
            def _(copy=copy):
                copy.start()

        bias = down_sum(total_of(*[down_sum(narrow[slot].astype(wide)) for slot in range(GROUPS)]))
        bias = jnp.broadcast_to(bias, (8, width)).astype(low_type)
        for half in range(2):
            made = (early[half] + weight_grad(slots[3:], half)).astype(low_type)
            for index in range(16):
                place = (half, index // 8, index // 2 % GROUPS, index % 2)
                gk[(*place, slice(None, s))] = made[index * s : (index + 1) * s]
                gk[(*place, slice(s, None))] = bias
        g_half = copies.push(gk.at[:, other], sk, me.sibling())

        for copy in wm_push:
            copy.wait_recv()
        square_sum(fm, sm, pm)
        wm_last = [
            copies.push(fm.at[to], tm.at[peer], me.at(g=to)) for peer, to in enumerate(line)
        ]
        for copy in w1_push:
            copy.wait_recv()

        def addw(index):
            x, y = index // 2, index % 2
            f1[x, y] = total_of(s1[x, me.g, y], *[p1[peer, x, y] for peer in range(3)]).astype(
                low_type
            )

        loop(4, addw)
        quarter = out1.at[me.x * 2 + me.y]
        g_half.wait_recv()

        def pair_sum(index):
            x, g, y = index // 8, index // 2 % GROUPS, index % 2
            sk[x, g, y] = sk[x, g, y] + gk[x, me.c, g, y]

        loop(16, pair_sum)
        push = square_push(sk, pp)
        arrivals = [copies.push(f1.at[x, y], quarter, me.at(x=x, y=y)) for x, y in square]
        kept = [copies.keep(f1.at[me.x, me.y], quarter)]

        @pl.when(me.crossing)
        def _():
            exchanged.wait_recv()
            exchanged.wait_send()

        @pl.when(jnp.logical_not(me.crossing))
        def _():
            stays.wait()

        for copy in w2_push:
            copy.wait_recv()
        out2[...] = total_of(*[p2[index] for index in range(4)])
        for copy in push:
            copy.wait_recv()
        square_sum(fk, sk, pp)
        arrivals += [copies.push(fk.at[to], outqk.at[me.g], me.at(g=to)) for to in line]
        kept.append(copies.keep(fk.at[me.g], outqk.at[me.g]))
        for copy in wm_last:
            copy.wait_recv()
        outm[...] = total_of(fm[me.g], *[tm[peer] for peer in range(3)])
        for copy in arrivals:
            copy.wait_recv()
        for g in range(GROUPS):
            pltpu.make_async_copy(dx_out.at[g], dx_out.at[g], dx_recv.at[g]).wait()
        for copy in kept:
            copy.wait()
        for copy, away in moves:
            if away is None:
                copy.wait_send()
                continue

            @pl.when(away)
            def _(copy=copy):
                copy.wait_send()

        for turn in range(4):
            to_sibling(turn).wait_send()
            for peer in range(3):
                to_peer(turn, peer).wait_send()
        copies.finish()

    vmem = pltpu.VMEM
    dma = pltpu.SemaphoreType.DMA
    total = 40
    return pl.pallas_call(
        body,
        name="turn_kernel",
        out_shape=(
            jax.ShapeDtypeStruct((GROUPS, n, depth), low_type),
            jax.ShapeDtypeStruct((GROUPS, rows, width), low_type),
            jax.ShapeDtypeStruct((4, rows, depth), low_type),
            jax.ShapeDtypeStruct((tall, depth), wide),
            jax.ShapeDtypeStruct((rows, depth), wide),
        ),
        in_specs=[pl.BlockSpec(memory_space=pltpu.SMEM)] + [pl.BlockSpec(memory_space=vmem)] * 10,
        out_specs=[pl.BlockSpec(memory_space=pl.ANY)] * 3 + [pl.BlockSpec(memory_space=vmem)] * 2,
        scratch_shapes=[
            dma((total,)), dma((total,)), dma((4,)), dma((4,)), dma((4,)), dma, dma,
            dma((4,)), dma((4,)), dma((12,)), dma((12,)),
            vmem((LOCAL, 2 * block, LANES), low_type),
            vmem((2, 4, 2, 2, n, WIDE), low_type),
            vmem((4, 2, 2, n, WIDE), low_type),
            vmem((4, 3, n, WIDE), low_type),
            vmem((GROUPS, n, WIDE), wide),
            vmem((GROUPS, n, width), low_type),
            vmem((GROUPS, n, depth), low_type),
            vmem((2, 2, GROUPS, 2, rows, width), low_type),
            vmem((2, GROUPS, 2, rows, width), low_type),
            vmem((3, GROUPS, rows, width), low_type),
            vmem((GROUPS, rows, width), low_type),
            vmem((3, 2, 2, rows, depth), low_type),
            vmem((2, 2, rows, depth), low_type),
            vmem((3, GROUPS, rows, depth), low_type),
            vmem((GROUPS, rows, depth), low_type),
            vmem((3, rows, depth), low_type),
            vmem((4, tall, depth), low_type),
            vmem((2, cut, width), wide),
        ],
        compiler_params=pltpu.CompilerParams(
            collective_id=11, has_side_effects=True, vmem_limit_bytes=TURN_LIMIT
        ),
    )(lengths, queries, keys, grads_in, mixed, lse, tokens, weights, sum1, sum2, summ)


def on_device_general(
    tokens,
    cotangent,
    doc_lengths,
    query_weight,
    query_bias,
    key_weight,
    value_weight,
    value_bias,
    mix_weight,
    mix_bias,
    early_gain,
    early_shift,
    inner_weight,
    inner_bias,
    outer_weight,
    outer_bias,
    final_gain,
    final_shift,
):
    n, depth = tokens.shape
    groups, cycle = lax.axis_size("au"), lax.axis_size("row")
    devices = groups * cycle
    zs = cycle // (2 * GROUPS)
    s = query_weight.shape[0]
    ff = inner_weight.shape[1]
    quarter = ff // 4
    e = outer_weight.shape[0]
    rows = GROUPS * n
    total_tokens = n * devices
    me = Place(zs)
    device = lax.axis_index("au") * cycle + lax.axis_index("row")
    w_me = me.x * 2 + me.y

    def by_head(weight):
        return weight.astype(low_type).reshape(-1, GROUPS, LOCAL, HEAD)

    def packed(query, key, value):
        kv = jnp.stack([key, value], axis=3).reshape(-1, GROUPS, WIDE)
        q = jnp.pad(query, ((0, 0), (0, 0), (0, 0), (0, HEAD))).reshape(-1, GROUPS, WIDE)
        return jnp.concatenate([kv, q], axis=2)

    slab = packed(by_head(query_weight), by_head(key_weight), by_head(value_weight))
    slab = jnp.transpose(slab, (1, 0, 2))
    small = jnp.concatenate(
        [
            vector.astype(low_type)
            for vector in (
                query_bias, value_bias, mix_bias, early_gain, early_shift,
                outer_bias, final_gain, final_shift, inner_bias,
            )
        ]
    )
    extra = -s % 8 or 8
    small = jnp.broadcast_to(
        jnp.pad(small, (0, 2 * WIDE - small.shape[0]))[None, None], (GROUPS, extra, 2 * WIDE)
    )
    slab = jnp.concatenate([slab, small], axis=1)
    tok_all, w_all = spread_tokens(zs, tokens, slab)
    tok_all = tok_all.reshape(rows, depth)
    w_qkv = w_all[..., :s, :].reshape(depth, 2 * WIDE)
    small = w_all[..., s, :].reshape(devices, 2 * WIDE)
    names = [small[:, i * s : (i + 1) * s].reshape(depth) for i in range(8)]
    q_bias, v_bias, m_bias, e_gain, e_shift, o_bias, f_gain, f_shift = names
    i_bias = small[:, 8 * s : 8 * s + e].reshape(4, quarter)[w_me].astype(wide)
    q_bias = q_bias.reshape(1, GROUPS, LOCAL, HEAD)
    v_bias = v_bias.reshape(1, GROUPS, LOCAL, HEAD)
    bias = packed(q_bias, jnp.zeros_like(q_bias), v_bias)[0, me.g].astype(wide)

    qkv = (jnp.dot(tok_all, w_qkv, preferred_element_type=wide) + bias).astype(low_type)
    queries = qkv[:, WIDE:]

    inner_slab = jnp.transpose(inner_weight.astype(low_type).reshape(s, 4, quarter), (1, 0, 2))
    kv_all, w1, w2, wm = spread_keys(
        zs,
        qkv[:, :WIDE].reshape(GROUPS, n, WIDE),
        inner_slab,
        outer_weight.astype(low_type),
        mix_weight.astype(low_type),
    )
    kv_all = kv_all.reshape(total_tokens, WIDE)
    w1 = w1.reshape(depth, quarter)
    w2 = w2.reshape(quarter, depth)
    wm = wm.reshape(depth, depth)

    tile, block = 128, 512
    count = doc_lengths.shape[0]
    upto = jnp.arange(count)[None, :] <= jnp.arange(count)[:, None]
    ends = jnp.sum(jnp.where(upto, doc_lengths[None, :], 0), axis=1)
    owners = ((me.x * 2 + me.c) * cycle + me.z * GROUPS * 2 + jnp.arange(GROUPS) * 2 + me.y) * n
    places = (owners[:, None] + jnp.arange(n)[None, :]).reshape(rows)
    before = ends[None, :] <= places[:, None]
    first = jnp.max(jnp.where(before, ends[None, :], 0), axis=1).astype(jnp.int32)
    last = jnp.min(jnp.where(before, total_tokens, ends[None, :]), axis=1).astype(jnp.int32)
    tiles = rows // tile
    bounds = jnp.stack(
        [
            first.reshape(tiles, tile)[:, 0] // block,
            (last.reshape(tiles, tile)[:, -1] + block - 1) // block,
        ],
        axis=1,
    )
    mixed, mixed_wide, lse = attend_forward(
        queries, kv_all, bounds, first[:, None], last[:, None], tile, block
    )
    mixed_tok = exchange_line(zs, 2, mixed.reshape(GROUPS, n, PACK))
    mixed_tok = jnp.transpose(mixed_tok[:, :, : LOCAL * HEAD], (1, 0, 2)).reshape(n, depth)

    attn = jnp.dot(mixed_tok, wm, preferred_element_type=wide) + m_bias.astype(wide)
    early, early_pull = jax.vjp(
        layer_norm, tokens.astype(wide) + attn, e_gain.astype(wide), e_shift.astype(wide)
    )
    early_all = gather_square(zs, 3, early.astype(low_type)).reshape(rows, depth)
    inner = jnp.dot(early_all, w1, preferred_element_type=wide) + i_bias
    act, gelu_pull = jax.vjp(gelu_exact, inner)
    act_low = act.astype(low_type)
    partial = jnp.dot(act_low, w2, preferred_element_type=wide).astype(low_type)
    partial = exchange_square(zs, 4, partial.reshape(2, 2, n, depth))
    branch = jnp.sum(partial.astype(wide), axis=(0, 1)) + o_bias.astype(wide)
    result, final_pull = jax.vjp(
        layer_norm, early + branch, f_gain.astype(wide), f_shift.astype(wide)
    )
    output = result.astype(low_type)
    final_grads = final_pull(cotangent.astype(wide))
    branch_grad = final_grads[0].astype(low_type)
    outer_bias_grad = jnp.sum(branch_grad.astype(wide), axis=0)
    branch_all = gather_square(zs, 5, branch_grad).reshape(rows, depth)
    act_grad = jnp.einsum("td,fd->tf", branch_all, w2, preferred_element_type=wide)
    inner_grad = gelu_pull(act_grad)[0].astype(low_type)
    partial = jnp.einsum("tf,df->td", inner_grad, w1, preferred_element_type=wide).astype(low_type)
    partial = exchange_square(zs, 6, partial.reshape(2, 2, n, depth))
    grad2 = jnp.einsum("tf,td->fd", act_low, branch_all, preferred_element_type=wide)
    grad1 = jnp.einsum("td,tf->df", early_all, inner_grad, preferred_element_type=wide)
    inner_bias_grad = jnp.sum(inner_grad.astype(wide), axis=0)
    early_grad = final_grads[0] + jnp.sum(partial.astype(wide), axis=(0, 1))
    early_grads = early_pull(early_grad)
    attn_grad = early_grads[0].astype(low_type)
    mixed_grad = jnp.einsum("td,cd->tc", attn_grad, wm, preferred_element_type=wide)
    mixed_grad = jnp.transpose(
        mixed_grad.astype(low_type).reshape(n, GROUPS, LOCAL * HEAD), (1, 0, 2)
    )
    mixed_grad = jnp.pad(mixed_grad, ((0, 0), (0, 0), (0, PACK - LOCAL * HEAD)))
    grad_all = exchange_line(zs, 7, mixed_grad).reshape(rows, PACK)
    gradm = jnp.einsum("tc,td->cd", mixed_tok, attn_grad, preferred_element_type=wide)
    mix_bias_grad = jnp.sum(attn_grad.astype(wide), axis=0)

    delta = jnp.sum(
        (grad_all.astype(wide) * mixed_wide)[:, : LOCAL * HEAD].reshape(rows, LOCAL, HEAD), axis=2
    )

    def as_stat(values):
        return jnp.transpose(values.reshape(tiles, tile, LOCAL), (0, 2, 1))

    def same_stat(values):
        return jnp.broadcast_to(
            values.astype(wide).reshape(tiles, 1, tile), (tiles, LOCAL, tile)
        )

    stats = jnp.stack(
        [same_stat(first), same_stat(last), as_stat(lse[:, :LOCAL]), as_stat(delta)], axis=2
    )
    stats = jnp.pad(stats, ((0, 0), (0, 0), (0, 4), (0, 0)))
    query_grad, dkv = attend_backward(queries, kv_all, grad_all, stats, bounds, tile, block)

    def slabs(grad, extras):
        grad = grad.astype(low_type).reshape(devices, s, -1)
        rest = -s % 8
        rest += 0 if rest >= extras.shape[0] else 8
        extras = jnp.concatenate(
            [extras.astype(low_type), jnp.zeros((rest - extras.shape[0], extras.shape[1]), low_type)]
        )
        extras = jnp.broadcast_to(extras[None], (devices,) + extras.shape)
        return jnp.concatenate([grad, extras], axis=1).reshape(2, 2, zs, GROUPS, 2, s + rest, -1)

    mix_extras = jnp.stack(
        [
            mix_bias_grad, early_grads[1], early_grads[2],
            outer_bias_grad, final_grads[1], final_grads[2],
        ]
    )
    dkv, out1, out2, outm = reduce_keys(
        zs,
        dkv.reshape(2, 2, zs, GROUPS, 2, n, WIDE),
        slabs(grad1, inner_bias_grad[None]),
        grad2.astype(low_type).reshape(zs, GROUPS, 2, e, depth),
        slabs(gradm, mix_extras),
    )
    key_grad = jnp.sum(dkv.astype(wide), axis=0).astype(low_type).reshape(rows, WIDE)
    grads = jnp.concatenate([key_grad, query_grad], axis=1)
    gradq = jnp.einsum("tc,td->cd", tok_all, grads, preferred_element_type=wide)
    bias_grad = jnp.sum(grads.astype(wide), axis=0)
    partial = jnp.einsum("td,cd->tc", grads, w_qkv, preferred_element_type=wide).astype(low_type)
    partial, outq = reduce_tokens(
        zs, partial.reshape(GROUPS, n, depth), slabs(gradq, bias_grad[None])
    )
    input_grad = early_grads[0] + jnp.sum(partial.astype(wide), axis=0)

    def own(vector, count):
        return lax.dynamic_slice_in_dim(vector, device * count, count, 0).astype(wide)

    outq = outq.astype(wide)
    kv_out = outq[:, :, :WIDE].reshape(GROUPS, -1, LOCAL, 2, HEAD)
    q_out = outq[:, :, WIDE:].reshape(GROUPS, -1, LOCAL, 2, HEAD)[:, :, :, 0]

    def unpacked(values):
        return jnp.transpose(values, (1, 0, 2, 3)).reshape(-1, depth)

    q_out, k_out, v_out = unpacked(q_out), unpacked(kv_out[:, :, :, 0]), unpacked(kv_out[:, :, :, 1])
    inner_out = jnp.transpose(out1[:, :s], (1, 0, 2)).reshape(s, ff).astype(wide)
    return (
        output,
        input_grad.astype(low_type),
        q_out[:s],
        own(q_out[s], s),
        k_out[:s],
        v_out[:s],
        own(v_out[s], s),
        outm[:s],
        own(outm[s], s),
        own(outm[s + 1], s),
        own(outm[s + 2], s),
        inner_out,
        own(out1[:, s].reshape(ff), e),
        out2,
        own(outm[s + 3], s),
        own(outm[s + 4], s),
        own(outm[s + 5], s),
    )


def on_device(
    tokens,
    cotangent,
    doc_lengths,
    query_weight,
    query_bias,
    key_weight,
    value_weight,
    value_bias,
    mix_weight,
    mix_bias,
    early_gain,
    early_shift,
    inner_weight,
    inner_bias,
    outer_weight,
    outer_bias,
    final_gain,
    final_shift,
):
    n, depth = tokens.shape
    cycle = lax.axis_size("row")
    devices = lax.axis_size("au") * cycle
    s = query_weight.shape[0]
    ff = inner_weight.shape[1]
    quarter = ff // 4
    e = outer_weight.shape[0]
    rows = GROUPS * n
    total_tokens = n * devices
    me = Spot()
    vectors = [
        vector.reshape(1, -1)
        for vector in (
            query_bias, value_bias, mix_bias, early_gain, early_shift,
            outer_bias, final_gain, final_shift,
        )
    ]
    vectors.append(inner_bias.reshape(1, -1))
    toks, queries, w_qkv, vec, kv_all, w1, wm, mixed, mixed_wide, lse = first_kernel(
        doc_lengths, tokens, query_weight, key_weight, value_weight, vectors,
        inner_weight, mix_weight, e,
    )
    queries = queries.reshape(rows, WIDE)
    kv_all = kv_all.reshape(total_tokens, WIDE)
    w_qkv = w_qkv.reshape(depth, -1)
    w1 = w1.reshape(depth, quarter)
    wm = wm.reshape(depth, depth)
    output, hidden_grad, grad_all, summ, sum1, sum2 = middle_kernel(
        mixed.reshape(GROUPS, n, PACK), tokens, cotangent, wm, w1, outer_weight, vec, s, e
    )
    grad_all = grad_all.reshape(rows, PACK)
    pieces, outqk, out1, out2, outm = turn_kernel(
        doc_lengths, queries, kv_all, grad_all, mixed_wide, lse, toks, w_qkv, sum1, sum2, summ
    )
    results = final_kernel(output, hidden_grad, pieces, outqk, out1, out2, outm, s, e)
    return tuple(
        result.reshape(-1) if result.shape[0] == 1 else result for result in results
    )


def solution(mesh):
    both = P(("au", "row"), None)
    flat = P(("au", "row"))
    in_specs = (
        both, both, P(), both, flat, both, both, flat, both, flat, flat, flat,
        both, flat, both, flat, flat, flat,
    )
    out_specs = (
        both, both, both, flat, both, both, flat, both, flat, flat, flat,
        both, flat, both, flat, flat, flat,
    )
    fast = mesh.shape["au"] == 4 and mesh.shape["row"] == 2 * GROUPS
    return jax.shard_map(
        on_device if fast else on_device_general, mesh=mesh, in_specs=in_specs, out_specs=out_specs, check_vma=False
    )
```

```python
import functools

import jax
import jax.numpy as jnp
import numpy as np
from jax import lax
from jax.experimental import pallas as pl
from jax.experimental.pallas import tpu as pltpu
from jax.sharding import PartitionSpec as P

HEAD = 64
HEADS = 12
GROUPS = 4
LOCAL = HEADS // GROUPS
LANES = 2 * HEAD
WIDE = LOCAL * LANES
PACK = 256
eps_norm = 1e-06
mask_fill = -1000000000.0
lowest_start = -1e30
low_type = jnp.bfloat16
wide = jnp.float32
MESH = pl.DeviceIdType.MESH
VMEM_LIMIT = 62 * 1024 * 1024
NEAR_LIMIT = 36 * 1024 * 1024
TURN_LIMIT = 40 * 1024 * 1024


def layer_norm(hidden, gain, shift):
    mean = jnp.mean(hidden, axis=-1, keepdims=True)
    centered = hidden - mean
    spread = jnp.mean(centered * centered, axis=-1, keepdims=True)
    return centered * lax.rsqrt(spread + eps_norm) * gain + shift


def gelu_exact(values):
    return jax.nn.gelu(values, approximate=False)


class Place:
    def __init__(self, zs):
        self.zs = zs
        a = lax.axis_index("au")
        r = lax.axis_index("row")
        self.x, self.c = a // 2, a % 2
        self.y, q = r % 2, r // 2
        self.g, self.z = q % GROUPS, q // GROUPS

    def at(self, x=None, c=None, z=None, g=None, y=None):
        x = self.x if x is None else x
        c = self.c if c is None else c
        z = self.z if z is None else z
        g = self.g if g is None else g
        y = self.y if y is None else y
        return (x * 2 + c, (z * GROUPS + g) * 2 + y)

    def sibling(self):
        return self.at(c=1 - self.c)

    def line(self):
        return [((self.g + k) % GROUPS, (self.g + GROUPS - k) % GROUPS) for k in range(1, GROUPS)]

    def column(self):
        count = self.zs * GROUPS
        q = self.z * GROUPS + self.g
        result = []
        for k in range(1, count):
            to, source = (q + k) % count, (q + count - k) % count
            result.append(((to // GROUPS, to % GROUPS), (source // GROUPS, source % GROUPS)))
        return result

    def plane(self, everywhere=True):
        result = []
        for dx in range(2):
            for dy in range(2):
                for dz in range(self.zs if everywhere else 1):
                    if dx + dy + dz == 0:
                        continue
                    to = ((self.x + dx) % 2, (self.z + dz) % self.zs, (self.y + dy) % 2)
                    source = (
                        (self.x + dx) % 2,
                        (self.z + self.zs - dz) % self.zs,
                        (self.y + dy) % 2,
                    )
                    result.append((to, source))
        return result


class Copies:
    def __init__(self, send, recv, local):
        self.send, self.recv, self.local = send, recv, local
        self.count = 0
        self.local_count = 0
        self.started = []
        self.local_started = []

    def push(self, source, target, device):
        copy = pltpu.make_async_remote_copy(
            src_ref=source,
            dst_ref=target,
            send_sem=self.send.at[self.count],
            recv_sem=self.recv.at[self.count],
            device_id=device,
            device_id_type=MESH,
        )
        self.count += 1
        copy.start()
        self.started.append(copy)
        return copy

    def keep(self, source, target):
        copy = pltpu.make_async_copy(source, target, self.local.at[self.local_count])
        self.local_count += 1
        copy.start()
        return copy

    def finish(self):
        for copy in self.started:
            copy.wait_send()


def greet(devices, partner=None, crossing=None):
    barrier = pltpu.get_barrier_semaphore()
    for device in devices:
        pl.semaphore_signal(barrier, inc=1, device_id=device, device_id_type=MESH)
    if partner is None:
        pl.semaphore_wait(barrier, len(devices))
        return

    @pl.when(crossing)
    def _():
        pl.semaphore_signal(barrier, inc=1, device_id=partner, device_id_type=MESH)
        pl.semaphore_wait(barrier, len(devices) + 1)

    @pl.when(jnp.logical_not(crossing))
    def _():
        pl.semaphore_wait(barrier, len(devices))


def comm_call(body, name, ident, outs, copies, locals_, args, spaces=None, out_spaces=None, scratch=()):
    spaces = [pl.ANY] * len(args) if spaces is None else spaces
    out_spaces = [pl.ANY] * len(outs) if out_spaces is None else out_spaces
    return pl.pallas_call(
        body,
        name=name,
        out_shape=tuple(outs),
        in_specs=[pl.BlockSpec(memory_space=space) for space in spaces],
        out_specs=tuple(pl.BlockSpec(memory_space=space) for space in out_spaces),
        scratch_shapes=[
            pltpu.SemaphoreType.DMA((max(copies, 1),)),
            pltpu.SemaphoreType.DMA((max(copies, 1),)),
            pltpu.SemaphoreType.DMA((max(locals_, 1),)),
            *scratch,
        ],
        compiler_params=pltpu.CompilerParams(
            collective_id=ident, has_side_effects=True, vmem_limit_bytes=VMEM_LIMIT
        ),
    )(*args)


def spread_tokens(zs, tokens, slab):
    n, width = tokens.shape
    groups, rows, columns = slab.shape
    plane = 4 * zs - 1

    def body(tok, piece, tok_all, w_all, send, recv, local):
        me = Place(zs)
        copies = Copies(send, recv, local)
        greet(
            [me.at(g=to) for to, _ in me.line()]
            + [me.at(x=to[0], z=to[1], y=to[2]) for to, _ in me.plane()]
            + [me.sibling()]
        )
        first = [
            copies.push(
                piece.at[to], w_all.at[me.x, me.c, me.z, me.g, me.y], me.at(g=to)
            )
            for to, _ in me.line()
        ]
        own = copies.keep(piece.at[me.g], w_all.at[me.x, me.c, me.z, me.g, me.y])
        arrivals = [copies.push(tok, tok_all.at[me.g], me.at(g=to)) for to, _ in me.line()]
        mine = copies.keep(tok, tok_all.at[me.g])
        own.wait()
        for copy in first:
            copy.wait_recv()
        block = w_all.at[me.x, me.c, me.z, :, me.y]
        second = [
            copies.push(block, block, me.at(x=to[0], z=to[1], y=to[2])) for to, _ in me.plane()
        ]
        arrivals.append(copies.push(block, block, me.sibling()))
        for copy, (_, source) in zip(second, me.plane()):
            copy.wait_recv()
            part = w_all.at[source[0], me.c, source[1], :, source[2]]
            arrivals.append(copies.push(part, part, me.sibling()))
        for copy in arrivals:
            copy.wait_recv()
        mine.wait()
        copies.finish()

    return comm_call(
        body,
        "spread_tokens",
        0,
        [
            jax.ShapeDtypeStruct((GROUPS, n, width), low_type),
            jax.ShapeDtypeStruct((2, 2, zs, GROUPS, 2, rows, columns), low_type),
        ],
        2 * (GROUPS - 1) + 2 * plane + 1,
        2,
        (tokens, slab),
    )


def spread_keys(zs, keys, inner, outer, mix):
    groups, n, width = keys.shape
    quarters, rows, columns = inner.shape
    tall, _ = outer.shape
    plane, column = 4 * zs - 1, GROUPS * zs - 1

    def body(kv, w1s, w2s, wms, kv_all, w1, w2, wm, send, recv, local, swap_send, swap_recv):
        me = Place(zs)
        copies = Copies(send, recv, local)
        crossing = me.c != me.y
        greet(
            [me.at(x=to[0], z=to[1], y=to[2]) for to, _ in me.plane()]
            + [me.at(z=to[0], g=to[1]) for to, _ in me.column()]
            + [me.at(z=to[0], g=to[1], c=me.y, y=me.c) for to, _ in me.column()]
            + [me.sibling()],
            me.at(c=me.y, y=me.c),
            crossing,
        )

        def here(ref):
            return ref.at[me.x, me.c, me.z, me.g, me.y]

        flat = me.plane(everywhere=False)
        own = [
            copies.keep(w1s.at[me.x * 2 + me.y], here(w1)),
            copies.keep(wms, here(wm)),
            copies.keep(kv, kv_all.at[me.x, me.c, me.z, :, me.y]),
        ]
        w1_first = [
            copies.push(w1s.at[to[0] * 2 + to[2]], here(w1), me.at(x=to[0], y=to[2]))
            for to, _ in flat
        ]
        wm_first = [
            copies.push(wms, here(wm), me.at(z=to[0], g=to[1])) for to, _ in me.column()
        ]
        mine = kv_all.at[me.x, me.c, me.z, :, me.y]
        kv_first = [
            copies.push(kv, mine, me.at(x=to[0], z=to[1], y=to[2])) for to, _ in me.plane()
        ]
        arrivals = [copies.push(kv, mine, me.sibling())]
        w2_first = [
            copies.push(
                w2s, w2.at[me.z, me.g, me.y], me.at(z=to[0], g=to[1], c=me.y, y=me.c)
            )
            for to, _ in me.column()
        ]
        exchanged = pltpu.make_async_remote_copy(
            src_ref=w2s,
            dst_ref=w2.at[me.z, me.g, me.y],
            send_sem=swap_send,
            recv_sem=swap_recv,
            device_id=me.at(c=me.y, y=me.c),
            device_id_type=MESH,
        )
        stays = pltpu.make_async_copy(w2s, w2.at[me.z, me.g, me.y], swap_recv)

        @pl.when(crossing)
        def _():
            exchanged.start()

        @pl.when(jnp.logical_not(crossing))
        def _():
            stays.start()

        own[0].wait()
        for copy in w1_first:
            copy.wait_recv()
        block = w1.at[:, me.c, me.z, me.g, :]
        w1_second = [
            copies.push(block, block, me.at(z=to[0], g=to[1])) for to, _ in me.column()
        ]
        arrivals.append(copies.push(block, block, me.sibling()))
        own[1].wait()
        for copy in wm_first:
            copy.wait_recv()
        block = wm.at[me.x, me.c, :, :, me.y]
        wm_second = [copies.push(block, block, me.at(x=to[0], y=to[2])) for to, _ in flat]
        arrivals.append(copies.push(block, block, me.sibling()))
        for copy, (_, source) in zip(kv_first, me.plane()):
            copy.wait_recv()
            part = kv_all.at[source[0], me.c, source[1], :, source[2]]
            arrivals.append(copies.push(part, part, me.sibling()))

        @pl.when(crossing)
        def _():
            exchanged.wait_recv()
            exchanged.wait_send()

        @pl.when(jnp.logical_not(crossing))
        def _():
            stays.wait()

        part = w2.at[me.z, me.g, me.c]
        arrivals.append(copies.push(part, part, me.sibling()))
        for copy, (_, source) in zip(wm_second, flat):
            copy.wait_recv()
            part = wm.at[source[0], me.c, :, :, source[2]]
            arrivals.append(copies.push(part, part, me.sibling()))
        for copy, (_, source) in zip(w2_first, me.column()):
            copy.wait_recv()
            part = w2.at[source[0], source[1], me.c]
            arrivals.append(copies.push(part, part, me.sibling()))
        for copy, (_, source) in zip(w1_second, me.column()):
            copy.wait_recv()
            part = w1.at[:, me.c, source[0], source[1], :]
            arrivals.append(copies.push(part, part, me.sibling()))
        for copy in arrivals:
            copy.wait_recv()
        own[2].wait()
        copies.finish()

    return comm_call(
        body,
        "spread_keys",
        1,
        [
            jax.ShapeDtypeStruct((2, 2, zs, GROUPS, 2, n, width), low_type),
            jax.ShapeDtypeStruct((2, 2, zs, GROUPS, 2, rows, columns), low_type),
            jax.ShapeDtypeStruct((zs, GROUPS, 2, tall, columns), low_type),
            jax.ShapeDtypeStruct((2, 2, zs, GROUPS, 2) + mix.shape, low_type),
        ],
        2 * plane + 1 + 2 * (3 + column + 1 + column) + column + 3 + 8,
        3,
        (keys, inner, outer, mix),
        scratch=(pltpu.SemaphoreType.DMA, pltpu.SemaphoreType.DMA),
    )


def exchange_line(zs, ident, pieces):
    def body(source, target, send, recv, local):
        me = Place(zs)
        copies = Copies(send, recv, local)
        greet([me.at(g=to) for to, _ in me.line()])
        arrivals = [
            copies.push(source.at[to], target.at[me.g], me.at(g=to)) for to, _ in me.line()
        ]
        own = copies.keep(source.at[me.g], target.at[me.g])
        for copy in arrivals:
            copy.wait_recv()
        own.wait()
        copies.finish()

    return comm_call(
        body,
        "exchange_line",
        ident,
        [jax.ShapeDtypeStruct(pieces.shape, pieces.dtype)],
        GROUPS - 1,
        1,
        (pieces,),
    )[0]


def gather_square(zs, ident, rows):
    def body(source, target, send, recv, local):
        me = Place(zs)
        copies = Copies(send, recv, local)
        flat = me.plane(everywhere=False)
        greet([me.at(x=to[0], y=to[2]) for to, _ in flat])
        place = target.at[me.x, me.y]
        arrivals = [copies.push(source, place, me.at(x=to[0], y=to[2])) for to, _ in flat]
        own = copies.keep(source, place)
        for copy in arrivals:
            copy.wait_recv()
        own.wait()
        copies.finish()

    return comm_call(
        body,
        "gather_square",
        ident,
        [jax.ShapeDtypeStruct((2, 2) + rows.shape, rows.dtype)],
        3,
        1,
        (rows,),
    )[0]


def exchange_square(zs, ident, pieces):
    def body(source, target, send, recv, local):
        me = Place(zs)
        copies = Copies(send, recv, local)
        flat = me.plane(everywhere=False)
        greet([me.at(x=to[0], y=to[2]) for to, _ in flat])
        place = target.at[me.x, me.y]
        arrivals = [
            copies.push(source.at[to[0], to[2]], place, me.at(x=to[0], y=to[2]))
            for to, _ in flat
        ]
        own = copies.keep(source.at[me.x, me.y], place)
        for copy in arrivals:
            copy.wait_recv()
        own.wait()
        copies.finish()

    return comm_call(
        body,
        "exchange_square",
        ident,
        [jax.ShapeDtypeStruct(pieces.shape, pieces.dtype)],
        3,
        1,
        (pieces,),
    )[0]


def loop(count, step):
    def body(index, carry):
        step(index)
        return carry

    lax.fori_loop(0, count, body, 0)


def total_of(*values):
    result = values[0].astype(wide)
    for value in values[1:]:
        result = result + value.astype(wide)
    return result


def reduce_keys(zs, dkv, grad1, grad2, gradm):
    n, width = dkv.shape[-2:]
    rows, columns = grad1.shape[-2:]
    rowsm = gradm.shape[-2]
    tall = grad2.shape[-2]
    plane, column = 4 * zs - 1, GROUPS * zs - 1
    count = GROUPS * zs

    def body(
        dkv_ref, g1, g2, gm, dkv_out, out1, out2, outm,
        send, recv, local,
        swap_send, swap_recv, kst, s1, p1, f1, s2, p2, sm, pm, fm, tm,
    ):
        me = Place(zs)
        copies = Copies(send, recv, local)
        crossing = me.c != me.y
        greet(
            [me.at(x=to[0], z=to[1], y=to[2]) for to, _ in me.plane()]
            + [me.at(z=to[0], g=to[1]) for to, _ in me.column()]
            + [me.at(z=to[0], g=to[1], c=me.y, y=me.c) for to, _ in me.column()]
            + [me.sibling()],
            me.at(c=me.y, y=me.c),
            crossing,
        )

        flat = me.plane(everywhere=False)
        other = 1 - me.c
        order = [to for to, _ in me.plane()] + [(me.x, me.z, me.y)]
        w1_half = copies.push(g1.at[:, other], s1, me.sibling())
        w2_half = copies.push(g2.at[:, :, other], s2, me.sibling())
        k_half = [
            copies.push(
                dkv_ref.at[to[0], other, to[1], :, to[2]], kst.at[to[0], to[1], to[2]], me.sibling()
            )
            for to in order
        ]
        wm_half = copies.push(gm.at[:, other], sm, me.sibling())

        w1_half.wait_recv()

        def add1(index):
            x, z, g, y = index // (count * 2), index // (GROUPS * 2) % zs, index // 2 % GROUPS, index % 2
            s1[x, z, g, y] = total_of(s1[x, z, g, y], g1[x, me.c, z, g, y]).astype(low_type)

        loop(4 * count, add1)
        w1_push = [
            copies.push(s1.at[:, to[0], to[1], :], p1.at[slot], me.at(z=to[0], g=to[1]))
            for slot, (to, _) in enumerate(me.column())
        ]
        w2_half.wait_recv()

        def add2(index):
            z, g = index // GROUPS, index % GROUPS
            s2[z, g] = total_of(s2[z, g], g2[z, g, me.c]).astype(low_type)

        loop(count, add2)
        w2_push = [
            copies.push(
                s2.at[to[0], to[1]], p2.at[slot + 1], me.at(z=to[0], g=to[1], c=me.y, y=me.c)
            )
            for slot, (to, _) in enumerate(me.column())
        ]
        exchanged = pltpu.make_async_remote_copy(
            src_ref=s2.at[me.z, me.g],
            dst_ref=p2.at[0],
            send_sem=swap_send,
            recv_sem=swap_recv,
            device_id=me.at(c=me.y, y=me.c),
            device_id_type=MESH,
        )
        stays = pltpu.make_async_copy(s2.at[me.z, me.g], p2.at[0], swap_recv)

        @pl.when(crossing)
        def _():
            exchanged.start()

        @pl.when(jnp.logical_not(crossing))
        def _():
            stays.start()

        k_push = []
        for slot, to in enumerate(order):
            k_half[slot].wait_recv()

            def addk(g, to=to):
                kst[to[0], to[1], to[2], g] = total_of(
                    kst[to[0], to[1], to[2], g], dkv_ref[to[0], me.c, to[1], g, to[2]]
                ).astype(low_type)

            loop(GROUPS, addk)
            if slot < plane:
                k_push.append(
                    copies.push(
                        kst.at[to[0], to[1], to[2]],
                        dkv_out.at[slot],
                        me.at(x=to[0], z=to[1], y=to[2]),
                    )
                )
        wm_half.wait_recv()

        def addm(index):
            x, z, g, y = index // (count * 2), index // (GROUPS * 2) % zs, index // 2 % GROUPS, index % 2
            sm[x, z, g, y] = total_of(sm[x, z, g, y], gm[x, me.c, z, g, y]).astype(low_type)

        loop(4 * count, addm)
        wm_push = [
            copies.push(sm.at[to[0], :, :, to[2]], pm.at[slot], me.at(x=to[0], y=to[2]))
            for slot, (to, _) in enumerate(flat)
        ]
        keep = copies.keep(kst.at[me.x, me.z, me.y], dkv_out.at[plane])
        for copy in wm_push:
            copy.wait_recv()

        def addf(index):
            z, g = index // GROUPS, index % GROUPS
            fm[z, g] = total_of(sm[me.x, z, g, me.y], pm[0, z, g], pm[1, z, g], pm[2, z, g]).astype(
                low_type
            )

        loop(count, addf)
        wm_last = [
            copies.push(fm.at[to[0], to[1]], tm.at[slot], me.at(z=to[0], g=to[1]))
            for slot, (to, _) in enumerate(me.column())
        ]
        for copy in w1_push:
            copy.wait_recv()

        def addg(index):
            x, y = index // 2, index % 2
            f1[x, y] = total_of(
                s1[x, me.z, me.g, y], *[p1[slot, x, y] for slot in range(column)]
            ).astype(low_type)

        loop(4, addg)
        quarter = out1.at[me.x * 2 + me.y]
        w1_last = [
            copies.push(f1.at[to[0], to[2]], quarter, me.at(x=to[0], y=to[2])) for to, _ in flat
        ]
        keep1 = copies.keep(f1.at[me.x, me.y], quarter)

        @pl.when(crossing)
        def _():
            exchanged.wait_recv()
            exchanged.wait_send()

        @pl.when(jnp.logical_not(crossing))
        def _():
            stays.wait()

        for copy in w2_push:
            copy.wait_recv()
        out2[...] = total_of(*[p2[slot] for slot in range(column + 1)])
        for copy in wm_last:
            copy.wait_recv()
        outm[...] = total_of(fm[me.z, me.g], *[tm[slot] for slot in range(column)])
        for copy in w1_last + k_push:
            copy.wait_recv()
        keep.wait()
        keep1.wait()
        copies.finish()

    vmem = pltpu.VMEM
    return comm_call(
        body,
        "reduce_keys",
        8,
        [
            jax.ShapeDtypeStruct((plane + 1, GROUPS, n, width), low_type),
            jax.ShapeDtypeStruct((4, rows, columns), low_type),
            jax.ShapeDtypeStruct((tall, columns), wide),
            jax.ShapeDtypeStruct((rowsm, columns), wide),
        ],
        3 + (plane + 1) + 2 * column + plane + 3 + column + 3,
        2,
        (dkv, grad1, grad2, gradm),
        spaces=[vmem] * 4,
        out_spaces=[pl.ANY, pl.ANY, vmem, vmem],
        scratch=(
            pltpu.SemaphoreType.DMA,
            pltpu.SemaphoreType.DMA,
            vmem((2, zs, 2, GROUPS, n, width), low_type),
            vmem((2, zs, GROUPS, 2, rows, columns), low_type),
            vmem((column, 2, 2, rows, columns), low_type),
            vmem((2, 2, rows, columns), low_type),
            vmem((zs, GROUPS, tall, columns), low_type),
            vmem((column + 1, tall, columns), low_type),
            vmem((2, zs, GROUPS, 2, rowsm, columns), low_type),
            vmem((3, zs, GROUPS, rowsm, columns), low_type),
            vmem((zs, GROUPS, rowsm, columns), low_type),
            vmem((column, rowsm, columns), low_type),
        ),
    )


def reduce_tokens(zs, dx, gradq):
    rows, columns = gradq.shape[-2:]
    plane = 4 * zs - 1
    count = GROUPS * zs

    def body(dx_ref, gq, dx_out, outq, send, recv, local, sq, pq, fq):
        me = Place(zs)
        copies = Copies(send, recv, local)
        greet(
            [me.at(g=to) for to, _ in me.line()]
            + [me.at(x=to[0], z=to[1], y=to[2]) for to, _ in me.plane()]
            + [me.sibling()]
        )
        half = copies.push(gq.at[:, 1 - me.c], sq, me.sibling())
        arrivals = [
            copies.push(dx_ref.at[to], dx_out.at[me.g], me.at(g=to)) for to, _ in me.line()
        ]
        own = copies.keep(dx_ref.at[me.g], dx_out.at[me.g])
        half.wait_recv()

        def add1(index):
            x, z, g, y = index // (count * 2), index // (GROUPS * 2) % zs, index // 2 % GROUPS, index % 2
            sq[x, z, g, y] = total_of(sq[x, z, g, y], gq[x, me.c, z, g, y]).astype(low_type)

        loop(4 * count, add1)
        second = [
            copies.push(
                sq.at[to[0], to[1], :, to[2]], pq.at[slot], me.at(x=to[0], z=to[1], y=to[2])
            )
            for slot, (to, _) in enumerate(me.plane())
        ]
        for copy in second:
            copy.wait_recv()

        def add2(g):
            fq[g] = total_of(
                sq[me.x, me.z, g, me.y], *[pq[slot, g] for slot in range(plane)]
            ).astype(low_type)

        loop(GROUPS, add2)
        arrivals += [
            copies.push(fq.at[to], outq.at[me.g], me.at(g=to)) for to, _ in me.line()
        ]
        keep = copies.keep(fq.at[me.g], outq.at[me.g])
        for copy in arrivals:
            copy.wait_recv()
        own.wait()
        keep.wait()
        copies.finish()

    vmem = pltpu.VMEM
    return comm_call(
        body,
        "reduce_tokens",
        9,
        [
            jax.ShapeDtypeStruct(dx.shape, low_type),
            jax.ShapeDtypeStruct((GROUPS, rows, columns), low_type),
        ],
        1 + 2 * (GROUPS - 1) + plane,
        2,
        (dx, gradq),
        spaces=[pl.ANY, vmem],
        scratch=(
            vmem((2, zs, GROUPS, 2, rows, columns), low_type),
            vmem((plane, GROUPS, rows, columns), low_type),
            vmem((GROUPS, rows, columns), low_type),
        ),
    )


NEXT = (((1,), (1,)), ((), ()))
DOWN = (((0,), (0,)), ((), ()))


def attend_forward(queries, keys, bounds, low, high, tile, block):
    total_rows = queries.shape[0]

    def body(bounds_ref, q_ref, kv_ref, low_ref, high_ref, out_ref, keep_ref, lse_ref):
        def one(turn, unused):
            rows = pl.ds(pl.multiple_of(turn * tile, tile), tile)
            first, last = low_ref[rows, :], high_ref[rows, :]
            heads = [
                q_ref[rows, h * LANES : (h + 1) * LANES] * jnp.asarray(0.125, low_type)
                for h in range(LOCAL)
            ]

            def step(j, carry):
                begin = pl.multiple_of(j * block, block)
                place = begin + lax.broadcasted_iota(jnp.int32, (tile, block), 1)
                same = (place >= first) & (place < last)
                result = []
                for h in range(LOCAL):
                    top, total, mixed = carry[h]
                    kv = kv_ref[pl.ds(begin, block), h * LANES : (h + 1) * LANES]
                    scores = lax.dot_general(heads[h], kv, NEXT, preferred_element_type=wide)
                    scores = jnp.where(same, scores, mask_fill)
                    new_top = jnp.maximum(top, jnp.max(scores, axis=1, keepdims=True))
                    factor = jnp.exp(top - new_top)
                    powers = jnp.exp(scores - new_top)
                    total = total * factor + jnp.sum(powers, axis=1, keepdims=True)
                    mixed = mixed * factor + jnp.dot(
                        powers.astype(low_type), kv, preferred_element_type=wide
                    )
                    result.append((new_top, total, mixed))
                return tuple(result)

            start = tuple(
                (
                    jnp.full((tile, 1), lowest_start, wide),
                    jnp.zeros((tile, 1), wide),
                    jnp.zeros((tile, LANES), wide),
                )
                for _ in range(LOCAL)
            )
            done = lax.fori_loop(bounds_ref[turn, 0], bounds_ref[turn, 1], step, start)
            lane = lax.broadcasted_iota(jnp.int32, (tile, LANES), 1)
            upper = lane >= HEAD
            mixes = [mixed / total for _, total, mixed in done]
            turned = [pltpu.roll(mixed, HEAD, 1) for mixed in mixes]
            front = jnp.where(upper, mixes[1], turned[0])
            back = jnp.where(upper, 0.0, turned[2])
            both = jnp.concatenate([front, back], axis=1)
            keep_ref[rows, :] = both
            out_ref[rows, :] = both.astype(low_type)
            ends = [top + jnp.log(total) for top, total, _ in done]
            lse_ref[rows, :] = jnp.where(lane == 0, ends[0], jnp.where(lane == 1, ends[1], ends[2]))
            return unused

        lax.fori_loop(0, total_rows // tile, one, 0)

    vmem = pl.BlockSpec(memory_space=pltpu.VMEM)
    return pl.pallas_call(
        body,
        name="attend_forward",
        out_shape=(
            jax.ShapeDtypeStruct((total_rows, PACK), low_type),
            jax.ShapeDtypeStruct((total_rows, PACK), wide),
            jax.ShapeDtypeStruct((total_rows, LANES), wide),
        ),
        in_specs=[pl.BlockSpec(memory_space=pltpu.SMEM)] + [vmem] * 4,
        out_specs=(vmem,) * 3,
        compiler_params=pltpu.CompilerParams(vmem_limit_bytes=VMEM_LIMIT),
    )(bounds, queries, keys, low, high)


def attend_backward(queries, keys, grads, stats, bounds, tile, block):
    total_rows = queries.shape[0]
    tokens = keys.shape[0]

    def body(bounds_ref, q_ref, kv_ref, do_ref, stat_ref, dq_ref, dkv_ref, sums):
        h = pl.program_id(0)
        zeros = jnp.zeros((block, LANES), wide)

        def clear(j, unused):
            sums[pl.ds(pl.multiple_of(j * block, block), block), :] = zeros
            return unused

        lax.fori_loop(0, tokens // block, clear, 0)
        lane = lax.broadcasted_iota(jnp.int32, (tile, LANES), 1)
        upper = lane >= HEAD

        def one(turn, unused):
            rows = pl.ds(pl.multiple_of(turn * tile, tile), tile)
            q = q_ref[rows, :] * jnp.asarray(0.125, low_type)
            front = do_ref[rows, :LANES].astype(wide)
            back = do_ref[rows, LANES:].astype(wide)
            grad = jnp.where(h == 1, front, pltpu.roll(jnp.where(h == 0, front, back), HEAD, 1))
            grad = jnp.where(upper, grad, 0.0).astype(low_type)
            stat = stat_ref[turn, 0]
            first, last = stat[0:1, :], stat[1:2, :]
            lse, delta = stat[2:3, :], stat[3:4, :]

            def step(j, total):
                begin = pl.multiple_of(j * block, block)
                place = (begin + lax.broadcasted_iota(jnp.int32, (block, tile), 0)).astype(wide)
                same = (place >= first) & (place < last)
                kv = kv_ref[pl.ds(begin, block), :]
                scores = lax.dot_general(kv, q, NEXT, preferred_element_type=wide)
                probs = jnp.exp(jnp.where(same, scores, mask_fill) - lse)
                dots = lax.dot_general(kv, grad, NEXT, preferred_element_type=wide)
                score_grad = (probs * (dots - delta)).astype(low_type)
                sums[pl.ds(begin, block), :] += jnp.dot(
                    score_grad, q, preferred_element_type=wide
                ) + jnp.dot(probs.astype(low_type), grad, preferred_element_type=wide)
                return total + lax.dot_general(score_grad, kv, DOWN, preferred_element_type=wide)

            total = lax.fori_loop(
                bounds_ref[turn, 0], bounds_ref[turn, 1], step, jnp.zeros((tile, LANES), wide)
            )
            dq_ref[rows, :] = jnp.where(upper, 0.0, total * 0.125).astype(low_type)
            return unused

        lax.fori_loop(0, total_rows // tile, one, 0)

        def store(j, unused):
            part = pl.ds(pl.multiple_of(j * block, block), block)
            dkv_ref[part, :] = sums[part, :].astype(low_type)
            return unused

        lax.fori_loop(0, tokens // block, store, 0)

    return pl.pallas_call(
        body,
        name="attend_backward",
        grid=(LOCAL,),
        out_shape=(
            jax.ShapeDtypeStruct((total_rows, WIDE), low_type),
            jax.ShapeDtypeStruct((tokens, WIDE), low_type),
        ),
        in_specs=[
            pl.BlockSpec(memory_space=pltpu.SMEM),
            pl.BlockSpec((total_rows, LANES), lambda h: (0, h)),
            pl.BlockSpec((tokens, LANES), lambda h: (0, h)),
            pl.BlockSpec((total_rows, PACK), lambda h: (0, 0)),
            pl.BlockSpec((total_rows // tile, 1, 8, tile), lambda h: (0, h, 0, 0)),
        ],
        out_specs=(
            pl.BlockSpec((total_rows, LANES), lambda h: (0, h)),
            pl.BlockSpec((tokens, LANES), lambda h: (0, h)),
        ),
        scratch_shapes=[pltpu.VMEM((tokens, LANES), wide)],
        compiler_params=pltpu.CompilerParams(vmem_limit_bytes=VMEM_LIMIT),
    )(bounds, queries, keys, grads, stats)


class Spot(Place):
    def __init__(self):
        super().__init__(1)
        self.half = self.g // 2
        self.a = self.x * 2 + self.c
        self.p = (self.x + self.c) % 2
        self.selfish = self.g % 2 == self.p
        self.crossing = self.c != self.y

    def square(self):
        return [(to[0], to[2]) for to, _ in reversed(self.plane())]

    def readers(self):
        result = []
        for k in range(GROUPS):
            g = (self.g + k) % GROUPS
            result.append((g, self.at(x=(self.g + self.c) % 2, g=g)))
        return result

    def owners(self):
        result = []
        for dv in range(2):
            for du in range(2):
                u, v = (self.x + du) % 2, (self.half + dv) % 2
                result.append((u * 2 + v, self.at(x=u, g=2 * v + self.p)))
        return result

    def slot(self):
        return self.x * 2 + self.half


def count_of(flag):
    return jnp.where(flag, 1, 0)


def announce(always, maybe):
    barrier = pltpu.get_barrier_semaphore()
    for device in always:
        pl.semaphore_signal(barrier, inc=1, device_id=device, device_id_type=MESH)
    for flag, device in maybe:

        @pl.when(flag)
        def _(device=device):
            pl.semaphore_signal(barrier, inc=1, device_id=device, device_id_type=MESH)

    total = len(always)
    for flag, _ in maybe:
        total = total + count_of(flag)
    return barrier, total


class Scatter:
    def __init__(self, send, recv, here):
        self.send, self.recv, self.here = send, recv, here
        self.copies = []

    def start(self, pieces, target, slot):
        for source, device in pieces:
            self.send_one(source, target, slot, device)

    def send_one(self, source, target, slot, device):
        index = len(self.copies)
        copy = pltpu.make_async_remote_copy(
            src_ref=source,
            dst_ref=target,
            send_sem=self.send.at[index],
            recv_sem=self.recv.at[slot],
            device_id=device,
            device_id_type=MESH,
        )
        self.copies.append(copy)
        if index:
            copy.start()
            return
        stay = pltpu.make_async_copy(source, target, self.recv.at[slot])

        @pl.when(self.here)
        def _():
            stay.start()

        @pl.when(jnp.logical_not(self.here))
        def _():
            copy.start()

    def arrived(self, slot, target):
        pltpu.make_async_copy(target, target, self.recv.at[slot]).wait()

    def finish(self):
        for copy in self.copies[1:]:
            copy.wait_send()

        @pl.when(jnp.logical_not(self.here))
        def _():
            self.copies[0].wait_send()


SMALL = 16


def first_tables(s, e, width):
    column = np.arange(width)
    rows = [column % s, column // s, column % e, column // e]
    return np.stack(rows + [np.zeros_like(column)] * 4).astype(np.int32)


def first_kernel(lengths, tokens, wq, wk, wv, vectors, inner, mix, e):
    n, depth = tokens.shape
    s = wq.shape[0]
    quarter = inner.shape[1] // 4
    width = WIDE + PACK
    cols = width + LANES
    tables = jnp.asarray(first_tables(s, e, 2 * WIDE))
    count = len(vectors)

    def body(*refs):
        lengths_in, tok = refs[:2]
        arguments = refs[2 : 8 + count]
        (
            tok_out, q_out, wqkv_out, vec_out, kv_out, w1, wm, mixed_out, mixed_wide, lse_out,
            send, recv, local, tok_send, tok_recv,
            slab, toks, weights, kv_own, q_own, w1s, wms, vec, few, kv_all, scaled, sums,
            loaded, lengths_ref, lengths_sem, *places,
        ) = refs[8 + count :]
        wq_ref, wk_ref, wv_ref, tab = places[:4]
        vecs = places[4 : 4 + count]
        w1f, wmf = places[4 + count :]
        loads = [pltpu.make_async_copy(lengths_in, lengths_ref, lengths_sem)]
        loads[0].start()
        for index, (argument, place) in enumerate(zip(arguments, places)):
            loads.append(pltpu.make_async_copy(argument, place, loaded.at[index]))
            loads[-1].start()
        me = Spot()
        copies = Copies(send, recv, local)
        square = me.square()
        line = [to for to, _ in me.line()]
        sources = [device for _, device in me.owners()]
        barrier, expected = announce(
            [me.at(x=x, y=y) for x, y in square]
            + [me.at(g=to) for to in line]
            + sources[1:]
            + [me.sibling()],
            [(jnp.logical_not(me.selfish), sources[0])],
        )
        for copy in loads:
            copy.wait()
        lane = lax.broadcasted_iota(jnp.int32, (s, LANES), 1)
        lower = lane < HEAD
        for head in range(HEADS):
            pair = slice(head // 2 * LANES, head // 2 * LANES + LANES)
            k, v = wk_ref[:, pair], wv_ref[:, pair]
            if head % 2:
                k = pltpu.roll(k, HEAD, 1)
            else:
                v = pltpu.roll(v, HEAD, 1)
            g, h = head // LOCAL, head % LOCAL
            slab[g, :, h * LANES : (h + 1) * LANES] = jnp.where(lower, k, v).astype(low_type)
        for half in range(2):
            b0, b1, b2 = [
                wq_ref[:, (3 * half + index) * LANES : (3 * half + index + 1) * LANES]
                for index in range(3)
            ]
            r1, r2 = pltpu.roll(b1, HEAD, 1), pltpu.roll(b2, HEAD, 1)
            tiles = [(b0, b1), (jnp.where(lower, r1, r2), r2)]
            for odd, (front, back) in enumerate(tiles):
                slab[2 * half + odd, :, WIDE : WIDE + LANES] = front.astype(low_type)
                slab[2 * half + odd, :, WIDE + LANES : width] = jnp.where(lower, back, 0.0).astype(
                    low_type
                )
        wms[...] = wmf[...].astype(low_type)
        few[...] = jnp.zeros((s, LANES), wide)
        for index in range(count):
            few[index : index + 1, : vecs[index].shape[1]] = vecs[index][...]
        small = few[...]
        for g in range(GROUPS):
            slab[g, :, width:] = small.astype(low_type)
        pl.semaphore_wait(barrier, expected)

        view = weights
        place = view.at[me.a, me.g, me.y]
        slab_first = [copies.push(slab.at[to], place, me.at(g=to)) for to in line]
        slab_own = copies.keep(slab.at[me.g], place)
        for w in range(4):
            w1s[w] = w1f[:, w * quarter : (w + 1) * quarter].astype(low_type)
        place = w1.at[me.x, me.c, me.g, me.y]
        w1_first = [
            copies.push(w1s.at[x * 2 + y], place, me.at(x=x, y=y)) for x, y in square
        ]
        w1_own = copies.keep(w1s.at[me.x * 2 + me.y], place)
        wm_own = copies.keep(wms, wm.at[me.x, me.c, me.g, me.y])

        arrivals, weight_arrivals = [], []
        slab_own.wait()
        for copy in slab_first:
            copy.wait_recv()
        tokens_go = Scatter(tok_send, tok_recv, me.selfish)
        tokens_go.start([(tok, device) for _, device in me.readers()], toks.at[me.slot()], me.slot())
        block = view.at[me.a, :, me.y]
        slab_second = [copies.push(block, block, me.at(x=x, y=y)) for x, y in square]
        weight_arrivals.append(copies.push(block, block, me.sibling()))
        for copy, (x, y) in zip(slab_second, square):
            copy.wait_recv()
            block = view.at[x * 2 + me.c, :, y]
            weight_arrivals.append(copies.push(block, block, me.sibling()))
        w1_own.wait()
        for copy in w1_first:
            copy.wait_recv()
        for copy in weight_arrivals:
            copy.wait_recv()

        table = tab[...]

        def spread(pieces, within, owner):
            count = pieces.shape[0] * SMALL
            item = lax.broadcasted_iota(jnp.int32, (count, 2 * WIDE), 0)
            index = lax.broadcasted_iota(jnp.int32, (LANES, 2 * WIDE), 0)
            chosen = jnp.where(index == within, 1.0, 0.0).astype(low_type)
            pieces = pieces.astype(wide).reshape(count, LANES).astype(low_type)
            found = jnp.dot(pieces, chosen, preferred_element_type=wide)
            found = jnp.where((item >> 4) == owner, found, 0.0)
            return jnp.sum(found.reshape(count // SMALL, SMALL, 2 * WIDE), axis=0)

        every = spread(
            view[:, :, :, :SMALL, width:].reshape(32, SMALL, LANES), table[0:1], table[1:2]
        )
        w_me = me.x * 2 + me.y
        inner_bias = spread(
            view[w_me, :, :, :SMALL, width:].reshape(8, SMALL, LANES), table[2:3], table[3:4]
        )
        rows16 = lax.broadcasted_iota(jnp.int32, (SMALL, 2 * WIDE), 0)
        vec[...] = jnp.where(rows16 == 8, inner_bias, every)
        turned = pltpu.roll(every, 2 * WIDE - me.g * LOCAL * HEAD, 1)
        lower = lax.broadcasted_iota(jnp.int32, (1, LANES), 1) < HEAD
        biases = []
        for h in range(LOCAL):
            v = turned[1:2, h // 2 * LANES : h // 2 * LANES + LANES]
            v = v if h % 2 else pltpu.roll(v, HEAD, 1)
            biases.append(jnp.where(lower, 0.0, v))
        biases.append(turned[0:1, :LANES])
        biases.append(jnp.where(lower, turned[0:1, LANES : 2 * LANES], 0.0))
        bias = jnp.concatenate(biases, axis=1)
        lower_rows = lax.broadcasted_iota(jnp.int32, (n, LANES), 1) < HEAD

        matrix = weights[:, :, :, :, :width].reshape(depth, width)
        kept, kv_first = [copies.keep(weights, wqkv_out), copies.keep(vec, vec_out)], []
        kv_sibling, kv_kept = [], []
        for dv in range(2):
            v = (me.half + dv) % 2
            for u in range(2):
                tokens_go.arrived(u * 2 + v, toks.at[u * 2 + v])
            if dv:
                block = w1.at[:, me.c, me.g, :]
                wm_first = [
                    copies.push(wms, wm.at[me.x, me.c, me.g, me.y], me.at(g=to)) for to in line
                ]
                w1_second = [copies.push(block, block, me.at(g=to)) for to in line]
            both = jnp.concatenate([toks[v], toks[2 + v]], axis=0)
            made = jnp.dot(both, matrix, preferred_element_type=wide)
            made = made + bias
            for u in range(2):
                mine = made[u * n : (u + 1) * n]
                kv_own[v, u] = mine[:, :WIDE].astype(low_type)
                front, back = mine[:, WIDE : WIDE + LANES], mine[:, WIDE + LANES :]
                for h, part in enumerate((front, pltpu.roll(front, HEAD, 1), back)):
                    q_own[u * 2 + v, :, h * LANES : (h + 1) * LANES] = jnp.where(
                        lower_rows, part, 0.0
                    ).astype(low_type)
            mine = kv_all.at[:, me.c, v, me.p, me.y]
            kv_first.append(
                [copies.push(kv_own.at[v], mine, me.at(x=x, y=y)) for x, y in square]
            )
            kv_sibling.append(copies.push(kv_own.at[v], mine, me.sibling()))
            kv_kept.append(copies.keep(kv_own.at[v], mine))
        block = w1.at[:, me.c, me.g, :]
        arrivals.append(copies.push(block, block, me.sibling()))
        kept += [copies.keep(toks, tok_out), copies.keep(q_own, q_out)]

        ends = ends_of(lengths_ref)
        rows = GROUPS * n
        spans = [slice(h * LANES, (h + 1) * LANES) for h in range(LOCAL)]
        along = lax.broadcasted_iota(jnp.int32, (1, n), 1)
        ranges = [document_of(along + tile_base(me, slot, n), ends) for slot in range(GROUPS)]
        first = jnp.concatenate([low for low, _ in ranges], axis=1)
        last = jnp.concatenate([high for _, high in ranges], axis=1)
        down = lax.broadcasted_iota(jnp.int32, (rows, rows), 0)
        for slot in range(GROUPS):
            for h, span in enumerate(spans):
                scaled[h, slot * n : (slot + 1) * n] = q_own[slot, :, span] * jnp.asarray(
                    0.125, low_type
                )
        sums[...] = jnp.zeros_like(sums)

        def attend(u, c, v, carry):
            begin = ((u * 2 + c) * 2 + v) * rows
            place = down + begin
            same = (place >= first) & (place < last)
            result = []
            for h, span in enumerate(spans):
                top, total = carry[h]
                kv = kv_all[u, c, v, :, :, :, span].reshape(rows, LANES)
                scores = lax.dot_general(kv, scaled[h], NEXT, preferred_element_type=wide)
                scores = jnp.where(same, scores, mask_fill)
                new_top = jnp.maximum(top, jnp.max(scores, axis=0, keepdims=True))
                factor = jnp.exp(top - new_top)
                powers = jnp.exp(scores - new_top)
                total = total * factor + jnp.sum(powers, axis=0, keepdims=True)
                sums[h] = sums[h] * factor + lax.dot_general(
                    kv, powers.astype(low_type), DOWN, preferred_element_type=wide
                )
                result.append((new_top, total))
            return tuple(result)

        state = tuple(
            (jnp.full((1, rows), lowest_start, wide), jnp.zeros((1, rows), wide))
            for _ in range(LOCAL)
        )
        for dv in range(2):
            v = (me.half + dv) % 2
            forwards = [kv_sibling[dv]]
            for copy, (x, y) in zip(kv_first[dv], square):
                copy.wait_recv()
                block = kv_all.at[:, me.c, v, (x + me.c) % 2, y]
                forwards.append(copies.push(block, block, me.sibling()))
            kv_kept[dv].wait()
            if dv:
                wm_own.wait()
                for copy in wm_first:
                    copy.wait_recv()
                block = wm.at[me.x, me.c, :, me.y]
                wm_second = [copies.push(block, block, me.at(x=x, y=y)) for x, y in square]
                arrivals.append(copies.push(block, block, me.sibling()))
            state = lax.fori_loop(
                0, 2, lambda u, carry, v=v: attend(u, me.c, v, carry), state
            )
            for copy in forwards:
                copy.wait_recv()
            state = lax.fori_loop(
                0, 2, lambda u, carry, v=v: attend(u, 1 - me.c, v, carry), state
            )
        kept.append(copies.keep(kv_all, kv_out))
        for copy, (x, y) in zip(wm_second, square):
            copy.wait_recv()
            block = wm.at[x, me.c, :, y]
            arrivals.append(copies.push(block, block, me.sibling()))
        for copy, (_, source) in zip(w1_second, me.line()):
            copy.wait_recv()
            block = w1.at[:, me.c, source, :]
            arrivals.append(copies.push(block, block, me.sibling()))
        lane = lax.broadcasted_iota(jnp.int32, (n, LANES), 1)
        upper = lane >= HEAD
        for slot in range(GROUPS):
            part = slice(slot * n, (slot + 1) * n)
            mixes = []
            for h in range(LOCAL):
                top, total = state[h]
                mixes.append(jnp.transpose(sums[h, :, part] / total[:, part]))
                lse_out[slot, h : h + 1, :] = top[:, part] + jnp.log(total[:, part])
            turned = [pltpu.roll(mixes[h], HEAD, 1) for h in (0, 2)]
            both = jnp.concatenate(
                [jnp.where(upper, mixes[1], turned[0]), jnp.where(upper, 0.0, turned[1])], axis=1
            )
            mixed_wide[part, :] = both
            mixed_out[slot] = both.astype(low_type)
        for copy in arrivals:
            copy.wait_recv()
        for copy in kept:
            copy.wait()
        tokens_go.finish()
        copies.finish()

    vmem = pltpu.VMEM
    dma = pltpu.SemaphoreType.DMA
    total = 64
    return pl.pallas_call(
        body,
        name="first_kernel",
        out_shape=(
            jax.ShapeDtypeStruct((GROUPS, n, depth), low_type),
            jax.ShapeDtypeStruct((GROUPS, n, WIDE), low_type),
            pltpu.HBM((4, GROUPS, 2, s, cols), low_type),
            jax.ShapeDtypeStruct((SMALL, 2 * WIDE), wide),
            pltpu.HBM((2, 2, 2, 2, 2, n, WIDE), low_type),
            jax.ShapeDtypeStruct((2, 2, GROUPS, 2, s, quarter), low_type),
            jax.ShapeDtypeStruct((2, 2, GROUPS, 2, s, depth), low_type),
            jax.ShapeDtypeStruct((GROUPS, n, PACK), low_type),
            jax.ShapeDtypeStruct((GROUPS * n, PACK), wide),
            jax.ShapeDtypeStruct((GROUPS, 8, n), wide),
        ),
        in_specs=[pl.BlockSpec(memory_space=pltpu.HBM)] * (8 + count),
        out_specs=(pl.BlockSpec(memory_space=pl.ANY),) * 7
        + (pl.BlockSpec(memory_space=vmem),) * 3,
        scratch_shapes=[
            dma((total,)), dma((total,)), dma((12,)), dma((4,)), dma((4,)),
            vmem((GROUPS, s, cols), low_type),
            vmem((GROUPS, n, depth), low_type),
            vmem((4, GROUPS, 2, s, cols), low_type),
            vmem((2, 2, n, WIDE), low_type),
            vmem((GROUPS, n, WIDE), low_type),
            vmem((4, s, quarter), low_type),
            vmem((s, depth), low_type),
            vmem((SMALL, 2 * WIDE), wide),
            vmem((s, LANES), wide),
            vmem((2, 2, 2, 2, 2, n, WIDE), low_type),
            vmem((LOCAL, GROUPS * n, LANES), low_type),
            vmem((LOCAL, LANES, GROUPS * n), wide),
            dma((6 + count,)),
            pltpu.SMEM(lengths.shape, jnp.int32),
            dma,
            *[vmem(item.shape, item.dtype) for item in (wq, wk, wv, tables, *vectors, inner, mix)],
        ],
        compiler_params=pltpu.CompilerParams(
            collective_id=10, has_side_effects=True, vmem_limit_bytes=NEAR_LIMIT
        ),
    )(*[pltpu.with_memory_space_constraint(item, pltpu.HBM) for item in (lengths, tokens, wq, wk, wv, tables, *vectors, inner, mix)])


def pass_back(ident, pieces):
    def body(source, target, send, recv):
        me = Spot()
        owners = me.owners()
        readers = [device for _, device in me.readers()]
        barrier, expected = announce(readers[1:], [(jnp.logical_not(me.selfish), readers[0])])
        pl.semaphore_wait(barrier, expected)
        move = Scatter(send, recv, me.selfish)
        move.start([(source.at[slot], device) for slot, device in owners], target.at[me.g], me.g)
        for g in range(GROUPS):
            move.arrived(g, target.at[g])
        move.finish()

    return scatter_call(body, "pass_back", ident, pieces)


def pass_on(ident, pieces):
    def body(source, target, send, recv):
        me = Spot()
        owners = [device for _, device in me.owners()]
        barrier, expected = announce(owners[1:], [(jnp.logical_not(me.selfish), owners[0])])
        pl.semaphore_wait(barrier, expected)
        move = Scatter(send, recv, me.selfish)
        slot = me.slot()
        move.start([(source.at[g], device) for g, device in me.readers()], target.at[slot], slot)
        for index in range(GROUPS):
            move.arrived(index, target.at[index])
        move.finish()

    return scatter_call(body, "pass_on", ident, pieces)


def scatter_call(body, name, ident, pieces):
    return pl.pallas_call(
        body,
        name=name,
        out_shape=jax.ShapeDtypeStruct(pieces.shape, pieces.dtype),
        in_specs=[pl.BlockSpec(memory_space=pl.ANY)],
        out_specs=pl.BlockSpec(memory_space=pl.ANY),
        scratch_shapes=[pltpu.SemaphoreType.DMA((4,)), pltpu.SemaphoreType.DMA((4,))],
        compiler_params=pltpu.CompilerParams(
            collective_id=ident, has_side_effects=True, vmem_limit_bytes=VMEM_LIMIT
        ),
    )(pieces)


def final_kernel(output, hidden, pieces, outqk, out1, out2, outm, s, e):
    n, depth = hidden.shape
    quarter = out1.shape[-1]

    def body(y_in, hid, dx, qk_in, i_in, o_in, m_in, yo, xg, qw, qb, kw, vw, vb, mw, mb, eg, es, iw, ib, ow, ob, fg, fs):
        device = lax.axis_index("au") * lax.axis_size("row") + lax.axis_index("row")
        yo[...] = y_in[...]
        xg[...] = total_of(hid[...], dx[0], dx[1], dx[2], dx[3]).astype(low_type)
        rows = qk_in.shape[1]
        q_in, k_in = qk_in.at[:, :, WIDE:], qk_in.at[:, :, :WIDE]
        lower = lax.broadcasted_iota(jnp.int32, (rows, LANES), 1) < HEAD

        def part(head):
            g, h = head // LOCAL, head % LOCAL
            return k_in[g, :, h * LANES : (h + 1) * LANES].astype(wide)

        made_q = []
        for g in range(0, GROUPS, 2):
            a0, b0 = q_in[g, :, :LANES].astype(wide), q_in[g, :, LANES:].astype(wide)
            a1 = pltpu.roll(q_in[g + 1, :, :LANES].astype(wide), HEAD, 1)
            b1 = pltpu.roll(q_in[g + 1, :, LANES:].astype(wide), HEAD, 1)
            made_q += [a0, jnp.where(lower, b0, a1), jnp.where(lower, a1, b1)]
        biases = [[], []]
        for pair in range(HEADS // 2):
            span = slice(pair * LANES, (pair + 1) * LANES)
            kv = [part(2 * pair), part(2 * pair + 1)]
            made_k = jnp.where(lower, kv[0], pltpu.roll(kv[1], HEAD, 1))
            made_v = jnp.where(lower, pltpu.roll(kv[0], HEAD, 1), kv[1])
            qw[:, span], kw[:, span], vw[:, span] = made_q[pair][:s], made_k[:s], made_v[:s]
            biases[0].append(made_q[pair][s:])
            biases[1].append(made_v[s:])

        def own(eight, width, shift):
            return pltpu.roll(eight, shift, 1)[0:1, :width]

        turn = (depth - device * s) % depth
        qb[...] = own(jnp.concatenate(biases[0], axis=1), s, turn)
        vb[...] = own(jnp.concatenate(biases[1], axis=1), s, turn)
        mw[...] = m_in[:s]
        extras = pltpu.roll(m_in[s : s + 8, :], turn, 1)
        for index, ref in enumerate((mb, eg, es, ob, fg, fs)):
            ref[...] = extras[index : index + 1, :s]
        for w in range(4):
            iw[:, w * quarter : (w + 1) * quarter] = i_in[w, :s].astype(wide)
        place = lax.axis_index("row") * e
        ib[...] = own(
            i_in[lax.axis_index("au"), s : s + 8, :].astype(wide), e, (quarter - place) % quarter
        )
        ow[...] = o_in[...]

    vmem = pltpu.VMEM

    def shape(*dims):
        return jax.ShapeDtypeStruct(dims, wide)

    return pl.pallas_call(
        body,
        name="final_kernel",
        out_shape=(
            jax.ShapeDtypeStruct((n, depth), low_type),
            jax.ShapeDtypeStruct((n, depth), low_type),
            shape(s, depth), shape(1, s), shape(s, depth), shape(s, depth), shape(1, s),
            shape(s, depth), shape(1, s), shape(1, s), shape(1, s),
            shape(s, 4 * quarter), shape(1, e), shape(e, depth),
            shape(1, s), shape(1, s), shape(1, s),
        ),
        in_specs=[pl.BlockSpec(memory_space=vmem)] * 7,
        out_specs=(pl.BlockSpec(memory_space=vmem),) * 17,
        compiler_params=pltpu.CompilerParams(vmem_limit_bytes=NEAR_LIMIT),
    )(output, hidden, pieces, outqk, out1, out2, outm)


def gelu_and_slope(value):
    t = 1.0 / (1.0 + (0.3275911 * 0.7071067811865476) * jnp.abs(value))
    bell = jnp.exp(-0.5 * value * value)
    tail = 1.061405429
    for weight in (-1.453152027, 1.421413741, -0.284496736, 0.254829592):
        tail = tail * t + weight
    tail = 0.5 * tail * t * bell
    below = jnp.where(value >= 0.0, 1.0 - tail, tail)
    return value * below, below + value * bell * 0.3989422804014327


def normed(hidden):
    mean = jnp.mean(hidden, axis=-1, keepdims=True)
    centered = hidden - mean
    spread = jnp.mean(centered * centered, axis=-1, keepdims=True)
    inverse = lax.rsqrt(spread + eps_norm)
    return centered * inverse, inverse


def normed_grad(grad, norm, inverse):
    mean = jnp.mean(grad, axis=-1, keepdims=True)
    along = jnp.mean(grad * norm, axis=-1, keepdims=True)
    return inverse * (grad - mean - norm * along)


def down_sum(values):
    return jnp.sum(values, axis=0, keepdims=True)


def middle_kernel(mixed, tokens, cotangent, mix, inner, outer, vec, s, e):
    n, depth = tokens.shape
    quarter = inner.shape[1]
    rows = s + 8
    cut = depth // 2
    hn = n // 2

    def body(
        mixed_ref, tok_in, cot_in, wm_in, w1_in, w2f_in, vec_in,
        out, hidden_out, do_out, sm, s1, s2,
        send, recv, local, back_send, back_recv, on_send, on_recv,
        swap_send2, swap_recv2, tok, cot, w2f, vec_ref, wm, w1, w2p, w2s, came, mixed_tok, xs, acts, slopes, parts, sums, bgs, igs, parts2, sums2,
        pieces, extra, attn, own1, own2, g1, g2, gm,
    ):
        me = Spot()
        copies = Copies(send, recv, local)
        square = me.square()
        line = [to for to, _ in me.line()]
        owners = me.owners()
        readers = me.readers()
        swapped = [me.at(g=to, c=me.y, y=me.c) for to in [me.g] + line]
        barrier, expected = announce(
            [me.at(x=x, y=y) for x, y in square]
            + swapped[1:]
            + [device for _, device in readers[1:]]
            + [device for _, device in owners[1:]]
            + [me.sibling()],
            [
                (jnp.logical_not(me.selfish), readers[0][1]),
                (jnp.logical_not(me.selfish), owners[0][1]),
                (me.crossing, swapped[0]),
            ],
        )
        loads = [copies.keep(wm_in, wm), copies.keep(w1_in, w1)]
        small_loads = [
            copies.keep(source, target)
            for source, target in ((tok_in, tok), (vec_in, vec_ref), (w2f_in, w2f), (cot_in, cot))
        ]
        pl.semaphore_wait(barrier, expected)

        back = Scatter(back_send, back_recv, me.selfish)
        back.start([(mixed_ref.at[slot], device) for slot, device in owners], came.at[me.g], me.g)
        lower = lax.broadcasted_iota(jnp.int32, (n, LANES), 1) < HEAD
        loads[0].wait()
        for copy in small_loads:
            copy.wait()
        w2s[...] = w2f[...].astype(low_type)
        for g in range(GROUPS):
            back.arrived(g, came.at[g])
        w2_place = w2p.at[me.g, me.y]
        w2_first = [copies.push(w2s, w2_place, device) for device in swapped[1:]]
        w2_swap = pltpu.make_async_remote_copy(
            src_ref=w2s,
            dst_ref=w2_place,
            send_sem=swap_send2,
            recv_sem=swap_recv2,
            device_id=swapped[0],
            device_id_type=MESH,
        )
        w2_stays = pltpu.make_async_copy(w2s, w2_place, swap_recv2)

        @pl.when(me.crossing)
        def _():
            w2_swap.start()

        @pl.when(jnp.logical_not(me.crossing))
        def _():
            w2_stays.start()

        for half in range(2):
            a0 = came[2 * half, :, :LANES]
            b0 = came[2 * half, :, LANES:].astype(wide)
            a1 = pltpu.roll(came[2 * half + 1, :, :LANES].astype(wide), HEAD, 1)
            b1 = pltpu.roll(came[2 * half + 1, :, LANES:].astype(wide), HEAD, 1)
            base = half * 3 * LANES
            mixed_tok[:, base : base + LANES] = a0
            mixed_tok[:, base + LANES : base + 2 * LANES] = jnp.where(lower, b0, a1).astype(low_type)
            mixed_tok[:, base + 2 * LANES : base + 3 * LANES] = jnp.where(lower, a1, b1).astype(
                low_type
            )

        def vector(index):
            return vec_ref[index : index + 1, :]

        mix = jnp.dot(mixed_tok[...], wm[...], preferred_element_type=wide) + vector(2)
        norm1, inverse1 = normed(tok[...].astype(wide) + mix)
        early = norm1 * vector(3) + vector(4)
        mine = me.x * 2 + me.y
        halves = [slice(0, hn), slice(hn, n)]

        def send_rows(ref, h):
            place = ref.at[h, mine]
            return [copies.push(place, place, me.at(x=x, y=y)) for x, y in square]

        def send_back(ref, landing, h):
            return [
                copies.push(ref.at[h, x * 2 + y], landing.at[h, mine], me.at(x=x, y=y))
                for x, y in square
            ]

        def arrive(started):
            for copy in started:
                copy.wait_recv()

        def received(landing, h):
            return [landing[h, x * 2 + y] for x, y in square]

        early_go = []
        for h, half in enumerate(halves):
            xs[h, mine] = early[half].astype(low_type)
            early_go.append(send_rows(xs, h))
            if h == 0:
                for copy in early_go[0]:
                    copy.wait_send()
                copies.started = [
                    item for item in copies.started if all(item is not copy for copy in early_go[0])
                ]
        loads[1].wait()

        def outer_weight():
            return w2p[...].reshape(quarter, depth)

        branch_go = []
        for h in range(2):
            arrive(early_go[h])
            inner = jnp.dot(
                xs[h].reshape(4 * hn, depth), w1[...], preferred_element_type=wide
            ) + vector(8)
            act, slope = gelu_and_slope(inner)
            act = act.astype(low_type)
            acts[h] = act.reshape(4, hn, quarter)
            slopes[h] = slope
            if h == 0:

                @pl.when(me.crossing)
                def _():
                    w2_swap.wait_recv()
                    w2_swap.wait_send()

                @pl.when(jnp.logical_not(me.crossing))
                def _():
                    w2_stays.wait()

                block = w2p.at[me.g, me.c]
                w2_last = [copies.push(block, block, me.sibling())]
                for copy, (_, source) in zip(w2_first, me.line()):
                    copy.wait_recv()
                    block = w2p.at[source, me.c]
                    w2_last.append(copies.push(block, block, me.sibling()))
                arrive(w2_last)
            made = jnp.dot(act, outer_weight(), preferred_element_type=wide).reshape(4, hn, depth)
            own1[h] = made
            parts[h] = made.astype(low_type)
            branch_go.append(send_back(parts, sums, h))

        grad_go, final_grads, norm_sums, cot_sums = [], [], [], []
        for h, half in enumerate(halves):
            arrive(branch_go[h])
            branch = total_of(own1[h, mine], *received(sums, h)) + vector(5)
            norm2, inverse2 = normed(early[half] + branch)
            out[half, :] = (norm2 * vector(6) + vector(7)).astype(low_type)
            cot_wide = cot[half, :].astype(wide)
            final_grad = normed_grad(cot_wide * vector(6), norm2, inverse2)
            bgs[h, mine] = final_grad.astype(low_type)
            grad_go.append(send_rows(bgs, h))
            final_grads.append(final_grad)
            norm_sums.append(down_sum(cot_wide * norm2))
            cot_sums.append(down_sum(cot_wide))
        extra[...] = jnp.zeros_like(extra)
        extra[3:4, :] = down_sum(bgs[0, mine].astype(wide)) + down_sum(bgs[1, mine].astype(wide))
        extra[4:5, :] = norm_sums[0] + norm_sums[1]
        extra[5:6, :] = cot_sums[0] + cot_sums[1]

        token_go = []
        for h in range(2):
            arrive(grad_go[h])
            grad = lax.dot_general(
                bgs[h].reshape(4 * hn, depth), outer_weight(), NEXT, preferred_element_type=wide
            )
            grad = (grad * slopes[h]).astype(low_type)
            igs[h] = grad.reshape(4, hn, quarter)
            made = lax.dot_general(grad, w1[...], NEXT, preferred_element_type=wide)
            made = made.reshape(4, hn, depth)
            own2[h] = made
            parts2[h] = made.astype(low_type)
            token_go.append(send_back(parts2, sums2, h))

        other = 1 - me.c
        grads = bgs[...].reshape(4 * n, depth)
        for half in range(2):
            span = slice(half * cut, (half + 1) * cut)
            made = lax.dot_general(
                acts[:, :, :, span].reshape(4 * n, cut), grads, DOWN, preferred_element_type=wide
            )
            g2[2 * half : 2 * half + 2] = made.astype(low_type).reshape(2, 2, e, depth)
        w2_half = copies.push(g2.at[:, other], s2, me.sibling())

        grads = igs[...].reshape(4 * n, quarter)
        bias = jnp.broadcast_to(down_sum(grads.astype(wide)), (8, quarter)).astype(low_type)
        for half in range(2):
            span = slice(half * cut, (half + 1) * cut)
            made = lax.dot_general(
                xs[:, :, :, span].reshape(4 * n, cut), grads, DOWN, preferred_element_type=wide
            ).astype(low_type)
            for index in range(16):
                place = (half, index // 8, index // 2 % GROUPS, index % 2)
                g1[(*place, slice(None, s))] = made[index * s : (index + 1) * s]
                g1[(*place, slice(s, None))] = bias
        w1_half = copies.push(g1.at[:, other], s1, me.sibling())
        w2_half.wait_recv()

        def add2(g):
            s2[g] = s2[g] + g2[g, me.c]

        loop(GROUPS, add2)
        w1_half.wait_recv()

        def add1(index):
            x, g, y = index // 8, index // 2 % GROUPS, index % 2
            s1[x, g, y] = s1[x, g, y] + g1[x, me.c, g, y]

        loop(16, add1)
        norm_sums, grad_sums, attn_sums = [], [], []
        for h, half in enumerate(halves):
            arrive(token_go[h])
            early_grad = total_of(final_grads[h], own2[h, mine], *received(sums2, h))
            norm_sums.append(down_sum(early_grad * norm1[half]))
            grad_sums.append(down_sum(early_grad))
            hidden = normed_grad(early_grad * vector(3), norm1[half], inverse1[half])
            hidden_out[half, :] = hidden
            attn[half, :] = hidden.astype(low_type)
            attn_sums.append(down_sum(hidden.astype(low_type).astype(wide)))
        extra[0:1, :] = attn_sums[0] + attn_sums[1]
        extra[1:2, :] = norm_sums[0] + norm_sums[1]
        extra[2:3, :] = grad_sums[0] + grad_sums[1]
        attn_grad = attn[...]
        back_grad = lax.dot_general(attn_grad, wm[...], NEXT, preferred_element_type=wide)
        for half in range(2):
            base = half * 3 * LANES
            t0 = back_grad[:, base : base + LANES]
            t1 = back_grad[:, base + LANES : base + 2 * LANES]
            t2 = back_grad[:, base + 2 * LANES : base + 3 * LANES]
            r1, r2 = pltpu.roll(t1, HEAD, 1), pltpu.roll(t2, HEAD, 1)
            pieces[2 * half, :, :LANES] = t0.astype(low_type)
            pieces[2 * half, :, LANES:] = jnp.where(lower, t1, 0.0).astype(low_type)
            pieces[2 * half + 1, :, :LANES] = jnp.where(lower, r1, r2).astype(low_type)
            pieces[2 * half + 1, :, LANES:] = jnp.where(lower, r2, 0.0).astype(low_type)
        onward = Scatter(on_send, on_recv, me.selfish)
        slot = me.slot()
        onward.start([(pieces.at[g], device) for g, device in readers], do_out.at[slot], slot)

        for half in range(2):
            span = slice(half * cut, (half + 1) * cut)
            made = lax.dot_general(
                mixed_tok[:, span], attn_grad, DOWN, preferred_element_type=wide
            ).astype(low_type)
            for index in range(16):
                place = (half, index // 8, index // 2 % GROUPS, index % 2)
                gm[(*place, slice(None, s))] = made[index * s : (index + 1) * s]
                gm[(*place, slice(s, None))] = extra[...].astype(low_type)
        wm_half = copies.push(gm.at[:, other], sm, me.sibling())
        wm_half.wait_recv()

        def addm(index):
            x, g, y = index // 8, index // 2 % GROUPS, index % 2
            sm[x, g, y] = sm[x, g, y] + gm[x, me.c, g, y]

        loop(16, addm)
        for index in range(GROUPS):
            onward.arrived(index, do_out.at[index])
        back.finish()
        onward.finish()
        copies.finish()

    vmem = pltpu.VMEM
    dma = pltpu.SemaphoreType.DMA
    tall = vmem((2, 4, hn, depth), low_type)
    full = vmem((2, 4, hn, depth), wide)
    high = vmem((2, 4, hn, quarter), low_type)
    tokens, cotangent, outer = [
        pltpu.with_memory_space_constraint(item, pltpu.HBM) for item in (tokens, cotangent, outer)
    ]
    return pl.pallas_call(
        body,
        name="middle_kernel",
        out_shape=(
            jax.ShapeDtypeStruct((n, depth), low_type),
            jax.ShapeDtypeStruct((n, depth), wide),
            jax.ShapeDtypeStruct((GROUPS, n, PACK), low_type),
            jax.ShapeDtypeStruct((2, GROUPS, 2, rows, depth), low_type),
            jax.ShapeDtypeStruct((2, GROUPS, 2, rows, quarter), low_type),
            jax.ShapeDtypeStruct((GROUPS, e, depth), low_type),
        ),
        in_specs=[
            pl.BlockSpec(memory_space=item)
            for item in (pl.ANY, pltpu.HBM, pltpu.HBM, pl.ANY, pl.ANY, pltpu.HBM, pl.ANY)
        ],
        out_specs=[
            pl.BlockSpec(memory_space=item) for item in (vmem, vmem, pl.ANY, vmem, vmem, vmem)
        ],
        scratch_shapes=[
            dma((48,)), dma((48,)), dma((8,)), dma((4,)), dma((4,)), dma((4,)), dma((4,)), dma, dma,
            vmem((n, depth), low_type),
            vmem((n, depth), low_type),
            vmem((e, depth), wide),
            vmem(vec.shape, wide),
            vmem((depth, depth), low_type),
            vmem((depth, quarter), low_type),
            vmem((GROUPS, 2, e, depth), low_type),
            vmem((e, depth), low_type),
            vmem((GROUPS, n, PACK), low_type),
            vmem((n, depth), low_type),
            tall, high,
            vmem((2, 4 * hn, quarter), wide),
            tall, tall, tall, high, tall, tall,
            vmem((GROUPS, n, PACK), low_type),
            vmem((8, depth), wide),
            vmem((n, depth), low_type),
            full, full,
            vmem((2, 2, GROUPS, 2, rows, quarter), low_type),
            vmem((GROUPS, 2, e, depth), low_type),
            vmem((2, 2, GROUPS, 2, rows, depth), low_type),
        ],
        compiler_params=pltpu.CompilerParams(
            collective_id=12, has_side_effects=True, vmem_limit_bytes=NEAR_LIMIT
        ),
    )(mixed, tokens, cotangent, mix, inner, outer, vec)


def tile_base(me, slot, n):
    u, v = slot // 2, slot % 2
    return ((u * 2 + me.c) * 2 * GROUPS + (v * 2 + me.p) * 2 + me.y) * n


def ends_of(lengths_ref):
    ends = [lengths_ref[0]]
    for index in range(1, lengths_ref.shape[0]):
        ends.append(ends[-1] + lengths_ref[index])
    return ends


def document_of(place, ends):
    first, last = place * 0, place * 0 + ends[-1]
    for end in ends[:-1]:
        before = end <= place
        first = jnp.where(before, end, first)
    for end in reversed(ends[:-1]):
        last = jnp.where(end <= place, last, end)
    return first, last


def turn_kernel(lengths, queries, keys, grads_in, mixed, lse, tokens, weights, sum1, sum2, summ):
    n = tokens.shape[1]
    depth = tokens.shape[-1]
    s = depth // 32
    rows = s + 8
    cut = depth // 2
    tall = sum2.shape[1]
    block = GROUPS * n
    width = WIDE + PACK
    spans = [slice(h * LANES, (h + 1) * LANES) for h in range(LOCAL)]

    def body(
        lengths_ref, q_ref, kv_ref, do_ref, mixed_ref, lse_ref, tok, w_ref, s1, s2, sm,
        dx_out, outqk, out1, out2, outm,
        send, recv, local, dx_send, dx_recv, swap_send, swap_recv, ks, kr, ps, pr,
        both, kbuf, kin, pk, dqs, narrow, dxs, gk, sk, pp, fk, p1, f1, pm, fm, tm, p2, early,
    ):
        me = Spot()
        copies = Copies(send, recv, local)
        square = me.square()
        line = [to for to, _ in me.line()]
        readers = [device for _, device in me.readers()]
        swapped = [me.at(g=to, c=me.y, y=me.c) for to in [me.g] + line]
        barrier, expected = announce(
            [me.at(x=x, y=y) for x, y in square]
            + [me.at(g=to) for to in line]
            + readers[1:]
            + swapped[1:]
            + [me.sibling()],
            [(jnp.logical_not(me.selfish), readers[0]), (me.crossing, swapped[0])],
        )
        ends = ends_of(lengths_ref)
        lane = lax.broadcasted_iota(jnp.int32, (n, LANES), 1)
        upper = lane >= HEAD
        along = lax.broadcasted_iota(jnp.int32, (1, n), 1)
        down = lax.broadcasted_iota(jnp.int32, (block, n), 0)

        def upper_halves(ref, part):
            front = ref[part, :LANES].astype(wide)
            back = ref[part, LANES:].astype(wide)
            parts = (pltpu.roll(front, HEAD, 1), front, pltpu.roll(back, HEAD, 1))
            return [jnp.where(upper, item, 0.0) for item in parts]

        firsts, lasts, logs, deltas = [], [], [], []
        for slot in range(GROUPS):
            part = slice(slot * n, (slot + 1) * n)
            first, last = document_of(along + tile_base(me, slot, n), ends)
            firsts.append(first)
            lasts.append(last)
            outs, inputs = upper_halves(mixed_ref, part), upper_halves(do_ref, part)
            for h, span in enumerate(spans):
                base = slot * 2 * n
                both[h, base : base + n] = q_ref[part, span] * jnp.asarray(0.125, low_type)
                both[h, base + n : base + 2 * n] = inputs[h].astype(low_type)
            deltas.append([down_sum(jnp.transpose(i * o)) for i, o in zip(inputs, outs)])
            logs.append([lse_ref[slot, h : h + 1, :] for h in range(LOCAL)])
        dqs[...] = jnp.zeros_like(dqs)
        pl.semaphore_wait(barrier, expected)

        wm_push = [
            copies.push(sm.at[x, :, y], pm.at[peer], me.at(x=x, y=y))
            for peer, (x, y) in enumerate(square)
        ]
        w1_push = [
            copies.push(s1.at[:, to, :], p1.at[slot], me.at(g=to)) for slot, to in enumerate(line)
        ]
        w2_push = [
            copies.push(s2.at[to], p2.at[index + 1], swapped[index + 1])
            for index, to in enumerate(line)
        ]
        exchanged = pltpu.make_async_remote_copy(
            src_ref=s2.at[me.g],
            dst_ref=p2.at[0],
            send_sem=swap_send,
            recv_sem=swap_recv,
            device_id=swapped[0],
            device_id_type=MESH,
        )
        stays = pltpu.make_async_copy(s2.at[me.g], p2.at[0], swap_recv)

        @pl.when(me.crossing)
        def _():
            exchanged.start()

        @pl.when(jnp.logical_not(me.crossing))
        def _():
            stays.start()

        other = 1 - me.c

        def attend(u, c, v, target):
            begin = pl.multiple_of(((u * 2 + c) * 2 + v) * block, block)
            place = down + begin
            same = [(place >= first) & (place < last) for first, last in zip(firsts, lasts)]
            for h, span in enumerate(spans):
                kv = kv_ref[pl.ds(begin, block), span]
                made = lax.dot_general(kv, both[h], NEXT, preferred_element_type=wide)
                pairs = []
                for slot in range(GROUPS):
                    base = slot * 2 * n
                    scores = jnp.where(same[slot], made[:, base : base + n], mask_fill)
                    probs = jnp.exp(scores - logs[slot][h])
                    dots = made[:, base + n : base + 2 * n]
                    score_grad = (probs * (dots - deltas[slot][h])).astype(low_type)
                    pairs += [score_grad, probs.astype(low_type)]
                    dqs[slot, :, span] += lax.dot_general(
                        score_grad, kv, DOWN, preferred_element_type=wide
                    )
                made = jnp.dot(
                    jnp.concatenate(pairs, axis=1), both[h], preferred_element_type=wide
                )
                target[:, :, :, span] = made.astype(low_type).reshape(2, 2, n, LANES)

        def to_sibling(turn):
            return pltpu.make_async_remote_copy(
                src_ref=kbuf.at[0, turn],
                dst_ref=kin.at[turn],
                send_sem=ks.at[turn],
                recv_sem=kr.at[turn],
                device_id=me.sibling(),
                device_id_type=MESH,
            )

        def to_peer(turn, peer):
            x, y = square[peer]
            return pltpu.make_async_remote_copy(
                src_ref=kbuf.at[1, turn, (x + me.c) % 2, y],
                dst_ref=pk.at[turn, peer],
                send_sem=ps.at[turn * 3 + peer],
                recv_sem=pr.at[turn * 3 + peer],
                device_id=me.at(x=x, y=y),
                device_id_type=MESH,
            )

        def key_turn(turn):
            u, v = turn % 2, (me.half + turn // 2) % 2

            def of_core(index):
                attend(u, jnp.where(index == 0, other, me.c), v, kbuf.at[index, turn])

                @pl.when(index == 0)
                def _():
                    to_sibling(turn).start()

            loop(2, of_core)
            to_sibling(turn).wait_recv()
            for p in range(2):
                for y in range(2):
                    kbuf[1, turn, p, y] = kbuf[1, turn, p, y] + kin[turn, p, y]
            for peer in range(3):
                to_peer(turn, peer).start()

        loop(4, key_turn)

        def square_push(total, landing):
            return [
                copies.push(total.at[x, :, y], landing.at[slot], me.at(x=x, y=y))
                for slot, (x, y) in enumerate(square)
            ]

        def square_sum(result, total, landed):
            def add(g):
                result[g] = total_of(
                    total[me.x, g, me.y], landed[0, g], landed[1, g], landed[2, g]
                ).astype(low_type)

            loop(GROUPS, add)

        def weight_grad(slots, half):
            span = slice(half * cut, (half + 1) * cut)
            return lax.dot_general(
                jnp.concatenate([tok[slot, :, span] for slot in slots], axis=0),
                jnp.concatenate([narrow[slot] for slot in slots], axis=0),
                DOWN,
                preferred_element_type=wide,
            )

        moves = []
        slots = [turn % 2 * 2 + (me.half + turn // 2) % 2 for turn in range(4)]
        for turn in range(4):
            if turn == 3:
                for half in range(2):
                    early[half] = weight_grad(slots[:3], half)
                for copy in wm_push:
                    copy.wait_recv()
                square_sum(fm, sm, pm)
                wm_last = [
                    copies.push(fm.at[to], tm.at[peer], me.at(g=to)) for peer, to in enumerate(line)
                ]
                for copy in w1_push:
                    copy.wait_recv()

                def addw(index):
                    x, y = index // 2, index % 2
                    f1[x, y] = total_of(s1[x, me.g, y], *[p1[peer, x, y] for peer in range(3)]).astype(
                        low_type
                    )

                loop(4, addw)
            u, dv = turn % 2, turn // 2
            v = (me.half + dv) % 2
            slot = u * 2 + v
            wides = [dqs[slot, :, span] * 0.125 for span in spans]
            narrow[slot, :, WIDE : WIDE + LANES] = jnp.where(
                upper, pltpu.roll(wides[1], HEAD, 1), wides[0]
            ).astype(low_type)
            narrow[slot, :, WIDE + LANES :] = jnp.where(upper, 0.0, wides[2]).astype(low_type)
            for peer in range(3):
                to_peer(turn, peer).wait_recv()
            here = total_of(
                kbuf[1, turn, me.p, me.y], *[pk[turn, peer] for peer in range(3)]
            ).astype(low_type)
            narrow[slot, :, :WIDE] = here
            dxs[slot] = lax.dot_general(
                narrow[slot], w_ref[:, :width], NEXT, preferred_element_type=wide
            ).astype(low_type)
            copy = pltpu.make_async_remote_copy(
                src_ref=dxs.at[slot],
                dst_ref=dx_out.at[me.g],
                send_sem=dx_send.at[turn],
                recv_sem=dx_recv.at[me.g],
                device_id=me.at(x=u, g=2 * v + me.p),
                device_id_type=MESH,
            )
            if dv:
                copy.start()
                moves.append((copy, None))
                continue
            stay = pltpu.make_async_copy(dxs.at[slot], dx_out.at[me.g], dx_recv.at[me.g])
            at_home = me.selfish & (me.x == u)
            away = jnp.logical_not(at_home)
            moves.append((copy, away))

            @pl.when(at_home)
            def _(stay=stay):
                stay.start()

            @pl.when(away)
            def _(copy=copy):
                copy.start()

        bias = down_sum(total_of(*[down_sum(narrow[slot].astype(wide)) for slot in range(GROUPS)]))
        bias = jnp.broadcast_to(bias, (8, width)).astype(low_type)
        for half in range(2):
            made = (early[half] + weight_grad(slots[3:], half)).astype(low_type)
            for index in range(16):
                place = (half, index // 8, index // 2 % GROUPS, index % 2)
                gk[(*place, slice(None, s))] = made[index * s : (index + 1) * s]
                gk[(*place, slice(s, None))] = bias
        g_half = copies.push(gk.at[:, other], sk, me.sibling())

        quarter = out1.at[me.x * 2 + me.y]
        g_half.wait_recv()

        def pair_sum(index):
            x, g, y = index // 8, index // 2 % GROUPS, index % 2
            sk[x, g, y] = sk[x, g, y] + gk[x, me.c, g, y]

        loop(16, pair_sum)
        push = square_push(sk, pp)
        arrivals = [copies.push(f1.at[x, y], quarter, me.at(x=x, y=y)) for x, y in square]
        kept = [copies.keep(f1.at[me.x, me.y], quarter)]

        @pl.when(me.crossing)
        def _():
            exchanged.wait_recv()
            exchanged.wait_send()

        @pl.when(jnp.logical_not(me.crossing))
        def _():
            stays.wait()

        for copy in w2_push:
            copy.wait_recv()
        out2[...] = total_of(*[p2[index] for index in range(4)])
        for copy in push:
            copy.wait_recv()
        square_sum(fk, sk, pp)
        arrivals += [copies.push(fk.at[to], outqk.at[me.g], me.at(g=to)) for to in line]
        kept.append(copies.keep(fk.at[me.g], outqk.at[me.g]))
        for copy in wm_last:
            copy.wait_recv()
        outm[...] = total_of(fm[me.g], *[tm[peer] for peer in range(3)])
        for copy in arrivals:
            copy.wait_recv()
        for g in range(GROUPS):
            pltpu.make_async_copy(dx_out.at[g], dx_out.at[g], dx_recv.at[g]).wait()
        for copy in kept:
            copy.wait()
        for copy, away in moves:
            if away is None:
                copy.wait_send()
                continue

            @pl.when(away)
            def _(copy=copy):
                copy.wait_send()

        for turn in range(4):
            to_sibling(turn).wait_send()
            for peer in range(3):
                to_peer(turn, peer).wait_send()
        copies.finish()

    vmem = pltpu.VMEM
    dma = pltpu.SemaphoreType.DMA
    total = 40
    return pl.pallas_call(
        body,
        name="turn_kernel",
        out_shape=(
            jax.ShapeDtypeStruct((GROUPS, n, depth), low_type),
            jax.ShapeDtypeStruct((GROUPS, rows, width), low_type),
            jax.ShapeDtypeStruct((4, rows, depth), low_type),
            jax.ShapeDtypeStruct((tall, depth), wide),
            jax.ShapeDtypeStruct((rows, depth), wide),
        ),
        in_specs=[pl.BlockSpec(memory_space=pltpu.SMEM)] + [pl.BlockSpec(memory_space=vmem)] * 10,
        out_specs=[pl.BlockSpec(memory_space=pl.ANY)] * 3 + [pl.BlockSpec(memory_space=vmem)] * 2,
        scratch_shapes=[
            dma((total,)), dma((total,)), dma((4,)), dma((4,)), dma((4,)), dma, dma,
            dma((4,)), dma((4,)), dma((12,)), dma((12,)),
            vmem((LOCAL, 2 * block, LANES), low_type),
            vmem((2, 4, 2, 2, n, WIDE), low_type),
            vmem((4, 2, 2, n, WIDE), low_type),
            vmem((4, 3, n, WIDE), low_type),
            vmem((GROUPS, n, WIDE), wide),
            vmem((GROUPS, n, width), low_type),
            vmem((GROUPS, n, depth), low_type),
            vmem((2, 2, GROUPS, 2, rows, width), low_type),
            vmem((2, GROUPS, 2, rows, width), low_type),
            vmem((3, GROUPS, rows, width), low_type),
            vmem((GROUPS, rows, width), low_type),
            vmem((3, 2, 2, rows, depth), low_type),
            vmem((2, 2, rows, depth), low_type),
            vmem((3, GROUPS, rows, depth), low_type),
            vmem((GROUPS, rows, depth), low_type),
            vmem((3, rows, depth), low_type),
            vmem((4, tall, depth), low_type),
            vmem((2, cut, width), wide),
        ],
        compiler_params=pltpu.CompilerParams(
            collective_id=11, has_side_effects=True, vmem_limit_bytes=TURN_LIMIT
        ),
    )(lengths, queries, keys, grads_in, mixed, lse, tokens, weights, sum1, sum2, summ)


def on_device_general(
    tokens,
    cotangent,
    doc_lengths,
    query_weight,
    query_bias,
    key_weight,
    value_weight,
    value_bias,
    mix_weight,
    mix_bias,
    early_gain,
    early_shift,
    inner_weight,
    inner_bias,
    outer_weight,
    outer_bias,
    final_gain,
    final_shift,
):
    n, depth = tokens.shape
    groups, cycle = lax.axis_size("au"), lax.axis_size("row")
    devices = groups * cycle
    zs = cycle // (2 * GROUPS)
    s = query_weight.shape[0]
    ff = inner_weight.shape[1]
    quarter = ff // 4
    e = outer_weight.shape[0]
    rows = GROUPS * n
    total_tokens = n * devices
    me = Place(zs)
    device = lax.axis_index("au") * cycle + lax.axis_index("row")
    w_me = me.x * 2 + me.y

    def by_head(weight):
        return weight.astype(low_type).reshape(-1, GROUPS, LOCAL, HEAD)

    def packed(query, key, value):
        kv = jnp.stack([key, value], axis=3).reshape(-1, GROUPS, WIDE)
        q = jnp.pad(query, ((0, 0), (0, 0), (0, 0), (0, HEAD))).reshape(-1, GROUPS, WIDE)
        return jnp.concatenate([kv, q], axis=2)

    slab = packed(by_head(query_weight), by_head(key_weight), by_head(value_weight))
    slab = jnp.transpose(slab, (1, 0, 2))
    small = jnp.concatenate(
        [
            vector.astype(low_type)
            for vector in (
                query_bias, value_bias, mix_bias, early_gain, early_shift,
                outer_bias, final_gain, final_shift, inner_bias,
            )
        ]
    )
    extra = -s % 8 or 8
    small = jnp.broadcast_to(
        jnp.pad(small, (0, 2 * WIDE - small.shape[0]))[None, None], (GROUPS, extra, 2 * WIDE)
    )
    slab = jnp.concatenate([slab, small], axis=1)
    tok_all, w_all = spread_tokens(zs, tokens, slab)
    tok_all = tok_all.reshape(rows, depth)
    w_qkv = w_all[..., :s, :].reshape(depth, 2 * WIDE)
    small = w_all[..., s, :].reshape(devices, 2 * WIDE)
    names = [small[:, i * s : (i + 1) * s].reshape(depth) for i in range(8)]
    q_bias, v_bias, m_bias, e_gain, e_shift, o_bias, f_gain, f_shift = names
    i_bias = small[:, 8 * s : 8 * s + e].reshape(4, quarter)[w_me].astype(wide)
    q_bias = q_bias.reshape(1, GROUPS, LOCAL, HEAD)
    v_bias = v_bias.reshape(1, GROUPS, LOCAL, HEAD)
    bias = packed(q_bias, jnp.zeros_like(q_bias), v_bias)[0, me.g].astype(wide)

    qkv = (jnp.dot(tok_all, w_qkv, preferred_element_type=wide) + bias).astype(low_type)
    queries = qkv[:, WIDE:]

    inner_slab = jnp.transpose(inner_weight.astype(low_type).reshape(s, 4, quarter), (1, 0, 2))
    kv_all, w1, w2, wm = spread_keys(
        zs,
        qkv[:, :WIDE].reshape(GROUPS, n, WIDE),
        inner_slab,
        outer_weight.astype(low_type),
        mix_weight.astype(low_type),
    )
    kv_all = kv_all.reshape(total_tokens, WIDE)
    w1 = w1.reshape(depth, quarter)
    w2 = w2.reshape(quarter, depth)
    wm = wm.reshape(depth, depth)

    tile, block = 128, 512
    count = doc_lengths.shape[0]
    upto = jnp.arange(count)[None, :] <= jnp.arange(count)[:, None]
    ends = jnp.sum(jnp.where(upto, doc_lengths[None, :], 0), axis=1)
    owners = ((me.x * 2 + me.c) * cycle + me.z * GROUPS * 2 + jnp.arange(GROUPS) * 2 + me.y) * n
    places = (owners[:, None] + jnp.arange(n)[None, :]).reshape(rows)
    before = ends[None, :] <= places[:, None]
    first = jnp.max(jnp.where(before, ends[None, :], 0), axis=1).astype(jnp.int32)
    last = jnp.min(jnp.where(before, total_tokens, ends[None, :]), axis=1).astype(jnp.int32)
    tiles = rows // tile
    bounds = jnp.stack(
        [
            first.reshape(tiles, tile)[:, 0] // block,
            (last.reshape(tiles, tile)[:, -1] + block - 1) // block,
        ],
        axis=1,
    )
    mixed, mixed_wide, lse = attend_forward(
        queries, kv_all, bounds, first[:, None], last[:, None], tile, block
    )
    mixed_tok = exchange_line(zs, 2, mixed.reshape(GROUPS, n, PACK))
    mixed_tok = jnp.transpose(mixed_tok[:, :, : LOCAL * HEAD], (1, 0, 2)).reshape(n, depth)

    attn = jnp.dot(mixed_tok, wm, preferred_element_type=wide) + m_bias.astype(wide)
    early, early_pull = jax.vjp(
        layer_norm, tokens.astype(wide) + attn, e_gain.astype(wide), e_shift.astype(wide)
    )
    early_all = gather_square(zs, 3, early.astype(low_type)).reshape(rows, depth)
    inner = jnp.dot(early_all, w1, preferred_element_type=wide) + i_bias
    act, gelu_pull = jax.vjp(gelu_exact, inner)
    act_low = act.astype(low_type)
    partial = jnp.dot(act_low, w2, preferred_element_type=wide).astype(low_type)
    partial = exchange_square(zs, 4, partial.reshape(2, 2, n, depth))
    branch = jnp.sum(partial.astype(wide), axis=(0, 1)) + o_bias.astype(wide)
    result, final_pull = jax.vjp(
        layer_norm, early + branch, f_gain.astype(wide), f_shift.astype(wide)
    )
    output = result.astype(low_type)
    final_grads = final_pull(cotangent.astype(wide))
    branch_grad = final_grads[0].astype(low_type)
    outer_bias_grad = jnp.sum(branch_grad.astype(wide), axis=0)
    branch_all = gather_square(zs, 5, branch_grad).reshape(rows, depth)
    act_grad = jnp.einsum("td,fd->tf", branch_all, w2, preferred_element_type=wide)
    inner_grad = gelu_pull(act_grad)[0].astype(low_type)
    partial = jnp.einsum("tf,df->td", inner_grad, w1, preferred_element_type=wide).astype(low_type)
    partial = exchange_square(zs, 6, partial.reshape(2, 2, n, depth))
    grad2 = jnp.einsum("tf,td->fd", act_low, branch_all, preferred_element_type=wide)
    grad1 = jnp.einsum("td,tf->df", early_all, inner_grad, preferred_element_type=wide)
    inner_bias_grad = jnp.sum(inner_grad.astype(wide), axis=0)
    early_grad = final_grads[0] + jnp.sum(partial.astype(wide), axis=(0, 1))
    early_grads = early_pull(early_grad)
    attn_grad = early_grads[0].astype(low_type)
    mixed_grad = jnp.einsum("td,cd->tc", attn_grad, wm, preferred_element_type=wide)
    mixed_grad = jnp.transpose(
        mixed_grad.astype(low_type).reshape(n, GROUPS, LOCAL * HEAD), (1, 0, 2)
    )
    mixed_grad = jnp.pad(mixed_grad, ((0, 0), (0, 0), (0, PACK - LOCAL * HEAD)))
    grad_all = exchange_line(zs, 7, mixed_grad).reshape(rows, PACK)
    gradm = jnp.einsum("tc,td->cd", mixed_tok, attn_grad, preferred_element_type=wide)
    mix_bias_grad = jnp.sum(attn_grad.astype(wide), axis=0)

    delta = jnp.sum(
        (grad_all.astype(wide) * mixed_wide)[:, : LOCAL * HEAD].reshape(rows, LOCAL, HEAD), axis=2
    )

    def as_stat(values):
        return jnp.transpose(values.reshape(tiles, tile, LOCAL), (0, 2, 1))

    def same_stat(values):
        return jnp.broadcast_to(
            values.astype(wide).reshape(tiles, 1, tile), (tiles, LOCAL, tile)
        )

    stats = jnp.stack(
        [same_stat(first), same_stat(last), as_stat(lse[:, :LOCAL]), as_stat(delta)], axis=2
    )
    stats = jnp.pad(stats, ((0, 0), (0, 0), (0, 4), (0, 0)))
    query_grad, dkv = attend_backward(queries, kv_all, grad_all, stats, bounds, tile, block)

    def slabs(grad, extras):
        grad = grad.astype(low_type).reshape(devices, s, -1)
        rest = -s % 8
        rest += 0 if rest >= extras.shape[0] else 8
        extras = jnp.concatenate(
            [extras.astype(low_type), jnp.zeros((rest - extras.shape[0], extras.shape[1]), low_type)]
        )
        extras = jnp.broadcast_to(extras[None], (devices,) + extras.shape)
        return jnp.concatenate([grad, extras], axis=1).reshape(2, 2, zs, GROUPS, 2, s + rest, -1)

    mix_extras = jnp.stack(
        [
            mix_bias_grad, early_grads[1], early_grads[2],
            outer_bias_grad, final_grads[1], final_grads[2],
        ]
    )
    dkv, out1, out2, outm = reduce_keys(
        zs,
        dkv.reshape(2, 2, zs, GROUPS, 2, n, WIDE),
        slabs(grad1, inner_bias_grad[None]),
        grad2.astype(low_type).reshape(zs, GROUPS, 2, e, depth),
        slabs(gradm, mix_extras),
    )
    key_grad = jnp.sum(dkv.astype(wide), axis=0).astype(low_type).reshape(rows, WIDE)
    grads = jnp.concatenate([key_grad, query_grad], axis=1)
    gradq = jnp.einsum("tc,td->cd", tok_all, grads, preferred_element_type=wide)
    bias_grad = jnp.sum(grads.astype(wide), axis=0)
    partial = jnp.einsum("td,cd->tc", grads, w_qkv, preferred_element_type=wide).astype(low_type)
    partial, outq = reduce_tokens(
        zs, partial.reshape(GROUPS, n, depth), slabs(gradq, bias_grad[None])
    )
    input_grad = early_grads[0] + jnp.sum(partial.astype(wide), axis=0)

    def own(vector, count):
        return lax.dynamic_slice_in_dim(vector, device * count, count, 0).astype(wide)

    outq = outq.astype(wide)
    kv_out = outq[:, :, :WIDE].reshape(GROUPS, -1, LOCAL, 2, HEAD)
    q_out = outq[:, :, WIDE:].reshape(GROUPS, -1, LOCAL, 2, HEAD)[:, :, :, 0]

    def unpacked(values):
        return jnp.transpose(values, (1, 0, 2, 3)).reshape(-1, depth)

    q_out, k_out, v_out = unpacked(q_out), unpacked(kv_out[:, :, :, 0]), unpacked(kv_out[:, :, :, 1])
    inner_out = jnp.transpose(out1[:, :s], (1, 0, 2)).reshape(s, ff).astype(wide)
    return (
        output,
        input_grad.astype(low_type),
        q_out[:s],
        own(q_out[s], s),
        k_out[:s],
        v_out[:s],
        own(v_out[s], s),
        outm[:s],
        own(outm[s], s),
        own(outm[s + 1], s),
        own(outm[s + 2], s),
        inner_out,
        own(out1[:, s].reshape(ff), e),
        out2,
        own(outm[s + 3], s),
        own(outm[s + 4], s),
        own(outm[s + 5], s),
    )


def on_device(
    tokens,
    cotangent,
    doc_lengths,
    query_weight,
    query_bias,
    key_weight,
    value_weight,
    value_bias,
    mix_weight,
    mix_bias,
    early_gain,
    early_shift,
    inner_weight,
    inner_bias,
    outer_weight,
    outer_bias,
    final_gain,
    final_shift,
):
    n, depth = tokens.shape
    cycle = lax.axis_size("row")
    devices = lax.axis_size("au") * cycle
    s = query_weight.shape[0]
    ff = inner_weight.shape[1]
    quarter = ff // 4
    e = outer_weight.shape[0]
    rows = GROUPS * n
    total_tokens = n * devices
    me = Spot()
    vectors = [
        vector.reshape(1, -1)
        for vector in (
            query_bias, value_bias, mix_bias, early_gain, early_shift,
            outer_bias, final_gain, final_shift,
        )
    ]
    vectors.append(inner_bias.reshape(1, -1))
    toks, queries, w_qkv, vec, kv_all, w1, wm, mixed, mixed_wide, lse = first_kernel(
        doc_lengths, tokens, query_weight, key_weight, value_weight, vectors,
        inner_weight, mix_weight, e,
    )
    queries = queries.reshape(rows, WIDE)
    kv_all = kv_all.reshape(total_tokens, WIDE)
    w_qkv = w_qkv.reshape(depth, -1)
    w1 = w1.reshape(depth, quarter)
    wm = wm.reshape(depth, depth)
    output, hidden_grad, grad_all, summ, sum1, sum2 = middle_kernel(
        mixed.reshape(GROUPS, n, PACK), tokens, cotangent, wm, w1, outer_weight, vec, s, e
    )
    grad_all = grad_all.reshape(rows, PACK)
    pieces, outqk, out1, out2, outm = turn_kernel(
        doc_lengths, queries, kv_all, grad_all, mixed_wide, lse, toks, w_qkv, sum1, sum2, summ
    )
    results = final_kernel(output, hidden_grad, pieces, outqk, out1, out2, outm, s, e)
    return tuple(
        result.reshape(-1) if result.shape[0] == 1 else result for result in results
    )


def solution(mesh):
    both = P(("au", "row"), None)
    flat = P(("au", "row"))
    in_specs = (
        both, both, P(), both, flat, both, both, flat, both, flat, flat, flat,
        both, flat, both, flat, flat, flat,
    )
    out_specs = (
        both, both, both, flat, both, both, flat, both, flat, flat, flat,
        both, flat, both, flat, flat, flat,
    )
    fast = mesh.shape["au"] == 4 and mesh.shape["row"] == 2 * GROUPS
    return jax.shard_map(
        on_device if fast else on_device_general, mesh=mesh, in_specs=in_specs, out_specs=out_specs, check_vma=False
    )
```
